32 devices in a mesh: dp: 16 (over z, x, core), tensor: 2 (over y).
Axes of the slice: x: 2, y: 2, z: 4, core: 2. Of those that a mesh axis runs over, the one named last changes fastest.
Arguments:
- patches: bfloat16 [16384, 768], P('dp'), may hold values from -6 to 6
- cotangent: bfloat16 [16384, 768], P('dp'), may hold values from -6 to 6
- image_size: int32 [16, 5], P('dp'), may hold values from 0 to 3, as said below
- block_slot: int32 [2, 504], P('tensor'), may hold values from 0 to 511, as said below
- pinv: bfloat16 [3, 3072, 768], replicated, may hold values from -0.109375 to 0.109375
- master_slots: float32 [2, 512, 128, 128], P('tensor', 'dp'), may hold values from -0.21875 to 0.21875
- left_basis: float32 [2, 512, 128, 128], P('tensor', 'dp'), may hold values from -0.5 to 0.5
- right_basis: float32 [2, 512, 128, 128], P('tensor', 'dp'), may hold values from -0.5 to 0.5
- mom_slots: float32 [2, 512, 128, 128], P('tensor', 'dp')
- var_slots: float32 [2, 512, 128, 128], P('tensor', 'dp'), as said below
- vec_master: float32 [2, 14336], P('tensor', 'dp')
- vec_mom: float32 [2, 14336], P('tensor', 'dp')
- vec_var: float32 [2, 14336], P('tensor', 'dp'), as said below
Outputs:
- output: float32 [16384, 768], P('dp')
- patch_grad: float32 [16384, 768], P('dp', 'tensor')
- grad_slots: float32 [2, 512, 128, 128], P('tensor', 'dp')
- new_master: float32 [2, 512, 128, 128], P('tensor', 'dp')
- new_mom: float32 [2, 512, 128, 128], P('tensor', 'dp')
- new_var: float32 [2, 512, 128, 128], P('tensor', 'dp')
- grad_vec: float32 [2, 14336], P('tensor', 'dp')
- new_vec: float32 [2, 14336], P('tensor', 'dp')
- new_vec_mom: float32 [2, 14336], P('tensor', 'dp')
- new_vec_var: float32 [2, 14336], P('tensor', 'dp')
The draws below stay inside these ranges and needn't reach their ends.
Inputs may be any that keep to these rules, and one draw needn't show every extreme that they name: `image_size`: each row lists the size classes of one index of dp's images in order; class 3 (no image) stands only after the others. A row's images hold at most 997 tokens, and some row holds exactly that many in every draw. `block_slot`: each row names 504 different slots; slot s belongs to index s // 32 of dp, and the slots 0 and 511 are always named. `var_slots`: Positive. `vec_var`: Positive.
All inputs are finite; a program needn't handle non-finite values.
Results may differ from the reference program's by a relative error of at most 0.04.
Values may be sent and summed in bfloat16 or wider, within the bound.
No kernel may reach another device: no remote copies, remote signals or barrier semaphores. Data moves between devices by JAX's collectives and lax.ppermute only.
A program may use at most 256 MiB of HBM per device.

```python
import jax
import jax.numpy as jnp
import numpy as np
from jax import lax

D = 768
HEAD_DIM = 64
FF = 3072
BASE_PIX = 3072
PIX = 768
LAYERS = 2
TOK_DEV = 1024
LEN_A = 196
LEN_B = 225
LEN_C = 576
IMG_DEV = 5
BS = 128
QBLK = 512
TOKENS = 16384
BLOCKS = 504
SLOTS = 512
VECS = 14336
N_DP = 16
N_TENSOR = 2


def draw_image_size(key, part):
    combos = jnp.array([[2, 1, 0, 3, 3], [1, 1, 1, 1, 3], [0, 0, 0, 0, 0], [2, 0, 0, 3, 3], [1, 1, 1, 0, 3], [1, 1, 0, 0, 3], [2, 1, 3, 3, 3]], dtype=jnp.int32)
    picked = jax.random.randint(jax.random.fold_in(key, 1), (N_DP,), 0, 7)
    fullest = jax.random.randint(jax.random.fold_in(key, 2), (), 0, N_DP)
    picked = jnp.where(jnp.arange(N_DP) == fullest, 0, picked)
    return combos[picked]


def slot_rows(key):
    row_list = []
    for tensor_idx in range(N_TENSOR):
        subkey = jax.random.fold_in(key, 10 + tensor_idx)
        middle = jax.random.permutation(jax.random.fold_in(subkey, 1), SLOTS - 2)[:BLOCKS - 2] + 1
        chosen = jnp.concatenate([jnp.array([0, SLOTS - 1], jnp.int32), middle.astype(jnp.int32)])
        shuffle = jax.random.permutation(jax.random.fold_in(subkey, 2), BLOCKS)
        row_list.append(chosen[shuffle])
    return jnp.stack(row_list)


def draw_block_slot(key, part):
    return slot_rows(key)


def grad_base_size():
    return (0.9 * TOKENS) ** 0.5


def tile_scales():
    part_d = D // N_TENSOR
    part_ff = FF // N_TENSOR
    attend_size = LEN_B ** (-0.5)
    pieces = [np.full(BASE_PIX // BS * (part_d // BS), 0.75)]
    for layer_idx in range(LAYERS):
        pieces.append(np.full(D // BS * (3 * part_d // BS), attend_size))
        pieces.append(np.full(part_d // BS * (D // BS), (0.09 + attend_size * attend_size) ** 0.5))
        pieces.append(np.full(D // BS * (part_ff // BS), 0.55))
        pieces.append(np.full(part_ff // BS * (D // BS), 0.8))
    return np.concatenate(pieces).astype(np.float32) * grad_base_size()


def slot_scale(key):
    rows = slot_rows(key)
    tiles = jnp.asarray(tile_scales())
    scale_list = []
    for tensor_idx in range(N_TENSOR):
        filled = jnp.full((SLOTS,), grad_base_size(), jnp.float32).at[rows[tensor_idx]].set(tiles)
        scale_list.append(filled)
    return jnp.stack(scale_list)


def draw_mom_slots(key, part):
    scale = slot_scale(key)[:, :, None, None]
    noise = jnp.clip(jax.random.normal(jax.random.fold_in(key, 31), (N_TENSOR, SLOTS, BS, BS), jnp.float32), -4.0, 4.0)
    return scale * noise


def draw_var_slots(key, part):
    scale = slot_scale(key)[:, :, None, None]
    factor = jnp.exp(jax.random.uniform(jax.random.fold_in(key, 32), (N_TENSOR, SLOTS, BS, BS), jnp.float32, 0.0, float(np.log(4.0))))
    return scale * scale * factor


def vector_scales():
    part_d = D // N_TENSOR
    part_ff = FF // N_TENSOR
    attend_size = LEN_B ** (-0.5)
    pieces = [np.full(part_d, 1.5)]
    for layer_idx in range(LAYERS):
        pieces += [np.full(D, 1.2 * attend_size), np.full(D, 1.2 * attend_size), np.full(part_d, attend_size), np.full(part_d, attend_size), np.full(D, 1.0), np.full(D, 0.7), np.full(D, 0.7), np.full(part_ff, 0.55), np.full(D, 1.0)]
    joined = np.concatenate(pieces)
    joined = np.concatenate([joined, np.ones(VECS - joined.shape[0])])
    return jnp.asarray(joined.astype(np.float32) * grad_base_size())[None, :]


def draw_vec_mom(key, part):
    noise = jnp.clip(jax.random.normal(jax.random.fold_in(key, 41), (N_TENSOR, VECS), jnp.float32), -4.0, 4.0)
    return vector_scales() * noise


def draw_vec_var(key, part):
    scale = vector_scales()
    factor = jnp.exp(jax.random.uniform(jax.random.fold_in(key, 42), (N_TENSOR, VECS), jnp.float32, 0.0, float(np.log(4.0))))
    return scale * scale * factor


def draw_vec_master(key, part):
    part_d = D // N_TENSOR
    part_ff = FF // N_TENSOR
    lengths = [part_d]
    flags = [0]
    for layer_idx in range(LAYERS):
        lengths += [D, D, part_d, part_d, D, D, D, part_ff, D]
        flags += [1, 0, 0, 0, 0, 1, 0, 0, 0]
    marks = np.concatenate([np.full(length, flag, dtype=np.int32) for length, flag in zip(lengths, flags)])
    marks = np.concatenate([marks, np.zeros(VECS - marks.shape[0], dtype=np.int32)])
    gain_mask = jnp.asarray(marks)[None, :] == 1
    gain_vals = jax.random.uniform(jax.random.fold_in(key, 1), (N_TENSOR, VECS), jnp.float32, 0.5, 1.5)
    bias_vals = 0.3 * jax.random.normal(jax.random.fold_in(key, 2), (N_TENSOR, VECS), jnp.float32)
    return jnp.where(gain_mask, gain_vals, bias_vals)


def level_of(rng, shape, cuts, smallest, high):
    def one(position, blocks):
        draws = jax.random.uniform(jax.random.fold_in(jax.random.fold_in(rng, 6), position), (blocks,), jnp.float32, smallest / len(cuts), high / len(cuts))
        return jnp.repeat(jnp.exp(draws), shape[position] // blocks).reshape((-1,) + (1,) * (len(shape) - position - 1))

    factor_of = one(*cuts[0])
    for cut in cuts[1:]:
        factor_of = factor_of * one(*cut)
    return factor_of


def bell_draw(rng, extent, deviation, reach, cuts=(), kind=jnp.bfloat16):
    values = deviation * jax.random.normal(rng, extent, jnp.float32)
    if cuts:
        values = values * level_of(rng, extent, cuts, -0.22, 0.18)
    return jnp.clip(values, -reach, reach).astype(kind)


def setup_inputs(seed: int = 0) -> dict:
    seeds = jax.random.split(jax.random.key(seed), 14)
    return {
        "patches": bell_draw(seeds[0], (TOKENS, PIX), 1.0, 6.0, ((0, 16),)),
        "cotangent": bell_draw(seeds[1], (TOKENS, D), 1.0, 6.0, ((0, 16),)),
        "image_size": draw_image_size(jax.random.fold_in(seeds[13], 71), 0),
        "block_slot": draw_block_slot(jax.random.fold_in(seeds[13], 71), 0),
        "pinv": bell_draw(seeds[4], (3, BASE_PIX, PIX), BASE_PIX ** -0.5, 0.109375),
        "master_slots": bell_draw(seeds[5], (N_TENSOR, SLOTS, BS, BS), D ** -0.5, 0.21875, ((0, 2), (1, 16)), jnp.float32),
        "left_basis": bell_draw(seeds[6], (N_TENSOR, SLOTS, BS, BS), BS ** -0.5, 0.5, ((0, 2), (1, 16)), jnp.float32),
        "right_basis": bell_draw(seeds[7], (N_TENSOR, SLOTS, BS, BS), BS ** -0.5, 0.5, ((0, 2), (1, 16)), jnp.float32),
        "mom_slots": draw_mom_slots(jax.random.fold_in(seeds[13], 71), 0),
        "var_slots": draw_var_slots(jax.random.fold_in(seeds[13], 71), 0),
        "vec_master": draw_vec_master(jax.random.fold_in(seeds[13], 71), 0),
        "vec_mom": draw_vec_mom(jax.random.fold_in(seeds[13], 71), 0),
        "vec_var": draw_vec_var(jax.random.fold_in(seeds[13], 71), 0),
    }


precise = lax.Precision.HIGHEST
masked_score = -1e+30
norm_eps = 1e-06
adam_eps = 1e-08
decay = 0.5
matrix_rate = 0.05
vector_rate = 0.3

@jax.custom_vjp
def low(v):
    return lax.optimization_barrier(v.astype(jnp.bfloat16)).astype(jnp.float32)

@jax.custom_vjp
def low_back(v):
    return v

def low_keep(v):
    return (low(v), None)

def low_pass(kept, grad):
    return (grad,)

def back_keep(v):
    return (v, None)

def back_low(kept, grad):
    return (low(grad),)
low.defvjp(low_keep, low_pass)
low_back.defvjp(back_keep, back_low)

def layer_norm(values, gain_vec, shift_vec):
    mean_val = lax.optimization_barrier(jnp.mean(values, axis=-1, keepdims=True))
    centered = values - mean_val
    inv_std = lax.rsqrt(lax.optimization_barrier(jnp.mean(centered * centered, axis=-1, keepdims=True)) + norm_eps)
    return centered * inv_std * gain_vec + shift_vec

def matrix_shapes(part_d, part_ff):
    shapes = [(BASE_PIX, part_d)]
    for layer_idx in range(LAYERS):
        shapes += [(D, 3 * part_d), (part_d, D), (D, part_ff), (part_ff, D)]
    return shapes

def from_tiles(tile_rows, shapes):
    matrices = []
    offset = 0
    for rows_n, cols_n in shapes:
        tile_count = rows_n // BS * (cols_n // BS)
        tile_block = tile_rows[offset:offset + tile_count]
        matrices.append(tile_block.reshape(rows_n // BS, cols_n // BS, BS, BS).transpose(0, 2, 1, 3).reshape(rows_n, cols_n))
        offset += tile_count
    return matrices

def to_tiles(matrix):
    rows_n, cols_n = matrix.shape
    return matrix.reshape(rows_n // BS, BS, cols_n // BS, BS).transpose(0, 2, 1, 3).reshape(-1, BS, BS)

def vector_lengths(part_d, part_ff):
    lengths = [part_d]
    for layer_idx in range(LAYERS):
        lengths += [D, D, part_d, part_d, D, D, D, part_ff, D]
    return lengths

def split_vector(vector, part_d, part_ff):
    pieces = []
    offset = 0
    for length in vector_lengths(part_d, part_ff):
        pieces.append(vector[offset:offset + length])
        offset += length
    return (pieces[0], [pieces[1 + 9 * layer_idx:10 + 9 * layer_idx] for layer_idx in range(LAYERS)])

def token_meta(size_row):
    lengths = jnp.where(size_row == 0, LEN_A, jnp.where(size_row == 1, LEN_B, jnp.where(size_row == 2, LEN_C, 0)))
    ends_at = jnp.cumsum(lengths)
    places = jnp.arange(TOK_DEV)
    segment = lax.optimization_barrier(jnp.sum((places[:, None] >= ends_at[None, :]).astype(jnp.int32), axis=1))
    onehot = (segment[:, None] == jnp.arange(IMG_DEV)[None, :]).astype(jnp.int32)
    size_class = lax.optimization_barrier(jnp.sum(onehot * size_row[None, :], axis=1)) + 3 * (segment == IMG_DEV).astype(jnp.int32)
    valid_rows = (segment < IMG_DEV).astype(jnp.float32)
    return (segment, size_class, valid_rows)

def attention(queries, key_rows, value_rows, segment):
    heads_here = queries.shape[1] // HEAD_DIM
    key_heads = key_rows.reshape(TOK_DEV, heads_here, HEAD_DIM)
    value_heads = value_rows.reshape(TOK_DEV, heads_here, HEAD_DIM)
    score_scale = HEAD_DIM ** (-0.5)

    def one_block(inputs):
        query_blk, seg_blk = inputs
        scores = jnp.einsum('qhd,khd->hqk', query_blk, key_heads, precision=precise) * score_scale
        scores = low_back(scores)
        allowed = seg_blk[:, None] == segment[None, :]
        scores = jnp.where(allowed[None, :, :], scores, masked_score)
        weights_p = low(jax.nn.softmax(scores, axis=-1))
        mixed_blk = jnp.einsum('hqk,khd->qhd', weights_p, value_heads, precision=precise)
        return mixed_blk.reshape(QBLK, heads_here * HEAD_DIM)
    blocks_n = TOK_DEV // QBLK
    mixed = lax.map(jax.checkpoint(one_block), (queries.reshape(blocks_n, QBLK, heads_here, HEAD_DIM), segment.reshape(blocks_n, QBLK)))
    return mixed.reshape(TOK_DEV, heads_here * HEAD_DIM)

def forward(weights, vectors, pinv_f, patch_rows, segment, size_class):
    part_d = D // N_TENSOR
    part_ff = FF // N_TENSOR
    embedded_parts = []
    for tensor_idx in range(N_TENSOR):
        base = low(weights[tensor_idx][0])
        emb_bias = split_vector(vectors[tensor_idx], part_d, part_ff)[0]
        embedded = jnp.zeros((TOK_DEV, part_d), jnp.float32)
        for size_idx in range(3):
            resized = low(low_back(jnp.dot(pinv_f[size_idx].T, base, precision=precise)))
            chosen = (size_class == size_idx).astype(jnp.float32)[:, None]
            embedded = embedded + chosen * jnp.dot(patch_rows, resized, precision=precise)
        embedded_parts.append(low(low_back(embedded + emb_bias)))
    hidden = jnp.concatenate(embedded_parts, axis=1)
    for layer_idx in range(LAYERS):
        attn_total = 0.0
        for tensor_idx in range(N_TENSOR):
            own_mats = weights[tensor_idx]
            layer_vecs = split_vector(vectors[tensor_idx], part_d, part_ff)[1][layer_idx]
            gain_one, shift_one, bias_q, bias_v, bias_out = layer_vecs[0:5]
            normed = low(layer_norm(hidden, gain_one, shift_one))
            projected = jnp.dot(normed, low(own_mats[1 + 4 * layer_idx]), precision=precise)
            queries = low(low_back(projected[:, :part_d] + bias_q))
            key_rows = low(low_back(projected[:, part_d:2 * part_d]))
            value_rows = low(low_back(projected[:, 2 * part_d:] + bias_v))
            mixed = low(low_back(attention(queries, key_rows, value_rows, segment)))
            partial_value = jnp.dot(mixed, low(own_mats[2 + 4 * layer_idx]), precision=precise) + bias_out
            attn_total = attn_total + low(low_back(partial_value))
        hidden = hidden + attn_total
        mlp_total = 0.0
        for tensor_idx in range(N_TENSOR):
            own_mats = weights[tensor_idx]
            layer_vecs = split_vector(vectors[tensor_idx], part_d, part_ff)[1][layer_idx]
            gain_two, shift_two, bias_up, bias_down = layer_vecs[5:9]
            normed = low(layer_norm(hidden, gain_two, shift_two))
            up_proj = low_back(jnp.dot(normed, low(own_mats[3 + 4 * layer_idx]), precision=precise) + bias_up)
            activated = low(jax.nn.gelu(up_proj, approximate=False))
            partial_value = jnp.dot(activated, low(own_mats[4 + 4 * layer_idx]), precision=precise) + bias_down
            mlp_total = mlp_total + low(low_back(partial_value))
        hidden = hidden + mlp_total
    return hidden

def rotate_step(master, grads, left, right, moment, variance):
    rotated = jnp.einsum('sji,sjk->sik', left, grads, precision=precise)
    rotated = jnp.einsum('sik,skl->sil', rotated, right, precision=precise)
    new_moment = decay * moment + (1.0 - decay) * rotated
    new_variance = decay * variance + (1.0 - decay) * rotated * rotated
    step_rot = new_moment / (jnp.sqrt(new_variance) + adam_eps)
    returned = jnp.einsum('sij,sjk->sik', left, step_rot, precision=precise)
    returned = jnp.einsum('sik,slk->sil', returned, right, precision=precise)
    return (master - matrix_rate * returned, new_moment, new_variance)

def reference(patches, cotangent, image_size, block_slot, pinv, master_slots, left_basis, right_basis, mom_slots, var_slots, vec_master, vec_mom, vec_var):
    part_d = D // N_TENSOR
    part_ff = FF // N_TENSOR
    shapes = matrix_shapes(part_d, part_ff)
    weights = []
    vectors = []
    for tensor_idx in range(N_TENSOR):
        tile_rows = jnp.take(master_slots[tensor_idx], block_slot[tensor_idx], axis=0)
        weights.append(from_tiles(tile_rows, shapes))
        vectors.append(vec_master[tensor_idx])
    pinv_f = pinv.astype(jnp.float32)
    patch_groups = patches.astype(jnp.float32).reshape(N_DP, TOK_DEV, PIX)
    cot_groups = cotangent.astype(jnp.float32).reshape(N_DP, TOK_DEV, D)

    def group_step(carried, inputs):
        patch_rows, cot_rows, size_row = inputs
        segment, size_class, valid_rows = token_meta(size_row)

        def run(weight_sets, vector_sets, rows_in):
            return forward(weight_sets, vector_sets, pinv_f, rows_in, segment, size_class)
        result, pullback = jax.vjp(run, weights, vectors, patch_rows)
        grad_w, grad_v, grad_x = pullback(cot_rows * valid_rows[:, None])
        carried = jax.tree.map(lambda first, second: first + second, carried, (grad_w, grad_v))
        return (carried, (result * valid_rows[:, None], grad_x * valid_rows[:, None]))
    zeroed = jax.tree.map(jnp.zeros_like, (weights, vectors))
    (grad_w, grad_v), (results, grad_x) = lax.scan(group_step, zeroed, (patch_groups, cot_groups, image_size))
    grad_list = []
    for tensor_idx in range(N_TENSOR):
        tiles_all = jnp.concatenate([to_tiles(matrix) for matrix in grad_w[tensor_idx]], axis=0)
        grad_list.append(jnp.zeros((SLOTS, BS, BS), jnp.float32).at[block_slot[tensor_idx]].set(tiles_all))
    grad_slots = jnp.stack(grad_list)
    grad_vec = jnp.stack(grad_v)
    new_master, new_mom, new_var = rotate_step(master_slots.reshape(-1, BS, BS), grad_slots.reshape(-1, BS, BS), left_basis.reshape(-1, BS, BS), right_basis.reshape(-1, BS, BS), mom_slots.reshape(-1, BS, BS), var_slots.reshape(-1, BS, BS))
    new_master = new_master.reshape(N_TENSOR, SLOTS, BS, BS)
    new_mom = new_mom.reshape(N_TENSOR, SLOTS, BS, BS)
    new_var = new_var.reshape(N_TENSOR, SLOTS, BS, BS)
    new_vec_mom = decay * vec_mom + (1.0 - decay) * grad_vec
    new_vec_var = decay * vec_var + (1.0 - decay) * grad_vec * grad_vec
    new_vec = vec_master - vector_rate * new_vec_mom / (jnp.sqrt(new_vec_var) + adam_eps)
    output = results.reshape(TOKENS, D)
    patch_grad = grad_x.reshape(TOKENS, PIX)
    return (output, patch_grad, grad_slots, new_master, new_mom, new_var, grad_vec, new_vec, new_vec_mom, new_vec_var)
```

```python
import functools

import jax
import jax.numpy as jnp
import numpy as np
from jax import lax
from jax.experimental import pallas as pl
from jax.experimental.pallas import tpu as pltpu
from jax.sharding import PartitionSpec as P

D = 768
HEAD_DIM = 64
FF = 3072
BASE_PIX = 3072
LAYERS = 2
LEN_A = 196
LEN_B = 225
LEN_C = 576
IMG_DEV = 5
BS = 128
TENSOR = 2
HALF = D // TENSOR
HALF_FF = FF // TENSOR
HEADS = HALF // HEAD_DIM
ROWS = 256
VEC_ROWS = 16

AXES = ("dp", "tensor")
precise = lax.Precision.HIGHEST
masked_score = -1e30
norm_eps = 1e-06
adam_eps = 1e-08
decay = 0.5
matrix_rate = 0.05
vector_rate = 0.3
f32 = jnp.float32
bf16 = jnp.bfloat16
BIG_VMEM = 56 * 1024 * 1024

PANELS = {
    "up": (0, 6144),
    "down": (3072, 9216),
    "base": 12288,
    "out": (15360, 20736),
    "qkv": (16128, 18432),
}
PANEL_ROWS = 21504


def tile_targets():
    rows, cols = [], []

    def add(start, rows_n, cols_n):
        for i in range(rows_n // BS):
            for j in range(cols_n // BS):
                panel, inner = divmod(j * BS, HALF)
                rows.append(start + panel * rows_n + i * BS)
                cols.append(inner)

    add(PANELS["base"], BASE_PIX, HALF)
    for layer in range(LAYERS):
        add(PANELS["qkv"][layer], D, 3 * HALF)
        add(PANELS["out"][layer], HALF, D)
        add(PANELS["up"][layer], D, HALF_FF)
        add(PANELS["down"][layer], HALF_FF, D)
    return np.array(rows, np.int32), np.array(cols, np.int32)


TARGET_ROW, TARGET_COL = tile_targets()
LAYER_VECS = (D, D, HALF, HALF, D, D, D, HALF_FF, D)
VEC_NAMES = ("g1", "s1", "bq", "bv", "bo", "g2", "s2", "b1", "b2")


def vec_offsets():
    offset = HALF
    found = []
    for layer in range(LAYERS):
        here = {}
        for name, length in zip(VEC_NAMES, LAYER_VECS):
            here[name] = (offset, length)
            offset += length
        found.append(here)
    return found


VEC_AT = vec_offsets()


def params(limit=BIG_VMEM):
    return pltpu.CompilerParams(
        dimension_semantics=("arbitrary",), vmem_limit_bytes=limit
    )


def cost(flops, nbytes, trans=0):
    return pl.CostEstimate(flops=flops, bytes_accessed=nbytes, transcendentals=trans)


def rows_spec(width):
    return pl.BlockSpec((ROWS, width), lambda i, *_: (i, 0))


def fixed(shape, at=0):
    return pl.BlockSpec(shape, lambda i, *_: (at,) + (0,) * (len(shape) - 1))


def vec_piece(vec_ref, layer, name):
    start, length = VEC_AT[layer][name]
    return vec_ref[:, start : start + length]


def dot(left, right):
    return jnp.dot(left, right, preferred_element_type=f32)


def dot_nt(left, right, precision=None):
    return lax.dot_general(
        left, right, (((1,), (1,)), ((), ())), precision=precision, preferred_element_type=f32
    )


def dot_tn(left, right):
    return lax.dot_general(left, right, (((0,), (0,)), ((), ())), preferred_element_type=f32)


def norm_stats(values):
    mean_val = jnp.mean(values, axis=-1, keepdims=True)
    centered = values - mean_val
    inv_std = lax.rsqrt(jnp.mean(centered * centered, axis=-1, keepdims=True) + norm_eps)
    return centered * inv_std, inv_std


def norm_back(values, gain, grad):
    unit, inv_std = norm_stats(values)
    scaled = grad * gain
    mean_s = jnp.mean(scaled, axis=-1, keepdims=True)
    mean_u = jnp.mean(scaled * unit, axis=-1, keepdims=True)
    back = inv_std * (scaled - mean_s - unit * mean_u)
    return (
        back,
        jnp.sum(grad * unit, axis=0, keepdims=True),
        jnp.sum(grad, axis=0, keepdims=True),
    )


def accumulate(ref, value):
    first = pl.program_id(0) == 0

    @pl.when(first)
    def _():
        ref[...] = value

    @pl.when(jnp.logical_not(first))
    def _():
        ref[...] += value


def fence(*arrays):
    def nothing(*refs):
        pass

    anywhere = pl.BlockSpec(memory_space=pl.ANY)
    return pl.pallas_call(
        nothing,
        out_shape=[jax.ShapeDtypeStruct(a.shape, a.dtype) for a in arrays],
        in_specs=[anywhere] * len(arrays),
        out_specs=[anywhere] * len(arrays),
        input_output_aliases={i: i for i in range(len(arrays))},
    )(*arrays)


def gather_kernel(slots, count_a, count_b, owner, drow, dcol, flag, *refs):
    first = refs[:count_a]
    second = refs[count_a : count_a + count_b]
    panels, vectors, held, sem, vec_sem = refs[count_a + count_b :]

    def copy_all(sources):
        at = 0
        for src in sources:
            for n in range(src.shape[0]):
                who = owner[at]
                at += 1

                def body(i, carried, src=src, n=n, who=who):
                    slot = who * slots + i
                    row = drow[slot]

                    @pl.when(row >= 0)
                    def _():
                        start = pl.multiple_of(i * BS, BS)
                        pltpu.make_async_copy(
                            src.at[n, pl.ds(start, BS), :],
                            held.at[
                                pl.ds(pl.multiple_of(row, BS), BS),
                                pl.ds(pl.multiple_of(dcol[slot], BS), BS),
                            ],
                            sem,
                        ).start()

                    return carried

                lax.fori_loop(0, slots, body, 0)
                pltpu.make_async_copy(
                    src.at[n, pl.ds(slots * BS, VEC_ROWS), :], vectors.at[who], vec_sem
                ).start()

    if count_b:

        @pl.when(flag[0] == 1)
        def _():
            copy_all(first)

        @pl.when(flag[0] == 0)
        def _():
            copy_all(second)
    else:
        copy_all(first)
    pltpu.make_async_copy(held, held, sem).wait()
    out = pltpu.make_async_copy(held, panels, sem)
    out.start()
    pltpu.make_async_copy(vectors, vectors, vec_sem).wait()
    out.wait()


def gather_tiles(first, second, owner, drow, dcol, flag, slots, owners):
    anywhere = pl.BlockSpec(memory_space=pl.ANY)
    return pl.pallas_call(
        functools.partial(gather_kernel, slots, len(first), len(second)),
        out_shape=(
            jax.ShapeDtypeStruct((PANEL_ROWS, HALF), bf16),
            jax.ShapeDtypeStruct((owners, VEC_ROWS, BS), bf16),
        ),
        grid_spec=pltpu.PrefetchScalarGridSpec(
            num_scalar_prefetch=4,
            grid=(1,),
            in_specs=[anywhere] * (len(first) + len(second)),
            out_specs=(anywhere, fixed((owners, VEC_ROWS, BS))),
            scratch_shapes=[
                pltpu.VMEM((PANEL_ROWS, HALF), bf16),
                pltpu.SemaphoreType.DMA,
                pltpu.SemaphoreType.DMA,
            ],
        ),
        compiler_params=params(),
        cost_estimate=cost(0, 4 * PANEL_ROWS * HALF),
    )(owner, drow, dcol, flag, *first, *second)


def scatter_kernel(rows_n, cols_n, paired, parts, pos, part, own, *refs):
    if paired:
        recv, *refs = refs
        span = pl.num_programs(0) // parts
        here = jnp.logical_or(parts == 1, pl.program_id(0) // span == part[0])
    target, buf, sems = refs[-3:]
    step = pl.program_id(0)
    slot = lax.rem(step, 2)
    per = rows_n // BS * (cols_n // BS)

    def wait(at):
        pltpu.make_async_copy(buf.at[at], buf.at[at], sems.at[at]).wait()

    @pl.when(step >= 2)
    def _():
        wait(slot)

    for i in range(rows_n // BS):
        for j in range(cols_n // BS):
            area = (slice(i * BS, (i + 1) * BS), slice(j * BS, (j + 1) * BS))
            value = own[area]
            if paired:
                more = jnp.where(here, recv[area].astype(f32), 0.0)
                value = (value.astype(f32) + more).astype(bf16)
            buf[slot, i * (cols_n // BS) + j] = value
    for n in range(per):
        pltpu.make_async_copy(
            buf.at[slot, n],
            target.at[pl.ds(pl.multiple_of(pos[step * per + n], 16), BS), :],
            sems.at[slot],
        ).start()

    @pl.when(step == pl.num_programs(0) - 1)
    def _():
        wait(1 - slot)
        wait(slot)


def scatter_matrix(pos, own, recv, part, target, total_rows, rows_n):
    cols_n = own.shape[1]
    steps = own.shape[0] // rows_n
    anywhere = pl.BlockSpec(memory_space=pl.ANY)
    block = pl.BlockSpec((rows_n, cols_n), lambda i, *_: (i, 0))
    paired = recv is not None
    parts = own.shape[0] // recv.shape[0] if paired else 1
    span = steps // parts
    arrived = pl.BlockSpec(
        (rows_n, cols_n), lambda i, pos, part: (jnp.clip(i - part[0] * span, 0, span - 1), 0)
    )
    operands = [own] + ([recv] if paired else []) + ([] if target is None else [target])
    specs = [block] + ([block if parts == 1 else arrived] if paired else [])
    specs += [] if target is None else [anywhere]
    return pl.pallas_call(
        functools.partial(scatter_kernel, rows_n, cols_n, paired, parts),
        out_shape=jax.ShapeDtypeStruct((total_rows, BS), bf16),
        grid_spec=pltpu.PrefetchScalarGridSpec(
            num_scalar_prefetch=2,
            grid=(steps,),
            in_specs=specs,
            out_specs=anywhere,
            scratch_shapes=[
                pltpu.VMEM((2, rows_n // BS * (cols_n // BS), BS, BS), bf16),
                pltpu.SemaphoreType.DMA((2,)),
            ],
        ),
        input_output_aliases={} if target is None else {len(operands) + 1: 0},
        compiler_params=params(),
        cost_estimate=cost(own.size, own.size * 6),
    )(pos, part, *operands)


def scatter_vec_kernel(paired, pos, own, *refs):
    if paired:
        recv, *refs = refs
    target, buf, sem = refs[-3:]
    value = own[...]
    if paired:
        value = (value.astype(f32) + recv[...].astype(f32)).astype(bf16)
    buf[...] = value

    def body(n, carried):
        pltpu.make_async_copy(
            buf.at[n], target.at[pl.ds(pl.multiple_of(pos[n], 16), VEC_ROWS), :], sem
        ).start()
        return carried

    lax.fori_loop(0, own.shape[0], body, 0)
    pltpu.make_async_copy(buf, buf, sem).wait()


def scatter_vec(pos, own, recv, target):
    anywhere = pl.BlockSpec(memory_space=pl.ANY)
    block = fixed(own.shape)
    paired = recv is not None
    operands = [own] + ([recv] if paired else []) + [target]
    return pl.pallas_call(
        functools.partial(scatter_vec_kernel, paired),
        out_shape=jax.ShapeDtypeStruct(target.shape, bf16),
        grid_spec=pltpu.PrefetchScalarGridSpec(
            num_scalar_prefetch=1,
            grid=(1,),
            in_specs=[block] * (len(operands) - 1) + [anywhere],
            out_specs=anywhere,
            scratch_shapes=[pltpu.VMEM(own.shape, bf16), pltpu.SemaphoreType.DMA],
        ),
        input_output_aliases={len(operands): 0},
        compiler_params=params(),
    )(pos, *operands)


def qkv_kernel(layer, summed, *refs):
    if summed:
        base, own, recv, vec, weight, hid, normed, q_ref, k_ref, v_ref = refs
        values = base[...] + (own[...].astype(f32) + recv[...].astype(f32))
        hid[...] = values
    else:
        base, vec, weight, normed, q_ref, k_ref, v_ref = refs
        values = base[...]
    unit, unused = norm_stats(values)
    low = (unit * vec_piece(vec, layer, "g1") + vec_piece(vec, layer, "s1")).astype(bf16)
    normed[...] = low
    q_ref[...] = (dot(low, weight[0:D, :]) + vec_piece(vec, layer, "bq")).astype(bf16)
    k_ref[...] = dot(low, weight[D : 2 * D, :]).astype(bf16)
    v_ref[...] = (dot(low, weight[2 * D : 3 * D, :]) + vec_piece(vec, layer, "bv")).astype(bf16)


def qkv_call(layer, base, own, recv, vec, panels):
    tokens = base.shape[0]
    summed = own is not None
    shape = lambda width, kind: jax.ShapeDtypeStruct((tokens, width), kind)
    outs = ([shape(D, f32)] if summed else []) + [shape(D, bf16)] + [shape(HALF, bf16)] * 3
    operands = [base] + ([own, recv] if summed else []) + [vec, panels]
    return pl.pallas_call(
        functools.partial(qkv_kernel, layer, summed),
        out_shape=outs,
        grid=(tokens // ROWS,),
        in_specs=[rows_spec(D)] * (3 if summed else 1)
        + [fixed(vec.shape), fixed((3 * D, HALF), PANELS["qkv"][layer] // (3 * D))],
        out_specs=[rows_spec(o.shape[1]) for o in outs],
        compiler_params=params(),
        cost_estimate=cost(2 * tokens * D * 3 * HALF, tokens * D * 14),
    )(*operands)


def head_masks():
    lane = lax.broadcasted_iota(jnp.int32, (1, 2 * HEAD_DIM), 1)
    low = (lane < HEAD_DIM).astype(f32).astype(bf16)
    high = (lane >= HEAD_DIM).astype(f32).astype(bf16)
    return low, high


def attend_kernel(layer, q_ref, k_ref, v_ref, seg_q, seg_k, vec, w_out, o_ref, lse_ref, part):
    masks = head_masks()
    same = seg_q[...] == seg_k[...]
    lane = lax.broadcasted_iota(jnp.int32, (ROWS, BS), 1)
    totals = jnp.zeros((ROWS, BS), f32)
    scale = jnp.asarray(HEAD_DIM ** (-0.5), bf16)
    for pair in range(HEADS // 2):
        cols = slice(pair * BS, (pair + 1) * BS)
        q_two = q_ref[:, cols] * scale
        k_two = k_ref[:, cols]
        v_two = v_ref[:, cols]
        mixed = None
        for side in range(2):
            scores = dot_nt(q_two * masks[side], k_two)
            scores = jnp.where(same, scores, masked_score)
            top = jnp.max(scores, axis=1, keepdims=True)
            expo = jnp.exp(scores - top)
            total = jnp.sum(expo, axis=1, keepdims=True)
            weights = (expo * (1.0 / total)).astype(bf16)
            term = dot(weights, v_two * masks[side])
            mixed = term if mixed is None else mixed + term
            totals = jnp.where(lane == 2 * pair + side, top + jnp.log(total), totals)
        o_ref[:, cols] = mixed.astype(bf16)
    lse_ref[...] = totals.T[0:8, :]
    low = o_ref[...]
    bias = vec_piece(vec, layer, "bo")
    for panel in range(TENSOR):
        area = slice(panel * HALF, (panel + 1) * HALF)
        part[:, area] = (dot(low, w_out[area, :]) + bias[:, area]).astype(bf16)


def attend_call(layer, queries, keys, values, seg_col, seg_row, vec, panels):
    tokens = queries.shape[0]
    return pl.pallas_call(
        functools.partial(attend_kernel, layer),
        out_shape=[
            jax.ShapeDtypeStruct((tokens, HALF), bf16),
            jax.ShapeDtypeStruct((8, tokens), f32),
            jax.ShapeDtypeStruct((tokens, D), bf16),
        ],
        grid=(tokens // ROWS,),
        in_specs=[
            rows_spec(HALF),
            fixed(keys.shape),
            fixed(values.shape),
            rows_spec(1),
            fixed(seg_row.shape),
            fixed(vec.shape),
            fixed((D, HALF), PANELS["out"][layer] // D),
        ],
        out_specs=[
            rows_spec(HALF),
            pl.BlockSpec((8, ROWS), lambda i: (0, i)),
            rows_spec(D),
        ],
        compiler_params=params(),
        cost_estimate=cost(8 * HEADS * tokens * tokens * BS, tokens * D * 8, HEADS * tokens * tokens),
    )(queries, keys, values, seg_col, seg_row, vec, panels)


def gelu_parts(values):
    cdf = 0.5 * (1.0 + lax.erf(values * 0.7071067811865476))
    pdf = 0.3989422804014327 * jnp.exp(-0.5 * values * values)
    return values * cdf, cdf + values * pdf


def mlp_kernel(layer, base, own, recv, vec, w_up, w_down, hid, normed, act, slope, part):
    values = base[...] + (own[...].astype(f32) + recv[...].astype(f32))
    hid[...] = values
    unit, unused = norm_stats(values)
    low = (unit * vec_piece(vec, layer, "g2") + vec_piece(vec, layer, "s2")).astype(bf16)
    normed[...] = low
    bias_up = vec_piece(vec, layer, "b1")
    for panel in range(HALF_FF // HALF):
        area = slice(panel * HALF, (panel + 1) * HALF)
        up = dot(low, w_up[panel * D : (panel + 1) * D, :]) + bias_up[:, area]
        gelu, grad = gelu_parts(up)
        act[:, area] = gelu.astype(bf16)
        slope[:, area] = grad.astype(bf16)
    bias_down = vec_piece(vec, layer, "b2")
    hidden_units = act[...]
    for panel in range(TENSOR):
        area = slice(panel * HALF, (panel + 1) * HALF)
        down = dot(hidden_units, w_down[panel * HALF_FF : (panel + 1) * HALF_FF, :])
        part[:, area] = (down + bias_down[:, area]).astype(bf16)


def mlp_call(layer, base, own, recv, vec, panels):
    tokens = base.shape[0]
    shape = lambda width, kind: jax.ShapeDtypeStruct((tokens, width), kind)
    outs = [shape(D, f32), shape(D, bf16), shape(HALF_FF, bf16), shape(HALF_FF, bf16), shape(D, bf16)]
    return pl.pallas_call(
        functools.partial(mlp_kernel, layer),
        out_shape=outs,
        grid=(tokens // ROWS,),
        in_specs=[rows_spec(D)] * 3
        + [
            fixed(vec.shape),
            fixed((2 * HALF_FF, HALF), PANELS["up"][layer] // (2 * HALF_FF)),
            fixed((2 * HALF_FF, HALF), PANELS["down"][layer] // (2 * HALF_FF)),
        ],
        out_specs=[rows_spec(o.shape[1]) for o in outs],
        compiler_params=params(),
        cost_estimate=cost(4 * tokens * D * HALF_FF, tokens * D * 24, 2 * tokens * HALF_FF),
    )(base, own, recv, vec, panels, panels)


def mlp_back_kernel(layer, summed, *refs):
    if summed:
        base, own, recv, *refs = refs
        (hid, slope, vec, w_up, w_down, grad_full, grad_low, du_ref, back, dgain, dshift, db1, db2) = refs
        values = base[...].astype(f32) + (own[...].astype(f32) + recv[...].astype(f32))
        grad_full[...] = values
        low = values.astype(bf16)
    else:
        base, valid, *refs = refs
        (hid, slope, vec, w_up, w_down, grad_low, du_ref, back, dgain, dshift, db1, db2) = refs
        low = (base[...].astype(f32) * valid[...]).astype(bf16)
    grad_low[...] = low
    accumulate(db2, jnp.sum(low.astype(f32), axis=0, keepdims=True))
    for part in range(HALF_FF // HALF):
        area = slice(part * HALF, (part + 1) * HALF)
        grad_act = None
        for panel in range(TENSOR):
            start = panel * HALF_FF + part * HALF
            term = dot_nt(low[:, panel * HALF : (panel + 1) * HALF], w_down[start : start + HALF, :])
            grad_act = term if grad_act is None else grad_act + term
        du_ref[:, area] = (grad_act * slope[:, area].astype(f32)).astype(bf16)
    grad_normed = None
    for panel in range(HALF_FF // HALF):
        area = slice(panel * HALF, (panel + 1) * HALF)
        term = dot_nt(du_ref[:, area], w_up[panel * D : (panel + 1) * D, :])
        grad_normed = term if grad_normed is None else grad_normed + term
    accumulate(db1, jnp.sum(du_ref[...].astype(f32), axis=0, keepdims=True))
    part_back, gain_grad, shift_grad = norm_back(hid[...], vec_piece(vec, layer, "g2"), grad_normed)
    back[...] = part_back.astype(bf16)
    accumulate(dgain, gain_grad)
    accumulate(dshift, shift_grad)


def mlp_back_call(layer, base, own, recv, valid, hid, slope, vec, panels):
    tokens = base.shape[0]
    summed = own is not None
    shape = lambda width, kind: jax.ShapeDtypeStruct((tokens, width), kind)
    line = lambda width: jax.ShapeDtypeStruct((1, width), f32)
    outs = ([shape(D, f32)] if summed else []) + [shape(D, bf16), shape(HALF_FF, bf16), shape(D, bf16)]
    lines = [line(D), line(D), line(HALF_FF), line(D)]
    extra = [own, recv] if summed else [valid]
    return pl.pallas_call(
        functools.partial(mlp_back_kernel, layer, summed),
        out_shape=outs + lines,
        grid=(tokens // ROWS,),
        in_specs=[rows_spec(D)]
        + [rows_spec(e.shape[1]) for e in extra]
        + [
            rows_spec(D),
            rows_spec(HALF_FF),
            fixed(vec.shape),
            fixed((2 * HALF_FF, HALF), PANELS["up"][layer] // (2 * HALF_FF)),
            fixed((2 * HALF_FF, HALF), PANELS["down"][layer] // (2 * HALF_FF)),
        ],
        out_specs=[rows_spec(o.shape[1]) for o in outs] + [fixed(o.shape) for o in lines],
        compiler_params=params(),
        cost_estimate=cost(4 * tokens * D * HALF_FF, tokens * D * 24),
    )(base, *extra, hid, slope, vec, panels, panels)


def attend_back_kernel(
    low_ref, high_ref, base, own, recv, q_ref, k_ref, v_ref, o_ref, lse_ref, seg_k, seg_q, w_out,
    full_ref, grad_low, dq_ref, dk_ref, dv_ref, dbo, dk_acc, dv_acc, dq_acc, do_ref,
):
    step = pl.program_id(0)

    @pl.when(step == 0)
    def _():
        dk_acc[...] = jnp.zeros_like(dk_acc)
        dv_acc[...] = jnp.zeros_like(dv_acc)

    values = base[...].astype(f32) + (own[...].astype(f32) + recv[...].astype(f32))
    full_ref[...] = values
    low = values.astype(bf16)
    grad_low[...] = low
    accumulate(dbo, jnp.sum(low.astype(f32), axis=0, keepdims=True))
    grad_mixed = None
    for panel in range(TENSOR):
        area = slice(panel * HALF, (panel + 1) * HALF)
        term = dot_nt(low[:, area], w_out[area, :])
        grad_mixed = term if grad_mixed is None else grad_mixed + term
    do_ref[...] = grad_mixed.astype(bf16)
    product = do_ref[...].astype(f32) * o_ref[...].astype(f32)
    head = lax.broadcasted_iota(jnp.int32, (8, HALF), 0)
    lane = lax.broadcasted_iota(jnp.int32, (8, HALF), 1)
    pick = ((lane >= head * HEAD_DIM) & (lane < (head + 1) * HEAD_DIM)).astype(f32)
    inner = dot_nt(pick, product, precise)
    dq_acc[...] = jnp.zeros_like(dq_acc)
    masks = head_masks()
    scale = jnp.asarray(HEAD_DIM ** (-0.5), bf16)
    seg_row = seg_q[...]

    def one_block(block, carried):
        rows = pl.ds(pl.multiple_of(block * ROWS, ROWS), ROWS)
        same = seg_k[rows, :] == seg_row
        for pair in range(HEADS // 2):
            cols = slice(pair * BS, (pair + 1) * BS)
            q_two = q_ref[:, cols] * scale
            do_two = do_ref[:, cols]
            k_two = k_ref[rows, cols]
            v_two = v_ref[rows, cols]
            dv_two = dk_two = dq_two = None
            for side in range(2):
                at = 2 * pair + side
                q_one = q_two * masks[side]
                do_one = do_two * masks[side]
                scores = dot_nt(k_two, q_one)
                prob = jnp.where(same, jnp.exp(scores - lse_ref[at : at + 1, :]), 0.0)
                grad_prob = dot_nt(v_two, do_one)
                grad_scores = (prob * (grad_prob - inner[at : at + 1, :])).astype(bf16)
                dv_one = dot(prob.astype(bf16), do_one)
                dk_one = dot(grad_scores, q_one)
                dq_one = dot_tn(grad_scores, k_two * masks[side])
                dv_two = dv_one if dv_two is None else dv_two + dv_one
                dk_two = dk_one if dk_two is None else dk_two + dk_one
                dq_two = dq_one if dq_two is None else dq_two + dq_one
            dv_acc[rows, cols] += dv_two
            dk_acc[rows, cols] += dk_two
            dq_acc[:, cols] += dq_two
        return carried

    lax.fori_loop(low_ref[step], high_ref[step], one_block, 0)
    dq_ref[...] = (dq_acc[...] * HEAD_DIM ** (-0.5)).astype(bf16)

    @pl.when(step == pl.num_programs(0) - 1)
    def _():
        dk_ref[...] = dk_acc[...].astype(bf16)
        dv_ref[...] = dv_acc[...].astype(bf16)


def attend_back_call(
    layer, first, last, base, own, recv, queries, keys, values, mixed, lse, seg_col, seg_row, panels
):
    tokens = base.shape[0]
    shape = lambda width, kind: jax.ShapeDtypeStruct((tokens, width), kind)
    whole = (tokens, HALF)
    return pl.pallas_call(
        attend_back_kernel,
        out_shape=[
            shape(D, f32),
            shape(D, bf16),
            shape(HALF, bf16),
            shape(HALF, bf16),
            shape(HALF, bf16),
            jax.ShapeDtypeStruct((1, D), f32),
        ],
        grid_spec=pltpu.PrefetchScalarGridSpec(
            num_scalar_prefetch=2,
            grid=(tokens // ROWS,),
            in_specs=[
                rows_spec(D),
                rows_spec(D),
                rows_spec(D),
                rows_spec(HALF),
                fixed(whole),
                fixed(whole),
                rows_spec(HALF),
                pl.BlockSpec((8, ROWS), lambda i, *_: (0, i)),
                fixed(seg_col.shape),
                pl.BlockSpec((1, ROWS), lambda i, *_: (0, i)),
                fixed((D, HALF), PANELS["out"][layer] // D),
            ],
            out_specs=[
                rows_spec(D),
                rows_spec(D),
                rows_spec(HALF),
                fixed(whole),
                fixed(whole),
                fixed((1, D)),
            ],
            scratch_shapes=[
                pltpu.VMEM(whole, f32),
                pltpu.VMEM(whole, f32),
                pltpu.VMEM((ROWS, HALF), f32),
                pltpu.VMEM((ROWS, HALF), bf16),
            ],
        ),
        compiler_params=params(),
        cost_estimate=cost(14 * HEADS * tokens * tokens * BS, tokens * D * 20, HEADS * tokens * tokens),
    )(first, last, base, own, recv, queries, keys, values, mixed, lse, seg_col, seg_row, panels)


def qkv_back_kernel(layer, dq, dk, dv, hid, vec, weight, back, dgain, dshift, dbq, dbv):
    grad_normed = (
        dot_nt(dq[...], weight[0:D, :])
        + dot_nt(dk[...], weight[D : 2 * D, :])
        + dot_nt(dv[...], weight[2 * D : 3 * D, :])
    )
    part_back, gain_grad, shift_grad = norm_back(hid[...], vec_piece(vec, layer, "g1"), grad_normed)
    back[...] = part_back.astype(bf16)
    accumulate(dgain, gain_grad)
    accumulate(dshift, shift_grad)
    accumulate(dbq, jnp.sum(dq[...].astype(f32), axis=0, keepdims=True))
    accumulate(dbv, jnp.sum(dv[...].astype(f32), axis=0, keepdims=True))


def qkv_back_call(layer, dq, dk, dv, hid, vec, panels):
    tokens = dq.shape[0]
    line = lambda width: jax.ShapeDtypeStruct((1, width), f32)
    lines = [line(D), line(D), line(HALF), line(HALF)]
    return pl.pallas_call(
        functools.partial(qkv_back_kernel, layer),
        out_shape=[jax.ShapeDtypeStruct((tokens, D), bf16)] + lines,
        grid=(tokens // ROWS,),
        in_specs=[rows_spec(HALF)] * 3
        + [
            rows_spec(D),
            fixed(vec.shape),
            fixed((3 * D, HALF), PANELS["qkv"][layer] // (3 * D)),
        ],
        out_specs=[rows_spec(D)] + [fixed(o.shape) for o in lines],
        compiler_params=params(),
        cost_estimate=cost(2 * tokens * D * 3 * HALF, tokens * D * 10),
    )(dq, dk, dv, hid, vec, panels)


def rotate_step(master, grads, left, right, moment, variance):
    rotated = jnp.einsum("sji,sjk->sik", left, grads, precision=precise)
    rotated = jnp.einsum("sik,skl->sil", rotated, right, precision=precise)
    new_moment = decay * moment + (1.0 - decay) * rotated
    new_variance = decay * variance + (1.0 - decay) * rotated * rotated
    step_rot = new_moment / (jnp.sqrt(new_variance) + adam_eps)
    returned = jnp.einsum("sij,sjk->sik", left, step_rot, precision=precise)
    returned = jnp.einsum("sik,slk->sil", returned, right, precision=precise)
    return (master - matrix_rate * returned, new_moment, new_variance)


class Routes:
    def __init__(self, dp_n):
        pairs = [(d, t) for d in range(dp_n) for t in range(TENSOR)]
        at = lambda d, t: d * TENSOR + t
        home = [(d, t) for d, t in pairs if d % 2 == t]
        away = [(d, t) for d, t in pairs if d % 2 != t]
        self.core_all = [(at(d, t), at(d ^ 1, t)) for d, t in pairs]
        self.core_out = [(at(d, t), at(d ^ 1, t)) for d, t in home]
        self.core_in = [(at(d, t), at(d ^ 1, t)) for d, t in away]
        self.y_all = [(at(d, t), at(d, 1 - t)) for d, t in pairs]
        self.y_out = [(at(d, t), at(d, 1 - t)) for d, t in home]
        self.y_in = [(at(d, t), at(d, 1 - t)) for d, t in away]
        self.x_home = [(at(d, t), at(d ^ 2, t)) for d, t in home]
        self.x_away = [(at(d, t), at(d ^ 2, t)) for d, t in away]
        self.z_home = [(at(d, t), at((d + 4) % dp_n, t)) for d, t in home]


def send(value, route):
    return lax.ppermute(value, AXES, route)


def shards(
    patches,
    cotangent,
    image_size,
    block_slot,
    pinv,
    master_slots,
    left_basis,
    right_basis,
    mom_slots,
    var_slots,
    vec_master,
    vec_mom,
    vec_var,
):
    dp_n = lax.axis_size("dp")
    dp_pos = lax.axis_index("dp")
    y_pos = lax.axis_index("tensor")
    core = dp_pos % 2
    home = core == y_pos
    routes = Routes(dp_n)
    grid3 = dp_n == 16
    tokens_n = patches.shape[0]
    slots_per = master_slots.shape[1]
    vec_per = vec_master.shape[1]
    slots_n = slots_per * dp_n
    payload = slots_per * BS + VEC_ROWS

    patches = jnp.where(home, patches, send(patches, routes.core_out))
    cotangent = jnp.where(home, cotangent, send(cotangent, routes.core_out))
    size_row = jnp.where(home, image_size, send(image_size, routes.core_out))[0]
    own_slots = block_slot[0]
    slot_list = jnp.where(home, block_slot, send(block_slot, routes.y_all))[0]

    lengths = jnp.where(
        size_row == 0, LEN_A, jnp.where(size_row == 1, LEN_B, jnp.where(size_row == 2, LEN_C, 0))
    )
    order = jnp.arange(IMG_DEV)
    ends_at = jnp.sum(jnp.where(order[None, :] <= order[:, None], lengths[None, :], 0), axis=1)
    places = jnp.arange(tokens_n)
    segment = jnp.sum((places[:, None] >= ends_at[None, :]).astype(jnp.int32), axis=1)
    in_image = segment[:, None] == order[None, :]
    select = jnp.stack(
        [jnp.any(in_image & (size_row == s)[None, :], axis=1) for s in range(3)], axis=1
    )
    valid_col = (segment < IMG_DEV).astype(f32)[:, None]
    seg_col = segment[:, None]
    seg_row = segment[None, :]
    blocks_n = tokens_n // ROWS
    starts = jnp.arange(blocks_n) * ROWS
    begun = ends_at[None, :] <= starts[:, None]
    first_tok = jnp.max(jnp.where(begun, ends_at[None, :], 0), axis=1)
    after = ends_at[None, :] > (starts + ROWS - 1)[:, None]
    last_tok = jnp.min(jnp.where(after, ends_at[None, :], tokens_n), axis=1)
    first_blk = (first_tok // ROWS).astype(jnp.int32)
    last_blk = ((last_tok + ROWS - 1) // ROWS).astype(jnp.int32)

    select_low = select.astype(bf16)
    spread_in = patches[:, None, :] * select_low[:, :, None]
    base_pix = lax.dot_general(
        spread_in, pinv, (((1, 2), (0, 2)), ((), ())), preferred_element_type=f32
    ).astype(bf16)

    vec_low = jnp.pad(vec_master[0].astype(bf16), (0, VEC_ROWS * BS - vec_per))
    own_pack = jnp.concatenate(
        [
            master_slots[0].astype(bf16).reshape(slots_per * BS, BS),
            vec_low.reshape(VEC_ROWS, BS),
        ],
        axis=0,
    )
    named = slot_list[None, :] == jnp.arange(slots_n)[:, None]
    used = jnp.any(named, axis=1)
    drow = jnp.where(used, jnp.sum(jnp.where(named, TARGET_ROW[None, :], 0), axis=1), -1)
    dcol = jnp.sum(jnp.where(named, TARGET_COL[None, :], 0), axis=1)
    flag = home.astype(jnp.int32).reshape(1)
    if grid3:
        x_pos = (dp_pos // 2) % 2
        z_pos = dp_pos // 4
        pack = jnp.stack([own_pack, send(own_pack, routes.core_in)], axis=0)
        packs, acrosses, overs, corners = [pack], [], [], []
        for j in range(5):
            moved = []
            if j < 3:
                moved.append(send(packs[j], routes.z_home))
            if j < 4:
                moved += [send(packs[j], routes.x_home), send(packs[j], routes.y_out)]
            if j:
                moved += [
                    send(acrosses[j - 1][0:1], routes.y_out),
                    send(overs[j - 1][1:2], routes.x_away),
                ]
            if j < 4:
                moved = list(fence(*moved))
            if j < 3:
                packs.append(moved.pop(0))
            if j < 4:
                acrosses.append(moved.pop(0))
                overs.append(moved.pop(0))
            if j:
                corners.append(moved)
        first, second, owner = [], [], []
        for j in range(4):
            first += [packs[j], acrosses[j]]
            second += [overs[j]] + corners[j]
            for x_rel in range(2):
                for n in range(2):
                    owner.append(((z_pos - j) % 4) * 4 + (x_pos ^ x_rel) * 2 + (core ^ n))
        owner = jnp.stack(owner).astype(jnp.int32)
    else:
        everything = lax.all_gather(own_pack, AXES, axis=0)
        everything = everything.reshape(dp_n, TENSOR, payload, BS)
        first = [jnp.where(core == 0, everything[:, 0], everything[:, 1])]
        second = []
        owner = jnp.arange(dp_n, dtype=jnp.int32)
    panels, vec_rows = gather_tiles(first, second, owner, drow, dcol, flag, slots_per, dp_n)
    vec = vec_rows.reshape(dp_n, VEC_ROWS * BS)[:, :vec_per].astype(f32).reshape(1, dp_n * vec_per)

    base_w = panels[PANELS["base"] : PANELS["base"] + BASE_PIX]
    embedded = (dot(base_pix, base_w) + vec[:, :HALF]).astype(bf16)
    embedded_other = send(embedded, routes.core_all)
    hidden = jnp.concatenate(
        [
            jnp.where(core == 0, embedded, embedded_other),
            jnp.where(core == 0, embedded_other, embedded),
        ],
        axis=1,
    ).astype(f32)

    caches = []
    own = recv = None
    for layer in range(LAYERS):
        made = qkv_call(layer, hidden, own, recv, vec, panels)
        if own is not None:
            hidden, *made = made
        normed, queries, keys, values = made
        mixed, lse, part = attend_call(
            layer, queries, keys, values, seg_col, seg_row, vec, panels
        )
        other = send(part, routes.core_all)
        middle, normed2, act, slope, own = mlp_call(layer, hidden, part, other, vec, panels)
        recv = send(own, routes.core_all)
        caches.append((hidden, normed, queries, keys, values, mixed, lse, middle, normed2, act, slope))
        hidden = middle
    out_low = ((hidden + (own.astype(f32) + recv.astype(f32))) * valid_col).astype(bf16)
    output = jnp.where(home, out_low, send(out_low, routes.y_out)).astype(f32)

    owners = jnp.arange(dp_n)
    if grid3:
        place = (
            ((z_pos - 1 - owners // 4) % 4) * 4
            + (x_pos ^ ((owners // 2) % 2)) * 2
            + (core ^ (owners % 2))
        ).astype(jnp.int32)
        half_at = x_pos.astype(jnp.int32).reshape(1)
    else:
        place = owners.astype(jnp.int32)
        half_at = jnp.zeros((1,), jnp.int32)
    slot_owner = slot_list // slots_per
    owner_place = jnp.sum(
        jnp.where(slot_owner[:, None] == owners[None, :], place[None, :], 0), axis=1
    )
    tile_pos = (owner_place * payload + (slot_list % slots_per) * BS).astype(jnp.int32)
    vec_pos = (place * payload + slots_per * BS).astype(jnp.int32)
    total_rows = dp_n * payload
    offsets = {"base": 0}
    count = BASE_PIX // BS * (HALF // BS)
    for layer in range(LAYERS):
        for name, size in (("qkv", 3 * D * HALF), ("out", D * HALF), ("up", D * HALF_FF), ("down", D * HALF_FF)):
            offsets[name, layer] = count
            count += size // (BS * BS)

    def place_tiles(key, matrix, arrived, buffer):
        tiles = matrix.size // (BS * BS)
        pos = tile_pos[offsets[key] : offsets[key] + tiles]
        rows_n = BS if matrix.shape[0] < BASE_PIX else 4 * BS
        return scatter_matrix(pos, matrix, arrived, half_at, buffer, total_rows, rows_n)

    def over(matrix):
        return send(matrix, routes.y_in) if grid3 else None

    def halves_of(matrix):
        size = matrix.shape[0] // 2
        mine = lax.dynamic_slice_in_dim(matrix, x_pos * size, size, 0)
        theirs = lax.dynamic_slice_in_dim(matrix, (1 - x_pos) * size, size, 0)
        return mine, theirs

    def half_sum(matrix, arrived):
        mine, unused = halves_of(matrix)
        return (mine.astype(f32) + arrived.astype(f32)).astype(bf16)

    def beside(matrix):
        return send(halves_of(matrix)[1], routes.x_away) if grid3 else None

    def hold(*arrays):
        kept = [a for a in arrays if a is not None]
        done = iter(fence(*kept))
        return [None if a is None else next(done) for a in arrays]

    top, low = 1, 0
    vec_grads = [None] * LAYERS

    def mlp_step(layer, grad, own, recv):
        middle, normed2, act, slope = caches[layer][7:11]
        made = mlp_back_call(layer, grad, own, recv, valid_col, middle, slope, vec, panels)
        if own is not None:
            return made
        return [made[0]] + list(made)

    def attend_step(layer, grad, part, other):
        hid_in, normed, queries, keys, values, mixed, lse = caches[layer][:7]
        return attend_back_call(
            layer, first_blk, last_blk, grad, part, other, queries, keys, values, mixed, lse,
            seg_col, seg_row, panels,
        )

    grad, grad_low, du, part, dg2, ds2, db1, db2 = mlp_step(top, cotangent, None, None)
    other = send(part, routes.core_all)
    gd1 = dot_tn(caches[top][9], grad_low).astype(bf16)
    gu1 = dot_tn(caches[top][8], du).astype(bf16)
    part, other, gd1, gu1 = fence(part, other, gd1, gu1)
    ad1 = over(gd1)
    grad, grad_low, dq, dk, dv, dbo = attend_step(top, grad, part, other)
    dq, dk, dv, ad1 = hold(dq, dk, dv, ad1)
    au1 = over(gu1)
    own, dg1, ds1, dbq, dbv = qkv_back_call(top, dq, dk, dv, caches[top][0], vec, panels)
    recv = send(own, routes.core_all)
    go1 = dot_tn(caches[top][5], grad_low).astype(bf16)
    gq1 = dot_tn(caches[top][1], jnp.concatenate([dq, dk, dv], axis=1)).astype(bf16)
    vec_grads[top] = [dg1, ds1, dbq, dbv, dbo, dg2, ds2, db1, db2]
    grad, grad_low, du, part, dg2, ds2, db1, db2 = mlp_step(low, grad, own, recv)
    du, part, au1, go1, gq1 = hold(du, part, au1, go1, gq1)
    other = send(part, routes.core_all)
    xq1, ao1 = beside(gq1), over(go1)
    gd0 = dot_tn(caches[low][9], grad_low).astype(bf16)
    gu0 = dot_tn(caches[low][8], du).astype(bf16)
    part, other, gd0, gu0, xq1, ao1 = hold(part, other, gd0, gu0, xq1, ao1)
    aq1 = over(half_sum(gq1, xq1)) if grid3 else None
    xd0, xu0 = beside(gd0), beside(gu0)
    buffer = place_tiles(("down", top), gd1, ad1, None)
    buffer = place_tiles(("up", top), gu1, au1, buffer)
    grad, grad_low, dq, dk, dv, dbo = attend_step(low, grad, part, other)
    grad, grad_low, dq, dk, dv, aq1, xd0, xu0, buffer = hold(
        grad, grad_low, dq, dk, dv, aq1, xd0, xu0, buffer
    )
    ad0 = over(half_sum(gd0, xd0)) if grid3 else None
    au0 = over(half_sum(gu0, xu0)) if grid3 else None
    own, dg1, ds1, dbq, dbv = qkv_back_call(low, dq, dk, dv, caches[low][0], vec, panels)
    recv = send(own, routes.core_all)
    go0 = dot_tn(caches[low][5], grad_low).astype(bf16)
    gq0 = dot_tn(caches[low][1], jnp.concatenate([dq, dk, dv], axis=1)).astype(bf16)
    vec_grads[low] = [dg1, ds1, dbq, dbv, dbo, dg2, ds2, db1, db2]
    sides = [
        grad[:, s * HALF : (s + 1) * HALF]
        + (
            own[:, s * HALF : (s + 1) * HALF].astype(f32)
            + recv[:, s * HALF : (s + 1) * HALF].astype(f32)
        )
        for s in range(TENSOR)
    ]
    grad_emb = jnp.where(core == 0, sides[0], sides[1]).astype(bf16)
    grad_emb_bias = jnp.sum(grad_emb.astype(f32), axis=0, keepdims=True)
    gb = dot_tn(base_pix, grad_emb).astype(bf16)
    vec_grad = jnp.concatenate([grad_emb_bias] + vec_grads[0] + vec_grads[1], axis=1)[0]
    vec_grad = jnp.pad(vec_grad, (0, dp_n * vec_per - vec_grad.shape[0])).reshape(dp_n, vec_per)
    vec_grad = jnp.pad(vec_grad, ((0, 0), (0, VEC_ROWS * BS - vec_per)))
    vec_grad = vec_grad.astype(bf16).reshape(dp_n, VEC_ROWS, BS)
    ad0, au0, go0, gq0, gb, vec_grad, grad_emb = hold(ad0, au0, go0, gq0, gb, vec_grad, grad_emb)
    xq0 = beside(gq0)
    ab, ao0, av = over(gb), over(go0), over(vec_grad)
    buffer = place_tiles(("out", top), go1, ao1, buffer)
    buffer = place_tiles(("qkv", top), gq1, aq1, buffer)
    buffer = place_tiles(("down", low), gd0, ad0, buffer)
    buffer = place_tiles(("up", low), gu0, au0, buffer)
    resized = [dot_tn(pinv[s], base_w).astype(bf16) for s in range(3)]
    xq0, ab, ao0, av, buffer, *resized = hold(xq0, ab, ao0, av, buffer, *resized)
    aq0 = over(half_sum(gq0, xq0)) if grid3 else None
    buffer = place_tiles("base", gb, ab, buffer)
    buffer = place_tiles(("out", low), go0, ao0, buffer)
    buffer = scatter_vec(vec_pos, vec_grad, av, buffer)
    grad_pixels = sum(
        dot_nt(grad_emb * select_low[:, s : s + 1], resized[s]) for s in range(3)
    ).astype(bf16)
    aq0, buffer, grad_pixels = hold(aq0, buffer, grad_pixels)
    buffer = place_tiles(("qkv", low), gq0, aq0, buffer)

    if grid3:
        carried = None
        for j in range(4):
            block = buffer.reshape(4, 2, 2, payload, BS)
            arrived = send(block[j, 1], routes.x_home)
            if carried is not None:
                arrived, carried, buffer = fence(arrived, carried, buffer)
            else:
                arrived, buffer = fence(arrived, buffer)
            block = buffer.reshape(4, 2, 2, payload, BS)
            total = block[j, 0].astype(f32) + arrived.astype(f32)
            if carried is not None:
                total = total + carried.astype(f32)
            if j < 3:
                carried = send(total.astype(bf16), routes.z_home)
        rounded = total.astype(bf16)
        mine = jnp.where(home, rounded[0], send(rounded[1], routes.core_out)).astype(f32)
    else:
        held = buffer.reshape(dp_n, 1, payload, BS).astype(f32)
        nothing = jnp.zeros_like(held)
        both = jnp.concatenate(
            [jnp.where(core == 0, held, nothing), jnp.where(core == 0, nothing, held)], axis=1
        )
        used_rows = jnp.repeat(used, BS).reshape(dp_n, 1, slots_per * BS, 1)
        used_rows = jnp.concatenate(
            [used_rows, jnp.ones((dp_n, 1, VEC_ROWS, 1), bool)], axis=2
        )
        both = jnp.where(used_rows, both, 0.0).reshape(dp_n * TENSOR * payload, BS)
        mine = lax.psum_scatter(both, AXES, scatter_dimension=0, tiled=True)

    pixels_other = send(grad_pixels, routes.core_all)
    pixel_sides = [
        grad_pixels[:, s * HALF : (s + 1) * HALF].astype(f32)
        + pixels_other[:, s * HALF : (s + 1) * HALF].astype(f32)
        for s in range(TENSOR)
    ]
    near = jnp.where(core == 0, pixel_sides[0], pixel_sides[1])
    far = jnp.where(core == 0, pixel_sides[1], pixel_sides[0]).astype(bf16)
    patch_grad = jnp.where(home, near, send(far, routes.y_out).astype(f32))

    my_slots = dp_pos * slots_per + jnp.arange(slots_per)
    mine_used = jnp.any(own_slots[None, :] == my_slots[:, None], axis=1)
    owned_grad = mine[: slots_per * BS].reshape(slots_per, BS, BS)
    owned_grad = jnp.where(mine_used[:, None, None], owned_grad, 0.0)
    owned_vec_grad = mine[slots_per * BS :].reshape(VEC_ROWS * BS)[:vec_per]
    new_master, new_mom, new_var = rotate_step(
        master_slots[0], owned_grad, left_basis[0], right_basis[0], mom_slots[0], var_slots[0]
    )
    new_vec_mom = decay * vec_mom[0] + (1.0 - decay) * owned_vec_grad
    new_vec_var = decay * vec_var[0] + (1.0 - decay) * owned_vec_grad * owned_vec_grad
    new_vec = vec_master[0] - vector_rate * new_vec_mom / (jnp.sqrt(new_vec_var) + adam_eps)
    return (
        output,
        patch_grad,
        owned_grad[None],
        new_master[None],
        new_mom[None],
        new_var[None],
        owned_vec_grad[None],
        new_vec[None],
        new_vec_mom[None],
        new_vec_var[None],
    )


def solution(mesh):
    slots = P("tensor", "dp", None, None)
    vectors = P("tensor", "dp")
    tokens = P("dp", None)
    in_specs = (tokens, tokens, tokens, P("tensor", None), P()) + (slots,) * 5 + (vectors,) * 3
    out_specs = (tokens, P("dp", "tensor")) + (slots,) * 4 + (vectors,) * 4
    return jax.shard_map(shards, mesh=mesh, in_specs=in_specs, out_specs=out_specs, check_vma=False)
```

```python
import functools

import jax
import jax.numpy as jnp
import numpy as np
from jax import lax
from jax.experimental import pallas as pl
from jax.experimental.pallas import tpu as pltpu
from jax.sharding import PartitionSpec as P

D = 768
HEAD_DIM = 64
FF = 3072
BASE_PIX = 3072
LAYERS = 2
LEN_A = 196
LEN_B = 225
LEN_C = 576
IMG_DEV = 5
BS = 128
TENSOR = 2
HALF = D // TENSOR
HALF_FF = FF // TENSOR
HEADS = HALF // HEAD_DIM
ROWS = 256
VEC_ROWS = 16

AXES = ("dp", "tensor")
precise = lax.Precision.HIGHEST
masked_score = -1e30
norm_eps = 1e-06
adam_eps = 1e-08
decay = 0.5
matrix_rate = 0.05
vector_rate = 0.3
f32 = jnp.float32
bf16 = jnp.bfloat16
BIG_VMEM = 56 * 1024 * 1024

PANELS = {
    "up": (0, 6144),
    "down": (3072, 9216),
    "base": 12288,
    "out": (15360, 20736),
    "qkv": (16128, 18432),
}
PANEL_ROWS = 21504


def tile_targets():
    rows, cols = [], []

    def add(start, rows_n, cols_n):
        for i in range(rows_n // BS):
            for j in range(cols_n // BS):
                panel, inner = divmod(j * BS, HALF)
                rows.append(start + panel * rows_n + i * BS)
                cols.append(inner)

    add(PANELS["base"], BASE_PIX, HALF)
    for layer in range(LAYERS):
        add(PANELS["qkv"][layer], D, 3 * HALF)
        add(PANELS["out"][layer], HALF, D)
        add(PANELS["up"][layer], D, HALF_FF)
        add(PANELS["down"][layer], HALF_FF, D)
    return np.array(rows, np.int32), np.array(cols, np.int32)


TARGET_ROW, TARGET_COL = tile_targets()
LAYER_VECS = (D, D, HALF, HALF, D, D, D, HALF_FF, D)
VEC_NAMES = ("g1", "s1", "bq", "bv", "bo", "g2", "s2", "b1", "b2")


def vec_offsets():
    offset = HALF
    found = []
    for layer in range(LAYERS):
        here = {}
        for name, length in zip(VEC_NAMES, LAYER_VECS):
            here[name] = (offset, length)
            offset += length
        found.append(here)
    return found


VEC_AT = vec_offsets()


def params(limit=BIG_VMEM):
    return pltpu.CompilerParams(
        dimension_semantics=("arbitrary",), vmem_limit_bytes=limit
    )


def cost(flops, nbytes, trans=0):
    return pl.CostEstimate(flops=flops, bytes_accessed=nbytes, transcendentals=trans)


def rows_spec(width):
    return pl.BlockSpec((ROWS, width), lambda i, *_: (i, 0))


def fixed(shape, at=0):
    return pl.BlockSpec(shape, lambda i, *_: (at,) + (0,) * (len(shape) - 1))


def vec_piece(vec_ref, layer, name):
    start, length = VEC_AT[layer][name]
    return vec_ref[:, start : start + length]


def dot(left, right):
    return jnp.dot(left, right, preferred_element_type=f32)


def dot_nt(left, right, precision=None):
    return lax.dot_general(
        left, right, (((1,), (1,)), ((), ())), precision=precision, preferred_element_type=f32
    )


def dot_tn(left, right):
    return lax.dot_general(left, right, (((0,), (0,)), ((), ())), preferred_element_type=f32)


def norm_stats(values):
    mean_val = jnp.mean(values, axis=-1, keepdims=True)
    centered = values - mean_val
    inv_std = lax.rsqrt(jnp.mean(centered * centered, axis=-1, keepdims=True) + norm_eps)
    return centered * inv_std, inv_std


def norm_back(values, gain, grad):
    unit, inv_std = norm_stats(values)
    scaled = grad * gain
    mean_s = jnp.mean(scaled, axis=-1, keepdims=True)
    mean_u = jnp.mean(scaled * unit, axis=-1, keepdims=True)
    back = inv_std * (scaled - mean_s - unit * mean_u)
    return (
        back,
        jnp.sum(grad * unit, axis=0, keepdims=True),
        jnp.sum(grad, axis=0, keepdims=True),
    )


def accumulate(ref, value):
    first = pl.program_id(0) == 0

    @pl.when(first)
    def _():
        ref[...] = value

    @pl.when(jnp.logical_not(first))
    def _():
        ref[...] += value


def fence(*arrays):
    def nothing(*refs):
        pass

    anywhere = pl.BlockSpec(memory_space=pl.ANY)
    return pl.pallas_call(
        nothing,
        out_shape=[jax.ShapeDtypeStruct(a.shape, a.dtype) for a in arrays],
        in_specs=[anywhere] * len(arrays),
        out_specs=[anywhere] * len(arrays),
        input_output_aliases={i: i for i in range(len(arrays))},
    )(*arrays)


def gather_kernel(slots, count_a, count_b, owner, drow, dcol, flag, *refs):
    first = refs[:count_a]
    second = refs[count_a : count_a + count_b]
    panels, vectors, held, sem, vec_sem = refs[count_a + count_b :]

    def copy_all(sources):
        at = 0
        for src in sources:
            for n in range(src.shape[0]):
                who = owner[at]
                at += 1

                def body(i, carried, src=src, n=n, who=who):
                    slot = who * slots + i
                    row = drow[slot]

                    @pl.when(row >= 0)
                    def _():
                        start = pl.multiple_of(i * BS, BS)
                        pltpu.make_async_copy(
                            src.at[n, pl.ds(start, BS), :],
                            held.at[
                                pl.ds(pl.multiple_of(row, BS), BS),
                                pl.ds(pl.multiple_of(dcol[slot], BS), BS),
                            ],
                            sem,
                        ).start()

                    return carried

                lax.fori_loop(0, slots, body, 0)
                pltpu.make_async_copy(
                    src.at[n, pl.ds(slots * BS, VEC_ROWS), :], vectors.at[who], vec_sem
                ).start()

    if count_b:

        @pl.when(flag[0] == 1)
        def _():
            copy_all(first)

        @pl.when(flag[0] == 0)
        def _():
            copy_all(second)
    else:
        copy_all(first)
    pltpu.make_async_copy(held, held, sem).wait()
    out = pltpu.make_async_copy(held, panels, sem)
    out.start()
    pltpu.make_async_copy(vectors, vectors, vec_sem).wait()
    out.wait()


def gather_tiles(first, second, owner, drow, dcol, flag, slots, owners):
    anywhere = pl.BlockSpec(memory_space=pl.ANY)
    return pl.pallas_call(
        functools.partial(gather_kernel, slots, len(first), len(second)),
        out_shape=(
            jax.ShapeDtypeStruct((PANEL_ROWS, HALF), bf16),
            jax.ShapeDtypeStruct((owners, VEC_ROWS, BS), bf16),
        ),
        grid_spec=pltpu.PrefetchScalarGridSpec(
            num_scalar_prefetch=4,
            grid=(1,),
            in_specs=[anywhere] * (len(first) + len(second)),
            out_specs=(anywhere, fixed((owners, VEC_ROWS, BS))),
            scratch_shapes=[
                pltpu.VMEM((PANEL_ROWS, HALF), bf16),
                pltpu.SemaphoreType.DMA,
                pltpu.SemaphoreType.DMA,
            ],
        ),
        compiler_params=params(),
        cost_estimate=cost(0, 4 * PANEL_ROWS * HALF),
    )(owner, drow, dcol, flag, *first, *second)


def scatter_kernel(rows_n, cols_n, steps, paired, parts, pos, part, own, *refs):
    if paired:
        recv, *refs = refs
        span = pl.num_programs(0) // parts
        here = jnp.logical_or(parts == 1, pl.program_id(0) // span == part[0])
    target, buf, sems = refs[-3:]
    step = pl.program_id(0)
    slot = lax.rem(step, 2)
    per = rows_n // BS * (cols_n // BS)

    def wait(at):
        pltpu.make_async_copy(buf.at[at], buf.at[at], sems.at[at]).wait()

    @pl.when(step >= 2)
    def _():
        wait(slot)

    for i in range(rows_n // BS):
        for j in range(cols_n // BS):
            area = (slice(i * BS, (i + 1) * BS), slice(j * BS, (j + 1) * BS))
            value = own[area]
            if paired:
                more = jnp.where(here, recv[area].astype(f32), 0.0)
                value = (value.astype(f32) + more).astype(bf16)
            buf[slot, i * (cols_n // BS) + j] = value
    for n in range(per):
        pltpu.make_async_copy(
            buf.at[slot, n],
            target.at[pl.ds(pl.multiple_of(pos[step * per + n], 16), BS), :],
            sems.at[slot],
        ).start()

    @pl.when(step == pl.num_programs(0) - 1)
    def _():
        if steps > 1:
            wait(1 - slot)
        wait(slot)


def scatter_matrix(pos, own, recv, part, target, total_rows, rows_n):
    cols_n = own.shape[1]
    steps = own.shape[0] // rows_n
    anywhere = pl.BlockSpec(memory_space=pl.ANY)
    block = pl.BlockSpec((rows_n, cols_n), lambda i, *_: (i, 0))
    paired = recv is not None
    parts = own.shape[0] // recv.shape[0] if paired else 1
    span = steps // parts
    arrived = pl.BlockSpec(
        (rows_n, cols_n), lambda i, pos, part: (jnp.clip(i - part[0] * span, 0, span - 1), 0)
    )
    operands = [own] + ([recv] if paired else []) + ([] if target is None else [target])
    specs = [block] + ([block if parts == 1 else arrived] if paired else [])
    specs += [] if target is None else [anywhere]
    return pl.pallas_call(
        functools.partial(scatter_kernel, rows_n, cols_n, steps, paired, parts),
        out_shape=jax.ShapeDtypeStruct((total_rows, BS), bf16),
        grid_spec=pltpu.PrefetchScalarGridSpec(
            num_scalar_prefetch=2,
            grid=(steps,),
            in_specs=specs,
            out_specs=anywhere,
            scratch_shapes=[
                pltpu.VMEM((2, rows_n // BS * (cols_n // BS), BS, BS), bf16),
                pltpu.SemaphoreType.DMA((2,)),
            ],
        ),
        input_output_aliases={} if target is None else {len(operands) + 1: 0},
        compiler_params=params(),
        cost_estimate=cost(own.size, own.size * 6),
    )(pos, part, *operands)


def scatter_vec_kernel(paired, pos, own, *refs):
    if paired:
        recv, *refs = refs
    target, buf, sem = refs[-3:]
    value = own[...]
    if paired:
        value = (value.astype(f32) + recv[...].astype(f32)).astype(bf16)
    buf[...] = value

    def body(n, carried):
        pltpu.make_async_copy(
            buf.at[n], target.at[pl.ds(pl.multiple_of(pos[n], 16), VEC_ROWS), :], sem
        ).start()
        return carried

    lax.fori_loop(0, own.shape[0], body, 0)
    pltpu.make_async_copy(buf, buf, sem).wait()


def scatter_vec(pos, own, recv, target):
    anywhere = pl.BlockSpec(memory_space=pl.ANY)
    block = fixed(own.shape)
    paired = recv is not None
    operands = [own] + ([recv] if paired else []) + [target]
    return pl.pallas_call(
        functools.partial(scatter_vec_kernel, paired),
        out_shape=jax.ShapeDtypeStruct(target.shape, bf16),
        grid_spec=pltpu.PrefetchScalarGridSpec(
            num_scalar_prefetch=1,
            grid=(1,),
            in_specs=[block] * (len(operands) - 1) + [anywhere],
            out_specs=anywhere,
            scratch_shapes=[pltpu.VMEM(own.shape, bf16), pltpu.SemaphoreType.DMA],
        ),
        input_output_aliases={len(operands): 0},
        compiler_params=params(),
    )(pos, *operands)


def qkv_kernel(layer, summed, *refs):
    if summed:
        base, own, recv, vec, weight, hid, normed, q_ref, k_ref, v_ref = refs
        values = base[...] + (own[...].astype(f32) + recv[...].astype(f32))
        hid[...] = values
    else:
        base, vec, weight, normed, q_ref, k_ref, v_ref = refs
        values = base[...]
    unit, unused = norm_stats(values)
    low = (unit * vec_piece(vec, layer, "g1") + vec_piece(vec, layer, "s1")).astype(bf16)
    normed[...] = low
    q_ref[...] = (dot(low, weight[0:D, :]) + vec_piece(vec, layer, "bq")).astype(bf16)
    k_ref[...] = dot(low, weight[D : 2 * D, :]).astype(bf16)
    v_ref[...] = (dot(low, weight[2 * D : 3 * D, :]) + vec_piece(vec, layer, "bv")).astype(bf16)


def qkv_call(layer, base, own, recv, vec, panels):
    tokens = base.shape[0]
    summed = own is not None
    shape = lambda width, kind: jax.ShapeDtypeStruct((tokens, width), kind)
    outs = ([shape(D, f32)] if summed else []) + [shape(D, bf16)] + [shape(HALF, bf16)] * 3
    operands = [base] + ([own, recv] if summed else []) + [vec, panels]
    return pl.pallas_call(
        functools.partial(qkv_kernel, layer, summed),
        out_shape=outs,
        grid=(tokens // ROWS,),
        in_specs=[rows_spec(D)] * (3 if summed else 1)
        + [fixed(vec.shape), fixed((3 * D, HALF), PANELS["qkv"][layer] // (3 * D))],
        out_specs=[rows_spec(o.shape[1]) for o in outs],
        compiler_params=params(),
        cost_estimate=cost(2 * tokens * D * 3 * HALF, tokens * D * 14),
    )(*operands)


def head_masks():
    lane = lax.broadcasted_iota(jnp.int32, (1, 2 * HEAD_DIM), 1)
    low = (lane < HEAD_DIM).astype(f32).astype(bf16)
    high = (lane >= HEAD_DIM).astype(f32).astype(bf16)
    return low, high


def attend_kernel(layer, q_ref, k_ref, v_ref, seg_q, seg_k, vec, w_out, o_ref, lse_ref, part):
    masks = head_masks()
    same = seg_q[...] == seg_k[...]
    lane = lax.broadcasted_iota(jnp.int32, (ROWS, BS), 1)
    totals = jnp.zeros((ROWS, BS), f32)
    scale = jnp.asarray(HEAD_DIM ** (-0.5), bf16)
    for pair in range(HEADS // 2):
        cols = slice(pair * BS, (pair + 1) * BS)
        q_two = q_ref[:, cols] * scale
        k_two = k_ref[:, cols]
        v_two = v_ref[:, cols]
        mixed = None
        for side in range(2):
            scores = dot_nt(q_two * masks[side], k_two)
            scores = jnp.where(same, scores, masked_score)
            top = jnp.max(scores, axis=1, keepdims=True)
            expo = jnp.exp(scores - top)
            total = jnp.sum(expo, axis=1, keepdims=True)
            weights = (expo * (1.0 / total)).astype(bf16)
            term = dot(weights, v_two * masks[side])
            mixed = term if mixed is None else mixed + term
            totals = jnp.where(lane == 2 * pair + side, top + jnp.log(total), totals)
        o_ref[:, cols] = mixed.astype(bf16)
    lse_ref[...] = totals.T[0:8, :]
    low = o_ref[...]
    bias = vec_piece(vec, layer, "bo")
    for panel in range(TENSOR):
        area = slice(panel * HALF, (panel + 1) * HALF)
        part[:, area] = (dot(low, w_out[area, :]) + bias[:, area]).astype(bf16)


def attend_call(layer, queries, keys, values, seg_col, seg_row, vec, panels):
    tokens = queries.shape[0]
    return pl.pallas_call(
        functools.partial(attend_kernel, layer),
        out_shape=[
            jax.ShapeDtypeStruct((tokens, HALF), bf16),
            jax.ShapeDtypeStruct((8, tokens), f32),
            jax.ShapeDtypeStruct((tokens, D), bf16),
        ],
        grid=(tokens // ROWS,),
        in_specs=[
            rows_spec(HALF),
            fixed(keys.shape),
            fixed(values.shape),
            rows_spec(1),
            fixed(seg_row.shape),
            fixed(vec.shape),
            fixed((D, HALF), PANELS["out"][layer] // D),
        ],
        out_specs=[
            rows_spec(HALF),
            pl.BlockSpec((8, ROWS), lambda i: (0, i)),
            rows_spec(D),
        ],
        compiler_params=params(),
        cost_estimate=cost(8 * HEADS * tokens * tokens * BS, tokens * D * 8, HEADS * tokens * tokens),
    )(queries, keys, values, seg_col, seg_row, vec, panels)


def gelu_parts(values):
    cdf = 0.5 * (1.0 + lax.erf(values * 0.7071067811865476))
    pdf = 0.3989422804014327 * jnp.exp(-0.5 * values * values)
    return values * cdf, cdf + values * pdf


def mlp_kernel(layer, base, own, recv, vec, w_up, w_down, hid, normed, act, slope, part):
    values = base[...] + (own[...].astype(f32) + recv[...].astype(f32))
    hid[...] = values
    unit, unused = norm_stats(values)
    low = (unit * vec_piece(vec, layer, "g2") + vec_piece(vec, layer, "s2")).astype(bf16)
    normed[...] = low
    bias_up = vec_piece(vec, layer, "b1")
    for panel in range(HALF_FF // HALF):
        area = slice(panel * HALF, (panel + 1) * HALF)
        up = dot(low, w_up[panel * D : (panel + 1) * D, :]) + bias_up[:, area]
        gelu, grad = gelu_parts(up)
        act[:, area] = gelu.astype(bf16)
        slope[:, area] = grad.astype(bf16)
    bias_down = vec_piece(vec, layer, "b2")
    hidden_units = act[...]
    for panel in range(TENSOR):
        area = slice(panel * HALF, (panel + 1) * HALF)
        down = dot(hidden_units, w_down[panel * HALF_FF : (panel + 1) * HALF_FF, :])
        part[:, area] = (down + bias_down[:, area]).astype(bf16)


def mlp_call(layer, base, own, recv, vec, panels):
    tokens = base.shape[0]
    shape = lambda width, kind: jax.ShapeDtypeStruct((tokens, width), kind)
    outs = [shape(D, f32), shape(D, bf16), shape(HALF_FF, bf16), shape(HALF_FF, bf16), shape(D, bf16)]
    return pl.pallas_call(
        functools.partial(mlp_kernel, layer),
        out_shape=outs,
        grid=(tokens // ROWS,),
        in_specs=[rows_spec(D)] * 3
        + [
            fixed(vec.shape),
            fixed((2 * HALF_FF, HALF), PANELS["up"][layer] // (2 * HALF_FF)),
            fixed((2 * HALF_FF, HALF), PANELS["down"][layer] // (2 * HALF_FF)),
        ],
        out_specs=[rows_spec(o.shape[1]) for o in outs],
        compiler_params=params(),
        cost_estimate=cost(4 * tokens * D * HALF_FF, tokens * D * 24, 2 * tokens * HALF_FF),
    )(base, own, recv, vec, panels, panels)


def mlp_back_kernel(layer, summed, *refs):
    if summed:
        base, own, recv, *refs = refs
        (hid, slope, vec, w_up, w_down, grad_full, grad_low, du_ref, back, dgain, dshift, db1, db2) = refs
        values = base[...].astype(f32) + (own[...].astype(f32) + recv[...].astype(f32))
        grad_full[...] = values
        low = values.astype(bf16)
    else:
        base, valid, *refs = refs
        (hid, slope, vec, w_up, w_down, grad_low, du_ref, back, dgain, dshift, db1, db2) = refs
        low = (base[...].astype(f32) * valid[...]).astype(bf16)
    grad_low[...] = low
    accumulate(db2, jnp.sum(low.astype(f32), axis=0, keepdims=True))
    for part in range(HALF_FF // HALF):
        area = slice(part * HALF, (part + 1) * HALF)
        grad_act = None
        for panel in range(TENSOR):
            start = panel * HALF_FF + part * HALF
            term = dot_nt(low[:, panel * HALF : (panel + 1) * HALF], w_down[start : start + HALF, :])
            grad_act = term if grad_act is None else grad_act + term
        du_ref[:, area] = (grad_act * slope[:, area].astype(f32)).astype(bf16)
    grad_normed = None
    for panel in range(HALF_FF // HALF):
        area = slice(panel * HALF, (panel + 1) * HALF)
        term = dot_nt(du_ref[:, area], w_up[panel * D : (panel + 1) * D, :])
        grad_normed = term if grad_normed is None else grad_normed + term
    accumulate(db1, jnp.sum(du_ref[...].astype(f32), axis=0, keepdims=True))
    part_back, gain_grad, shift_grad = norm_back(hid[...], vec_piece(vec, layer, "g2"), grad_normed)
    back[...] = part_back.astype(bf16)
    accumulate(dgain, gain_grad)
    accumulate(dshift, shift_grad)


def mlp_back_call(layer, base, own, recv, valid, hid, slope, vec, panels):
    tokens = base.shape[0]
    summed = own is not None
    shape = lambda width, kind: jax.ShapeDtypeStruct((tokens, width), kind)
    line = lambda width: jax.ShapeDtypeStruct((1, width), f32)
    outs = ([shape(D, f32)] if summed else []) + [shape(D, bf16), shape(HALF_FF, bf16), shape(D, bf16)]
    lines = [line(D), line(D), line(HALF_FF), line(D)]
    extra = [own, recv] if summed else [valid]
    return pl.pallas_call(
        functools.partial(mlp_back_kernel, layer, summed),
        out_shape=outs + lines,
        grid=(tokens // ROWS,),
        in_specs=[rows_spec(D)]
        + [rows_spec(e.shape[1]) for e in extra]
        + [
            rows_spec(D),
            rows_spec(HALF_FF),
            fixed(vec.shape),
            fixed((2 * HALF_FF, HALF), PANELS["up"][layer] // (2 * HALF_FF)),
            fixed((2 * HALF_FF, HALF), PANELS["down"][layer] // (2 * HALF_FF)),
        ],
        out_specs=[rows_spec(o.shape[1]) for o in outs] + [fixed(o.shape) for o in lines],
        compiler_params=params(),
        cost_estimate=cost(4 * tokens * D * HALF_FF, tokens * D * 24),
    )(base, *extra, hid, slope, vec, panels, panels)


def attend_back_kernel(
    low_ref, high_ref, base, own, recv, q_ref, k_ref, v_ref, o_ref, lse_ref, seg_k, seg_q, w_out,
    full_ref, grad_low, dq_ref, dk_ref, dv_ref, dbo, dk_acc, dv_acc, dq_acc, do_ref,
):
    step = pl.program_id(0)

    @pl.when(step == 0)
    def _():
        dk_acc[...] = jnp.zeros_like(dk_acc)
        dv_acc[...] = jnp.zeros_like(dv_acc)

    values = base[...].astype(f32) + (own[...].astype(f32) + recv[...].astype(f32))
    full_ref[...] = values
    low = values.astype(bf16)
    grad_low[...] = low
    accumulate(dbo, jnp.sum(low.astype(f32), axis=0, keepdims=True))
    grad_mixed = None
    for panel in range(TENSOR):
        area = slice(panel * HALF, (panel + 1) * HALF)
        term = dot_nt(low[:, area], w_out[area, :])
        grad_mixed = term if grad_mixed is None else grad_mixed + term
    do_ref[...] = grad_mixed.astype(bf16)
    product = do_ref[...].astype(f32) * o_ref[...].astype(f32)
    head = lax.broadcasted_iota(jnp.int32, (8, HALF), 0)
    lane = lax.broadcasted_iota(jnp.int32, (8, HALF), 1)
    pick = ((lane >= head * HEAD_DIM) & (lane < (head + 1) * HEAD_DIM)).astype(f32)
    inner = dot_nt(pick, product, precise)
    dq_acc[...] = jnp.zeros_like(dq_acc)
    masks = head_masks()
    scale = jnp.asarray(HEAD_DIM ** (-0.5), bf16)
    seg_row = seg_q[...]

    def one_block(block, carried):
        rows = pl.ds(pl.multiple_of(block * ROWS, ROWS), ROWS)
        same = seg_k[rows, :] == seg_row
        for pair in range(HEADS // 2):
            cols = slice(pair * BS, (pair + 1) * BS)
            q_two = q_ref[:, cols] * scale
            do_two = do_ref[:, cols]
            k_two = k_ref[rows, cols]
            v_two = v_ref[rows, cols]
            dv_two = dk_two = dq_two = None
            for side in range(2):
                at = 2 * pair + side
                q_one = q_two * masks[side]
                do_one = do_two * masks[side]
                scores = dot_nt(k_two, q_one)
                prob = jnp.where(same, jnp.exp(scores - lse_ref[at : at + 1, :]), 0.0)
                grad_prob = dot_nt(v_two, do_one)
                grad_scores = (prob * (grad_prob - inner[at : at + 1, :])).astype(bf16)
                dv_one = dot(prob.astype(bf16), do_one)
                dk_one = dot(grad_scores, q_one)
                dq_one = dot_tn(grad_scores, k_two * masks[side])
                dv_two = dv_one if dv_two is None else dv_two + dv_one
                dk_two = dk_one if dk_two is None else dk_two + dk_one
                dq_two = dq_one if dq_two is None else dq_two + dq_one
            dv_acc[rows, cols] += dv_two
            dk_acc[rows, cols] += dk_two
            dq_acc[:, cols] += dq_two
        return carried

    lax.fori_loop(low_ref[step], high_ref[step], one_block, 0)
    dq_ref[...] = (dq_acc[...] * HEAD_DIM ** (-0.5)).astype(bf16)

    @pl.when(step == pl.num_programs(0) - 1)
    def _():
        dk_ref[...] = dk_acc[...].astype(bf16)
        dv_ref[...] = dv_acc[...].astype(bf16)


def attend_back_call(
    layer, first, last, base, own, recv, queries, keys, values, mixed, lse, seg_col, seg_row, panels
):
    tokens = base.shape[0]
    shape = lambda width, kind: jax.ShapeDtypeStruct((tokens, width), kind)
    whole = (tokens, HALF)
    return pl.pallas_call(
        attend_back_kernel,
        out_shape=[
            shape(D, f32),
            shape(D, bf16),
            shape(HALF, bf16),
            shape(HALF, bf16),
            shape(HALF, bf16),
            jax.ShapeDtypeStruct((1, D), f32),
        ],
        grid_spec=pltpu.PrefetchScalarGridSpec(
            num_scalar_prefetch=2,
            grid=(tokens // ROWS,),
            in_specs=[
                rows_spec(D),
                rows_spec(D),
                rows_spec(D),
                rows_spec(HALF),
                fixed(whole),
                fixed(whole),
                rows_spec(HALF),
                pl.BlockSpec((8, ROWS), lambda i, *_: (0, i)),
                fixed(seg_col.shape),
                pl.BlockSpec((1, ROWS), lambda i, *_: (0, i)),
                fixed((D, HALF), PANELS["out"][layer] // D),
            ],
            out_specs=[
                rows_spec(D),
                rows_spec(D),
                rows_spec(HALF),
                fixed(whole),
                fixed(whole),
                fixed((1, D)),
            ],
            scratch_shapes=[
                pltpu.VMEM(whole, f32),
                pltpu.VMEM(whole, f32),
                pltpu.VMEM((ROWS, HALF), f32),
                pltpu.VMEM((ROWS, HALF), bf16),
            ],
        ),
        compiler_params=params(),
        cost_estimate=cost(14 * HEADS * tokens * tokens * BS, tokens * D * 20, HEADS * tokens * tokens),
    )(first, last, base, own, recv, queries, keys, values, mixed, lse, seg_col, seg_row, panels)


def qkv_back_kernel(layer, dq, dk, dv, hid, vec, weight, back, dgain, dshift, dbq, dbv):
    grad_normed = (
        dot_nt(dq[...], weight[0:D, :])
        + dot_nt(dk[...], weight[D : 2 * D, :])
        + dot_nt(dv[...], weight[2 * D : 3 * D, :])
    )
    part_back, gain_grad, shift_grad = norm_back(hid[...], vec_piece(vec, layer, "g1"), grad_normed)
    back[...] = part_back.astype(bf16)
    accumulate(dgain, gain_grad)
    accumulate(dshift, shift_grad)
    accumulate(dbq, jnp.sum(dq[...].astype(f32), axis=0, keepdims=True))
    accumulate(dbv, jnp.sum(dv[...].astype(f32), axis=0, keepdims=True))


def qkv_back_call(layer, dq, dk, dv, hid, vec, panels):
    tokens = dq.shape[0]
    line = lambda width: jax.ShapeDtypeStruct((1, width), f32)
    lines = [line(D), line(D), line(HALF), line(HALF)]
    return pl.pallas_call(
        functools.partial(qkv_back_kernel, layer),
        out_shape=[jax.ShapeDtypeStruct((tokens, D), bf16)] + lines,
        grid=(tokens // ROWS,),
        in_specs=[rows_spec(HALF)] * 3
        + [
            rows_spec(D),
            fixed(vec.shape),
            fixed((3 * D, HALF), PANELS["qkv"][layer] // (3 * D)),
        ],
        out_specs=[rows_spec(D)] + [fixed(o.shape) for o in lines],
        compiler_params=params(),
        cost_estimate=cost(2 * tokens * D * 3 * HALF, tokens * D * 10),
    )(dq, dk, dv, hid, vec, panels)


def split(values):
    high = values.astype(bf16)
    return high, (values - high.astype(f32)).astype(bf16)


def product(left, right, left_dim, right_dim):
    def one(a, b):
        return lax.dot_general(
            a, b, (((left_dim,), (right_dim,)), ((), ())), preferred_element_type=f32
        )

    return one(left[0], right[0]) + (one(left[0], right[1]) + one(left[1], right[0]))


def owner_kernel(per, used, low, master, left, right, moment, variance, grad, out, out_mom, out_var):
    here = range(per)
    first = pl.program_id(0) * per
    lefts = [split(left[i]) for i in here]
    rights = [split(right[i]) for i in here]
    rotated = []
    for i in here:
        tile = jnp.where(used[first + i] > 0, low[i * BS : (i + 1) * BS, :].astype(f32), 0.0)
        grad[i] = tile
        tile = tile.astype(bf16)
        rotated.append(split(dot_tn(lefts[i][0], tile) + dot_tn(lefts[i][1], tile)))
    rotated = [product(rotated[i], rights[i], 1, 0) for i in here]
    steps = []
    for i in here:
        new_moment = decay * moment[i] + (1.0 - decay) * rotated[i]
        new_variance = decay * variance[i] + (1.0 - decay) * rotated[i] * rotated[i]
        out_mom[i] = new_moment
        out_var[i] = new_variance
        steps.append(split(new_moment / (jnp.sqrt(new_variance) + adam_eps)))
    returned = [split(product(lefts[i], steps[i], 1, 0)) for i in here]
    returned = [product(returned[i], rights[i], 1, 1) for i in here]
    for i in here:
        out[i] = master[i] - matrix_rate * returned[i]


def owner_call(used, low, *arrays):
    count = arrays[0].shape[0]
    per = min(8, count)
    block = pl.BlockSpec((per, BS, BS), lambda i, *_: (i, 0, 0))
    return pl.pallas_call(
        functools.partial(owner_kernel, per),
        out_shape=[jax.ShapeDtypeStruct(arrays[0].shape, f32)] * 4,
        grid_spec=pltpu.PrefetchScalarGridSpec(
            num_scalar_prefetch=1,
            grid=(count // per,),
            in_specs=[pl.BlockSpec((per * BS, BS), lambda i, *_: (i, 0))] + [block] * 5,
            out_specs=[block] * 4,
        ),
        compiler_params=params(),
        cost_estimate=cost(count * 88 * BS**3, count * BS * BS * 38),
    )(used, low, *arrays)


class Routes:
    def __init__(self, dp_n):
        pairs = [(d, t) for d in range(dp_n) for t in range(TENSOR)]
        at = lambda d, t: d * TENSOR + t
        home = [(d, t) for d, t in pairs if d % 2 == t]
        away = [(d, t) for d, t in pairs if d % 2 != t]
        self.core_all = [(at(d, t), at(d ^ 1, t)) for d, t in pairs]
        self.core_out = [(at(d, t), at(d ^ 1, t)) for d, t in home]
        self.core_in = [(at(d, t), at(d ^ 1, t)) for d, t in away]
        self.y_all = [(at(d, t), at(d, 1 - t)) for d, t in pairs]
        self.y_out = [(at(d, t), at(d, 1 - t)) for d, t in home]
        self.y_in = [(at(d, t), at(d, 1 - t)) for d, t in away]
        self.x_home = [(at(d, t), at(d ^ 2, t)) for d, t in home]
        self.x_away = [(at(d, t), at(d ^ 2, t)) for d, t in away]
        self.z_home = [(at(d, t), at((d + 4) % dp_n, t)) for d, t in home]


def send(value, route):
    return lax.ppermute(value, AXES, route)


def shards(
    patches,
    cotangent,
    image_size,
    block_slot,
    pinv,
    master_slots,
    left_basis,
    right_basis,
    mom_slots,
    var_slots,
    vec_master,
    vec_mom,
    vec_var,
):
    dp_n = lax.axis_size("dp")
    dp_pos = lax.axis_index("dp")
    y_pos = lax.axis_index("tensor")
    core = dp_pos % 2
    home = core == y_pos
    routes = Routes(dp_n)
    grid3 = dp_n == 16
    tokens_n = patches.shape[0]
    slots_per = master_slots.shape[1]
    vec_per = vec_master.shape[1]
    slots_n = slots_per * dp_n
    payload = slots_per * BS + VEC_ROWS

    patches = jnp.where(home, patches, send(patches, routes.core_out))
    cotangent = jnp.where(home, cotangent, send(cotangent, routes.core_out))
    size_row = jnp.where(home, image_size, send(image_size, routes.core_out))[0]
    own_slots = block_slot[0]
    slot_list = jnp.where(home, block_slot, send(block_slot, routes.y_all))[0]

    lengths = jnp.where(
        size_row == 0, LEN_A, jnp.where(size_row == 1, LEN_B, jnp.where(size_row == 2, LEN_C, 0))
    )
    order = jnp.arange(IMG_DEV)
    ends_at = jnp.sum(jnp.where(order[None, :] <= order[:, None], lengths[None, :], 0), axis=1)
    places = jnp.arange(tokens_n)
    segment = jnp.sum((places[:, None] >= ends_at[None, :]).astype(jnp.int32), axis=1)
    in_image = segment[:, None] == order[None, :]
    select = jnp.stack(
        [jnp.any(in_image & (size_row == s)[None, :], axis=1) for s in range(3)], axis=1
    )
    valid_col = (segment < IMG_DEV).astype(f32)[:, None]
    seg_col = segment[:, None]
    seg_row = segment[None, :]
    blocks_n = tokens_n // ROWS
    starts = jnp.arange(blocks_n) * ROWS
    begun = ends_at[None, :] <= starts[:, None]
    first_tok = jnp.max(jnp.where(begun, ends_at[None, :], 0), axis=1)
    after = ends_at[None, :] > (starts + ROWS - 1)[:, None]
    last_tok = jnp.min(jnp.where(after, ends_at[None, :], tokens_n), axis=1)
    first_blk = (first_tok // ROWS).astype(jnp.int32)
    last_blk = ((last_tok + ROWS - 1) // ROWS).astype(jnp.int32)

    select_low = select.astype(bf16)
    spread_in = patches[:, None, :] * select_low[:, :, None]
    base_pix = lax.dot_general(
        spread_in, pinv, (((1, 2), (0, 2)), ((), ())), preferred_element_type=f32
    ).astype(bf16)

    vec_low = jnp.pad(vec_master[0].astype(bf16), (0, VEC_ROWS * BS - vec_per))
    own_pack = jnp.concatenate(
        [
            master_slots[0].astype(bf16).reshape(slots_per * BS, BS),
            vec_low.reshape(VEC_ROWS, BS),
        ],
        axis=0,
    )
    named = slot_list[None, :] == jnp.arange(slots_n)[:, None]
    used = jnp.any(named, axis=1)
    drow = jnp.where(used, jnp.sum(jnp.where(named, TARGET_ROW[None, :], 0), axis=1), -1)
    dcol = jnp.sum(jnp.where(named, TARGET_COL[None, :], 0), axis=1)
    flag = home.astype(jnp.int32).reshape(1)
    if grid3:
        x_pos = (dp_pos // 2) % 2
        z_pos = dp_pos // 4
        pack = jnp.stack([own_pack, send(own_pack, routes.core_in)], axis=0)
        packs, acrosses, overs, corners = [pack], [], [], []
        for j in range(5):
            moved = []
            if j < 3:
                moved.append(send(packs[j], routes.z_home))
            if j < 4:
                moved += [send(packs[j], routes.x_home), send(packs[j], routes.y_out)]
            if j:
                moved += [
                    send(acrosses[j - 1][0:1], routes.y_out),
                    send(overs[j - 1][1:2], routes.x_away),
                ]
            if j == 1:
                *moved, base_pix = fence(*moved, base_pix)
            elif j < 4:
                moved = list(fence(*moved))
            if j < 3:
                packs.append(moved.pop(0))
            if j < 4:
                acrosses.append(moved.pop(0))
                overs.append(moved.pop(0))
            if j:
                corners.append(moved)
        first, second, owner = [], [], []
        for j in range(4):
            first += [packs[j], acrosses[j]]
            second += [overs[j]] + corners[j]
            for x_rel in range(2):
                for n in range(2):
                    owner.append(((z_pos - j) % 4) * 4 + (x_pos ^ x_rel) * 2 + (core ^ n))
        owner = jnp.stack(owner).astype(jnp.int32)
    else:
        everything = lax.all_gather(own_pack, AXES, axis=0)
        everything = everything.reshape(dp_n, TENSOR, payload, BS)
        first = [jnp.where(core == 0, everything[:, 0], everything[:, 1])]
        second = []
        owner = jnp.arange(dp_n, dtype=jnp.int32)
    panels, vec_rows = gather_tiles(first, second, owner, drow, dcol, flag, slots_per, dp_n)
    vec = vec_rows.reshape(dp_n, VEC_ROWS * BS)[:, :vec_per].astype(f32).reshape(1, dp_n * vec_per)

    base_w = panels[PANELS["base"] : PANELS["base"] + BASE_PIX]
    embedded = (dot(base_pix, base_w) + vec[:, :HALF]).astype(bf16)
    embedded_other = send(embedded, routes.core_all)
    hidden = jnp.concatenate(
        [
            jnp.where(core == 0, embedded, embedded_other),
            jnp.where(core == 0, embedded_other, embedded),
        ],
        axis=1,
    ).astype(f32)

    caches = []
    own = recv = None
    for layer in range(LAYERS):
        made = qkv_call(layer, hidden, own, recv, vec, panels)
        if own is not None:
            hidden, *made = made
        normed, queries, keys, values = made
        mixed, lse, part = attend_call(
            layer, queries, keys, values, seg_col, seg_row, vec, panels
        )
        other = send(part, routes.core_all)
        middle, normed2, act, slope, own = mlp_call(layer, hidden, part, other, vec, panels)
        recv = send(own, routes.core_all)
        caches.append((hidden, normed, queries, keys, values, mixed, lse, middle, normed2, act, slope))
        hidden = middle
    out_low = ((hidden + (own.astype(f32) + recv.astype(f32))) * valid_col).astype(bf16)
    out_other = send(out_low, routes.y_out)

    owners = jnp.arange(dp_n)
    if grid3:
        place = (
            ((z_pos - 1 - owners // 4) % 4) * 4
            + (x_pos ^ ((owners // 2) % 2)) * 2
            + (core ^ (owners % 2))
        ).astype(jnp.int32)
        half_at = x_pos.astype(jnp.int32).reshape(1)
    else:
        place = owners.astype(jnp.int32)
        half_at = jnp.zeros((1,), jnp.int32)
    slot_owner = slot_list // slots_per
    owner_place = jnp.sum(
        jnp.where(slot_owner[:, None] == owners[None, :], place[None, :], 0), axis=1
    )
    tile_pos = (owner_place * payload + (slot_list % slots_per) * BS).astype(jnp.int32)
    vec_pos = (place * payload + slots_per * BS).astype(jnp.int32)
    total_rows = dp_n * payload
    offsets = {"base": 0}
    count = BASE_PIX // BS * (HALF // BS)
    for layer in range(LAYERS):
        for name, size in (("qkv", 3 * D * HALF), ("out", D * HALF), ("up", D * HALF_FF), ("down", D * HALF_FF)):
            offsets[name, layer] = count
            count += size // (BS * BS)

    def place_tiles(key, matrix, arrived, buffer):
        tiles = matrix.size // (BS * BS)
        pos = tile_pos[offsets[key] : offsets[key] + tiles]
        rows_n = matrix.shape[0] // 2 if matrix.shape[0] > HALF else HALF
        return scatter_matrix(pos, matrix, arrived, half_at, buffer, total_rows, rows_n)

    def over(matrix):
        return send(matrix, routes.y_in) if grid3 else None

    def halves_of(matrix):
        size = matrix.shape[0] // 2
        mine = lax.dynamic_slice_in_dim(matrix, x_pos * size, size, 0)
        theirs = lax.dynamic_slice_in_dim(matrix, (1 - x_pos) * size, size, 0)
        return mine, theirs

    def half_sum(matrix, arrived):
        mine, unused = halves_of(matrix)
        return (mine.astype(f32) + arrived.astype(f32)).astype(bf16)

    def beside(matrix):
        return send(halves_of(matrix)[1], routes.x_away) if grid3 else None

    def hold(*arrays):
        kept = [a for a in arrays if a is not None]
        done = iter(fence(*kept))
        return [None if a is None else next(done) for a in arrays]

    top, low = 1, 0
    vec_grads = [None] * LAYERS

    def mlp_step(layer, grad, own, recv):
        middle, normed2, act, slope = caches[layer][7:11]
        made = mlp_back_call(layer, grad, own, recv, valid_col, middle, slope, vec, panels)
        if own is not None:
            return made
        return [made[0]] + list(made)

    def attend_step(layer, grad, part, other):
        hid_in, normed, queries, keys, values, mixed, lse = caches[layer][:7]
        return attend_back_call(
            layer, first_blk, last_blk, grad, part, other, queries, keys, values, mixed, lse,
            seg_col, seg_row, panels,
        )

    grad, grad_low, du, part, dg2, ds2, db1, db2 = mlp_step(top, cotangent, None, None)
    other = send(part, routes.core_all)
    gd1 = dot_tn(caches[top][9], grad_low).astype(bf16)
    gu1 = dot_tn(caches[top][8], du).astype(bf16)
    part, other, gd1, gu1, out_other = fence(part, other, gd1, gu1, out_other)
    output = jnp.where(home, out_low, out_other).astype(f32)
    ad1 = over(gd1)
    grad, grad_low, dq, dk, dv, dbo = attend_step(top, grad, part, other)
    dq, dk, dv, ad1 = hold(dq, dk, dv, ad1)
    au1 = over(gu1)
    own, dg1, ds1, dbq, dbv = qkv_back_call(top, dq, dk, dv, caches[top][0], vec, panels)
    recv = send(own, routes.core_all)
    go1 = dot_tn(caches[top][5], grad_low).astype(bf16)
    gq1 = dot_tn(caches[top][1], jnp.concatenate([dq, dk, dv], axis=1)).astype(bf16)
    vec_grads[top] = [dg1, ds1, dbq, dbv, dbo, dg2, ds2, db1, db2]
    grad, grad_low, du, part, dg2, ds2, db1, db2 = mlp_step(low, grad, own, recv)
    du, part, au1, go1, gq1 = hold(du, part, au1, go1, gq1)
    other = send(part, routes.core_all)
    xq1, ao1 = beside(gq1), over(go1)
    gd0 = dot_tn(caches[low][9], grad_low).astype(bf16)
    gu0 = dot_tn(caches[low][8], du).astype(bf16)
    part, other, gd0, gu0, xq1, ao1 = hold(part, other, gd0, gu0, xq1, ao1)
    aq1 = over(half_sum(gq1, xq1)) if grid3 else None
    xd0, xu0 = beside(gd0), beside(gu0)
    buffer = place_tiles(("down", top), gd1, ad1, None)
    buffer = place_tiles(("up", top), gu1, au1, buffer)
    grad, grad_low, dq, dk, dv, dbo = attend_step(low, grad, part, other)
    grad, grad_low, dq, dk, dv, aq1, xd0, xu0, buffer = hold(
        grad, grad_low, dq, dk, dv, aq1, xd0, xu0, buffer
    )
    hd0 = half_sum(gd0, xd0) if grid3 else None
    hu0 = half_sum(gu0, xu0) if grid3 else None
    go0 = dot_tn(caches[low][5], grad_low).astype(bf16)
    gq0 = dot_tn(caches[low][1], jnp.concatenate([dq, dk, dv], axis=1)).astype(bf16)
    dq, dk, dv, hd0, hu0, go0, gq0 = hold(dq, dk, dv, hd0, hu0, go0, gq0)
    ad0, au0 = over(hd0), over(hu0)
    xq0 = beside(gq0)
    own, dg1, ds1, dbq, dbv = qkv_back_call(low, dq, dk, dv, caches[low][0], vec, panels)
    recv = send(own, routes.core_all)
    vec_grads[low] = [dg1, ds1, dbq, dbv, dbo, dg2, ds2, db1, db2]
    sides = [
        grad[:, s * HALF : (s + 1) * HALF]
        + (
            own[:, s * HALF : (s + 1) * HALF].astype(f32)
            + recv[:, s * HALF : (s + 1) * HALF].astype(f32)
        )
        for s in range(TENSOR)
    ]
    grad_emb = jnp.where(core == 0, sides[0], sides[1]).astype(bf16)
    grad_emb_bias = jnp.sum(grad_emb.astype(f32), axis=0, keepdims=True)
    gb = dot_tn(base_pix, grad_emb).astype(bf16)
    vec_grad = jnp.concatenate([grad_emb_bias] + vec_grads[0] + vec_grads[1], axis=1)[0]
    vec_grad = jnp.pad(vec_grad, (0, dp_n * vec_per - vec_grad.shape[0])).reshape(dp_n, vec_per)
    vec_grad = jnp.pad(vec_grad, ((0, 0), (0, VEC_ROWS * BS - vec_per)))
    vec_grad = vec_grad.astype(bf16).reshape(dp_n, VEC_ROWS, BS)
    gb, vec_grad, grad_emb, gq0, xq0 = hold(gb, vec_grad, grad_emb, gq0, xq0)
    xb = beside(gb)
    aq0 = over(half_sum(gq0, xq0)) if grid3 else None
    ao0, av = over(go0), over(vec_grad)
    buffer = place_tiles(("out", top), go1, ao1, buffer)
    buffer = place_tiles(("qkv", top), gq1, aq1, buffer)
    buffer = place_tiles(("down", low), gd0, ad0, buffer)
    buffer = place_tiles(("up", low), gu0, au0, buffer)
    xb, buffer = hold(xb, buffer)
    ab = over(half_sum(gb, xb)) if grid3 else None
    buffer = place_tiles(("out", low), go0, ao0, buffer)
    buffer = scatter_vec(vec_pos, vec_grad, av, buffer)
    buffer = place_tiles(("qkv", low), gq0, aq0, buffer)
    ab, buffer, panels, grad_emb = hold(ab, buffer, panels, grad_emb)
    buffer = place_tiles("base", gb, ab, buffer)

    def pixel_part(which):
        base_here = panels[PANELS["base"] : PANELS["base"] + BASE_PIX]
        return dot_tn(pinv[which], base_here).astype(bf16)

    resized = []
    grad_pixels = None
    if grid3:
        order = (1, 0)
        block_of = lambda j, x_rel, n: buffer.reshape(4, 2, 2, payload, BS)[j, x_rel, n]
        across = {n: send(block_of(0, 1, n), routes.x_home) for n in order}
        carried = {n: None for n in order}
        rounded = {}
        for j in range(4):
            for n in order:
                extra = []
                if j == 0 or (j == 1 and n == order[0]):
                    extra = [pixel_part(len(resized))]
                elif j == 1:
                    grad_pixels = sum(
                        dot_nt(grad_emb * select_low[:, s : s + 1], resized[s]) for s in range(3)
                    ).astype(bf16)
                    extra = [grad_pixels]
                across[n], buffer, carried[n], *extra = hold(across[n], buffer, carried[n], *extra)
                if j == 0 or (j == 1 and n == order[0]):
                    resized += extra
                elif j == 1:
                    [grad_pixels] = extra
                total = block_of(j, 0, n).astype(f32) + across[n].astype(f32)
                if carried[n] is not None:
                    total = total + carried[n].astype(f32)
                if j < 3:
                    carried[n] = send(total.astype(bf16), routes.z_home)
                    across[n] = send(block_of(j + 1, 1, n), routes.x_home)
                else:
                    rounded[n] = total.astype(bf16)
        mine = jnp.where(home, rounded[0], send(rounded[1], routes.core_out))
    else:
        held = buffer.reshape(dp_n, 1, payload, BS).astype(f32)
        nothing = jnp.zeros_like(held)
        both = jnp.concatenate(
            [jnp.where(core == 0, held, nothing), jnp.where(core == 0, nothing, held)], axis=1
        )
        used_rows = jnp.repeat(used, BS).reshape(dp_n, 1, slots_per * BS, 1)
        used_rows = jnp.concatenate(
            [used_rows, jnp.ones((dp_n, 1, VEC_ROWS, 1), bool)], axis=2
        )
        both = jnp.where(used_rows, both, 0.0).reshape(dp_n * TENSOR * payload, BS)
        mine = lax.psum_scatter(both, AXES, scatter_dimension=0, tiled=True).astype(bf16)
        resized = [pixel_part(s) for s in range(3)]
        grad_pixels = sum(
            dot_nt(grad_emb * select_low[:, s : s + 1], resized[s]) for s in range(3)
        ).astype(bf16)

    pixels_other = send(grad_pixels, routes.core_all)
    pixel_sides = [
        grad_pixels[:, s * HALF : (s + 1) * HALF].astype(f32)
        + pixels_other[:, s * HALF : (s + 1) * HALF].astype(f32)
        for s in range(TENSOR)
    ]
    near = jnp.where(core == 0, pixel_sides[0], pixel_sides[1])
    far = jnp.where(core == 0, pixel_sides[1], pixel_sides[0]).astype(bf16)
    patch_grad = jnp.where(home, near, send(far, routes.y_out).astype(f32))

    my_slots = dp_pos * slots_per + jnp.arange(slots_per)
    mine_used = jnp.any(own_slots[None, :] == my_slots[:, None], axis=1).astype(jnp.int32)
    owned_grad, new_master, new_mom, new_var = owner_call(
        mine_used, mine, master_slots[0], left_basis[0], right_basis[0], mom_slots[0], var_slots[0]
    )
    owned_vec_grad = mine[slots_per * BS :].astype(f32).reshape(VEC_ROWS * BS)[:vec_per]
    new_vec_mom = decay * vec_mom[0] + (1.0 - decay) * owned_vec_grad
    new_vec_var = decay * vec_var[0] + (1.0 - decay) * owned_vec_grad * owned_vec_grad
    new_vec = vec_master[0] - vector_rate * new_vec_mom / (jnp.sqrt(new_vec_var) + adam_eps)
    return (
        output,
        patch_grad,
        owned_grad[None],
        new_master[None],
        new_mom[None],
        new_var[None],
        owned_vec_grad[None],
        new_vec[None],
        new_vec_mom[None],
        new_vec_var[None],
    )


def solution(mesh):
    slots = P("tensor", "dp", None, None)
    vectors = P("tensor", "dp")
    tokens = P("dp", None)
    in_specs = (tokens, tokens, tokens, P("tensor", None), P()) + (slots,) * 5 + (vectors,) * 3
    out_specs = (tokens, P("dp", "tensor")) + (slots,) * 4 + (vectors,) * 4
    return jax.shard_map(shards, mesh=mesh, in_specs=in_specs, out_specs=out_specs, check_vma=False)
```

```python
import functools

import jax
import jax.numpy as jnp
import numpy as np
from jax import lax
from jax.experimental import pallas as pl
from jax.experimental.pallas import tpu as pltpu
from jax.sharding import PartitionSpec as P

D = 768
HEAD_DIM = 64
FF = 3072
BASE_PIX = 3072
LAYERS = 2
LEN_A = 196
LEN_B = 225
LEN_C = 576
IMG_DEV = 5
BS = 128
TENSOR = 2
HALF = D // TENSOR
HALF_FF = FF // TENSOR
HEADS = HALF // HEAD_DIM
ROWS = 256
VEC_ROWS = 16
CHUNKS = 4

AXES = ("dp", "tensor")
precise = lax.Precision.HIGHEST
masked_score = -1e30
norm_eps = 1e-06
adam_eps = 1e-08
decay = 0.5
matrix_rate = 0.05
vector_rate = 0.3
f32 = jnp.float32
bf16 = jnp.bfloat16
BIG_VMEM = 56 * 1024 * 1024

PANELS = {
    "up": (0, 6144),
    "down": (3072, 9216),
    "base": 12288,
    "out": (15360, 20736),
    "qkv": (16128, 18432),
}
PANEL_ROWS = 21504


def tile_targets():
    rows, cols = [], []

    def add(start, rows_n, cols_n):
        for i in range(rows_n // BS):
            for j in range(cols_n // BS):
                panel, inner = divmod(j * BS, HALF)
                rows.append(start + panel * rows_n + i * BS)
                cols.append(inner)

    add(PANELS["base"], BASE_PIX, HALF)
    for layer in range(LAYERS):
        add(PANELS["qkv"][layer], D, 3 * HALF)
        add(PANELS["out"][layer], HALF, D)
        add(PANELS["up"][layer], D, HALF_FF)
        add(PANELS["down"][layer], HALF_FF, D)
    return np.array(rows, np.int32), np.array(cols, np.int32)


TARGET_ROW, TARGET_COL = tile_targets()
LAYER_VECS = (D, D, HALF, HALF, D, D, D, HALF_FF, D)
VEC_NAMES = ("g1", "s1", "bq", "bv", "bo", "g2", "s2", "b1", "b2")


def vec_offsets():
    offset = HALF
    found = []
    for layer in range(LAYERS):
        here = {}
        for name, length in zip(VEC_NAMES, LAYER_VECS):
            here[name] = (offset, length)
            offset += length
        found.append(here)
    return found


VEC_AT = vec_offsets()


def params(limit=BIG_VMEM):
    return pltpu.CompilerParams(
        dimension_semantics=("arbitrary",), vmem_limit_bytes=limit
    )


def cost(flops, nbytes, trans=0):
    return pl.CostEstimate(flops=flops, bytes_accessed=nbytes, transcendentals=trans)


def rows_spec(width):
    return pl.BlockSpec((ROWS, width), lambda i, *_: (i, 0))


def fixed(shape, at=0):
    return pl.BlockSpec(shape, lambda i, *_: (at,) + (0,) * (len(shape) - 1))


def vec_piece(vec_ref, layer, name):
    start, length = VEC_AT[layer][name]
    return vec_ref[:, start : start + length]


def dot(left, right):
    return jnp.dot(left, right, preferred_element_type=f32)


def dot_nt(left, right, precision=None):
    return lax.dot_general(
        left, right, (((1,), (1,)), ((), ())), precision=precision, preferred_element_type=f32
    )


def dot_tn(left, right):
    return lax.dot_general(left, right, (((0,), (0,)), ((), ())), preferred_element_type=f32)


def norm_stats(values):
    mean_val = jnp.mean(values, axis=-1, keepdims=True)
    centered = values - mean_val
    inv_std = lax.rsqrt(jnp.mean(centered * centered, axis=-1, keepdims=True) + norm_eps)
    return centered * inv_std, inv_std


def norm_back(values, gain, grad):
    unit, inv_std = norm_stats(values)
    scaled = grad * gain
    mean_s = jnp.mean(scaled, axis=-1, keepdims=True)
    mean_u = jnp.mean(scaled * unit, axis=-1, keepdims=True)
    back = inv_std * (scaled - mean_s - unit * mean_u)
    return (
        back,
        jnp.sum(grad * unit, axis=0, keepdims=True),
        jnp.sum(grad, axis=0, keepdims=True),
    )


def accumulate(ref, value):
    first = pl.program_id(0) == 0

    @pl.when(first)
    def _():
        ref[...] = value

    @pl.when(jnp.logical_not(first))
    def _():
        ref[...] += value


def fence(*arrays):
    def nothing(*refs):
        pass

    anywhere = pl.BlockSpec(memory_space=pl.ANY)
    return pl.pallas_call(
        nothing,
        out_shape=[jax.ShapeDtypeStruct(a.shape, a.dtype) for a in arrays],
        in_specs=[anywhere] * len(arrays),
        out_specs=[anywhere] * len(arrays),
        input_output_aliases={i: i for i in range(len(arrays))},
    )(*arrays)


def gather_kernel(slots, count_a, count_b, owner, drow, dcol, flag, *refs):
    first = refs[:count_a]
    second = refs[count_a : count_a + count_b]
    panels, vectors, held, sem, vec_sem = refs[count_a + count_b :]

    def copy_all(sources):
        at = 0
        for src in sources:
            for n in range(src.shape[0]):
                who = owner[at]
                at += 1

                def body(i, carried, src=src, n=n, who=who):
                    slot = who * slots + i
                    row = drow[slot]

                    @pl.when(row >= 0)
                    def _():
                        start = pl.multiple_of(i * BS, BS)
                        pltpu.make_async_copy(
                            src.at[n, pl.ds(start, BS), :],
                            held.at[
                                pl.ds(pl.multiple_of(row, BS), BS),
                                pl.ds(pl.multiple_of(dcol[slot], BS), BS),
                            ],
                            sem,
                        ).start()

                    return carried

                lax.fori_loop(0, slots, body, 0)
                pltpu.make_async_copy(
                    src.at[n, pl.ds(slots * BS, VEC_ROWS), :], vectors.at[who], vec_sem
                ).start()

    if count_b:

        @pl.when(flag[0] == 1)
        def _():
            copy_all(first)

        @pl.when(flag[0] == 0)
        def _():
            copy_all(second)
    else:
        copy_all(first)
    pltpu.make_async_copy(held, held, sem).wait()
    out = pltpu.make_async_copy(held, panels, sem)
    out.start()
    pltpu.make_async_copy(vectors, vectors, vec_sem).wait()
    out.wait()


def gather_tiles(first, second, owner, drow, dcol, flag, slots, owners):
    anywhere = pl.BlockSpec(memory_space=pl.ANY)
    return pl.pallas_call(
        functools.partial(gather_kernel, slots, len(first), len(second)),
        out_shape=(
            jax.ShapeDtypeStruct((PANEL_ROWS, HALF), bf16),
            jax.ShapeDtypeStruct((owners, VEC_ROWS, BS), bf16),
        ),
        grid_spec=pltpu.PrefetchScalarGridSpec(
            num_scalar_prefetch=4,
            grid=(1,),
            in_specs=[anywhere] * (len(first) + len(second)),
            out_specs=(anywhere, fixed((owners, VEC_ROWS, BS))),
            scratch_shapes=[
                pltpu.VMEM((PANEL_ROWS, HALF), bf16),
                pltpu.SemaphoreType.DMA,
                pltpu.SemaphoreType.DMA,
            ],
        ),
        compiler_params=params(),
        cost_estimate=cost(0, 4 * PANEL_ROWS * HALF),
    )(owner, drow, dcol, flag, *first, *second)


def scatter_kernel(rows_n, cols_n, steps, paired, parts, pos, part, own, *refs):
    if paired:
        recv, *refs = refs
        span = pl.num_programs(0) // parts
        here = jnp.logical_or(parts == 1, pl.program_id(0) // span == part[0])
    target, buf, sems = refs[-3:]
    step = pl.program_id(0)
    slot = lax.rem(step, 2)
    per = rows_n // BS * (cols_n // BS)

    def wait(at):
        pltpu.make_async_copy(buf.at[at], buf.at[at], sems.at[at]).wait()

    @pl.when(step >= 2)
    def _():
        wait(slot)

    for i in range(rows_n // BS):
        for j in range(cols_n // BS):
            area = (slice(i * BS, (i + 1) * BS), slice(j * BS, (j + 1) * BS))
            value = own[area]
            if paired:
                more = jnp.where(here, recv[area].astype(f32), 0.0)
                value = (value.astype(f32) + more).astype(bf16)
            buf[slot, i * (cols_n // BS) + j] = value
    for n in range(per):
        pltpu.make_async_copy(
            buf.at[slot, n],
            target.at[pl.ds(pl.multiple_of(pos[step * per + n], 16), BS), :],
            sems.at[slot],
        ).start()

    @pl.when(step == pl.num_programs(0) - 1)
    def _():
        if steps > 1:
            wait(1 - slot)
        wait(slot)


def scatter_matrix(pos, own, recv, part, target, total_rows, rows_n):
    cols_n = own.shape[1]
    steps = own.shape[0] // rows_n
    anywhere = pl.BlockSpec(memory_space=pl.ANY)
    block = pl.BlockSpec((rows_n, cols_n), lambda i, *_: (i, 0))
    paired = recv is not None
    parts = own.shape[0] // recv.shape[0] if paired else 1
    span = steps // parts
    arrived = pl.BlockSpec(
        (rows_n, cols_n), lambda i, pos, part: (jnp.clip(i - part[0] * span, 0, span - 1), 0)
    )
    operands = [own] + ([recv] if paired else []) + ([] if target is None else [target])
    specs = [block] + ([block if parts == 1 else arrived] if paired else [])
    specs += [] if target is None else [anywhere]
    return pl.pallas_call(
        functools.partial(scatter_kernel, rows_n, cols_n, steps, paired, parts),
        out_shape=jax.ShapeDtypeStruct((total_rows, BS), bf16),
        grid_spec=pltpu.PrefetchScalarGridSpec(
            num_scalar_prefetch=2,
            grid=(steps,),
            in_specs=specs,
            out_specs=anywhere,
            scratch_shapes=[
                pltpu.VMEM((2, rows_n // BS * (cols_n // BS), BS, BS), bf16),
                pltpu.SemaphoreType.DMA((2,)),
            ],
        ),
        input_output_aliases={} if target is None else {len(operands) + 1: 0},
        compiler_params=params(),
        cost_estimate=cost(own.size, own.size * 6),
    )(pos, part, *operands)


def scatter_vec_kernel(paired, pos, own, *refs):
    if paired:
        recv, *refs = refs
    target, buf, sem = refs[-3:]
    value = own[...]
    if paired:
        value = (value.astype(f32) + recv[...].astype(f32)).astype(bf16)
    buf[...] = value

    def body(n, carried):
        pltpu.make_async_copy(
            buf.at[n], target.at[pl.ds(pl.multiple_of(pos[n], 16), VEC_ROWS), :], sem
        ).start()
        return carried

    lax.fori_loop(0, own.shape[0], body, 0)
    pltpu.make_async_copy(buf, buf, sem).wait()


def scatter_vec(pos, own, recv, target):
    anywhere = pl.BlockSpec(memory_space=pl.ANY)
    block = fixed(own.shape)
    paired = recv is not None
    operands = [own] + ([recv] if paired else []) + [target]
    return pl.pallas_call(
        functools.partial(scatter_vec_kernel, paired),
        out_shape=jax.ShapeDtypeStruct(target.shape, bf16),
        grid_spec=pltpu.PrefetchScalarGridSpec(
            num_scalar_prefetch=1,
            grid=(1,),
            in_specs=[block] * (len(operands) - 1) + [anywhere],
            out_specs=anywhere,
            scratch_shapes=[pltpu.VMEM(own.shape, bf16), pltpu.SemaphoreType.DMA],
        ),
        input_output_aliases={len(operands): 0},
        compiler_params=params(),
    )(pos, *operands)


def embed_kernel(*refs):
    *parts, vec, weight, out = refs
    size = BASE_PIX // CHUNKS
    total = vec[:, :HALF]
    for c in range(CHUNKS):
        total = total + dot(parts[c][...], weight[c * size : (c + 1) * size, :])
    out[...] = total.astype(bf16)


def embed_call(chunks, vec, panels):
    tokens = chunks[0].shape[0]
    return pl.pallas_call(
        embed_kernel,
        out_shape=jax.ShapeDtypeStruct((tokens, HALF), bf16),
        grid=(tokens // ROWS,),
        in_specs=[rows_spec(BASE_PIX // CHUNKS)] * CHUNKS
        + [fixed(vec.shape), fixed((BASE_PIX, HALF), PANELS["base"] // BASE_PIX)],
        out_specs=rows_spec(HALF),
        compiler_params=params(),
        cost_estimate=cost(2 * tokens * BASE_PIX * HALF, tokens * BASE_PIX * 3),
    )(*chunks, vec, panels)


def qkv_kernel(layer, first, core, *refs):
    if first:
        own, recv, vec, weight, hid, normed, q_ref, k_ref, v_ref = refs
        mine, theirs = own[...].astype(f32), recv[...].astype(f32)
        low = core[0] == 0
        values = jnp.concatenate(
            [jnp.where(low, mine, theirs), jnp.where(low, theirs, mine)], axis=1
        )
    else:
        base, own, recv, vec, weight, hid, normed, q_ref, k_ref, v_ref = refs
        values = base[...] + (own[...].astype(f32) + recv[...].astype(f32))
    hid[...] = values
    unit, unused = norm_stats(values)
    low = (unit * vec_piece(vec, layer, "g1") + vec_piece(vec, layer, "s1")).astype(bf16)
    normed[...] = low
    q_ref[...] = (dot(low, weight[0:D, :]) + vec_piece(vec, layer, "bq")).astype(bf16)
    k_ref[...] = dot(low, weight[D : 2 * D, :]).astype(bf16)
    v_ref[...] = (dot(low, weight[2 * D : 3 * D, :]) + vec_piece(vec, layer, "bv")).astype(bf16)


def qkv_call(layer, base, own, recv, core, vec, panels):
    tokens = own.shape[0]
    shape = lambda width, kind: jax.ShapeDtypeStruct((tokens, width), kind)
    outs = [shape(D, f32), shape(D, bf16)] + [shape(HALF, bf16)] * 3
    operands = ([] if base is None else [base]) + [own, recv]
    return pl.pallas_call(
        functools.partial(qkv_kernel, layer, base is None),
        out_shape=outs,
        grid_spec=pltpu.PrefetchScalarGridSpec(
            num_scalar_prefetch=1,
            grid=(tokens // ROWS,),
            in_specs=[rows_spec(o.shape[1]) for o in operands]
            + [fixed(vec.shape), fixed((3 * D, HALF), PANELS["qkv"][layer] // (3 * D))],
            out_specs=[rows_spec(o.shape[1]) for o in outs],
        ),
        compiler_params=params(),
        cost_estimate=cost(2 * tokens * D * 3 * HALF, tokens * D * 14),
    )(core, *operands, vec, panels)


def head_masks():
    lane = lax.broadcasted_iota(jnp.int32, (1, 2 * HEAD_DIM), 1)
    low = (lane < HEAD_DIM).astype(f32).astype(bf16)
    high = (lane >= HEAD_DIM).astype(f32).astype(bf16)
    return low, high


def attend_kernel(layer, q_ref, k_ref, v_ref, seg_q, seg_k, vec, w_out, o_ref, lse_ref, part):
    masks = head_masks()
    same = seg_q[...] == seg_k[...]
    lane = lax.broadcasted_iota(jnp.int32, (ROWS, BS), 1)
    totals = jnp.zeros((ROWS, BS), f32)
    scale = jnp.asarray(HEAD_DIM ** (-0.5), bf16)
    for pair in range(HEADS // 2):
        cols = slice(pair * BS, (pair + 1) * BS)
        q_two = q_ref[:, cols] * scale
        k_two = k_ref[:, cols]
        v_two = v_ref[:, cols]
        mixed = None
        for side in range(2):
            scores = dot_nt(q_two * masks[side], k_two)
            scores = jnp.where(same, scores, masked_score)
            top = jnp.max(scores, axis=1, keepdims=True)
            expo = jnp.exp(scores - top)
            total = jnp.sum(expo, axis=1, keepdims=True)
            weights = (expo * (1.0 / total)).astype(bf16)
            term = dot(weights, v_two * masks[side])
            mixed = term if mixed is None else mixed + term
            totals = jnp.where(lane == 2 * pair + side, top + jnp.log(total), totals)
        o_ref[:, cols] = mixed.astype(bf16)
    lse_ref[...] = totals.T[0:8, :]
    low = o_ref[...]
    bias = vec_piece(vec, layer, "bo")
    for panel in range(TENSOR):
        area = slice(panel * HALF, (panel + 1) * HALF)
        part[:, area] = (dot(low, w_out[area, :]) + bias[:, area]).astype(bf16)


def attend_call(layer, queries, keys, values, seg_col, seg_row, vec, panels):
    tokens = queries.shape[0]
    return pl.pallas_call(
        functools.partial(attend_kernel, layer),
        out_shape=[
            jax.ShapeDtypeStruct((tokens, HALF), bf16),
            jax.ShapeDtypeStruct((8, tokens), f32),
            jax.ShapeDtypeStruct((tokens, D), bf16),
        ],
        grid=(tokens // ROWS,),
        in_specs=[
            rows_spec(HALF),
            fixed(keys.shape),
            fixed(values.shape),
            rows_spec(1),
            fixed(seg_row.shape),
            fixed(vec.shape),
            fixed((D, HALF), PANELS["out"][layer] // D),
        ],
        out_specs=[
            rows_spec(HALF),
            pl.BlockSpec((8, ROWS), lambda i: (0, i)),
            rows_spec(D),
        ],
        compiler_params=params(),
        cost_estimate=cost(8 * HEADS * tokens * tokens * BS, tokens * D * 8, HEADS * tokens * tokens),
    )(queries, keys, values, seg_col, seg_row, vec, panels)


def gelu_parts(values):
    cdf = 0.5 * (1.0 + lax.erf(values * 0.7071067811865476))
    pdf = 0.3989422804014327 * jnp.exp(-0.5 * values * values)
    return values * cdf, cdf + values * pdf


def mlp_kernel(layer, base, own, recv, vec, w_up, w_down, hid, normed, act, slope, part):
    values = base[...] + (own[...].astype(f32) + recv[...].astype(f32))
    hid[...] = values
    unit, unused = norm_stats(values)
    low = (unit * vec_piece(vec, layer, "g2") + vec_piece(vec, layer, "s2")).astype(bf16)
    normed[...] = low
    bias_up = vec_piece(vec, layer, "b1")
    for panel in range(HALF_FF // HALF):
        area = slice(panel * HALF, (panel + 1) * HALF)
        up = dot(low, w_up[panel * D : (panel + 1) * D, :]) + bias_up[:, area]
        gelu, grad = gelu_parts(up)
        act[:, area] = gelu.astype(bf16)
        slope[:, area] = grad.astype(bf16)
    bias_down = vec_piece(vec, layer, "b2")
    hidden_units = act[...]
    for panel in range(TENSOR):
        area = slice(panel * HALF, (panel + 1) * HALF)
        down = dot(hidden_units, w_down[panel * HALF_FF : (panel + 1) * HALF_FF, :])
        part[:, area] = (down + bias_down[:, area]).astype(bf16)


def mlp_call(layer, base, own, recv, vec, panels):
    tokens = base.shape[0]
    shape = lambda width, kind: jax.ShapeDtypeStruct((tokens, width), kind)
    outs = [shape(D, f32), shape(D, bf16), shape(HALF_FF, bf16), shape(HALF_FF, bf16), shape(D, bf16)]
    return pl.pallas_call(
        functools.partial(mlp_kernel, layer),
        out_shape=outs,
        grid=(tokens // ROWS,),
        in_specs=[rows_spec(D)] * 3
        + [
            fixed(vec.shape),
            fixed((2 * HALF_FF, HALF), PANELS["up"][layer] // (2 * HALF_FF)),
            fixed((2 * HALF_FF, HALF), PANELS["down"][layer] // (2 * HALF_FF)),
        ],
        out_specs=[rows_spec(o.shape[1]) for o in outs],
        compiler_params=params(),
        cost_estimate=cost(4 * tokens * D * HALF_FF, tokens * D * 24, 2 * tokens * HALF_FF),
    )(base, own, recv, vec, panels, panels)


def mlp_back_kernel(layer, summed, *refs):
    if summed:
        base, own, recv, *refs = refs
        (hid, slope, vec, w_up, w_down, grad_full, grad_low, du_ref, back, dgain, dshift, db1, db2) = refs
        values = base[...].astype(f32) + (own[...].astype(f32) + recv[...].astype(f32))
        grad_full[...] = values
        low = values.astype(bf16)
    else:
        base, valid, *refs = refs
        (hid, slope, vec, w_up, w_down, grad_low, du_ref, back, dgain, dshift, db1, db2) = refs
        low = (base[...].astype(f32) * valid[...]).astype(bf16)
    grad_low[...] = low
    accumulate(db2, jnp.sum(low.astype(f32), axis=0, keepdims=True))
    for part in range(HALF_FF // HALF):
        area = slice(part * HALF, (part + 1) * HALF)
        grad_act = None
        for panel in range(TENSOR):
            start = panel * HALF_FF + part * HALF
            term = dot_nt(low[:, panel * HALF : (panel + 1) * HALF], w_down[start : start + HALF, :])
            grad_act = term if grad_act is None else grad_act + term
        du_ref[:, area] = (grad_act * slope[:, area].astype(f32)).astype(bf16)
    grad_normed = None
    for panel in range(HALF_FF // HALF):
        area = slice(panel * HALF, (panel + 1) * HALF)
        term = dot_nt(du_ref[:, area], w_up[panel * D : (panel + 1) * D, :])
        grad_normed = term if grad_normed is None else grad_normed + term
    accumulate(db1, jnp.sum(du_ref[...].astype(f32), axis=0, keepdims=True))
    part_back, gain_grad, shift_grad = norm_back(hid[...], vec_piece(vec, layer, "g2"), grad_normed)
    back[...] = part_back.astype(bf16)
    accumulate(dgain, gain_grad)
    accumulate(dshift, shift_grad)


def mlp_back_call(layer, base, own, recv, valid, hid, slope, vec, panels):
    tokens = base.shape[0]
    summed = own is not None
    shape = lambda width, kind: jax.ShapeDtypeStruct((tokens, width), kind)
    line = lambda width: jax.ShapeDtypeStruct((1, width), f32)
    outs = ([shape(D, f32)] if summed else []) + [shape(D, bf16), shape(HALF_FF, bf16), shape(D, bf16)]
    lines = [line(D), line(D), line(HALF_FF), line(D)]
    extra = [own, recv] if summed else [valid]
    return pl.pallas_call(
        functools.partial(mlp_back_kernel, layer, summed),
        out_shape=outs + lines,
        grid=(tokens // ROWS,),
        in_specs=[rows_spec(D)]
        + [rows_spec(e.shape[1]) for e in extra]
        + [
            rows_spec(D),
            rows_spec(HALF_FF),
            fixed(vec.shape),
            fixed((2 * HALF_FF, HALF), PANELS["up"][layer] // (2 * HALF_FF)),
            fixed((2 * HALF_FF, HALF), PANELS["down"][layer] // (2 * HALF_FF)),
        ],
        out_specs=[rows_spec(o.shape[1]) for o in outs] + [fixed(o.shape) for o in lines],
        compiler_params=params(),
        cost_estimate=cost(4 * tokens * D * HALF_FF, tokens * D * 24),
    )(base, *extra, hid, slope, vec, panels, panels)


def attend_back_kernel(
    low_ref, high_ref, base, own, recv, q_ref, k_ref, v_ref, o_ref, lse_ref, seg_k, seg_q, w_out,
    full_ref, grad_low, dq_ref, dk_ref, dv_ref, dbo, dk_acc, dv_acc, dq_acc, do_ref,
):
    step = pl.program_id(0)

    @pl.when(step == 0)
    def _():
        dk_acc[...] = jnp.zeros_like(dk_acc)
        dv_acc[...] = jnp.zeros_like(dv_acc)

    values = base[...].astype(f32) + (own[...].astype(f32) + recv[...].astype(f32))
    full_ref[...] = values
    low = values.astype(bf16)
    grad_low[...] = low
    accumulate(dbo, jnp.sum(low.astype(f32), axis=0, keepdims=True))
    grad_mixed = None
    for panel in range(TENSOR):
        area = slice(panel * HALF, (panel + 1) * HALF)
        term = dot_nt(low[:, area], w_out[area, :])
        grad_mixed = term if grad_mixed is None else grad_mixed + term
    do_ref[...] = grad_mixed.astype(bf16)
    product = do_ref[...].astype(f32) * o_ref[...].astype(f32)
    head = lax.broadcasted_iota(jnp.int32, (8, HALF), 0)
    lane = lax.broadcasted_iota(jnp.int32, (8, HALF), 1)
    pick = ((lane >= head * HEAD_DIM) & (lane < (head + 1) * HEAD_DIM)).astype(f32)
    inner = dot_nt(pick, product, precise)
    dq_acc[...] = jnp.zeros_like(dq_acc)
    masks = head_masks()
    scale = jnp.asarray(HEAD_DIM ** (-0.5), bf16)
    seg_row = seg_q[...]

    def one_block(block, carried):
        rows = pl.ds(pl.multiple_of(block * ROWS, ROWS), ROWS)
        same = seg_k[rows, :] == seg_row
        for pair in range(HEADS // 2):
            cols = slice(pair * BS, (pair + 1) * BS)
            q_two = q_ref[:, cols] * scale
            do_two = do_ref[:, cols]
            k_two = k_ref[rows, cols]
            v_two = v_ref[rows, cols]
            dv_two = dk_two = dq_two = None
            for side in range(2):
                at = 2 * pair + side
                q_one = q_two * masks[side]
                do_one = do_two * masks[side]
                scores = dot_nt(k_two, q_one)
                prob = jnp.where(same, jnp.exp(scores - lse_ref[at : at + 1, :]), 0.0)
                grad_prob = dot_nt(v_two, do_one)
                grad_scores = (prob * (grad_prob - inner[at : at + 1, :])).astype(bf16)
                dv_one = dot(prob.astype(bf16), do_one)
                dk_one = dot(grad_scores, q_one)
                dq_one = dot_tn(grad_scores, k_two * masks[side])
                dv_two = dv_one if dv_two is None else dv_two + dv_one
                dk_two = dk_one if dk_two is None else dk_two + dk_one
                dq_two = dq_one if dq_two is None else dq_two + dq_one
            dv_acc[rows, cols] += dv_two
            dk_acc[rows, cols] += dk_two
            dq_acc[:, cols] += dq_two
        return carried

    lax.fori_loop(low_ref[step], high_ref[step], one_block, 0)
    dq_ref[...] = (dq_acc[...] * HEAD_DIM ** (-0.5)).astype(bf16)

    @pl.when(step == pl.num_programs(0) - 1)
    def _():
        dk_ref[...] = dk_acc[...].astype(bf16)
        dv_ref[...] = dv_acc[...].astype(bf16)


def attend_back_call(
    layer, first, last, base, own, recv, queries, keys, values, mixed, lse, seg_col, seg_row, panels
):
    tokens = base.shape[0]
    shape = lambda width, kind: jax.ShapeDtypeStruct((tokens, width), kind)
    whole = (tokens, HALF)
    return pl.pallas_call(
        attend_back_kernel,
        out_shape=[
            shape(D, f32),
            shape(D, bf16),
            shape(HALF, bf16),
            shape(HALF, bf16),
            shape(HALF, bf16),
            jax.ShapeDtypeStruct((1, D), f32),
        ],
        grid_spec=pltpu.PrefetchScalarGridSpec(
            num_scalar_prefetch=2,
            grid=(tokens // ROWS,),
            in_specs=[
                rows_spec(D),
                rows_spec(D),
                rows_spec(D),
                rows_spec(HALF),
                fixed(whole),
                fixed(whole),
                rows_spec(HALF),
                pl.BlockSpec((8, ROWS), lambda i, *_: (0, i)),
                fixed(seg_col.shape),
                pl.BlockSpec((1, ROWS), lambda i, *_: (0, i)),
                fixed((D, HALF), PANELS["out"][layer] // D),
            ],
            out_specs=[
                rows_spec(D),
                rows_spec(D),
                rows_spec(HALF),
                fixed(whole),
                fixed(whole),
                fixed((1, D)),
            ],
            scratch_shapes=[
                pltpu.VMEM(whole, f32),
                pltpu.VMEM(whole, f32),
                pltpu.VMEM((ROWS, HALF), f32),
                pltpu.VMEM((ROWS, HALF), bf16),
            ],
        ),
        compiler_params=params(),
        cost_estimate=cost(14 * HEADS * tokens * tokens * BS, tokens * D * 20, HEADS * tokens * tokens),
    )(first, last, base, own, recv, queries, keys, values, mixed, lse, seg_col, seg_row, panels)


def qkv_back_kernel(layer, dq, dk, dv, hid, vec, weight, back, dgain, dshift, dbq, dbv):
    grad_normed = (
        dot_nt(dq[...], weight[0:D, :])
        + dot_nt(dk[...], weight[D : 2 * D, :])
        + dot_nt(dv[...], weight[2 * D : 3 * D, :])
    )
    part_back, gain_grad, shift_grad = norm_back(hid[...], vec_piece(vec, layer, "g1"), grad_normed)
    back[...] = part_back.astype(bf16)
    accumulate(dgain, gain_grad)
    accumulate(dshift, shift_grad)
    accumulate(dbq, jnp.sum(dq[...].astype(f32), axis=0, keepdims=True))
    accumulate(dbv, jnp.sum(dv[...].astype(f32), axis=0, keepdims=True))


def qkv_back_call(layer, dq, dk, dv, hid, vec, panels):
    tokens = dq.shape[0]
    line = lambda width: jax.ShapeDtypeStruct((1, width), f32)
    lines = [line(D), line(D), line(HALF), line(HALF)]
    return pl.pallas_call(
        functools.partial(qkv_back_kernel, layer),
        out_shape=[jax.ShapeDtypeStruct((tokens, D), bf16)] + lines,
        grid=(tokens // ROWS,),
        in_specs=[rows_spec(HALF)] * 3
        + [
            rows_spec(D),
            fixed(vec.shape),
            fixed((3 * D, HALF), PANELS["qkv"][layer] // (3 * D)),
        ],
        out_specs=[rows_spec(D)] + [fixed(o.shape) for o in lines],
        compiler_params=params(),
        cost_estimate=cost(2 * tokens * D * 3 * HALF, tokens * D * 10),
    )(dq, dk, dv, hid, vec, panels)


def split(values):
    high = values.astype(bf16)
    return high, (values - high.astype(f32)).astype(bf16)


def product(left, right, left_dim, right_dim):
    def one(a, b):
        return lax.dot_general(
            a, b, (((left_dim,), (right_dim,)), ((), ())), preferred_element_type=f32
        )

    return one(left[0], right[0]) + (one(left[0], right[1]) + one(left[1], right[0]))


def owner_kernel(per, used, home, near, far, master, left, right, moment, variance, grad, out, out_mom, out_var):
    here = range(per)
    first = pl.program_id(0) * per
    lefts = [split(left[i]) for i in here]
    rights = [split(right[i]) for i in here]
    rotated = []
    for i in here:
        rows = slice(i * BS, (i + 1) * BS)
        tile = jnp.where(home[0] > 0, near[rows, :].astype(f32), far[rows, :].astype(f32))
        tile = jnp.where(used[first + i] > 0, tile, 0.0)
        grad[i] = tile
        tile = tile.astype(bf16)
        rotated.append(split(dot_tn(lefts[i][0], tile) + dot_tn(lefts[i][1], tile)))
    rotated = [product(rotated[i], rights[i], 1, 0) for i in here]
    steps = []
    for i in here:
        new_moment = decay * moment[i] + (1.0 - decay) * rotated[i]
        new_variance = decay * variance[i] + (1.0 - decay) * rotated[i] * rotated[i]
        out_mom[i] = new_moment
        out_var[i] = new_variance
        steps.append(split(new_moment / (jnp.sqrt(new_variance) + adam_eps)))
    returned = [split(product(lefts[i], steps[i], 1, 0)) for i in here]
    returned = [product(returned[i], rights[i], 1, 1) for i in here]
    for i in here:
        out[i] = master[i] - matrix_rate * returned[i]


def owner_call(used, home, near, far, *arrays):
    count = arrays[0].shape[0]
    per = min(8, count)
    block = pl.BlockSpec((per, BS, BS), lambda i, *_: (i, 0, 0))
    return pl.pallas_call(
        functools.partial(owner_kernel, per),
        out_shape=[jax.ShapeDtypeStruct(arrays[0].shape, f32)] * 4,
        grid_spec=pltpu.PrefetchScalarGridSpec(
            num_scalar_prefetch=2,
            grid=(count // per,),
            in_specs=[pl.BlockSpec((per * BS, BS), lambda i, *_: (i, 0))] * 2 + [block] * 5,
            out_specs=[block] * 4,
        ),
        compiler_params=params(),
        cost_estimate=cost(count * 88 * BS**3, count * BS * BS * 38),
    )(used, home, near, far, *arrays)


def reduce_kernel(carrying, last, *refs):
    block, arrived, *refs = refs
    total = block[...].astype(f32) + arrived[...].astype(f32)
    if carrying:
        carried, *refs = refs
        total = total + carried[...].astype(f32)
    if last:
        [out] = refs
    else:
        following, out, later = refs
        later[...] = following[...]
    out[...] = total.astype(bf16)


def reduce_call(j, n, buffer, arrived, carried, payload):
    last = j == 3
    at = lambda j, x_rel: pl.BlockSpec((payload, BS), lambda i: ((j * 2 + x_rel) * 2 + n, 0))
    whole = fixed((payload, BS))
    operands = [buffer, arrived] + ([] if carried is None else [carried])
    specs = [at(j, 0)] + [whole] * (len(operands) - 1)
    if not last:
        operands.append(buffer)
        specs.append(at(j + 1, 1))
    outs = [jax.ShapeDtypeStruct((payload, BS), bf16)] * (1 if last else 2)
    made = pl.pallas_call(
        functools.partial(reduce_kernel, carried is not None, last),
        out_shape=outs,
        grid=(1,),
        in_specs=specs,
        out_specs=[whole] * len(outs),
        compiler_params=params(),
        cost_estimate=cost(payload * BS * 3, payload * BS * 12),
    )(*operands)
    return (made[0], None) if last else made


class Routes:
    def __init__(self, dp_n):
        pairs = [(d, t) for d in range(dp_n) for t in range(TENSOR)]
        at = lambda d, t: d * TENSOR + t
        home = [(d, t) for d, t in pairs if d % 2 == t]
        away = [(d, t) for d, t in pairs if d % 2 != t]
        self.core_all = [(at(d, t), at(d ^ 1, t)) for d, t in pairs]
        self.core_out = [(at(d, t), at(d ^ 1, t)) for d, t in home]
        self.core_in = [(at(d, t), at(d ^ 1, t)) for d, t in away]
        self.y_all = [(at(d, t), at(d, 1 - t)) for d, t in pairs]
        self.y_out = [(at(d, t), at(d, 1 - t)) for d, t in home]
        self.y_in = [(at(d, t), at(d, 1 - t)) for d, t in away]
        self.x_home = [(at(d, t), at(d ^ 2, t)) for d, t in home]
        self.x_away = [(at(d, t), at(d ^ 2, t)) for d, t in away]
        self.z_home = [(at(d, t), at((d + 4) % dp_n, t)) for d, t in home]


def send(value, route):
    return lax.ppermute(value, AXES, route)


def shards(
    patches,
    cotangent,
    image_size,
    block_slot,
    pinv,
    master_slots,
    left_basis,
    right_basis,
    mom_slots,
    var_slots,
    vec_master,
    vec_mom,
    vec_var,
):
    dp_n = lax.axis_size("dp")
    dp_pos = lax.axis_index("dp")
    y_pos = lax.axis_index("tensor")
    core = dp_pos % 2
    home = core == y_pos
    routes = Routes(dp_n)
    grid3 = dp_n == 16
    tokens_n = patches.shape[0]
    slots_per = master_slots.shape[1]
    vec_per = vec_master.shape[1]
    slots_n = slots_per * dp_n
    payload = slots_per * BS + VEC_ROWS

    patches = jnp.where(home, patches, send(patches, routes.core_out))
    cotangent = jnp.where(home, cotangent, send(cotangent, routes.core_out))
    size_row = jnp.where(home, image_size, send(image_size, routes.core_out))[0]
    own_slots = block_slot[0]
    slot_other = send(block_slot, routes.y_all)

    lengths = jnp.where(
        size_row == 0, LEN_A, jnp.where(size_row == 1, LEN_B, jnp.where(size_row == 2, LEN_C, 0))
    )
    order = jnp.arange(IMG_DEV)
    ends_at = jnp.sum(jnp.where(order[None, :] <= order[:, None], lengths[None, :], 0), axis=1)
    places = jnp.arange(tokens_n)
    segment = jnp.sum((places[:, None] >= ends_at[None, :]).astype(jnp.int32), axis=1)
    in_image = segment[:, None] == order[None, :]
    select = jnp.stack(
        [jnp.any(in_image & (size_row == s)[None, :], axis=1) for s in range(3)], axis=1
    )
    valid_col = (segment < IMG_DEV).astype(f32)[:, None]
    seg_col = segment[:, None]
    seg_row = segment[None, :]
    blocks_n = tokens_n // ROWS
    starts = jnp.arange(blocks_n) * ROWS
    begun = ends_at[None, :] <= starts[:, None]
    first_tok = jnp.max(jnp.where(begun, ends_at[None, :], 0), axis=1)
    after = ends_at[None, :] > (starts + ROWS - 1)[:, None]
    last_tok = jnp.min(jnp.where(after, ends_at[None, :], tokens_n), axis=1)
    first_blk = (first_tok // ROWS).astype(jnp.int32)
    last_blk = ((last_tok + ROWS - 1) // ROWS).astype(jnp.int32)

    select_low = select.astype(bf16)
    spread_in = patches[:, None, :] * select_low[:, :, None]

    def expand(which):
        size = BASE_PIX // CHUNKS
        return lax.dot_general(
            spread_in,
            pinv[:, which * size : (which + 1) * size],
            (((1, 2), (0, 2)), ((), ())),
            preferred_element_type=f32,
        ).astype(bf16)

    vec_low = jnp.pad(vec_master[0].astype(bf16), (0, VEC_ROWS * BS - vec_per))
    own_pack = jnp.concatenate(
        [
            master_slots[0].astype(bf16).reshape(slots_per * BS, BS),
            vec_low.reshape(VEC_ROWS, BS),
        ],
        axis=0,
    )
    flag = home.astype(jnp.int32).reshape(1)
    if grid3:
        x_pos = (dp_pos // 2) % 2
        z_pos = dp_pos // 4
        packs = [[own_pack], [send(own_pack, routes.core_in)]]
        across, over_y, corner = [[], []], [[], []], [[], []]
        token = jnp.zeros((8, BS), f32)
        chunks = []
        for j in range(5):
            for n in range(2):
                moved = []
                if j < 4:
                    moved += [send(packs[n][j], routes.x_home), send(packs[n][j], routes.y_out)]
                if j:
                    source, route = (across, routes.y_out) if n == 0 else (over_y, routes.x_away)
                    moved.append(send(source[n][j - 1], route))
                if j < 3:
                    moved.append(send(packs[n][j], routes.z_home))
                work = []
                if j + n == 0:
                    work = [slot_other]
                if 1 <= 2 * j + n <= CHUNKS:
                    work = [expand(2 * j + n - 1)]
                if j < 4:
                    token, *moved = fence(token, *moved, *work)
                    if j + n == 0:
                        slot_other = moved.pop()
                    elif work:
                        chunks.append(moved.pop())
                if j < 3:
                    packs[n].append(moved.pop())
                if j:
                    corner[n].append(moved.pop())
                if j < 4:
                    across[n].append(moved[0])
                    over_y[n].append(moved[1])
        first, second, owner = [], [], []
        for j in range(4):
            first += [packs[0][j], packs[1][j], across[0][j], across[1][j]]
            second += [over_y[0][j], over_y[1][j], corner[0][j], corner[1][j]]
            for x_rel in range(2):
                for n in range(2):
                    owner.append(((z_pos - j) % 4) * 4 + (x_pos ^ x_rel) * 2 + (core ^ n))
        first = [v[None] for v in first]
        second = [v[None] for v in second]
        owner = jnp.stack(owner).astype(jnp.int32)
    else:
        everything = lax.all_gather(own_pack, AXES, axis=0)
        everything = everything.reshape(dp_n, TENSOR, payload, BS)
        first = [jnp.where(core == 0, everything[:, 0], everything[:, 1])]
        second = []
        owner = jnp.arange(dp_n, dtype=jnp.int32)
        chunks = [expand(c) for c in range(CHUNKS)]
    slot_list = jnp.where(home, block_slot, slot_other)[0]
    named = slot_list[None, :] == jnp.arange(slots_n)[:, None]
    used = jnp.any(named, axis=1)
    drow = jnp.where(used, jnp.sum(jnp.where(named, TARGET_ROW[None, :], 0), axis=1), -1)
    dcol = jnp.sum(jnp.where(named, TARGET_COL[None, :], 0), axis=1)
    panels, vec_rows = gather_tiles(first, second, owner, drow, dcol, flag, slots_per, dp_n)
    vec = vec_rows.reshape(dp_n, VEC_ROWS * BS)[:, :vec_per].astype(f32).reshape(1, dp_n * vec_per)

    embedded = embed_call(chunks, vec, panels)
    embedded_other = send(embedded, routes.core_all)
    core_flag = core.astype(jnp.int32).reshape(1)

    caches = []
    hidden, own, recv = None, embedded, embedded_other
    for layer in range(LAYERS):
        hidden, normed, queries, keys, values = qkv_call(
            layer, hidden, own, recv, core_flag, vec, panels
        )
        mixed, lse, part = attend_call(
            layer, queries, keys, values, seg_col, seg_row, vec, panels
        )
        other = send(part, routes.core_all)
        middle, normed2, act, slope, own = mlp_call(layer, hidden, part, other, vec, panels)
        recv = send(own, routes.core_all)
        caches.append((hidden, normed, queries, keys, values, mixed, lse, middle, normed2, act, slope))
        hidden = middle
    out_low = ((hidden + (own.astype(f32) + recv.astype(f32))) * valid_col).astype(bf16)
    out_other = send(out_low, routes.y_out)

    owners = jnp.arange(dp_n)
    if grid3:
        place = (
            ((z_pos - 1 - owners // 4) % 4) * 4
            + (x_pos ^ ((owners // 2) % 2)) * 2
            + (core ^ (owners % 2))
        ).astype(jnp.int32)
        half_at = x_pos.astype(jnp.int32).reshape(1)
    else:
        place = owners.astype(jnp.int32)
        half_at = jnp.zeros((1,), jnp.int32)
    slot_owner = slot_list // slots_per
    owner_place = jnp.sum(
        jnp.where(slot_owner[:, None] == owners[None, :], place[None, :], 0), axis=1
    )
    tile_pos = (owner_place * payload + (slot_list % slots_per) * BS).astype(jnp.int32)
    vec_pos = (place * payload + slots_per * BS).astype(jnp.int32)
    total_rows = dp_n * payload
    offsets = {"base": 0}
    count = BASE_PIX // BS * (HALF // BS)
    for layer in range(LAYERS):
        for name, size in (("qkv", 3 * D * HALF), ("out", D * HALF), ("up", D * HALF_FF), ("down", D * HALF_FF)):
            offsets[name, layer] = count
            count += size // (BS * BS)

    def place_tiles(key, matrix, arrived, buffer):
        tiles = matrix.size // (BS * BS)
        pos = tile_pos[offsets[key] : offsets[key] + tiles]
        rows_n = matrix.shape[0] // 2 if matrix.shape[0] > HALF else HALF
        return scatter_matrix(pos, matrix, arrived, half_at, buffer, total_rows, rows_n)

    def over(matrix):
        return send(matrix, routes.y_in) if grid3 else None

    def halves_of(matrix):
        size = matrix.shape[0] // 2
        mine = lax.dynamic_slice_in_dim(matrix, x_pos * size, size, 0)
        theirs = lax.dynamic_slice_in_dim(matrix, (1 - x_pos) * size, size, 0)
        return mine, theirs

    def half_sum(matrix, arrived):
        mine, unused = halves_of(matrix)
        return (mine.astype(f32) + arrived.astype(f32)).astype(bf16)

    def beside(matrix):
        return send(halves_of(matrix)[1], routes.x_away) if grid3 else None

    def hold(*arrays):
        kept = [a for a in arrays if a is not None]
        done = iter(fence(*kept))
        return [None if a is None else next(done) for a in arrays]

    top, low = 1, 0
    vec_grads = [None] * LAYERS

    def mlp_step(layer, grad, own, recv):
        middle, normed2, act, slope = caches[layer][7:11]
        made = mlp_back_call(layer, grad, own, recv, valid_col, middle, slope, vec, panels)
        if own is not None:
            return made
        return [made[0]] + list(made)

    def attend_step(layer, grad, part, other):
        hid_in, normed, queries, keys, values, mixed, lse = caches[layer][:7]
        return attend_back_call(
            layer, first_blk, last_blk, grad, part, other, queries, keys, values, mixed, lse,
            seg_col, seg_row, panels,
        )

    grad, grad_low, du, part, dg2, ds2, db1, db2 = mlp_step(top, cotangent, None, None)
    other = send(part, routes.core_all)
    gd1 = dot_tn(caches[top][9], grad_low).astype(bf16)
    gu1 = dot_tn(caches[top][8], du).astype(bf16)
    part, other, gd1, gu1, out_other = fence(part, other, gd1, gu1, out_other)
    output = jnp.where(home, out_low, out_other).astype(f32)
    ad1 = over(gd1)
    grad, grad_low, dq, dk, dv, dbo = attend_step(top, grad, part, other)
    dq, dk, dv, ad1 = hold(dq, dk, dv, ad1)
    au1 = over(gu1)
    own, dg1, ds1, dbq, dbv = qkv_back_call(top, dq, dk, dv, caches[top][0], vec, panels)
    recv = send(own, routes.core_all)
    go1 = dot_tn(caches[top][5], grad_low).astype(bf16)
    gq1 = dot_tn(caches[top][1], jnp.concatenate([dq, dk, dv], axis=1)).astype(bf16)
    vec_grads[top] = [dg1, ds1, dbq, dbv, dbo, dg2, ds2, db1, db2]
    grad, grad_low, du, part, dg2, ds2, db1, db2 = mlp_step(low, grad, own, recv)
    du, part, au1, go1, gq1 = hold(du, part, au1, go1, gq1)
    other = send(part, routes.core_all)
    xq1, ao1 = beside(gq1), over(go1)
    gd0 = dot_tn(caches[low][9], grad_low).astype(bf16)
    gu0 = dot_tn(caches[low][8], du).astype(bf16)
    part, other, gd0, gu0, xq1, ao1 = hold(part, other, gd0, gu0, xq1, ao1)
    aq1 = over(half_sum(gq1, xq1)) if grid3 else None
    xd0, xu0 = beside(gd0), beside(gu0)
    buffer = place_tiles(("down", top), gd1, ad1, None)
    buffer = place_tiles(("up", top), gu1, au1, buffer)
    grad, grad_low, dq, dk, dv, dbo = attend_step(low, grad, part, other)
    grad, grad_low, dq, dk, dv, aq1, xd0, xu0, buffer = hold(
        grad, grad_low, dq, dk, dv, aq1, xd0, xu0, buffer
    )
    hd0 = half_sum(gd0, xd0) if grid3 else None
    hu0 = half_sum(gu0, xu0) if grid3 else None
    go0 = dot_tn(caches[low][5], grad_low).astype(bf16)
    gq0 = dot_tn(caches[low][1], jnp.concatenate([dq, dk, dv], axis=1)).astype(bf16)
    dq, dk, dv, hd0, hu0, go0, gq0 = hold(dq, dk, dv, hd0, hu0, go0, gq0)
    ad0, au0 = over(hd0), over(hu0)
    xq0 = beside(gq0)
    own, dg1, ds1, dbq, dbv = qkv_back_call(low, dq, dk, dv, caches[low][0], vec, panels)
    recv = send(own, routes.core_all)
    vec_grads[low] = [dg1, ds1, dbq, dbv, dbo, dg2, ds2, db1, db2]
    sides = [
        grad[:, s * HALF : (s + 1) * HALF]
        + (
            own[:, s * HALF : (s + 1) * HALF].astype(f32)
            + recv[:, s * HALF : (s + 1) * HALF].astype(f32)
        )
        for s in range(TENSOR)
    ]
    grad_emb = jnp.where(core == 0, sides[0], sides[1]).astype(bf16)
    grad_emb_bias = jnp.sum(grad_emb.astype(f32), axis=0, keepdims=True)
    gb = jnp.concatenate([dot_tn(c, grad_emb).astype(bf16) for c in chunks], axis=0)
    vec_grad = jnp.concatenate([grad_emb_bias] + vec_grads[0] + vec_grads[1], axis=1)[0]
    vec_grad = jnp.pad(vec_grad, (0, dp_n * vec_per - vec_grad.shape[0])).reshape(dp_n, vec_per)
    vec_grad = jnp.pad(vec_grad, ((0, 0), (0, VEC_ROWS * BS - vec_per)))
    vec_grad = vec_grad.astype(bf16).reshape(dp_n, VEC_ROWS, BS)
    hq0 = half_sum(gq0, xq0) if grid3 else None
    gb, vec_grad, grad_emb, hq0 = hold(gb, vec_grad, grad_emb, hq0)
    aq0, ao0, av = over(hq0), over(go0), over(vec_grad)
    xb = beside(gb)
    buffer = place_tiles(("out", top), go1, ao1, buffer)
    buffer = place_tiles(("qkv", top), gq1, aq1, buffer)
    buffer = place_tiles(("down", low), gd0, ad0, buffer)
    buffer = place_tiles(("up", low), gu0, au0, buffer)
    hb = half_sum(gb, xb) if grid3 else None
    hb, aq0, ao0, av, buffer, panels, grad_emb = hold(hb, aq0, ao0, av, buffer, panels, grad_emb)
    ab = over(hb)
    buffer = place_tiles(("out", low), go0, ao0, buffer)
    buffer = scatter_vec(vec_pos, vec_grad, av, buffer)
    buffer = place_tiles(("qkv", low), gq0, aq0, buffer)
    base_here = panels[PANELS["base"] : PANELS["base"] + BASE_PIX]
    resized = [dot_tn(pinv[s], base_here).astype(bf16) for s in range(3)]
    ab, buffer, *resized = hold(ab, buffer, *resized)
    buffer = place_tiles("base", gb, ab, buffer)
    grad_pixels = sum(
        dot_nt(grad_emb * select_low[:, s : s + 1], resized[s]) for s in range(3)
    ).astype(bf16)

    if grid3:
        token = jnp.zeros((8, BS), f32)
        order = (1, 0)
        carried = {n: None for n in order}
        across = {n: send(buffer.reshape(4, 2, 2, payload, BS)[0, 1, n], routes.x_home) for n in order}
        rounded = {}
        for j in range(4):
            for n in order:
                extra = None
                if j == 0 and n == order[1]:
                    extra = grad_pixels
                token, across[n], carried[n], extra = hold(token, across[n], carried[n], extra)
                if extra is not None:
                    grad_pixels = extra
                total, later = reduce_call(j, n, buffer, across[n], carried[n], payload)
                if j < 3:
                    carried[n] = send(total, routes.z_home)
                    across[n] = send(later, routes.x_home)
                else:
                    rounded[n] = total
        near_grad, far_grad = rounded[0], send(rounded[1], routes.core_out)
    else:
        held = buffer.reshape(dp_n, 1, payload, BS).astype(f32)
        nothing = jnp.zeros_like(held)
        both = jnp.concatenate(
            [jnp.where(core == 0, held, nothing), jnp.where(core == 0, nothing, held)], axis=1
        )
        used_rows = jnp.repeat(used, BS).reshape(dp_n, 1, slots_per * BS, 1)
        used_rows = jnp.concatenate(
            [used_rows, jnp.ones((dp_n, 1, VEC_ROWS, 1), bool)], axis=2
        )
        both = jnp.where(used_rows, both, 0.0).reshape(dp_n * TENSOR * payload, BS)
        near_grad = lax.psum_scatter(both, AXES, scatter_dimension=0, tiled=True).astype(bf16)
        far_grad = near_grad

    pixels_other = send(grad_pixels, routes.core_all)
    pixel_sides = [
        grad_pixels[:, s * HALF : (s + 1) * HALF].astype(f32)
        + pixels_other[:, s * HALF : (s + 1) * HALF].astype(f32)
        for s in range(TENSOR)
    ]
    near = jnp.where(core == 0, pixel_sides[0], pixel_sides[1])
    far = jnp.where(core == 0, pixel_sides[1], pixel_sides[0]).astype(bf16)
    patch_grad = jnp.where(home, near, send(far, routes.y_out).astype(f32))

    my_slots = dp_pos * slots_per + jnp.arange(slots_per)
    mine_used = jnp.any(own_slots[None, :] == my_slots[:, None], axis=1).astype(jnp.int32)
    owned_grad, new_master, new_mom, new_var = owner_call(
        mine_used, flag, near_grad, far_grad, master_slots[0], left_basis[0], right_basis[0], mom_slots[0], var_slots[0]
    )
    vec_rows = jnp.where(home, near_grad[slots_per * BS :], far_grad[slots_per * BS :])
    owned_vec_grad = vec_rows.astype(f32).reshape(VEC_ROWS * BS)[:vec_per]
    new_vec_mom = decay * vec_mom[0] + (1.0 - decay) * owned_vec_grad
    new_vec_var = decay * vec_var[0] + (1.0 - decay) * owned_vec_grad * owned_vec_grad
    new_vec = vec_master[0] - vector_rate * new_vec_mom / (jnp.sqrt(new_vec_var) + adam_eps)
    return (
        output,
        patch_grad,
        owned_grad[None],
        new_master[None],
        new_mom[None],
        new_var[None],
        owned_vec_grad[None],
        new_vec[None],
        new_vec_mom[None],
        new_vec_var[None],
    )


def solution(mesh):
    slots = P("tensor", "dp", None, None)
    vectors = P("tensor", "dp")
    tokens = P("dp", None)
    in_specs = (tokens, tokens, tokens, P("tensor", None), P()) + (slots,) * 5 + (vectors,) * 3
    out_specs = (tokens, P("dp", "tensor")) + (slots,) * 4 + (vectors,) * 4
    return jax.shard_map(shards, mesh=mesh, in_specs=in_specs, out_specs=out_specs, check_vma=False)
```

```python
import functools

import jax
import jax.numpy as jnp
import numpy as np
from jax import lax
from jax.experimental import pallas as pl
from jax.experimental.pallas import tpu as pltpu
from jax.sharding import PartitionSpec as P

D = 768
HEAD_DIM = 64
FF = 3072
BASE_PIX = 3072
LAYERS = 2
LEN_A = 196
LEN_B = 225
LEN_C = 576
IMG_DEV = 5
BS = 128
TENSOR = 2
HALF = D // TENSOR
HALF_FF = FF // TENSOR
HEADS = HALF // HEAD_DIM
ROWS = 256
VEC_ROWS = 16
CHUNKS = 4

AXES = ("dp", "tensor")
precise = lax.Precision.HIGHEST
masked_score = -1e30
norm_eps = 1e-06
adam_eps = 1e-08
decay = 0.5
matrix_rate = 0.05
vector_rate = 0.3
f32 = jnp.float32
bf16 = jnp.bfloat16
BIG_VMEM = 56 * 1024 * 1024

PANELS = {
    "up": (0, 6144),
    "down": (3072, 9216),
    "base": 12288,
    "out": (15360, 20736),
    "qkv": (16128, 18432),
}
PANEL_ROWS = 21504


def tile_targets():
    rows, cols = [], []

    def add(start, rows_n, cols_n):
        for i in range(rows_n // BS):
            for j in range(cols_n // BS):
                panel, inner = divmod(j * BS, HALF)
                rows.append(start + panel * rows_n + i * BS)
                cols.append(inner)

    add(PANELS["base"], BASE_PIX, HALF)
    for layer in range(LAYERS):
        add(PANELS["qkv"][layer], D, 3 * HALF)
        add(PANELS["out"][layer], HALF, D)
        add(PANELS["up"][layer], D, HALF_FF)
        add(PANELS["down"][layer], HALF_FF, D)
    return np.array(rows, np.int32), np.array(cols, np.int32)


TARGET_ROW, TARGET_COL = tile_targets()
LAYER_VECS = (D, D, HALF, HALF, D, D, D, HALF_FF, D)
VEC_NAMES = ("g1", "s1", "bq", "bv", "bo", "g2", "s2", "b1", "b2")


def vec_offsets():
    offset = HALF
    found = []
    for layer in range(LAYERS):
        here = {}
        for name, length in zip(VEC_NAMES, LAYER_VECS):
            here[name] = (offset, length)
            offset += length
        found.append(here)
    return found


VEC_AT = vec_offsets()


def params(limit=BIG_VMEM):
    return pltpu.CompilerParams(
        dimension_semantics=("arbitrary",), vmem_limit_bytes=limit
    )


def cost(flops, nbytes, trans=0):
    return pl.CostEstimate(flops=flops, bytes_accessed=nbytes, transcendentals=trans)


def rows_spec(width):
    return pl.BlockSpec((ROWS, width), lambda i, *_: (i, 0))


def fixed(shape, at=0):
    return pl.BlockSpec(shape, lambda i, *_: (at,) + (0,) * (len(shape) - 1))


def vec_piece(vec_ref, layer, name):
    start, length = VEC_AT[layer][name]
    return vec_ref[:, start : start + length]


def dot(left, right):
    return jnp.dot(left, right, preferred_element_type=f32)


def dot_nt(left, right, precision=None):
    return lax.dot_general(
        left, right, (((1,), (1,)), ((), ())), precision=precision, preferred_element_type=f32
    )


def dot_tn(left, right):
    return lax.dot_general(left, right, (((0,), (0,)), ((), ())), preferred_element_type=f32)


def norm_stats(values):
    mean_val = jnp.mean(values, axis=-1, keepdims=True)
    centered = values - mean_val
    inv_std = lax.rsqrt(jnp.mean(centered * centered, axis=-1, keepdims=True) + norm_eps)
    return centered * inv_std, inv_std


def norm_back(values, gain, grad):
    unit, inv_std = norm_stats(values)
    scaled = grad * gain
    mean_s = jnp.mean(scaled, axis=-1, keepdims=True)
    mean_u = jnp.mean(scaled * unit, axis=-1, keepdims=True)
    back = inv_std * (scaled - mean_s - unit * mean_u)
    return (
        back,
        jnp.sum(grad * unit, axis=0, keepdims=True),
        jnp.sum(grad, axis=0, keepdims=True),
    )


def accumulate(ref, value):
    first = pl.program_id(0) == 0

    @pl.when(first)
    def _():
        ref[...] = value

    @pl.when(jnp.logical_not(first))
    def _():
        ref[...] += value


def fence(*arrays):
    def nothing(*refs):
        pass

    anywhere = pl.BlockSpec(memory_space=pl.ANY)
    return pl.pallas_call(
        nothing,
        out_shape=[jax.ShapeDtypeStruct(a.shape, a.dtype) for a in arrays],
        in_specs=[anywhere] * len(arrays),
        out_specs=[anywhere] * len(arrays),
        input_output_aliases={i: i for i in range(len(arrays))},
    )(*arrays)


def gather_kernel(slots, count_a, count_b, owner, drow, dcol, flag, *refs):
    first = refs[:count_a]
    second = refs[count_a : count_a + count_b]
    panels, vectors, held, sem, vec_sem = refs[count_a + count_b :]

    def copy_all(sources):
        at = 0
        for src in sources:
            for n in range(src.shape[0]):
                who = owner[at]
                at += 1

                def body(i, carried, src=src, n=n, who=who):
                    slot = who * slots + i
                    row = drow[slot]

                    @pl.when(row >= 0)
                    def _():
                        start = pl.multiple_of(i * BS, BS)
                        pltpu.make_async_copy(
                            src.at[n, pl.ds(start, BS), :],
                            held.at[
                                pl.ds(pl.multiple_of(row, BS), BS),
                                pl.ds(pl.multiple_of(dcol[slot], BS), BS),
                            ],
                            sem,
                        ).start()

                    return carried

                lax.fori_loop(0, slots, body, 0)
                pltpu.make_async_copy(
                    src.at[n, pl.ds(slots * BS, VEC_ROWS), :], vectors.at[who], vec_sem
                ).start()

    if count_b:

        @pl.when(flag[0] == 1)
        def _():
            copy_all(first)

        @pl.when(flag[0] == 0)
        def _():
            copy_all(second)
    else:
        copy_all(first)
    pltpu.make_async_copy(held, held, sem).wait()
    out = pltpu.make_async_copy(held, panels, sem)
    out.start()
    pltpu.make_async_copy(vectors, vectors, vec_sem).wait()
    out.wait()


def gather_tiles(first, second, owner, drow, dcol, flag, slots, owners):
    anywhere = pl.BlockSpec(memory_space=pl.ANY)
    return pl.pallas_call(
        functools.partial(gather_kernel, slots, len(first), len(second)),
        out_shape=(
            jax.ShapeDtypeStruct((PANEL_ROWS, HALF), bf16),
            jax.ShapeDtypeStruct((owners, VEC_ROWS, BS), bf16),
        ),
        grid_spec=pltpu.PrefetchScalarGridSpec(
            num_scalar_prefetch=4,
            grid=(1,),
            in_specs=[anywhere] * (len(first) + len(second)),
            out_specs=(anywhere, fixed((owners, VEC_ROWS, BS))),
            scratch_shapes=[
                pltpu.VMEM((PANEL_ROWS, HALF), bf16),
                pltpu.SemaphoreType.DMA,
                pltpu.SemaphoreType.DMA,
            ],
        ),
        compiler_params=params(),
        cost_estimate=cost(0, 4 * PANEL_ROWS * HALF),
    )(owner, drow, dcol, flag, *first, *second)


def scatter_kernel(rows_n, cols_n, steps, paired, parts, pos, part, own, *refs):
    if paired:
        recv, *refs = refs
        span = pl.num_programs(0) // parts
        here = jnp.logical_or(parts == 1, pl.program_id(0) // span == part[0])
    target, buf, sems = refs[-3:]
    step = pl.program_id(0)
    slot = lax.rem(step, 2)
    per = rows_n // BS * (cols_n // BS)

    def wait(at):
        pltpu.make_async_copy(buf.at[at], buf.at[at], sems.at[at]).wait()

    @pl.when(step >= 2)
    def _():
        wait(slot)

    for i in range(rows_n // BS):
        for j in range(cols_n // BS):
            area = (slice(i * BS, (i + 1) * BS), slice(j * BS, (j + 1) * BS))
            value = own[area]
            if paired:
                more = jnp.where(here, recv[area].astype(f32), 0.0)
                value = (value.astype(f32) + more).astype(bf16)
            buf[slot, i * (cols_n // BS) + j] = value
    for n in range(per):
        pltpu.make_async_copy(
            buf.at[slot, n],
            target.at[pl.ds(pl.multiple_of(pos[step * per + n], 16), BS), :],
            sems.at[slot],
        ).start()

    @pl.when(step == pl.num_programs(0) - 1)
    def _():
        if steps > 1:
            wait(1 - slot)
        wait(slot)


def scatter_matrix(pos, own, recv, part, target, total_rows, rows_n):
    cols_n = own.shape[1]
    steps = own.shape[0] // rows_n
    anywhere = pl.BlockSpec(memory_space=pl.ANY)
    block = pl.BlockSpec((rows_n, cols_n), lambda i, *_: (i, 0))
    paired = recv is not None
    parts = own.shape[0] // recv.shape[0] if paired else 1
    span = steps // parts
    arrived = pl.BlockSpec(
        (rows_n, cols_n), lambda i, pos, part: (jnp.clip(i - part[0] * span, 0, span - 1), 0)
    )
    operands = [own] + ([recv] if paired else []) + ([] if target is None else [target])
    specs = [block] + ([block if parts == 1 else arrived] if paired else [])
    specs += [] if target is None else [anywhere]
    return pl.pallas_call(
        functools.partial(scatter_kernel, rows_n, cols_n, steps, paired, parts),
        out_shape=jax.ShapeDtypeStruct((total_rows, BS), bf16),
        grid_spec=pltpu.PrefetchScalarGridSpec(
            num_scalar_prefetch=2,
            grid=(steps,),
            in_specs=specs,
            out_specs=anywhere,
            scratch_shapes=[
                pltpu.VMEM((2, rows_n // BS * (cols_n // BS), BS, BS), bf16),
                pltpu.SemaphoreType.DMA((2,)),
            ],
        ),
        input_output_aliases={} if target is None else {len(operands) + 1: 0},
        compiler_params=params(),
        cost_estimate=cost(own.size, own.size * 6),
    )(pos, part, *operands)


def scatter_vec_kernel(paired, pos, own, *refs):
    if paired:
        recv, *refs = refs
    target, buf, sem = refs[-3:]
    value = own[...]
    if paired:
        value = (value.astype(f32) + recv[...].astype(f32)).astype(bf16)
    buf[...] = value

    def body(n, carried):
        pltpu.make_async_copy(
            buf.at[n], target.at[pl.ds(pl.multiple_of(pos[n], 16), VEC_ROWS), :], sem
        ).start()
        return carried

    lax.fori_loop(0, own.shape[0], body, 0)
    pltpu.make_async_copy(buf, buf, sem).wait()


def scatter_vec(pos, own, recv, target):
    anywhere = pl.BlockSpec(memory_space=pl.ANY)
    block = fixed(own.shape)
    paired = recv is not None
    operands = [own] + ([recv] if paired else []) + [target]
    return pl.pallas_call(
        functools.partial(scatter_vec_kernel, paired),
        out_shape=jax.ShapeDtypeStruct(target.shape, bf16),
        grid_spec=pltpu.PrefetchScalarGridSpec(
            num_scalar_prefetch=1,
            grid=(1,),
            in_specs=[block] * (len(operands) - 1) + [anywhere],
            out_specs=anywhere,
            scratch_shapes=[pltpu.VMEM(own.shape, bf16), pltpu.SemaphoreType.DMA],
        ),
        input_output_aliases={len(operands): 0},
        compiler_params=params(),
    )(pos, *operands)


def expand_kernel(present, patch_ref, class_ref, pinv_ref, out, total):
    for block in range(patch_ref.shape[0] // ROWS):
        rows = slice(block * ROWS, (block + 1) * ROWS)
        total[...] = jnp.zeros_like(total)
        for which in range(3):

            @pl.when(present[block, which] > 0)
            def _(which=which, rows=rows):
                chosen = jnp.where(class_ref[rows, :] == which, patch_ref[rows, :].astype(f32), 0.0)
                total[...] += dot_nt(chosen.astype(bf16), pinv_ref[which])

        out[rows, :] = total[...].astype(bf16)


def expand_call(which, present, patches, class_col, pinv):
    tokens = patches.shape[0]
    size = BASE_PIX // CHUNKS
    step = size // 3
    return pl.pallas_call(
        expand_kernel,
        out_shape=jax.ShapeDtypeStruct((tokens, size), bf16),
        grid_spec=pltpu.PrefetchScalarGridSpec(
            num_scalar_prefetch=1,
            grid=(3,),
            in_specs=[
                fixed(patches.shape),
                fixed(class_col.shape),
                pl.BlockSpec((3, step, pinv.shape[2]), lambda i, *_: (0, which * 3 + i, 0)),
            ],
            out_specs=pl.BlockSpec((tokens, step), lambda i, *_: (0, i)),
            scratch_shapes=[pltpu.VMEM((ROWS, step), f32)],
        ),
        compiler_params=params(),
        cost_estimate=cost(3 * tokens * size * D, tokens * size * 4 + size * D * 6),
    )(present, patches, class_col, pinv)


def resize_kernel(base, pinv_ref, out, turned):
    @pl.when(pl.program_id(0) == 0)
    def _():
        turned[...] = base[...].T

    out[0] = dot(turned[...], pinv_ref[0]).astype(bf16)


def resize_call(panels, pinv):
    return pl.pallas_call(
        resize_kernel,
        out_shape=jax.ShapeDtypeStruct((3, HALF, pinv.shape[2]), bf16),
        grid=(3,),
        in_specs=[
            fixed((BASE_PIX, HALF), PANELS["base"] // BASE_PIX),
            pl.BlockSpec((1, BASE_PIX, pinv.shape[2]), lambda i: (i, 0, 0)),
        ],
        out_specs=pl.BlockSpec((1, HALF, pinv.shape[2]), lambda i: (i, 0, 0)),
        scratch_shapes=[pltpu.VMEM((HALF, BASE_PIX), bf16)],
        compiler_params=params(),
        cost_estimate=cost(6 * D * BASE_PIX * HALF, 6 * D * BASE_PIX),
    )(panels, pinv)


def embed_back_kernel(core, base, own, recv, out, bias):
    low = (base[...] + (own[...].astype(f32) + recv[...].astype(f32))).astype(bf16)
    out[...] = low
    accumulate(bias, jnp.sum(low.astype(f32), axis=0, keepdims=True))


def embed_back_call(core, base, own, recv):
    tokens = base.shape[0]
    half = pl.BlockSpec((ROWS, HALF), lambda i, core: (i, core[0]))
    return pl.pallas_call(
        embed_back_kernel,
        out_shape=[
            jax.ShapeDtypeStruct((tokens, HALF), bf16),
            jax.ShapeDtypeStruct((1, HALF), f32),
        ],
        grid_spec=pltpu.PrefetchScalarGridSpec(
            num_scalar_prefetch=1,
            grid=(tokens // ROWS,),
            in_specs=[half] * 3,
            out_specs=[rows_spec(HALF), fixed((1, HALF))],
        ),
        compiler_params=params(),
        cost_estimate=cost(tokens * D, tokens * D * 5),
    )(core, base, own, recv)


def pack_kernel(vec_per, *refs):
    *pieces, out = refs
    out[...] = jnp.zeros_like(out)
    at = 0
    for piece in pieces:
        for k in range(piece.shape[1] // BS):
            owner, row = divmod(at, vec_per // BS)
            out[owner, row : row + 1, :] = piece[:, k * BS : (k + 1) * BS]
            at += 1


def pack_call(pieces, owners, vec_per):
    if vec_per % BS:
        joined = jnp.concatenate(pieces, axis=1)[0]
        joined = jnp.pad(joined, (0, owners * vec_per - joined.shape[0])).reshape(owners, vec_per)
        joined = jnp.pad(joined, ((0, 0), (0, VEC_ROWS * BS - vec_per)))
        return joined.astype(bf16).reshape(owners, VEC_ROWS, BS)
    return pl.pallas_call(
        functools.partial(pack_kernel, vec_per),
        out_shape=jax.ShapeDtypeStruct((owners, VEC_ROWS, BS), f32),
        grid=(1,),
        in_specs=[fixed(p.shape) for p in pieces],
        out_specs=fixed((owners, VEC_ROWS, BS)),
        compiler_params=params(),
        cost_estimate=cost(0, owners * vec_per * 8),
    )(*pieces).astype(bf16)


def embed_kernel(*refs):
    *parts, vec, weight, out = refs
    size = BASE_PIX // CHUNKS
    total = vec[:, :HALF]
    for c in range(CHUNKS):
        total = total + dot(parts[c][...], weight[c * size : (c + 1) * size, :])
    out[...] = total.astype(bf16)


def embed_call(chunks, vec, panels):
    tokens = chunks[0].shape[0]
    return pl.pallas_call(
        embed_kernel,
        out_shape=jax.ShapeDtypeStruct((tokens, HALF), bf16),
        grid=(tokens // ROWS,),
        in_specs=[rows_spec(BASE_PIX // CHUNKS)] * CHUNKS
        + [fixed(vec.shape), fixed((BASE_PIX, HALF), PANELS["base"] // BASE_PIX)],
        out_specs=rows_spec(HALF),
        compiler_params=params(),
        cost_estimate=cost(2 * tokens * BASE_PIX * HALF, tokens * BASE_PIX * 3),
    )(*chunks, vec, panels)


def qkv_kernel(layer, first, core, *refs):
    if first:
        own, recv, vec, weight, hid, normed, q_ref, k_ref, v_ref = refs
        mine, theirs = own[...].astype(f32), recv[...].astype(f32)
        low = core[0] == 0
        values = jnp.concatenate(
            [jnp.where(low, mine, theirs), jnp.where(low, theirs, mine)], axis=1
        )
    else:
        base, own, recv, vec, weight, hid, normed, q_ref, k_ref, v_ref = refs
        values = base[...] + (own[...].astype(f32) + recv[...].astype(f32))
    hid[...] = values
    unit, unused = norm_stats(values)
    low = (unit * vec_piece(vec, layer, "g1") + vec_piece(vec, layer, "s1")).astype(bf16)
    normed[...] = low
    q_ref[...] = (dot(low, weight[0:D, :]) + vec_piece(vec, layer, "bq")).astype(bf16)
    k_ref[...] = dot(low, weight[D : 2 * D, :]).astype(bf16)
    v_ref[...] = (dot(low, weight[2 * D : 3 * D, :]) + vec_piece(vec, layer, "bv")).astype(bf16)


def qkv_call(layer, base, own, recv, core, vec, panels):
    tokens = own.shape[0]
    shape = lambda width, kind: jax.ShapeDtypeStruct((tokens, width), kind)
    outs = [shape(D, f32), shape(D, bf16)] + [shape(HALF, bf16)] * 3
    operands = ([] if base is None else [base]) + [own, recv]
    return pl.pallas_call(
        functools.partial(qkv_kernel, layer, base is None),
        out_shape=outs,
        grid_spec=pltpu.PrefetchScalarGridSpec(
            num_scalar_prefetch=1,
            grid=(tokens // ROWS,),
            in_specs=[rows_spec(o.shape[1]) for o in operands]
            + [fixed(vec.shape), fixed((3 * D, HALF), PANELS["qkv"][layer] // (3 * D))],
            out_specs=[rows_spec(o.shape[1]) for o in outs],
        ),
        compiler_params=params(),
        cost_estimate=cost(2 * tokens * D * 3 * HALF, tokens * D * 14),
    )(core, *operands, vec, panels)


def head_masks():
    lane = lax.broadcasted_iota(jnp.int32, (1, 2 * HEAD_DIM), 1)
    low = (lane < HEAD_DIM).astype(f32).astype(bf16)
    high = (lane >= HEAD_DIM).astype(f32).astype(bf16)
    return low, high


def attend_kernel(layer, q_ref, k_ref, v_ref, seg_q, seg_k, vec, w_out, o_ref, lse_ref, part):
    masks = head_masks()
    same = seg_q[...] == seg_k[...]
    lane = lax.broadcasted_iota(jnp.int32, (ROWS, BS), 1)
    totals = jnp.zeros((ROWS, BS), f32)
    scale = jnp.asarray(HEAD_DIM ** (-0.5), bf16)
    for pair in range(HEADS // 2):
        cols = slice(pair * BS, (pair + 1) * BS)
        q_two = q_ref[:, cols] * scale
        k_two = k_ref[:, cols]
        v_two = v_ref[:, cols]
        mixed = None
        for side in range(2):
            scores = dot_nt(q_two * masks[side], k_two)
            scores = jnp.where(same, scores, masked_score)
            top = jnp.max(scores, axis=1, keepdims=True)
            expo = jnp.exp(scores - top)
            total = jnp.sum(expo, axis=1, keepdims=True)
            weights = (expo * (1.0 / total)).astype(bf16)
            term = dot(weights, v_two * masks[side])
            mixed = term if mixed is None else mixed + term
            totals = jnp.where(lane == 2 * pair + side, top + jnp.log(total), totals)
        o_ref[:, cols] = mixed.astype(bf16)
    lse_ref[...] = totals.T[0:8, :]
    low = o_ref[...]
    bias = vec_piece(vec, layer, "bo")
    for panel in range(TENSOR):
        area = slice(panel * HALF, (panel + 1) * HALF)
        part[:, area] = (dot(low, w_out[area, :]) + bias[:, area]).astype(bf16)


def attend_call(layer, queries, keys, values, seg_col, seg_row, vec, panels):
    tokens = queries.shape[0]
    return pl.pallas_call(
        functools.partial(attend_kernel, layer),
        out_shape=[
            jax.ShapeDtypeStruct((tokens, HALF), bf16),
            jax.ShapeDtypeStruct((8, tokens), f32),
            jax.ShapeDtypeStruct((tokens, D), bf16),
        ],
        grid=(tokens // ROWS,),
        in_specs=[
            rows_spec(HALF),
            fixed(keys.shape),
            fixed(values.shape),
            rows_spec(1),
            fixed(seg_row.shape),
            fixed(vec.shape),
            fixed((D, HALF), PANELS["out"][layer] // D),
        ],
        out_specs=[
            rows_spec(HALF),
            pl.BlockSpec((8, ROWS), lambda i: (0, i)),
            rows_spec(D),
        ],
        compiler_params=params(),
        cost_estimate=cost(8 * HEADS * tokens * tokens * BS, tokens * D * 8, HEADS * tokens * tokens),
    )(queries, keys, values, seg_col, seg_row, vec, panels)


def gelu_parts(values):
    cdf = 0.5 * (1.0 + lax.erf(values * 0.7071067811865476))
    pdf = 0.3989422804014327 * jnp.exp(-0.5 * values * values)
    return values * cdf, cdf + values * pdf


def mlp_kernel(layer, base, own, recv, vec, w_up, w_down, hid, normed, act, slope, part):
    values = base[...] + (own[...].astype(f32) + recv[...].astype(f32))
    hid[...] = values
    unit, unused = norm_stats(values)
    low = (unit * vec_piece(vec, layer, "g2") + vec_piece(vec, layer, "s2")).astype(bf16)
    normed[...] = low
    bias_up = vec_piece(vec, layer, "b1")
    for panel in range(HALF_FF // HALF):
        area = slice(panel * HALF, (panel + 1) * HALF)
        up = dot(low, w_up[panel * D : (panel + 1) * D, :]) + bias_up[:, area]
        gelu, grad = gelu_parts(up)
        act[:, area] = gelu.astype(bf16)
        slope[:, area] = grad.astype(bf16)
    bias_down = vec_piece(vec, layer, "b2")
    hidden_units = act[...]
    for panel in range(TENSOR):
        area = slice(panel * HALF, (panel + 1) * HALF)
        down = dot(hidden_units, w_down[panel * HALF_FF : (panel + 1) * HALF_FF, :])
        part[:, area] = (down + bias_down[:, area]).astype(bf16)


def mlp_call(layer, base, own, recv, vec, panels):
    tokens = base.shape[0]
    shape = lambda width, kind: jax.ShapeDtypeStruct((tokens, width), kind)
    outs = [shape(D, f32), shape(D, bf16), shape(HALF_FF, bf16), shape(HALF_FF, bf16), shape(D, bf16)]
    return pl.pallas_call(
        functools.partial(mlp_kernel, layer),
        out_shape=outs,
        grid=(tokens // ROWS,),
        in_specs=[rows_spec(D)] * 3
        + [
            fixed(vec.shape),
            fixed((2 * HALF_FF, HALF), PANELS["up"][layer] // (2 * HALF_FF)),
            fixed((2 * HALF_FF, HALF), PANELS["down"][layer] // (2 * HALF_FF)),
        ],
        out_specs=[rows_spec(o.shape[1]) for o in outs],
        compiler_params=params(),
        cost_estimate=cost(4 * tokens * D * HALF_FF, tokens * D * 24, 2 * tokens * HALF_FF),
    )(base, own, recv, vec, panels, panels)


def mlp_back_kernel(layer, summed, *refs):
    if summed:
        base, own, recv, *refs = refs
        (hid, slope, vec, w_up, w_down, grad_full, grad_low, du_ref, back, dgain, dshift, db1, db2) = refs
        values = base[...].astype(f32) + (own[...].astype(f32) + recv[...].astype(f32))
        grad_full[...] = values
        low = values.astype(bf16)
    else:
        base, valid, *refs = refs
        (hid, slope, vec, w_up, w_down, grad_low, du_ref, back, dgain, dshift, db1, db2) = refs
        low = (base[...].astype(f32) * valid[...]).astype(bf16)
    grad_low[...] = low
    accumulate(db2, jnp.sum(low.astype(f32), axis=0, keepdims=True))
    for part in range(HALF_FF // HALF):
        area = slice(part * HALF, (part + 1) * HALF)
        grad_act = None
        for panel in range(TENSOR):
            start = panel * HALF_FF + part * HALF
            term = dot_nt(low[:, panel * HALF : (panel + 1) * HALF], w_down[start : start + HALF, :])
            grad_act = term if grad_act is None else grad_act + term
        du_ref[:, area] = (grad_act * slope[:, area].astype(f32)).astype(bf16)
    grad_normed = None
    for panel in range(HALF_FF // HALF):
        area = slice(panel * HALF, (panel + 1) * HALF)
        term = dot_nt(du_ref[:, area], w_up[panel * D : (panel + 1) * D, :])
        grad_normed = term if grad_normed is None else grad_normed + term
    accumulate(db1, jnp.sum(du_ref[...].astype(f32), axis=0, keepdims=True))
    part_back, gain_grad, shift_grad = norm_back(hid[...], vec_piece(vec, layer, "g2"), grad_normed)
    back[...] = part_back.astype(bf16)
    accumulate(dgain, gain_grad)
    accumulate(dshift, shift_grad)


def mlp_back_call(layer, base, own, recv, valid, hid, slope, vec, panels):
    tokens = base.shape[0]
    summed = own is not None
    shape = lambda width, kind: jax.ShapeDtypeStruct((tokens, width), kind)
    line = lambda width: jax.ShapeDtypeStruct((1, width), f32)
    outs = ([shape(D, f32)] if summed else []) + [shape(D, bf16), shape(HALF_FF, bf16), shape(D, bf16)]
    lines = [line(D), line(D), line(HALF_FF), line(D)]
    extra = [own, recv] if summed else [valid]
    return pl.pallas_call(
        functools.partial(mlp_back_kernel, layer, summed),
        out_shape=outs + lines,
        grid=(tokens // ROWS,),
        in_specs=[rows_spec(D)]
        + [rows_spec(e.shape[1]) for e in extra]
        + [
            rows_spec(D),
            rows_spec(HALF_FF),
            fixed(vec.shape),
            fixed((2 * HALF_FF, HALF), PANELS["up"][layer] // (2 * HALF_FF)),
            fixed((2 * HALF_FF, HALF), PANELS["down"][layer] // (2 * HALF_FF)),
        ],
        out_specs=[rows_spec(o.shape[1]) for o in outs] + [fixed(o.shape) for o in lines],
        compiler_params=params(),
        cost_estimate=cost(4 * tokens * D * HALF_FF, tokens * D * 24),
    )(base, *extra, hid, slope, vec, panels, panels)


def attend_back_kernel(
    low_ref, high_ref, base, own, recv, q_ref, k_ref, v_ref, o_ref, lse_ref, seg_k, seg_q, w_out,
    full_ref, grad_low, dq_ref, dk_ref, dv_ref, dbo, dk_acc, dv_acc, dq_acc, do_ref,
):
    step = pl.program_id(0)

    @pl.when(step == 0)
    def _():
        dk_acc[...] = jnp.zeros_like(dk_acc)
        dv_acc[...] = jnp.zeros_like(dv_acc)

    values = base[...].astype(f32) + (own[...].astype(f32) + recv[...].astype(f32))
    full_ref[...] = values
    low = values.astype(bf16)
    grad_low[...] = low
    accumulate(dbo, jnp.sum(low.astype(f32), axis=0, keepdims=True))
    grad_mixed = None
    for panel in range(TENSOR):
        area = slice(panel * HALF, (panel + 1) * HALF)
        term = dot_nt(low[:, area], w_out[area, :])
        grad_mixed = term if grad_mixed is None else grad_mixed + term
    do_ref[...] = grad_mixed.astype(bf16)
    product = do_ref[...].astype(f32) * o_ref[...].astype(f32)
    head = lax.broadcasted_iota(jnp.int32, (8, HALF), 0)
    lane = lax.broadcasted_iota(jnp.int32, (8, HALF), 1)
    pick = ((lane >= head * HEAD_DIM) & (lane < (head + 1) * HEAD_DIM)).astype(f32)
    inner = dot_nt(pick, product, precise)
    dq_acc[...] = jnp.zeros_like(dq_acc)
    masks = head_masks()
    scale = jnp.asarray(HEAD_DIM ** (-0.5), bf16)
    seg_row = seg_q[...]

    def one_block(block, carried):
        rows = pl.ds(pl.multiple_of(block * ROWS, ROWS), ROWS)
        same = seg_k[rows, :] == seg_row
        for pair in range(HEADS // 2):
            cols = slice(pair * BS, (pair + 1) * BS)
            q_two = q_ref[:, cols] * scale
            do_two = do_ref[:, cols]
            k_two = k_ref[rows, cols]
            v_two = v_ref[rows, cols]
            dv_two = dk_two = dq_two = None
            for side in range(2):
                at = 2 * pair + side
                q_one = q_two * masks[side]
                do_one = do_two * masks[side]
                scores = dot_nt(k_two, q_one)
                prob = jnp.where(same, jnp.exp(scores - lse_ref[at : at + 1, :]), 0.0)
                grad_prob = dot_nt(v_two, do_one)
                grad_scores = (prob * (grad_prob - inner[at : at + 1, :])).astype(bf16)
                dv_one = dot(prob.astype(bf16), do_one)
                dk_one = dot(grad_scores, q_one)
                dq_one = dot_tn(grad_scores, k_two * masks[side])
                dv_two = dv_one if dv_two is None else dv_two + dv_one
                dk_two = dk_one if dk_two is None else dk_two + dk_one
                dq_two = dq_one if dq_two is None else dq_two + dq_one
            dv_acc[rows, cols] += dv_two
            dk_acc[rows, cols] += dk_two
            dq_acc[:, cols] += dq_two
        return carried

    lax.fori_loop(low_ref[step], high_ref[step], one_block, 0)
    dq_ref[...] = (dq_acc[...] * HEAD_DIM ** (-0.5)).astype(bf16)

    @pl.when(step == pl.num_programs(0) - 1)
    def _():
        dk_ref[...] = dk_acc[...].astype(bf16)
        dv_ref[...] = dv_acc[...].astype(bf16)


def attend_back_call(
    layer, first, last, base, own, recv, queries, keys, values, mixed, lse, seg_col, seg_row, panels
):
    tokens = base.shape[0]
    shape = lambda width, kind: jax.ShapeDtypeStruct((tokens, width), kind)
    whole = (tokens, HALF)
    return pl.pallas_call(
        attend_back_kernel,
        out_shape=[
            shape(D, f32),
            shape(D, bf16),
            shape(HALF, bf16),
            shape(HALF, bf16),
            shape(HALF, bf16),
            jax.ShapeDtypeStruct((1, D), f32),
        ],
        grid_spec=pltpu.PrefetchScalarGridSpec(
            num_scalar_prefetch=2,
            grid=(tokens // ROWS,),
            in_specs=[
                rows_spec(D),
                rows_spec(D),
                rows_spec(D),
                rows_spec(HALF),
                fixed(whole),
                fixed(whole),
                rows_spec(HALF),
                pl.BlockSpec((8, ROWS), lambda i, *_: (0, i)),
                fixed(seg_col.shape),
                pl.BlockSpec((1, ROWS), lambda i, *_: (0, i)),
                fixed((D, HALF), PANELS["out"][layer] // D),
            ],
            out_specs=[
                rows_spec(D),
                rows_spec(D),
                rows_spec(HALF),
                fixed(whole),
                fixed(whole),
                fixed((1, D)),
            ],
            scratch_shapes=[
                pltpu.VMEM(whole, f32),
                pltpu.VMEM(whole, f32),
                pltpu.VMEM((ROWS, HALF), f32),
                pltpu.VMEM((ROWS, HALF), bf16),
            ],
        ),
        compiler_params=params(),
        cost_estimate=cost(14 * HEADS * tokens * tokens * BS, tokens * D * 20, HEADS * tokens * tokens),
    )(first, last, base, own, recv, queries, keys, values, mixed, lse, seg_col, seg_row, panels)


def qkv_back_kernel(layer, dq, dk, dv, hid, vec, weight, back, dgain, dshift, dbq, dbv):
    grad_normed = (
        dot_nt(dq[...], weight[0:D, :])
        + dot_nt(dk[...], weight[D : 2 * D, :])
        + dot_nt(dv[...], weight[2 * D : 3 * D, :])
    )
    part_back, gain_grad, shift_grad = norm_back(hid[...], vec_piece(vec, layer, "g1"), grad_normed)
    back[...] = part_back.astype(bf16)
    accumulate(dgain, gain_grad)
    accumulate(dshift, shift_grad)
    accumulate(dbq, jnp.sum(dq[...].astype(f32), axis=0, keepdims=True))
    accumulate(dbv, jnp.sum(dv[...].astype(f32), axis=0, keepdims=True))


def qkv_back_call(layer, dq, dk, dv, hid, vec, panels):
    tokens = dq.shape[0]
    line = lambda width: jax.ShapeDtypeStruct((1, width), f32)
    lines = [line(D), line(D), line(HALF), line(HALF)]
    return pl.pallas_call(
        functools.partial(qkv_back_kernel, layer),
        out_shape=[jax.ShapeDtypeStruct((tokens, D), bf16)] + lines,
        grid=(tokens // ROWS,),
        in_specs=[rows_spec(HALF)] * 3
        + [
            rows_spec(D),
            fixed(vec.shape),
            fixed((3 * D, HALF), PANELS["qkv"][layer] // (3 * D)),
        ],
        out_specs=[rows_spec(D)] + [fixed(o.shape) for o in lines],
        compiler_params=params(),
        cost_estimate=cost(2 * tokens * D * 3 * HALF, tokens * D * 10),
    )(dq, dk, dv, hid, vec, panels)


def split(values):
    high = values.astype(bf16)
    return high, (values - high.astype(f32)).astype(bf16)


def product(left, right, left_dim, right_dim):
    def one(a, b):
        return lax.dot_general(
            a, b, (((left_dim,), (right_dim,)), ((), ())), preferred_element_type=f32
        )

    return one(left[0], right[0]) + (one(left[0], right[1]) + one(left[1], right[0]))


def owner_kernel(per, used, home, near, far, master, left, right, moment, variance, grad, out, out_mom, out_var):
    here = range(per)
    first = pl.program_id(0) * per
    lefts = [split(left[i]) for i in here]
    rights = [split(right[i]) for i in here]
    rotated = []
    for i in here:
        rows = slice(i * BS, (i + 1) * BS)
        tile = jnp.where(home[0] > 0, near[rows, :].astype(f32), far[rows, :].astype(f32))
        tile = jnp.where(used[first + i] > 0, tile, 0.0)
        grad[i] = tile
        tile = tile.astype(bf16)
        rotated.append(split(dot_tn(lefts[i][0], tile) + dot_tn(lefts[i][1], tile)))
    rotated = [product(rotated[i], rights[i], 1, 0) for i in here]
    steps = []
    for i in here:
        new_moment = decay * moment[i] + (1.0 - decay) * rotated[i]
        new_variance = decay * variance[i] + (1.0 - decay) * rotated[i] * rotated[i]
        out_mom[i] = new_moment
        out_var[i] = new_variance
        steps.append(split(new_moment / (jnp.sqrt(new_variance) + adam_eps)))
    returned = [split(product(lefts[i], steps[i], 1, 0)) for i in here]
    returned = [product(returned[i], rights[i], 1, 1) for i in here]
    for i in here:
        out[i] = master[i] - matrix_rate * returned[i]


def owner_call(used, home, near, far, *arrays):
    count = arrays[0].shape[0]
    per = min(8, count)
    block = pl.BlockSpec((per, BS, BS), lambda i, *_: (i, 0, 0))
    return pl.pallas_call(
        functools.partial(owner_kernel, per),
        out_shape=[jax.ShapeDtypeStruct(arrays[0].shape, f32)] * 4,
        grid_spec=pltpu.PrefetchScalarGridSpec(
            num_scalar_prefetch=2,
            grid=(count // per,),
            in_specs=[pl.BlockSpec((per * BS, BS), lambda i, *_: (i, 0))] * 2 + [block] * 5,
            out_specs=[block] * 4,
        ),
        compiler_params=params(),
        cost_estimate=cost(count * 88 * BS**3, count * BS * BS * 38),
    )(used, home, near, far, *arrays)


def reduce_kernel(carrying, last, *refs):
    block, arrived, *refs = refs
    total = block[...].astype(f32) + arrived[...].astype(f32)
    if carrying:
        carried, *refs = refs
        total = total + carried[...].astype(f32)
    if last:
        [out] = refs
    else:
        following, out, later = refs
        later[...] = following[...]
    out[...] = total.astype(bf16)


def reduce_call(j, n, buffer, arrived, carried, payload):
    last = j == 3
    at = lambda j, x_rel: pl.BlockSpec((payload, BS), lambda i: ((j * 2 + x_rel) * 2 + n, 0))
    whole = fixed((payload, BS))
    operands = [buffer, arrived] + ([] if carried is None else [carried])
    specs = [at(j, 0)] + [whole] * (len(operands) - 1)
    if not last:
        operands.append(buffer)
        specs.append(at(j + 1, 1))
    outs = [jax.ShapeDtypeStruct((payload, BS), bf16)] * (1 if last else 2)
    made = pl.pallas_call(
        functools.partial(reduce_kernel, carried is not None, last),
        out_shape=outs,
        grid=(1,),
        in_specs=specs,
        out_specs=[whole] * len(outs),
        compiler_params=params(),
        cost_estimate=cost(payload * BS * 3, payload * BS * 12),
    )(*operands)
    return (made[0], None) if last else made


class Routes:
    def __init__(self, dp_n):
        pairs = [(d, t) for d in range(dp_n) for t in range(TENSOR)]
        at = lambda d, t: d * TENSOR + t
        home = [(d, t) for d, t in pairs if d % 2 == t]
        away = [(d, t) for d, t in pairs if d % 2 != t]
        self.core_all = [(at(d, t), at(d ^ 1, t)) for d, t in pairs]
        self.core_out = [(at(d, t), at(d ^ 1, t)) for d, t in home]
        self.core_in = [(at(d, t), at(d ^ 1, t)) for d, t in away]
        self.y_all = [(at(d, t), at(d, 1 - t)) for d, t in pairs]
        self.y_out = [(at(d, t), at(d, 1 - t)) for d, t in home]
        self.y_in = [(at(d, t), at(d, 1 - t)) for d, t in away]
        self.x_home = [(at(d, t), at(d ^ 2, t)) for d, t in home]
        self.x_away = [(at(d, t), at(d ^ 2, t)) for d, t in away]
        self.z_home = [(at(d, t), at((d + 4) % dp_n, t)) for d, t in home]


def send(value, route):
    return lax.ppermute(value, AXES, route)


def shards(
    patches,
    cotangent,
    image_size,
    block_slot,
    pinv,
    master_slots,
    left_basis,
    right_basis,
    mom_slots,
    var_slots,
    vec_master,
    vec_mom,
    vec_var,
):
    dp_n = lax.axis_size("dp")
    dp_pos = lax.axis_index("dp")
    y_pos = lax.axis_index("tensor")
    core = dp_pos % 2
    home = core == y_pos
    routes = Routes(dp_n)
    grid3 = dp_n == 16
    tokens_n = patches.shape[0]
    slots_per = master_slots.shape[1]
    vec_per = vec_master.shape[1]
    slots_n = slots_per * dp_n
    payload = slots_per * BS + VEC_ROWS

    patches = jnp.where(home, patches, send(patches, routes.core_out))
    cotangent = jnp.where(home, cotangent, send(cotangent, routes.core_out))
    size_row = jnp.where(home, image_size, send(image_size, routes.core_out))[0]
    own_slots = block_slot[0]
    slot_other = send(block_slot, routes.y_all)

    lengths = jnp.where(
        size_row == 0, LEN_A, jnp.where(size_row == 1, LEN_B, jnp.where(size_row == 2, LEN_C, 0))
    )
    order = jnp.arange(IMG_DEV)
    ends_at = jnp.sum(jnp.where(order[None, :] <= order[:, None], lengths[None, :], 0), axis=1)
    places = jnp.arange(tokens_n)
    segment = jnp.sum((places[:, None] >= ends_at[None, :]).astype(jnp.int32), axis=1)
    in_image = segment[:, None] == order[None, :]
    select = jnp.stack(
        [jnp.any(in_image & (size_row == s)[None, :], axis=1) for s in range(3)], axis=1
    )
    valid_col = (segment < IMG_DEV).astype(f32)[:, None]
    seg_col = segment[:, None]
    seg_row = segment[None, :]
    blocks_n = tokens_n // ROWS
    starts = jnp.arange(blocks_n) * ROWS
    begun = ends_at[None, :] <= starts[:, None]
    first_tok = jnp.max(jnp.where(begun, ends_at[None, :], 0), axis=1)
    after = ends_at[None, :] > (starts + ROWS - 1)[:, None]
    last_tok = jnp.min(jnp.where(after, ends_at[None, :], tokens_n), axis=1)
    first_blk = (first_tok // ROWS).astype(jnp.int32)
    last_blk = ((last_tok + ROWS - 1) // ROWS).astype(jnp.int32)

    select_low = select.astype(bf16)
    class_col = jnp.sum(jnp.where(select, jnp.arange(1, 4)[None, :], 0), axis=1, keepdims=True) - 1
    present = jnp.any(select.reshape(blocks_n, ROWS, 3), axis=1).astype(jnp.int32)

    def expand(which):
        return expand_call(which, present, patches, class_col, pinv)

    vec_low = jnp.pad(vec_master[0].astype(bf16), (0, VEC_ROWS * BS - vec_per))
    own_pack = jnp.concatenate(
        [
            master_slots[0].astype(bf16).reshape(slots_per * BS, BS),
            vec_low.reshape(VEC_ROWS, BS),
        ],
        axis=0,
    )
    flag = home.astype(jnp.int32).reshape(1)
    if grid3:
        x_pos = (dp_pos // 2) % 2
        z_pos = dp_pos // 4
        packs = [[own_pack], [send(own_pack, routes.core_in)]]
        across, over_y, corner = [[], []], [[], []], [[], []]
        token = jnp.zeros((8, BS), f32)
        chunks = []
        for j in range(5):
            for n in range(2):
                moved = []
                if j < 4:
                    moved += [send(packs[n][j], routes.x_home), send(packs[n][j], routes.y_out)]
                if j:
                    source, route = (across, routes.y_out) if n == 0 else (over_y, routes.x_away)
                    moved.append(send(source[n][j - 1], route))
                if j < 3:
                    moved.append(send(packs[n][j], routes.z_home))
                work = []
                if j + n == 0:
                    work = [slot_other]
                if 1 <= 2 * j + n <= CHUNKS:
                    work = [expand(2 * j + n - 1)]
                if j < 4:
                    token, *moved = fence(token, *moved, *work)
                    if j + n == 0:
                        slot_other = moved.pop()
                    elif work:
                        chunks.append(moved.pop())
                if j < 3:
                    packs[n].append(moved.pop())
                if j:
                    corner[n].append(moved.pop())
                if j < 4:
                    across[n].append(moved[0])
                    over_y[n].append(moved[1])
        first, second, owner = [], [], []
        for j in range(4):
            first += [packs[0][j], packs[1][j], across[0][j], across[1][j]]
            second += [over_y[0][j], over_y[1][j], corner[0][j], corner[1][j]]
            for x_rel in range(2):
                for n in range(2):
                    owner.append(((z_pos - j) % 4) * 4 + (x_pos ^ x_rel) * 2 + (core ^ n))
        first = [v[None] for v in first]
        second = [v[None] for v in second]
        owner = jnp.stack(owner).astype(jnp.int32)
    else:
        everything = lax.all_gather(own_pack, AXES, axis=0)
        everything = everything.reshape(dp_n, TENSOR, payload, BS)
        first = [jnp.where(core == 0, everything[:, 0], everything[:, 1])]
        second = []
        owner = jnp.arange(dp_n, dtype=jnp.int32)
        chunks = [expand(c) for c in range(CHUNKS)]
    slot_list = jnp.where(home, block_slot, slot_other)[0]
    named = slot_list[None, :] == jnp.arange(slots_n)[:, None]
    used = jnp.any(named, axis=1)
    drow = jnp.where(used, jnp.sum(jnp.where(named, TARGET_ROW[None, :], 0), axis=1), -1)
    dcol = jnp.sum(jnp.where(named, TARGET_COL[None, :], 0), axis=1)
    panels, vec_rows = gather_tiles(first, second, owner, drow, dcol, flag, slots_per, dp_n)
    vec = vec_rows.reshape(dp_n, VEC_ROWS * BS)[:, :vec_per].astype(f32).reshape(1, dp_n * vec_per)

    embedded = embed_call(chunks, vec, panels)
    embedded_other = send(embedded, routes.core_all)
    core_flag = core.astype(jnp.int32).reshape(1)

    caches = []
    hidden, own, recv = None, embedded, embedded_other
    for layer in range(LAYERS):
        hidden, normed, queries, keys, values = qkv_call(
            layer, hidden, own, recv, core_flag, vec, panels
        )
        mixed, lse, part = attend_call(
            layer, queries, keys, values, seg_col, seg_row, vec, panels
        )
        other = send(part, routes.core_all)
        middle, normed2, act, slope, own = mlp_call(layer, hidden, part, other, vec, panels)
        recv = send(own, routes.core_all)
        caches.append((hidden, normed, queries, keys, values, mixed, lse, middle, normed2, act, slope))
        hidden = middle
    out_low = ((hidden + (own.astype(f32) + recv.astype(f32))) * valid_col).astype(bf16)

    owners = jnp.arange(dp_n)
    if grid3:
        place = (
            ((z_pos - 1 - owners // 4) % 4) * 4
            + (x_pos ^ ((owners // 2) % 2)) * 2
            + (core ^ (owners % 2))
        ).astype(jnp.int32)
        half_at = x_pos.astype(jnp.int32).reshape(1)
    else:
        place = owners.astype(jnp.int32)
        half_at = jnp.zeros((1,), jnp.int32)
    slot_owner = slot_list // slots_per
    owner_place = jnp.sum(
        jnp.where(slot_owner[:, None] == owners[None, :], place[None, :], 0), axis=1
    )
    tile_pos = (owner_place * payload + (slot_list % slots_per) * BS).astype(jnp.int32)
    vec_pos = (place * payload + slots_per * BS).astype(jnp.int32)
    total_rows = dp_n * payload
    offsets = {"base": 0}
    count = BASE_PIX // BS * (HALF // BS)
    for layer in range(LAYERS):
        for name, size in (("qkv", 3 * D * HALF), ("out", D * HALF), ("up", D * HALF_FF), ("down", D * HALF_FF)):
            offsets[name, layer] = count
            count += size // (BS * BS)

    def place_tiles(key, matrix, arrived, buffer):
        tiles = matrix.size // (BS * BS)
        pos = tile_pos[offsets[key] : offsets[key] + tiles]
        rows_n = matrix.shape[0] // 2 if matrix.shape[0] > HALF else HALF
        return scatter_matrix(pos, matrix, arrived, half_at, buffer, total_rows, rows_n)

    def over(matrix):
        return send(matrix, routes.y_in) if grid3 else None

    def halves_of(matrix):
        size = matrix.shape[0] // 2
        mine = lax.dynamic_slice_in_dim(matrix, x_pos * size, size, 0)
        theirs = lax.dynamic_slice_in_dim(matrix, (1 - x_pos) * size, size, 0)
        return mine, theirs

    def half_sum(matrix, arrived):
        mine, unused = halves_of(matrix)
        return (mine.astype(f32) + arrived.astype(f32)).astype(bf16)

    def beside(matrix):
        return send(halves_of(matrix)[1], routes.x_away) if grid3 else None

    def hold(*arrays):
        kept = [a for a in arrays if a is not None]
        done = iter(fence(*kept))
        return [None if a is None else next(done) for a in arrays]

    top, low = 1, 0
    vec_grads = [None] * LAYERS

    def mlp_step(layer, grad, own, recv):
        middle, normed2, act, slope = caches[layer][7:11]
        made = mlp_back_call(layer, grad, own, recv, valid_col, middle, slope, vec, panels)
        if own is not None:
            return made
        return [made[0]] + list(made)

    def attend_step(layer, grad, part, other):
        hid_in, normed, queries, keys, values, mixed, lse = caches[layer][:7]
        return attend_back_call(
            layer, first_blk, last_blk, grad, part, other, queries, keys, values, mixed, lse,
            seg_col, seg_row, panels,
        )

    grad, grad_low, du, part, dg2, ds2, db1, db2 = mlp_step(top, cotangent, None, None)
    other = send(part, routes.core_all)
    gd1 = dot_tn(caches[top][9], grad_low).astype(bf16)
    gu1 = dot_tn(caches[top][8], du).astype(bf16)
    part, other, gd1, gu1 = fence(part, other, gd1, gu1)
    ad1 = over(gd1)
    grad, grad_low, dq, dk, dv, dbo = attend_step(top, grad, part, other)
    dq, dk, dv, ad1 = hold(dq, dk, dv, ad1)
    au1 = over(gu1)
    own, dg1, ds1, dbq, dbv = qkv_back_call(top, dq, dk, dv, caches[top][0], vec, panels)
    recv = send(own, routes.core_all)
    go1 = dot_tn(caches[top][5], grad_low).astype(bf16)
    gq1 = dot_tn(caches[top][1], jnp.concatenate([dq, dk, dv], axis=1)).astype(bf16)
    vec_grads[top] = [dg1, ds1, dbq, dbv, dbo, dg2, ds2, db1, db2]
    grad, grad_low, du, part, dg2, ds2, db1, db2 = mlp_step(low, grad, own, recv)
    du, part, au1, go1, gq1 = hold(du, part, au1, go1, gq1)
    other = send(part, routes.core_all)
    xq1, ao1 = beside(gq1), over(go1)
    gd0 = dot_tn(caches[low][9], grad_low).astype(bf16)
    gu0 = dot_tn(caches[low][8], du).astype(bf16)
    part, other, gd0, gu0, xq1, ao1 = hold(part, other, gd0, gu0, xq1, ao1)
    aq1 = over(half_sum(gq1, xq1)) if grid3 else None
    xd0, xu0 = beside(gd0), beside(gu0)
    buffer = place_tiles(("down", top), gd1, ad1, None)
    buffer = place_tiles(("up", top), gu1, au1, buffer)
    grad, grad_low, dq, dk, dv, dbo = attend_step(low, grad, part, other)
    grad, grad_low, dq, dk, dv, aq1, xd0, xu0, buffer = hold(
        grad, grad_low, dq, dk, dv, aq1, xd0, xu0, buffer
    )
    hd0 = half_sum(gd0, xd0) if grid3 else None
    hu0 = half_sum(gu0, xu0) if grid3 else None
    dq, dk, dv, hd0, hu0 = hold(dq, dk, dv, hd0, hu0)
    ad0, au0 = over(hd0), over(hu0)
    own, dg1, ds1, dbq, dbv = qkv_back_call(low, dq, dk, dv, caches[low][0], vec, panels)
    recv = send(own, routes.core_all)
    gq0 = dot_tn(caches[low][1], jnp.concatenate([dq, dk, dv], axis=1)).astype(bf16)
    vec_grads[low] = [dg1, ds1, dbq, dbv, dbo, dg2, ds2, db1, db2]
    own, recv, gq0 = hold(own, recv, gq0)
    xq0 = beside(gq0)
    grad_emb, grad_emb_bias = embed_back_call(core_flag, grad, own, recv)
    gb = jnp.concatenate([dot_tn(c, grad_emb).astype(bf16) for c in chunks], axis=0)
    vec_grad = pack_call([grad_emb_bias] + vec_grads[0] + vec_grads[1], dp_n, vec_per)
    go0 = dot_tn(caches[low][5], grad_low).astype(bf16)
    gb, vec_grad, grad_emb, go0, gq0, xq0 = hold(gb, vec_grad, grad_emb, go0, gq0, xq0)
    xb = beside(gb)
    hq0 = half_sum(gq0, xq0) if grid3 else None
    aq0, ao0, av = over(hq0), over(go0), over(vec_grad)
    buffer = place_tiles(("out", top), go1, ao1, buffer)
    buffer = place_tiles(("qkv", top), gq1, aq1, buffer)
    buffer = place_tiles(("down", low), gd0, ad0, buffer)
    buffer = place_tiles(("up", low), gu0, au0, buffer)
    gb, xb, aq0, ao0, av, buffer = hold(gb, xb, aq0, ao0, av, buffer)
    hb = half_sum(gb, xb) if grid3 else None
    hb, gb, aq0, buffer = hold(hb, gb, aq0, buffer)
    ab = over(hb)
    buffer = place_tiles(("out", low), go0, ao0, buffer)
    buffer = scatter_vec(vec_pos, vec_grad, av, buffer)
    buffer = place_tiles(("qkv", low), gq0, aq0, buffer)
    ab, buffer, panels, grad_emb, out_low = hold(ab, buffer, panels, grad_emb, out_low)
    buffer = place_tiles("base", gb, ab, buffer)

    if grid3:
        token = jnp.zeros((8, BS), f32)
        order = (1, 0)
        resized = resize_call(panels, pinv)
        carried = {n: None for n in order}
        across = {n: send(buffer.reshape(4, 2, 2, payload, BS)[0, 1, n], routes.x_home) for n in order}
        rounded = {}
        for j in range(4):
            for n in order:
                extra = None
                if j == 0 and n == order[0]:
                    extra = resized
                token, across[n], carried[n], extra = hold(token, across[n], carried[n], extra)
                if extra is not None:
                    resized = extra
                total, later = reduce_call(j, n, buffer, across[n], carried[n], payload)
                if j < 3:
                    carried[n] = send(total, routes.z_home)
                    across[n] = send(later, routes.x_home)
                else:
                    rounded[n] = total
        near_grad, far_grad = rounded[0], send(rounded[1], routes.core_out)
    else:
        held = buffer.reshape(dp_n, 1, payload, BS).astype(f32)
        nothing = jnp.zeros_like(held)
        both = jnp.concatenate(
            [jnp.where(core == 0, held, nothing), jnp.where(core == 0, nothing, held)], axis=1
        )
        used_rows = jnp.repeat(used, BS).reshape(dp_n, 1, slots_per * BS, 1)
        used_rows = jnp.concatenate(
            [used_rows, jnp.ones((dp_n, 1, VEC_ROWS, 1), bool)], axis=2
        )
        both = jnp.where(used_rows, both, 0.0).reshape(dp_n * TENSOR * payload, BS)
        near_grad = lax.psum_scatter(both, AXES, scatter_dimension=0, tiled=True).astype(bf16)
        far_grad = near_grad
        resized = resize_call(panels, pinv)

    output = jnp.where(home, out_low, send(out_low, routes.y_out)).astype(f32)
    grad_pixels = sum(
        dot(grad_emb * select_low[:, s : s + 1], resized[s]) for s in range(3)
    ).astype(bf16)
    pixels_other = send(grad_pixels, routes.core_all)
    pixel_sides = [
        grad_pixels[:, s * HALF : (s + 1) * HALF].astype(f32)
        + pixels_other[:, s * HALF : (s + 1) * HALF].astype(f32)
        for s in range(TENSOR)
    ]
    near = jnp.where(core == 0, pixel_sides[0], pixel_sides[1])
    far = jnp.where(core == 0, pixel_sides[1], pixel_sides[0]).astype(bf16)
    patch_grad = jnp.where(home, near, send(far, routes.y_out).astype(f32))

    my_slots = dp_pos * slots_per + jnp.arange(slots_per)
    mine_used = jnp.any(own_slots[None, :] == my_slots[:, None], axis=1).astype(jnp.int32)
    owned_grad, new_master, new_mom, new_var = owner_call(
        mine_used, flag, near_grad, far_grad, master_slots[0], left_basis[0], right_basis[0], mom_slots[0], var_slots[0]
    )
    vec_rows = jnp.where(home, near_grad[slots_per * BS :], far_grad[slots_per * BS :])
    owned_vec_grad = vec_rows.astype(f32).reshape(VEC_ROWS * BS)[:vec_per]
    new_vec_mom = decay * vec_mom[0] + (1.0 - decay) * owned_vec_grad
    new_vec_var = decay * vec_var[0] + (1.0 - decay) * owned_vec_grad * owned_vec_grad
    new_vec = vec_master[0] - vector_rate * new_vec_mom / (jnp.sqrt(new_vec_var) + adam_eps)
    return (
        output,
        patch_grad,
        owned_grad[None],
        new_master[None],
        new_mom[None],
        new_var[None],
        owned_vec_grad[None],
        new_vec[None],
        new_vec_mom[None],
        new_vec_var[None],
    )


def solution(mesh):
    slots = P("tensor", "dp", None, None)
    vectors = P("tensor", "dp")
    tokens = P("dp", None)
    in_specs = (tokens, tokens, tokens, P("tensor", None), P()) + (slots,) * 5 + (vectors,) * 3
    out_specs = (tokens, P("dp", "tensor")) + (slots,) * 4 + (vectors,) * 4
    return jax.shard_map(shards, mesh=mesh, in_specs=in_specs, out_specs=out_specs, check_vma=False)
```

```python
import functools

import jax
import jax.numpy as jnp
import numpy as np
from jax import lax
from jax.experimental import pallas as pl
from jax.experimental.pallas import tpu as pltpu
from jax.sharding import PartitionSpec as P

D = 768
HEAD_DIM = 64
FF = 3072
BASE_PIX = 3072
LAYERS = 2
LEN_A = 196
LEN_B = 225
LEN_C = 576
IMG_DEV = 5
BS = 128
TENSOR = 2
HALF = D // TENSOR
HALF_FF = FF // TENSOR
HEADS = HALF // HEAD_DIM
ROWS = 256
KEYS = 512
VEC_ROWS = 16
CHUNKS = 4

AXES = ("dp", "tensor")
precise = lax.Precision.HIGHEST
masked_score = -1e30
norm_eps = 1e-06
adam_eps = 1e-08
decay = 0.5
matrix_rate = 0.05
vector_rate = 0.3
f32 = jnp.float32
bf16 = jnp.bfloat16
MIB = 1024 * 1024

PANELS = {
    "up": (0, 6144),
    "down": (3072, 9216),
    "base": 12288,
    "out": (15360, 20736),
    "qkv": (16128, 18432),
}
PANEL_ROWS = 21504


def tile_targets():
    rows, cols = [], []

    def add(start, rows_n, cols_n):
        for i in range(rows_n // BS):
            for j in range(cols_n // BS):
                panel, inner = divmod(j * BS, HALF)
                rows.append(start + panel * rows_n + i * BS)
                cols.append(inner)

    add(PANELS["base"], BASE_PIX, HALF)
    for layer in range(LAYERS):
        add(PANELS["qkv"][layer], D, 3 * HALF)
        add(PANELS["out"][layer], HALF, D)
        add(PANELS["up"][layer], D, HALF_FF)
        add(PANELS["down"][layer], HALF_FF, D)
    return np.array(rows, np.int32), np.array(cols, np.int32)


TARGET_ROW, TARGET_COL = tile_targets()
LAYER_VECS = (D, D, HALF, HALF, D, D, D, HALF_FF, D)
VEC_NAMES = ("g1", "s1", "bq", "bv", "bo", "g2", "s2", "b1", "b2")


def vec_offsets():
    offset = HALF
    found = []
    for layer in range(LAYERS):
        here = {}
        for name, length in zip(VEC_NAMES, LAYER_VECS):
            here[name] = (offset, length)
            offset += length
        found.append(here)
    return found


VEC_AT = vec_offsets()


def params(limit=24):
    return pltpu.CompilerParams(
        dimension_semantics=("arbitrary",), vmem_limit_bytes=limit * MIB
    )


def cost(flops, nbytes, trans=0):
    return pl.CostEstimate(flops=flops, bytes_accessed=nbytes, transcendentals=trans)


def rows_spec(width):
    return pl.BlockSpec((ROWS, width), lambda i, *_: (i, 0))


def fixed(shape, at=0):
    return pl.BlockSpec(shape, lambda i, *_: (at,) + (0,) * (len(shape) - 1))


def vec_piece(vec_ref, layer, name):
    start, length = VEC_AT[layer][name]
    return vec_ref[:, start : start + length]


def dot(left, right):
    return jnp.dot(left, right, preferred_element_type=f32)


def dot_nt(left, right, precision=None):
    return lax.dot_general(
        left, right, (((1,), (1,)), ((), ())), precision=precision, preferred_element_type=f32
    )


def dot_tn(left, right):
    return lax.dot_general(left, right, (((0,), (0,)), ((), ())), preferred_element_type=f32)


def joined(ref, start, rows_n, panels):
    return jnp.concatenate(
        [ref[start + p * rows_n : start + (p + 1) * rows_n, :] for p in range(panels)], axis=1
    )


def norm_stats(values):
    mean_val = jnp.mean(values, axis=-1, keepdims=True)
    centered = values - mean_val
    inv_std = lax.rsqrt(jnp.mean(centered * centered, axis=-1, keepdims=True) + norm_eps)
    return centered * inv_std, inv_std


def norm_back(values, gain, grad):
    unit, inv_std = norm_stats(values)
    scaled = grad * gain
    mean_s = jnp.mean(scaled, axis=-1, keepdims=True)
    mean_u = jnp.mean(scaled * unit, axis=-1, keepdims=True)
    back = inv_std * (scaled - mean_s - unit * mean_u)
    return (
        back,
        jnp.sum(grad * unit, axis=0, keepdims=True),
        jnp.sum(grad, axis=0, keepdims=True),
    )


def accumulate(ref, value):
    first = pl.program_id(0) == 0

    @pl.when(first)
    def _():
        ref[...] = value

    @pl.when(jnp.logical_not(first))
    def _():
        ref[...] += value


def fence(*arrays):
    def nothing(*refs):
        pass

    anywhere = pl.BlockSpec(memory_space=pl.ANY)
    return pl.pallas_call(
        nothing,
        out_shape=[jax.ShapeDtypeStruct(a.shape, a.dtype) for a in arrays],
        in_specs=[anywhere] * len(arrays),
        out_specs=[anywhere] * len(arrays),
        input_output_aliases={i: i for i in range(len(arrays))},
    )(*arrays)


def gather_kernel(slots, count_a, count_b, owner, drow, dcol, flag, *refs):
    first = refs[:count_a]
    second = refs[count_a : count_a + count_b]
    panels, vectors, held, sem, vec_sem = refs[count_a + count_b :]

    def copy_all(sources):
        at = 0
        for src in sources:
            for n in range(src.shape[0]):
                who = owner[at]
                at += 1

                def body(i, carried, src=src, n=n, who=who):
                    slot = who * slots + i
                    row = drow[slot]

                    @pl.when(row >= 0)
                    def _():
                        start = pl.multiple_of(i * BS, BS)
                        pltpu.make_async_copy(
                            src.at[n, pl.ds(start, BS), :],
                            held.at[
                                pl.ds(pl.multiple_of(row, BS), BS),
                                pl.ds(pl.multiple_of(dcol[slot], BS), BS),
                            ],
                            sem,
                        ).start()

                    return carried

                lax.fori_loop(0, slots, body, 0)
                pltpu.make_async_copy(
                    src.at[n, pl.ds(slots * BS, VEC_ROWS), :], vectors.at[who], vec_sem
                ).start()

    if count_b:

        @pl.when(flag[0] == 1)
        def _():
            copy_all(first)

        @pl.when(flag[0] == 0)
        def _():
            copy_all(second)
    else:
        copy_all(first)
    pltpu.make_async_copy(held, held, sem).wait()
    out = pltpu.make_async_copy(held, panels, sem)
    out.start()
    pltpu.make_async_copy(vectors, vectors, vec_sem).wait()
    out.wait()


def gather_tiles(first, second, owner, drow, dcol, flag, slots, owners):
    anywhere = pl.BlockSpec(memory_space=pl.ANY)
    return pl.pallas_call(
        functools.partial(gather_kernel, slots, len(first), len(second)),
        out_shape=(
            jax.ShapeDtypeStruct((PANEL_ROWS, HALF), bf16),
            jax.ShapeDtypeStruct((owners, VEC_ROWS, BS), bf16),
        ),
        grid_spec=pltpu.PrefetchScalarGridSpec(
            num_scalar_prefetch=4,
            grid=(1,),
            in_specs=[anywhere] * (len(first) + len(second)),
            out_specs=(anywhere, fixed((owners, VEC_ROWS, BS))),
            scratch_shapes=[
                pltpu.VMEM((PANEL_ROWS, HALF), bf16),
                pltpu.SemaphoreType.DMA,
                pltpu.SemaphoreType.DMA,
            ],
        ),
        compiler_params=params(),
        cost_estimate=cost(0, 4 * PANEL_ROWS * HALF),
    )(owner, drow, dcol, flag, *first, *second)


def scatter_kernel(rows_n, cols_n, steps, paired, parts, pos, part, own, *refs):
    @pl.when(part[1] > 0)
    def _():
        scatter_body(rows_n, cols_n, steps, paired, parts, pos, part, own, *refs)


def scatter_body(rows_n, cols_n, steps, paired, parts, pos, part, own, *refs):
    if paired:
        recv, *refs = refs
        span = pl.num_programs(0) // parts
        here = jnp.logical_or(parts == 1, pl.program_id(0) // span == part[0])
    target, buf, sems = refs[-3:]
    step = pl.program_id(0)
    slot = lax.rem(step, 2)
    per = rows_n // BS * (cols_n // BS)

    def wait(at):
        pltpu.make_async_copy(buf.at[at], buf.at[at], sems.at[at]).wait()

    @pl.when(step >= 2)
    def _():
        wait(slot)

    for i in range(rows_n // BS):
        for j in range(cols_n // BS):
            area = (slice(i * BS, (i + 1) * BS), slice(j * BS, (j + 1) * BS))
            value = own[area]
            if paired:
                more = jnp.where(here, recv[area].astype(f32), 0.0)
                value = (value.astype(f32) + more).astype(bf16)
            buf[slot, i * (cols_n // BS) + j] = value
    for n in range(per):
        pltpu.make_async_copy(
            buf.at[slot, n],
            target.at[pl.ds(pl.multiple_of(pos[step * per + n], 16), BS), :],
            sems.at[slot],
        ).start()

    @pl.when(step == pl.num_programs(0) - 1)
    def _():
        if steps > 1:
            wait(1 - slot)
        wait(slot)


def scatter_matrix(pos, own, recv, part, target, total_rows, rows_n):
    cols_n = own.shape[1]
    steps = own.shape[0] // rows_n
    anywhere = pl.BlockSpec(memory_space=pl.ANY)
    block = pl.BlockSpec((rows_n, cols_n), lambda i, *_: (i, 0))
    paired = recv is not None
    parts = own.shape[0] // recv.shape[0] if paired else 1
    span = steps // parts
    arrived = pl.BlockSpec(
        (rows_n, cols_n), lambda i, pos, part: (jnp.clip(i - part[0] * span, 0, span - 1), 0)
    )
    operands = [own] + ([recv] if paired else []) + ([] if target is None else [target])
    specs = [block] + ([block if parts == 1 else arrived] if paired else [])
    specs += [] if target is None else [anywhere]
    return pl.pallas_call(
        functools.partial(scatter_kernel, rows_n, cols_n, steps, paired, parts),
        out_shape=jax.ShapeDtypeStruct((total_rows, BS), bf16),
        grid_spec=pltpu.PrefetchScalarGridSpec(
            num_scalar_prefetch=2,
            grid=(steps,),
            in_specs=specs,
            out_specs=anywhere,
            scratch_shapes=[
                pltpu.VMEM((2, rows_n // BS * (cols_n // BS), BS, BS), bf16),
                pltpu.SemaphoreType.DMA((2,)),
            ],
        ),
        input_output_aliases={} if target is None else {len(operands) + 1: 0},
        compiler_params=params(),
        cost_estimate=cost(own.size, own.size * 6),
    )(pos, part, *operands)


def half_sum_kernel(part, own, arrived, out):
    out[...] = (own[...].astype(f32) + arrived[...].astype(f32)).astype(bf16)


def half_sum(part, own, arrived):
    block = arrived.shape
    return pl.pallas_call(
        half_sum_kernel,
        out_shape=jax.ShapeDtypeStruct(block, bf16),
        grid_spec=pltpu.PrefetchScalarGridSpec(
            num_scalar_prefetch=1,
            grid=(1,),
            in_specs=[pl.BlockSpec(block, lambda i, part: (part[0], 0)), fixed(block)],
            out_specs=fixed(block),
        ),
        compiler_params=params(),
        cost_estimate=cost(arrived.size, arrived.size * 6),
    )(part, own, arrived)


def half_copy_kernel(part, own, out):
    out[...] = own[...]


def other_half(part, own):
    block = (own.shape[0] // 2, own.shape[1])
    return pl.pallas_call(
        half_copy_kernel,
        out_shape=jax.ShapeDtypeStruct(block, bf16),
        grid_spec=pltpu.PrefetchScalarGridSpec(
            num_scalar_prefetch=1,
            grid=(1,),
            in_specs=[pl.BlockSpec(block, lambda i, part: (1 - part[0], 0))],
            out_specs=fixed(block),
        ),
        compiler_params=params(),
        cost_estimate=cost(0, own.size * 2),
    )(part, own)


def scatter_vec_kernel(paired, pos, own, *refs):
    if paired:
        recv, *refs = refs
    target, buf, sem = refs[-3:]
    value = own[...]
    if paired:
        value = (value.astype(f32) + recv[...].astype(f32)).astype(bf16)
    buf[...] = value

    def body(n, carried):
        pltpu.make_async_copy(
            buf.at[n], target.at[pl.ds(pl.multiple_of(pos[n], 16), VEC_ROWS), :], sem
        ).start()
        return carried

    lax.fori_loop(0, own.shape[0], body, 0)
    pltpu.make_async_copy(buf, buf, sem).wait()


def scatter_vec(pos, own, recv, target):
    anywhere = pl.BlockSpec(memory_space=pl.ANY)
    block = fixed(own.shape)
    paired = recv is not None
    operands = [own] + ([recv] if paired else []) + [target]
    return pl.pallas_call(
        functools.partial(scatter_vec_kernel, paired),
        out_shape=jax.ShapeDtypeStruct(target.shape, bf16),
        grid_spec=pltpu.PrefetchScalarGridSpec(
            num_scalar_prefetch=1,
            grid=(1,),
            in_specs=[block] * (len(operands) - 1) + [anywhere],
            out_specs=anywhere,
            scratch_shapes=[pltpu.VMEM(own.shape, bf16), pltpu.SemaphoreType.DMA],
        ),
        input_output_aliases={len(operands): 0},
        compiler_params=params(),
    )(pos, *operands)


def expand_kernel(present, half, patch_ref, class_ref, pinv_ref, out, total):
    for block in range(patch_ref.shape[0] // ROWS):
        rows = slice(block * ROWS, (block + 1) * ROWS)
        total[...] = jnp.zeros_like(total)
        for which in range(3):

            @pl.when(present[block, which] > 0)
            def _(which=which, rows=rows):
                chosen = jnp.where(class_ref[rows, :] == which, patch_ref[rows, :].astype(f32), 0.0)
                total[...] += dot_nt(chosen.astype(bf16), pinv_ref[which])

        out[rows, :] = total[...].astype(bf16)


def expand_call(which, present, half, patches, class_col, pinv):
    tokens = patches.shape[0]
    size = BASE_PIX // CHUNKS
    step = size
    return pl.pallas_call(
        expand_kernel,
        out_shape=jax.ShapeDtypeStruct((tokens, size), bf16),
        grid_spec=pltpu.PrefetchScalarGridSpec(
            num_scalar_prefetch=2,
            grid=(1,),
            in_specs=[
                fixed(patches.shape),
                fixed(class_col.shape),
                pl.BlockSpec(
                    (3, step, pinv.shape[2]),
                    lambda i, present, half: (0, (which + half[0] * (CHUNKS // 2)) % CHUNKS, 0),
                ),
            ],
            out_specs=pl.BlockSpec((tokens, step), lambda i, *_: (0, i)),
            scratch_shapes=[pltpu.VMEM((ROWS, step), f32)],
        ),
        compiler_params=params(),
        cost_estimate=cost(3 * tokens * size * D, tokens * size * 4 + size * D * 6),
    )(present, half, patches, class_col, pinv)


def resize_kernel(base, pinv_ref, out, turned):
    @pl.when(pl.program_id(0) == 0)
    def _():
        turned[...] = base[...].T

    out[0] = dot(turned[...], pinv_ref[0]).astype(bf16)


def resize_call(panels, pinv):
    return pl.pallas_call(
        resize_kernel,
        out_shape=jax.ShapeDtypeStruct((3, HALF, pinv.shape[2]), bf16),
        grid=(3,),
        in_specs=[
            fixed((BASE_PIX, HALF), PANELS["base"] // BASE_PIX),
            pl.BlockSpec((1, BASE_PIX, pinv.shape[2]), lambda i: (i, 0, 0)),
        ],
        out_specs=pl.BlockSpec((1, HALF, pinv.shape[2]), lambda i: (i, 0, 0)),
        scratch_shapes=[pltpu.VMEM((HALF, BASE_PIX), bf16)],
        compiler_params=params(),
        cost_estimate=cost(6 * D * BASE_PIX * HALF, 6 * D * BASE_PIX),
    )(panels, pinv)


def embed_back_kernel(core, base, own, recv, out, bias):
    low = (base[...] + (own[...].astype(f32) + recv[...].astype(f32))).astype(bf16)
    out[...] = low
    accumulate(bias, jnp.sum(low.astype(f32), axis=0, keepdims=True))


def embed_back_call(core, base, own, recv):
    tokens = base.shape[0]
    half = pl.BlockSpec((ROWS, HALF), lambda i, core: (i, core[0]))
    return pl.pallas_call(
        embed_back_kernel,
        out_shape=[
            jax.ShapeDtypeStruct((tokens, HALF), bf16),
            jax.ShapeDtypeStruct((1, HALF), f32),
        ],
        grid_spec=pltpu.PrefetchScalarGridSpec(
            num_scalar_prefetch=1,
            grid=(tokens // ROWS,),
            in_specs=[half] * 3,
            out_specs=[rows_spec(HALF), fixed((1, HALF))],
        ),
        compiler_params=params(),
        cost_estimate=cost(tokens * D, tokens * D * 5),
    )(core, base, own, recv)


def pack_kernel(vec_per, *refs):
    *pieces, out = refs
    out[...] = jnp.zeros_like(out)
    at = 0
    for piece in pieces:
        for k in range(piece.shape[1] // BS):
            owner, row = divmod(at, vec_per // BS)
            out[owner, row : row + 1, :] = piece[:, k * BS : (k + 1) * BS]
            at += 1


def pack_call(pieces, owners, vec_per):
    if vec_per % BS:
        joined = jnp.concatenate(pieces, axis=1)[0]
        joined = jnp.pad(joined, (0, owners * vec_per - joined.shape[0])).reshape(owners, vec_per)
        joined = jnp.pad(joined, ((0, 0), (0, VEC_ROWS * BS - vec_per)))
        return joined.astype(bf16).reshape(owners, VEC_ROWS, BS)
    return pl.pallas_call(
        functools.partial(pack_kernel, vec_per),
        out_shape=jax.ShapeDtypeStruct((owners, VEC_ROWS, BS), f32),
        grid=(1,),
        in_specs=[fixed(p.shape) for p in pieces],
        out_specs=fixed((owners, VEC_ROWS, BS)),
        compiler_params=params(),
        cost_estimate=cost(0, owners * vec_per * 8),
    )(*pieces).astype(bf16)


def embed_kernel(half, *refs):
    *parts, vec, weight, out = refs
    size = BASE_PIX // CHUNKS
    total = vec[:, :HALF]
    for c in range(CHUNKS):
        at = lax.rem(c + half[0] * (CHUNKS // 2), CHUNKS)
        rows = pl.ds(pl.multiple_of(at * size, size), size)
        total = total + dot(parts[c][...], weight[rows, :])
    out[...] = total.astype(bf16)


def embed_call(half, chunks, vec, panels):
    tokens = chunks[0].shape[0]
    return pl.pallas_call(
        embed_kernel,
        out_shape=jax.ShapeDtypeStruct((tokens, HALF), bf16),
        grid_spec=pltpu.PrefetchScalarGridSpec(
            num_scalar_prefetch=1,
            grid=(tokens // ROWS,),
            in_specs=[rows_spec(BASE_PIX // CHUNKS)] * CHUNKS
            + [fixed(vec.shape), fixed((BASE_PIX, HALF), PANELS["base"] // BASE_PIX)],
            out_specs=rows_spec(HALF),
        ),
        compiler_params=params(),
        cost_estimate=cost(2 * tokens * BASE_PIX * HALF, tokens * BASE_PIX * 3),
    )(half, *chunks, vec, panels)


def qkv_kernel(layer, first, core, *refs):
    if first:
        own, recv, vec, weight, hid, normed, q_ref, k_ref, v_ref = refs
        mine, theirs = own[...].astype(f32), recv[...].astype(f32)
        low = core[0] == 0
        values = jnp.concatenate(
            [jnp.where(low, mine, theirs), jnp.where(low, theirs, mine)], axis=1
        )
    else:
        base, own, recv, vec, weight, hid, normed, q_ref, k_ref, v_ref = refs
        values = base[...] + (own[...].astype(f32) + recv[...].astype(f32))
    hid[...] = values
    unit, unused = norm_stats(values)
    low = (unit * vec_piece(vec, layer, "g1") + vec_piece(vec, layer, "s1")).astype(bf16)
    normed[...] = low
    made = dot(low, joined(weight, 0, D, 3))
    q_ref[...] = (made[:, :HALF] + vec_piece(vec, layer, "bq")).astype(bf16)
    k_ref[...] = made[:, HALF : 2 * HALF].astype(bf16)
    v_ref[...] = (made[:, 2 * HALF :] + vec_piece(vec, layer, "bv")).astype(bf16)


def qkv_call(layer, base, own, recv, core, vec, panels):
    tokens = own.shape[0]
    shape = lambda width, kind: jax.ShapeDtypeStruct((tokens, width), kind)
    outs = [shape(D, f32), shape(D, bf16)] + [shape(HALF, bf16)] * 3
    operands = ([] if base is None else [base]) + [own, recv]
    return pl.pallas_call(
        functools.partial(qkv_kernel, layer, base is None),
        out_shape=outs,
        grid_spec=pltpu.PrefetchScalarGridSpec(
            num_scalar_prefetch=1,
            grid=(tokens // ROWS,),
            in_specs=[rows_spec(o.shape[1]) for o in operands]
            + [fixed(vec.shape), fixed((3 * D, HALF), PANELS["qkv"][layer] // (3 * D))],
            out_specs=[rows_spec(o.shape[1]) for o in outs],
        ),
        compiler_params=params(),
        cost_estimate=cost(2 * tokens * D * 3 * HALF, tokens * D * 14),
    )(core, *operands, vec, panels)


def head_masks():
    lane = lax.broadcasted_iota(jnp.int32, (1, 2 * HEAD_DIM), 1)
    low = (lane < HEAD_DIM).astype(f32).astype(bf16)
    high = (lane >= HEAD_DIM).astype(f32).astype(bf16)
    return low, high


def attend_kernel(
    layer, low_ref, high_ref, q_ref, k_ref, v_ref, seg_q, seg_k, vec, w_out, o_ref, lse_ref, part,
    scores_ref, top_ref, acc_ref,
):
    step = pl.program_id(0)
    first, last = low_ref[step], high_ref[step]
    masks = head_masks()
    scale = jnp.asarray(HEAD_DIM ** (-0.5), bf16)
    lane = lax.broadcasted_iota(jnp.int32, (1, BS), 1)
    sums = [(lane == HEAD_DIM).astype(f32).astype(bf16), (lane == 0).astype(f32).astype(bf16)]
    top_ref[...] = jnp.full(top_ref.shape, masked_score, f32)
    acc_ref[...] = jnp.zeros_like(acc_ref)
    seg_col = seg_q[...]

    def score_block(block, carried):
        rows = pl.ds(pl.multiple_of(block * ROWS, ROWS), ROWS)
        same = seg_col == seg_k[:, rows]
        for pair in range(HEADS // 2):
            cols = slice(pair * BS, (pair + 1) * BS)
            q_two = q_ref[:, cols] * scale
            k_two = k_ref[rows, cols]
            for side in range(2):
                head = 2 * pair + side
                scores = jnp.where(same, dot_nt(q_two * masks[side], k_two), masked_score)
                scores_ref[head, block] = scores
                top = top_ref[head]
                for piece in range(ROWS // BS):
                    top = jnp.maximum(top, scores[:, piece * BS : (piece + 1) * BS])
                top_ref[head] = top
        return carried

    lax.fori_loop(first, last, score_block, 0)
    tops = [jnp.max(top_ref[head], axis=1, keepdims=True) for head in range(HEADS)]

    def mix_block(block, carried):
        rows = pl.ds(pl.multiple_of(block * ROWS, ROWS), ROWS)
        for pair in range(HEADS // 2):
            v_two = v_ref[rows, pair * BS : (pair + 1) * BS]
            for side in range(2):
                head = 2 * pair + side
                expo = jnp.exp(scores_ref[head, block] - tops[head]).astype(bf16)
                acc_ref[head] += dot(expo, v_two * masks[side] + sums[side])
        return carried

    lax.fori_loop(first, last, mix_block, 0)
    totals = jnp.zeros((ROWS, BS), f32)
    for pair in range(HEADS // 2):
        sides = []
        for side in range(2):
            head = 2 * pair + side
            mixed = acc_ref[head]
            at = HEAD_DIM * (1 - side)
            total = mixed[:, at : at + 1]
            totals = jnp.where(lane == head, tops[head] + jnp.log(total), totals)
            sides.append(mixed * (1.0 / total))
        o_ref[:, pair * BS : (pair + 1) * BS] = jnp.where(lane < HEAD_DIM, *sides).astype(bf16)
    lse_ref[...] = totals.T[0:8, :]
    low = o_ref[...]
    bias = vec_piece(vec, layer, "bo")
    part[...] = (dot(low, joined(w_out, 0, HALF, TENSOR)) + bias).astype(bf16)


def attend_call(layer, first, last, queries, keys, values, seg_col, seg_row, vec, panels):
    tokens = queries.shape[0]
    return pl.pallas_call(
        functools.partial(attend_kernel, layer),
        out_shape=[
            jax.ShapeDtypeStruct((tokens, HALF), bf16),
            jax.ShapeDtypeStruct((8, tokens), f32),
            jax.ShapeDtypeStruct((tokens, D), bf16),
        ],
        grid_spec=pltpu.PrefetchScalarGridSpec(
            num_scalar_prefetch=2,
            grid=(tokens // ROWS,),
            in_specs=[
                rows_spec(HALF),
                fixed(keys.shape),
                fixed(values.shape),
                rows_spec(1),
                fixed(seg_row.shape),
                fixed(vec.shape),
                fixed((D, HALF), PANELS["out"][layer] // D),
            ],
            out_specs=[
                rows_spec(HALF),
                pl.BlockSpec((8, ROWS), lambda i, *_: (0, i)),
                rows_spec(D),
            ],
            scratch_shapes=[
                pltpu.VMEM((HEADS, tokens // ROWS, ROWS, ROWS), f32),
                pltpu.VMEM((HEADS, ROWS, BS), f32),
                pltpu.VMEM((HEADS, ROWS, BS), f32),
            ],
        ),
        compiler_params=params(),
        cost_estimate=cost(8 * HEADS * tokens * tokens * BS, tokens * D * 8, HEADS * tokens * tokens),
    )(first, last, queries, keys, values, seg_col, seg_row, vec, panels)


def gelu_parts(values):
    cdf = 0.5 * (1.0 + lax.erf(values * 0.7071067811865476))
    pdf = 0.3989422804014327 * jnp.exp(-0.5 * values * values)
    return values * cdf, cdf + values * pdf


def mlp_kernel(layer, base, own, recv, vec, w_up, w_down, hid, normed, act, slope, part):
    values = base[...] + (own[...].astype(f32) + recv[...].astype(f32))
    hid[...] = values
    unit, unused = norm_stats(values)
    low = (unit * vec_piece(vec, layer, "g2") + vec_piece(vec, layer, "s2")).astype(bf16)
    normed[...] = low
    bias_up = vec_piece(vec, layer, "b1")
    for pair in range(HALF_FF // D):
        area = slice(pair * D, (pair + 1) * D)
        up = dot(low, joined(w_up, pair * 2 * D, D, 2)) + bias_up[:, area]
        gelu, grad = gelu_parts(up)
        act[:, area] = gelu.astype(bf16)
        slope[:, area] = grad.astype(bf16)
    bias_down = vec_piece(vec, layer, "b2")
    part[...] = (dot(act[...], joined(w_down, 0, HALF_FF, TENSOR)) + bias_down).astype(bf16)


def mlp_call(layer, base, own, recv, vec, panels):
    tokens = base.shape[0]
    shape = lambda width, kind: jax.ShapeDtypeStruct((tokens, width), kind)
    outs = [shape(D, f32), shape(D, bf16), shape(HALF_FF, bf16), shape(HALF_FF, bf16), shape(D, bf16)]
    return pl.pallas_call(
        functools.partial(mlp_kernel, layer),
        out_shape=outs,
        grid=(tokens // ROWS,),
        in_specs=[rows_spec(D)] * 3
        + [
            fixed(vec.shape),
            fixed((2 * HALF_FF, HALF), PANELS["up"][layer] // (2 * HALF_FF)),
            fixed((2 * HALF_FF, HALF), PANELS["down"][layer] // (2 * HALF_FF)),
        ],
        out_specs=[rows_spec(o.shape[1]) for o in outs],
        compiler_params=params(),
        cost_estimate=cost(4 * tokens * D * HALF_FF, tokens * D * 24, 2 * tokens * HALF_FF),
    )(base, own, recv, vec, panels, panels)


def mlp_back_kernel(layer, summed, *refs):
    if summed:
        base, own, recv, *refs = refs
        (hid, slope, vec, w_up, w_down, grad_full, grad_low, du_ref, back, dgain, dshift, db1, db2) = refs
        values = base[...].astype(f32) + (own[...].astype(f32) + recv[...].astype(f32))
        grad_full[...] = values
        low = values.astype(bf16)
    else:
        base, valid, *refs = refs
        (hid, slope, vec, w_up, w_down, grad_low, du_ref, back, dgain, dshift, db1, db2) = refs
        low = (base[...].astype(f32) * valid[...]).astype(bf16)
    grad_low[...] = low
    accumulate(db2, jnp.sum(low.astype(f32), axis=0, keepdims=True))
    for part in range(HALF_FF // D):
        area = slice(part * D, (part + 1) * D)
        rows = jnp.concatenate(
            [w_down[p * HALF_FF + part * D : p * HALF_FF + (part + 1) * D, :] for p in range(TENSOR)],
            axis=1,
        )
        du_ref[:, area] = (dot_nt(low, rows) * slope[:, area].astype(f32)).astype(bf16)
    grad_normed = dot_nt(du_ref[...], joined(w_up, 0, D, HALF_FF // HALF))
    accumulate(db1, jnp.sum(du_ref[...].astype(f32), axis=0, keepdims=True))
    part_back, gain_grad, shift_grad = norm_back(hid[...], vec_piece(vec, layer, "g2"), grad_normed)
    back[...] = part_back.astype(bf16)
    accumulate(dgain, gain_grad)
    accumulate(dshift, shift_grad)


def mlp_back_call(layer, base, own, recv, valid, hid, slope, vec, panels):
    tokens = base.shape[0]
    summed = own is not None
    shape = lambda width, kind: jax.ShapeDtypeStruct((tokens, width), kind)
    line = lambda width: jax.ShapeDtypeStruct((1, width), f32)
    outs = ([shape(D, f32)] if summed else []) + [shape(D, bf16), shape(HALF_FF, bf16), shape(D, bf16)]
    lines = [line(D), line(D), line(HALF_FF), line(D)]
    extra = [own, recv] if summed else [valid]
    return pl.pallas_call(
        functools.partial(mlp_back_kernel, layer, summed),
        out_shape=outs + lines,
        grid=(tokens // ROWS,),
        in_specs=[rows_spec(D)]
        + [rows_spec(e.shape[1]) for e in extra]
        + [
            rows_spec(D),
            rows_spec(HALF_FF),
            fixed(vec.shape),
            fixed((2 * HALF_FF, HALF), PANELS["up"][layer] // (2 * HALF_FF)),
            fixed((2 * HALF_FF, HALF), PANELS["down"][layer] // (2 * HALF_FF)),
        ],
        out_specs=[rows_spec(o.shape[1]) for o in outs] + [fixed(o.shape) for o in lines],
        compiler_params=params(),
        cost_estimate=cost(4 * tokens * D * HALF_FF, tokens * D * 24),
    )(base, *extra, hid, slope, vec, panels, panels)


def attend_back_kernel(
    low_ref, high_ref, base, own, recv, q_ref, k_ref, v_ref, o_ref, lse_ref, seg_k, seg_q, w_out,
    full_ref, grad_low, dq_ref, dk_ref, dv_ref, dbo, dk_acc, dv_acc, dq_acc, do_ref,
):
    step = pl.program_id(0)

    @pl.when(step == 0)
    def _():
        dk_acc[...] = jnp.zeros_like(dk_acc)
        dv_acc[...] = jnp.zeros_like(dv_acc)

    values = base[...].astype(f32) + (own[...].astype(f32) + recv[...].astype(f32))
    full_ref[...] = values
    low = values.astype(bf16)
    grad_low[...] = low
    accumulate(dbo, jnp.sum(low.astype(f32), axis=0, keepdims=True))
    do_ref[...] = dot_nt(low, joined(w_out, 0, HALF, TENSOR)).astype(bf16)
    product = do_ref[...].astype(f32) * o_ref[...].astype(f32)
    head = lax.broadcasted_iota(jnp.int32, (8, HALF), 0)
    lane = lax.broadcasted_iota(jnp.int32, (8, HALF), 1)
    pick = ((lane >= head * HEAD_DIM) & (lane < (head + 1) * HEAD_DIM)).astype(f32)
    high, rest = split(product)
    pick = pick.astype(bf16)
    inner = dot_nt(pick, high) + dot_nt(pick, rest)
    dq_acc[...] = jnp.zeros_like(dq_acc)
    masks = head_masks()
    scale = jnp.asarray(HEAD_DIM ** (-0.5), bf16)
    seg_row = seg_q[...]

    def one_block(block, carried):
        rows = pl.ds(pl.multiple_of(block * KEYS, KEYS), KEYS)
        same = seg_k[rows, :] == seg_row
        for pair in range(HEADS // 2):
            cols = slice(pair * BS, (pair + 1) * BS)
            q_two = q_ref[:, cols] * scale
            do_two = do_ref[:, cols]
            k_two = k_ref[rows, cols]
            v_two = v_ref[rows, cols]
            dv_two = dk_two = dq_two = None
            for side in range(2):
                at = 2 * pair + side
                q_one = q_two * masks[side]
                do_one = do_two * masks[side]
                scores = dot_nt(k_two, q_one)
                prob = jnp.where(same, jnp.exp(scores - lse_ref[at : at + 1, :]), 0.0)
                grad_prob = dot_nt(v_two, do_one)
                grad_scores = (prob * (grad_prob - inner[at : at + 1, :])).astype(bf16)
                dv_one = dot(prob.astype(bf16), do_one)
                dk_one = dot(grad_scores, q_one)
                dq_one = dot_tn(grad_scores, k_two * masks[side])
                dq_two = dq_one if dq_two is None else dq_two + dq_one
                dv_two = dv_one if dv_two is None else dv_two + dv_one
                dk_two = dk_one if dk_two is None else dk_two + dk_one
            dv_acc[rows, cols] += dv_two
            dk_acc[rows, cols] += dk_two
            dq_acc[:, cols] += dq_two
        return carried

    lax.fori_loop(low_ref[step], high_ref[step], one_block, 0)
    dq_ref[...] = (dq_acc[...] * HEAD_DIM ** (-0.5)).astype(bf16)

    @pl.when(step == pl.num_programs(0) - 1)
    def _():
        dk_ref[...] = dk_acc[...].astype(bf16)
        dv_ref[...] = dv_acc[...].astype(bf16)


def attend_back_call(
    layer, first, last, base, own, recv, queries, keys, values, mixed, lse, seg_col, seg_row, panels
):
    tokens = base.shape[0]
    shape = lambda width, kind: jax.ShapeDtypeStruct((tokens, width), kind)
    whole = (tokens, HALF)
    return pl.pallas_call(
        attend_back_kernel,
        out_shape=[
            shape(D, f32),
            shape(D, bf16),
            shape(HALF, bf16),
            shape(HALF, bf16),
            shape(HALF, bf16),
            jax.ShapeDtypeStruct((1, D), f32),
        ],
        grid_spec=pltpu.PrefetchScalarGridSpec(
            num_scalar_prefetch=2,
            grid=(tokens // ROWS,),
            in_specs=[
                rows_spec(D),
                rows_spec(D),
                rows_spec(D),
                rows_spec(HALF),
                fixed(whole),
                fixed(whole),
                rows_spec(HALF),
                pl.BlockSpec((8, ROWS), lambda i, *_: (0, i)),
                fixed(seg_col.shape),
                pl.BlockSpec((1, ROWS), lambda i, *_: (0, i)),
                fixed((D, HALF), PANELS["out"][layer] // D),
            ],
            out_specs=[
                rows_spec(D),
                rows_spec(D),
                rows_spec(HALF),
                fixed(whole),
                fixed(whole),
                fixed((1, D)),
            ],
            scratch_shapes=[
                pltpu.VMEM(whole, f32),
                pltpu.VMEM(whole, f32),
                pltpu.VMEM((ROWS, HALF), f32),
                pltpu.VMEM((ROWS, HALF), bf16),
            ],
        ),
        compiler_params=params(),
        cost_estimate=cost(14 * HEADS * tokens * tokens * BS, tokens * D * 20, HEADS * tokens * tokens),
    )(first, last, base, own, recv, queries, keys, values, mixed, lse, seg_col, seg_row, panels)


def qkv_back_kernel(layer, dq, dk, dv, hid, vec, weight, back, dgain, dshift, dbq, dbv):
    grad_three = jnp.concatenate([dq[...], dk[...], dv[...]], axis=1)
    grad_normed = dot_nt(grad_three, joined(weight, 0, D, 3))
    part_back, gain_grad, shift_grad = norm_back(hid[...], vec_piece(vec, layer, "g1"), grad_normed)
    back[...] = part_back.astype(bf16)
    accumulate(dgain, gain_grad)
    accumulate(dshift, shift_grad)
    accumulate(dbq, jnp.sum(dq[...].astype(f32), axis=0, keepdims=True))
    accumulate(dbv, jnp.sum(dv[...].astype(f32), axis=0, keepdims=True))


def qkv_back_call(layer, dq, dk, dv, hid, vec, panels):
    tokens = dq.shape[0]
    line = lambda width: jax.ShapeDtypeStruct((1, width), f32)
    lines = [line(D), line(D), line(HALF), line(HALF)]
    return pl.pallas_call(
        functools.partial(qkv_back_kernel, layer),
        out_shape=[jax.ShapeDtypeStruct((tokens, D), bf16)] + lines,
        grid=(tokens // ROWS,),
        in_specs=[rows_spec(HALF)] * 3
        + [
            rows_spec(D),
            fixed(vec.shape),
            fixed((3 * D, HALF), PANELS["qkv"][layer] // (3 * D)),
        ],
        out_specs=[rows_spec(D)] + [fixed(o.shape) for o in lines],
        compiler_params=params(),
        cost_estimate=cost(2 * tokens * D * 3 * HALF, tokens * D * 10),
    )(dq, dk, dv, hid, vec, panels)


def split(values):
    high = values.astype(bf16)
    return high, (values - high.astype(f32)).astype(bf16)


def product(left, right, left_dim, right_dim):
    def one(a, b):
        return lax.dot_general(
            a, b, (((left_dim,), (right_dim,)), ((), ())), preferred_element_type=f32
        )

    return one(left[0], right[0]) + (one(left[0], right[1]) + one(left[1], right[0]))


def owner_kernel(per, used, home, near, far, master, left, right, moment, variance, grad, out, out_mom, out_var):
    here = range(per)
    first = pl.program_id(0) * per
    lefts = [split(left[i]) for i in here]
    rights = [split(right[i]) for i in here]
    rotated = []
    for i in here:
        rows = slice(i * BS, (i + 1) * BS)
        tile = jnp.where(home[0] > 0, near[rows, :].astype(f32), far[rows, :].astype(f32))
        tile = jnp.where(used[first + i] > 0, tile, 0.0)
        grad[i] = tile
        tile = tile.astype(bf16)
        rotated.append(split(dot_tn(lefts[i][0], tile) + dot_tn(lefts[i][1], tile)))
    rotated = [product(rotated[i], rights[i], 1, 0) for i in here]
    steps = []
    for i in here:
        new_moment = decay * moment[i] + (1.0 - decay) * rotated[i]
        new_variance = decay * variance[i] + (1.0 - decay) * rotated[i] * rotated[i]
        out_mom[i] = new_moment
        out_var[i] = new_variance
        steps.append(split(new_moment / (jnp.sqrt(new_variance) + adam_eps)))
    returned = [split(product(lefts[i], steps[i], 1, 0)) for i in here]
    returned = [product(returned[i], rights[i], 1, 1) for i in here]
    for i in here:
        out[i] = master[i] - matrix_rate * returned[i]


def owner_call(used, home, near, far, *arrays):
    count = arrays[0].shape[0]
    per = min(8, count)
    block = pl.BlockSpec((per, BS, BS), lambda i, *_: (i, 0, 0))
    return pl.pallas_call(
        functools.partial(owner_kernel, per),
        out_shape=[jax.ShapeDtypeStruct(arrays[0].shape, f32)] * 4,
        grid_spec=pltpu.PrefetchScalarGridSpec(
            num_scalar_prefetch=2,
            grid=(count // per,),
            in_specs=[pl.BlockSpec((per * BS, BS), lambda i, *_: (i, 0))] * 2 + [block] * 5,
            out_specs=[block] * 4,
        ),
        compiler_params=params(),
        cost_estimate=cost(count * 88 * BS**3, count * BS * BS * 38),
    )(used, home, near, far, *arrays)


def reduce_kernel(carrying, last, *refs):
    block, arrived, *refs = refs
    total = block[...].astype(f32) + arrived[...].astype(f32)
    if carrying:
        carried, *refs = refs
        total = total + carried[...].astype(f32)
    if last:
        [out] = refs
    else:
        following, out, later = refs
        later[...] = following[...]
    out[...] = total.astype(bf16)


def reduce_call(j, n, buffer, arrived, carried, payload):
    last = j == 3
    at = lambda j, x_rel: pl.BlockSpec((payload, BS), lambda i: ((j * 2 + x_rel) * 2 + n, 0))
    whole = fixed((payload, BS))
    operands = [buffer, arrived] + ([] if carried is None else [carried])
    specs = [at(j, 0)] + [whole] * (len(operands) - 1)
    if not last:
        operands.append(buffer)
        specs.append(at(j + 1, 1))
    outs = [jax.ShapeDtypeStruct((payload, BS), bf16)] * (1 if last else 2)
    made = pl.pallas_call(
        functools.partial(reduce_kernel, carried is not None, last),
        out_shape=outs,
        grid=(1,),
        in_specs=specs,
        out_specs=[whole] * len(outs),
        compiler_params=params(),
        cost_estimate=cost(payload * BS * 3, payload * BS * 12),
    )(*operands)
    return (made[0], None) if last else made


class Routes:
    def __init__(self, dp_n):
        pairs = [(d, t) for d in range(dp_n) for t in range(TENSOR)]
        at = lambda d, t: d * TENSOR + t
        home = [(d, t) for d, t in pairs if d % 2 == t]
        away = [(d, t) for d, t in pairs if d % 2 != t]
        self.core_all = [(at(d, t), at(d ^ 1, t)) for d, t in pairs]
        self.core_out = [(at(d, t), at(d ^ 1, t)) for d, t in home]
        self.core_in = [(at(d, t), at(d ^ 1, t)) for d, t in away]
        self.y_all = [(at(d, t), at(d, 1 - t)) for d, t in pairs]
        self.y_out = [(at(d, t), at(d, 1 - t)) for d, t in home]
        self.y_in = [(at(d, t), at(d, 1 - t)) for d, t in away]
        self.x_home = [(at(d, t), at(d ^ 2, t)) for d, t in home]
        self.x_away = [(at(d, t), at(d ^ 2, t)) for d, t in away]
        self.z_home = [(at(d, t), at((d + 4) % dp_n, t)) for d, t in home]


def send(value, route):
    return lax.ppermute(value, AXES, route)


def shards(
    patches,
    cotangent,
    image_size,
    block_slot,
    pinv,
    master_slots,
    left_basis,
    right_basis,
    mom_slots,
    var_slots,
    vec_master,
    vec_mom,
    vec_var,
):
    dp_n = lax.axis_size("dp")
    dp_pos = lax.axis_index("dp")
    y_pos = lax.axis_index("tensor")
    core = dp_pos % 2
    home = core == y_pos
    routes = Routes(dp_n)
    grid3 = dp_n == 16
    x_pos = (dp_pos // 2) % 2
    half_at = (x_pos if grid3 else x_pos * 0).astype(jnp.int32).reshape(1)
    tokens_n = patches.shape[0]
    slots_per = master_slots.shape[1]
    vec_per = vec_master.shape[1]
    slots_n = slots_per * dp_n
    payload = slots_per * BS + VEC_ROWS

    patches = jnp.where(home, patches, send(patches, routes.core_out))
    cotangent = jnp.where(home, cotangent, send(cotangent, routes.core_out))
    size_row = jnp.where(home, image_size, send(image_size, routes.core_out))[0]
    own_slots = block_slot[0]
    slot_other = send(block_slot, routes.y_all)

    lengths = jnp.where(
        size_row == 0, LEN_A, jnp.where(size_row == 1, LEN_B, jnp.where(size_row == 2, LEN_C, 0))
    )
    order = jnp.arange(IMG_DEV)
    ends_at = jnp.sum(jnp.where(order[None, :] <= order[:, None], lengths[None, :], 0), axis=1)
    places = jnp.arange(tokens_n)
    segment = jnp.sum((places[:, None] >= ends_at[None, :]).astype(jnp.int32), axis=1)
    in_image = segment[:, None] == order[None, :]
    select = jnp.stack(
        [jnp.any(in_image & (size_row == s)[None, :], axis=1) for s in range(3)], axis=1
    )
    valid_col = (segment < IMG_DEV).astype(f32)[:, None]
    seg_col = segment[:, None]
    seg_row = segment[None, :]
    blocks_n = tokens_n // ROWS
    starts = jnp.arange(blocks_n) * ROWS
    begun = ends_at[None, :] <= starts[:, None]
    first_tok = jnp.max(jnp.where(begun, ends_at[None, :], 0), axis=1)
    after = ends_at[None, :] > (starts + ROWS - 1)[:, None]
    last_tok = jnp.min(jnp.where(after, ends_at[None, :], tokens_n), axis=1)
    first_blk = (first_tok // ROWS).astype(jnp.int32)
    last_blk = ((last_tok + ROWS - 1) // ROWS).astype(jnp.int32)
    first_key = (first_tok // KEYS).astype(jnp.int32)
    last_key = ((last_tok + KEYS - 1) // KEYS).astype(jnp.int32)

    select_low = select.astype(bf16)
    class_col = jnp.sum(jnp.where(select, jnp.arange(1, 4)[None, :], 0), axis=1, keepdims=True) - 1
    present = jnp.any(select.reshape(blocks_n, ROWS, 3), axis=1).astype(jnp.int32)

    def expand(which):
        return expand_call(which, present, half_at, patches, class_col, pinv)

    vec_low = jnp.pad(vec_master[0].astype(bf16), (0, VEC_ROWS * BS - vec_per))
    own_pack = jnp.concatenate(
        [
            master_slots[0].astype(bf16).reshape(slots_per * BS, BS),
            vec_low.reshape(VEC_ROWS, BS),
        ],
        axis=0,
    )
    flag = home.astype(jnp.int32).reshape(1)
    if grid3:
        z_pos = dp_pos // 4
        packs = [[own_pack], [send(own_pack, routes.core_in)]]
        across, over_y, corner = [[], []], [[], []], [[], []]
        token = jnp.zeros((8, BS), f32)
        chunks = []
        for j in range(5):
            for n in range(2):
                moved = []
                if j < 4:
                    moved += [send(packs[n][j], routes.x_home), send(packs[n][j], routes.y_out)]
                if j:
                    source, route = (across, routes.y_out) if n == 0 else (over_y, routes.x_away)
                    moved.append(send(source[n][j - 1], route))
                if j < 3:
                    moved.append(send(packs[n][j], routes.z_home))
                work = []
                if j + n == 0:
                    work = [slot_other]
                if 1 <= 2 * j + n <= CHUNKS:
                    work = [expand(2 * j + n - 1)]
                if j < 4:
                    token, *moved = fence(token, *moved, *work)
                    if j + n == 0:
                        slot_other = moved.pop()
                    elif work:
                        chunks.append(moved.pop())
                if j < 3:
                    packs[n].append(moved.pop())
                if j:
                    corner[n].append(moved.pop())
                if j < 4:
                    across[n].append(moved[0])
                    over_y[n].append(moved[1])
        first, second, owner = [], [], []
        for j in range(4):
            first += [packs[0][j], packs[1][j], across[0][j], across[1][j]]
            second += [over_y[0][j], over_y[1][j], corner[0][j], corner[1][j]]
            for x_rel in range(2):
                for n in range(2):
                    owner.append(((z_pos - j) % 4) * 4 + (x_pos ^ x_rel) * 2 + (core ^ n))
        first = [v[None] for v in first]
        second = [v[None] for v in second]
        owner = jnp.stack(owner).astype(jnp.int32)
    else:
        everything = lax.all_gather(own_pack, AXES, axis=0)
        everything = everything.reshape(dp_n, TENSOR, payload, BS)
        first = [jnp.where(core == 0, everything[:, 0], everything[:, 1])]
        second = []
        owner = jnp.arange(dp_n, dtype=jnp.int32)
        chunks = [expand(c) for c in range(CHUNKS)]
    slot_list = jnp.where(home, block_slot, slot_other)[0]
    named = slot_list[None, :] == jnp.arange(slots_n)[:, None]
    used = jnp.any(named, axis=1)
    drow = jnp.where(used, jnp.sum(jnp.where(named, TARGET_ROW[None, :], 0), axis=1), -1)
    dcol = jnp.sum(jnp.where(named, TARGET_COL[None, :], 0), axis=1)
    panels, vec_rows = gather_tiles(first, second, owner, drow, dcol, flag, slots_per, dp_n)
    vec = vec_rows.reshape(dp_n, VEC_ROWS * BS)[:, :vec_per].astype(f32).reshape(1, dp_n * vec_per)

    embedded = embed_call(half_at, chunks, vec, panels)
    embedded_other = send(embedded, routes.core_all)
    core_flag = core.astype(jnp.int32).reshape(1)

    caches = []
    hidden, own, recv = None, embedded, embedded_other
    for layer in range(LAYERS):
        hidden, normed, queries, keys, values = qkv_call(
            layer, hidden, own, recv, core_flag, vec, panels
        )
        mixed, lse, part = attend_call(
            layer, first_blk, last_blk, queries, keys, values, seg_col, seg_row, vec, panels
        )
        other = send(part, routes.core_all)
        middle, normed2, act, slope, own = mlp_call(layer, hidden, part, other, vec, panels)
        recv = send(own, routes.core_all)
        caches.append((hidden, normed, queries, keys, values, mixed, lse, middle, normed2, act, slope))
        hidden = middle
    out_low = ((hidden + (own.astype(f32) + recv.astype(f32))) * valid_col).astype(bf16)

    owners = jnp.arange(dp_n)
    if grid3:
        place = (
            ((z_pos - 1 - owners // 4) % 4) * 4
            + (x_pos ^ ((owners // 2) % 2)) * 2
            + (core ^ (owners % 2))
        ).astype(jnp.int32)
    else:
        place = owners.astype(jnp.int32)
    slot_owner = slot_list // slots_per
    owner_place = jnp.sum(
        jnp.where(slot_owner[:, None] == owners[None, :], place[None, :], 0), axis=1
    )
    tile_pos = (owner_place * payload + (slot_list % slots_per) * BS).astype(jnp.int32)
    vec_pos = (place * payload + slots_per * BS).astype(jnp.int32)
    total_rows = dp_n * payload
    where_to = jnp.concatenate([half_at, flag if grid3 else flag * 0 + 1])
    offsets = {"base": 0}
    count = BASE_PIX // BS * (HALF // BS)
    for layer in range(LAYERS):
        for name, size in (("qkv", 3 * D * HALF), ("out", D * HALF), ("up", D * HALF_FF), ("down", D * HALF_FF)):
            offsets[name, layer] = count
            count += size // (BS * BS)

    def place_tiles(key, matrix, arrived, buffer):
        tiles = matrix.size // (BS * BS)
        pos = tile_pos[offsets[key] : offsets[key] + tiles]
        rows_n = matrix.shape[0] // 2 if matrix.shape[0] > HALF else HALF
        return scatter_matrix(pos, matrix, arrived, where_to, buffer, total_rows, rows_n)

    def place_base(rel, matrix, arrived, buffer):
        size = BASE_PIX * HALF // (BS * BS) // 2
        low_pos, high_pos = tile_pos[:size], tile_pos[size : 2 * size]
        pos = jnp.where(half_at[0] == rel, low_pos, high_pos)
        return scatter_matrix(pos, matrix, arrived, where_to, buffer, total_rows, D)

    def over(matrix):
        return send(matrix, routes.y_in) if grid3 else None

    def beside(matrix):
        return send(other_half(half_at, matrix), routes.x_away) if grid3 else None

    def summed(matrix, arrived):
        return half_sum(half_at, matrix, arrived) if grid3 else None

    def hold(*arrays):
        kept = [a for a in arrays if a is not None]
        done = iter(fence(*kept))
        return [None if a is None else next(done) for a in arrays]

    top, low = 1, 0
    vec_grads = [None] * LAYERS

    def mlp_step(layer, grad, own, recv):
        middle, normed2, act, slope = caches[layer][7:11]
        made = mlp_back_call(layer, grad, own, recv, valid_col, middle, slope, vec, panels)
        if own is not None:
            return made
        return [made[0]] + list(made)

    def attend_step(layer, grad, part, other):
        hid_in, normed, queries, keys, values, mixed, lse = caches[layer][:7]
        return attend_back_call(
            layer, first_key, last_key, grad, part, other, queries, keys, values, mixed, lse,
            seg_col, seg_row, panels,
        )

    grad, grad_low, du, part, dg2, ds2, db1, db2 = mlp_step(top, cotangent, None, None)
    other = send(part, routes.core_all)
    gd1 = dot_tn(caches[top][9], grad_low).astype(bf16)
    gu1 = dot_tn(caches[top][8], du).astype(bf16)
    part, other, gd1, gu1, out_low = fence(part, other, gd1, gu1, out_low)
    ad1 = over(gd1)
    grad, grad_low, dq, dk, dv, dbo = attend_step(top, grad, part, other)
    dq, dk, dv, ad1 = hold(dq, dk, dv, ad1)
    au1 = over(gu1)
    own, dg1, ds1, dbq, dbv = qkv_back_call(top, dq, dk, dv, caches[top][0], vec, panels)
    recv = send(own, routes.core_all)
    go1 = dot_tn(caches[top][5], grad_low).astype(bf16)
    gq1 = dot_tn(caches[top][1], jnp.concatenate([dq, dk, dv], axis=1)).astype(bf16)
    vec_grads[top] = [dg1, ds1, dbq, dbv, dbo, dg2, ds2, db1, db2]
    grad, grad_low, du, part, dg2, ds2, db1, db2 = mlp_step(low, grad, own, recv)
    du, part, au1, go1, gq1 = hold(du, part, au1, go1, gq1)
    other = send(part, routes.core_all)
    xq1, ao1 = beside(gq1), over(go1)
    gd0 = dot_tn(caches[low][9], grad_low).astype(bf16)
    gu0 = dot_tn(caches[low][8], du).astype(bf16)
    part, other, gd0, gu0, xq1, ao1 = hold(part, other, gd0, gu0, xq1, ao1)
    aq1 = over(summed(gq1, xq1)) if grid3 else None
    xd0, xu0 = beside(gd0), beside(gu0)
    buffer = place_tiles(("down", top), gd1, ad1, None)
    buffer = place_tiles(("up", top), gu1, au1, buffer)
    grad, grad_low, dq, dk, dv, dbo = attend_step(low, grad, part, other)
    grad, grad_low, dq, dk, dv, aq1, xd0, xu0, buffer = hold(
        grad, grad_low, dq, dk, dv, aq1, xd0, xu0, buffer
    )
    hd0, hu0 = summed(gd0, xd0), summed(gu0, xu0)
    dq, dk, dv, hd0, hu0 = hold(dq, dk, dv, hd0, hu0)
    ad0, au0 = over(hd0), over(hu0)
    own, dg1, ds1, dbq, dbv = qkv_back_call(low, dq, dk, dv, caches[low][0], vec, panels)
    recv = send(own, routes.core_all)
    gq0 = dot_tn(caches[low][1], jnp.concatenate([dq, dk, dv], axis=1)).astype(bf16)
    vec_grads[low] = [dg1, ds1, dbq, dbv, dbo, dg2, ds2, db1, db2]
    own, recv, gq0 = hold(own, recv, gq0)
    xq0 = beside(gq0)
    grad_emb, grad_emb_bias = embed_back_call(core_flag, grad, own, recv)
    middle = CHUNKS // 2

    def base_grad(parts):
        return jnp.concatenate([dot_tn(c, grad_emb).astype(bf16) for c in parts], axis=0)

    gbt = base_grad(chunks[middle:])
    gbt, grad_emb, gq0 = hold(gbt, grad_emb, gq0)
    xb = send(gbt, routes.x_away) if grid3 else None
    gbm = base_grad(chunks[:middle])
    vec_grad = pack_call([grad_emb_bias] + vec_grads[0] + vec_grads[1], dp_n, vec_per)
    go0 = dot_tn(caches[low][5], grad_low).astype(bf16)
    hq0 = summed(gq0, xq0)
    gbm, vec_grad, go0, hq0 = hold(gbm, vec_grad, go0, hq0)
    aq0, ao0, av = over(hq0), over(go0), over(vec_grad)
    gbm, xb = hold(gbm, xb)
    hb = (gbm.astype(f32) + xb.astype(f32)).astype(bf16) if grid3 else None
    hb, gbm, gbt, buffer = hold(hb, gbm, gbt, buffer)
    ab = over(hb)
    buffer = place_tiles(("out", top), go1, ao1, buffer)
    buffer = place_tiles(("qkv", top), gq1, aq1, buffer)
    buffer = place_tiles(("down", low), gd0, ad0, buffer)
    buffer = place_tiles(("up", low), gu0, au0, buffer)
    buffer = place_base(1, gbt, None, buffer)
    buffer = place_tiles(("out", low), go0, ao0, buffer)
    buffer = scatter_vec(vec_pos, vec_grad, av, buffer)
    buffer = place_tiles(("qkv", low), gq0, aq0, buffer)
    ab, buffer, panels, grad_emb, out_low = hold(ab, buffer, panels, grad_emb, out_low)
    buffer = place_base(0, gbm, ab, buffer)

    if grid3:
        token = jnp.zeros((8, BS), f32)
        order = (1, 0)
        resized = resize_call(panels, pinv)
        carried = {n: None for n in order}
        across = {n: send(buffer.reshape(4, 2, 2, payload, BS)[0, 1, n], routes.x_home) for n in order}
        rounded = {}
        for j in range(4):
            for n in order:
                extra = None
                if j == 0 and n == order[0]:
                    extra = resized
                token, across[n], carried[n], extra = hold(token, across[n], carried[n], extra)
                if extra is not None:
                    resized = extra
                total, later = reduce_call(j, n, buffer, across[n], carried[n], payload)
                if j < 3:
                    carried[n] = send(total, routes.z_home)
                    across[n] = send(later, routes.x_home)
                else:
                    rounded[n] = total
        near_grad, far_grad = rounded[0], send(rounded[1], routes.core_out)
    else:
        held = buffer.reshape(dp_n, 1, payload, BS).astype(f32)
        nothing = jnp.zeros_like(held)
        both = jnp.concatenate(
            [jnp.where(core == 0, held, nothing), jnp.where(core == 0, nothing, held)], axis=1
        )
        used_rows = jnp.repeat(used, BS).reshape(dp_n, 1, slots_per * BS, 1)
        used_rows = jnp.concatenate(
            [used_rows, jnp.ones((dp_n, 1, VEC_ROWS, 1), bool)], axis=2
        )
        both = jnp.where(used_rows, both, 0.0).reshape(dp_n * TENSOR * payload, BS)
        near_grad = lax.psum_scatter(both, AXES, scatter_dimension=0, tiled=True).astype(bf16)
        far_grad = near_grad
        resized = resize_call(panels, pinv)

    output = jnp.where(home, out_low, send(out_low, routes.y_out)).astype(f32)
    grad_pixels = sum(
        dot(grad_emb * select_low[:, s : s + 1], resized[s]) for s in range(3)
    ).astype(bf16)
    pixels_other = send(grad_pixels, routes.core_all)
    pixel_sides = [
        grad_pixels[:, s * HALF : (s + 1) * HALF].astype(f32)
        + pixels_other[:, s * HALF : (s + 1) * HALF].astype(f32)
        for s in range(TENSOR)
    ]
    near = jnp.where(core == 0, pixel_sides[0], pixel_sides[1])
    far = jnp.where(core == 0, pixel_sides[1], pixel_sides[0]).astype(bf16)
    patch_grad = jnp.where(home, near, send(far, routes.y_out).astype(f32))

    my_slots = dp_pos * slots_per + jnp.arange(slots_per)
    mine_used = jnp.any(own_slots[None, :] == my_slots[:, None], axis=1).astype(jnp.int32)
    owned_grad, new_master, new_mom, new_var = owner_call(
        mine_used, flag, near_grad, far_grad, master_slots[0], left_basis[0], right_basis[0], mom_slots[0], var_slots[0]
    )
    vec_rows = jnp.where(home, near_grad[slots_per * BS :], far_grad[slots_per * BS :])
    owned_vec_grad = vec_rows.astype(f32).reshape(VEC_ROWS * BS)[:vec_per]
    new_vec_mom = decay * vec_mom[0] + (1.0 - decay) * owned_vec_grad
    new_vec_var = decay * vec_var[0] + (1.0 - decay) * owned_vec_grad * owned_vec_grad
    new_vec = vec_master[0] - vector_rate * new_vec_mom / (jnp.sqrt(new_vec_var) + adam_eps)
    return (
        output,
        patch_grad,
        owned_grad[None],
        new_master[None],
        new_mom[None],
        new_var[None],
        owned_vec_grad[None],
        new_vec[None],
        new_vec_mom[None],
        new_vec_var[None],
    )


def solution(mesh):
    slots = P("tensor", "dp", None, None)
    vectors = P("tensor", "dp")
    tokens = P("dp", None)
    in_specs = (tokens, tokens, tokens, P("tensor", None), P()) + (slots,) * 5 + (vectors,) * 3
    out_specs = (tokens, P("dp", "tensor")) + (slots,) * 4 + (vectors,) * 4
    return jax.shard_map(shards, mesh=mesh, in_specs=in_specs, out_specs=out_specs, check_vma=False)
```

```python
import functools

import jax
import jax.numpy as jnp
import numpy as np
from jax import lax
from jax.experimental import pallas as pl
from jax.experimental.pallas import tpu as pltpu
from jax.sharding import PartitionSpec as P

D = 768
HEAD_DIM = 64
FF = 3072
BASE_PIX = 3072
LAYERS = 2
LEN_A = 196
LEN_B = 225
LEN_C = 576
IMG_DEV = 5
BS = 128
TENSOR = 2
HALF = D // TENSOR
HALF_FF = FF // TENSOR
HEADS = HALF // HEAD_DIM
ROWS = 256
KEYS = 512
VEC_ROWS = 16
CHUNKS = 4

AXES = ("dp", "tensor")
precise = lax.Precision.HIGHEST
masked_score = -1e30
norm_eps = 1e-06
adam_eps = 1e-08
decay = 0.5
matrix_rate = 0.05
vector_rate = 0.3
f32 = jnp.float32
bf16 = jnp.bfloat16
MIB = 1024 * 1024

PANELS = {
    "up": (0, 6144),
    "down": (3072, 9216),
    "base": 12288,
    "out": (15360, 20736),
    "qkv": (16128, 18432),
}
PANEL_ROWS = 21504


def tile_targets():
    rows, cols = [], []

    def add(start, rows_n, cols_n):
        for i in range(rows_n // BS):
            for j in range(cols_n // BS):
                panel, inner = divmod(j * BS, HALF)
                rows.append(start + panel * rows_n + i * BS)
                cols.append(inner)

    add(PANELS["base"], BASE_PIX, HALF)
    for layer in range(LAYERS):
        add(PANELS["qkv"][layer], D, 3 * HALF)
        add(PANELS["out"][layer], HALF, D)
        add(PANELS["up"][layer], D, HALF_FF)
        add(PANELS["down"][layer], HALF_FF, D)
    return np.array(rows, np.int32), np.array(cols, np.int32)


TARGET_ROW, TARGET_COL = tile_targets()
LAYER_VECS = (D, D, HALF, HALF, D, D, D, HALF_FF, D)
VEC_NAMES = ("g1", "s1", "bq", "bv", "bo", "g2", "s2", "b1", "b2")


def vec_offsets():
    offset = HALF
    found = []
    for layer in range(LAYERS):
        here = {}
        for name, length in zip(VEC_NAMES, LAYER_VECS):
            here[name] = (offset, length)
            offset += length
        found.append(here)
    return found


VEC_AT = vec_offsets()


def params(limit=24):
    return pltpu.CompilerParams(
        dimension_semantics=("arbitrary",), vmem_limit_bytes=limit * MIB
    )


def cost(flops, nbytes, trans=0):
    return pl.CostEstimate(flops=flops, bytes_accessed=nbytes, transcendentals=trans)


def rows_spec(width):
    return pl.BlockSpec((ROWS, width), lambda i, *_: (i, 0))


def fixed(shape, at=0):
    return pl.BlockSpec(shape, lambda i, *_: (at,) + (0,) * (len(shape) - 1))


def vec_piece(vec_ref, layer, name):
    start, length = VEC_AT[layer][name]
    return vec_ref[:, start : start + length]


def dot(left, right):
    return jnp.dot(left, right, preferred_element_type=f32)


def dot_nt(left, right, precision=None):
    return lax.dot_general(
        left, right, (((1,), (1,)), ((), ())), precision=precision, preferred_element_type=f32
    )


def dot_tn(left, right):
    return lax.dot_general(left, right, (((0,), (0,)), ((), ())), preferred_element_type=f32)


def joined(ref, start, rows_n, panels):
    return jnp.concatenate(
        [ref[start + p * rows_n : start + (p + 1) * rows_n, :] for p in range(panels)], axis=1
    )


def norm_stats(values):
    mean_val = jnp.mean(values, axis=-1, keepdims=True)
    centered = values - mean_val
    inv_std = lax.rsqrt(jnp.mean(centered * centered, axis=-1, keepdims=True) + norm_eps)
    return centered * inv_std, inv_std


def norm_back(values, gain, grad):
    unit, inv_std = norm_stats(values)
    scaled = grad * gain
    mean_s = jnp.mean(scaled, axis=-1, keepdims=True)
    mean_u = jnp.mean(scaled * unit, axis=-1, keepdims=True)
    back = inv_std * (scaled - mean_s - unit * mean_u)
    return (
        back,
        jnp.sum(grad * unit, axis=0, keepdims=True),
        jnp.sum(grad, axis=0, keepdims=True),
    )


def accumulate(ref, value):
    first = pl.program_id(0) == 0

    @pl.when(first)
    def _():
        ref[...] = value

    @pl.when(jnp.logical_not(first))
    def _():
        ref[...] += value


def stay(value):
    return pltpu.with_memory_space_constraint(value, pltpu.HBM)


def fence(*arrays):
    def nothing(*refs):
        pass

    anywhere = pl.BlockSpec(memory_space=pl.ANY)
    return pl.pallas_call(
        nothing,
        out_shape=[jax.ShapeDtypeStruct(a.shape, a.dtype) for a in arrays],
        in_specs=[anywhere] * len(arrays),
        out_specs=[anywhere] * len(arrays),
        input_output_aliases={i: i for i in range(len(arrays))},
    )(*[stay(a) if a.size > 4 * MIB else a for a in arrays])


def gather_kernel(slots, count_a, count_b, owner, drow, dcol, flag, *refs):
    first = refs[:count_a]
    second = refs[count_a : count_a + count_b]
    panels, vectors, held, sem, vec_sem = refs[count_a + count_b :]

    def copy_all(sources):
        at = 0
        for src in sources:
            for n in range(src.shape[0]):
                who = owner[at]
                at += 1

                def body(i, carried, src=src, n=n, who=who):
                    slot = who * slots + i
                    row = drow[slot]

                    @pl.when(row >= 0)
                    def _():
                        start = pl.multiple_of(i * BS, BS)
                        pltpu.make_async_copy(
                            src.at[n, pl.ds(start, BS), :],
                            held.at[
                                pl.ds(pl.multiple_of(row, BS), BS),
                                pl.ds(pl.multiple_of(dcol[slot], BS), BS),
                            ],
                            sem,
                        ).start()

                    return carried

                lax.fori_loop(0, slots, body, 0)
                pltpu.make_async_copy(
                    src.at[n, pl.ds(slots * BS, VEC_ROWS), :], vectors.at[who], vec_sem
                ).start()

    if count_b:

        @pl.when(flag[0] == 1)
        def _():
            copy_all(first)

        @pl.when(flag[0] == 0)
        def _():
            copy_all(second)
    else:
        copy_all(first)
    pltpu.make_async_copy(held, held, sem).wait()
    out = pltpu.make_async_copy(held, panels, sem)
    out.start()
    pltpu.make_async_copy(vectors, vectors, vec_sem).wait()
    out.wait()


def gather_tiles(first, second, owner, drow, dcol, flag, slots, owners):
    anywhere = pl.BlockSpec(memory_space=pl.ANY)
    return pl.pallas_call(
        functools.partial(gather_kernel, slots, len(first), len(second)),
        out_shape=(
            pltpu.HBM((PANEL_ROWS, HALF), bf16),
            jax.ShapeDtypeStruct((owners, VEC_ROWS, BS), bf16),
        ),
        grid_spec=pltpu.PrefetchScalarGridSpec(
            num_scalar_prefetch=4,
            grid=(1,),
            in_specs=[anywhere] * (len(first) + len(second)),
            out_specs=(anywhere, fixed((owners, VEC_ROWS, BS))),
            scratch_shapes=[
                pltpu.VMEM((PANEL_ROWS, HALF), bf16),
                pltpu.SemaphoreType.DMA,
                pltpu.SemaphoreType.DMA,
            ],
        ),
        compiler_params=params(),
        cost_estimate=cost(0, 4 * PANEL_ROWS * HALF),
    )(owner, drow, dcol, flag, *first, *second)


def scatter_kernel(rows_n, cols_n, steps, paired, parts, pos, part, own, *refs):
    @pl.when(part[1] > 0)
    def _():
        scatter_body(rows_n, cols_n, steps, paired, parts, pos, part, own, *refs)


def scatter_body(rows_n, cols_n, steps, paired, parts, pos, part, own, *refs):
    if paired:
        recv, *refs = refs
        span = pl.num_programs(0) // parts
        here = jnp.logical_or(parts == 1, pl.program_id(0) // span == part[0])
    target, buf, sems = refs[-3:]
    step = pl.program_id(0)
    slot = lax.rem(step, 2)
    per = rows_n // BS * (cols_n // BS)

    def wait(at):
        pltpu.make_async_copy(buf.at[at], buf.at[at], sems.at[at]).wait()

    @pl.when(step >= 2)
    def _():
        wait(slot)

    for i in range(rows_n // BS):
        for j in range(cols_n // BS):
            area = (slice(i * BS, (i + 1) * BS), slice(j * BS, (j + 1) * BS))
            value = own[area]
            if paired:
                more = jnp.where(here, recv[area].astype(f32), 0.0)
                value = (value.astype(f32) + more).astype(bf16)
            buf[slot, i * (cols_n // BS) + j] = value
    for n in range(per):
        pltpu.make_async_copy(
            buf.at[slot, n],
            target.at[pl.ds(pl.multiple_of(pos[step * per + n], 16), BS), :],
            sems.at[slot],
        ).start()

    @pl.when(step == pl.num_programs(0) - 1)
    def _():
        if steps > 1:
            wait(1 - slot)
        wait(slot)


def scatter_matrix(pos, own, recv, part, target, total_rows, rows_n):
    cols_n = own.shape[1]
    steps = own.shape[0] // rows_n
    anywhere = pl.BlockSpec(memory_space=pl.ANY)
    block = pl.BlockSpec((rows_n, cols_n), lambda i, *_: (i, 0))
    paired = recv is not None
    parts = own.shape[0] // recv.shape[0] if paired else 1
    span = steps // parts
    arrived = pl.BlockSpec(
        (rows_n, cols_n), lambda i, pos, part: (jnp.clip(i - part[0] * span, 0, span - 1), 0)
    )
    operands = [own] + ([recv] if paired else []) + ([] if target is None else [stay(target)])
    specs = [block] + ([block if parts == 1 else arrived] if paired else [])
    specs += [] if target is None else [anywhere]
    return pl.pallas_call(
        functools.partial(scatter_kernel, rows_n, cols_n, steps, paired, parts),
        out_shape=pltpu.HBM((total_rows, BS), bf16),
        grid_spec=pltpu.PrefetchScalarGridSpec(
            num_scalar_prefetch=2,
            grid=(steps,),
            in_specs=specs,
            out_specs=anywhere,
            scratch_shapes=[
                pltpu.VMEM((2, rows_n // BS * (cols_n // BS), BS, BS), bf16),
                pltpu.SemaphoreType.DMA((2,)),
            ],
        ),
        input_output_aliases={} if target is None else {len(operands) + 1: 0},
        compiler_params=params(),
        cost_estimate=cost(own.size, own.size * 6),
    )(pos, part, *operands)


def half_sum_kernel(part, own, arrived, out):
    out[...] = (own[...].astype(f32) + arrived[...].astype(f32)).astype(bf16)


def half_sum(part, own, arrived):
    block = arrived.shape
    return pl.pallas_call(
        half_sum_kernel,
        out_shape=jax.ShapeDtypeStruct(block, bf16),
        grid_spec=pltpu.PrefetchScalarGridSpec(
            num_scalar_prefetch=1,
            grid=(1,),
            in_specs=[pl.BlockSpec(block, lambda i, part: (part[0], 0)), fixed(block)],
            out_specs=fixed(block),
        ),
        compiler_params=params(),
        cost_estimate=cost(arrived.size, arrived.size * 6),
    )(part, own, arrived)


def half_copy_kernel(part, own, out):
    out[...] = own[...]


def other_half(part, own):
    block = (own.shape[0] // 2, own.shape[1])
    return pl.pallas_call(
        half_copy_kernel,
        out_shape=jax.ShapeDtypeStruct(block, bf16),
        grid_spec=pltpu.PrefetchScalarGridSpec(
            num_scalar_prefetch=1,
            grid=(1,),
            in_specs=[pl.BlockSpec(block, lambda i, part: (1 - part[0], 0))],
            out_specs=fixed(block),
        ),
        compiler_params=params(),
        cost_estimate=cost(0, own.size * 2),
    )(part, own)


def scatter_vec_kernel(paired, pos, own, *refs):
    if paired:
        recv, *refs = refs
    target, buf, sem = refs[-3:]
    value = own[...]
    if paired:
        value = (value.astype(f32) + recv[...].astype(f32)).astype(bf16)
    buf[...] = value

    def body(n, carried):
        pltpu.make_async_copy(
            buf.at[n], target.at[pl.ds(pl.multiple_of(pos[n], 16), VEC_ROWS), :], sem
        ).start()
        return carried

    lax.fori_loop(0, own.shape[0], body, 0)
    pltpu.make_async_copy(buf, buf, sem).wait()


def scatter_vec(pos, own, recv, target):
    anywhere = pl.BlockSpec(memory_space=pl.ANY)
    block = fixed(own.shape)
    paired = recv is not None
    operands = [own] + ([recv] if paired else []) + [stay(target)]
    return pl.pallas_call(
        functools.partial(scatter_vec_kernel, paired),
        out_shape=pltpu.HBM(target.shape, bf16),
        grid_spec=pltpu.PrefetchScalarGridSpec(
            num_scalar_prefetch=1,
            grid=(1,),
            in_specs=[block] * (len(operands) - 1) + [anywhere],
            out_specs=anywhere,
            scratch_shapes=[pltpu.VMEM(own.shape, bf16), pltpu.SemaphoreType.DMA],
        ),
        input_output_aliases={len(operands): 0},
        compiler_params=params(),
    )(pos, *operands)


def expand_kernel(present, half, patch_ref, class_ref, pinv_ref, out, total):
    for block in range(patch_ref.shape[0] // ROWS):
        rows = slice(block * ROWS, (block + 1) * ROWS)
        total[...] = jnp.zeros_like(total)
        for which in range(3):

            @pl.when(present[block, which] > 0)
            def _(which=which, rows=rows):
                chosen = jnp.where(class_ref[rows, :] == which, patch_ref[rows, :].astype(f32), 0.0)
                total[...] += dot_nt(chosen.astype(bf16), pinv_ref[which])

        out[rows, :] = total[...].astype(bf16)


def expand_call(which, present, half, patches, class_col, pinv):
    tokens = patches.shape[0]
    size = BASE_PIX // CHUNKS
    step = size
    return pl.pallas_call(
        expand_kernel,
        out_shape=jax.ShapeDtypeStruct((tokens, size), bf16),
        grid_spec=pltpu.PrefetchScalarGridSpec(
            num_scalar_prefetch=2,
            grid=(1,),
            in_specs=[
                fixed(patches.shape),
                fixed(class_col.shape),
                pl.BlockSpec(
                    (3, step, pinv.shape[2]),
                    lambda i, present, half: (0, (which + half[0] * (CHUNKS // 2)) % CHUNKS, 0),
                ),
            ],
            out_specs=pl.BlockSpec((tokens, step), lambda i, *_: (0, i)),
            scratch_shapes=[pltpu.VMEM((ROWS, step), f32)],
        ),
        compiler_params=params(),
        cost_estimate=cost(3 * tokens * size * D, tokens * size * 4 + size * D * 6),
    )(present, half, patches, class_col, stay(pinv))


def resize_kernel(base, pinv_ref, out, turned):
    @pl.when(pl.program_id(0) == 0)
    def _():
        turned[...] = base[...].T

    out[0] = dot(turned[...], pinv_ref[0]).astype(bf16)


def resize_call(panels, pinv):
    return pl.pallas_call(
        resize_kernel,
        out_shape=jax.ShapeDtypeStruct((3, HALF, pinv.shape[2]), bf16),
        grid=(3,),
        in_specs=[
            fixed((BASE_PIX, HALF), PANELS["base"] // BASE_PIX),
            pl.BlockSpec((1, BASE_PIX, pinv.shape[2]), lambda i: (i, 0, 0)),
        ],
        out_specs=pl.BlockSpec((1, HALF, pinv.shape[2]), lambda i: (i, 0, 0)),
        scratch_shapes=[pltpu.VMEM((HALF, BASE_PIX), bf16)],
        compiler_params=params(),
        cost_estimate=cost(6 * D * BASE_PIX * HALF, 6 * D * BASE_PIX),
    )(stay(panels), stay(pinv))


def embed_back_kernel(core, base, own, recv, out, bias):
    low = (base[...] + (own[...].astype(f32) + recv[...].astype(f32))).astype(bf16)
    out[...] = low
    accumulate(bias, jnp.sum(low.astype(f32), axis=0, keepdims=True))


def embed_back_call(core, base, own, recv):
    tokens = base.shape[0]
    half = pl.BlockSpec((ROWS, HALF), lambda i, core: (i, core[0]))
    return pl.pallas_call(
        embed_back_kernel,
        out_shape=[
            jax.ShapeDtypeStruct((tokens, HALF), bf16),
            jax.ShapeDtypeStruct((1, HALF), f32),
        ],
        grid_spec=pltpu.PrefetchScalarGridSpec(
            num_scalar_prefetch=1,
            grid=(tokens // ROWS,),
            in_specs=[half] * 3,
            out_specs=[rows_spec(HALF), fixed((1, HALF))],
        ),
        compiler_params=params(),
        cost_estimate=cost(tokens * D, tokens * D * 5),
    )(core, base, own, recv)


def pack_kernel(vec_per, *refs):
    *pieces, out = refs
    out[...] = jnp.zeros_like(out)
    at = 0
    for piece in pieces:
        for k in range(piece.shape[1] // BS):
            owner, row = divmod(at, vec_per // BS)
            out[owner, row : row + 1, :] = piece[:, k * BS : (k + 1) * BS]
            at += 1


def pack_call(pieces, owners, vec_per):
    if vec_per % BS:
        joined = jnp.concatenate(pieces, axis=1)[0]
        joined = jnp.pad(joined, (0, owners * vec_per - joined.shape[0])).reshape(owners, vec_per)
        joined = jnp.pad(joined, ((0, 0), (0, VEC_ROWS * BS - vec_per)))
        return joined.astype(bf16).reshape(owners, VEC_ROWS, BS)
    return pl.pallas_call(
        functools.partial(pack_kernel, vec_per),
        out_shape=jax.ShapeDtypeStruct((owners, VEC_ROWS, BS), f32),
        grid=(1,),
        in_specs=[fixed(p.shape) for p in pieces],
        out_specs=fixed((owners, VEC_ROWS, BS)),
        compiler_params=params(),
        cost_estimate=cost(0, owners * vec_per * 8),
    )(*pieces).astype(bf16)


def embed_kernel(half, *refs):
    *parts, vec, weight, out = refs
    size = BASE_PIX // CHUNKS
    total = vec[:, :HALF]
    for c in range(CHUNKS):
        at = lax.rem(c + half[0] * (CHUNKS // 2), CHUNKS)
        rows = pl.ds(pl.multiple_of(at * size, size), size)
        total = total + dot(parts[c][...], weight[rows, :])
    out[...] = total.astype(bf16)


def embed_call(half, chunks, vec, panels):
    tokens = chunks[0].shape[0]
    return pl.pallas_call(
        embed_kernel,
        out_shape=jax.ShapeDtypeStruct((tokens, HALF), bf16),
        grid_spec=pltpu.PrefetchScalarGridSpec(
            num_scalar_prefetch=1,
            grid=(tokens // ROWS,),
            in_specs=[rows_spec(BASE_PIX // CHUNKS)] * CHUNKS
            + [fixed(vec.shape), fixed((BASE_PIX, HALF), PANELS["base"] // BASE_PIX)],
            out_specs=rows_spec(HALF),
        ),
        compiler_params=params(),
        cost_estimate=cost(2 * tokens * BASE_PIX * HALF, tokens * BASE_PIX * 3),
    )(half, *chunks, vec, stay(panels))


def qkv_kernel(layer, first, core, *refs):
    if first:
        own, recv, vec, weight, hid, normed, q_ref, k_ref, v_ref = refs
        mine, theirs = own[...].astype(f32), recv[...].astype(f32)
        low = core[0] == 0
        values = jnp.concatenate(
            [jnp.where(low, mine, theirs), jnp.where(low, theirs, mine)], axis=1
        )
    else:
        base, own, recv, vec, weight, hid, normed, q_ref, k_ref, v_ref = refs
        values = base[...] + (own[...].astype(f32) + recv[...].astype(f32))
    hid[...] = values
    unit, unused = norm_stats(values)
    low = (unit * vec_piece(vec, layer, "g1") + vec_piece(vec, layer, "s1")).astype(bf16)
    normed[...] = low
    made = dot(low, joined(weight, 0, D, 3))
    q_ref[...] = (made[:, :HALF] + vec_piece(vec, layer, "bq")).astype(bf16)
    k_ref[...] = made[:, HALF : 2 * HALF].astype(bf16)
    v_ref[...] = (made[:, 2 * HALF :] + vec_piece(vec, layer, "bv")).astype(bf16)


def qkv_call(layer, base, own, recv, core, vec, panels):
    tokens = own.shape[0]
    shape = lambda width, kind: jax.ShapeDtypeStruct((tokens, width), kind)
    outs = [shape(D, f32), pltpu.HBM((tokens, D), bf16)] + [shape(HALF, bf16)] * 3
    operands = ([] if base is None else [base]) + [own, recv]
    return pl.pallas_call(
        functools.partial(qkv_kernel, layer, base is None),
        out_shape=outs,
        grid_spec=pltpu.PrefetchScalarGridSpec(
            num_scalar_prefetch=1,
            grid=(tokens // ROWS,),
            in_specs=[rows_spec(o.shape[1]) for o in operands]
            + [fixed(vec.shape), fixed((3 * D, HALF), PANELS["qkv"][layer] // (3 * D))],
            out_specs=[rows_spec(o.shape[1]) for o in outs],
        ),
        compiler_params=params(),
        cost_estimate=cost(2 * tokens * D * 3 * HALF, tokens * D * 14),
    )(core, *operands, vec, stay(panels))


def head_masks():
    lane = lax.broadcasted_iota(jnp.int32, (1, 2 * HEAD_DIM), 1)
    low = (lane < HEAD_DIM).astype(f32).astype(bf16)
    high = (lane >= HEAD_DIM).astype(f32).astype(bf16)
    return low, high


def attend_kernel(
    layer, low_ref, high_ref, q_ref, k_ref, v_ref, seg_q, seg_k, vec, w_out, o_ref, lse_ref, part,
    scores_ref, top_ref, acc_ref,
):
    step = pl.program_id(0)
    first, last = low_ref[step], high_ref[step]
    masks = head_masks()
    scale = jnp.asarray(HEAD_DIM ** (-0.5), bf16)
    lane = lax.broadcasted_iota(jnp.int32, (1, BS), 1)
    sums = [(lane == HEAD_DIM).astype(f32).astype(bf16), (lane == 0).astype(f32).astype(bf16)]
    top_ref[...] = jnp.full(top_ref.shape, masked_score, f32)
    acc_ref[...] = jnp.zeros_like(acc_ref)
    seg_col = seg_q[...]

    def score_block(block, carried):
        rows = pl.ds(pl.multiple_of(block * ROWS, ROWS), ROWS)
        same = seg_col == seg_k[:, rows]
        for pair in range(HEADS // 2):
            cols = slice(pair * BS, (pair + 1) * BS)
            q_two = q_ref[:, cols] * scale
            k_two = k_ref[rows, cols]
            for side in range(2):
                head = 2 * pair + side
                scores = jnp.where(same, dot_nt(q_two * masks[side], k_two), masked_score)
                scores_ref[head, block] = scores
                top = top_ref[head]
                for piece in range(ROWS // BS):
                    top = jnp.maximum(top, scores[:, piece * BS : (piece + 1) * BS])
                top_ref[head] = top
        return carried

    lax.fori_loop(first, last, score_block, 0)
    tops = [jnp.max(top_ref[head], axis=1, keepdims=True) for head in range(HEADS)]

    def mix_block(block, carried):
        rows = pl.ds(pl.multiple_of(block * ROWS, ROWS), ROWS)
        for pair in range(HEADS // 2):
            v_two = v_ref[rows, pair * BS : (pair + 1) * BS]
            for side in range(2):
                head = 2 * pair + side
                expo = jnp.exp(scores_ref[head, block] - tops[head]).astype(bf16)
                acc_ref[head] += dot(expo, v_two * masks[side] + sums[side])
        return carried

    lax.fori_loop(first, last, mix_block, 0)
    totals = jnp.zeros((ROWS, BS), f32)
    for pair in range(HEADS // 2):
        sides = []
        for side in range(2):
            head = 2 * pair + side
            mixed = acc_ref[head]
            at = HEAD_DIM * (1 - side)
            total = mixed[:, at : at + 1]
            totals = jnp.where(lane == head, tops[head] + jnp.log(total), totals)
            sides.append(mixed * (1.0 / total))
        o_ref[:, pair * BS : (pair + 1) * BS] = jnp.where(lane < HEAD_DIM, *sides).astype(bf16)
    lse_ref[...] = totals.T[0:8, :]
    low = o_ref[...]
    bias = vec_piece(vec, layer, "bo")
    part[...] = (dot(low, joined(w_out, 0, HALF, TENSOR)) + bias).astype(bf16)


def attend_call(layer, first, last, queries, keys, values, seg_col, seg_row, vec, panels):
    tokens = queries.shape[0]
    return pl.pallas_call(
        functools.partial(attend_kernel, layer),
        out_shape=[
            jax.ShapeDtypeStruct((tokens, HALF), bf16),
            jax.ShapeDtypeStruct((8, tokens), f32),
            jax.ShapeDtypeStruct((tokens, D), bf16),
        ],
        grid_spec=pltpu.PrefetchScalarGridSpec(
            num_scalar_prefetch=2,
            grid=(tokens // ROWS,),
            in_specs=[
                rows_spec(HALF),
                fixed(keys.shape),
                fixed(values.shape),
                rows_spec(1),
                fixed(seg_row.shape),
                fixed(vec.shape),
                fixed((D, HALF), PANELS["out"][layer] // D),
            ],
            out_specs=[
                rows_spec(HALF),
                pl.BlockSpec((8, ROWS), lambda i, *_: (0, i)),
                rows_spec(D),
            ],
            scratch_shapes=[
                pltpu.VMEM((HEADS, tokens // ROWS, ROWS, ROWS), f32),
                pltpu.VMEM((HEADS, ROWS, BS), f32),
                pltpu.VMEM((HEADS, ROWS, BS), f32),
            ],
        ),
        compiler_params=params(),
        cost_estimate=cost(8 * HEADS * tokens * tokens * BS, tokens * D * 8, HEADS * tokens * tokens),
    )(first, last, queries, keys, values, seg_col, seg_row, vec, stay(panels))


def gelu_parts(values):
    cdf = 0.5 * (1.0 + lax.erf(values * 0.7071067811865476))
    pdf = 0.3989422804014327 * jnp.exp(-0.5 * values * values)
    return values * cdf, cdf + values * pdf


def mlp_kernel(layer, base, own, recv, vec, w_up, w_down, hid, normed, act, slope, part):
    values = base[...] + (own[...].astype(f32) + recv[...].astype(f32))
    hid[...] = values
    unit, unused = norm_stats(values)
    low = (unit * vec_piece(vec, layer, "g2") + vec_piece(vec, layer, "s2")).astype(bf16)
    normed[...] = low
    bias_up = vec_piece(vec, layer, "b1")
    for pair in range(HALF_FF // D):
        area = slice(pair * D, (pair + 1) * D)
        up = dot(low, joined(w_up, pair * 2 * D, D, 2)) + bias_up[:, area]
        gelu, grad = gelu_parts(up)
        act[:, area] = gelu.astype(bf16)
        slope[:, area] = grad.astype(bf16)
    bias_down = vec_piece(vec, layer, "b2")
    part[...] = (dot(act[...], joined(w_down, 0, HALF_FF, TENSOR)) + bias_down).astype(bf16)


def mlp_call(layer, base, own, recv, vec, panels):
    tokens = base.shape[0]
    shape = lambda width, kind: jax.ShapeDtypeStruct((tokens, width), kind)
    kept = lambda width: pltpu.HBM((tokens, width), bf16)
    outs = [shape(D, f32), kept(D), kept(HALF_FF), kept(HALF_FF), shape(D, bf16)]
    return pl.pallas_call(
        functools.partial(mlp_kernel, layer),
        out_shape=outs,
        grid=(tokens // ROWS,),
        in_specs=[rows_spec(D)] * 3
        + [
            fixed(vec.shape),
            fixed((2 * HALF_FF, HALF), PANELS["up"][layer] // (2 * HALF_FF)),
            fixed((2 * HALF_FF, HALF), PANELS["down"][layer] // (2 * HALF_FF)),
        ],
        out_specs=[rows_spec(o.shape[1]) for o in outs],
        compiler_params=params(),
        cost_estimate=cost(4 * tokens * D * HALF_FF, tokens * D * 24, 2 * tokens * HALF_FF),
    )(base, own, recv, vec, stay(panels), stay(panels))


def mlp_back_kernel(layer, summed, *refs):
    if summed:
        base, own, recv, *refs = refs
        (hid, slope, vec, w_up, w_down, grad_full, grad_low, du_ref, back, dgain, dshift, db1, db2) = refs
        values = base[...].astype(f32) + (own[...].astype(f32) + recv[...].astype(f32))
        grad_full[...] = values
        low = values.astype(bf16)
    else:
        base, valid, *refs = refs
        (hid, slope, vec, w_up, w_down, grad_low, du_ref, back, dgain, dshift, db1, db2) = refs
        low = (base[...].astype(f32) * valid[...]).astype(bf16)
    grad_low[...] = low
    accumulate(db2, jnp.sum(low.astype(f32), axis=0, keepdims=True))
    for part in range(HALF_FF // D):
        area = slice(part * D, (part + 1) * D)
        rows = jnp.concatenate(
            [w_down[p * HALF_FF + part * D : p * HALF_FF + (part + 1) * D, :] for p in range(TENSOR)],
            axis=1,
        )
        du_ref[:, area] = (dot_nt(low, rows) * slope[:, area].astype(f32)).astype(bf16)
    grad_normed = dot_nt(du_ref[...], joined(w_up, 0, D, HALF_FF // HALF))
    accumulate(db1, jnp.sum(du_ref[...].astype(f32), axis=0, keepdims=True))
    part_back, gain_grad, shift_grad = norm_back(hid[...], vec_piece(vec, layer, "g2"), grad_normed)
    back[...] = part_back.astype(bf16)
    accumulate(dgain, gain_grad)
    accumulate(dshift, shift_grad)


def mlp_back_call(layer, base, own, recv, valid, hid, slope, vec, panels):
    tokens = base.shape[0]
    summed = own is not None
    shape = lambda width, kind: jax.ShapeDtypeStruct((tokens, width), kind)
    line = lambda width: jax.ShapeDtypeStruct((1, width), f32)
    outs = ([shape(D, f32)] if summed else []) + [shape(D, bf16), shape(HALF_FF, bf16), shape(D, bf16)]
    lines = [line(D), line(D), line(HALF_FF), line(D)]
    extra = [own, recv] if summed else [valid]
    return pl.pallas_call(
        functools.partial(mlp_back_kernel, layer, summed),
        out_shape=outs + lines,
        grid=(tokens // ROWS,),
        in_specs=[rows_spec(D)]
        + [rows_spec(e.shape[1]) for e in extra]
        + [
            rows_spec(D),
            rows_spec(HALF_FF),
            fixed(vec.shape),
            fixed((2 * HALF_FF, HALF), PANELS["up"][layer] // (2 * HALF_FF)),
            fixed((2 * HALF_FF, HALF), PANELS["down"][layer] // (2 * HALF_FF)),
        ],
        out_specs=[rows_spec(o.shape[1]) for o in outs] + [fixed(o.shape) for o in lines],
        compiler_params=params(),
        cost_estimate=cost(4 * tokens * D * HALF_FF, tokens * D * 24),
    )(base, *extra, stay(hid), stay(slope), vec, stay(panels), stay(panels))


def attend_back_kernel(
    low_ref, high_ref, base, own, recv, q_ref, k_ref, v_ref, o_ref, lse_ref, seg_k, seg_q, w_out,
    full_ref, grad_low, dq_ref, dk_ref, dv_ref, dbo, dk_acc, dv_acc, dq_acc, do_ref,
):
    step = pl.program_id(0)

    @pl.when(step == 0)
    def _():
        dk_acc[...] = jnp.zeros_like(dk_acc)
        dv_acc[...] = jnp.zeros_like(dv_acc)

    values = base[...].astype(f32) + (own[...].astype(f32) + recv[...].astype(f32))
    full_ref[...] = values
    low = values.astype(bf16)
    grad_low[...] = low
    accumulate(dbo, jnp.sum(low.astype(f32), axis=0, keepdims=True))
    do_ref[...] = dot_nt(low, joined(w_out, 0, HALF, TENSOR)).astype(bf16)
    product = do_ref[...].astype(f32) * o_ref[...].astype(f32)
    head = lax.broadcasted_iota(jnp.int32, (8, HALF), 0)
    lane = lax.broadcasted_iota(jnp.int32, (8, HALF), 1)
    pick = ((lane >= head * HEAD_DIM) & (lane < (head + 1) * HEAD_DIM)).astype(f32)
    high, rest = split(product)
    pick = pick.astype(bf16)
    inner = dot_nt(pick, high) + dot_nt(pick, rest)
    dq_acc[...] = jnp.zeros_like(dq_acc)
    masks = head_masks()
    scale = jnp.asarray(HEAD_DIM ** (-0.5), bf16)
    seg_row = seg_q[...]

    def one_block(block, carried):
        rows = pl.ds(pl.multiple_of(block * KEYS, KEYS), KEYS)
        same = seg_k[rows, :] == seg_row
        for pair in range(HEADS // 2):
            cols = slice(pair * BS, (pair + 1) * BS)
            q_two = q_ref[:, cols] * scale
            do_two = do_ref[:, cols]
            k_two = k_ref[rows, cols]
            v_two = v_ref[rows, cols]
            dv_two = dk_two = dq_two = None
            for side in range(2):
                at = 2 * pair + side
                q_one = q_two * masks[side]
                do_one = do_two * masks[side]
                scores = dot_nt(k_two, q_one)
                prob = jnp.where(same, jnp.exp(scores - lse_ref[at : at + 1, :]), 0.0)
                grad_prob = dot_nt(v_two, do_one)
                grad_scores = (prob * (grad_prob - inner[at : at + 1, :])).astype(bf16)
                dv_one = dot(prob.astype(bf16), do_one)
                dk_one = dot(grad_scores, q_one)
                dq_one = dot_tn(grad_scores, k_two * masks[side])
                dq_two = dq_one if dq_two is None else dq_two + dq_one
                dv_two = dv_one if dv_two is None else dv_two + dv_one
                dk_two = dk_one if dk_two is None else dk_two + dk_one
            dv_acc[rows, cols] += dv_two
            dk_acc[rows, cols] += dk_two
            dq_acc[:, cols] += dq_two
        return carried

    lax.fori_loop(low_ref[step], high_ref[step], one_block, 0)
    dq_ref[...] = (dq_acc[...] * HEAD_DIM ** (-0.5)).astype(bf16)

    @pl.when(step == pl.num_programs(0) - 1)
    def _():
        dk_ref[...] = dk_acc[...].astype(bf16)
        dv_ref[...] = dv_acc[...].astype(bf16)


def attend_back_call(
    layer, first, last, base, own, recv, queries, keys, values, mixed, lse, seg_col, seg_row, panels
):
    tokens = base.shape[0]
    shape = lambda width, kind: jax.ShapeDtypeStruct((tokens, width), kind)
    whole = (tokens, HALF)
    return pl.pallas_call(
        attend_back_kernel,
        out_shape=[
            shape(D, f32),
            shape(D, bf16),
            shape(HALF, bf16),
            shape(HALF, bf16),
            shape(HALF, bf16),
            jax.ShapeDtypeStruct((1, D), f32),
        ],
        grid_spec=pltpu.PrefetchScalarGridSpec(
            num_scalar_prefetch=2,
            grid=(tokens // ROWS,),
            in_specs=[
                rows_spec(D),
                rows_spec(D),
                rows_spec(D),
                rows_spec(HALF),
                fixed(whole),
                fixed(whole),
                rows_spec(HALF),
                pl.BlockSpec((8, ROWS), lambda i, *_: (0, i)),
                fixed(seg_col.shape),
                pl.BlockSpec((1, ROWS), lambda i, *_: (0, i)),
                fixed((D, HALF), PANELS["out"][layer] // D),
            ],
            out_specs=[
                rows_spec(D),
                rows_spec(D),
                rows_spec(HALF),
                fixed(whole),
                fixed(whole),
                fixed((1, D)),
            ],
            scratch_shapes=[
                pltpu.VMEM(whole, f32),
                pltpu.VMEM(whole, f32),
                pltpu.VMEM((ROWS, HALF), f32),
                pltpu.VMEM((ROWS, HALF), bf16),
            ],
        ),
        compiler_params=params(),
        cost_estimate=cost(14 * HEADS * tokens * tokens * BS, tokens * D * 20, HEADS * tokens * tokens),
    )(
        first, last, base, own, recv, stay(queries), stay(keys), stay(values), stay(mixed), stay(lse),
        seg_col, seg_row, stay(panels),
    )


def qkv_back_kernel(layer, dq, dk, dv, hid, vec, weight, back, dgain, dshift, dbq, dbv):
    grad_three = jnp.concatenate([dq[...], dk[...], dv[...]], axis=1)
    grad_normed = dot_nt(grad_three, joined(weight, 0, D, 3))
    part_back, gain_grad, shift_grad = norm_back(hid[...], vec_piece(vec, layer, "g1"), grad_normed)
    back[...] = part_back.astype(bf16)
    accumulate(dgain, gain_grad)
    accumulate(dshift, shift_grad)
    accumulate(dbq, jnp.sum(dq[...].astype(f32), axis=0, keepdims=True))
    accumulate(dbv, jnp.sum(dv[...].astype(f32), axis=0, keepdims=True))


def qkv_back_call(layer, dq, dk, dv, hid, vec, panels):
    tokens = dq.shape[0]
    line = lambda width: jax.ShapeDtypeStruct((1, width), f32)
    lines = [line(D), line(D), line(HALF), line(HALF)]
    return pl.pallas_call(
        functools.partial(qkv_back_kernel, layer),
        out_shape=[jax.ShapeDtypeStruct((tokens, D), bf16)] + lines,
        grid=(tokens // ROWS,),
        in_specs=[rows_spec(HALF)] * 3
        + [
            rows_spec(D),
            fixed(vec.shape),
            fixed((3 * D, HALF), PANELS["qkv"][layer] // (3 * D)),
        ],
        out_specs=[rows_spec(D)] + [fixed(o.shape) for o in lines],
        compiler_params=params(),
        cost_estimate=cost(2 * tokens * D * 3 * HALF, tokens * D * 10),
    )(dq, dk, dv, stay(hid), vec, stay(panels))


def split(values):
    high = values.astype(bf16)
    return high, (values - high.astype(f32)).astype(bf16)


def product(left, right, left_dim, right_dim):
    def one(a, b):
        return lax.dot_general(
            a, b, (((left_dim,), (right_dim,)), ((), ())), preferred_element_type=f32
        )

    return one(left[0], right[0]) + (one(left[0], right[1]) + one(left[1], right[0]))


def owner_kernel(per, used, home, near, far, master, left, right, moment, variance, grad, out, out_mom, out_var):
    here = range(per)
    first = pl.program_id(0) * per
    lefts = [split(left[i]) for i in here]
    rights = [split(right[i]) for i in here]
    rotated = []
    for i in here:
        rows = slice(i * BS, (i + 1) * BS)
        tile = jnp.where(home[0] > 0, near[rows, :].astype(f32), far[rows, :].astype(f32))
        tile = jnp.where(used[first + i] > 0, tile, 0.0)
        grad[i] = tile
        tile = tile.astype(bf16)
        rotated.append(split(dot_tn(lefts[i][0], tile) + dot_tn(lefts[i][1], tile)))
    rotated = [product(rotated[i], rights[i], 1, 0) for i in here]
    steps = []
    for i in here:
        new_moment = decay * moment[i] + (1.0 - decay) * rotated[i]
        new_variance = decay * variance[i] + (1.0 - decay) * rotated[i] * rotated[i]
        out_mom[i] = new_moment
        out_var[i] = new_variance
        steps.append(split(new_moment / (jnp.sqrt(new_variance) + adam_eps)))
    returned = [split(product(lefts[i], steps[i], 1, 0)) for i in here]
    returned = [product(returned[i], rights[i], 1, 1) for i in here]
    for i in here:
        out[i] = master[i] - matrix_rate * returned[i]


def owner_call(used, home, near, far, *arrays):
    count = arrays[0].shape[0]
    per = min(8, count)
    block = pl.BlockSpec((per, BS, BS), lambda i, *_: (i, 0, 0))
    return pl.pallas_call(
        functools.partial(owner_kernel, per),
        out_shape=[jax.ShapeDtypeStruct(arrays[0].shape, f32)] * 4,
        grid_spec=pltpu.PrefetchScalarGridSpec(
            num_scalar_prefetch=2,
            grid=(count // per,),
            in_specs=[pl.BlockSpec((per * BS, BS), lambda i, *_: (i, 0))] * 2 + [block] * 5,
            out_specs=[block] * 4,
        ),
        compiler_params=params(),
        cost_estimate=cost(count * 88 * BS**3, count * BS * BS * 38),
    )(used, home, near, far, *[stay(a) for a in arrays])


def reduce_kernel(carrying, last, *refs):
    block, arrived, *refs = refs
    total = block[...].astype(f32) + arrived[...].astype(f32)
    if carrying:
        carried, *refs = refs
        total = total + carried[...].astype(f32)
    if last:
        [out] = refs
    else:
        following, out, later = refs
        later[...] = following[...]
    out[...] = total.astype(bf16)


def reduce_call(j, n, buffer, arrived, carried, payload):
    last = j == 3
    at = lambda j, x_rel: pl.BlockSpec((payload, BS), lambda i: ((j * 2 + x_rel) * 2 + n, 0))
    whole = fixed((payload, BS))
    operands = [stay(buffer), arrived] + ([] if carried is None else [carried])
    specs = [at(j, 0)] + [whole] * (len(operands) - 1)
    if not last:
        operands.append(stay(buffer))
        specs.append(at(j + 1, 1))
    outs = [jax.ShapeDtypeStruct((payload, BS), bf16)] * (1 if last else 2)
    made = pl.pallas_call(
        functools.partial(reduce_kernel, carried is not None, last),
        out_shape=outs,
        grid=(1,),
        in_specs=specs,
        out_specs=[whole] * len(outs),
        compiler_params=params(),
        cost_estimate=cost(payload * BS * 3, payload * BS * 12),
    )(*operands)
    return (made[0], None) if last else made


class Routes:
    def __init__(self, dp_n):
        pairs = [(d, t) for d in range(dp_n) for t in range(TENSOR)]
        at = lambda d, t: d * TENSOR + t
        home = [(d, t) for d, t in pairs if d % 2 == t]
        away = [(d, t) for d, t in pairs if d % 2 != t]
        self.core_all = [(at(d, t), at(d ^ 1, t)) for d, t in pairs]
        self.core_out = [(at(d, t), at(d ^ 1, t)) for d, t in home]
        self.core_in = [(at(d, t), at(d ^ 1, t)) for d, t in away]
        self.y_all = [(at(d, t), at(d, 1 - t)) for d, t in pairs]
        self.y_out = [(at(d, t), at(d, 1 - t)) for d, t in home]
        self.y_in = [(at(d, t), at(d, 1 - t)) for d, t in away]
        self.x_home = [(at(d, t), at(d ^ 2, t)) for d, t in home]
        self.x_away = [(at(d, t), at(d ^ 2, t)) for d, t in away]
        self.z_home = [(at(d, t), at((d + 4) % dp_n, t)) for d, t in home]


def send(value, route):
    return lax.ppermute(value, AXES, route)


def shards(
    patches,
    cotangent,
    image_size,
    block_slot,
    pinv,
    master_slots,
    left_basis,
    right_basis,
    mom_slots,
    var_slots,
    vec_master,
    vec_mom,
    vec_var,
):
    dp_n = lax.axis_size("dp")
    dp_pos = lax.axis_index("dp")
    y_pos = lax.axis_index("tensor")
    core = dp_pos % 2
    home = core == y_pos
    routes = Routes(dp_n)
    grid3 = dp_n == 16
    x_pos = (dp_pos // 2) % 2
    half_at = (x_pos if grid3 else x_pos * 0).astype(jnp.int32).reshape(1)
    tokens_n = patches.shape[0]
    slots_per = master_slots.shape[1]
    vec_per = vec_master.shape[1]
    slots_n = slots_per * dp_n
    payload = slots_per * BS + VEC_ROWS

    patches = jnp.where(home, patches, send(patches, routes.core_out))
    cotangent = jnp.where(home, cotangent, send(cotangent, routes.core_out))
    size_row = jnp.where(home, image_size, send(image_size, routes.core_out))[0]
    own_slots = block_slot[0]
    slot_other = send(block_slot, routes.y_all)

    lengths = jnp.where(
        size_row == 0, LEN_A, jnp.where(size_row == 1, LEN_B, jnp.where(size_row == 2, LEN_C, 0))
    )
    order = jnp.arange(IMG_DEV)
    ends_at = jnp.sum(jnp.where(order[None, :] <= order[:, None], lengths[None, :], 0), axis=1)
    places = jnp.arange(tokens_n)
    segment = jnp.sum((places[:, None] >= ends_at[None, :]).astype(jnp.int32), axis=1)
    in_image = segment[:, None] == order[None, :]
    select = jnp.stack(
        [jnp.any(in_image & (size_row == s)[None, :], axis=1) for s in range(3)], axis=1
    )
    valid_col = (segment < IMG_DEV).astype(f32)[:, None]
    seg_col = segment[:, None]
    seg_row = segment[None, :]
    blocks_n = tokens_n // ROWS
    starts = jnp.arange(blocks_n) * ROWS
    begun = ends_at[None, :] <= starts[:, None]
    first_tok = jnp.max(jnp.where(begun, ends_at[None, :], 0), axis=1)
    after = ends_at[None, :] > (starts + ROWS - 1)[:, None]
    last_tok = jnp.min(jnp.where(after, ends_at[None, :], tokens_n), axis=1)
    first_blk = (first_tok // ROWS).astype(jnp.int32)
    last_blk = ((last_tok + ROWS - 1) // ROWS).astype(jnp.int32)
    first_key = (first_tok // KEYS).astype(jnp.int32)
    last_key = ((last_tok + KEYS - 1) // KEYS).astype(jnp.int32)

    select_low = select.astype(bf16)
    class_col = jnp.sum(jnp.where(select, jnp.arange(1, 4)[None, :], 0), axis=1, keepdims=True) - 1
    present = jnp.any(select.reshape(blocks_n, ROWS, 3), axis=1).astype(jnp.int32)

    def expand(which):
        return expand_call(which, present, half_at, patches, class_col, pinv)

    vec_low = jnp.pad(vec_master[0].astype(bf16), (0, VEC_ROWS * BS - vec_per))
    own_pack = jnp.concatenate(
        [
            master_slots[0].astype(bf16).reshape(slots_per * BS, BS),
            vec_low.reshape(VEC_ROWS, BS),
        ],
        axis=0,
    )
    flag = home.astype(jnp.int32).reshape(1)
    if grid3:
        z_pos = dp_pos // 4
        packs = [[own_pack], [send(own_pack, routes.core_in)]]
        across, over_y, corner = [[], []], [[], []], [[], []]
        token = jnp.zeros((8, BS), f32)
        chunks = []
        for j in range(5):
            for n in range(2):
                moved = []
                if j < 4:
                    moved += [send(packs[n][j], routes.x_home), send(packs[n][j], routes.y_out)]
                if j:
                    source, route = (across, routes.y_out) if n == 0 else (over_y, routes.x_away)
                    moved.append(send(source[n][j - 1], route))
                if j < 3:
                    moved.append(send(packs[n][j], routes.z_home))
                work = []
                if j + n == 0:
                    work = [slot_other]
                if 1 <= 2 * j + n <= CHUNKS:
                    work = [expand(2 * j + n - 1)]
                if j < 4:
                    token, *moved = fence(token, *moved, *work)
                    if j + n == 0:
                        slot_other = moved.pop()
                    elif work:
                        chunks.append(moved.pop())
                if j < 3:
                    packs[n].append(moved.pop())
                if j:
                    corner[n].append(moved.pop())
                if j < 4:
                    across[n].append(moved[0])
                    over_y[n].append(moved[1])
        first, second, owner = [], [], []
        for j in range(4):
            first += [packs[0][j], packs[1][j], across[0][j], across[1][j]]
            second += [over_y[0][j], over_y[1][j], corner[0][j], corner[1][j]]
            for x_rel in range(2):
                for n in range(2):
                    owner.append(((z_pos - j) % 4) * 4 + (x_pos ^ x_rel) * 2 + (core ^ n))
        first = [v[None] for v in first]
        second = [v[None] for v in second]
        owner = jnp.stack(owner).astype(jnp.int32)
    else:
        everything = lax.all_gather(own_pack, AXES, axis=0)
        everything = everything.reshape(dp_n, TENSOR, payload, BS)
        first = [jnp.where(core == 0, everything[:, 0], everything[:, 1])]
        second = []
        owner = jnp.arange(dp_n, dtype=jnp.int32)
        chunks = [expand(c) for c in range(CHUNKS)]
    slot_list = jnp.where(home, block_slot, slot_other)[0]
    named = slot_list[None, :] == jnp.arange(slots_n)[:, None]
    used = jnp.any(named, axis=1)
    drow = jnp.where(used, jnp.sum(jnp.where(named, TARGET_ROW[None, :], 0), axis=1), -1)
    dcol = jnp.sum(jnp.where(named, TARGET_COL[None, :], 0), axis=1)
    panels, vec_rows = gather_tiles(first, second, owner, drow, dcol, flag, slots_per, dp_n)
    vec = vec_rows.reshape(dp_n, VEC_ROWS * BS)[:, :vec_per].astype(f32).reshape(1, dp_n * vec_per)

    embedded = embed_call(half_at, chunks, vec, panels)
    embedded_other = send(embedded, routes.core_all)
    core_flag = core.astype(jnp.int32).reshape(1)

    caches = []
    hidden, own, recv = None, embedded, embedded_other
    for layer in range(LAYERS):
        hidden, normed, queries, keys, values = qkv_call(
            layer, hidden, own, recv, core_flag, vec, panels
        )
        mixed, lse, part = attend_call(
            layer, first_blk, last_blk, queries, keys, values, seg_col, seg_row, vec, panels
        )
        other = send(part, routes.core_all)
        middle, normed2, act, slope, own = mlp_call(layer, hidden, part, other, vec, panels)
        recv = send(own, routes.core_all)
        caches.append((hidden, normed, queries, keys, values, mixed, lse, middle, normed2, act, slope))
        hidden = middle
    out_low = ((hidden + (own.astype(f32) + recv.astype(f32))) * valid_col).astype(bf16)

    owners = jnp.arange(dp_n)
    if grid3:
        place = (
            ((z_pos - 1 - owners // 4) % 4) * 4
            + (x_pos ^ ((owners // 2) % 2)) * 2
            + (core ^ (owners % 2))
        ).astype(jnp.int32)
    else:
        place = owners.astype(jnp.int32)
    slot_owner = slot_list // slots_per
    owner_place = jnp.sum(
        jnp.where(slot_owner[:, None] == owners[None, :], place[None, :], 0), axis=1
    )
    tile_pos = (owner_place * payload + (slot_list % slots_per) * BS).astype(jnp.int32)
    vec_pos = (place * payload + slots_per * BS).astype(jnp.int32)
    total_rows = dp_n * payload
    where_to = jnp.concatenate([half_at, flag if grid3 else flag * 0 + 1])
    offsets = {"base": 0}
    count = BASE_PIX // BS * (HALF // BS)
    for layer in range(LAYERS):
        for name, size in (("qkv", 3 * D * HALF), ("out", D * HALF), ("up", D * HALF_FF), ("down", D * HALF_FF)):
            offsets[name, layer] = count
            count += size // (BS * BS)

    def place_tiles(key, matrix, arrived, buffer):
        tiles = matrix.size // (BS * BS)
        pos = tile_pos[offsets[key] : offsets[key] + tiles]
        rows_n = matrix.shape[0] // 2 if matrix.shape[0] > HALF else HALF
        return scatter_matrix(pos, matrix, arrived, where_to, buffer, total_rows, rows_n)

    def place_base(rel, matrix, arrived, buffer):
        size = BASE_PIX * HALF // (BS * BS) // 2
        low_pos, high_pos = tile_pos[:size], tile_pos[size : 2 * size]
        pos = jnp.where(half_at[0] == rel, low_pos, high_pos)
        return scatter_matrix(pos, matrix, arrived, where_to, buffer, total_rows, D)

    def over(matrix):
        return send(matrix, routes.y_in) if grid3 else None

    def beside(matrix):
        return send(other_half(half_at, matrix), routes.x_away) if grid3 else None

    def summed(matrix, arrived):
        return half_sum(half_at, matrix, arrived) if grid3 else None

    def hold(*arrays):
        kept = [a for a in arrays if a is not None]
        done = iter(fence(*kept))
        return [None if a is None else next(done) for a in arrays]

    top, low = 1, 0
    vec_grads = [None] * LAYERS

    def mlp_step(layer, grad, own, recv):
        middle, normed2, act, slope = caches[layer][7:11]
        made = mlp_back_call(layer, grad, own, recv, valid_col, middle, slope, vec, panels)
        if own is not None:
            return made
        return [made[0]] + list(made)

    def attend_step(layer, grad, part, other):
        hid_in, normed, queries, keys, values, mixed, lse = caches[layer][:7]
        return attend_back_call(
            layer, first_key, last_key, grad, part, other, queries, keys, values, mixed, lse,
            seg_col, seg_row, panels,
        )

    grad, grad_low, du, part, dg2, ds2, db1, db2 = mlp_step(top, cotangent, None, None)
    other = send(part, routes.core_all)
    gd1 = dot_tn(caches[top][9], grad_low).astype(bf16)
    gu1 = dot_tn(caches[top][8], du).astype(bf16)
    part, other, gd1, gu1, out_low = fence(part, other, gd1, gu1, out_low)
    ad1 = over(gd1)
    grad, grad_low, dq, dk, dv, dbo = attend_step(top, grad, part, other)
    dq, dk, dv, ad1 = hold(dq, dk, dv, ad1)
    au1 = over(gu1)
    own, dg1, ds1, dbq, dbv = qkv_back_call(top, dq, dk, dv, caches[top][0], vec, panels)
    recv = send(own, routes.core_all)
    go1 = dot_tn(caches[top][5], grad_low).astype(bf16)
    gq1 = dot_tn(caches[top][1], jnp.concatenate([dq, dk, dv], axis=1)).astype(bf16)
    vec_grads[top] = [dg1, ds1, dbq, dbv, dbo, dg2, ds2, db1, db2]
    grad, grad_low, du, part, dg2, ds2, db1, db2 = mlp_step(low, grad, own, recv)
    du, part, au1, go1, gq1 = hold(du, part, au1, go1, gq1)
    other = send(part, routes.core_all)
    xq1, ao1 = beside(gq1), over(go1)
    gd0 = dot_tn(caches[low][9], grad_low).astype(bf16)
    gu0 = dot_tn(caches[low][8], du).astype(bf16)
    part, other, gd0, gu0, xq1, ao1 = hold(part, other, gd0, gu0, xq1, ao1)
    aq1 = over(summed(gq1, xq1)) if grid3 else None
    xd0, xu0 = beside(gd0), beside(gu0)
    buffer = place_tiles(("down", top), gd1, ad1, None)
    buffer = place_tiles(("up", top), gu1, au1, buffer)
    grad, grad_low, dq, dk, dv, dbo = attend_step(low, grad, part, other)
    grad, grad_low, dq, dk, dv, aq1, xd0, xu0, buffer = hold(
        grad, grad_low, dq, dk, dv, aq1, xd0, xu0, buffer
    )
    hd0, hu0 = summed(gd0, xd0), summed(gu0, xu0)
    dq, dk, dv, hd0, hu0 = hold(dq, dk, dv, hd0, hu0)
    ad0, au0 = over(hd0), over(hu0)
    own, dg1, ds1, dbq, dbv = qkv_back_call(low, dq, dk, dv, caches[low][0], vec, panels)
    recv = send(own, routes.core_all)
    gq0 = dot_tn(caches[low][1], jnp.concatenate([dq, dk, dv], axis=1)).astype(bf16)
    vec_grads[low] = [dg1, ds1, dbq, dbv, dbo, dg2, ds2, db1, db2]
    own, recv, gq0 = hold(own, recv, gq0)
    xq0 = beside(gq0)
    grad_emb, grad_emb_bias = embed_back_call(core_flag, grad, own, recv)
    middle = CHUNKS // 2

    def base_grad(parts):
        return jnp.concatenate([dot_tn(c, grad_emb).astype(bf16) for c in parts], axis=0)

    gbt = base_grad(chunks[middle:])
    gbt, grad_emb, gq0 = hold(gbt, grad_emb, gq0)
    xb = send(gbt, routes.x_away) if grid3 else None
    gbm = base_grad(chunks[:middle])
    vec_grad = pack_call([grad_emb_bias] + vec_grads[0] + vec_grads[1], dp_n, vec_per)
    go0 = dot_tn(caches[low][5], grad_low).astype(bf16)
    hq0 = summed(gq0, xq0)
    gbm, vec_grad, go0, hq0 = hold(gbm, vec_grad, go0, hq0)
    aq0, ao0, av = over(hq0), over(go0), over(vec_grad)
    gbm, xb = hold(gbm, xb)
    hb = (gbm.astype(f32) + xb.astype(f32)).astype(bf16) if grid3 else None
    hb, gbm, gbt, buffer = hold(hb, gbm, gbt, buffer)
    ab = over(hb)
    buffer = place_tiles(("out", top), go1, ao1, buffer)
    buffer = place_tiles(("qkv", top), gq1, aq1, buffer)
    buffer = place_tiles(("down", low), gd0, ad0, buffer)
    buffer = place_tiles(("up", low), gu0, au0, buffer)
    buffer = place_base(1, gbt, None, buffer)
    buffer = place_tiles(("out", low), go0, ao0, buffer)
    buffer = scatter_vec(vec_pos, vec_grad, av, buffer)
    buffer = place_tiles(("qkv", low), gq0, aq0, buffer)
    ab, buffer, panels, grad_emb, out_low = hold(ab, buffer, panels, grad_emb, out_low)
    buffer = place_base(0, gbm, ab, buffer)

    if grid3:
        token = jnp.zeros((8, BS), f32)
        order = (1, 0)
        resized = resize_call(panels, pinv)
        carried = {n: None for n in order}
        across = {n: send(buffer.reshape(4, 2, 2, payload, BS)[0, 1, n], routes.x_home) for n in order}
        rounded = {}
        for j in range(4):
            for n in order:
                extra = None
                if j == 0 and n == order[0]:
                    extra = resized
                token, across[n], carried[n], extra = hold(token, across[n], carried[n], extra)
                if extra is not None:
                    resized = extra
                total, later = reduce_call(j, n, buffer, across[n], carried[n], payload)
                if j < 3:
                    carried[n] = send(total, routes.z_home)
                    across[n] = send(later, routes.x_home)
                else:
                    rounded[n] = total
        near_grad, far_grad = rounded[0], send(rounded[1], routes.core_out)
    else:
        held = buffer.reshape(dp_n, 1, payload, BS).astype(f32)
        nothing = jnp.zeros_like(held)
        both = jnp.concatenate(
            [jnp.where(core == 0, held, nothing), jnp.where(core == 0, nothing, held)], axis=1
        )
        used_rows = jnp.repeat(used, BS).reshape(dp_n, 1, slots_per * BS, 1)
        used_rows = jnp.concatenate(
            [used_rows, jnp.ones((dp_n, 1, VEC_ROWS, 1), bool)], axis=2
        )
        both = jnp.where(used_rows, both, 0.0).reshape(dp_n * TENSOR * payload, BS)
        near_grad = lax.psum_scatter(both, AXES, scatter_dimension=0, tiled=True).astype(bf16)
        far_grad = near_grad
        resized = resize_call(panels, pinv)

    output = jnp.where(home, out_low, send(out_low, routes.y_out)).astype(f32)
    grad_pixels = sum(
        dot(grad_emb * select_low[:, s : s + 1], resized[s]) for s in range(3)
    ).astype(bf16)
    pixels_other = send(grad_pixels, routes.core_all)
    pixel_sides = [
        grad_pixels[:, s * HALF : (s + 1) * HALF].astype(f32)
        + pixels_other[:, s * HALF : (s + 1) * HALF].astype(f32)
        for s in range(TENSOR)
    ]
    near = jnp.where(core == 0, pixel_sides[0], pixel_sides[1])
    far = jnp.where(core == 0, pixel_sides[1], pixel_sides[0]).astype(bf16)
    patch_grad = jnp.where(home, near, send(far, routes.y_out).astype(f32))

    my_slots = dp_pos * slots_per + jnp.arange(slots_per)
    mine_used = jnp.any(own_slots[None, :] == my_slots[:, None], axis=1).astype(jnp.int32)
    owned_grad, new_master, new_mom, new_var = owner_call(
        mine_used, flag, near_grad, far_grad, master_slots[0], left_basis[0], right_basis[0], mom_slots[0], var_slots[0]
    )
    vec_rows = jnp.where(home, near_grad[slots_per * BS :], far_grad[slots_per * BS :])
    owned_vec_grad = vec_rows.astype(f32).reshape(VEC_ROWS * BS)[:vec_per]
    new_vec_mom = decay * vec_mom[0] + (1.0 - decay) * owned_vec_grad
    new_vec_var = decay * vec_var[0] + (1.0 - decay) * owned_vec_grad * owned_vec_grad
    new_vec = vec_master[0] - vector_rate * new_vec_mom / (jnp.sqrt(new_vec_var) + adam_eps)
    return (
        output,
        patch_grad,
        owned_grad[None],
        new_master[None],
        new_mom[None],
        new_var[None],
        owned_vec_grad[None],
        new_vec[None],
        new_vec_mom[None],
        new_vec_var[None],
    )


def solution(mesh):
    slots = P("tensor", "dp", None, None)
    vectors = P("tensor", "dp")
    tokens = P("dp", None)
    in_specs = (tokens, tokens, tokens, P("tensor", None), P()) + (slots,) * 5 + (vectors,) * 3
    out_specs = (tokens, P("dp", "tensor")) + (slots,) * 4 + (vectors,) * 4
    return jax.shard_map(shards, mesh=mesh, in_specs=in_specs, out_specs=out_specs, check_vma=False)
```

```python
import functools

import jax
import jax.numpy as jnp
import numpy as np
from jax import lax
from jax.experimental import pallas as pl
from jax.experimental.pallas import tpu as pltpu
from jax.sharding import PartitionSpec as P

D = 768
HEAD_DIM = 64
FF = 3072
BASE_PIX = 3072
LAYERS = 2
LEN_A = 196
LEN_B = 225
LEN_C = 576
IMG_DEV = 5
BS = 128
TENSOR = 2
HALF = D // TENSOR
HALF_FF = FF // TENSOR
HEADS = HALF // HEAD_DIM
ROWS = 256
KEYS = 512
VEC_ROWS = 16
CHUNKS = 4

AXES = ("dp", "tensor")
precise = lax.Precision.HIGHEST
masked_score = -1e30
norm_eps = 1e-06
adam_eps = 1e-08
decay = 0.5
matrix_rate = 0.05
vector_rate = 0.3
f32 = jnp.float32
bf16 = jnp.bfloat16
MIB = 1024 * 1024

WEIGHTS = [("base", 0, BASE_PIX)]
for layer in range(LAYERS):
    WEIGHTS += [("qkv", layer, 3 * D), ("out", layer, D), ("up", layer, FF), ("down", layer, FF)]
STARTS = {}
PANEL_ROWS = 0
for name, layer, size in WEIGHTS:
    STARTS[name, layer] = PANEL_ROWS
    PANEL_ROWS += size


def tile_targets():
    rows, cols = [], []

    def add(start, rows_n, cols_n):
        for i in range(rows_n // BS):
            for j in range(cols_n // BS):
                panel, inner = divmod(j * BS, HALF)
                rows.append(start + panel * rows_n + i * BS)
                cols.append(inner)

    add(STARTS["base", 0], BASE_PIX, HALF)
    for layer in range(LAYERS):
        add(STARTS["qkv", layer], D, 3 * HALF)
        add(STARTS["out", layer], HALF, D)
        add(STARTS["up", layer], D, HALF_FF)
        add(STARTS["down", layer], HALF_FF, D)
    return np.array(rows, np.int32), np.array(cols, np.int32)


TARGET_ROW, TARGET_COL = tile_targets()
LAYER_VECS = (D, D, HALF, HALF, D, D, D, HALF_FF, D)
VEC_NAMES = ("g1", "s1", "bq", "bv", "bo", "g2", "s2", "b1", "b2")


def vec_offsets():
    offset = HALF
    found = []
    for layer in range(LAYERS):
        here = {}
        for name, length in zip(VEC_NAMES, LAYER_VECS):
            here[name] = (offset, length)
            offset += length
        found.append(here)
    return found


VEC_AT = vec_offsets()


def params(limit=24):
    return pltpu.CompilerParams(
        dimension_semantics=("arbitrary",), vmem_limit_bytes=limit * MIB
    )


def cost(flops, nbytes, trans=0):
    return pl.CostEstimate(flops=flops, bytes_accessed=nbytes, transcendentals=trans)


def rows_spec(width):
    return pl.BlockSpec((ROWS, width), lambda i, *_: (i, 0))


def fixed(shape, at=0):
    return pl.BlockSpec(shape, lambda i, *_: (at,) + (0,) * (len(shape) - 1))


def vec_piece(vec_ref, layer, name):
    start, length = VEC_AT[layer][name]
    return vec_ref[:, start : start + length]


def dot(left, right):
    return jnp.dot(left, right, preferred_element_type=f32)


def dot_nt(left, right, precision=None):
    return lax.dot_general(
        left, right, (((1,), (1,)), ((), ())), precision=precision, preferred_element_type=f32
    )


def dot_tn(left, right):
    return lax.dot_general(left, right, (((0,), (0,)), ((), ())), preferred_element_type=f32)


def joined(ref, start, rows_n, panels):
    return jnp.concatenate(
        [ref[start + p * rows_n : start + (p + 1) * rows_n, :] for p in range(panels)], axis=1
    )


def norm_stats(values):
    mean_val = jnp.mean(values, axis=-1, keepdims=True)
    centered = values - mean_val
    inv_std = lax.rsqrt(jnp.mean(centered * centered, axis=-1, keepdims=True) + norm_eps)
    return centered * inv_std, inv_std


def norm_back(values, gain, grad):
    unit, inv_std = norm_stats(values)
    scaled = grad * gain
    mean_s = jnp.mean(scaled, axis=-1, keepdims=True)
    mean_u = jnp.mean(scaled * unit, axis=-1, keepdims=True)
    back = inv_std * (scaled - mean_s - unit * mean_u)
    return (
        back,
        jnp.sum(grad * unit, axis=0, keepdims=True),
        jnp.sum(grad, axis=0, keepdims=True),
    )


def accumulate(ref, value):
    first = pl.program_id(0) == 0

    @pl.when(first)
    def _():
        ref[...] = value

    @pl.when(jnp.logical_not(first))
    def _():
        ref[...] += value


def stay(value):
    return pltpu.with_memory_space_constraint(value, pltpu.HBM)


def fence(*arrays):
    def nothing(*refs):
        pass

    anywhere = pl.BlockSpec(memory_space=pl.ANY)
    return pl.pallas_call(
        nothing,
        out_shape=[jax.ShapeDtypeStruct(a.shape, a.dtype) for a in arrays],
        in_specs=[anywhere] * len(arrays),
        out_specs=[anywhere] * len(arrays),
        input_output_aliases={i: i for i in range(len(arrays))},
    )(*[stay(a) if a.size > 32 * 1024 else a for a in arrays])


def gather_kernel(slots, count_a, count_b, owner, drow, dcol, flag, *refs):
    first = refs[:count_a]
    second = refs[count_a : count_a + count_b]
    *panels, vectors, held, sem, vec_sem = refs[count_a + count_b :]

    def copy_all(sources):
        at = 0
        for src in sources:
            for n in range(src.shape[0]):
                who = owner[at]
                at += 1

                def body(i, carried, src=src, n=n, who=who):
                    slot = who * slots + i
                    row = drow[slot]

                    @pl.when(row >= 0)
                    def _():
                        start = pl.multiple_of(i * BS, BS)
                        pltpu.make_async_copy(
                            src.at[n, pl.ds(start, BS), :],
                            held.at[
                                pl.ds(pl.multiple_of(row, BS), BS),
                                pl.ds(pl.multiple_of(dcol[slot], BS), BS),
                            ],
                            sem,
                        ).start()

                    return carried

                lax.fori_loop(0, slots, body, 0)
                pltpu.make_async_copy(
                    src.at[n, pl.ds(slots * BS, VEC_ROWS), :], vectors.at[who], vec_sem
                ).start()

    if count_b:

        @pl.when(flag[0] == 1)
        def _():
            copy_all(first)

        @pl.when(flag[0] == 0)
        def _():
            copy_all(second)
    else:
        copy_all(first)
    pltpu.make_async_copy(held, held, sem).wait()
    at = 0
    for panel in panels:
        size = panel.shape[0]
        pltpu.make_async_copy(held.at[pl.ds(at, size), :], panel, sem).start()
        at += size
    pltpu.make_async_copy(vectors, vectors, vec_sem).wait()
    pltpu.make_async_copy(held, held, sem).wait()


def gather_tiles(first, second, owner, drow, dcol, flag, slots, owners):
    anywhere = pl.BlockSpec(memory_space=pl.ANY)
    *panels, vectors = pl.pallas_call(
        functools.partial(gather_kernel, slots, len(first), len(second)),
        out_shape=[pltpu.HBM((size, HALF), bf16) for unused, unused2, size in WEIGHTS]
        + [jax.ShapeDtypeStruct((owners, VEC_ROWS, BS), bf16)],
        grid_spec=pltpu.PrefetchScalarGridSpec(
            num_scalar_prefetch=4,
            grid=(1,),
            in_specs=[anywhere] * (len(first) + len(second)),
            out_specs=[anywhere] * len(WEIGHTS) + [fixed((owners, VEC_ROWS, BS))],
            scratch_shapes=[
                pltpu.VMEM((PANEL_ROWS, HALF), bf16),
                pltpu.SemaphoreType.DMA,
                pltpu.SemaphoreType.DMA,
            ],
        ),
        compiler_params=params(),
        cost_estimate=cost(0, 4 * PANEL_ROWS * HALF),
    )(owner, drow, dcol, flag, *[stay(v) for v in first], *[stay(v) for v in second])
    return {(name, layer): p for (name, layer, unused), p in zip(WEIGHTS, panels)}, vectors


def scatter_kernel(rows_n, cols_n, steps, paired, parts, pos, part, own, *refs):
    @pl.when(part[1] > 0)
    def _():
        scatter_body(rows_n, cols_n, steps, paired, parts, pos, part, own, *refs)


def scatter_body(rows_n, cols_n, steps, paired, parts, pos, part, own, *refs):
    if paired:
        recv, *refs = refs
        span = pl.num_programs(0) // parts
        here = jnp.logical_or(parts == 1, pl.program_id(0) // span == part[0])
    target, buf, sems = refs[-3:]
    step = pl.program_id(0)
    slot = lax.rem(step, 2)
    per = rows_n // BS * (cols_n // BS)

    def wait(at):
        pltpu.make_async_copy(buf.at[at], buf.at[at], sems.at[at]).wait()

    @pl.when(step >= 2)
    def _():
        wait(slot)

    for i in range(rows_n // BS):
        for j in range(cols_n // BS):
            area = (slice(i * BS, (i + 1) * BS), slice(j * BS, (j + 1) * BS))
            value = own[area]
            if paired:
                more = jnp.where(here, recv[area].astype(f32), 0.0)
                value = (value.astype(f32) + more).astype(bf16)
            buf[slot, i * (cols_n // BS) + j] = value
    for n in range(per):
        pltpu.make_async_copy(
            buf.at[slot, n],
            target.at[pl.ds(pl.multiple_of(pos[step * per + n], 16), BS), :],
            sems.at[slot],
        ).start()

    @pl.when(step == pl.num_programs(0) - 1)
    def _():
        if steps > 1:
            wait(1 - slot)
        wait(slot)


def scatter_matrix(pos, own, recv, part, target, total_rows, rows_n):
    cols_n = own.shape[1]
    steps = own.shape[0] // rows_n
    anywhere = pl.BlockSpec(memory_space=pl.ANY)
    block = pl.BlockSpec((rows_n, cols_n), lambda i, *_: (i, 0))
    paired = recv is not None
    parts = own.shape[0] // recv.shape[0] if paired else 1
    span = steps // parts
    arrived = pl.BlockSpec(
        (rows_n, cols_n), lambda i, pos, part: (jnp.clip(i - part[0] * span, 0, span - 1), 0)
    )
    operands = [stay(own)] + ([stay(recv)] if paired else []) + ([] if target is None else [stay(target)])
    specs = [block] + ([block if parts == 1 else arrived] if paired else [])
    specs += [] if target is None else [anywhere]
    return pl.pallas_call(
        functools.partial(scatter_kernel, rows_n, cols_n, steps, paired, parts),
        out_shape=pltpu.HBM((total_rows, BS), bf16),
        grid_spec=pltpu.PrefetchScalarGridSpec(
            num_scalar_prefetch=2,
            grid=(steps,),
            in_specs=specs,
            out_specs=anywhere,
            scratch_shapes=[
                pltpu.VMEM((2, rows_n // BS * (cols_n // BS), BS, BS), bf16),
                pltpu.SemaphoreType.DMA((2,)),
            ],
        ),
        input_output_aliases={} if target is None else {len(operands) + 1: 0},
        compiler_params=params(),
        cost_estimate=cost(own.size, own.size * 6),
    )(pos, part, *operands)


def half_sum_kernel(part, own, arrived, out):
    out[...] = (own[...].astype(f32) + arrived[...].astype(f32)).astype(bf16)


def half_sum(part, own, arrived):
    block = arrived.shape
    return pl.pallas_call(
        half_sum_kernel,
        out_shape=pltpu.HBM(block, bf16),
        grid_spec=pltpu.PrefetchScalarGridSpec(
            num_scalar_prefetch=1,
            grid=(1,),
            in_specs=[pl.BlockSpec(block, lambda i, part: (part[0], 0)), fixed(block)],
            out_specs=fixed(block),
        ),
        compiler_params=params(),
        cost_estimate=cost(arrived.size, arrived.size * 6),
    )(part, stay(own), stay(arrived))


def half_copy_kernel(part, own, out):
    out[...] = own[...]


def other_half(part, own):
    block = (own.shape[0] // 2, own.shape[1])
    return pl.pallas_call(
        half_copy_kernel,
        out_shape=pltpu.HBM(block, bf16),
        grid_spec=pltpu.PrefetchScalarGridSpec(
            num_scalar_prefetch=1,
            grid=(1,),
            in_specs=[pl.BlockSpec(block, lambda i, part: (1 - part[0], 0))],
            out_specs=fixed(block),
        ),
        compiler_params=params(),
        cost_estimate=cost(0, own.size * 2),
    )(part, stay(own))


def scatter_vec_kernel(paired, pos, own, *refs):
    if paired:
        recv, *refs = refs
    target, buf, sem = refs[-3:]
    value = own[...]
    if paired:
        value = (value.astype(f32) + recv[...].astype(f32)).astype(bf16)
    buf[...] = value

    def body(n, carried):
        pltpu.make_async_copy(
            buf.at[n], target.at[pl.ds(pl.multiple_of(pos[n], 16), VEC_ROWS), :], sem
        ).start()
        return carried

    lax.fori_loop(0, own.shape[0], body, 0)
    pltpu.make_async_copy(buf, buf, sem).wait()


def scatter_vec(pos, own, recv, target):
    anywhere = pl.BlockSpec(memory_space=pl.ANY)
    block = fixed(own.shape)
    paired = recv is not None
    operands = [own] + ([recv] if paired else []) + [stay(target)]
    return pl.pallas_call(
        functools.partial(scatter_vec_kernel, paired),
        out_shape=pltpu.HBM(target.shape, bf16),
        grid_spec=pltpu.PrefetchScalarGridSpec(
            num_scalar_prefetch=1,
            grid=(1,),
            in_specs=[block] * (len(operands) - 1) + [anywhere],
            out_specs=anywhere,
            scratch_shapes=[pltpu.VMEM(own.shape, bf16), pltpu.SemaphoreType.DMA],
        ),
        input_output_aliases={len(operands): 0},
        compiler_params=params(),
    )(pos, *operands)


def expand_kernel(present, half, patch_ref, class_ref, pinv_ref, out, total):
    for block in range(patch_ref.shape[0] // ROWS):
        rows = slice(block * ROWS, (block + 1) * ROWS)
        total[...] = jnp.zeros_like(total)
        for which in range(3):

            @pl.when(present[block, which] > 0)
            def _(which=which, rows=rows):
                chosen = jnp.where(class_ref[rows, :] == which, patch_ref[rows, :].astype(f32), 0.0)
                total[...] += dot_nt(chosen.astype(bf16), pinv_ref[which])

        out[rows, :] = total[...].astype(bf16)


def expand_call(which, present, half, patches, class_col, pinv):
    tokens = patches.shape[0]
    size = BASE_PIX // CHUNKS
    step = size
    return pl.pallas_call(
        expand_kernel,
        out_shape=jax.ShapeDtypeStruct((tokens, size), bf16),
        grid_spec=pltpu.PrefetchScalarGridSpec(
            num_scalar_prefetch=2,
            grid=(1,),
            in_specs=[
                fixed(patches.shape),
                fixed(class_col.shape),
                pl.BlockSpec(
                    (3, step, pinv.shape[2]),
                    lambda i, present, half: (0, (which + half[0] * (CHUNKS // 2)) % CHUNKS, 0),
                ),
            ],
            out_specs=pl.BlockSpec((tokens, step), lambda i, *_: (0, i)),
            scratch_shapes=[pltpu.VMEM((ROWS, step), f32)],
        ),
        compiler_params=params(),
        cost_estimate=cost(3 * tokens * size * D, tokens * size * 4 + size * D * 6),
    )(present, half, patches, class_col, stay(pinv))


def resize_kernel(base, pinv_ref, out, turned):
    @pl.when(pl.program_id(0) == 0)
    def _():
        turned[...] = base[...].T

    out[0] = dot(turned[...], pinv_ref[0]).astype(bf16)


def resize_call(weights, pinv):
    return pl.pallas_call(
        resize_kernel,
        out_shape=jax.ShapeDtypeStruct((3, HALF, pinv.shape[2]), bf16),
        grid=(3,),
        in_specs=[
            fixed((BASE_PIX, HALF)),
            pl.BlockSpec((1, BASE_PIX, pinv.shape[2]), lambda i: (i, 0, 0)),
        ],
        out_specs=pl.BlockSpec((1, HALF, pinv.shape[2]), lambda i: (i, 0, 0)),
        scratch_shapes=[pltpu.VMEM((HALF, BASE_PIX), bf16)],
        compiler_params=params(),
        cost_estimate=cost(6 * D * BASE_PIX * HALF, 6 * D * BASE_PIX),
    )(stay(weights["base", 0]), stay(pinv))


def embed_back_kernel(core, base, own, recv, out, bias):
    low = (base[...] + (own[...].astype(f32) + recv[...].astype(f32))).astype(bf16)
    out[...] = low
    accumulate(bias, jnp.sum(low.astype(f32), axis=0, keepdims=True))


def embed_back_call(core, base, own, recv):
    tokens = base.shape[0]
    half = pl.BlockSpec((ROWS, HALF), lambda i, core: (i, core[0]))
    return pl.pallas_call(
        embed_back_kernel,
        out_shape=[
            jax.ShapeDtypeStruct((tokens, HALF), bf16),
            jax.ShapeDtypeStruct((1, HALF), f32),
        ],
        grid_spec=pltpu.PrefetchScalarGridSpec(
            num_scalar_prefetch=1,
            grid=(tokens // ROWS,),
            in_specs=[half] * 3,
            out_specs=[rows_spec(HALF), fixed((1, HALF))],
        ),
        compiler_params=params(),
        cost_estimate=cost(tokens * D, tokens * D * 5),
    )(core, base, own, recv)


def pack_kernel(vec_per, *refs):
    *pieces, out = refs
    out[...] = jnp.zeros_like(out)
    at = 0
    for piece in pieces:
        for k in range(piece.shape[1] // BS):
            owner, row = divmod(at, vec_per // BS)
            out[owner, row : row + 1, :] = piece[:, k * BS : (k + 1) * BS]
            at += 1


def pack_call(pieces, owners, vec_per):
    if vec_per % BS:
        joined = jnp.concatenate(pieces, axis=1)[0]
        joined = jnp.pad(joined, (0, owners * vec_per - joined.shape[0])).reshape(owners, vec_per)
        joined = jnp.pad(joined, ((0, 0), (0, VEC_ROWS * BS - vec_per)))
        return joined.astype(bf16).reshape(owners, VEC_ROWS, BS)
    return pl.pallas_call(
        functools.partial(pack_kernel, vec_per),
        out_shape=jax.ShapeDtypeStruct((owners, VEC_ROWS, BS), f32),
        grid=(1,),
        in_specs=[fixed(p.shape) for p in pieces],
        out_specs=fixed((owners, VEC_ROWS, BS)),
        compiler_params=params(),
        cost_estimate=cost(0, owners * vec_per * 8),
    )(*pieces).astype(bf16)


def embed_kernel(half, *refs):
    *parts, vec, weight, out = refs
    size = BASE_PIX // CHUNKS
    total = vec[:, :HALF]
    for c in range(CHUNKS):
        at = lax.rem(c + half[0] * (CHUNKS // 2), CHUNKS)
        rows = pl.ds(pl.multiple_of(at * size, size), size)
        total = total + dot(parts[c][...], weight[rows, :])
    out[...] = total.astype(bf16)


def embed_call(half, chunks, vec, weights):
    tokens = chunks[0].shape[0]
    return pl.pallas_call(
        embed_kernel,
        out_shape=jax.ShapeDtypeStruct((tokens, HALF), bf16),
        grid_spec=pltpu.PrefetchScalarGridSpec(
            num_scalar_prefetch=1,
            grid=(tokens // ROWS,),
            in_specs=[rows_spec(BASE_PIX // CHUNKS)] * CHUNKS
            + [fixed(vec.shape), fixed((BASE_PIX, HALF))],
            out_specs=rows_spec(HALF),
        ),
        compiler_params=params(),
        cost_estimate=cost(2 * tokens * BASE_PIX * HALF, tokens * BASE_PIX * 3),
    )(half, *[stay(c) for c in chunks], vec, stay(weights["base", 0]))


def qkv_kernel(layer, first, core, *refs):
    if first:
        own, recv, vec, weight, hid, normed, q_ref, k_ref, v_ref = refs
        mine, theirs = own[...].astype(f32), recv[...].astype(f32)
        low = core[0] == 0
        values = jnp.concatenate(
            [jnp.where(low, mine, theirs), jnp.where(low, theirs, mine)], axis=1
        )
    else:
        base, own, recv, vec, weight, hid, normed, q_ref, k_ref, v_ref = refs
        values = base[...] + (own[...].astype(f32) + recv[...].astype(f32))
    hid[...] = values
    unit, unused = norm_stats(values)
    low = (unit * vec_piece(vec, layer, "g1") + vec_piece(vec, layer, "s1")).astype(bf16)
    normed[...] = low
    made = dot(low, joined(weight, 0, D, 3))
    q_ref[...] = (made[:, :HALF] + vec_piece(vec, layer, "bq")).astype(bf16)
    k_ref[...] = made[:, HALF : 2 * HALF].astype(bf16)
    v_ref[...] = (made[:, 2 * HALF :] + vec_piece(vec, layer, "bv")).astype(bf16)


def qkv_call(layer, base, own, recv, core, vec, weights):
    tokens = own.shape[0]
    shape = lambda width, kind: jax.ShapeDtypeStruct((tokens, width), kind)
    outs = [shape(D, f32), pltpu.HBM((tokens, D), bf16)] + [shape(HALF, bf16)] * 3
    operands = ([] if base is None else [base]) + [own, recv]
    return pl.pallas_call(
        functools.partial(qkv_kernel, layer, base is None),
        out_shape=outs,
        grid_spec=pltpu.PrefetchScalarGridSpec(
            num_scalar_prefetch=1,
            grid=(tokens // ROWS,),
            in_specs=[rows_spec(o.shape[1]) for o in operands]
            + [fixed(vec.shape), fixed((3 * D, HALF))],
            out_specs=[rows_spec(o.shape[1]) for o in outs],
        ),
        compiler_params=params(),
        cost_estimate=cost(2 * tokens * D * 3 * HALF, tokens * D * 14),
    )(core, *operands, vec, weights["qkv", layer])


def head_masks():
    lane = lax.broadcasted_iota(jnp.int32, (1, 2 * HEAD_DIM), 1)
    low = (lane < HEAD_DIM).astype(f32).astype(bf16)
    high = (lane >= HEAD_DIM).astype(f32).astype(bf16)
    return low, high


def attend_kernel(
    layer, low_ref, high_ref, q_ref, k_ref, v_ref, seg_q, seg_k, vec, w_out, o_ref, lse_ref, part,
    scores_ref, top_ref, acc_ref,
):
    step = pl.program_id(0)
    first, last = low_ref[step], high_ref[step]
    masks = head_masks()
    scale = jnp.asarray(HEAD_DIM ** (-0.5), bf16)
    lane = lax.broadcasted_iota(jnp.int32, (1, BS), 1)
    sums = [(lane == HEAD_DIM).astype(f32).astype(bf16), (lane == 0).astype(f32).astype(bf16)]
    top_ref[...] = jnp.full(top_ref.shape, masked_score, f32)
    acc_ref[...] = jnp.zeros_like(acc_ref)
    seg_col = seg_q[...]

    def score_block(block, carried):
        rows = pl.ds(pl.multiple_of(block * ROWS, ROWS), ROWS)
        same = seg_col == seg_k[:, rows]
        for pair in range(HEADS // 2):
            cols = slice(pair * BS, (pair + 1) * BS)
            q_two = q_ref[:, cols] * scale
            k_two = k_ref[rows, cols]
            for side in range(2):
                head = 2 * pair + side
                scores = jnp.where(same, dot_nt(q_two * masks[side], k_two), masked_score)
                scores_ref[head, block] = scores
                top = top_ref[head]
                for piece in range(ROWS // BS):
                    top = jnp.maximum(top, scores[:, piece * BS : (piece + 1) * BS])
                top_ref[head] = top
        return carried

    lax.fori_loop(first, last, score_block, 0)
    tops = [jnp.max(top_ref[head], axis=1, keepdims=True) for head in range(HEADS)]

    def mix_block(block, carried):
        rows = pl.ds(pl.multiple_of(block * ROWS, ROWS), ROWS)
        for pair in range(HEADS // 2):
            v_two = v_ref[rows, pair * BS : (pair + 1) * BS]
            for side in range(2):
                head = 2 * pair + side
                expo = jnp.exp(scores_ref[head, block] - tops[head]).astype(bf16)
                acc_ref[head] += dot(expo, v_two * masks[side] + sums[side])
        return carried

    lax.fori_loop(first, last, mix_block, 0)
    totals = jnp.zeros((ROWS, BS), f32)
    for pair in range(HEADS // 2):
        sides = []
        for side in range(2):
            head = 2 * pair + side
            mixed = acc_ref[head]
            at = HEAD_DIM * (1 - side)
            total = mixed[:, at : at + 1]
            totals = jnp.where(lane == head, tops[head] + jnp.log(total), totals)
            sides.append(mixed * (1.0 / total))
        o_ref[:, pair * BS : (pair + 1) * BS] = jnp.where(lane < HEAD_DIM, *sides).astype(bf16)
    lse_ref[...] = totals.T[0:8, :]
    low = o_ref[...]
    bias = vec_piece(vec, layer, "bo")
    part[...] = (dot(low, joined(w_out, 0, HALF, TENSOR)) + bias).astype(bf16)


def attend_call(layer, first, last, queries, keys, values, seg_col, seg_row, vec, weights):
    tokens = queries.shape[0]
    return pl.pallas_call(
        functools.partial(attend_kernel, layer),
        out_shape=[
            jax.ShapeDtypeStruct((tokens, HALF), bf16),
            jax.ShapeDtypeStruct((8, tokens), f32),
            jax.ShapeDtypeStruct((tokens, D), bf16),
        ],
        grid_spec=pltpu.PrefetchScalarGridSpec(
            num_scalar_prefetch=2,
            grid=(tokens // ROWS,),
            in_specs=[
                rows_spec(HALF),
                fixed(keys.shape),
                fixed(values.shape),
                rows_spec(1),
                fixed(seg_row.shape),
                fixed(vec.shape),
                fixed((D, HALF)),
            ],
            out_specs=[
                rows_spec(HALF),
                pl.BlockSpec((8, ROWS), lambda i, *_: (0, i)),
                rows_spec(D),
            ],
            scratch_shapes=[
                pltpu.VMEM((HEADS, tokens // ROWS, ROWS, ROWS), f32),
                pltpu.VMEM((HEADS, ROWS, BS), f32),
                pltpu.VMEM((HEADS, ROWS, BS), f32),
            ],
        ),
        compiler_params=params(),
        cost_estimate=cost(8 * HEADS * tokens * tokens * BS, tokens * D * 8, HEADS * tokens * tokens),
    )(first, last, queries, keys, values, seg_col, seg_row, vec, weights["out", layer])


def gelu_parts(values):
    cdf = 0.5 * (1.0 + lax.erf(values * 0.7071067811865476))
    pdf = 0.3989422804014327 * jnp.exp(-0.5 * values * values)
    return values * cdf, cdf + values * pdf


def mlp_kernel(layer, base, own, recv, vec, w_up, w_down, hid, normed, act, slope, part):
    values = base[...] + (own[...].astype(f32) + recv[...].astype(f32))
    hid[...] = values
    unit, unused = norm_stats(values)
    low = (unit * vec_piece(vec, layer, "g2") + vec_piece(vec, layer, "s2")).astype(bf16)
    normed[...] = low
    bias_up = vec_piece(vec, layer, "b1")
    for pair in range(HALF_FF // D):
        area = slice(pair * D, (pair + 1) * D)
        up = dot(low, joined(w_up, pair * 2 * D, D, 2)) + bias_up[:, area]
        gelu, grad = gelu_parts(up)
        act[:, area] = gelu.astype(bf16)
        slope[:, area] = grad.astype(bf16)
    bias_down = vec_piece(vec, layer, "b2")
    part[...] = (dot(act[...], joined(w_down, 0, HALF_FF, TENSOR)) + bias_down).astype(bf16)


def mlp_call(layer, base, own, recv, vec, weights):
    tokens = base.shape[0]
    shape = lambda width, kind: jax.ShapeDtypeStruct((tokens, width), kind)
    kept = lambda width: pltpu.HBM((tokens, width), bf16)
    outs = [shape(D, f32), kept(D), kept(HALF_FF), kept(HALF_FF), shape(D, bf16)]
    return pl.pallas_call(
        functools.partial(mlp_kernel, layer),
        out_shape=outs,
        grid=(tokens // ROWS,),
        in_specs=[rows_spec(D)] * 3
        + [
            fixed(vec.shape),
            fixed((2 * HALF_FF, HALF)),
            fixed((2 * HALF_FF, HALF)),
        ],
        out_specs=[rows_spec(o.shape[1]) for o in outs],
        compiler_params=params(),
        cost_estimate=cost(4 * tokens * D * HALF_FF, tokens * D * 24, 2 * tokens * HALF_FF),
    )(base, own, recv, vec, weights["up", layer], weights["down", layer])


def mlp_back_kernel(layer, summed, *refs):
    if summed:
        base, own, recv, *refs = refs
        (hid, slope, vec, w_up, w_down, grad_full, grad_low, du_ref, back, dgain, dshift, db1, db2) = refs
        values = base[...].astype(f32) + (own[...].astype(f32) + recv[...].astype(f32))
        grad_full[...] = values
        low = values.astype(bf16)
    else:
        base, valid, *refs = refs
        (hid, slope, vec, w_up, w_down, grad_low, du_ref, back, dgain, dshift, db1, db2) = refs
        low = (base[...].astype(f32) * valid[...]).astype(bf16)
    grad_low[...] = low
    accumulate(db2, jnp.sum(low.astype(f32), axis=0, keepdims=True))
    for part in range(HALF_FF // D):
        area = slice(part * D, (part + 1) * D)
        rows = jnp.concatenate(
            [w_down[p * HALF_FF + part * D : p * HALF_FF + (part + 1) * D, :] for p in range(TENSOR)],
            axis=1,
        )
        du_ref[:, area] = (dot_nt(low, rows) * slope[:, area].astype(f32)).astype(bf16)
    grad_normed = dot_nt(du_ref[...], joined(w_up, 0, D, HALF_FF // HALF))
    accumulate(db1, jnp.sum(du_ref[...].astype(f32), axis=0, keepdims=True))
    part_back, gain_grad, shift_grad = norm_back(hid[...], vec_piece(vec, layer, "g2"), grad_normed)
    back[...] = part_back.astype(bf16)
    accumulate(dgain, gain_grad)
    accumulate(dshift, shift_grad)


def mlp_back_call(layer, base, own, recv, valid, hid, slope, vec, weights):
    tokens = base.shape[0]
    summed = own is not None
    shape = lambda width, kind: jax.ShapeDtypeStruct((tokens, width), kind)
    line = lambda width: jax.ShapeDtypeStruct((1, width), f32)
    outs = ([shape(D, f32)] if summed else []) + [shape(D, bf16), shape(HALF_FF, bf16), shape(D, bf16)]
    lines = [line(D), line(D), line(HALF_FF), line(D)]
    extra = [own, recv] if summed else [valid]
    return pl.pallas_call(
        functools.partial(mlp_back_kernel, layer, summed),
        out_shape=outs + lines,
        grid=(tokens // ROWS,),
        in_specs=[rows_spec(D)]
        + [rows_spec(e.shape[1]) for e in extra]
        + [
            rows_spec(D),
            rows_spec(HALF_FF),
            fixed(vec.shape),
            fixed((2 * HALF_FF, HALF)),
            fixed((2 * HALF_FF, HALF)),
        ],
        out_specs=[rows_spec(o.shape[1]) for o in outs] + [fixed(o.shape) for o in lines],
        compiler_params=params(),
        cost_estimate=cost(4 * tokens * D * HALF_FF, tokens * D * 24),
    )(base, *extra, stay(hid), stay(slope), vec, weights["up", layer], weights["down", layer])


def attend_back_kernel(
    low_ref, high_ref, base, own, recv, q_ref, k_ref, v_ref, o_ref, lse_ref, seg_k, seg_q, w_out,
    full_ref, grad_low, dq_ref, dk_ref, dv_ref, dbo, dk_acc, dv_acc, dq_acc, do_ref,
):
    step = pl.program_id(0)

    @pl.when(step == 0)
    def _():
        dk_acc[...] = jnp.zeros_like(dk_acc)
        dv_acc[...] = jnp.zeros_like(dv_acc)

    values = base[...].astype(f32) + (own[...].astype(f32) + recv[...].astype(f32))
    full_ref[...] = values
    low = values.astype(bf16)
    grad_low[...] = low
    accumulate(dbo, jnp.sum(low.astype(f32), axis=0, keepdims=True))
    do_ref[...] = dot_nt(low, joined(w_out, 0, HALF, TENSOR)).astype(bf16)
    product = do_ref[...].astype(f32) * o_ref[...].astype(f32)
    head = lax.broadcasted_iota(jnp.int32, (8, HALF), 0)
    lane = lax.broadcasted_iota(jnp.int32, (8, HALF), 1)
    pick = ((lane >= head * HEAD_DIM) & (lane < (head + 1) * HEAD_DIM)).astype(f32)
    high, rest = split(product)
    pick = pick.astype(bf16)
    inner = dot_nt(pick, high) + dot_nt(pick, rest)
    dq_acc[...] = jnp.zeros_like(dq_acc)
    masks = head_masks()
    scale = jnp.asarray(HEAD_DIM ** (-0.5), bf16)
    seg_row = seg_q[...]

    def one_block(block, carried):
        rows = pl.ds(pl.multiple_of(block * KEYS, KEYS), KEYS)
        same = seg_k[rows, :] == seg_row
        for pair in range(HEADS // 2):
            cols = slice(pair * BS, (pair + 1) * BS)
            q_two = q_ref[:, cols] * scale
            do_two = do_ref[:, cols]
            k_two = k_ref[rows, cols]
            v_two = v_ref[rows, cols]
            dv_two = dk_two = dq_two = None
            for side in range(2):
                at = 2 * pair + side
                q_one = q_two * masks[side]
                do_one = do_two * masks[side]
                scores = dot_nt(k_two, q_one)
                prob = jnp.where(same, jnp.exp(scores - lse_ref[at : at + 1, :]), 0.0)
                grad_prob = dot_nt(v_two, do_one)
                grad_scores = (prob * (grad_prob - inner[at : at + 1, :])).astype(bf16)
                dv_one = dot(prob.astype(bf16), do_one)
                dk_one = dot(grad_scores, q_one)
                dq_one = dot_tn(grad_scores, k_two * masks[side])
                dq_two = dq_one if dq_two is None else dq_two + dq_one
                dv_two = dv_one if dv_two is None else dv_two + dv_one
                dk_two = dk_one if dk_two is None else dk_two + dk_one
            dv_acc[rows, cols] += dv_two
            dk_acc[rows, cols] += dk_two
            dq_acc[:, cols] += dq_two
        return carried

    lax.fori_loop(low_ref[step], high_ref[step], one_block, 0)
    dq_ref[...] = (dq_acc[...] * HEAD_DIM ** (-0.5)).astype(bf16)

    @pl.when(step == pl.num_programs(0) - 1)
    def _():
        dk_ref[...] = dk_acc[...].astype(bf16)
        dv_ref[...] = dv_acc[...].astype(bf16)


def attend_back_call(
    layer, first, last, base, own, recv, queries, keys, values, mixed, lse, seg_col, seg_row, weights
):
    tokens = base.shape[0]
    shape = lambda width, kind: jax.ShapeDtypeStruct((tokens, width), kind)
    whole = (tokens, HALF)
    return pl.pallas_call(
        attend_back_kernel,
        out_shape=[
            shape(D, f32),
            shape(D, bf16),
            shape(HALF, bf16),
            shape(HALF, bf16),
            shape(HALF, bf16),
            jax.ShapeDtypeStruct((1, D), f32),
        ],
        grid_spec=pltpu.PrefetchScalarGridSpec(
            num_scalar_prefetch=2,
            grid=(tokens // ROWS,),
            in_specs=[
                rows_spec(D),
                rows_spec(D),
                rows_spec(D),
                rows_spec(HALF),
                fixed(whole),
                fixed(whole),
                rows_spec(HALF),
                pl.BlockSpec((8, ROWS), lambda i, *_: (0, i)),
                fixed(seg_col.shape),
                pl.BlockSpec((1, ROWS), lambda i, *_: (0, i)),
                fixed((D, HALF)),
            ],
            out_specs=[
                rows_spec(D),
                rows_spec(D),
                rows_spec(HALF),
                fixed(whole),
                fixed(whole),
                fixed((1, D)),
            ],
            scratch_shapes=[
                pltpu.VMEM(whole, f32),
                pltpu.VMEM(whole, f32),
                pltpu.VMEM((ROWS, HALF), f32),
                pltpu.VMEM((ROWS, HALF), bf16),
            ],
        ),
        compiler_params=params(),
        cost_estimate=cost(14 * HEADS * tokens * tokens * BS, tokens * D * 20, HEADS * tokens * tokens),
    )(
        first, last, base, own, recv, stay(queries), stay(keys), stay(values), stay(mixed), lse,
        seg_col, seg_row, weights["out", layer],
    )


def qkv_back_kernel(layer, dq, dk, dv, hid, vec, weight, back, dgain, dshift, dbq, dbv):
    grad_three = jnp.concatenate([dq[...], dk[...], dv[...]], axis=1)
    grad_normed = dot_nt(grad_three, joined(weight, 0, D, 3))
    part_back, gain_grad, shift_grad = norm_back(hid[...], vec_piece(vec, layer, "g1"), grad_normed)
    back[...] = part_back.astype(bf16)
    accumulate(dgain, gain_grad)
    accumulate(dshift, shift_grad)
    accumulate(dbq, jnp.sum(dq[...].astype(f32), axis=0, keepdims=True))
    accumulate(dbv, jnp.sum(dv[...].astype(f32), axis=0, keepdims=True))


def qkv_back_call(layer, dq, dk, dv, hid, vec, weights):
    tokens = dq.shape[0]
    line = lambda width: jax.ShapeDtypeStruct((1, width), f32)
    lines = [line(D), line(D), line(HALF), line(HALF)]
    return pl.pallas_call(
        functools.partial(qkv_back_kernel, layer),
        out_shape=[jax.ShapeDtypeStruct((tokens, D), bf16)] + lines,
        grid=(tokens // ROWS,),
        in_specs=[rows_spec(HALF)] * 3
        + [
            rows_spec(D),
            fixed(vec.shape),
            fixed((3 * D, HALF)),
        ],
        out_specs=[rows_spec(D)] + [fixed(o.shape) for o in lines],
        compiler_params=params(),
        cost_estimate=cost(2 * tokens * D * 3 * HALF, tokens * D * 10),
    )(dq, dk, dv, stay(hid), vec, weights["qkv", layer])


def split(values):
    high = values.astype(bf16)
    return high, (values - high.astype(f32)).astype(bf16)


def product(left, right, left_dim, right_dim):
    def one(a, b):
        return lax.dot_general(
            a, b, (((left_dim,), (right_dim,)), ((), ())), preferred_element_type=f32
        )

    return one(left[0], right[0]) + (one(left[0], right[1]) + one(left[1], right[0]))


def owner_kernel(per, used, home, near, far, master, left, right, moment, variance, grad, out, out_mom, out_var):
    here = range(per)
    first = pl.program_id(0) * per
    lefts = [split(left[i]) for i in here]
    rights = [split(right[i]) for i in here]
    rotated = []
    for i in here:
        rows = slice(i * BS, (i + 1) * BS)
        tile = jnp.where(home[0] > 0, near[rows, :].astype(f32), far[rows, :].astype(f32))
        tile = jnp.where(used[first + i] > 0, tile, 0.0)
        grad[i] = tile
        tile = tile.astype(bf16)
        rotated.append(split(dot_tn(lefts[i][0], tile) + dot_tn(lefts[i][1], tile)))
    rotated = [product(rotated[i], rights[i], 1, 0) for i in here]
    steps = []
    for i in here:
        new_moment = decay * moment[i] + (1.0 - decay) * rotated[i]
        new_variance = decay * variance[i] + (1.0 - decay) * rotated[i] * rotated[i]
        out_mom[i] = new_moment
        out_var[i] = new_variance
        steps.append(split(new_moment / (jnp.sqrt(new_variance) + adam_eps)))
    returned = [split(product(lefts[i], steps[i], 1, 0)) for i in here]
    returned = [product(returned[i], rights[i], 1, 1) for i in here]
    for i in here:
        out[i] = master[i] - matrix_rate * returned[i]


def owner_call(used, home, near, far, *arrays):
    count = arrays[0].shape[0]
    per = min(8, count)
    block = pl.BlockSpec((per, BS, BS), lambda i, *_: (i, 0, 0))
    return pl.pallas_call(
        functools.partial(owner_kernel, per),
        out_shape=[jax.ShapeDtypeStruct(arrays[0].shape, f32)] * 4,
        grid_spec=pltpu.PrefetchScalarGridSpec(
            num_scalar_prefetch=2,
            grid=(count // per,),
            in_specs=[pl.BlockSpec((per * BS, BS), lambda i, *_: (i, 0))] * 2 + [block] * 5,
            out_specs=[block] * 4,
        ),
        compiler_params=params(),
        cost_estimate=cost(count * 88 * BS**3, count * BS * BS * 38),
    )(used, home, stay(near), stay(far), *[stay(a) for a in arrays])


def reduce_kernel(carrying, last, *refs):
    block, arrived, *refs = refs
    total = block[...].astype(f32) + arrived[...].astype(f32)
    if carrying:
        carried, *refs = refs
        total = total + carried[...].astype(f32)
    if last:
        [out] = refs
    else:
        following, out, later = refs
        later[...] = following[...]
    out[...] = total.astype(bf16)


def reduce_call(j, n, buffer, arrived, carried, payload):
    last = j == 3
    at = lambda j, x_rel: pl.BlockSpec((payload, BS), lambda i: ((j * 2 + x_rel) * 2 + n, 0))
    whole = fixed((payload, BS))
    operands = [stay(buffer), stay(arrived)] + ([] if carried is None else [stay(carried)])
    specs = [at(j, 0)] + [whole] * (len(operands) - 1)
    if not last:
        operands.append(stay(buffer))
        specs.append(at(j + 1, 1))
    outs = [pltpu.HBM((payload, BS), bf16)] * (1 if last else 2)
    made = pl.pallas_call(
        functools.partial(reduce_kernel, carried is not None, last),
        out_shape=outs,
        grid=(1,),
        in_specs=specs,
        out_specs=[whole] * len(outs),
        compiler_params=params(),
        cost_estimate=cost(payload * BS * 3, payload * BS * 12),
    )(*operands)
    return (made[0], None) if last else made


class Routes:
    def __init__(self, dp_n):
        pairs = [(d, t) for d in range(dp_n) for t in range(TENSOR)]
        at = lambda d, t: d * TENSOR + t
        home = [(d, t) for d, t in pairs if d % 2 == t]
        away = [(d, t) for d, t in pairs if d % 2 != t]
        self.core_all = [(at(d, t), at(d ^ 1, t)) for d, t in pairs]
        self.core_out = [(at(d, t), at(d ^ 1, t)) for d, t in home]
        self.core_in = [(at(d, t), at(d ^ 1, t)) for d, t in away]
        self.y_all = [(at(d, t), at(d, 1 - t)) for d, t in pairs]
        self.y_out = [(at(d, t), at(d, 1 - t)) for d, t in home]
        self.y_in = [(at(d, t), at(d, 1 - t)) for d, t in away]
        self.x_home = [(at(d, t), at(d ^ 2, t)) for d, t in home]
        self.x_away = [(at(d, t), at(d ^ 2, t)) for d, t in away]
        self.z_all = [(at(d, t), at((d + 4) % dp_n, t)) for d, t in pairs]
        self.z_home = [(at(d, t), at((d + 4) % dp_n, t)) for d, t in home]


def send(value, route):
    return lax.ppermute(value, AXES, route)


def shards(
    patches,
    cotangent,
    image_size,
    block_slot,
    pinv,
    master_slots,
    left_basis,
    right_basis,
    mom_slots,
    var_slots,
    vec_master,
    vec_mom,
    vec_var,
):
    dp_n = lax.axis_size("dp")
    dp_pos = lax.axis_index("dp")
    y_pos = lax.axis_index("tensor")
    core = dp_pos % 2
    home = core == y_pos
    routes = Routes(dp_n)
    grid3 = dp_n == 16
    x_pos = (dp_pos // 2) % 2
    half_at = (x_pos if grid3 else x_pos * 0).astype(jnp.int32).reshape(1)
    tokens_n = patches.shape[0]
    slots_per = master_slots.shape[1]
    vec_per = vec_master.shape[1]
    slots_n = slots_per * dp_n
    payload = slots_per * BS + VEC_ROWS

    patches = jnp.where(home, patches, send(patches, routes.core_out))
    cotangent = jnp.where(home, cotangent, send(cotangent, routes.core_out))
    size_row = jnp.where(home, image_size, send(image_size, routes.core_out))[0]
    own_slots = block_slot[0]
    slot_other = send(block_slot, routes.y_all)

    lengths = jnp.where(
        size_row == 0, LEN_A, jnp.where(size_row == 1, LEN_B, jnp.where(size_row == 2, LEN_C, 0))
    )
    order = jnp.arange(IMG_DEV)
    ends_at = jnp.sum(jnp.where(order[None, :] <= order[:, None], lengths[None, :], 0), axis=1)
    places = jnp.arange(tokens_n)
    segment = jnp.sum((places[:, None] >= ends_at[None, :]).astype(jnp.int32), axis=1)
    in_image = segment[:, None] == order[None, :]
    select = jnp.stack(
        [jnp.any(in_image & (size_row == s)[None, :], axis=1) for s in range(3)], axis=1
    )
    valid_col = (segment < IMG_DEV).astype(f32)[:, None]
    seg_col = segment[:, None]
    seg_row = segment[None, :]
    blocks_n = tokens_n // ROWS
    starts = jnp.arange(blocks_n) * ROWS
    begun = ends_at[None, :] <= starts[:, None]
    first_tok = jnp.max(jnp.where(begun, ends_at[None, :], 0), axis=1)
    after = ends_at[None, :] > (starts + ROWS - 1)[:, None]
    last_tok = jnp.min(jnp.where(after, ends_at[None, :], tokens_n), axis=1)
    first_blk = (first_tok // ROWS).astype(jnp.int32)
    last_blk = ((last_tok + ROWS - 1) // ROWS).astype(jnp.int32)
    first_key = (first_tok // KEYS).astype(jnp.int32)
    last_key = ((last_tok + KEYS - 1) // KEYS).astype(jnp.int32)

    select_low = select.astype(bf16)
    class_col = jnp.sum(jnp.where(select, jnp.arange(1, 4)[None, :], 0), axis=1, keepdims=True) - 1
    present = jnp.any(select.reshape(blocks_n, ROWS, 3), axis=1).astype(jnp.int32)

    def expand(which):
        return expand_call(which, present, half_at, patches, class_col, pinv)

    vec_low = jnp.pad(vec_master[0].astype(bf16), (0, VEC_ROWS * BS - vec_per))
    own_pack = jnp.concatenate(
        [
            master_slots[0].astype(bf16).reshape(slots_per * BS, BS),
            vec_low.reshape(VEC_ROWS, BS),
        ],
        axis=0,
    )
    flag = home.astype(jnp.int32).reshape(1)
    if grid3:
        z_pos = dp_pos // 4
        packs = [[own_pack], [send(own_pack, routes.core_in)]]
        across, over_y, corner = [[], []], [[], []], [[], []]
        token = jnp.zeros((8, BS), f32)
        chunks = []
        for j in range(5):
            for n in range(2):
                moved = {}
                if j < 3:
                    moved["x"] = send(packs[n][j], routes.x_home)
                    moved["y"] = send(packs[n][j], routes.y_out)
                if j:
                    source, route = (across, routes.y_out) if n == 0 else (over_y, routes.x_away)
                    moved["corner"] = send(source[n][j - 1], route)
                if j < 3:
                    moved["z"] = send(packs[n][j], routes.z_home)
                if j == 3:
                    ring = jnp.where(home, across[n][2], over_y[n][2])
                    moved["x"] = moved["y"] = send(ring, routes.z_all)
                work = []
                if j + n == 0:
                    work = [slot_other]
                if 1 <= 2 * j + n <= CHUNKS:
                    work = [expand(2 * j + n - 1)]
                if j < 4:
                    keys_here = [k for k in moved if k != "y" or j < 3]
                    token, *made = fence(token, *[moved[k] for k in keys_here], *work)
                    if j + n == 0:
                        slot_other = made.pop()
                    elif work:
                        chunks.append(made.pop())
                    moved = dict(zip(keys_here, made))
                    across[n].append(moved["x"])
                    over_y[n].append(moved["y"] if j < 3 else moved["x"])
                if j < 3:
                    packs[n].append(moved["z"])
                if j:
                    corner[n].append(moved["corner"])
        first, second, owner = [], [], []
        for j in range(4):
            first += [packs[0][j], packs[1][j], across[0][j], across[1][j]]
            second += [over_y[0][j], over_y[1][j], corner[0][j], corner[1][j]]
            for x_rel in range(2):
                for n in range(2):
                    owner.append(((z_pos - j) % 4) * 4 + (x_pos ^ x_rel) * 2 + (core ^ n))
        first = [v[None] for v in first]
        second = [v[None] for v in second]
        owner = jnp.stack(owner).astype(jnp.int32)
    else:
        everything = lax.all_gather(own_pack, AXES, axis=0)
        everything = everything.reshape(dp_n, TENSOR, payload, BS)
        first = [jnp.where(core == 0, everything[:, 0], everything[:, 1])]
        second = []
        owner = jnp.arange(dp_n, dtype=jnp.int32)
        chunks = [expand(c) for c in range(CHUNKS)]
    slot_list = jnp.where(home, block_slot, slot_other)[0]
    named = slot_list[None, :] == jnp.arange(slots_n)[:, None]
    used = jnp.any(named, axis=1)
    drow = jnp.where(used, jnp.sum(jnp.where(named, TARGET_ROW[None, :], 0), axis=1), -1)
    dcol = jnp.sum(jnp.where(named, TARGET_COL[None, :], 0), axis=1)
    weights, vec_rows = gather_tiles(first, second, owner, drow, dcol, flag, slots_per, dp_n)
    vec = vec_rows.reshape(dp_n, VEC_ROWS * BS)[:, :vec_per].astype(f32).reshape(1, dp_n * vec_per)

    embedded = embed_call(half_at, chunks, vec, weights)
    embedded_other = send(embedded, routes.core_all)
    core_flag = core.astype(jnp.int32).reshape(1)

    caches = []
    hidden, own, recv = None, embedded, embedded_other
    for layer in range(LAYERS):
        hidden, normed, queries, keys, values = qkv_call(
            layer, hidden, own, recv, core_flag, vec, weights
        )
        mixed, lse, part = attend_call(
            layer, first_blk, last_blk, queries, keys, values, seg_col, seg_row, vec, weights
        )
        other = send(part, routes.core_all)
        middle, normed2, act, slope, own = mlp_call(layer, hidden, part, other, vec, weights)
        recv = send(own, routes.core_all)
        caches.append((hidden, normed, queries, keys, values, mixed, lse, middle, normed2, act, slope))
        hidden = middle
    out_low = ((hidden + (own.astype(f32) + recv.astype(f32))) * valid_col).astype(bf16)

    owners = jnp.arange(dp_n)
    if grid3:
        place = (
            ((z_pos - 1 - owners // 4) % 4) * 4
            + (x_pos ^ ((owners // 2) % 2)) * 2
            + (core ^ (owners % 2))
        ).astype(jnp.int32)
    else:
        place = owners.astype(jnp.int32)
    slot_owner = slot_list // slots_per
    owner_place = jnp.sum(
        jnp.where(slot_owner[:, None] == owners[None, :], place[None, :], 0), axis=1
    )
    tile_pos = (owner_place * payload + (slot_list % slots_per) * BS).astype(jnp.int32)
    vec_pos = (place * payload + slots_per * BS).astype(jnp.int32)
    total_rows = dp_n * payload
    where_to = jnp.concatenate([half_at, flag if grid3 else flag * 0 + 1])
    offsets = {"base": 0}
    count = BASE_PIX // BS * (HALF // BS)
    for layer in range(LAYERS):
        for name, size in (("qkv", 3 * D * HALF), ("out", D * HALF), ("up", D * HALF_FF), ("down", D * HALF_FF)):
            offsets[name, layer] = count
            count += size // (BS * BS)

    def place_tiles(key, matrix, arrived, buffer):
        tiles = matrix.size // (BS * BS)
        pos = tile_pos[offsets[key] : offsets[key] + tiles]
        rows_n = matrix.shape[0] // 2 if matrix.shape[0] > HALF else HALF
        return scatter_matrix(pos, matrix, arrived, where_to, buffer, total_rows, rows_n)

    def place_base(rel, matrix, arrived, buffer):
        size = BASE_PIX * HALF // (BS * BS) // 2
        low_pos, high_pos = tile_pos[:size], tile_pos[size : 2 * size]
        pos = jnp.where(half_at[0] == rel, low_pos, high_pos)
        return scatter_matrix(pos, matrix, arrived, where_to, buffer, total_rows, D)

    def over(matrix):
        return send(matrix, routes.y_in) if grid3 else None

    def beside(matrix):
        return send(other_half(half_at, matrix), routes.x_away) if grid3 else None

    def summed(matrix, arrived):
        return half_sum(half_at, matrix, arrived) if grid3 else None

    def hold(*arrays):
        kept = [a for a in arrays if a is not None]
        done = iter(fence(*kept))
        return [None if a is None else next(done) for a in arrays]

    top, low = 1, 0
    vec_grads = [None] * LAYERS

    def mlp_step(layer, grad, own, recv):
        middle, normed2, act, slope = caches[layer][7:11]
        made = mlp_back_call(layer, grad, own, recv, valid_col, middle, slope, vec, weights)
        if own is not None:
            return made
        return [made[0]] + list(made)

    def attend_step(layer, grad, part, other, lse):
        hid_in, normed, queries, keys, values, mixed = caches[layer][:6]
        return attend_back_call(
            layer, first_key, last_key, grad, part, other, queries, keys, values, mixed, lse,
            seg_col, seg_row, weights,
        )

    grad, grad_low, du, part, dg2, ds2, db1, db2 = mlp_step(top, cotangent, None, None)
    other = send(part, routes.core_all)
    gd1 = dot_tn(caches[top][9], grad_low).astype(bf16)
    gu1 = dot_tn(caches[top][8], du).astype(bf16)
    lse, gd1, gu1, out_low = fence(caches[top][6], gd1, gu1, out_low)
    ad1 = over(gd1)
    grad, grad_low, dq, dk, dv, dbo = attend_step(top, grad, part, other, lse)
    vec, dbo, ad1, gu1 = hold(vec, dbo, ad1, gu1)
    au1 = over(gu1)
    own, dg1, ds1, dbq, dbv = qkv_back_call(top, dq, dk, dv, caches[top][0], vec, weights)
    recv = send(own, routes.core_all)
    go1 = dot_tn(caches[top][5], grad_low).astype(bf16)
    gq1 = dot_tn(caches[top][1], jnp.concatenate([dq, dk, dv], axis=1)).astype(bf16)
    vec_grads[top] = [dg1, ds1, dbq, dbv, dbo, dg2, ds2, db1, db2]
    grad, grad_low, du, part, dg2, ds2, db1, db2 = mlp_step(low, grad, own, recv)
    other = send(part, routes.core_all)
    db2, au1, go1, gq1 = hold(db2, au1, go1, gq1)
    xq1, ao1 = beside(gq1), over(go1)
    gd0 = dot_tn(caches[low][9], grad_low).astype(bf16)
    gu0 = dot_tn(caches[low][8], du).astype(bf16)
    lse, gd0, gu0, xq1, ao1 = hold(caches[low][6], gd0, gu0, xq1, ao1)
    aq1 = over(summed(gq1, xq1))
    ad0 = over(gd0)
    xu0 = beside(gu0)
    buffer = place_tiles(("down", top), gd1, ad1, None)
    buffer = place_tiles(("up", top), gu1, au1, buffer)
    grad, grad_low, dq, dk, dv, dbo = attend_step(low, grad, part, other, lse)
    vec, dbo, aq1, xu0, buffer = hold(vec, dbo, aq1, xu0, buffer)
    au0 = over(summed(gu0, xu0))
    own, dg1, ds1, dbq, dbv = qkv_back_call(low, dq, dk, dv, caches[low][0], vec, weights)
    recv = send(own, routes.core_all)
    gq0 = dot_tn(caches[low][1], jnp.concatenate([dq, dk, dv], axis=1)).astype(bf16)
    vec_grads[low] = [dg1, ds1, dbq, dbv, dbo, dg2, ds2, db1, db2]
    xq0 = beside(gq0)
    grad_emb, grad_emb_bias = embed_back_call(core_flag, grad, own, recv)
    middle = CHUNKS // 2

    def base_grad(parts):
        return jnp.concatenate([dot_tn(c, grad_emb).astype(bf16) for c in parts], axis=0)

    gbt = base_grad(chunks[middle:])
    gbt, ad0, au0, xq0 = hold(gbt, ad0, au0, xq0)
    xb = send(gbt, routes.x_away) if grid3 else None
    aq0 = over(summed(gq0, xq0))
    gbm = base_grad(chunks[:middle])
    vec_grad = pack_call([grad_emb_bias] + vec_grads[0] + vec_grads[1], dp_n, vec_per)
    go0 = dot_tn(caches[low][5], grad_low).astype(bf16)
    ao0, av = over(go0), over(vec_grad)
    gbm, xb, aq0, ao0, av, buffer = hold(gbm, xb, aq0, ao0, av, buffer)
    ab = over(half_sum(half_at * 0, gbm, xb)) if grid3 else None
    buffer = place_tiles(("out", top), go1, ao1, buffer)
    buffer = place_tiles(("qkv", top), gq1, aq1, buffer)
    buffer = place_tiles(("down", low), gd0, ad0, buffer)
    buffer = place_tiles(("up", low), gu0, au0, buffer)
    buffer = place_base(1, gbt, None, buffer)
    buffer = place_tiles(("out", low), go0, ao0, buffer)
    buffer = scatter_vec(vec_pos, vec_grad, av, buffer)
    buffer = place_tiles(("qkv", low), gq0, aq0, buffer)
    base_weight = weights["base", 0]
    ab, buffer, base_weight, out_low = hold(ab, buffer, base_weight, out_low)
    weights["base", 0] = base_weight
    buffer = place_base(0, gbm, ab, buffer)

    if grid3:
        token = jnp.zeros((8, BS), f32)
        order = (1, 0)
        resized = resize_call(weights, pinv)
        carried = {n: None for n in order}
        across = {n: send(buffer.reshape(4, 2, 2, payload, BS)[0, 1, n], routes.x_home) for n in order}
        rounded = {}
        for j in range(4):
            for n in order:
                extra = None
                if j == 0 and n == order[0]:
                    extra = resized
                token, across[n], carried[n], extra = hold(token, across[n], carried[n], extra)
                if extra is not None:
                    resized = extra
                total, later = reduce_call(j, n, buffer, across[n], carried[n], payload)
                if j < 3:
                    carried[n] = send(total, routes.z_home)
                    across[n] = send(later, routes.x_home)
                else:
                    rounded[n] = total
        near_grad, far_grad = rounded[0], send(rounded[1], routes.core_out)
    else:
        held = buffer.reshape(dp_n, 1, payload, BS).astype(f32)
        nothing = jnp.zeros_like(held)
        both = jnp.concatenate(
            [jnp.where(core == 0, held, nothing), jnp.where(core == 0, nothing, held)], axis=1
        )
        used_rows = jnp.repeat(used, BS).reshape(dp_n, 1, slots_per * BS, 1)
        used_rows = jnp.concatenate(
            [used_rows, jnp.ones((dp_n, 1, VEC_ROWS, 1), bool)], axis=2
        )
        both = jnp.where(used_rows, both, 0.0).reshape(dp_n * TENSOR * payload, BS)
        near_grad = lax.psum_scatter(both, AXES, scatter_dimension=0, tiled=True).astype(bf16)
        far_grad = near_grad
        resized = resize_call(weights, pinv)

    output = jnp.where(home, out_low, send(out_low, routes.y_out)).astype(f32)
    grad_pixels = sum(
        dot(grad_emb * select_low[:, s : s + 1], resized[s]) for s in range(3)
    ).astype(bf16)
    pixels_other = send(grad_pixels, routes.core_all)
    pixel_sides = [
        grad_pixels[:, s * HALF : (s + 1) * HALF].astype(f32)
        + pixels_other[:, s * HALF : (s + 1) * HALF].astype(f32)
        for s in range(TENSOR)
    ]
    near = jnp.where(core == 0, pixel_sides[0], pixel_sides[1])
    far = jnp.where(core == 0, pixel_sides[1], pixel_sides[0]).astype(bf16)
    patch_grad = jnp.where(home, near, send(far, routes.y_out).astype(f32))

    my_slots = dp_pos * slots_per + jnp.arange(slots_per)
    mine_used = jnp.any(own_slots[None, :] == my_slots[:, None], axis=1).astype(jnp.int32)
    owned_grad, new_master, new_mom, new_var = owner_call(
        mine_used, flag, near_grad, far_grad, master_slots[0], left_basis[0], right_basis[0], mom_slots[0], var_slots[0]
    )
    vec_rows = jnp.where(home, near_grad[slots_per * BS :], far_grad[slots_per * BS :])
    owned_vec_grad = vec_rows.astype(f32).reshape(VEC_ROWS * BS)[:vec_per]
    new_vec_mom = decay * vec_mom[0] + (1.0 - decay) * owned_vec_grad
    new_vec_var = decay * vec_var[0] + (1.0 - decay) * owned_vec_grad * owned_vec_grad
    new_vec = vec_master[0] - vector_rate * new_vec_mom / (jnp.sqrt(new_vec_var) + adam_eps)
    return (
        output,
        patch_grad,
        owned_grad[None],
        new_master[None],
        new_mom[None],
        new_var[None],
        owned_vec_grad[None],
        new_vec[None],
        new_vec_mom[None],
        new_vec_var[None],
    )


def solution(mesh):
    slots = P("tensor", "dp", None, None)
    vectors = P("tensor", "dp")
    tokens = P("dp", None)
    in_specs = (tokens, tokens, tokens, P("tensor", None), P()) + (slots,) * 5 + (vectors,) * 3
    out_specs = (tokens, P("dp", "tensor")) + (slots,) * 4 + (vectors,) * 4
    return jax.shard_map(shards, mesh=mesh, in_specs=in_specs, out_specs=out_specs, check_vma=False)
```

```python
import functools

import jax
import jax.numpy as jnp
import numpy as np
from jax import lax
from jax.experimental import pallas as pl
from jax.experimental.pallas import tpu as pltpu
from jax.sharding import PartitionSpec as P

D = 768
HEAD_DIM = 64
FF = 3072
BASE_PIX = 3072
LAYERS = 2
LEN_A = 196
LEN_B = 225
LEN_C = 576
IMG_DEV = 5
BS = 128
TENSOR = 2
HALF = D // TENSOR
HALF_FF = FF // TENSOR
HEADS = HALF // HEAD_DIM
ROWS = 256
KEYS = 512
VEC_ROWS = 16
CHUNKS = 4

AXES = ("dp", "tensor")
precise = lax.Precision.HIGHEST
masked_score = -1e30
norm_eps = 1e-06
adam_eps = 1e-08
decay = 0.5
matrix_rate = 0.05
vector_rate = 0.3
f32 = jnp.float32
bf16 = jnp.bfloat16
MIB = 1024 * 1024

WEIGHTS = [("base", 0, BASE_PIX)]
for layer in range(LAYERS):
    WEIGHTS += [("qkv", layer, 3 * D), ("out", layer, D), ("up", layer, FF), ("down", layer, FF)]
STARTS = {}
PANEL_ROWS = 0
for name, layer, size in WEIGHTS:
    STARTS[name, layer] = PANEL_ROWS
    PANEL_ROWS += size


def tile_targets():
    rows, cols = [], []

    def add(start, rows_n, cols_n):
        for i in range(rows_n // BS):
            for j in range(cols_n // BS):
                panel, inner = divmod(j * BS, HALF)
                rows.append(start + panel * rows_n + i * BS)
                cols.append(inner)

    add(STARTS["base", 0], BASE_PIX, HALF)
    for layer in range(LAYERS):
        add(STARTS["qkv", layer], D, 3 * HALF)
        add(STARTS["out", layer], HALF, D)
        add(STARTS["up", layer], D, HALF_FF)
        add(STARTS["down", layer], HALF_FF, D)
    return np.array(rows, np.int32), np.array(cols, np.int32)


TARGET_ROW, TARGET_COL = tile_targets()
LAYER_VECS = (D, D, HALF, HALF, D, D, D, HALF_FF, D)
VEC_NAMES = ("g1", "s1", "bq", "bv", "bo", "g2", "s2", "b1", "b2")


def vec_offsets():
    offset = HALF
    found = []
    for layer in range(LAYERS):
        here = {}
        for name, length in zip(VEC_NAMES, LAYER_VECS):
            here[name] = (offset, length)
            offset += length
        found.append(here)
    return found


VEC_AT = vec_offsets()


def params(limit=24):
    return pltpu.CompilerParams(
        dimension_semantics=("arbitrary",), vmem_limit_bytes=limit * MIB
    )


def cost(flops, nbytes, trans=0):
    return pl.CostEstimate(flops=flops, bytes_accessed=nbytes, transcendentals=trans)


def rows_spec(width):
    return pl.BlockSpec((ROWS, width), lambda i, *_: (i, 0))


def fixed(shape, at=0):
    return pl.BlockSpec(shape, lambda i, *_: (at,) + (0,) * (len(shape) - 1))


def vec_piece(vec_ref, layer, name):
    start, length = VEC_AT[layer][name]
    return vec_ref[:, start : start + length]


def dot(left, right):
    return jnp.dot(left, right, preferred_element_type=f32)


def dot_nt(left, right, precision=None):
    return lax.dot_general(
        left, right, (((1,), (1,)), ((), ())), precision=precision, preferred_element_type=f32
    )


def dot_tn(left, right):
    return lax.dot_general(left, right, (((0,), (0,)), ((), ())), preferred_element_type=f32)


def joined(ref, start, rows_n, panels):
    return jnp.concatenate(
        [ref[start + p * rows_n : start + (p + 1) * rows_n, :] for p in range(panels)], axis=1
    )


def norm_stats(values):
    mean_val = jnp.mean(values, axis=-1, keepdims=True)
    centered = values - mean_val
    inv_std = lax.rsqrt(jnp.mean(centered * centered, axis=-1, keepdims=True) + norm_eps)
    return centered * inv_std, inv_std


def norm_back(values, gain, grad):
    unit, inv_std = norm_stats(values)
    scaled = grad * gain
    mean_s = jnp.mean(scaled, axis=-1, keepdims=True)
    mean_u = jnp.mean(scaled * unit, axis=-1, keepdims=True)
    back = inv_std * (scaled - mean_s - unit * mean_u)
    return (
        back,
        jnp.sum(grad * unit, axis=0, keepdims=True),
        jnp.sum(grad, axis=0, keepdims=True),
    )


def accumulate(ref, value):
    first = pl.program_id(0) == 0

    @pl.when(first)
    def _():
        ref[...] = value

    @pl.when(jnp.logical_not(first))
    def _():
        ref[...] += value


def stay(value):
    return pltpu.with_memory_space_constraint(value, pltpu.HBM)


def fence(*arrays):
    def nothing(*refs):
        pass

    anywhere = pl.BlockSpec(memory_space=pl.ANY)
    return pl.pallas_call(
        nothing,
        out_shape=[jax.ShapeDtypeStruct(a.shape, a.dtype) for a in arrays],
        in_specs=[anywhere] * len(arrays),
        out_specs=[anywhere] * len(arrays),
        input_output_aliases={i: i for i in range(len(arrays))},
        compiler_params=pltpu.CompilerParams(vmem_limit_bytes=MIB),
    )(*[stay(a) if a.size > 32 * 1024 else a for a in arrays])


def gather_kernel(slots, count_a, count_b, owner, drow, dcol, flag, *refs):
    first = refs[:count_a]
    second = refs[count_a : count_a + count_b]
    *panels, vectors, held, sem, vec_sem = refs[count_a + count_b :]

    def copy_all(sources):
        at = 0
        for src in sources:
            for n in range(src.shape[0]):
                who = owner[at]
                at += 1

                def body(i, carried, src=src, n=n, who=who):
                    slot = who * slots + i
                    row = drow[slot]

                    @pl.when(row >= 0)
                    def _():
                        start = pl.multiple_of(i * BS, BS)
                        pltpu.make_async_copy(
                            src.at[n, pl.ds(start, BS), :],
                            held.at[
                                pl.ds(pl.multiple_of(row, BS), BS),
                                pl.ds(pl.multiple_of(dcol[slot], BS), BS),
                            ],
                            sem,
                        ).start()

                    return carried

                lax.fori_loop(0, slots, body, 0)
                pltpu.make_async_copy(
                    src.at[n, pl.ds(slots * BS, VEC_ROWS), :], vectors.at[who], vec_sem
                ).start()

    if count_b:

        @pl.when(flag[0] == 1)
        def _():
            copy_all(first)

        @pl.when(flag[0] == 0)
        def _():
            copy_all(second)
    else:
        copy_all(first)
    pltpu.make_async_copy(held, held, sem).wait()
    at = 0
    for panel in panels:
        size = panel.shape[0]
        pltpu.make_async_copy(held.at[pl.ds(at, size), :], panel, sem).start()
        at += size
    pltpu.make_async_copy(vectors, vectors, vec_sem).wait()
    pltpu.make_async_copy(held, held, sem).wait()


def gather_tiles(first, second, owner, drow, dcol, flag, slots, owners):
    anywhere = pl.BlockSpec(memory_space=pl.ANY)
    *panels, vectors = pl.pallas_call(
        functools.partial(gather_kernel, slots, len(first), len(second)),
        out_shape=[pltpu.HBM((size, HALF), bf16) for unused, unused2, size in WEIGHTS]
        + [jax.ShapeDtypeStruct((owners, VEC_ROWS, BS), bf16)],
        grid_spec=pltpu.PrefetchScalarGridSpec(
            num_scalar_prefetch=4,
            grid=(1,),
            in_specs=[anywhere] * (len(first) + len(second)),
            out_specs=[anywhere] * len(WEIGHTS) + [fixed((owners, VEC_ROWS, BS))],
            scratch_shapes=[
                pltpu.VMEM((PANEL_ROWS, HALF), bf16),
                pltpu.SemaphoreType.DMA,
                pltpu.SemaphoreType.DMA,
            ],
        ),
        compiler_params=params(),
        cost_estimate=cost(0, 4 * PANEL_ROWS * HALF),
    )(owner, drow, dcol, flag, *[stay(v) for v in first], *[stay(v) for v in second])
    return {(name, layer): p for (name, layer, unused), p in zip(WEIGHTS, panels)}, vectors


def scatter_kernel(rows_n, cols_n, steps, paired, parts, pos, part, own, *refs):
    @pl.when(part[1] > 0)
    def _():
        scatter_body(rows_n, cols_n, steps, paired, parts, pos, part, own, *refs)


def scatter_body(rows_n, cols_n, steps, paired, parts, pos, part, own, *refs):
    if paired:
        recv, *refs = refs
        span = pl.num_programs(0) // parts
        here = jnp.logical_or(parts == 1, pl.program_id(0) // span == part[0])
    target, buf, sems = refs[-3:]
    step = pl.program_id(0)
    slot = lax.rem(step, 2)
    per = rows_n // BS * (cols_n // BS)

    def wait(at):
        pltpu.make_async_copy(buf.at[at], buf.at[at], sems.at[at]).wait()

    @pl.when(step >= 2)
    def _():
        wait(slot)

    for i in range(rows_n // BS):
        for j in range(cols_n // BS):
            area = (slice(i * BS, (i + 1) * BS), slice(j * BS, (j + 1) * BS))
            value = own[area]
            if paired:
                more = jnp.where(here, recv[area].astype(f32), 0.0)
                value = (value.astype(f32) + more).astype(bf16)
            buf[slot, i * (cols_n // BS) + j] = value
    for n in range(per):
        pltpu.make_async_copy(
            buf.at[slot, n],
            target.at[pl.ds(pl.multiple_of(pos[step * per + n], 16), BS), :],
            sems.at[slot],
        ).start()

    @pl.when(step == pl.num_programs(0) - 1)
    def _():
        if steps > 1:
            wait(1 - slot)
        wait(slot)


def scatter_matrix(pos, own, recv, part, target, total_rows, rows_n):
    cols_n = own.shape[1]
    steps = own.shape[0] // rows_n
    anywhere = pl.BlockSpec(memory_space=pl.ANY)
    block = pl.BlockSpec((rows_n, cols_n), lambda i, *_: (i, 0))
    paired = recv is not None
    parts = own.shape[0] // recv.shape[0] if paired else 1
    span = steps // parts
    arrived = pl.BlockSpec(
        (rows_n, cols_n), lambda i, pos, part: (jnp.clip(i - part[0] * span, 0, span - 1), 0)
    )
    operands = [stay(own)] + ([stay(recv)] if paired else []) + ([] if target is None else [stay(target)])
    specs = [block] + ([block if parts == 1 else arrived] if paired else [])
    specs += [] if target is None else [anywhere]
    return pl.pallas_call(
        functools.partial(scatter_kernel, rows_n, cols_n, steps, paired, parts),
        out_shape=pltpu.HBM((total_rows, BS), bf16),
        grid_spec=pltpu.PrefetchScalarGridSpec(
            num_scalar_prefetch=2,
            grid=(steps,),
            in_specs=specs,
            out_specs=anywhere,
            scratch_shapes=[
                pltpu.VMEM((2, rows_n // BS * (cols_n // BS), BS, BS), bf16),
                pltpu.SemaphoreType.DMA((2,)),
            ],
        ),
        input_output_aliases={} if target is None else {len(operands) + 1: 0},
        compiler_params=params(12),
        cost_estimate=cost(own.size, own.size * 6),
    )(pos, part, *operands)


def half_sum_kernel(part, own, arrived, out):
    out[...] = (own[...].astype(f32) + arrived[...].astype(f32)).astype(bf16)


def half_sum(part, own, arrived):
    block = arrived.shape
    return pl.pallas_call(
        half_sum_kernel,
        out_shape=pltpu.HBM(block, bf16),
        grid_spec=pltpu.PrefetchScalarGridSpec(
            num_scalar_prefetch=1,
            grid=(1,),
            in_specs=[pl.BlockSpec(block, lambda i, part: (part[0], 0)), fixed(block)],
            out_specs=fixed(block),
        ),
        compiler_params=params(8),
        cost_estimate=cost(arrived.size, arrived.size * 6),
    )(part, stay(own), stay(arrived))


def half_copy_kernel(part, own, out):
    out[...] = own[...]


def other_half(part, own):
    block = (own.shape[0] // 2, own.shape[1])
    return pl.pallas_call(
        half_copy_kernel,
        out_shape=pltpu.HBM(block, bf16),
        grid_spec=pltpu.PrefetchScalarGridSpec(
            num_scalar_prefetch=1,
            grid=(1,),
            in_specs=[pl.BlockSpec(block, lambda i, part: (1 - part[0], 0))],
            out_specs=fixed(block),
        ),
        compiler_params=params(8),
        cost_estimate=cost(0, own.size * 2),
    )(part, stay(own))


def scatter_vec_kernel(paired, pos, own, *refs):
    if paired:
        recv, *refs = refs
    target, buf, sem = refs[-3:]
    value = own[...]
    if paired:
        value = (value.astype(f32) + recv[...].astype(f32)).astype(bf16)
    buf[...] = value

    def body(n, carried):
        pltpu.make_async_copy(
            buf.at[n], target.at[pl.ds(pl.multiple_of(pos[n], 16), VEC_ROWS), :], sem
        ).start()
        return carried

    lax.fori_loop(0, own.shape[0], body, 0)
    pltpu.make_async_copy(buf, buf, sem).wait()


def scatter_vec(pos, own, recv, target):
    anywhere = pl.BlockSpec(memory_space=pl.ANY)
    block = fixed(own.shape)
    paired = recv is not None
    operands = [own] + ([recv] if paired else []) + [stay(target)]
    return pl.pallas_call(
        functools.partial(scatter_vec_kernel, paired),
        out_shape=pltpu.HBM(target.shape, bf16),
        grid_spec=pltpu.PrefetchScalarGridSpec(
            num_scalar_prefetch=1,
            grid=(1,),
            in_specs=[block] * (len(operands) - 1) + [anywhere],
            out_specs=anywhere,
            scratch_shapes=[pltpu.VMEM(own.shape, bf16), pltpu.SemaphoreType.DMA],
        ),
        input_output_aliases={len(operands): 0},
        compiler_params=params(4),
    )(pos, *operands)


def expand_kernel(present, half, patch_ref, class_ref, pinv_ref, out, total):
    for block in range(patch_ref.shape[0] // ROWS):
        rows = slice(block * ROWS, (block + 1) * ROWS)
        total[...] = jnp.zeros_like(total)
        for which in range(3):

            @pl.when(present[block, which] > 0)
            def _(which=which, rows=rows):
                chosen = jnp.where(class_ref[rows, :] == which, patch_ref[rows, :].astype(f32), 0.0)
                total[...] += dot_nt(chosen.astype(bf16), pinv_ref[which])

        out[rows, :] = total[...].astype(bf16)


def expand_call(which, present, half, patches, class_col, pinv):
    tokens = patches.shape[0]
    size = BASE_PIX // CHUNKS
    step = size
    return pl.pallas_call(
        expand_kernel,
        out_shape=jax.ShapeDtypeStruct((tokens, size), bf16),
        grid_spec=pltpu.PrefetchScalarGridSpec(
            num_scalar_prefetch=2,
            grid=(1,),
            in_specs=[
                fixed(patches.shape),
                fixed(class_col.shape),
                pl.BlockSpec(
                    (3, step, pinv.shape[2]),
                    lambda i, present, half: (0, (which + half[0] * (CHUNKS // 2)) % CHUNKS, 0),
                ),
            ],
            out_specs=pl.BlockSpec((tokens, step), lambda i, *_: (0, i)),
            scratch_shapes=[pltpu.VMEM((ROWS, step), f32)],
        ),
        compiler_params=params(),
        cost_estimate=cost(3 * tokens * size * D, tokens * size * 4 + size * D * 6),
    )(present, half, patches, class_col, stay(pinv))


def resize_kernel(base, pinv_ref, out, turned):
    @pl.when(pl.program_id(0) == 0)
    def _():
        turned[...] = base[...].T

    out[0] = dot(turned[...], pinv_ref[0]).astype(bf16)


def resize_call(weights, pinv):
    return pl.pallas_call(
        resize_kernel,
        out_shape=jax.ShapeDtypeStruct((3, HALF, pinv.shape[2]), bf16),
        grid=(3,),
        in_specs=[
            fixed((BASE_PIX, HALF)),
            pl.BlockSpec((1, BASE_PIX, pinv.shape[2]), lambda i: (i, 0, 0)),
        ],
        out_specs=pl.BlockSpec((1, HALF, pinv.shape[2]), lambda i: (i, 0, 0)),
        scratch_shapes=[pltpu.VMEM((HALF, BASE_PIX), bf16)],
        compiler_params=params(),
        cost_estimate=cost(6 * D * BASE_PIX * HALF, 6 * D * BASE_PIX),
    )(stay(weights["base", 0]), stay(pinv))


def embed_back_kernel(core, base, own, recv, out, bias):
    low = (base[...] + (own[...].astype(f32) + recv[...].astype(f32))).astype(bf16)
    out[...] = low
    accumulate(bias, jnp.sum(low.astype(f32), axis=0, keepdims=True))


def embed_back_call(core, base, own, recv):
    tokens = base.shape[0]
    half = pl.BlockSpec((ROWS, HALF), lambda i, core: (i, core[0]))
    return pl.pallas_call(
        embed_back_kernel,
        out_shape=[
            jax.ShapeDtypeStruct((tokens, HALF), bf16),
            jax.ShapeDtypeStruct((1, HALF), f32),
        ],
        grid_spec=pltpu.PrefetchScalarGridSpec(
            num_scalar_prefetch=1,
            grid=(tokens // ROWS,),
            in_specs=[half] * 3,
            out_specs=[rows_spec(HALF), fixed((1, HALF))],
        ),
        compiler_params=params(8),
        cost_estimate=cost(tokens * D, tokens * D * 5),
    )(core, base, own, recv)


def pack_kernel(vec_per, *refs):
    *pieces, out = refs
    out[...] = jnp.zeros_like(out)
    at = 0
    for piece in pieces:
        for k in range(piece.shape[1] // BS):
            owner, row = divmod(at, vec_per // BS)
            out[owner, row : row + 1, :] = piece[:, k * BS : (k + 1) * BS]
            at += 1


def pack_call(pieces, owners, vec_per):
    if vec_per % BS:
        joined = jnp.concatenate(pieces, axis=1)[0]
        joined = jnp.pad(joined, (0, owners * vec_per - joined.shape[0])).reshape(owners, vec_per)
        joined = jnp.pad(joined, ((0, 0), (0, VEC_ROWS * BS - vec_per)))
        return joined.astype(bf16).reshape(owners, VEC_ROWS, BS)
    return pl.pallas_call(
        functools.partial(pack_kernel, vec_per),
        out_shape=jax.ShapeDtypeStruct((owners, VEC_ROWS, BS), f32),
        grid=(1,),
        in_specs=[fixed(p.shape) for p in pieces],
        out_specs=fixed((owners, VEC_ROWS, BS)),
        compiler_params=params(4),
        cost_estimate=cost(0, owners * vec_per * 8),
    )(*pieces).astype(bf16)


def embed_kernel(half, *refs):
    *parts, vec, weight, out = refs
    size = BASE_PIX // CHUNKS
    total = vec[:, :HALF]
    for c in range(CHUNKS):
        at = lax.rem(c + half[0] * (CHUNKS // 2), CHUNKS)
        rows = pl.ds(pl.multiple_of(at * size, size), size)
        total = total + dot(parts[c][...], weight[rows, :])
    out[...] = total.astype(bf16)


def embed_call(half, chunks, vec, weights):
    tokens = chunks[0].shape[0]
    return pl.pallas_call(
        embed_kernel,
        out_shape=jax.ShapeDtypeStruct((tokens, HALF), bf16),
        grid_spec=pltpu.PrefetchScalarGridSpec(
            num_scalar_prefetch=1,
            grid=(tokens // ROWS,),
            in_specs=[rows_spec(BASE_PIX // CHUNKS)] * CHUNKS
            + [fixed(vec.shape), fixed((BASE_PIX, HALF))],
            out_specs=rows_spec(HALF),
        ),
        compiler_params=params(),
        cost_estimate=cost(2 * tokens * BASE_PIX * HALF, tokens * BASE_PIX * 3),
    )(half, *[stay(c) for c in chunks], vec, stay(weights["base", 0]))


def qkv_kernel(layer, first, core, *refs):
    if first:
        own, recv, vec, weight, hid, normed, q_ref, k_ref, v_ref = refs
        mine, theirs = own[...].astype(f32), recv[...].astype(f32)
        low = core[0] == 0
        values = jnp.concatenate(
            [jnp.where(low, mine, theirs), jnp.where(low, theirs, mine)], axis=1
        )
    else:
        base, own, recv, vec, weight, hid, normed, q_ref, k_ref, v_ref = refs
        values = base[...] + (own[...].astype(f32) + recv[...].astype(f32))
    hid[...] = values
    unit, unused = norm_stats(values)
    low = (unit * vec_piece(vec, layer, "g1") + vec_piece(vec, layer, "s1")).astype(bf16)
    normed[...] = low
    made = dot(low, joined(weight, 0, D, 3))
    q_ref[...] = (made[:, :HALF] + vec_piece(vec, layer, "bq")).astype(bf16)
    k_ref[...] = made[:, HALF : 2 * HALF].astype(bf16)
    v_ref[...] = (made[:, 2 * HALF :] + vec_piece(vec, layer, "bv")).astype(bf16)


def qkv_call(layer, base, own, recv, core, vec, weights):
    tokens = own.shape[0]
    shape = lambda width, kind: jax.ShapeDtypeStruct((tokens, width), kind)
    outs = [shape(D, f32), pltpu.HBM((tokens, D), bf16)] + [shape(HALF, bf16)] * 3
    operands = ([] if base is None else [base]) + [own, recv]
    return pl.pallas_call(
        functools.partial(qkv_kernel, layer, base is None),
        out_shape=outs,
        grid_spec=pltpu.PrefetchScalarGridSpec(
            num_scalar_prefetch=1,
            grid=(tokens // ROWS,),
            in_specs=[rows_spec(o.shape[1]) for o in operands]
            + [fixed(vec.shape), fixed((3 * D, HALF))],
            out_specs=[rows_spec(o.shape[1]) for o in outs],
        ),
        compiler_params=params(),
        cost_estimate=cost(2 * tokens * D * 3 * HALF, tokens * D * 14),
    )(core, *operands, vec, weights["qkv", layer])


def head_masks():
    lane = lax.broadcasted_iota(jnp.int32, (1, 2 * HEAD_DIM), 1)
    low = (lane < HEAD_DIM).astype(f32).astype(bf16)
    high = (lane >= HEAD_DIM).astype(f32).astype(bf16)
    return low, high


def attend_kernel(
    layer, low_ref, high_ref, q_ref, k_ref, v_ref, seg_q, seg_k, vec, w_out, o_ref, lse_ref, part,
    scores_ref, top_ref, acc_ref,
):
    step = pl.program_id(0)
    first, last = low_ref[step], high_ref[step]
    masks = head_masks()
    scale = jnp.asarray(HEAD_DIM ** (-0.5), bf16)
    lane = lax.broadcasted_iota(jnp.int32, (1, BS), 1)
    sums = [(lane == HEAD_DIM).astype(f32).astype(bf16), (lane == 0).astype(f32).astype(bf16)]
    top_ref[...] = jnp.full(top_ref.shape, masked_score, f32)
    acc_ref[...] = jnp.zeros_like(acc_ref)
    seg_col = seg_q[...]

    def score_block(block, carried):
        rows = pl.ds(pl.multiple_of(block * ROWS, ROWS), ROWS)
        same = seg_col == seg_k[:, rows]
        for pair in range(HEADS // 2):
            cols = slice(pair * BS, (pair + 1) * BS)
            q_two = q_ref[:, cols] * scale
            k_two = k_ref[rows, cols]
            for side in range(2):
                head = 2 * pair + side
                scores = jnp.where(same, dot_nt(q_two * masks[side], k_two), masked_score)
                scores_ref[head, block] = scores
                top = top_ref[head]
                for piece in range(ROWS // BS):
                    top = jnp.maximum(top, scores[:, piece * BS : (piece + 1) * BS])
                top_ref[head] = top
        return carried

    lax.fori_loop(first, last, score_block, 0)
    tops = [jnp.max(top_ref[head], axis=1, keepdims=True) for head in range(HEADS)]

    def mix_block(block, carried):
        rows = pl.ds(pl.multiple_of(block * ROWS, ROWS), ROWS)
        for pair in range(HEADS // 2):
            v_two = v_ref[rows, pair * BS : (pair + 1) * BS]
            for side in range(2):
                head = 2 * pair + side
                expo = jnp.exp(scores_ref[head, block] - tops[head]).astype(bf16)
                acc_ref[head] += dot(expo, v_two * masks[side] + sums[side])
        return carried

    lax.fori_loop(first, last, mix_block, 0)
    totals = jnp.zeros((ROWS, BS), f32)
    for pair in range(HEADS // 2):
        sides = []
        for side in range(2):
            head = 2 * pair + side
            mixed = acc_ref[head]
            at = HEAD_DIM * (1 - side)
            total = mixed[:, at : at + 1]
            totals = jnp.where(lane == head, tops[head] + jnp.log(total), totals)
            sides.append(mixed * (1.0 / total))
        o_ref[:, pair * BS : (pair + 1) * BS] = jnp.where(lane < HEAD_DIM, *sides).astype(bf16)
    lse_ref[...] = totals.T[0:8, :]
    low = o_ref[...]
    bias = vec_piece(vec, layer, "bo")
    part[...] = (dot(low, joined(w_out, 0, HALF, TENSOR)) + bias).astype(bf16)


def attend_call(layer, first, last, queries, keys, values, seg_col, seg_row, vec, weights):
    tokens = queries.shape[0]
    return pl.pallas_call(
        functools.partial(attend_kernel, layer),
        out_shape=[
            jax.ShapeDtypeStruct((tokens, HALF), bf16),
            jax.ShapeDtypeStruct((8, tokens), f32),
            jax.ShapeDtypeStruct((tokens, D), bf16),
        ],
        grid_spec=pltpu.PrefetchScalarGridSpec(
            num_scalar_prefetch=2,
            grid=(tokens // ROWS,),
            in_specs=[
                rows_spec(HALF),
                fixed(keys.shape),
                fixed(values.shape),
                rows_spec(1),
                fixed(seg_row.shape),
                fixed(vec.shape),
                fixed((D, HALF)),
            ],
            out_specs=[
                rows_spec(HALF),
                pl.BlockSpec((8, ROWS), lambda i, *_: (0, i)),
                rows_spec(D),
            ],
            scratch_shapes=[
                pltpu.VMEM((HEADS, tokens // ROWS, ROWS, ROWS), f32),
                pltpu.VMEM((HEADS, ROWS, BS), f32),
                pltpu.VMEM((HEADS, ROWS, BS), f32),
            ],
        ),
        compiler_params=params(),
        cost_estimate=cost(8 * HEADS * tokens * tokens * BS, tokens * D * 8, HEADS * tokens * tokens),
    )(first, last, queries, keys, values, seg_col, seg_row, vec, weights["out", layer])


def gelu_parts(values):
    cdf = 0.5 * (1.0 + lax.erf(values * 0.7071067811865476))
    pdf = 0.3989422804014327 * jnp.exp(-0.5 * values * values)
    return values * cdf, cdf + values * pdf


def mlp_kernel(layer, base, own, recv, vec, w_up, w_down, hid, normed, act, slope, part):
    values = base[...] + (own[...].astype(f32) + recv[...].astype(f32))
    hid[...] = values
    unit, unused = norm_stats(values)
    low = (unit * vec_piece(vec, layer, "g2") + vec_piece(vec, layer, "s2")).astype(bf16)
    normed[...] = low
    bias_up = vec_piece(vec, layer, "b1")
    for pair in range(HALF_FF // D):
        area = slice(pair * D, (pair + 1) * D)
        up = dot(low, joined(w_up, pair * 2 * D, D, 2)) + bias_up[:, area]
        gelu, grad = gelu_parts(up)
        act[:, area] = gelu.astype(bf16)
        slope[:, area] = grad.astype(bf16)
    bias_down = vec_piece(vec, layer, "b2")
    part[...] = (dot(act[...], joined(w_down, 0, HALF_FF, TENSOR)) + bias_down).astype(bf16)


def mlp_call(layer, base, own, recv, vec, weights):
    tokens = base.shape[0]
    shape = lambda width, kind: jax.ShapeDtypeStruct((tokens, width), kind)
    kept = lambda width: pltpu.HBM((tokens, width), bf16)
    outs = [shape(D, f32), kept(D), kept(HALF_FF), kept(HALF_FF), shape(D, bf16)]
    return pl.pallas_call(
        functools.partial(mlp_kernel, layer),
        out_shape=outs,
        grid=(tokens // ROWS,),
        in_specs=[rows_spec(D)] * 3
        + [
            fixed(vec.shape),
            fixed((2 * HALF_FF, HALF)),
            fixed((2 * HALF_FF, HALF)),
        ],
        out_specs=[rows_spec(o.shape[1]) for o in outs],
        compiler_params=params(),
        cost_estimate=cost(4 * tokens * D * HALF_FF, tokens * D * 24, 2 * tokens * HALF_FF),
    )(base, own, recv, vec, weights["up", layer], weights["down", layer])


def mlp_back_kernel(layer, summed, *refs):
    if summed:
        base, own, recv, *refs = refs
        (hid, slope, vec, w_up, w_down, grad_full, grad_low, du_ref, back, dgain, dshift, db1, db2) = refs
        values = base[...].astype(f32) + (own[...].astype(f32) + recv[...].astype(f32))
        grad_full[...] = values
        low = values.astype(bf16)
    else:
        base, valid, *refs = refs
        (hid, slope, vec, w_up, w_down, grad_low, du_ref, back, dgain, dshift, db1, db2) = refs
        low = (base[...].astype(f32) * valid[...]).astype(bf16)
    grad_low[...] = low
    accumulate(db2, jnp.sum(low.astype(f32), axis=0, keepdims=True))
    for part in range(HALF_FF // D):
        area = slice(part * D, (part + 1) * D)
        rows = jnp.concatenate(
            [w_down[p * HALF_FF + part * D : p * HALF_FF + (part + 1) * D, :] for p in range(TENSOR)],
            axis=1,
        )
        du_ref[:, area] = (dot_nt(low, rows) * slope[:, area].astype(f32)).astype(bf16)
    grad_normed = dot_nt(du_ref[...], joined(w_up, 0, D, HALF_FF // HALF))
    accumulate(db1, jnp.sum(du_ref[...].astype(f32), axis=0, keepdims=True))
    part_back, gain_grad, shift_grad = norm_back(hid[...], vec_piece(vec, layer, "g2"), grad_normed)
    back[...] = part_back.astype(bf16)
    accumulate(dgain, gain_grad)
    accumulate(dshift, shift_grad)


def mlp_back_call(layer, base, own, recv, valid, hid, slope, vec, weights):
    tokens = base.shape[0]
    summed = own is not None
    shape = lambda width, kind: jax.ShapeDtypeStruct((tokens, width), kind)
    line = lambda width: jax.ShapeDtypeStruct((1, width), f32)
    outs = ([shape(D, f32)] if summed else []) + [shape(D, bf16), shape(HALF_FF, bf16), shape(D, bf16)]
    lines = [line(D), line(D), line(HALF_FF), line(D)]
    extra = [own, recv] if summed else [valid]
    return pl.pallas_call(
        functools.partial(mlp_back_kernel, layer, summed),
        out_shape=outs + lines,
        grid=(tokens // ROWS,),
        in_specs=[rows_spec(D)]
        + [rows_spec(e.shape[1]) for e in extra]
        + [
            rows_spec(D),
            rows_spec(HALF_FF),
            fixed(vec.shape),
            fixed((2 * HALF_FF, HALF)),
            fixed((2 * HALF_FF, HALF)),
        ],
        out_specs=[rows_spec(o.shape[1]) for o in outs] + [fixed(o.shape) for o in lines],
        compiler_params=params(),
        cost_estimate=cost(4 * tokens * D * HALF_FF, tokens * D * 24),
    )(base, *extra, stay(hid), stay(slope), vec, weights["up", layer], weights["down", layer])


def attend_back_kernel(
    low_ref, high_ref, base, own, recv, q_ref, k_ref, v_ref, o_ref, lse_ref, seg_k, seg_q, w_out,
    full_ref, grad_low, dq_ref, dk_ref, dv_ref, dbo, dk_acc, dv_acc, dq_acc, do_ref,
):
    step = pl.program_id(0)

    @pl.when(step == 0)
    def _():
        dk_acc[...] = jnp.zeros_like(dk_acc)
        dv_acc[...] = jnp.zeros_like(dv_acc)

    values = base[...].astype(f32) + (own[...].astype(f32) + recv[...].astype(f32))
    full_ref[...] = values
    low = values.astype(bf16)
    grad_low[...] = low
    accumulate(dbo, jnp.sum(low.astype(f32), axis=0, keepdims=True))
    do_ref[...] = dot_nt(low, joined(w_out, 0, HALF, TENSOR)).astype(bf16)
    product = do_ref[...].astype(f32) * o_ref[...].astype(f32)
    head = lax.broadcasted_iota(jnp.int32, (8, HALF), 0)
    lane = lax.broadcasted_iota(jnp.int32, (8, HALF), 1)
    pick = ((lane >= head * HEAD_DIM) & (lane < (head + 1) * HEAD_DIM)).astype(f32)
    high, rest = split(product)
    pick = pick.astype(bf16)
    inner = dot_nt(pick, high) + dot_nt(pick, rest)
    dq_acc[...] = jnp.zeros_like(dq_acc)
    masks = head_masks()
    scale = jnp.asarray(HEAD_DIM ** (-0.5), bf16)
    seg_row = seg_q[...]

    def one_block(block, carried):
        rows = pl.ds(pl.multiple_of(block * KEYS, KEYS), KEYS)
        same = seg_k[rows, :] == seg_row
        for pair in range(HEADS // 2):
            cols = slice(pair * BS, (pair + 1) * BS)
            q_two = q_ref[:, cols] * scale
            do_two = do_ref[:, cols]
            k_two = k_ref[rows, cols]
            v_two = v_ref[rows, cols]
            dv_two = dk_two = dq_two = None
            for side in range(2):
                at = 2 * pair + side
                q_one = q_two * masks[side]
                do_one = do_two * masks[side]
                scores = dot_nt(k_two, q_one)
                prob = jnp.where(same, jnp.exp(scores - lse_ref[at : at + 1, :]), 0.0)
                grad_prob = dot_nt(v_two, do_one)
                grad_scores = (prob * (grad_prob - inner[at : at + 1, :])).astype(bf16)
                dv_one = dot(prob.astype(bf16), do_one)
                dk_one = dot(grad_scores, q_one)
                dq_one = dot_tn(grad_scores, k_two * masks[side])
                dq_two = dq_one if dq_two is None else dq_two + dq_one
                dv_two = dv_one if dv_two is None else dv_two + dv_one
                dk_two = dk_one if dk_two is None else dk_two + dk_one
            dv_acc[rows, cols] += dv_two
            dk_acc[rows, cols] += dk_two
            dq_acc[:, cols] += dq_two
        return carried

    lax.fori_loop(low_ref[step], high_ref[step], one_block, 0)
    dq_ref[...] = (dq_acc[...] * HEAD_DIM ** (-0.5)).astype(bf16)

    @pl.when(step == pl.num_programs(0) - 1)
    def _():
        dk_ref[...] = dk_acc[...].astype(bf16)
        dv_ref[...] = dv_acc[...].astype(bf16)


def attend_back_call(
    layer, first, last, base, own, recv, queries, keys, values, mixed, lse, seg_col, seg_row, weights
):
    tokens = base.shape[0]
    shape = lambda width, kind: jax.ShapeDtypeStruct((tokens, width), kind)
    whole = (tokens, HALF)
    return pl.pallas_call(
        attend_back_kernel,
        out_shape=[
            shape(D, f32),
            shape(D, bf16),
            shape(HALF, bf16),
            shape(HALF, bf16),
            shape(HALF, bf16),
            jax.ShapeDtypeStruct((1, D), f32),
        ],
        grid_spec=pltpu.PrefetchScalarGridSpec(
            num_scalar_prefetch=2,
            grid=(tokens // ROWS,),
            in_specs=[
                rows_spec(D),
                rows_spec(D),
                rows_spec(D),
                rows_spec(HALF),
                fixed(whole),
                fixed(whole),
                rows_spec(HALF),
                pl.BlockSpec((8, ROWS), lambda i, *_: (0, i)),
                fixed(seg_col.shape),
                pl.BlockSpec((1, ROWS), lambda i, *_: (0, i)),
                fixed((D, HALF)),
            ],
            out_specs=[
                rows_spec(D),
                rows_spec(D),
                rows_spec(HALF),
                fixed(whole),
                fixed(whole),
                fixed((1, D)),
            ],
            scratch_shapes=[
                pltpu.VMEM(whole, f32),
                pltpu.VMEM(whole, f32),
                pltpu.VMEM((ROWS, HALF), f32),
                pltpu.VMEM((ROWS, HALF), bf16),
            ],
        ),
        compiler_params=params(),
        cost_estimate=cost(14 * HEADS * tokens * tokens * BS, tokens * D * 20, HEADS * tokens * tokens),
    )(
        first, last, base, own, recv, stay(queries), stay(keys), stay(values), stay(mixed), lse,
        seg_col, seg_row, weights["out", layer],
    )


def qkv_back_kernel(layer, dq, dk, dv, hid, vec, weight, back, dgain, dshift, dbq, dbv):
    grad_three = jnp.concatenate([dq[...], dk[...], dv[...]], axis=1)
    grad_normed = dot_nt(grad_three, joined(weight, 0, D, 3))
    part_back, gain_grad, shift_grad = norm_back(hid[...], vec_piece(vec, layer, "g1"), grad_normed)
    back[...] = part_back.astype(bf16)
    accumulate(dgain, gain_grad)
    accumulate(dshift, shift_grad)
    accumulate(dbq, jnp.sum(dq[...].astype(f32), axis=0, keepdims=True))
    accumulate(dbv, jnp.sum(dv[...].astype(f32), axis=0, keepdims=True))


def qkv_back_call(layer, dq, dk, dv, hid, vec, weights):
    tokens = dq.shape[0]
    line = lambda width: jax.ShapeDtypeStruct((1, width), f32)
    lines = [line(D), line(D), line(HALF), line(HALF)]
    return pl.pallas_call(
        functools.partial(qkv_back_kernel, layer),
        out_shape=[jax.ShapeDtypeStruct((tokens, D), bf16)] + lines,
        grid=(tokens // ROWS,),
        in_specs=[rows_spec(HALF)] * 3
        + [
            rows_spec(D),
            fixed(vec.shape),
            fixed((3 * D, HALF)),
        ],
        out_specs=[rows_spec(D)] + [fixed(o.shape) for o in lines],
        compiler_params=params(),
        cost_estimate=cost(2 * tokens * D * 3 * HALF, tokens * D * 10),
    )(dq, dk, dv, stay(hid), vec, weights["qkv", layer])


def split(values):
    high = values.astype(bf16)
    return high, (values - high.astype(f32)).astype(bf16)


def product(left, right, left_dim, right_dim):
    def one(a, b):
        return lax.dot_general(
            a, b, (((left_dim,), (right_dim,)), ((), ())), preferred_element_type=f32
        )

    return one(left[0], right[0]) + (one(left[0], right[1]) + one(left[1], right[0]))


def owner_kernel(per, used, home, near, far, master, left, right, moment, variance, grad, out, out_mom, out_var):
    here = range(per)
    first = pl.program_id(0) * per
    lefts = [split(left[i]) for i in here]
    rights = [split(right[i]) for i in here]
    rotated = []
    for i in here:
        rows = slice(i * BS, (i + 1) * BS)
        tile = jnp.where(home[0] > 0, near[rows, :].astype(f32), far[rows, :].astype(f32))
        tile = jnp.where(used[first + i] > 0, tile, 0.0)
        grad[i] = tile
        tile = tile.astype(bf16)
        rotated.append(split(dot_tn(lefts[i][0], tile) + dot_tn(lefts[i][1], tile)))
    rotated = [product(rotated[i], rights[i], 1, 0) for i in here]
    steps = []
    for i in here:
        new_moment = decay * moment[i] + (1.0 - decay) * rotated[i]
        new_variance = decay * variance[i] + (1.0 - decay) * rotated[i] * rotated[i]
        out_mom[i] = new_moment
        out_var[i] = new_variance
        steps.append(split(new_moment / (jnp.sqrt(new_variance) + adam_eps)))
    returned = [split(product(lefts[i], steps[i], 1, 0)) for i in here]
    returned = [product(returned[i], rights[i], 1, 1) for i in here]
    for i in here:
        out[i] = master[i] - matrix_rate * returned[i]


def owner_call(used, home, near, far, *arrays):
    count = arrays[0].shape[0]
    per = min(8, count)
    block = pl.BlockSpec((per, BS, BS), lambda i, *_: (i, 0, 0))
    return pl.pallas_call(
        functools.partial(owner_kernel, per),
        out_shape=[jax.ShapeDtypeStruct(arrays[0].shape, f32)] * 4,
        grid_spec=pltpu.PrefetchScalarGridSpec(
            num_scalar_prefetch=2,
            grid=(count // per,),
            in_specs=[pl.BlockSpec((per * BS, BS), lambda i, *_: (i, 0))] * 2 + [block] * 5,
            out_specs=[block] * 4,
        ),
        compiler_params=params(),
        cost_estimate=cost(count * 88 * BS**3, count * BS * BS * 38),
    )(used, home, stay(near), stay(far), *arrays)


def reduce_kernel(carrying, last, *refs):
    block, arrived, *refs = refs
    total = block[...].astype(f32) + arrived[...].astype(f32)
    if carrying:
        carried, *refs = refs
        total = total + carried[...].astype(f32)
    if last:
        [out] = refs
    else:
        following, out, later = refs
        later[...] = following[...]
    out[...] = total.astype(bf16)


def reduce_call(j, n, buffer, arrived, carried, payload):
    last = j == 3
    at = lambda j, x_rel: pl.BlockSpec((payload, BS), lambda i: ((j * 2 + x_rel) * 2 + n, 0))
    whole = fixed((payload, BS))
    operands = [stay(buffer), stay(arrived)] + ([] if carried is None else [stay(carried)])
    specs = [at(j, 0)] + [whole] * (len(operands) - 1)
    if not last:
        operands.append(stay(buffer))
        specs.append(at(j + 1, 1))
    outs = [pltpu.HBM((payload, BS), bf16)] * (1 if last else 2)
    made = pl.pallas_call(
        functools.partial(reduce_kernel, carried is not None, last),
        out_shape=outs,
        grid=(1,),
        in_specs=specs,
        out_specs=[whole] * len(outs),
        compiler_params=params(8),
        cost_estimate=cost(payload * BS * 3, payload * BS * 12),
    )(*operands)
    return (made[0], None) if last else made


class Routes:
    def __init__(self, dp_n):
        pairs = [(d, t) for d in range(dp_n) for t in range(TENSOR)]
        at = lambda d, t: d * TENSOR + t
        home = [(d, t) for d, t in pairs if d % 2 == t]
        away = [(d, t) for d, t in pairs if d % 2 != t]
        self.core_all = [(at(d, t), at(d ^ 1, t)) for d, t in pairs]
        self.core_out = [(at(d, t), at(d ^ 1, t)) for d, t in home]
        self.core_in = [(at(d, t), at(d ^ 1, t)) for d, t in away]
        self.y_all = [(at(d, t), at(d, 1 - t)) for d, t in pairs]
        self.y_out = [(at(d, t), at(d, 1 - t)) for d, t in home]
        self.y_in = [(at(d, t), at(d, 1 - t)) for d, t in away]
        self.x_home = [(at(d, t), at(d ^ 2, t)) for d, t in home]
        self.x_away = [(at(d, t), at(d ^ 2, t)) for d, t in away]
        self.z_home = [(at(d, t), at((d + 4) % dp_n, t)) for d, t in home]


def send(value, route):
    return lax.ppermute(value, AXES, route)


def shards(
    patches,
    cotangent,
    image_size,
    block_slot,
    pinv,
    master_slots,
    left_basis,
    right_basis,
    mom_slots,
    var_slots,
    vec_master,
    vec_mom,
    vec_var,
):
    dp_n = lax.axis_size("dp")
    dp_pos = lax.axis_index("dp")
    y_pos = lax.axis_index("tensor")
    core = dp_pos % 2
    home = core == y_pos
    routes = Routes(dp_n)
    grid3 = dp_n == 16
    x_pos = (dp_pos // 2) % 2
    half_at = (x_pos if grid3 else x_pos * 0).astype(jnp.int32).reshape(1)
    tokens_n = patches.shape[0]
    slots_per = master_slots.shape[1]
    vec_per = vec_master.shape[1]
    slots_n = slots_per * dp_n
    payload = slots_per * BS + VEC_ROWS

    patches = jnp.where(home, patches, send(patches, routes.core_out))
    cotangent = jnp.where(home, cotangent, send(cotangent, routes.core_out))
    size_row = jnp.where(home, image_size, send(image_size, routes.core_out))[0]
    own_slots = block_slot[0]
    slot_other = send(block_slot, routes.y_all)

    lengths = jnp.where(
        size_row == 0, LEN_A, jnp.where(size_row == 1, LEN_B, jnp.where(size_row == 2, LEN_C, 0))
    )
    order = jnp.arange(IMG_DEV)
    ends_at = jnp.sum(jnp.where(order[None, :] <= order[:, None], lengths[None, :], 0), axis=1)
    places = jnp.arange(tokens_n)
    segment = jnp.sum((places[:, None] >= ends_at[None, :]).astype(jnp.int32), axis=1)
    in_image = segment[:, None] == order[None, :]
    select = jnp.stack(
        [jnp.any(in_image & (size_row == s)[None, :], axis=1) for s in range(3)], axis=1
    )
    valid_col = (segment < IMG_DEV).astype(f32)[:, None]
    seg_col = segment[:, None]
    seg_row = segment[None, :]
    blocks_n = tokens_n // ROWS
    starts = jnp.arange(blocks_n) * ROWS
    begun = ends_at[None, :] <= starts[:, None]
    first_tok = jnp.max(jnp.where(begun, ends_at[None, :], 0), axis=1)
    after = ends_at[None, :] > (starts + ROWS - 1)[:, None]
    last_tok = jnp.min(jnp.where(after, ends_at[None, :], tokens_n), axis=1)
    first_blk = (first_tok // ROWS).astype(jnp.int32)
    last_blk = ((last_tok + ROWS - 1) // ROWS).astype(jnp.int32)
    first_key = (first_tok // KEYS).astype(jnp.int32)
    last_key = ((last_tok + KEYS - 1) // KEYS).astype(jnp.int32)

    select_low = select.astype(bf16)
    class_col = jnp.sum(jnp.where(select, jnp.arange(1, 4)[None, :], 0), axis=1, keepdims=True) - 1
    present = jnp.any(select.reshape(blocks_n, ROWS, 3), axis=1).astype(jnp.int32)

    def expand(which):
        return expand_call(which, present, half_at, patches, class_col, pinv)

    vec_low = jnp.pad(vec_master[0].astype(bf16), (0, VEC_ROWS * BS - vec_per))
    own_pack = jnp.concatenate(
        [
            master_slots[0].astype(bf16).reshape(slots_per * BS, BS),
            vec_low.reshape(VEC_ROWS, BS),
        ],
        axis=0,
    )
    flag = home.astype(jnp.int32).reshape(1)
    if grid3:
        z_pos = dp_pos // 4
        packs = [[own_pack], [send(own_pack, routes.core_in)]]
        across, over_y, corner = [[], []], [[], []], [[], []]
        token = jnp.zeros((8, BS), f32)
        chunks = []
        for j in range(5):
            for n in range(2):
                moved = {}
                if j < 4:
                    moved["x"] = send(packs[n][j], routes.x_home)
                    moved["y"] = send(packs[n][j], routes.y_out)
                if j:
                    source, route = (across, routes.y_out) if n == 0 else (over_y, routes.x_away)
                    moved["corner"] = send(source[n][j - 1], route)
                if j < 3:
                    moved["z"] = send(packs[n][j], routes.z_home)
                work = []
                if j + n == 0:
                    work = [slot_other]
                if 1 <= 2 * j + n <= CHUNKS:
                    work = [expand(2 * j + n - 1)]
                if j < 4:
                    token, *made = fence(token, *moved.values(), *work)
                    if j + n == 0:
                        slot_other = made.pop()
                    elif work:
                        chunks.append(made.pop())
                    moved = dict(zip(moved, made))
                    across[n].append(moved["x"])
                    over_y[n].append(moved["y"])
                if j < 3:
                    packs[n].append(moved["z"])
                if j:
                    corner[n].append(moved["corner"])
        first, second, owner = [], [], []
        for j in range(4):
            first += [packs[0][j], packs[1][j], across[0][j], across[1][j]]
            second += [over_y[0][j], over_y[1][j], corner[0][j], corner[1][j]]
            for x_rel in range(2):
                for n in range(2):
                    owner.append(((z_pos - j) % 4) * 4 + (x_pos ^ x_rel) * 2 + (core ^ n))
        first = [v[None] for v in first]
        second = [v[None] for v in second]
        owner = jnp.stack(owner).astype(jnp.int32)
    else:
        everything = lax.all_gather(own_pack, AXES, axis=0)
        everything = everything.reshape(dp_n, TENSOR, payload, BS)
        first = [jnp.where(core == 0, everything[:, 0], everything[:, 1])]
        second = []
        owner = jnp.arange(dp_n, dtype=jnp.int32)
        chunks = [expand(c) for c in range(CHUNKS)]
    slot_list = jnp.where(home, block_slot, slot_other)[0]
    named = slot_list[None, :] == jnp.arange(slots_n)[:, None]
    used = jnp.any(named, axis=1)
    drow = jnp.where(used, jnp.sum(jnp.where(named, TARGET_ROW[None, :], 0), axis=1), -1)
    dcol = jnp.sum(jnp.where(named, TARGET_COL[None, :], 0), axis=1)
    weights, vec_rows = gather_tiles(first, second, owner, drow, dcol, flag, slots_per, dp_n)
    vec = vec_rows.reshape(dp_n, VEC_ROWS * BS)[:, :vec_per].astype(f32).reshape(1, dp_n * vec_per)

    embedded = embed_call(half_at, chunks, vec, weights)
    embedded_other = send(embedded, routes.core_all)
    core_flag = core.astype(jnp.int32).reshape(1)

    caches = []
    hidden, own, recv = None, embedded, embedded_other
    for layer in range(LAYERS):
        hidden, normed, queries, keys, values = qkv_call(
            layer, hidden, own, recv, core_flag, vec, weights
        )
        mixed, lse, part = attend_call(
            layer, first_blk, last_blk, queries, keys, values, seg_col, seg_row, vec, weights
        )
        other = send(part, routes.core_all)
        middle, normed2, act, slope, own = mlp_call(layer, hidden, part, other, vec, weights)
        recv = send(own, routes.core_all)
        caches.append((hidden, normed, queries, keys, values, mixed, lse, middle, normed2, act, slope))
        hidden = middle
    out_low = ((hidden + (own.astype(f32) + recv.astype(f32))) * valid_col).astype(bf16)

    owners = jnp.arange(dp_n)
    if grid3:
        place = (
            ((z_pos - 1 - owners // 4) % 4) * 4
            + (x_pos ^ ((owners // 2) % 2)) * 2
            + (core ^ (owners % 2))
        ).astype(jnp.int32)
    else:
        place = owners.astype(jnp.int32)
    slot_owner = slot_list // slots_per
    owner_place = jnp.sum(
        jnp.where(slot_owner[:, None] == owners[None, :], place[None, :], 0), axis=1
    )
    tile_pos = (owner_place * payload + (slot_list % slots_per) * BS).astype(jnp.int32)
    vec_pos = (place * payload + slots_per * BS).astype(jnp.int32)
    total_rows = dp_n * payload
    where_to = jnp.concatenate([half_at, flag if grid3 else flag * 0 + 1])
    offsets = {"base": 0}
    count = BASE_PIX // BS * (HALF // BS)
    for layer in range(LAYERS):
        for name, size in (("qkv", 3 * D * HALF), ("out", D * HALF), ("up", D * HALF_FF), ("down", D * HALF_FF)):
            offsets[name, layer] = count
            count += size // (BS * BS)

    def place_tiles(key, matrix, arrived, buffer):
        tiles = matrix.size // (BS * BS)
        pos = tile_pos[offsets[key] : offsets[key] + tiles]
        rows_n = matrix.shape[0] // 2 if matrix.shape[0] > HALF else HALF
        return scatter_matrix(pos, matrix, arrived, where_to, buffer, total_rows, rows_n)

    def place_base(rel, matrix, arrived, buffer):
        size = BASE_PIX * HALF // (BS * BS) // 2
        low_pos, high_pos = tile_pos[:size], tile_pos[size : 2 * size]
        pos = jnp.where(half_at[0] == rel, low_pos, high_pos)
        return scatter_matrix(pos, matrix, arrived, where_to, buffer, total_rows, D)

    def over(matrix):
        return send(matrix, routes.y_in) if grid3 else None

    def beside(matrix):
        return send(other_half(half_at, matrix), routes.x_away) if grid3 else None

    def summed(matrix, arrived):
        return half_sum(half_at, matrix, arrived) if grid3 else None

    def hold(*arrays):
        kept = [a for a in arrays if a is not None]
        done = iter(fence(*kept))
        return [None if a is None else next(done) for a in arrays]

    top, low = 1, 0
    vec_grads = [None] * LAYERS

    def mlp_step(layer, grad, own, recv):
        middle, normed2, act, slope = caches[layer][7:11]
        made = mlp_back_call(layer, grad, own, recv, valid_col, middle, slope, vec, weights)
        if own is not None:
            return made
        return [made[0]] + list(made)

    def attend_step(layer, grad, part, other, lse):
        hid_in, normed, queries, keys, values, mixed = caches[layer][:6]
        return attend_back_call(
            layer, first_key, last_key, grad, part, other, queries, keys, values, mixed, lse,
            seg_col, seg_row, weights,
        )

    grad, grad_low, du, part, dg2, ds2, db1, db2 = mlp_step(top, cotangent, None, None)
    other = send(part, routes.core_all)
    gd1 = dot_tn(caches[top][9], grad_low).astype(bf16)
    gu1 = dot_tn(caches[top][8], du).astype(bf16)
    lse, gd1, gu1, out_low = fence(caches[top][6], gd1, gu1, out_low)
    ad1 = over(gd1)
    grad, grad_low, dq, dk, dv, dbo = attend_step(top, grad, part, other, lse)
    vec, dbo, ad1, gu1 = hold(vec, dbo, ad1, gu1)
    au1 = over(gu1)
    own, dg1, ds1, dbq, dbv = qkv_back_call(top, dq, dk, dv, caches[top][0], vec, weights)
    recv = send(own, routes.core_all)
    go1 = dot_tn(caches[top][5], grad_low).astype(bf16)
    gq1 = dot_tn(caches[top][1], jnp.concatenate([dq, dk, dv], axis=1)).astype(bf16)
    vec_grads[top] = [dg1, ds1, dbq, dbv, dbo, dg2, ds2, db1, db2]
    grad, grad_low, du, part, dg2, ds2, db1, db2 = mlp_step(low, grad, own, recv)
    other = send(part, routes.core_all)
    db2, au1, go1, gq1 = hold(db2, au1, go1, gq1)
    xq1, ao1 = beside(gq1), over(go1)
    gd0 = dot_tn(caches[low][9], grad_low).astype(bf16)
    gu0 = dot_tn(caches[low][8], du).astype(bf16)
    lse, gd0, gu0, xq1, ao1 = hold(caches[low][6], gd0, gu0, xq1, ao1)
    hq1 = summed(gq1, xq1)
    ad0 = over(gd0)
    xu0 = beside(gu0)
    buffer = place_tiles(("down", top), gd1, ad1, None)
    buffer = place_tiles(("up", top), gu1, au1, buffer)
    grad, grad_low, dq, dk, dv, dbo = attend_step(low, grad, part, other, lse)
    vec, dbo, ad0, xu0, hq1, buffer = hold(vec, dbo, ad0, xu0, hq1, buffer)
    au0 = over(summed(gu0, xu0))
    aq1 = over(hq1)
    own, dg1, ds1, dbq, dbv = qkv_back_call(low, dq, dk, dv, caches[low][0], vec, weights)
    recv = send(own, routes.core_all)
    gq0 = dot_tn(caches[low][1], jnp.concatenate([dq, dk, dv], axis=1)).astype(bf16)
    vec_grads[low] = [dg1, ds1, dbq, dbv, dbo, dg2, ds2, db1, db2]
    xq0 = beside(gq0)
    grad_emb, grad_emb_bias = embed_back_call(core_flag, grad, own, recv)
    middle = CHUNKS // 2

    def base_grad(parts):
        return jnp.concatenate([dot_tn(c, grad_emb).astype(bf16) for c in parts], axis=0)

    gbt = base_grad(chunks[middle:])
    gbt, au0, xq0 = hold(gbt, au0, xq0)
    xb = send(gbt, routes.x_away) if grid3 else None
    aq0 = over(summed(gq0, xq0))
    gbm = base_grad(chunks[:middle])
    vec_grad = pack_call([grad_emb_bias] + vec_grads[0] + vec_grads[1], dp_n, vec_per)
    go0 = dot_tn(caches[low][5], grad_low).astype(bf16)
    ao0, av = over(go0), over(vec_grad)
    gbm, xb, aq0, ao0, av, aq1, buffer = hold(gbm, xb, aq0, ao0, av, aq1, buffer)
    ab = over(half_sum(half_at * 0, gbm, xb)) if grid3 else None
    buffer = place_tiles(("out", top), go1, ao1, buffer)
    buffer = place_tiles(("qkv", top), gq1, aq1, buffer)
    buffer = place_tiles(("down", low), gd0, ad0, buffer)
    buffer = place_tiles(("up", low), gu0, au0, buffer)
    buffer = place_base(1, gbt, None, buffer)
    buffer = place_tiles(("out", low), go0, ao0, buffer)
    buffer = scatter_vec(vec_pos, vec_grad, av, buffer)
    buffer = place_tiles(("qkv", low), gq0, aq0, buffer)
    base_weight = weights["base", 0]
    ab, buffer, base_weight, out_low = hold(ab, buffer, base_weight, out_low)
    weights["base", 0] = base_weight
    buffer = place_base(0, gbm, ab, buffer)

    if grid3:
        token = jnp.zeros((8, BS), f32)
        order = (1, 0)
        resized = resize_call(weights, pinv)
        carried = {n: None for n in order}
        across = {n: send(buffer.reshape(4, 2, 2, payload, BS)[0, 1, n], routes.x_home) for n in order}
        rounded = {}
        for j in range(4):
            for n in order:
                extra = None
                if j == 0 and n == order[0]:
                    extra = resized
                token, across[n], carried[n], extra = hold(token, across[n], carried[n], extra)
                if extra is not None:
                    resized = extra
                total, later = reduce_call(j, n, buffer, across[n], carried[n], payload)
                if j < 3:
                    carried[n] = send(total, routes.z_home)
                    across[n] = send(later, routes.x_home)
                else:
                    rounded[n] = total
        near_grad, far_grad = rounded[0], send(rounded[1], routes.core_out)
    else:
        held = buffer.reshape(dp_n, 1, payload, BS).astype(f32)
        nothing = jnp.zeros_like(held)
        both = jnp.concatenate(
            [jnp.where(core == 0, held, nothing), jnp.where(core == 0, nothing, held)], axis=1
        )
        used_rows = jnp.repeat(used, BS).reshape(dp_n, 1, slots_per * BS, 1)
        used_rows = jnp.concatenate(
            [used_rows, jnp.ones((dp_n, 1, VEC_ROWS, 1), bool)], axis=2
        )
        both = jnp.where(used_rows, both, 0.0).reshape(dp_n * TENSOR * payload, BS)
        near_grad = lax.psum_scatter(both, AXES, scatter_dimension=0, tiled=True).astype(bf16)
        far_grad = near_grad
        resized = resize_call(weights, pinv)

    output = jnp.where(home, out_low, send(out_low, routes.y_out)).astype(f32)
    grad_pixels = sum(
        dot(grad_emb * select_low[:, s : s + 1], resized[s]) for s in range(3)
    ).astype(bf16)
    pixels_other = send(grad_pixels, routes.core_all)
    pixel_sides = [
        grad_pixels[:, s * HALF : (s + 1) * HALF].astype(f32)
        + pixels_other[:, s * HALF : (s + 1) * HALF].astype(f32)
        for s in range(TENSOR)
    ]
    near = jnp.where(core == 0, pixel_sides[0], pixel_sides[1])
    far = jnp.where(core == 0, pixel_sides[1], pixel_sides[0]).astype(bf16)
    patch_grad = jnp.where(home, near, send(far, routes.y_out).astype(f32))

    my_slots = dp_pos * slots_per + jnp.arange(slots_per)
    mine_used = jnp.any(own_slots[None, :] == my_slots[:, None], axis=1).astype(jnp.int32)
    owned_grad, new_master, new_mom, new_var = owner_call(
        mine_used, flag, near_grad, far_grad, master_slots[0], left_basis[0], right_basis[0], mom_slots[0], var_slots[0]
    )
    vec_rows = jnp.where(home, near_grad[slots_per * BS :], far_grad[slots_per * BS :])
    owned_vec_grad = vec_rows.astype(f32).reshape(VEC_ROWS * BS)[:vec_per]
    new_vec_mom = decay * vec_mom[0] + (1.0 - decay) * owned_vec_grad
    new_vec_var = decay * vec_var[0] + (1.0 - decay) * owned_vec_grad * owned_vec_grad
    new_vec = vec_master[0] - vector_rate * new_vec_mom / (jnp.sqrt(new_vec_var) + adam_eps)
    return (
        output,
        patch_grad,
        owned_grad[None],
        new_master[None],
        new_mom[None],
        new_var[None],
        owned_vec_grad[None],
        new_vec[None],
        new_vec_mom[None],
        new_vec_var[None],
    )


def solution(mesh):
    slots = P("tensor", "dp", None, None)
    vectors = P("tensor", "dp")
    tokens = P("dp", None)
    in_specs = (tokens, tokens, tokens, P("tensor", None), P()) + (slots,) * 5 + (vectors,) * 3
    out_specs = (tokens, P("dp", "tensor")) + (slots,) * 4 + (vectors,) * 4
    return jax.shard_map(shards, mesh=mesh, in_specs=in_specs, out_specs=out_specs, check_vma=False)
```

```python
import functools

import jax
import jax.numpy as jnp
import numpy as np
from jax import lax
from jax.experimental import pallas as pl
from jax.experimental.pallas import tpu as pltpu
from jax.sharding import PartitionSpec as P

D = 768
HEAD_DIM = 64
FF = 3072
BASE_PIX = 3072
LAYERS = 2
LEN_A = 196
LEN_B = 225
LEN_C = 576
IMG_DEV = 5
BS = 128
TENSOR = 2
HALF = D // TENSOR
HALF_FF = FF // TENSOR
HEADS = HALF // HEAD_DIM
ROWS = 256
KEYS = 512
VEC_ROWS = 16
CHUNKS = 4

AXES = ("dp", "tensor")
precise = lax.Precision.HIGHEST
masked_score = -1e30
norm_eps = 1e-06
adam_eps = 1e-08
decay = 0.5
matrix_rate = 0.05
vector_rate = 0.3
f32 = jnp.float32
bf16 = jnp.bfloat16
MIB = 1024 * 1024

WEIGHTS = [("base", 0, BASE_PIX)]
for layer in range(LAYERS):
    WEIGHTS += [("qkv", layer, 3 * D), ("out", layer, D), ("up", layer, FF), ("down", layer, FF)]
STARTS = {}
PANEL_ROWS = 0
for name, layer, size in WEIGHTS:
    STARTS[name, layer] = PANEL_ROWS
    PANEL_ROWS += size


def tile_targets():
    rows, cols = [], []

    def add(start, rows_n, cols_n):
        for i in range(rows_n // BS):
            for j in range(cols_n // BS):
                panel, inner = divmod(j * BS, HALF)
                rows.append(start + panel * rows_n + i * BS)
                cols.append(inner)

    add(STARTS["base", 0], BASE_PIX, HALF)
    for layer in range(LAYERS):
        add(STARTS["qkv", layer], D, 3 * HALF)
        add(STARTS["out", layer], HALF, D)
        add(STARTS["up", layer], D, HALF_FF)
        add(STARTS["down", layer], HALF_FF, D)
    return np.array(rows, np.int32), np.array(cols, np.int32)


TARGET_ROW, TARGET_COL = tile_targets()
LAYER_VECS = (D, D, HALF, HALF, D, D, D, HALF_FF, D)
VEC_NAMES = ("g1", "s1", "bq", "bv", "bo", "g2", "s2", "b1", "b2")


def vec_offsets():
    offset = HALF
    found = []
    for layer in range(LAYERS):
        here = {}
        for name, length in zip(VEC_NAMES, LAYER_VECS):
            here[name] = (offset, length)
            offset += length
        found.append(here)
    return found


VEC_AT = vec_offsets()


def params(limit=24):
    return pltpu.CompilerParams(
        dimension_semantics=("arbitrary",), vmem_limit_bytes=limit * MIB
    )


def cost(flops, nbytes, trans=0):
    return pl.CostEstimate(flops=flops, bytes_accessed=nbytes, transcendentals=trans)


def rows_spec(width):
    return pl.BlockSpec((ROWS, width), lambda i, *_: (i, 0))


def fixed(shape, at=0):
    return pl.BlockSpec(shape, lambda i, *_: (at,) + (0,) * (len(shape) - 1))


def vec_piece(vec_ref, layer, name):
    start, length = VEC_AT[layer][name]
    return vec_ref[:, start : start + length]


def dot(left, right):
    return jnp.dot(left, right, preferred_element_type=f32)


def dot_nt(left, right, precision=None):
    return lax.dot_general(
        left, right, (((1,), (1,)), ((), ())), precision=precision, preferred_element_type=f32
    )


def dot_tn(left, right):
    return lax.dot_general(left, right, (((0,), (0,)), ((), ())), preferred_element_type=f32)


def joined(ref, start, rows_n, panels, stride=None):
    stride = rows_n if stride is None else stride
    return jnp.concatenate(
        [ref[pl.ds(start + p * stride, rows_n), :] for p in range(panels)], axis=1
    )


def part_at(half, part):
    return lax.rem(part + half[0], 2)


def swapped(half, values):
    size = values.shape[1] // 2
    left, right = values[:, :size], values[:, size:]
    first = half[0] == 0
    return jnp.where(first, left, right), jnp.where(first, right, left)


def norm_stats(values):
    mean_val = jnp.mean(values, axis=-1, keepdims=True)
    centered = values - mean_val
    inv_std = lax.rsqrt(jnp.mean(centered * centered, axis=-1, keepdims=True) + norm_eps)
    return centered * inv_std, inv_std


def norm_back(values, gain, grad):
    unit, inv_std = norm_stats(values)
    scaled = grad * gain
    mean_s = jnp.mean(scaled, axis=-1, keepdims=True)
    mean_u = jnp.mean(scaled * unit, axis=-1, keepdims=True)
    back = inv_std * (scaled - mean_s - unit * mean_u)
    return (
        back,
        jnp.sum(grad * unit, axis=0, keepdims=True),
        jnp.sum(grad, axis=0, keepdims=True),
    )


def accumulate(ref, value):
    first = pl.program_id(0) == 0

    @pl.when(first)
    def _():
        ref[...] = value

    @pl.when(jnp.logical_not(first))
    def _():
        ref[...] += value


def stay(value):
    return pltpu.with_memory_space_constraint(value, pltpu.HBM)


def fence(*arrays):
    def nothing(*refs):
        pass

    anywhere = pl.BlockSpec(memory_space=pl.ANY)
    return pl.pallas_call(
        nothing,
        out_shape=[jax.ShapeDtypeStruct(a.shape, a.dtype) for a in arrays],
        in_specs=[anywhere] * len(arrays),
        out_specs=[anywhere] * len(arrays),
        input_output_aliases={i: i for i in range(len(arrays))},
        compiler_params=pltpu.CompilerParams(vmem_limit_bytes=MIB),
    )(*[stay(a) if a.size > 32 * 1024 else a for a in arrays])


def gather_kernel(slots, count_a, count_b, owner, drow, dcol, flag, *refs):
    first = refs[:count_a]
    second = refs[count_a : count_a + count_b]
    *panels, vectors, held, sem, vec_sem = refs[count_a + count_b :]

    def copy_all(sources):
        at = 0
        for src in sources:
            for n in range(src.shape[0]):
                who = owner[at]
                at += 1

                def body(i, carried, src=src, n=n, who=who):
                    slot = who * slots + i
                    row = drow[slot]

                    @pl.when(row >= 0)
                    def _():
                        start = pl.multiple_of(i * BS, BS)
                        pltpu.make_async_copy(
                            src.at[n, pl.ds(start, BS), :],
                            held.at[
                                pl.ds(pl.multiple_of(row, BS), BS),
                                pl.ds(pl.multiple_of(dcol[slot], BS), BS),
                            ],
                            sem,
                        ).start()

                    return carried

                lax.fori_loop(0, slots, body, 0)
                pltpu.make_async_copy(
                    src.at[n, pl.ds(slots * BS, VEC_ROWS), :], vectors.at[who], vec_sem
                ).start()

    if count_b:

        @pl.when(flag[0] == 1)
        def _():
            copy_all(first)

        @pl.when(flag[0] == 0)
        def _():
            copy_all(second)
    else:
        copy_all(first)
    pltpu.make_async_copy(held, held, sem).wait()
    at = 0
    for panel in panels:
        size = panel.shape[0]
        pltpu.make_async_copy(held.at[pl.ds(at, size), :], panel, sem).start()
        at += size
    pltpu.make_async_copy(vectors, vectors, vec_sem).wait()
    pltpu.make_async_copy(held, held, sem).wait()


def gather_tiles(first, second, owner, drow, dcol, flag, slots, owners):
    anywhere = pl.BlockSpec(memory_space=pl.ANY)
    *panels, vectors = pl.pallas_call(
        functools.partial(gather_kernel, slots, len(first), len(second)),
        out_shape=[pltpu.HBM((size, HALF), bf16) for unused, unused2, size in WEIGHTS]
        + [jax.ShapeDtypeStruct((owners, VEC_ROWS, BS), bf16)],
        grid_spec=pltpu.PrefetchScalarGridSpec(
            num_scalar_prefetch=4,
            grid=(1,),
            in_specs=[anywhere] * (len(first) + len(second)),
            out_specs=[anywhere] * len(WEIGHTS) + [fixed((owners, VEC_ROWS, BS))],
            scratch_shapes=[
                pltpu.VMEM((PANEL_ROWS, HALF), bf16),
                pltpu.SemaphoreType.DMA,
                pltpu.SemaphoreType.DMA,
            ],
        ),
        compiler_params=params(),
        cost_estimate=cost(0, 4 * PANEL_ROWS * HALF),
    )(owner, drow, dcol, flag, *[stay(v) for v in first], *[stay(v) for v in second])
    return {(name, layer): p for (name, layer, unused), p in zip(WEIGHTS, panels)}, vectors


def scatter_kernel(rows_n, cols_n, steps, paired, parts, pos, part, own, *refs):
    @pl.when(part[1] > 0)
    def _():
        scatter_body(rows_n, cols_n, steps, paired, parts, pos, part, own, *refs)


def scatter_body(rows_n, cols_n, steps, paired, parts, pos, part, own, *refs):
    if paired:
        recv, *refs = refs
        span = pl.num_programs(0) // parts
        here = jnp.logical_or(parts == 1, pl.program_id(0) // span == part[0])
    target, buf, sems = refs[-3:]
    step = pl.program_id(0)
    slot = lax.rem(step, 2)
    per = rows_n // BS * (cols_n // BS)

    def wait(at):
        pltpu.make_async_copy(buf.at[at], buf.at[at], sems.at[at]).wait()

    @pl.when(step >= 2)
    def _():
        wait(slot)

    for i in range(rows_n // BS):
        for j in range(cols_n // BS):
            area = (slice(i * BS, (i + 1) * BS), slice(j * BS, (j + 1) * BS))
            value = own[area]
            if paired:
                more = jnp.where(here, recv[area].astype(f32), 0.0)
                value = (value.astype(f32) + more).astype(bf16)
            buf[slot, i * (cols_n // BS) + j] = value
    for n in range(per):
        pltpu.make_async_copy(
            buf.at[slot, n],
            target.at[pl.ds(pl.multiple_of(pos[step * per + n], 16), BS), :],
            sems.at[slot],
        ).start()

    @pl.when(step == pl.num_programs(0) - 1)
    def _():
        if steps > 1:
            wait(1 - slot)
        wait(slot)


def scatter_matrix(pos, own, recv, part, target, total_rows, rows_n):
    cols_n = own.shape[1]
    steps = own.shape[0] // rows_n
    anywhere = pl.BlockSpec(memory_space=pl.ANY)
    block = pl.BlockSpec((rows_n, cols_n), lambda i, *_: (i, 0))
    paired = recv is not None
    parts = own.shape[0] // recv.shape[0] if paired else 1
    span = steps // parts
    arrived = pl.BlockSpec(
        (rows_n, cols_n), lambda i, pos, part: (jnp.clip(i - part[0] * span, 0, span - 1), 0)
    )
    operands = [stay(own)] + ([stay(recv)] if paired else []) + ([] if target is None else [stay(target)])
    specs = [block] + ([block if parts == 1 else arrived] if paired else [])
    specs += [] if target is None else [anywhere]
    return pl.pallas_call(
        functools.partial(scatter_kernel, rows_n, cols_n, steps, paired, parts),
        out_shape=pltpu.HBM((total_rows, BS), bf16),
        grid_spec=pltpu.PrefetchScalarGridSpec(
            num_scalar_prefetch=2,
            grid=(steps,),
            in_specs=specs,
            out_specs=anywhere,
            scratch_shapes=[
                pltpu.VMEM((2, rows_n // BS * (cols_n // BS), BS, BS), bf16),
                pltpu.SemaphoreType.DMA((2,)),
            ],
        ),
        input_output_aliases={} if target is None else {len(operands) + 1: 0},
        compiler_params=params(12),
        cost_estimate=cost(own.size, own.size * 6),
    )(pos, part, *operands)


def scatter_vec_kernel(paired, pos, own, *refs):
    if paired:
        recv, *refs = refs
    target, buf, sem = refs[-3:]
    value = own[...]
    if paired:
        value = (value.astype(f32) + recv[...].astype(f32)).astype(bf16)
    buf[...] = value

    def body(n, carried):
        pltpu.make_async_copy(
            buf.at[n], target.at[pl.ds(pl.multiple_of(pos[n], 16), VEC_ROWS), :], sem
        ).start()
        return carried

    lax.fori_loop(0, own.shape[0], body, 0)
    pltpu.make_async_copy(buf, buf, sem).wait()


def scatter_vec(pos, own, recv, target):
    anywhere = pl.BlockSpec(memory_space=pl.ANY)
    block = fixed(own.shape)
    paired = recv is not None
    operands = [own] + ([recv] if paired else []) + [stay(target)]
    return pl.pallas_call(
        functools.partial(scatter_vec_kernel, paired),
        out_shape=pltpu.HBM(target.shape, bf16),
        grid_spec=pltpu.PrefetchScalarGridSpec(
            num_scalar_prefetch=1,
            grid=(1,),
            in_specs=[block] * (len(operands) - 1) + [anywhere],
            out_specs=anywhere,
            scratch_shapes=[pltpu.VMEM(own.shape, bf16), pltpu.SemaphoreType.DMA],
        ),
        input_output_aliases={len(operands): 0},
        compiler_params=params(4),
    )(pos, *operands)


def expand_kernel(present, half, patch_ref, class_ref, pinv_ref, out, total):
    for block in range(patch_ref.shape[0] // ROWS):
        rows = slice(block * ROWS, (block + 1) * ROWS)
        total[...] = jnp.zeros_like(total)
        for which in range(3):

            @pl.when(present[block, which] > 0)
            def _(which=which, rows=rows):
                chosen = jnp.where(class_ref[rows, :] == which, patch_ref[rows, :].astype(f32), 0.0)
                total[...] += dot_nt(chosen.astype(bf16), pinv_ref[which])

        out[rows, :] = total[...].astype(bf16)


def expand_call(which, present, half, patches, class_col, pinv):
    tokens = patches.shape[0]
    size = BASE_PIX // CHUNKS
    step = size
    return pl.pallas_call(
        expand_kernel,
        out_shape=jax.ShapeDtypeStruct((tokens, size), bf16),
        grid_spec=pltpu.PrefetchScalarGridSpec(
            num_scalar_prefetch=2,
            grid=(1,),
            in_specs=[
                fixed(patches.shape),
                fixed(class_col.shape),
                pl.BlockSpec(
                    (3, step, pinv.shape[2]),
                    lambda i, present, half: (0, (which + half[0] * (CHUNKS // 2)) % CHUNKS, 0),
                ),
            ],
            out_specs=pl.BlockSpec((tokens, step), lambda i, *_: (0, i)),
            scratch_shapes=[pltpu.VMEM((ROWS, step), f32)],
        ),
        compiler_params=params(),
        cost_estimate=cost(3 * tokens * size * D, tokens * size * 4 + size * D * 6),
    )(present, half, patches, class_col, stay(pinv))


def resize_kernel(base, pinv_ref, out, turned):
    @pl.when(pl.program_id(0) == 0)
    def _():
        turned[...] = base[...].T

    out[0] = dot(turned[...], pinv_ref[0]).astype(bf16)


def resize_call(weights, pinv):
    return pl.pallas_call(
        resize_kernel,
        out_shape=jax.ShapeDtypeStruct((3, HALF, pinv.shape[2]), bf16),
        grid=(3,),
        in_specs=[
            fixed((BASE_PIX, HALF)),
            pl.BlockSpec((1, BASE_PIX, pinv.shape[2]), lambda i: (i, 0, 0)),
        ],
        out_specs=pl.BlockSpec((1, HALF, pinv.shape[2]), lambda i: (i, 0, 0)),
        scratch_shapes=[pltpu.VMEM((HALF, BASE_PIX), bf16)],
        compiler_params=params(),
        cost_estimate=cost(6 * D * BASE_PIX * HALF, 6 * D * BASE_PIX),
    )(stay(weights["base", 0]), stay(pinv))


def embed_back_kernel(core, base, own, recv, out, bias):
    low = (base[...] + (own[...].astype(f32) + recv[...].astype(f32))).astype(bf16)
    out[...] = low
    accumulate(bias, jnp.sum(low.astype(f32), axis=0, keepdims=True))


def embed_back_call(core, base, own, recv):
    tokens = base.shape[0]
    half = pl.BlockSpec((ROWS, HALF), lambda i, core: (i, core[0]))
    return pl.pallas_call(
        embed_back_kernel,
        out_shape=[
            jax.ShapeDtypeStruct((tokens, HALF), bf16),
            jax.ShapeDtypeStruct((1, HALF), f32),
        ],
        grid_spec=pltpu.PrefetchScalarGridSpec(
            num_scalar_prefetch=1,
            grid=(tokens // ROWS,),
            in_specs=[half] * 3,
            out_specs=[rows_spec(HALF), fixed((1, HALF))],
        ),
        compiler_params=params(8),
        cost_estimate=cost(tokens * D, tokens * D * 5),
    )(core, base, own, recv)


def pack_kernel(vec_per, *refs):
    *pieces, out = refs
    out[...] = jnp.zeros_like(out)
    at = 0
    for piece in pieces:
        for k in range(piece.shape[1] // BS):
            owner, row = divmod(at, vec_per // BS)
            out[owner, row : row + 1, :] = piece[:, k * BS : (k + 1) * BS]
            at += 1


def pack_call(pieces, owners, vec_per):
    if vec_per % BS:
        joined = jnp.concatenate(pieces, axis=1)[0]
        joined = jnp.pad(joined, (0, owners * vec_per - joined.shape[0])).reshape(owners, vec_per)
        joined = jnp.pad(joined, ((0, 0), (0, VEC_ROWS * BS - vec_per)))
        return joined.astype(bf16).reshape(owners, VEC_ROWS, BS)
    return pl.pallas_call(
        functools.partial(pack_kernel, vec_per),
        out_shape=jax.ShapeDtypeStruct((owners, VEC_ROWS, BS), f32),
        grid=(1,),
        in_specs=[fixed(p.shape) for p in pieces],
        out_specs=fixed((owners, VEC_ROWS, BS)),
        compiler_params=params(4),
        cost_estimate=cost(0, owners * vec_per * 8),
    )(*pieces).astype(bf16)


def embed_kernel(half, *refs):
    *parts, vec, weight, out = refs
    size = BASE_PIX // CHUNKS
    total = vec[:, :HALF]
    for c in range(CHUNKS):
        at = lax.rem(c + half[0] * (CHUNKS // 2), CHUNKS)
        rows = pl.ds(pl.multiple_of(at * size, size), size)
        total = total + dot(parts[c][...], weight[rows, :])
    out[...] = total.astype(bf16)


def embed_call(half, chunks, vec, weights):
    tokens = chunks[0].shape[0]
    return pl.pallas_call(
        embed_kernel,
        out_shape=jax.ShapeDtypeStruct((tokens, HALF), bf16),
        grid_spec=pltpu.PrefetchScalarGridSpec(
            num_scalar_prefetch=1,
            grid=(tokens // ROWS,),
            in_specs=[rows_spec(BASE_PIX // CHUNKS)] * CHUNKS
            + [fixed(vec.shape), fixed((BASE_PIX, HALF))],
            out_specs=rows_spec(HALF),
        ),
        compiler_params=params(),
        cost_estimate=cost(2 * tokens * BASE_PIX * HALF, tokens * BASE_PIX * 3),
    )(half, *[stay(c) for c in chunks], vec, stay(weights["base", 0]))


def qkv_kernel(layer, first, core, half, *refs):
    if first:
        own, recv, vec, weight, hid, normed_m, normed_t, q_ref, k_ref, v_ref = refs
        mine, theirs = own[...].astype(f32), recv[...].astype(f32)
        low = core[0] == 0
        values = jnp.concatenate(
            [jnp.where(low, mine, theirs), jnp.where(low, theirs, mine)], axis=1
        )
    else:
        base, own, recv, vec, weight, hid, normed_m, normed_t, q_ref, k_ref, v_ref = refs
        values = base[...] + (own[...].astype(f32) + recv[...].astype(f32))
    hid[...] = values
    unit, unused = norm_stats(values)
    low = unit * vec_piece(vec, layer, "g1") + vec_piece(vec, layer, "s1")
    halves = swapped(half, low)
    normed_m[...] = halves[0].astype(bf16)
    normed_t[...] = halves[1].astype(bf16)
    low = low.astype(bf16)
    made = dot(low, joined(weight, 0, D, 3))
    q_ref[...] = (made[:, :HALF] + vec_piece(vec, layer, "bq")).astype(bf16)
    k_ref[...] = made[:, HALF : 2 * HALF].astype(bf16)
    v_ref[...] = (made[:, 2 * HALF :] + vec_piece(vec, layer, "bv")).astype(bf16)


def qkv_call(layer, base, own, recv, core, half, vec, weights):
    tokens = own.shape[0]
    shape = lambda width, kind: jax.ShapeDtypeStruct((tokens, width), kind)
    outs = [shape(D, f32)] + [pltpu.HBM((tokens, HALF), bf16)] * 2 + [shape(HALF, bf16)] * 3
    operands = ([] if base is None else [base]) + [own, recv]
    return pl.pallas_call(
        functools.partial(qkv_kernel, layer, base is None),
        out_shape=outs,
        grid_spec=pltpu.PrefetchScalarGridSpec(
            num_scalar_prefetch=2,
            grid=(tokens // ROWS,),
            in_specs=[rows_spec(o.shape[1]) for o in operands]
            + [fixed(vec.shape), fixed((3 * D, HALF))],
            out_specs=[rows_spec(o.shape[1]) for o in outs],
        ),
        compiler_params=params(),
        cost_estimate=cost(2 * tokens * D * 3 * HALF, tokens * D * 14),
    )(core, half, *operands, vec, weights["qkv", layer])


def head_masks():
    lane = lax.broadcasted_iota(jnp.int32, (1, 2 * HEAD_DIM), 1)
    low = (lane < HEAD_DIM).astype(f32).astype(bf16)
    high = (lane >= HEAD_DIM).astype(f32).astype(bf16)
    return low, high


def attend_kernel(
    layer, low_ref, high_ref, q_ref, k_ref, v_ref, seg_q, seg_k, vec, w_out, o_ref, lse_ref, part,
    scores_ref, top_ref, acc_ref,
):
    step = pl.program_id(0)
    first, last = low_ref[step], high_ref[step]
    masks = head_masks()
    scale = jnp.asarray(HEAD_DIM ** (-0.5), bf16)
    lane = lax.broadcasted_iota(jnp.int32, (1, BS), 1)
    sums = [(lane == HEAD_DIM).astype(f32).astype(bf16), (lane == 0).astype(f32).astype(bf16)]
    top_ref[...] = jnp.full(top_ref.shape, masked_score, f32)
    acc_ref[...] = jnp.zeros_like(acc_ref)
    seg_col = seg_q[...]

    def score_block(block, carried):
        rows = pl.ds(pl.multiple_of(block * ROWS, ROWS), ROWS)
        same = seg_col == seg_k[:, rows]
        for pair in range(HEADS // 2):
            cols = slice(pair * BS, (pair + 1) * BS)
            q_two = q_ref[:, cols] * scale
            k_two = k_ref[rows, cols]
            for side in range(2):
                head = 2 * pair + side
                scores = jnp.where(same, dot_nt(q_two * masks[side], k_two), masked_score)
                scores_ref[head, block] = scores
                top = top_ref[head]
                for piece in range(ROWS // BS):
                    top = jnp.maximum(top, scores[:, piece * BS : (piece + 1) * BS])
                top_ref[head] = top
        return carried

    lax.fori_loop(first, last, score_block, 0)
    tops = [jnp.max(top_ref[head], axis=1, keepdims=True) for head in range(HEADS)]

    def mix_block(block, carried):
        rows = pl.ds(pl.multiple_of(block * ROWS, ROWS), ROWS)
        for pair in range(HEADS // 2):
            v_two = v_ref[rows, pair * BS : (pair + 1) * BS]
            for side in range(2):
                head = 2 * pair + side
                expo = jnp.exp(scores_ref[head, block] - tops[head]).astype(bf16)
                acc_ref[head] += dot(expo, v_two * masks[side] + sums[side])
        return carried

    lax.fori_loop(first, last, mix_block, 0)
    totals = jnp.zeros((ROWS, BS), f32)
    for pair in range(HEADS // 2):
        sides = []
        for side in range(2):
            head = 2 * pair + side
            mixed = acc_ref[head]
            at = HEAD_DIM * (1 - side)
            total = mixed[:, at : at + 1]
            totals = jnp.where(lane == head, tops[head] + jnp.log(total), totals)
            sides.append(mixed * (1.0 / total))
        o_ref[:, pair * BS : (pair + 1) * BS] = jnp.where(lane < HEAD_DIM, *sides).astype(bf16)
    lse_ref[...] = totals.T[0:8, :]
    low = o_ref[...]
    bias = vec_piece(vec, layer, "bo")
    part[...] = (dot(low, joined(w_out, 0, HALF, TENSOR)) + bias).astype(bf16)


def attend_call(layer, first, last, queries, keys, values, seg_col, seg_row, vec, weights):
    tokens = queries.shape[0]
    return pl.pallas_call(
        functools.partial(attend_kernel, layer),
        out_shape=[
            jax.ShapeDtypeStruct((tokens, HALF), bf16),
            jax.ShapeDtypeStruct((8, tokens), f32),
            jax.ShapeDtypeStruct((tokens, D), bf16),
        ],
        grid_spec=pltpu.PrefetchScalarGridSpec(
            num_scalar_prefetch=2,
            grid=(tokens // ROWS,),
            in_specs=[
                rows_spec(HALF),
                fixed(keys.shape),
                fixed(values.shape),
                rows_spec(1),
                fixed(seg_row.shape),
                fixed(vec.shape),
                fixed((D, HALF)),
            ],
            out_specs=[
                rows_spec(HALF),
                pl.BlockSpec((8, ROWS), lambda i, *_: (0, i)),
                rows_spec(D),
            ],
            scratch_shapes=[
                pltpu.VMEM((HEADS, tokens // ROWS, ROWS, ROWS), f32),
                pltpu.VMEM((HEADS, ROWS, BS), f32),
                pltpu.VMEM((HEADS, ROWS, BS), f32),
            ],
        ),
        compiler_params=params(),
        cost_estimate=cost(8 * HEADS * tokens * tokens * BS, tokens * D * 8, HEADS * tokens * tokens),
    )(first, last, queries, keys, values, seg_col, seg_row, vec, weights["out", layer])


def gelu_parts(values):
    cdf = 0.5 * (1.0 + lax.erf(values * 0.7071067811865476))
    pdf = 0.3989422804014327 * jnp.exp(-0.5 * values * values)
    return values * cdf, cdf + values * pdf


def mlp_kernel(
    layer, half, base, own, recv, vec, w_up, w_down, hid, normed, act_m, act_t, slope, part
):
    values = base[...] + (own[...].astype(f32) + recv[...].astype(f32))
    hid[...] = values
    unit, unused = norm_stats(values)
    low = (unit * vec_piece(vec, layer, "g2") + vec_piece(vec, layer, "s2")).astype(bf16)
    normed[...] = low
    biases = swapped(half, vec_piece(vec, layer, "b1"))
    down = vec_piece(vec, layer, "b2")
    for which, act in enumerate((act_m, act_t)):
        at = part_at(half, which)
        up = dot(low, joined(w_up, pl.multiple_of(at * 2 * D, D), D, 2)) + biases[which]
        gelu, grad = gelu_parts(up)
        units = gelu.astype(bf16)
        act[...] = units
        slope[:, which * D : (which + 1) * D] = grad.astype(bf16)
        down = down + dot(units, joined(w_down, pl.multiple_of(at * D, D), D, TENSOR, HALF_FF))
    part[...] = down.astype(bf16)


def mlp_call(layer, half, base, own, recv, vec, weights):
    tokens = base.shape[0]
    shape = lambda width, kind: jax.ShapeDtypeStruct((tokens, width), kind)
    kept = lambda width: pltpu.HBM((tokens, width), bf16)
    outs = [shape(D, f32), kept(D), kept(D), kept(D), kept(HALF_FF), shape(D, bf16)]
    return pl.pallas_call(
        functools.partial(mlp_kernel, layer),
        out_shape=outs,
        grid_spec=pltpu.PrefetchScalarGridSpec(
            num_scalar_prefetch=1,
            grid=(tokens // ROWS,),
            in_specs=[rows_spec(D)] * 3
            + [fixed(vec.shape), fixed((2 * HALF_FF, HALF)), fixed((2 * HALF_FF, HALF))],
            out_specs=[rows_spec(o.shape[1]) for o in outs],
        ),
        compiler_params=params(),
        cost_estimate=cost(4 * tokens * D * HALF_FF, tokens * D * 24, 2 * tokens * HALF_FF),
    )(half, base, own, recv, vec, weights["up", layer], weights["down", layer])


def mlp_back_kernel(layer, summed, half, *refs):
    if summed:
        base, own, recv, *refs = refs
        (hid, slope, vec, w_up, w_down, grad_full, grad_low, du_m, du_t, back, dgain, dshift, db1, db2) = refs
        values = base[...].astype(f32) + (own[...].astype(f32) + recv[...].astype(f32))
        grad_full[...] = values
        low = values.astype(bf16)
    else:
        base, valid, *refs = refs
        (hid, slope, vec, w_up, w_down, grad_low, du_m, du_t, back, dgain, dshift, db1, db2) = refs
        low = (base[...].astype(f32) * valid[...]).astype(bf16)
    grad_low[...] = low
    accumulate(db2, jnp.sum(low.astype(f32), axis=0, keepdims=True))
    grad_normed = None
    sums = []
    for which, out in enumerate((du_m, du_t)):
        at = part_at(half, which)
        rows = joined(w_down, pl.multiple_of(at * D, D), D, TENSOR, HALF_FF)
        grads = dot_nt(low, rows) * slope[:, which * D : (which + 1) * D].astype(f32)
        grads = grads.astype(bf16)
        out[...] = grads
        sums.append(jnp.sum(grads.astype(f32), axis=0, keepdims=True))
        term = dot_nt(grads, joined(w_up, pl.multiple_of(at * 2 * D, D), D, 2))
        grad_normed = term if grad_normed is None else grad_normed + term
    accumulate(db1, jnp.concatenate(swapped(half, jnp.concatenate(sums, axis=1)), axis=1))
    part_back, gain_grad, shift_grad = norm_back(hid[...], vec_piece(vec, layer, "g2"), grad_normed)
    back[...] = part_back.astype(bf16)
    accumulate(dgain, gain_grad)
    accumulate(dshift, shift_grad)


def mlp_back_call(layer, half, base, own, recv, valid, hid, slope, vec, weights):
    tokens = base.shape[0]
    summed = own is not None
    shape = lambda width, kind: jax.ShapeDtypeStruct((tokens, width), kind)
    line = lambda width: jax.ShapeDtypeStruct((1, width), f32)
    outs = ([shape(D, f32)] if summed else []) + [shape(D, bf16)] * 4
    lines = [line(D), line(D), line(HALF_FF), line(D)]
    extra = [own, recv] if summed else [valid]
    return pl.pallas_call(
        functools.partial(mlp_back_kernel, layer, summed),
        out_shape=outs + lines,
        grid_spec=pltpu.PrefetchScalarGridSpec(
            num_scalar_prefetch=1,
            grid=(tokens // ROWS,),
            in_specs=[rows_spec(D)]
            + [rows_spec(e.shape[1]) for e in extra]
            + [rows_spec(D), rows_spec(HALF_FF), fixed(vec.shape)]
            + [fixed((2 * HALF_FF, HALF))] * 2,
            out_specs=[rows_spec(o.shape[1]) for o in outs] + [fixed(o.shape) for o in lines],
        ),
        compiler_params=params(),
        cost_estimate=cost(4 * tokens * D * HALF_FF, tokens * D * 24),
    )(half, base, *extra, stay(hid), stay(slope), vec, weights["up", layer], weights["down", layer])


def attend_back_kernel(
    low_ref, high_ref, half, base, own, recv, q_ref, k_ref, v_ref, o_ref, lse_ref, seg_k, seg_q, w_out,
    full_ref, low_m, low_t, dq_ref, dk_ref, dv_ref, dbo, dk_acc, dv_acc, dq_acc, do_ref,
):
    step = pl.program_id(0)

    @pl.when(step == 0)
    def _():
        dk_acc[...] = jnp.zeros_like(dk_acc)
        dv_acc[...] = jnp.zeros_like(dv_acc)

    values = base[...].astype(f32) + (own[...].astype(f32) + recv[...].astype(f32))
    full_ref[...] = values
    low = values.astype(bf16)
    halves = swapped(half, values)
    low_m[...] = halves[0].astype(bf16)
    low_t[...] = halves[1].astype(bf16)
    accumulate(dbo, jnp.sum(low.astype(f32), axis=0, keepdims=True))
    do_ref[...] = dot_nt(low, joined(w_out, 0, HALF, TENSOR)).astype(bf16)
    product = do_ref[...].astype(f32) * o_ref[...].astype(f32)
    head = lax.broadcasted_iota(jnp.int32, (8, HALF), 0)
    lane = lax.broadcasted_iota(jnp.int32, (8, HALF), 1)
    pick = ((lane >= head * HEAD_DIM) & (lane < (head + 1) * HEAD_DIM)).astype(f32)
    high, rest = split(product)
    pick = pick.astype(bf16)
    inner = dot_nt(pick, high) + dot_nt(pick, rest)
    dq_acc[...] = jnp.zeros_like(dq_acc)
    masks = head_masks()
    scale = jnp.asarray(HEAD_DIM ** (-0.5), bf16)
    seg_row = seg_q[...]

    def one_block(block, carried):
        rows = pl.ds(pl.multiple_of(block * KEYS, KEYS), KEYS)
        same = seg_k[rows, :] == seg_row
        for pair in range(HEADS // 2):
            cols = slice(pair * BS, (pair + 1) * BS)
            q_two = q_ref[:, cols] * scale
            do_two = do_ref[:, cols]
            k_two = k_ref[rows, cols]
            v_two = v_ref[rows, cols]
            dv_two = dk_two = dq_two = None
            for side in range(2):
                at = 2 * pair + side
                q_one = q_two * masks[side]
                do_one = do_two * masks[side]
                scores = dot_nt(k_two, q_one)
                prob = jnp.where(same, jnp.exp(scores - lse_ref[at : at + 1, :]), 0.0)
                grad_prob = dot_nt(v_two, do_one)
                grad_scores = (prob * (grad_prob - inner[at : at + 1, :])).astype(bf16)
                dv_one = dot(prob.astype(bf16), do_one)
                dk_one = dot(grad_scores, q_one)
                dq_one = dot_tn(grad_scores, k_two * masks[side])
                dq_two = dq_one if dq_two is None else dq_two + dq_one
                dv_two = dv_one if dv_two is None else dv_two + dv_one
                dk_two = dk_one if dk_two is None else dk_two + dk_one
            dv_acc[rows, cols] += dv_two
            dk_acc[rows, cols] += dk_two
            dq_acc[:, cols] += dq_two
        return carried

    lax.fori_loop(low_ref[step], high_ref[step], one_block, 0)
    dq_ref[...] = (dq_acc[...] * HEAD_DIM ** (-0.5)).astype(bf16)

    @pl.when(step == pl.num_programs(0) - 1)
    def _():
        dk_ref[...] = dk_acc[...].astype(bf16)
        dv_ref[...] = dv_acc[...].astype(bf16)


def attend_back_call(
    layer, first, last, half, base, own, recv, queries, keys, values, mixed, lse, seg_col, seg_row, weights
):
    tokens = base.shape[0]
    shape = lambda width, kind: jax.ShapeDtypeStruct((tokens, width), kind)
    whole = (tokens, HALF)
    return pl.pallas_call(
        attend_back_kernel,
        out_shape=[
            shape(D, f32),
            shape(HALF, bf16),
            shape(HALF, bf16),
            shape(HALF, bf16),
            shape(HALF, bf16),
            shape(HALF, bf16),
            jax.ShapeDtypeStruct((1, D), f32),
        ],
        grid_spec=pltpu.PrefetchScalarGridSpec(
            num_scalar_prefetch=3,
            grid=(tokens // ROWS,),
            in_specs=[
                rows_spec(D),
                rows_spec(D),
                rows_spec(D),
                rows_spec(HALF),
                fixed(whole),
                fixed(whole),
                rows_spec(HALF),
                pl.BlockSpec((8, ROWS), lambda i, *_: (0, i)),
                fixed(seg_col.shape),
                pl.BlockSpec((1, ROWS), lambda i, *_: (0, i)),
                fixed((D, HALF)),
            ],
            out_specs=[
                rows_spec(D),
                rows_spec(HALF),
                rows_spec(HALF),
                rows_spec(HALF),
                fixed(whole),
                fixed(whole),
                fixed((1, D)),
            ],
            scratch_shapes=[
                pltpu.VMEM(whole, f32),
                pltpu.VMEM(whole, f32),
                pltpu.VMEM((ROWS, HALF), f32),
                pltpu.VMEM((ROWS, HALF), bf16),
            ],
        ),
        compiler_params=params(),
        cost_estimate=cost(14 * HEADS * tokens * tokens * BS, tokens * D * 20, HEADS * tokens * tokens),
    )(
        first, last, half, base, own, recv, stay(queries), stay(keys), stay(values), stay(mixed), lse,
        seg_col, seg_row, weights["out", layer],
    )


def qkv_back_kernel(layer, dq, dk, dv, hid, vec, weight, back, dgain, dshift, dbq, dbv):
    grad_three = jnp.concatenate([dq[...], dk[...], dv[...]], axis=1)
    grad_normed = dot_nt(grad_three, joined(weight, 0, D, 3))
    part_back, gain_grad, shift_grad = norm_back(hid[...], vec_piece(vec, layer, "g1"), grad_normed)
    back[...] = part_back.astype(bf16)
    accumulate(dgain, gain_grad)
    accumulate(dshift, shift_grad)
    accumulate(dbq, jnp.sum(dq[...].astype(f32), axis=0, keepdims=True))
    accumulate(dbv, jnp.sum(dv[...].astype(f32), axis=0, keepdims=True))


def qkv_back_call(layer, dq, dk, dv, hid, vec, weights):
    tokens = dq.shape[0]
    line = lambda width: jax.ShapeDtypeStruct((1, width), f32)
    lines = [line(D), line(D), line(HALF), line(HALF)]
    return pl.pallas_call(
        functools.partial(qkv_back_kernel, layer),
        out_shape=[jax.ShapeDtypeStruct((tokens, D), bf16)] + lines,
        grid=(tokens // ROWS,),
        in_specs=[rows_spec(HALF)] * 3
        + [
            rows_spec(D),
            fixed(vec.shape),
            fixed((3 * D, HALF)),
        ],
        out_specs=[rows_spec(D)] + [fixed(o.shape) for o in lines],
        compiler_params=params(),
        cost_estimate=cost(2 * tokens * D * 3 * HALF, tokens * D * 10),
    )(dq, dk, dv, stay(hid), vec, weights["qkv", layer])


def split(values):
    high = values.astype(bf16)
    return high, (values - high.astype(f32)).astype(bf16)


def product(left, right, left_dim, right_dim):
    def one(a, b):
        return lax.dot_general(
            a, b, (((left_dim,), (right_dim,)), ((), ())), preferred_element_type=f32
        )

    return one(left[0], right[0]) + (one(left[0], right[1]) + one(left[1], right[0]))


def owner_kernel(per, used, home, near, far, master, left, right, moment, variance, grad, out, out_mom, out_var):
    here = range(per)
    first = pl.program_id(0) * per
    lefts = [split(left[i]) for i in here]
    rights = [split(right[i]) for i in here]
    rotated = []
    for i in here:
        rows = slice(i * BS, (i + 1) * BS)
        tile = jnp.where(home[0] > 0, near[rows, :].astype(f32), far[rows, :].astype(f32))
        tile = jnp.where(used[first + i] > 0, tile, 0.0)
        grad[i] = tile
        tile = tile.astype(bf16)
        rotated.append(split(dot_tn(lefts[i][0], tile) + dot_tn(lefts[i][1], tile)))
    rotated = [product(rotated[i], rights[i], 1, 0) for i in here]
    steps = []
    for i in here:
        new_moment = decay * moment[i] + (1.0 - decay) * rotated[i]
        new_variance = decay * variance[i] + (1.0 - decay) * rotated[i] * rotated[i]
        out_mom[i] = new_moment
        out_var[i] = new_variance
        steps.append(split(new_moment / (jnp.sqrt(new_variance) + adam_eps)))
    returned = [split(product(lefts[i], steps[i], 1, 0)) for i in here]
    returned = [product(returned[i], rights[i], 1, 1) for i in here]
    for i in here:
        out[i] = master[i] - matrix_rate * returned[i]


def owner_call(used, home, near, far, *arrays):
    count = arrays[0].shape[0]
    per = min(8, count)
    block = pl.BlockSpec((per, BS, BS), lambda i, *_: (i, 0, 0))
    return pl.pallas_call(
        functools.partial(owner_kernel, per),
        out_shape=[jax.ShapeDtypeStruct(arrays[0].shape, f32)] * 4,
        grid_spec=pltpu.PrefetchScalarGridSpec(
            num_scalar_prefetch=2,
            grid=(count // per,),
            in_specs=[pl.BlockSpec((per * BS, BS), lambda i, *_: (i, 0))] * 2 + [block] * 5,
            out_specs=[block] * 4,
        ),
        compiler_params=params(),
        cost_estimate=cost(count * 88 * BS**3, count * BS * BS * 38),
    )(used, home, stay(near), stay(far), *arrays)


def reduce_kernel(carrying, last, *refs):
    block, arrived, *refs = refs
    total = block[...].astype(f32) + arrived[...].astype(f32)
    if carrying:
        carried, *refs = refs
        total = total + carried[...].astype(f32)
    if last:
        [out] = refs
    else:
        following, out, later = refs
        later[...] = following[...]
    out[...] = total.astype(bf16)


def reduce_call(j, n, buffer, arrived, carried, payload):
    last = j == 3
    at = lambda j, x_rel: pl.BlockSpec((payload, BS), lambda i: ((j * 2 + x_rel) * 2 + n, 0))
    whole = fixed((payload, BS))
    operands = [stay(buffer), stay(arrived)] + ([] if carried is None else [stay(carried)])
    specs = [at(j, 0)] + [whole] * (len(operands) - 1)
    if not last:
        operands.append(stay(buffer))
        specs.append(at(j + 1, 1))
    outs = [pltpu.HBM((payload, BS), bf16)] * (1 if last else 2)
    made = pl.pallas_call(
        functools.partial(reduce_kernel, carried is not None, last),
        out_shape=outs,
        grid=(1,),
        in_specs=specs,
        out_specs=[whole] * len(outs),
        compiler_params=params(8),
        cost_estimate=cost(payload * BS * 3, payload * BS * 12),
    )(*operands)
    return (made[0], None) if last else made


class Routes:
    def __init__(self, dp_n):
        pairs = [(d, t) for d in range(dp_n) for t in range(TENSOR)]
        at = lambda d, t: d * TENSOR + t
        home = [(d, t) for d, t in pairs if d % 2 == t]
        away = [(d, t) for d, t in pairs if d % 2 != t]
        self.core_all = [(at(d, t), at(d ^ 1, t)) for d, t in pairs]
        self.core_out = [(at(d, t), at(d ^ 1, t)) for d, t in home]
        self.core_in = [(at(d, t), at(d ^ 1, t)) for d, t in away]
        self.y_all = [(at(d, t), at(d, 1 - t)) for d, t in pairs]
        self.y_out = [(at(d, t), at(d, 1 - t)) for d, t in home]
        self.y_in = [(at(d, t), at(d, 1 - t)) for d, t in away]
        self.x_home = [(at(d, t), at(d ^ 2, t)) for d, t in home]
        self.x_away = [(at(d, t), at(d ^ 2, t)) for d, t in away]
        self.z_home = [(at(d, t), at((d + 4) % dp_n, t)) for d, t in home]


def send(value, route):
    return lax.ppermute(value, AXES, route)


def shards(
    patches,
    cotangent,
    image_size,
    block_slot,
    pinv,
    master_slots,
    left_basis,
    right_basis,
    mom_slots,
    var_slots,
    vec_master,
    vec_mom,
    vec_var,
):
    dp_n = lax.axis_size("dp")
    dp_pos = lax.axis_index("dp")
    y_pos = lax.axis_index("tensor")
    core = dp_pos % 2
    home = core == y_pos
    routes = Routes(dp_n)
    grid3 = dp_n == 16
    x_pos = (dp_pos // 2) % 2
    half_at = (x_pos if grid3 else x_pos * 0).astype(jnp.int32).reshape(1)
    tokens_n = patches.shape[0]
    slots_per = master_slots.shape[1]
    vec_per = vec_master.shape[1]
    slots_n = slots_per * dp_n
    payload = slots_per * BS + VEC_ROWS

    patches = jnp.where(home, patches, send(patches, routes.core_out))
    cotangent = jnp.where(home, cotangent, send(cotangent, routes.core_out))
    size_row = jnp.where(home, image_size, send(image_size, routes.core_out))[0]
    own_slots = block_slot[0]
    slot_other = send(block_slot, routes.y_all)

    lengths = jnp.where(
        size_row == 0, LEN_A, jnp.where(size_row == 1, LEN_B, jnp.where(size_row == 2, LEN_C, 0))
    )
    order = jnp.arange(IMG_DEV)
    ends_at = jnp.sum(jnp.where(order[None, :] <= order[:, None], lengths[None, :], 0), axis=1)
    places = jnp.arange(tokens_n)
    segment = jnp.sum((places[:, None] >= ends_at[None, :]).astype(jnp.int32), axis=1)
    in_image = segment[:, None] == order[None, :]
    select = jnp.stack(
        [jnp.any(in_image & (size_row == s)[None, :], axis=1) for s in range(3)], axis=1
    )
    valid_col = (segment < IMG_DEV).astype(f32)[:, None]
    seg_col = segment[:, None]
    seg_row = segment[None, :]
    blocks_n = tokens_n // ROWS
    starts = jnp.arange(blocks_n) * ROWS
    begun = ends_at[None, :] <= starts[:, None]
    first_tok = jnp.max(jnp.where(begun, ends_at[None, :], 0), axis=1)
    after = ends_at[None, :] > (starts + ROWS - 1)[:, None]
    last_tok = jnp.min(jnp.where(after, ends_at[None, :], tokens_n), axis=1)
    first_blk = (first_tok // ROWS).astype(jnp.int32)
    last_blk = ((last_tok + ROWS - 1) // ROWS).astype(jnp.int32)
    first_key = (first_tok // KEYS).astype(jnp.int32)
    last_key = ((last_tok + KEYS - 1) // KEYS).astype(jnp.int32)

    select_low = select.astype(bf16)
    class_col = jnp.sum(jnp.where(select, jnp.arange(1, 4)[None, :], 0), axis=1, keepdims=True) - 1
    present = jnp.any(select.reshape(blocks_n, ROWS, 3), axis=1).astype(jnp.int32)

    def expand(which):
        return expand_call(which, present, half_at, patches, class_col, pinv)

    vec_low = jnp.pad(vec_master[0].astype(bf16), (0, VEC_ROWS * BS - vec_per))
    own_pack = jnp.concatenate(
        [
            master_slots[0].astype(bf16).reshape(slots_per * BS, BS),
            vec_low.reshape(VEC_ROWS, BS),
        ],
        axis=0,
    )
    flag = home.astype(jnp.int32).reshape(1)
    if grid3:
        z_pos = dp_pos // 4
        packs = [[own_pack], [send(own_pack, routes.core_in)]]
        across, over_y, corner = [[], []], [[], []], [[], []]
        token = jnp.zeros((8, BS), f32)
        chunks = []
        for j in range(5):
            for n in range(2):
                moved = {}
                if j < 4:
                    moved["x"] = send(packs[n][j], routes.x_home)
                    moved["y"] = send(packs[n][j], routes.y_out)
                if j:
                    source, route = (across, routes.y_out) if n == 0 else (over_y, routes.x_away)
                    moved["corner"] = send(source[n][j - 1], route)
                if j < 3:
                    moved["z"] = send(packs[n][j], routes.z_home)
                work = []
                if j + n == 0:
                    work = [slot_other]
                if 1 <= 2 * j + n <= CHUNKS:
                    work = [expand(2 * j + n - 1)]
                if j < 4:
                    token, *made = fence(token, *moved.values(), *work)
                    if j + n == 0:
                        slot_other = made.pop()
                    elif work:
                        chunks.append(made.pop())
                    moved = dict(zip(moved, made))
                    across[n].append(moved["x"])
                    over_y[n].append(moved["y"])
                if j < 3:
                    packs[n].append(moved["z"])
                if j:
                    corner[n].append(moved["corner"])
        first, second, owner = [], [], []
        for j in range(4):
            first += [packs[0][j], packs[1][j], across[0][j], across[1][j]]
            second += [over_y[0][j], over_y[1][j], corner[0][j], corner[1][j]]
            for x_rel in range(2):
                for n in range(2):
                    owner.append(((z_pos - j) % 4) * 4 + (x_pos ^ x_rel) * 2 + (core ^ n))
        first = [v[None] for v in first]
        second = [v[None] for v in second]
        owner = jnp.stack(owner).astype(jnp.int32)
    else:
        everything = lax.all_gather(own_pack, AXES, axis=0)
        everything = everything.reshape(dp_n, TENSOR, payload, BS)
        first = [jnp.where(core == 0, everything[:, 0], everything[:, 1])]
        second = []
        owner = jnp.arange(dp_n, dtype=jnp.int32)
        chunks = [expand(c) for c in range(CHUNKS)]
    slot_list = jnp.where(home, block_slot, slot_other)[0]
    named = slot_list[None, :] == jnp.arange(slots_n)[:, None]
    used = jnp.any(named, axis=1)
    drow = jnp.where(used, jnp.sum(jnp.where(named, TARGET_ROW[None, :], 0), axis=1), -1)
    dcol = jnp.sum(jnp.where(named, TARGET_COL[None, :], 0), axis=1)
    weights, vec_rows = gather_tiles(first, second, owner, drow, dcol, flag, slots_per, dp_n)
    vec = vec_rows.reshape(dp_n, VEC_ROWS * BS)[:, :vec_per].astype(f32).reshape(1, dp_n * vec_per)

    embedded = embed_call(half_at, chunks, vec, weights)
    embedded_other = send(embedded, routes.core_all)
    core_flag = core.astype(jnp.int32).reshape(1)

    caches = []
    hidden, own, recv = None, embedded, embedded_other
    for layer in range(LAYERS):
        hidden, normed_m, normed_t, queries, keys, values = qkv_call(
            layer, hidden, own, recv, core_flag, half_at, vec, weights
        )
        mixed, lse, part = attend_call(
            layer, first_blk, last_blk, queries, keys, values, seg_col, seg_row, vec, weights
        )
        other = send(part, routes.core_all)
        middle, normed2, act_m, act_t, slope, own = mlp_call(
            layer, half_at, hidden, part, other, vec, weights
        )
        recv = send(own, routes.core_all)
        caches.append(
            dict(
                hidden=hidden, normed=(normed_m, normed_t), qkv=(queries, keys, values), mixed=mixed,
                lse=lse, middle=middle, normed2=normed2, act=(act_m, act_t), slope=slope,
            )
        )
        hidden = middle
    out_low = ((hidden + (own.astype(f32) + recv.astype(f32))) * valid_col).astype(bf16)

    owners = jnp.arange(dp_n)
    if grid3:
        place = (
            ((z_pos - 1 - owners // 4) % 4) * 4
            + (x_pos ^ ((owners // 2) % 2)) * 2
            + (core ^ (owners % 2))
        ).astype(jnp.int32)
    else:
        place = owners.astype(jnp.int32)
    slot_owner = slot_list // slots_per
    owner_place = jnp.sum(
        jnp.where(slot_owner[:, None] == owners[None, :], place[None, :], 0), axis=1
    )
    tile_pos = (owner_place * payload + (slot_list % slots_per) * BS).astype(jnp.int32)
    vec_pos = (place * payload + slots_per * BS).astype(jnp.int32)
    total_rows = dp_n * payload
    where_to = jnp.concatenate([half_at, flag if grid3 else flag * 0 + 1])
    offsets = {"base": 0}
    count = BASE_PIX // BS * (HALF // BS)
    for layer in range(LAYERS):
        for name, size in (("qkv", 3 * D * HALF), ("out", D * HALF), ("up", D * HALF_FF), ("down", D * HALF_FF)):
            offsets[name, layer] = count
            count += size // (BS * BS)

    tile_grid = {
        "base": (BASE_PIX // BS, HALF // BS),
        "qkv": (D // BS, 3 * HALF // BS),
        "out": (HALF // BS, D // BS),
        "up": (D // BS, HALF_FF // BS),
        "down": (HALF_FF // BS, D // BS),
    }

    def place_tiles(name, layer, rel, matrix, arrived, buffer):
        key = "base" if name == "base" else (name, layer)
        rows_n, cols_n = tile_grid[name]
        pos = tile_pos[offsets[key] : offsets[key] + rows_n * cols_n].reshape(rows_n, cols_n)
        axis = 1 if name in ("up", "out") else 0
        low_pos, high_pos = jnp.split(pos, 2, axis=axis)
        pos = jnp.where(half_at[0] == rel, low_pos, high_pos).reshape(-1)
        steps = 1 if name in ("qkv", "out") else 2
        return scatter_matrix(
            pos, matrix, arrived, where_to, buffer, total_rows, matrix.shape[0] // steps
        )

    def over(matrix):
        return send(matrix, routes.y_in) if grid3 else None

    def beside(matrix):
        return send(matrix, routes.x_away) if grid3 else None

    def with_arrived(product, arrived):
        if arrived is not None:
            product = product + arrived.astype(f32)
        return product.astype(bf16)

    def hold(*arrays):
        kept = [a for a in arrays if a is not None]
        done = iter(fence(*kept))
        return [None if a is None else next(done) for a in arrays]

    top, low = 1, 0
    vec_grads = [None] * LAYERS

    def mlp_step(layer, grad, own, recv):
        kept = caches[layer]
        made = mlp_back_call(
            layer, half_at, grad, own, recv, valid_col, kept["middle"], kept["slope"], vec, weights
        )
        if own is not None:
            return made
        return [made[0]] + list(made)

    def attend_step(layer, grad, part, other, lse):
        kept = caches[layer]
        return attend_back_call(
            layer, first_key, last_key, half_at, grad, part, other, *kept["qkv"], kept["mixed"], lse,
            seg_col, seg_row, weights,
        )

    def down_grad(layer, which, grad_low):
        return dot_tn(caches[layer]["act"][which], grad_low)

    def up_grad(layer, du_part):
        return dot_tn(caches[layer]["normed2"], du_part)

    def qkv_grad(layer, which, three):
        return dot_tn(caches[layer]["normed"][which], three)

    def out_grad(layer, low_part):
        return dot_tn(caches[layer]["mixed"], low_part)

    grad, grad_low, du_m, du_t, part, dg2, ds2, db1, db2 = mlp_step(top, cotangent, None, None)
    other = send(part, routes.core_all)
    gd1t = down_grad(top, 1, grad_low).astype(bf16)
    gu1t = up_grad(top, du_t).astype(bf16)
    lse, gd1t, gu1t, out_low = fence(caches[top]["lse"], gd1t, gu1t, out_low)
    xd1 = beside(gd1t)
    xu1 = beside(gu1t)
    mlp_low1 = grad_low
    grad, low_m, low_t, dq, dk, dv, dbo = attend_step(top, grad, part, other, lse)
    vec, dbo, xd1 = hold(vec, dbo, xd1)
    gd1 = with_arrived(down_grad(top, 0, mlp_low1), xd1)
    yd1 = over(gd1)
    own, dg1, ds1, dbq, dbv = qkv_back_call(
        top, dq, dk, dv, caches[top]["hidden"], vec, weights
    )
    recv = send(own, routes.core_all)
    three = jnp.concatenate([dq, dk, dv], axis=1)
    go1t = out_grad(top, low_t).astype(bf16)
    gq1t = qkv_grad(top, 1, three).astype(bf16)
    vec_grads[top] = [dg1, ds1, dbq, dbv, dbo, dg2, ds2, db1, db2]
    upper = (du_m, low_m, three)
    grad, grad_low, du_m, du_t, part, dg2, ds2, db1, db2 = mlp_step(low, grad, own, recv)
    other = send(part, routes.core_all)
    db2, xu1, yd1, go1t, gq1t = hold(db2, xu1, yd1, go1t, gq1t)
    gu1 = with_arrived(up_grad(top, upper[0]), xu1)
    yu1 = over(gu1)
    xq1, xo1 = beside(gq1t), beside(go1t)
    gd0t = down_grad(low, 1, grad_low).astype(bf16)
    gu0t = up_grad(low, du_t).astype(bf16)
    lse, gd0t, gu0t, gu1 = hold(caches[low]["lse"], gd0t, gu0t, gu1)
    xd0 = beside(gd0t)
    buffer = place_tiles("down", top, 1, gd1t, None, None)
    buffer = place_tiles("up", top, 1, gu1t, None, buffer)
    mlp_low0 = grad_low
    grad, low_m, low_t, dq, dk, dv, dbo = attend_step(low, grad, part, other, lse)
    vec, dbo, yu1, xq1, xo1, xd0, buffer = hold(vec, dbo, yu1, xq1, xo1, xd0, buffer)
    gq1 = with_arrived(qkv_grad(top, 0, upper[2]), xq1)
    go1 = with_arrived(out_grad(top, upper[1]), xo1)
    gd0 = with_arrived(down_grad(low, 0, mlp_low0), xd0)
    yq1, yo1, yd0 = over(gq1), over(go1), over(gd0)
    xu0 = beside(gu0t)
    own, dg1, ds1, dbq, dbv = qkv_back_call(
        low, dq, dk, dv, caches[low]["hidden"], vec, weights
    )
    recv = send(own, routes.core_all)
    three = jnp.concatenate([dq, dk, dv], axis=1)
    gq0t = qkv_grad(low, 1, three).astype(bf16)
    go0t = out_grad(low, low_t).astype(bf16)
    vec_grads[low] = [dg1, ds1, dbq, dbv, dbo, dg2, ds2, db1, db2]
    grad_emb, grad_emb_bias = embed_back_call(core_flag, grad, own, recv)
    middle = CHUNKS // 2
    gbt = jnp.concatenate([dot_tn(c, grad_emb).astype(bf16) for c in chunks[middle:]], axis=0)
    gbt, xu0, gq0t, go0t, yq1 = hold(gbt, xu0, gq0t, go0t, yq1)
    xb = beside(gbt)
    xq0, xo0 = beside(gq0t), beside(go0t)
    gu0 = with_arrived(up_grad(low, du_m), xu0)
    yu0 = over(gu0)
    vec_grad = pack_call([grad_emb_bias] + vec_grads[0] + vec_grads[1], dp_n, vec_per)
    av = over(vec_grad)
    buffer = place_tiles("down", top, 0, gd1, yd1, buffer)
    buffer = place_tiles("up", top, 0, gu1, yu1, buffer)
    buffer = place_tiles("qkv", top, 1, gq1t, None, buffer)
    buffer = place_tiles("out", top, 1, go1t, None, buffer)
    buffer = place_tiles("down", low, 1, gd0t, None, buffer)
    buffer = place_tiles("up", low, 1, gu0t, None, buffer)
    xb, xq0, xo0, yd0, buffer = hold(xb, xq0, xo0, yd0, buffer)
    gbm = jnp.concatenate(
        [
            with_arrived(
                dot_tn(c, grad_emb),
                None if xb is None else xb[k * D : (k + 1) * D],
            )
            for k, c in enumerate(chunks[:middle])
        ],
        axis=0,
    )
    yb = over(gbm)
    gq0 = with_arrived(qkv_grad(low, 0, three), xq0)
    go0 = with_arrived(out_grad(low, low_m), xo0)
    yq0, yo0 = over(gq0), over(go0)
    buffer = place_tiles("qkv", top, 0, gq1, yq1, buffer)
    buffer = place_tiles("out", top, 0, go1, yo1, buffer)
    buffer = place_tiles("down", low, 0, gd0, yd0, buffer)
    buffer = place_tiles("base", 0, 1, gbt, None, buffer)
    buffer = place_tiles("qkv", low, 1, gq0t, None, buffer)
    buffer = place_tiles("out", low, 1, go0t, None, buffer)
    yu0, av, buffer = hold(yu0, av, buffer)
    buffer = place_tiles("up", low, 0, gu0, yu0, buffer)
    buffer = scatter_vec(vec_pos, vec_grad, av, buffer)
    base_weight = weights["base", 0]
    yb, yq0, yo0, buffer, base_weight, out_low = hold(yb, yq0, yo0, buffer, base_weight, out_low)
    weights["base", 0] = base_weight
    buffer = place_tiles("out", low, 0, go0, yo0, buffer)
    buffer = place_tiles("qkv", low, 0, gq0, yq0, buffer)
    buffer = place_tiles("base", 0, 0, gbm, yb, buffer)

    if grid3:
        token = jnp.zeros((8, BS), f32)
        order = (1, 0)
        resized = resize_call(weights, pinv)
        carried = {n: None for n in order}
        across = {n: send(buffer.reshape(4, 2, 2, payload, BS)[0, 1, n], routes.x_home) for n in order}
        rounded = {}
        for j in range(4):
            for n in order:
                extra = None
                if j == 0 and n == order[0]:
                    extra = resized
                token, across[n], carried[n], extra = hold(token, across[n], carried[n], extra)
                if extra is not None:
                    resized = extra
                total, later = reduce_call(j, n, buffer, across[n], carried[n], payload)
                if j < 3:
                    carried[n] = send(total, routes.z_home)
                    across[n] = send(later, routes.x_home)
                else:
                    rounded[n] = total
        near_grad, far_grad = rounded[0], send(rounded[1], routes.core_out)
    else:
        held = buffer.reshape(dp_n, 1, payload, BS).astype(f32)
        nothing = jnp.zeros_like(held)
        both = jnp.concatenate(
            [jnp.where(core == 0, held, nothing), jnp.where(core == 0, nothing, held)], axis=1
        )
        used_rows = jnp.repeat(used, BS).reshape(dp_n, 1, slots_per * BS, 1)
        used_rows = jnp.concatenate(
            [used_rows, jnp.ones((dp_n, 1, VEC_ROWS, 1), bool)], axis=2
        )
        both = jnp.where(used_rows, both, 0.0).reshape(dp_n * TENSOR * payload, BS)
        near_grad = lax.psum_scatter(both, AXES, scatter_dimension=0, tiled=True).astype(bf16)
        far_grad = near_grad
        resized = resize_call(weights, pinv)

    output = jnp.where(home, out_low, send(out_low, routes.y_out)).astype(f32)
    grad_pixels = sum(
        dot(grad_emb * select_low[:, s : s + 1], resized[s]) for s in range(3)
    ).astype(bf16)
    pixels_other = send(grad_pixels, routes.core_all)
    pixel_sides = [
        grad_pixels[:, s * HALF : (s + 1) * HALF].astype(f32)
        + pixels_other[:, s * HALF : (s + 1) * HALF].astype(f32)
        for s in range(TENSOR)
    ]
    near = jnp.where(core == 0, pixel_sides[0], pixel_sides[1])
    far = jnp.where(core == 0, pixel_sides[1], pixel_sides[0]).astype(bf16)
    patch_grad = jnp.where(home, near, send(far, routes.y_out).astype(f32))

    my_slots = dp_pos * slots_per + jnp.arange(slots_per)
    mine_used = jnp.any(own_slots[None, :] == my_slots[:, None], axis=1).astype(jnp.int32)
    owned_grad, new_master, new_mom, new_var = owner_call(
        mine_used, flag, near_grad, far_grad, master_slots[0], left_basis[0], right_basis[0], mom_slots[0], var_slots[0]
    )
    vec_rows = jnp.where(home, near_grad[slots_per * BS :], far_grad[slots_per * BS :])
    owned_vec_grad = vec_rows.astype(f32).reshape(VEC_ROWS * BS)[:vec_per]
    new_vec_mom = decay * vec_mom[0] + (1.0 - decay) * owned_vec_grad
    new_vec_var = decay * vec_var[0] + (1.0 - decay) * owned_vec_grad * owned_vec_grad
    new_vec = vec_master[0] - vector_rate * new_vec_mom / (jnp.sqrt(new_vec_var) + adam_eps)
    return (
        output,
        patch_grad,
        owned_grad[None],
        new_master[None],
        new_mom[None],
        new_var[None],
        owned_vec_grad[None],
        new_vec[None],
        new_vec_mom[None],
        new_vec_var[None],
    )


def solution(mesh):
    slots = P("tensor", "dp", None, None)
    vectors = P("tensor", "dp")
    tokens = P("dp", None)
    in_specs = (tokens, tokens, tokens, P("tensor", None), P()) + (slots,) * 5 + (vectors,) * 3
    out_specs = (tokens, P("dp", "tensor")) + (slots,) * 4 + (vectors,) * 4
    return jax.shard_map(shards, mesh=mesh, in_specs=in_specs, out_specs=out_specs, check_vma=False)
```

```python
import functools

import jax
import jax.numpy as jnp
import numpy as np
from jax import lax
from jax.experimental import pallas as pl
from jax.experimental.pallas import tpu as pltpu
from jax.sharding import PartitionSpec as P

D = 768
HEAD_DIM = 64
FF = 3072
BASE_PIX = 3072
LAYERS = 2
LEN_A = 196
LEN_B = 225
LEN_C = 576
IMG_DEV = 5
BS = 128
TENSOR = 2
HALF = D // TENSOR
HALF_FF = FF // TENSOR
HEADS = HALF // HEAD_DIM
ROWS = 256
KEYS = 512
VEC_ROWS = 16
CHUNKS = 4

AXES = ("dp", "tensor")
precise = lax.Precision.HIGHEST
masked_score = -1e30
norm_eps = 1e-06
adam_eps = 1e-08
decay = 0.5
matrix_rate = 0.05
vector_rate = 0.3
f32 = jnp.float32
bf16 = jnp.bfloat16
MIB = 1024 * 1024

WEIGHTS = [("base", 0, BASE_PIX)]
for layer in range(LAYERS):
    WEIGHTS += [("qkv", layer, 3 * D), ("out", layer, D), ("up", layer, FF), ("down", layer, FF)]
STARTS = {}
PANEL_ROWS = 0
for name, layer, size in WEIGHTS:
    STARTS[name, layer] = PANEL_ROWS
    PANEL_ROWS += size


def tile_targets():
    rows, cols = [], []

    def add(start, rows_n, cols_n):
        for i in range(rows_n // BS):
            for j in range(cols_n // BS):
                panel, inner = divmod(j * BS, HALF)
                rows.append(start + panel * rows_n + i * BS)
                cols.append(inner)

    add(STARTS["base", 0], BASE_PIX, HALF)
    for layer in range(LAYERS):
        add(STARTS["qkv", layer], D, 3 * HALF)
        add(STARTS["out", layer], HALF, D)
        add(STARTS["up", layer], D, HALF_FF)
        add(STARTS["down", layer], HALF_FF, D)
    return np.array(rows, np.int32), np.array(cols, np.int32)


TARGET_ROW, TARGET_COL = tile_targets()
LAYER_VECS = (D, D, HALF, HALF, D, D, D, HALF_FF, D)
VEC_NAMES = ("g1", "s1", "bq", "bv", "bo", "g2", "s2", "b1", "b2")


def vec_offsets():
    offset = HALF
    found = []
    for layer in range(LAYERS):
        here = {}
        for name, length in zip(VEC_NAMES, LAYER_VECS):
            here[name] = (offset, length)
            offset += length
        found.append(here)
    return found


VEC_AT = vec_offsets()


def params(limit=24):
    return pltpu.CompilerParams(
        dimension_semantics=("arbitrary",), vmem_limit_bytes=limit * MIB
    )


def cost(flops, nbytes, trans=0):
    return pl.CostEstimate(flops=flops, bytes_accessed=nbytes, transcendentals=trans)


def rows_spec(width):
    return pl.BlockSpec((ROWS, width), lambda i, *_: (i, 0))


def fixed(shape, at=0):
    return pl.BlockSpec(shape, lambda i, *_: (at,) + (0,) * (len(shape) - 1))


def vec_piece(vec_ref, layer, name):
    start, length = VEC_AT[layer][name]
    return vec_ref[:, start : start + length]


def dot(left, right):
    return jnp.dot(left, right, preferred_element_type=f32)


def dot_nt(left, right, precision=None):
    return lax.dot_general(
        left, right, (((1,), (1,)), ((), ())), precision=precision, preferred_element_type=f32
    )


def dot_tn(left, right):
    return lax.dot_general(left, right, (((0,), (0,)), ((), ())), preferred_element_type=f32)


def joined(ref, start, rows_n, panels):
    return jnp.concatenate(
        [ref[start + p * rows_n : start + (p + 1) * rows_n, :] for p in range(panels)], axis=1
    )


def norm_stats(values):
    mean_val = jnp.mean(values, axis=-1, keepdims=True)
    centered = values - mean_val
    inv_std = lax.rsqrt(jnp.mean(centered * centered, axis=-1, keepdims=True) + norm_eps)
    return centered * inv_std, inv_std


def norm_back(values, gain, grad):
    unit, inv_std = norm_stats(values)
    scaled = grad * gain
    mean_s = jnp.mean(scaled, axis=-1, keepdims=True)
    mean_u = jnp.mean(scaled * unit, axis=-1, keepdims=True)
    back = inv_std * (scaled - mean_s - unit * mean_u)
    return (
        back,
        jnp.sum(grad * unit, axis=0, keepdims=True),
        jnp.sum(grad, axis=0, keepdims=True),
    )


def accumulate(ref, value):
    first = pl.program_id(0) == 0

    @pl.when(first)
    def _():
        ref[...] = value

    @pl.when(jnp.logical_not(first))
    def _():
        ref[...] += value


def stay(value):
    return pltpu.with_memory_space_constraint(value, pltpu.HBM)


def fence(*arrays):
    def nothing(*refs):
        pass

    anywhere = pl.BlockSpec(memory_space=pl.ANY)
    return pl.pallas_call(
        nothing,
        out_shape=[jax.ShapeDtypeStruct(a.shape, a.dtype) for a in arrays],
        in_specs=[anywhere] * len(arrays),
        out_specs=[anywhere] * len(arrays),
        input_output_aliases={i: i for i in range(len(arrays))},
        compiler_params=pltpu.CompilerParams(vmem_limit_bytes=MIB),
    )(*[stay(a) if a.size > 32 * 1024 else a for a in arrays])


def gather_kernel(slots, count_a, count_b, owner, drow, dcol, flag, *refs):
    first = refs[:count_a]
    second = refs[count_a : count_a + count_b]
    *panels, vectors, held, sem, vec_sem = refs[count_a + count_b :]

    def copy_all(sources):
        at = 0
        for src in sources:
            for n in range(src.shape[0]):
                who = owner[at]
                at += 1

                def body(i, carried, src=src, n=n, who=who):
                    slot = who * slots + i
                    row = drow[slot]

                    @pl.when(row >= 0)
                    def _():
                        start = pl.multiple_of(i * BS, BS)
                        pltpu.make_async_copy(
                            src.at[n, pl.ds(start, BS), :],
                            held.at[
                                pl.ds(pl.multiple_of(row, BS), BS),
                                pl.ds(pl.multiple_of(dcol[slot], BS), BS),
                            ],
                            sem,
                        ).start()

                    return carried

                lax.fori_loop(0, slots, body, 0)
                pltpu.make_async_copy(
                    src.at[n, pl.ds(slots * BS, VEC_ROWS), :], vectors.at[who], vec_sem
                ).start()

    if count_b:

        @pl.when(flag[0] == 1)
        def _():
            copy_all(first)

        @pl.when(flag[0] == 0)
        def _():
            copy_all(second)
    else:
        copy_all(first)
    pltpu.make_async_copy(held, held, sem).wait()
    at = 0
    for panel in panels:
        size = panel.shape[0]
        pltpu.make_async_copy(held.at[pl.ds(at, size), :], panel, sem).start()
        at += size
    pltpu.make_async_copy(vectors, vectors, vec_sem).wait()
    pltpu.make_async_copy(held, held, sem).wait()


def gather_tiles(first, second, owner, drow, dcol, flag, slots, owners):
    anywhere = pl.BlockSpec(memory_space=pl.ANY)
    *panels, vectors = pl.pallas_call(
        functools.partial(gather_kernel, slots, len(first), len(second)),
        out_shape=[pltpu.HBM((size, HALF), bf16) for unused, unused2, size in WEIGHTS]
        + [jax.ShapeDtypeStruct((owners, VEC_ROWS, BS), bf16)],
        grid_spec=pltpu.PrefetchScalarGridSpec(
            num_scalar_prefetch=4,
            grid=(1,),
            in_specs=[anywhere] * (len(first) + len(second)),
            out_specs=[anywhere] * len(WEIGHTS) + [fixed((owners, VEC_ROWS, BS))],
            scratch_shapes=[
                pltpu.VMEM((PANEL_ROWS, HALF), bf16),
                pltpu.SemaphoreType.DMA,
                pltpu.SemaphoreType.DMA,
            ],
        ),
        compiler_params=params(),
        cost_estimate=cost(0, 4 * PANEL_ROWS * HALF),
    )(owner, drow, dcol, flag, *[stay(v) for v in first], *[stay(v) for v in second])
    return {(name, layer): p for (name, layer, unused), p in zip(WEIGHTS, panels)}, vectors


def scatter_kernel(rows_n, cols_n, steps, paired, parts, pos, part, own, *refs):
    @pl.when(part[1] > 0)
    def _():
        scatter_body(rows_n, cols_n, steps, paired, parts, pos, part, own, *refs)


def scatter_body(rows_n, cols_n, steps, paired, parts, pos, part, own, *refs):
    if paired:
        recv, *refs = refs
        span = pl.num_programs(0) // parts
        here = jnp.logical_or(parts == 1, pl.program_id(0) // span == part[0])
    target, buf, sems = refs[-3:]
    step = pl.program_id(0)
    slot = lax.rem(step, 2)
    per = rows_n // BS * (cols_n // BS)

    def wait(at):
        pltpu.make_async_copy(buf.at[at], buf.at[at], sems.at[at]).wait()

    @pl.when(step >= 2)
    def _():
        wait(slot)

    for i in range(rows_n // BS):
        for j in range(cols_n // BS):
            area = (slice(i * BS, (i + 1) * BS), slice(j * BS, (j + 1) * BS))
            value = own[area]
            if paired:
                more = jnp.where(here, recv[area].astype(f32), 0.0)
                value = (value.astype(f32) + more).astype(bf16)
            buf[slot, i * (cols_n // BS) + j] = value
    for n in range(per):
        pltpu.make_async_copy(
            buf.at[slot, n],
            target.at[pl.ds(pl.multiple_of(pos[step * per + n], 16), BS), :],
            sems.at[slot],
        ).start()

    @pl.when(step == pl.num_programs(0) - 1)
    def _():
        if steps > 1:
            wait(1 - slot)
        wait(slot)


def scatter_matrix(pos, own, recv, part, target, total_rows, rows_n):
    cols_n = own.shape[1]
    steps = own.shape[0] // rows_n
    anywhere = pl.BlockSpec(memory_space=pl.ANY)
    block = pl.BlockSpec((rows_n, cols_n), lambda i, *_: (i, 0))
    paired = recv is not None
    parts = own.shape[0] // recv.shape[0] if paired else 1
    span = steps // parts
    arrived = pl.BlockSpec(
        (rows_n, cols_n), lambda i, pos, part: (jnp.clip(i - part[0] * span, 0, span - 1), 0)
    )
    operands = [stay(own)] + ([stay(recv)] if paired else []) + ([] if target is None else [stay(target)])
    specs = [block] + ([block if parts == 1 else arrived] if paired else [])
    specs += [] if target is None else [anywhere]
    return pl.pallas_call(
        functools.partial(scatter_kernel, rows_n, cols_n, steps, paired, parts),
        out_shape=pltpu.HBM((total_rows, BS), bf16),
        grid_spec=pltpu.PrefetchScalarGridSpec(
            num_scalar_prefetch=2,
            grid=(steps,),
            in_specs=specs,
            out_specs=anywhere,
            scratch_shapes=[
                pltpu.VMEM((2, rows_n // BS * (cols_n // BS), BS, BS), bf16),
                pltpu.SemaphoreType.DMA((2,)),
            ],
        ),
        input_output_aliases={} if target is None else {len(operands) + 1: 0},
        compiler_params=params(12),
        cost_estimate=cost(own.size, own.size * 6),
    )(pos, part, *operands)


def half_sum_kernel(part, own, arrived, out):
    out[...] = (own[...].astype(f32) + arrived[...].astype(f32)).astype(bf16)


def half_sum(part, own, arrived):
    block = arrived.shape
    return pl.pallas_call(
        half_sum_kernel,
        out_shape=pltpu.HBM(block, bf16),
        grid_spec=pltpu.PrefetchScalarGridSpec(
            num_scalar_prefetch=1,
            grid=(1,),
            in_specs=[pl.BlockSpec(block, lambda i, part: (part[0], 0)), fixed(block)],
            out_specs=fixed(block),
        ),
        compiler_params=params(8),
        cost_estimate=cost(arrived.size, arrived.size * 6),
    )(part, stay(own), stay(arrived))


def half_copy_kernel(part, own, out):
    out[...] = own[...]


def other_half(part, own):
    block = (own.shape[0] // 2, own.shape[1])
    return pl.pallas_call(
        half_copy_kernel,
        out_shape=pltpu.HBM(block, bf16),
        grid_spec=pltpu.PrefetchScalarGridSpec(
            num_scalar_prefetch=1,
            grid=(1,),
            in_specs=[pl.BlockSpec(block, lambda i, part: (1 - part[0], 0))],
            out_specs=fixed(block),
        ),
        compiler_params=params(8),
        cost_estimate=cost(0, own.size * 2),
    )(part, stay(own))


def scatter_vec_kernel(paired, pos, own, *refs):
    if paired:
        recv, *refs = refs
    target, buf, sem = refs[-3:]
    value = own[...]
    if paired:
        value = (value.astype(f32) + recv[...].astype(f32)).astype(bf16)
    buf[...] = value

    def body(n, carried):
        pltpu.make_async_copy(
            buf.at[n], target.at[pl.ds(pl.multiple_of(pos[n], 16), VEC_ROWS), :], sem
        ).start()
        return carried

    lax.fori_loop(0, own.shape[0], body, 0)
    pltpu.make_async_copy(buf, buf, sem).wait()


def scatter_vec(pos, own, recv, target):
    anywhere = pl.BlockSpec(memory_space=pl.ANY)
    block = fixed(own.shape)
    paired = recv is not None
    operands = [own] + ([recv] if paired else []) + [stay(target)]
    return pl.pallas_call(
        functools.partial(scatter_vec_kernel, paired),
        out_shape=pltpu.HBM(target.shape, bf16),
        grid_spec=pltpu.PrefetchScalarGridSpec(
            num_scalar_prefetch=1,
            grid=(1,),
            in_specs=[block] * (len(operands) - 1) + [anywhere],
            out_specs=anywhere,
            scratch_shapes=[pltpu.VMEM(own.shape, bf16), pltpu.SemaphoreType.DMA],
        ),
        input_output_aliases={len(operands): 0},
        compiler_params=params(4),
    )(pos, *operands)


def expand_kernel(present, half, patch_ref, class_ref, pinv_ref, out, total):
    for block in range(patch_ref.shape[0] // ROWS):
        rows = slice(block * ROWS, (block + 1) * ROWS)
        total[...] = jnp.zeros_like(total)
        for which in range(3):

            @pl.when(present[block, which] > 0)
            def _(which=which, rows=rows):
                chosen = jnp.where(class_ref[rows, :] == which, patch_ref[rows, :].astype(f32), 0.0)
                total[...] += dot_nt(chosen.astype(bf16), pinv_ref[which])

        out[rows, :] = total[...].astype(bf16)


def expand_call(which, present, half, patches, class_col, pinv):
    tokens = patches.shape[0]
    size = BASE_PIX // CHUNKS
    step = size
    return pl.pallas_call(
        expand_kernel,
        out_shape=jax.ShapeDtypeStruct((tokens, size), bf16),
        grid_spec=pltpu.PrefetchScalarGridSpec(
            num_scalar_prefetch=2,
            grid=(1,),
            in_specs=[
                fixed(patches.shape),
                fixed(class_col.shape),
                pl.BlockSpec(
                    (3, step, pinv.shape[2]),
                    lambda i, present, half: (0, (which + half[0] * (CHUNKS // 2)) % CHUNKS, 0),
                ),
            ],
            out_specs=pl.BlockSpec((tokens, step), lambda i, *_: (0, i)),
            scratch_shapes=[pltpu.VMEM((ROWS, step), f32)],
        ),
        compiler_params=params(),
        cost_estimate=cost(3 * tokens * size * D, tokens * size * 4 + size * D * 6),
    )(present, half, patches, class_col, stay(pinv))


def resize_kernel(base, pinv_ref, out, turned):
    @pl.when(pl.program_id(0) == 0)
    def _():
        turned[...] = base[...].T

    out[0] = dot(turned[...], pinv_ref[0]).astype(bf16)


def resize_call(weights, pinv):
    return pl.pallas_call(
        resize_kernel,
        out_shape=jax.ShapeDtypeStruct((3, HALF, pinv.shape[2]), bf16),
        grid=(3,),
        in_specs=[
            fixed((BASE_PIX, HALF)),
            pl.BlockSpec((1, BASE_PIX, pinv.shape[2]), lambda i: (i, 0, 0)),
        ],
        out_specs=pl.BlockSpec((1, HALF, pinv.shape[2]), lambda i: (i, 0, 0)),
        scratch_shapes=[pltpu.VMEM((HALF, BASE_PIX), bf16)],
        compiler_params=params(),
        cost_estimate=cost(6 * D * BASE_PIX * HALF, 6 * D * BASE_PIX),
    )(stay(weights["base", 0]), stay(pinv))


def embed_back_kernel(core, base, own, recv, out, bias):
    low = (base[...] + (own[...].astype(f32) + recv[...].astype(f32))).astype(bf16)
    out[...] = low
    accumulate(bias, jnp.sum(low.astype(f32), axis=0, keepdims=True))


def embed_back_call(core, base, own, recv):
    tokens = base.shape[0]
    half = pl.BlockSpec((ROWS, HALF), lambda i, core: (i, core[0]))
    return pl.pallas_call(
        embed_back_kernel,
        out_shape=[
            jax.ShapeDtypeStruct((tokens, HALF), bf16),
            jax.ShapeDtypeStruct((1, HALF), f32),
        ],
        grid_spec=pltpu.PrefetchScalarGridSpec(
            num_scalar_prefetch=1,
            grid=(tokens // ROWS,),
            in_specs=[half] * 3,
            out_specs=[rows_spec(HALF), fixed((1, HALF))],
        ),
        compiler_params=params(8),
        cost_estimate=cost(tokens * D, tokens * D * 5),
    )(core, base, own, recv)


def pack_kernel(vec_per, *refs):
    *pieces, out = refs
    out[...] = jnp.zeros_like(out)
    at = 0
    for piece in pieces:
        for k in range(piece.shape[1] // BS):
            owner, row = divmod(at, vec_per // BS)
            out[owner, row : row + 1, :] = piece[:, k * BS : (k + 1) * BS]
            at += 1


def pack_call(pieces, owners, vec_per):
    if vec_per % BS:
        joined = jnp.concatenate(pieces, axis=1)[0]
        joined = jnp.pad(joined, (0, owners * vec_per - joined.shape[0])).reshape(owners, vec_per)
        joined = jnp.pad(joined, ((0, 0), (0, VEC_ROWS * BS - vec_per)))
        return joined.astype(bf16).reshape(owners, VEC_ROWS, BS)
    return pl.pallas_call(
        functools.partial(pack_kernel, vec_per),
        out_shape=jax.ShapeDtypeStruct((owners, VEC_ROWS, BS), f32),
        grid=(1,),
        in_specs=[fixed(p.shape) for p in pieces],
        out_specs=fixed((owners, VEC_ROWS, BS)),
        compiler_params=params(4),
        cost_estimate=cost(0, owners * vec_per * 8),
    )(*pieces).astype(bf16)


def embed_kernel(half, *refs):
    *parts, vec, weight, out = refs
    size = BASE_PIX // CHUNKS
    total = vec[:, :HALF]
    for c in range(CHUNKS):
        at = lax.rem(c + half[0] * (CHUNKS // 2), CHUNKS)
        rows = pl.ds(pl.multiple_of(at * size, size), size)
        total = total + dot(parts[c][...], weight[rows, :])
    out[...] = total.astype(bf16)


def embed_call(half, chunks, vec, weights):
    tokens = chunks[0].shape[0]
    return pl.pallas_call(
        embed_kernel,
        out_shape=jax.ShapeDtypeStruct((tokens, HALF), bf16),
        grid_spec=pltpu.PrefetchScalarGridSpec(
            num_scalar_prefetch=1,
            grid=(tokens // ROWS,),
            in_specs=[rows_spec(BASE_PIX // CHUNKS)] * CHUNKS
            + [fixed(vec.shape), fixed((BASE_PIX, HALF))],
            out_specs=rows_spec(HALF),
        ),
        compiler_params=params(),
        cost_estimate=cost(2 * tokens * BASE_PIX * HALF, tokens * BASE_PIX * 3),
    )(half, *[stay(c) for c in chunks], vec, stay(weights["base", 0]))


def qkv_kernel(layer, first, core, *refs):
    if first:
        own, recv, vec, weight, hid, normed, q_ref, k_ref, v_ref = refs
        mine, theirs = own[...].astype(f32), recv[...].astype(f32)
        low = core[0] == 0
        values = jnp.concatenate(
            [jnp.where(low, mine, theirs), jnp.where(low, theirs, mine)], axis=1
        )
    else:
        base, own, recv, vec, weight, hid, normed, q_ref, k_ref, v_ref = refs
        values = base[...] + (own[...].astype(f32) + recv[...].astype(f32))
    hid[...] = values
    unit, unused = norm_stats(values)
    low = (unit * vec_piece(vec, layer, "g1") + vec_piece(vec, layer, "s1")).astype(bf16)
    normed[...] = low
    made = dot(low, joined(weight, 0, D, 3))
    q_ref[...] = (made[:, :HALF] + vec_piece(vec, layer, "bq")).astype(bf16)
    k_ref[...] = made[:, HALF : 2 * HALF].astype(bf16)
    v_ref[...] = (made[:, 2 * HALF :] + vec_piece(vec, layer, "bv")).astype(bf16)


def qkv_call(layer, base, own, recv, core, vec, weights):
    tokens = own.shape[0]
    shape = lambda width, kind: jax.ShapeDtypeStruct((tokens, width), kind)
    outs = [shape(D, f32), pltpu.HBM((tokens, D), bf16)] + [shape(HALF, bf16)] * 3
    operands = ([] if base is None else [base]) + [own, recv]
    return pl.pallas_call(
        functools.partial(qkv_kernel, layer, base is None),
        out_shape=outs,
        grid_spec=pltpu.PrefetchScalarGridSpec(
            num_scalar_prefetch=1,
            grid=(tokens // ROWS,),
            in_specs=[rows_spec(o.shape[1]) for o in operands]
            + [fixed(vec.shape), fixed((3 * D, HALF))],
            out_specs=[rows_spec(o.shape[1]) for o in outs],
        ),
        compiler_params=params(),
        cost_estimate=cost(2 * tokens * D * 3 * HALF, tokens * D * 14),
    )(core, *operands, vec, weights["qkv", layer])


def head_masks():
    lane = lax.broadcasted_iota(jnp.int32, (1, 2 * HEAD_DIM), 1)
    low = (lane < HEAD_DIM).astype(f32).astype(bf16)
    high = (lane >= HEAD_DIM).astype(f32).astype(bf16)
    return low, high


def attend_kernel(
    layer, low_ref, high_ref, q_ref, k_ref, v_ref, seg_q, seg_k, vec, w_out, o_ref, lse_ref, part,
    scores_ref, top_ref, acc_ref,
):
    step = pl.program_id(0)
    first, last = low_ref[step], high_ref[step]
    masks = head_masks()
    scale = jnp.asarray(HEAD_DIM ** (-0.5), bf16)
    lane = lax.broadcasted_iota(jnp.int32, (1, BS), 1)
    sums = [(lane == HEAD_DIM).astype(f32).astype(bf16), (lane == 0).astype(f32).astype(bf16)]
    top_ref[...] = jnp.full(top_ref.shape, masked_score, f32)
    acc_ref[...] = jnp.zeros_like(acc_ref)
    seg_col = seg_q[...]

    def score_block(block, carried):
        rows = pl.ds(pl.multiple_of(block * ROWS, ROWS), ROWS)
        same = seg_col == seg_k[:, rows]
        for pair in range(HEADS // 2):
            cols = slice(pair * BS, (pair + 1) * BS)
            q_two = q_ref[:, cols] * scale
            k_two = k_ref[rows, cols]
            for side in range(2):
                head = 2 * pair + side
                scores = jnp.where(same, dot_nt(q_two * masks[side], k_two), masked_score)
                scores_ref[head, block] = scores
                top = top_ref[head]
                for piece in range(ROWS // BS):
                    top = jnp.maximum(top, scores[:, piece * BS : (piece + 1) * BS])
                top_ref[head] = top
        return carried

    lax.fori_loop(first, last, score_block, 0)
    tops = [jnp.max(top_ref[head], axis=1, keepdims=True) for head in range(HEADS)]

    def mix_block(block, carried):
        rows = pl.ds(pl.multiple_of(block * ROWS, ROWS), ROWS)
        for pair in range(HEADS // 2):
            v_two = v_ref[rows, pair * BS : (pair + 1) * BS]
            for side in range(2):
                head = 2 * pair + side
                expo = jnp.exp(scores_ref[head, block] - tops[head]).astype(bf16)
                acc_ref[head] += dot(expo, v_two * masks[side] + sums[side])
        return carried

    lax.fori_loop(first, last, mix_block, 0)
    totals = jnp.zeros((ROWS, BS), f32)
    for pair in range(HEADS // 2):
        sides = []
        for side in range(2):
            head = 2 * pair + side
            mixed = acc_ref[head]
            at = HEAD_DIM * (1 - side)
            total = mixed[:, at : at + 1]
            totals = jnp.where(lane == head, tops[head] + jnp.log(total), totals)
            sides.append(mixed * (1.0 / total))
        o_ref[:, pair * BS : (pair + 1) * BS] = jnp.where(lane < HEAD_DIM, *sides).astype(bf16)
    lse_ref[...] = totals.T[0:8, :]
    low = o_ref[...]
    bias = vec_piece(vec, layer, "bo")
    part[...] = (dot(low, joined(w_out, 0, HALF, TENSOR)) + bias).astype(bf16)


def attend_call(layer, first, last, queries, keys, values, seg_col, seg_row, vec, weights):
    tokens = queries.shape[0]
    return pl.pallas_call(
        functools.partial(attend_kernel, layer),
        out_shape=[
            jax.ShapeDtypeStruct((tokens, HALF), bf16),
            jax.ShapeDtypeStruct((8, tokens), f32),
            jax.ShapeDtypeStruct((tokens, D), bf16),
        ],
        grid_spec=pltpu.PrefetchScalarGridSpec(
            num_scalar_prefetch=2,
            grid=(tokens // ROWS,),
            in_specs=[
                rows_spec(HALF),
                fixed(keys.shape),
                fixed(values.shape),
                rows_spec(1),
                fixed(seg_row.shape),
                fixed(vec.shape),
                fixed((D, HALF)),
            ],
            out_specs=[
                rows_spec(HALF),
                pl.BlockSpec((8, ROWS), lambda i, *_: (0, i)),
                rows_spec(D),
            ],
            scratch_shapes=[
                pltpu.VMEM((HEADS, tokens // ROWS, ROWS, ROWS), f32),
                pltpu.VMEM((HEADS, ROWS, BS), f32),
                pltpu.VMEM((HEADS, ROWS, BS), f32),
            ],
        ),
        compiler_params=params(),
        cost_estimate=cost(8 * HEADS * tokens * tokens * BS, tokens * D * 8, HEADS * tokens * tokens),
    )(first, last, queries, keys, values, seg_col, seg_row, vec, weights["out", layer])


def gelu_parts(values):
    cdf = 0.5 * (1.0 + lax.erf(values * 0.7071067811865476))
    pdf = 0.3989422804014327 * jnp.exp(-0.5 * values * values)
    return values * cdf, cdf + values * pdf


def mlp_kernel(layer, base, own, recv, vec, w_up, w_down, hid, normed, act, slope, part):
    values = base[...] + (own[...].astype(f32) + recv[...].astype(f32))
    hid[...] = values
    unit, unused = norm_stats(values)
    low = (unit * vec_piece(vec, layer, "g2") + vec_piece(vec, layer, "s2")).astype(bf16)
    normed[...] = low
    bias_up = vec_piece(vec, layer, "b1")
    for pair in range(HALF_FF // D):
        area = slice(pair * D, (pair + 1) * D)
        up = dot(low, joined(w_up, pair * 2 * D, D, 2)) + bias_up[:, area]
        gelu, grad = gelu_parts(up)
        act[:, area] = gelu.astype(bf16)
        slope[:, area] = grad.astype(bf16)
    bias_down = vec_piece(vec, layer, "b2")
    part[...] = (dot(act[...], joined(w_down, 0, HALF_FF, TENSOR)) + bias_down).astype(bf16)


def mlp_call(layer, base, own, recv, vec, weights):
    tokens = base.shape[0]
    shape = lambda width, kind: jax.ShapeDtypeStruct((tokens, width), kind)
    kept = lambda width: pltpu.HBM((tokens, width), bf16)
    outs = [shape(D, f32), kept(D), kept(HALF_FF), kept(HALF_FF), shape(D, bf16)]
    return pl.pallas_call(
        functools.partial(mlp_kernel, layer),
        out_shape=outs,
        grid=(tokens // ROWS,),
        in_specs=[rows_spec(D)] * 3
        + [
            fixed(vec.shape),
            fixed((2 * HALF_FF, HALF)),
            fixed((2 * HALF_FF, HALF)),
        ],
        out_specs=[rows_spec(o.shape[1]) for o in outs],
        compiler_params=params(),
        cost_estimate=cost(4 * tokens * D * HALF_FF, tokens * D * 24, 2 * tokens * HALF_FF),
    )(base, own, recv, vec, weights["up", layer], weights["down", layer])


def mlp_back_kernel(layer, summed, *refs):
    if summed:
        base, own, recv, *refs = refs
        (hid, slope, vec, w_up, w_down, grad_full, grad_low, du_ref, back, dgain, dshift, db1, db2) = refs
        values = base[...].astype(f32) + (own[...].astype(f32) + recv[...].astype(f32))
        grad_full[...] = values
        low = values.astype(bf16)
    else:
        base, valid, *refs = refs
        (hid, slope, vec, w_up, w_down, grad_low, du_ref, back, dgain, dshift, db1, db2) = refs
        low = (base[...].astype(f32) * valid[...]).astype(bf16)
    grad_low[...] = low
    accumulate(db2, jnp.sum(low.astype(f32), axis=0, keepdims=True))
    for part in range(HALF_FF // D):
        area = slice(part * D, (part + 1) * D)
        rows = jnp.concatenate(
            [w_down[p * HALF_FF + part * D : p * HALF_FF + (part + 1) * D, :] for p in range(TENSOR)],
            axis=1,
        )
        du_ref[:, area] = (dot_nt(low, rows) * slope[:, area].astype(f32)).astype(bf16)
    grad_normed = dot_nt(du_ref[...], joined(w_up, 0, D, HALF_FF // HALF))
    accumulate(db1, jnp.sum(du_ref[...].astype(f32), axis=0, keepdims=True))
    part_back, gain_grad, shift_grad = norm_back(hid[...], vec_piece(vec, layer, "g2"), grad_normed)
    back[...] = part_back.astype(bf16)
    accumulate(dgain, gain_grad)
    accumulate(dshift, shift_grad)


def mlp_back_call(layer, base, own, recv, valid, hid, slope, vec, weights):
    tokens = base.shape[0]
    summed = own is not None
    shape = lambda width, kind: jax.ShapeDtypeStruct((tokens, width), kind)
    line = lambda width: jax.ShapeDtypeStruct((1, width), f32)
    outs = ([shape(D, f32)] if summed else []) + [shape(D, bf16), shape(HALF_FF, bf16), shape(D, bf16)]
    lines = [line(D), line(D), line(HALF_FF), line(D)]
    extra = [own, recv] if summed else [valid]
    return pl.pallas_call(
        functools.partial(mlp_back_kernel, layer, summed),
        out_shape=outs + lines,
        grid=(tokens // ROWS,),
        in_specs=[rows_spec(D)]
        + [rows_spec(e.shape[1]) for e in extra]
        + [
            rows_spec(D),
            rows_spec(HALF_FF),
            fixed(vec.shape),
            fixed((2 * HALF_FF, HALF)),
            fixed((2 * HALF_FF, HALF)),
        ],
        out_specs=[rows_spec(o.shape[1]) for o in outs] + [fixed(o.shape) for o in lines],
        compiler_params=params(),
        cost_estimate=cost(4 * tokens * D * HALF_FF, tokens * D * 24),
    )(base, *extra, stay(hid), stay(slope), vec, weights["up", layer], weights["down", layer])


def attend_back_kernel(
    low_ref, high_ref, base, own, recv, q_ref, k_ref, v_ref, o_ref, lse_ref, seg_k, seg_q, w_out,
    full_ref, grad_low, dq_ref, dk_ref, dv_ref, dbo, dk_acc, dv_acc, dq_acc, do_ref,
):
    step = pl.program_id(0)

    @pl.when(step == 0)
    def _():
        dk_acc[...] = jnp.zeros_like(dk_acc)
        dv_acc[...] = jnp.zeros_like(dv_acc)

    values = base[...].astype(f32) + (own[...].astype(f32) + recv[...].astype(f32))
    full_ref[...] = values
    low = values.astype(bf16)
    grad_low[...] = low
    accumulate(dbo, jnp.sum(low.astype(f32), axis=0, keepdims=True))
    do_ref[...] = dot_nt(low, joined(w_out, 0, HALF, TENSOR)).astype(bf16)
    product = do_ref[...].astype(f32) * o_ref[...].astype(f32)
    head = lax.broadcasted_iota(jnp.int32, (8, HALF), 0)
    lane = lax.broadcasted_iota(jnp.int32, (8, HALF), 1)
    pick = ((lane >= head * HEAD_DIM) & (lane < (head + 1) * HEAD_DIM)).astype(f32)
    high, rest = split(product)
    pick = pick.astype(bf16)
    inner = dot_nt(pick, high) + dot_nt(pick, rest)
    dq_acc[...] = jnp.zeros_like(dq_acc)
    masks = head_masks()
    scale = jnp.asarray(HEAD_DIM ** (-0.5), bf16)
    seg_row = seg_q[...]

    def one_block(block, carried):
        rows = pl.ds(pl.multiple_of(block * KEYS, KEYS), KEYS)
        same = seg_k[rows, :] == seg_row
        for pair in range(HEADS // 2):
            cols = slice(pair * BS, (pair + 1) * BS)
            q_two = q_ref[:, cols] * scale
            do_two = do_ref[:, cols]
            k_two = k_ref[rows, cols]
            v_two = v_ref[rows, cols]
            dv_two = dk_two = dq_two = None
            for side in range(2):
                at = 2 * pair + side
                q_one = q_two * masks[side]
                do_one = do_two * masks[side]
                scores = dot_nt(k_two, q_one)
                prob = jnp.where(same, jnp.exp(scores - lse_ref[at : at + 1, :]), 0.0)
                grad_prob = dot_nt(v_two, do_one)
                grad_scores = (prob * (grad_prob - inner[at : at + 1, :])).astype(bf16)
                dv_one = dot(prob.astype(bf16), do_one)
                dk_one = dot(grad_scores, q_one)
                dq_one = dot_tn(grad_scores, k_two * masks[side])
                dq_two = dq_one if dq_two is None else dq_two + dq_one
                dv_two = dv_one if dv_two is None else dv_two + dv_one
                dk_two = dk_one if dk_two is None else dk_two + dk_one
            dv_acc[rows, cols] += dv_two
            dk_acc[rows, cols] += dk_two
            dq_acc[:, cols] += dq_two
        return carried

    lax.fori_loop(low_ref[step], high_ref[step], one_block, 0)
    dq_ref[...] = (dq_acc[...] * HEAD_DIM ** (-0.5)).astype(bf16)

    @pl.when(step == pl.num_programs(0) - 1)
    def _():
        dk_ref[...] = dk_acc[...].astype(bf16)
        dv_ref[...] = dv_acc[...].astype(bf16)


def attend_back_call(
    layer, first, last, base, own, recv, queries, keys, values, mixed, lse, seg_col, seg_row, weights
):
    tokens = base.shape[0]
    shape = lambda width, kind: jax.ShapeDtypeStruct((tokens, width), kind)
    whole = (tokens, HALF)
    return pl.pallas_call(
        attend_back_kernel,
        out_shape=[
            shape(D, f32),
            shape(D, bf16),
            shape(HALF, bf16),
            shape(HALF, bf16),
            shape(HALF, bf16),
            jax.ShapeDtypeStruct((1, D), f32),
        ],
        grid_spec=pltpu.PrefetchScalarGridSpec(
            num_scalar_prefetch=2,
            grid=(tokens // ROWS,),
            in_specs=[
                rows_spec(D),
                rows_spec(D),
                rows_spec(D),
                rows_spec(HALF),
                fixed(whole),
                fixed(whole),
                rows_spec(HALF),
                pl.BlockSpec((8, ROWS), lambda i, *_: (0, i)),
                fixed(seg_col.shape),
                pl.BlockSpec((1, ROWS), lambda i, *_: (0, i)),
                fixed((D, HALF)),
            ],
            out_specs=[
                rows_spec(D),
                rows_spec(D),
                rows_spec(HALF),
                fixed(whole),
                fixed(whole),
                fixed((1, D)),
            ],
            scratch_shapes=[
                pltpu.VMEM(whole, f32),
                pltpu.VMEM(whole, f32),
                pltpu.VMEM((ROWS, HALF), f32),
                pltpu.VMEM((ROWS, HALF), bf16),
            ],
        ),
        compiler_params=params(),
        cost_estimate=cost(14 * HEADS * tokens * tokens * BS, tokens * D * 20, HEADS * tokens * tokens),
    )(
        first, last, base, own, recv, stay(queries), stay(keys), stay(values), stay(mixed), lse,
        seg_col, seg_row, weights["out", layer],
    )


def qkv_back_kernel(layer, dq, dk, dv, hid, vec, weight, back, dgain, dshift, dbq, dbv):
    grad_three = jnp.concatenate([dq[...], dk[...], dv[...]], axis=1)
    grad_normed = dot_nt(grad_three, joined(weight, 0, D, 3))
    part_back, gain_grad, shift_grad = norm_back(hid[...], vec_piece(vec, layer, "g1"), grad_normed)
    back[...] = part_back.astype(bf16)
    accumulate(dgain, gain_grad)
    accumulate(dshift, shift_grad)
    accumulate(dbq, jnp.sum(dq[...].astype(f32), axis=0, keepdims=True))
    accumulate(dbv, jnp.sum(dv[...].astype(f32), axis=0, keepdims=True))


def qkv_back_call(layer, dq, dk, dv, hid, vec, weights):
    tokens = dq.shape[0]
    line = lambda width: jax.ShapeDtypeStruct((1, width), f32)
    lines = [line(D), line(D), line(HALF), line(HALF)]
    return pl.pallas_call(
        functools.partial(qkv_back_kernel, layer),
        out_shape=[jax.ShapeDtypeStruct((tokens, D), bf16)] + lines,
        grid=(tokens // ROWS,),
        in_specs=[rows_spec(HALF)] * 3
        + [
            rows_spec(D),
            fixed(vec.shape),
            fixed((3 * D, HALF)),
        ],
        out_specs=[rows_spec(D)] + [fixed(o.shape) for o in lines],
        compiler_params=params(),
        cost_estimate=cost(2 * tokens * D * 3 * HALF, tokens * D * 10),
    )(dq, dk, dv, stay(hid), vec, weights["qkv", layer])


def split(values):
    high = values.astype(bf16)
    return high, (values - high.astype(f32)).astype(bf16)


def product(left, right, left_dim, right_dim):
    def one(a, b):
        return lax.dot_general(
            a, b, (((left_dim,), (right_dim,)), ((), ())), preferred_element_type=f32
        )

    return one(left[0], right[0]) + (one(left[0], right[1]) + one(left[1], right[0]))


def owner_kernel(per, used, home, near, far, master, left, right, moment, variance, grad, out, out_mom, out_var):
    here = range(per)
    first = pl.program_id(0) * per
    lefts = [split(left[i]) for i in here]
    rights = [split(right[i]) for i in here]
    rotated = []
    for i in here:
        rows = slice(i * BS, (i + 1) * BS)
        tile = jnp.where(home[0] > 0, near[rows, :].astype(f32), far[rows, :].astype(f32))
        tile = jnp.where(used[first + i] > 0, tile, 0.0)
        grad[i] = tile
        tile = tile.astype(bf16)
        rotated.append(split(dot_tn(lefts[i][0], tile) + dot_tn(lefts[i][1], tile)))
    rotated = [product(rotated[i], rights[i], 1, 0) for i in here]
    steps = []
    for i in here:
        new_moment = decay * moment[i] + (1.0 - decay) * rotated[i]
        new_variance = decay * variance[i] + (1.0 - decay) * rotated[i] * rotated[i]
        out_mom[i] = new_moment
        out_var[i] = new_variance
        steps.append(split(new_moment / (jnp.sqrt(new_variance) + adam_eps)))
    returned = [split(product(lefts[i], steps[i], 1, 0)) for i in here]
    returned = [product(returned[i], rights[i], 1, 1) for i in here]
    for i in here:
        out[i] = master[i] - matrix_rate * returned[i]


def owner_call(used, home, near, far, *arrays):
    count = arrays[0].shape[0]
    per = min(8, count)
    block = pl.BlockSpec((per, BS, BS), lambda i, *_: (i, 0, 0))
    return pl.pallas_call(
        functools.partial(owner_kernel, per),
        out_shape=[jax.ShapeDtypeStruct(arrays[0].shape, f32)] * 4,
        grid_spec=pltpu.PrefetchScalarGridSpec(
            num_scalar_prefetch=2,
            grid=(count // per,),
            in_specs=[pl.BlockSpec((per * BS, BS), lambda i, *_: (i, 0))] * 2 + [block] * 5,
            out_specs=[block] * 4,
        ),
        compiler_params=params(),
        cost_estimate=cost(count * 88 * BS**3, count * BS * BS * 38),
    )(used, home, stay(near), stay(far), *arrays)


def reduce_kernel(carrying, last, *refs):
    block, arrived, *refs = refs
    total = block[...].astype(f32) + arrived[...].astype(f32)
    if carrying:
        carried, *refs = refs
        total = total + carried[...].astype(f32)
    if last:
        [out] = refs
    else:
        following, out, later = refs
        later[...] = following[...]
    out[...] = total.astype(bf16)


def reduce_call(j, n, buffer, arrived, carried, payload):
    last = j >= 2
    at = lambda j, x_rel: pl.BlockSpec((payload, BS), lambda i: ((j * 2 + x_rel) * 2 + n, 0))
    whole = fixed((payload, BS))
    operands = [stay(buffer), stay(arrived)] + ([] if carried is None else [stay(carried)])
    specs = [at(j, 0)] + [whole] * (len(operands) - 1)
    if not last:
        operands.append(stay(buffer))
        specs.append(at(j + 2, 1))
    outs = [pltpu.HBM((payload, BS), bf16)] * (1 if last else 2)
    made = pl.pallas_call(
        functools.partial(reduce_kernel, carried is not None, last),
        out_shape=outs,
        grid=(1,),
        in_specs=specs,
        out_specs=[whole] * len(outs),
        compiler_params=params(8),
        cost_estimate=cost(payload * BS * 3, payload * BS * 12),
    )(*operands)
    return (made[0], None) if last else made


class Routes:
    def __init__(self, dp_n):
        pairs = [(d, t) for d in range(dp_n) for t in range(TENSOR)]
        at = lambda d, t: d * TENSOR + t
        home = [(d, t) for d, t in pairs if d % 2 == t]
        away = [(d, t) for d, t in pairs if d % 2 != t]
        self.core_all = [(at(d, t), at(d ^ 1, t)) for d, t in pairs]
        self.core_out = [(at(d, t), at(d ^ 1, t)) for d, t in home]
        self.core_in = [(at(d, t), at(d ^ 1, t)) for d, t in away]
        self.y_all = [(at(d, t), at(d, 1 - t)) for d, t in pairs]
        self.y_out = [(at(d, t), at(d, 1 - t)) for d, t in home]
        self.y_in = [(at(d, t), at(d, 1 - t)) for d, t in away]
        self.x_home = [(at(d, t), at(d ^ 2, t)) for d, t in home]
        self.x_away = [(at(d, t), at(d ^ 2, t)) for d, t in away]
        self.x_all = [(at(d, t), at(d ^ 2, t)) for d, t in pairs]
        self.z_all = [(at(d, t), at((d + 4) % dp_n, t)) for d, t in pairs]
        self.z_home = [(at(d, t), at((d + 4) % dp_n, t)) for d, t in home]


def send(value, route):
    return lax.ppermute(value, AXES, route)


def shards(
    patches,
    cotangent,
    image_size,
    block_slot,
    pinv,
    master_slots,
    left_basis,
    right_basis,
    mom_slots,
    var_slots,
    vec_master,
    vec_mom,
    vec_var,
):
    dp_n = lax.axis_size("dp")
    dp_pos = lax.axis_index("dp")
    y_pos = lax.axis_index("tensor")
    core = dp_pos % 2
    home = core == y_pos
    routes = Routes(dp_n)
    grid3 = dp_n == 16
    x_pos = (dp_pos // 2) % 2
    half_at = (x_pos if grid3 else x_pos * 0).astype(jnp.int32).reshape(1)
    tokens_n = patches.shape[0]
    slots_per = master_slots.shape[1]
    vec_per = vec_master.shape[1]
    slots_n = slots_per * dp_n
    payload = slots_per * BS + VEC_ROWS

    patches = jnp.where(home, patches, send(patches, routes.core_out))
    cotangent = jnp.where(home, cotangent, send(cotangent, routes.core_out))
    size_row = jnp.where(home, image_size, send(image_size, routes.core_out))[0]
    own_slots = block_slot[0]
    slot_other = send(block_slot, routes.y_all)

    lengths = jnp.where(
        size_row == 0, LEN_A, jnp.where(size_row == 1, LEN_B, jnp.where(size_row == 2, LEN_C, 0))
    )
    order = jnp.arange(IMG_DEV)
    ends_at = jnp.sum(jnp.where(order[None, :] <= order[:, None], lengths[None, :], 0), axis=1)
    places = jnp.arange(tokens_n)
    segment = jnp.sum((places[:, None] >= ends_at[None, :]).astype(jnp.int32), axis=1)
    in_image = segment[:, None] == order[None, :]
    select = jnp.stack(
        [jnp.any(in_image & (size_row == s)[None, :], axis=1) for s in range(3)], axis=1
    )
    valid_col = (segment < IMG_DEV).astype(f32)[:, None]
    seg_col = segment[:, None]
    seg_row = segment[None, :]
    blocks_n = tokens_n // ROWS
    starts = jnp.arange(blocks_n) * ROWS
    begun = ends_at[None, :] <= starts[:, None]
    first_tok = jnp.max(jnp.where(begun, ends_at[None, :], 0), axis=1)
    after = ends_at[None, :] > (starts + ROWS - 1)[:, None]
    last_tok = jnp.min(jnp.where(after, ends_at[None, :], tokens_n), axis=1)
    first_blk = (first_tok // ROWS).astype(jnp.int32)
    last_blk = ((last_tok + ROWS - 1) // ROWS).astype(jnp.int32)
    first_key = (first_tok // KEYS).astype(jnp.int32)
    last_key = ((last_tok + KEYS - 1) // KEYS).astype(jnp.int32)

    select_low = select.astype(bf16)
    class_col = jnp.sum(jnp.where(select, jnp.arange(1, 4)[None, :], 0), axis=1, keepdims=True) - 1
    present = jnp.any(select.reshape(blocks_n, ROWS, 3), axis=1).astype(jnp.int32)

    def expand(which):
        return expand_call(which, present, half_at, patches, class_col, pinv)

    vec_low = jnp.pad(vec_master[0].astype(bf16), (0, VEC_ROWS * BS - vec_per))
    own_pack = jnp.concatenate(
        [
            master_slots[0].astype(bf16).reshape(slots_per * BS, BS),
            vec_low.reshape(VEC_ROWS, BS),
        ],
        axis=0,
    )
    flag = home.astype(jnp.int32).reshape(1)
    if grid3:
        z_pos = dp_pos // 4
        pack = own_pack
        chunks, first, second, owner = [], [], [], []
        middle_row = slots_per * BS // 2
        for j in range(4):
            beside_x, beside_y = send(pack, routes.x_all), send(pack, routes.y_all)
            if j < 3:
                further = send(pack, routes.z_all)
                work = [expand(j)] + ([slot_other] if j == 0 else [])
                further, chunk, *work = fence(further, *work)
                chunks.append(chunk)
                if j == 0:
                    [slot_other] = work
            else:
                beside_x, chunk = fence(beside_x, expand(j))
                chunks.append(chunk)
            corner = jnp.concatenate(
                [send(beside_x[:middle_row], routes.y_all), send(beside_y[middle_row:], routes.x_all)],
                axis=0,
            )
            near_two = send(jnp.where(home, beside_y, pack), routes.core_all)
            far_two = send(jnp.where(home, corner, beside_x), routes.core_all)
            first += [pack, near_two, beside_x, far_two]
            second += [beside_y, near_two, corner, far_two]
            for x_rel in range(2):
                for n in range(2):
                    owner.append(((z_pos - j) % 4) * 4 + (x_pos ^ x_rel) * 2 + (core ^ n))
            if j < 3:
                pack = further
        first = [v[None] for v in first]
        second = [v[None] for v in second]
        owner = jnp.stack(owner).astype(jnp.int32)
    else:
        everything = lax.all_gather(own_pack, AXES, axis=0)
        everything = everything.reshape(dp_n, TENSOR, payload, BS)
        first = [jnp.where(core == 0, everything[:, 0], everything[:, 1])]
        second = []
        owner = jnp.arange(dp_n, dtype=jnp.int32)
        chunks = [expand(c) for c in range(CHUNKS)]
    slot_list = jnp.where(home, block_slot, slot_other)[0]
    named = slot_list[None, :] == jnp.arange(slots_n)[:, None]
    used = jnp.any(named, axis=1)
    drow = jnp.where(used, jnp.sum(jnp.where(named, TARGET_ROW[None, :], 0), axis=1), -1)
    dcol = jnp.sum(jnp.where(named, TARGET_COL[None, :], 0), axis=1)
    weights, vec_rows = gather_tiles(first, second, owner, drow, dcol, flag, slots_per, dp_n)
    vec = vec_rows.reshape(dp_n, VEC_ROWS * BS)[:, :vec_per].astype(f32).reshape(1, dp_n * vec_per)

    embedded = embed_call(half_at, chunks, vec, weights)
    embedded_other = send(embedded, routes.core_all)
    core_flag = core.astype(jnp.int32).reshape(1)

    caches = []
    hidden, own, recv = None, embedded, embedded_other
    for layer in range(LAYERS):
        hidden, normed, queries, keys, values = qkv_call(
            layer, hidden, own, recv, core_flag, vec, weights
        )
        mixed, lse, part = attend_call(
            layer, first_blk, last_blk, queries, keys, values, seg_col, seg_row, vec, weights
        )
        other = send(part, routes.core_all)
        middle, normed2, act, slope, own = mlp_call(layer, hidden, part, other, vec, weights)
        recv = send(own, routes.core_all)
        caches.append((hidden, normed, queries, keys, values, mixed, lse, middle, normed2, act, slope))
        hidden = middle
    out_low = ((hidden + (own.astype(f32) + recv.astype(f32))) * valid_col).astype(bf16)

    owners = jnp.arange(dp_n)
    if grid3:
        place = (
            ((z_pos - 1 - owners // 4) % 4) * 4
            + (x_pos ^ ((owners // 2) % 2)) * 2
            + (core ^ (owners % 2))
        ).astype(jnp.int32)
    else:
        place = owners.astype(jnp.int32)
    slot_owner = slot_list // slots_per
    owner_place = jnp.sum(
        jnp.where(slot_owner[:, None] == owners[None, :], place[None, :], 0), axis=1
    )
    tile_pos = (owner_place * payload + (slot_list % slots_per) * BS).astype(jnp.int32)
    vec_pos = (place * payload + slots_per * BS).astype(jnp.int32)
    total_rows = dp_n * payload
    where_to = jnp.concatenate([half_at, flag if grid3 else flag * 0 + 1])
    offsets = {"base": 0}
    count = BASE_PIX // BS * (HALF // BS)
    for layer in range(LAYERS):
        for name, size in (("qkv", 3 * D * HALF), ("out", D * HALF), ("up", D * HALF_FF), ("down", D * HALF_FF)):
            offsets[name, layer] = count
            count += size // (BS * BS)

    def place_tiles(key, matrix, arrived, buffer):
        tiles = matrix.size // (BS * BS)
        pos = tile_pos[offsets[key] : offsets[key] + tiles]
        rows_n = matrix.shape[0] // 2 if matrix.shape[0] > HALF else HALF
        return scatter_matrix(pos, matrix, arrived, where_to, buffer, total_rows, rows_n)

    def place_base(rel, matrix, arrived, buffer):
        size = BASE_PIX * HALF // (BS * BS) // 2
        low_pos, high_pos = tile_pos[:size], tile_pos[size : 2 * size]
        pos = jnp.where(half_at[0] == rel, low_pos, high_pos)
        return scatter_matrix(pos, matrix, arrived, where_to, buffer, total_rows, D)

    def over(matrix):
        return send(matrix, routes.y_in) if grid3 else None

    def beside(matrix):
        return send(other_half(half_at, matrix), routes.x_away) if grid3 else None

    def summed(matrix, arrived):
        return half_sum(half_at, matrix, arrived) if grid3 else None

    def hold(*arrays):
        kept = [a for a in arrays if a is not None]
        done = iter(fence(*kept))
        return [None if a is None else next(done) for a in arrays]

    top, low = 1, 0
    vec_grads = [None] * LAYERS

    def mlp_step(layer, grad, own, recv):
        middle, normed2, act, slope = caches[layer][7:11]
        made = mlp_back_call(layer, grad, own, recv, valid_col, middle, slope, vec, weights)
        if own is not None:
            return made
        return [made[0]] + list(made)

    def attend_step(layer, grad, part, other, lse):
        hid_in, normed, queries, keys, values, mixed = caches[layer][:6]
        return attend_back_call(
            layer, first_key, last_key, grad, part, other, queries, keys, values, mixed, lse,
            seg_col, seg_row, weights,
        )

    grad, grad_low, du, part, dg2, ds2, db1, db2 = mlp_step(top, cotangent, None, None)
    other = send(part, routes.core_all)
    gd1 = dot_tn(caches[top][9], grad_low).astype(bf16)
    gu1 = dot_tn(caches[top][8], du).astype(bf16)
    lse, gd1, gu1, out_low = fence(caches[top][6], gd1, gu1, out_low)
    ad1 = over(gd1)
    grad, grad_low, dq, dk, dv, dbo = attend_step(top, grad, part, other, lse)
    vec, dbo, ad1, gu1 = hold(vec, dbo, ad1, gu1)
    au1 = over(gu1)
    own, dg1, ds1, dbq, dbv = qkv_back_call(top, dq, dk, dv, caches[top][0], vec, weights)
    recv = send(own, routes.core_all)
    go1 = dot_tn(caches[top][5], grad_low).astype(bf16)
    gq1 = dot_tn(caches[top][1], jnp.concatenate([dq, dk, dv], axis=1)).astype(bf16)
    vec_grads[top] = [dg1, ds1, dbq, dbv, dbo, dg2, ds2, db1, db2]
    grad, grad_low, du, part, dg2, ds2, db1, db2 = mlp_step(low, grad, own, recv)
    other = send(part, routes.core_all)
    db2, au1, go1, gq1 = hold(db2, au1, go1, gq1)
    xq1, ao1 = beside(gq1), over(go1)
    gd0 = dot_tn(caches[low][9], grad_low).astype(bf16)
    gu0 = dot_tn(caches[low][8], du).astype(bf16)
    lse, gd0, gu0, xq1, ao1 = hold(caches[low][6], gd0, gu0, xq1, ao1)
    hq1 = summed(gq1, xq1)
    ad0 = over(gd0)
    xu0 = beside(gu0)
    buffer = place_tiles(("down", top), gd1, ad1, None)
    buffer = place_tiles(("up", top), gu1, au1, buffer)
    grad, grad_low, dq, dk, dv, dbo = attend_step(low, grad, part, other, lse)
    vec, dbo, ad0, xu0, hq1, buffer = hold(vec, dbo, ad0, xu0, hq1, buffer)
    au0 = over(summed(gu0, xu0))
    aq1 = over(hq1)
    own, dg1, ds1, dbq, dbv = qkv_back_call(low, dq, dk, dv, caches[low][0], vec, weights)
    recv = send(own, routes.core_all)
    gq0 = dot_tn(caches[low][1], jnp.concatenate([dq, dk, dv], axis=1)).astype(bf16)
    vec_grads[low] = [dg1, ds1, dbq, dbv, dbo, dg2, ds2, db1, db2]
    xq0 = beside(gq0)
    grad_emb, grad_emb_bias = embed_back_call(core_flag, grad, own, recv)
    middle = CHUNKS // 2

    def base_grad(parts):
        return jnp.concatenate([dot_tn(c, grad_emb).astype(bf16) for c in parts], axis=0)

    gbt = base_grad(chunks[middle:])
    gbt, au0, xq0 = hold(gbt, au0, xq0)
    xb = send(gbt, routes.x_away) if grid3 else None
    aq0 = over(summed(gq0, xq0))
    gbm = base_grad(chunks[:middle])
    vec_grad = pack_call([grad_emb_bias] + vec_grads[0] + vec_grads[1], dp_n, vec_per)
    go0 = dot_tn(caches[low][5], grad_low).astype(bf16)
    ao0, av = over(go0), over(vec_grad)
    buffer = place_tiles(("out", top), go1, ao1, buffer)
    buffer = place_tiles(("down", low), gd0, ad0, buffer)
    buffer = place_tiles(("up", low), gu0, au0, buffer)
    buffer = place_base(1, gbt, None, buffer)
    gbm, xb, aq0, ao0, av, aq1, buffer = hold(gbm, xb, aq0, ao0, av, aq1, buffer)
    ab = over(half_sum(half_at * 0, gbm, xb)) if grid3 else None
    buffer = place_tiles(("qkv", top), gq1, aq1, buffer)
    buffer = place_tiles(("out", low), go0, ao0, buffer)
    buffer = scatter_vec(vec_pos, vec_grad, av, buffer)
    buffer = place_tiles(("qkv", low), gq0, aq0, buffer)
    base_weight = weights["base", 0]
    ab, buffer, base_weight, out_low = hold(ab, buffer, base_weight, out_low)
    weights["base", 0] = base_weight
    buffer = place_base(0, gbm, ab, buffer)

    if grid3:
        token = jnp.zeros((8, BS), f32)
        order = (1, 0)
        resized = resize_call(weights, pinv)
        carried = {n: None for n in order}
        blocks = buffer.reshape(4, 2, 2, payload, BS)
        across = {n: send(blocks[0, 1, n], routes.x_home) for n in order}
        following = {n: blocks[1, 1, n] for n in order}
        rounded = {}
        for j in range(4):
            for n in order:
                extra = None
                if j == 0 and n == order[0]:
                    extra = resized
                token, across[n], carried[n], extra = hold(token, across[n], carried[n], extra)
                if extra is not None:
                    resized = extra
                arrived = across[n]
                if j < 3:
                    across[n] = send(following[n], routes.x_home)
                total, following[n] = reduce_call(j, n, buffer, arrived, carried[n], payload)
                if j < 3:
                    carried[n] = send(total, routes.z_home)
                else:
                    rounded[n] = total
        near_grad, far_grad = rounded[0], send(rounded[1], routes.core_out)
    else:
        held = buffer.reshape(dp_n, 1, payload, BS).astype(f32)
        nothing = jnp.zeros_like(held)
        both = jnp.concatenate(
            [jnp.where(core == 0, held, nothing), jnp.where(core == 0, nothing, held)], axis=1
        )
        used_rows = jnp.repeat(used, BS).reshape(dp_n, 1, slots_per * BS, 1)
        used_rows = jnp.concatenate(
            [used_rows, jnp.ones((dp_n, 1, VEC_ROWS, 1), bool)], axis=2
        )
        both = jnp.where(used_rows, both, 0.0).reshape(dp_n * TENSOR * payload, BS)
        near_grad = lax.psum_scatter(both, AXES, scatter_dimension=0, tiled=True).astype(bf16)
        far_grad = near_grad
        resized = resize_call(weights, pinv)

    output = jnp.where(home, out_low, send(out_low, routes.y_out)).astype(f32)
    grad_pixels = sum(
        dot(grad_emb * select_low[:, s : s + 1], resized[s]) for s in range(3)
    ).astype(bf16)
    pixels_other = send(grad_pixels, routes.core_all)
    pixel_sides = [
        grad_pixels[:, s * HALF : (s + 1) * HALF].astype(f32)
        + pixels_other[:, s * HALF : (s + 1) * HALF].astype(f32)
        for s in range(TENSOR)
    ]
    near = jnp.where(core == 0, pixel_sides[0], pixel_sides[1])
    far = jnp.where(core == 0, pixel_sides[1], pixel_sides[0]).astype(bf16)
    patch_grad = jnp.where(home, near, send(far, routes.y_out).astype(f32))

    my_slots = dp_pos * slots_per + jnp.arange(slots_per)
    mine_used = jnp.any(own_slots[None, :] == my_slots[:, None], axis=1).astype(jnp.int32)
    owned_grad, new_master, new_mom, new_var = owner_call(
        mine_used, flag, near_grad, far_grad, master_slots[0], left_basis[0], right_basis[0], mom_slots[0], var_slots[0]
    )
    vec_rows = jnp.where(home, near_grad[slots_per * BS :], far_grad[slots_per * BS :])
    owned_vec_grad = vec_rows.astype(f32).reshape(VEC_ROWS * BS)[:vec_per]
    new_vec_mom = decay * vec_mom[0] + (1.0 - decay) * owned_vec_grad
    new_vec_var = decay * vec_var[0] + (1.0 - decay) * owned_vec_grad * owned_vec_grad
    new_vec = vec_master[0] - vector_rate * new_vec_mom / (jnp.sqrt(new_vec_var) + adam_eps)
    return (
        output,
        patch_grad,
        owned_grad[None],
        new_master[None],
        new_mom[None],
        new_var[None],
        owned_vec_grad[None],
        new_vec[None],
        new_vec_mom[None],
        new_vec_var[None],
    )


def solution(mesh):
    slots = P("tensor", "dp", None, None)
    vectors = P("tensor", "dp")
    tokens = P("dp", None)
    in_specs = (tokens, tokens, tokens, P("tensor", None), P()) + (slots,) * 5 + (vectors,) * 3
    out_specs = (tokens, P("dp", "tensor")) + (slots,) * 4 + (vectors,) * 4
    return jax.shard_map(shards, mesh=mesh, in_specs=in_specs, out_specs=out_specs, check_vma=False)
```

```python
import functools

import jax
import jax.numpy as jnp
import numpy as np
from jax import lax
from jax.experimental import pallas as pl
from jax.experimental.pallas import tpu as pltpu
from jax.sharding import PartitionSpec as P

D = 768
HEAD_DIM = 64
FF = 3072
BASE_PIX = 3072
LAYERS = 2
LEN_A = 196
LEN_B = 225
LEN_C = 576
IMG_DEV = 5
BS = 128
TENSOR = 2
HALF = D // TENSOR
HALF_FF = FF // TENSOR
HEADS = HALF // HEAD_DIM
ROWS = 256
KEYS = 512
VEC_ROWS = 16
CHUNKS = 4

AXES = ("dp", "tensor")
precise = lax.Precision.HIGHEST
masked_score = -1e30
norm_eps = 1e-06
adam_eps = 1e-08
decay = 0.5
matrix_rate = 0.05
vector_rate = 0.3
f32 = jnp.float32
bf16 = jnp.bfloat16
MIB = 1024 * 1024

WEIGHTS = [("base", 0, BASE_PIX)]
for layer in range(LAYERS):
    WEIGHTS += [("qkv", layer, 3 * D), ("out", layer, D), ("up", layer, FF), ("down", layer, FF)]
STARTS = {}
PANEL_ROWS = 0
for name, layer, size in WEIGHTS:
    STARTS[name, layer] = PANEL_ROWS
    PANEL_ROWS += size


def tile_targets():
    rows, cols = [], []

    def add(start, rows_n, cols_n):
        for i in range(rows_n // BS):
            for j in range(cols_n // BS):
                panel, inner = divmod(j * BS, HALF)
                rows.append(start + panel * rows_n + i * BS)
                cols.append(inner)

    add(STARTS["base", 0], BASE_PIX, HALF)
    for layer in range(LAYERS):
        add(STARTS["qkv", layer], D, 3 * HALF)
        add(STARTS["out", layer], HALF, D)
        add(STARTS["up", layer], D, HALF_FF)
        add(STARTS["down", layer], HALF_FF, D)
    return np.array(rows, np.int32), np.array(cols, np.int32)


TARGET_ROW, TARGET_COL = tile_targets()
LAYER_VECS = (D, D, HALF, HALF, D, D, D, HALF_FF, D)
VEC_NAMES = ("g1", "s1", "bq", "bv", "bo", "g2", "s2", "b1", "b2")


def vec_offsets():
    offset = HALF
    found = []
    for layer in range(LAYERS):
        here = {}
        for name, length in zip(VEC_NAMES, LAYER_VECS):
            here[name] = (offset, length)
            offset += length
        found.append(here)
    return found


VEC_AT = vec_offsets()


def params(limit=24):
    return pltpu.CompilerParams(
        dimension_semantics=("arbitrary",), vmem_limit_bytes=limit * MIB
    )


def cost(flops, nbytes, trans=0):
    return pl.CostEstimate(flops=flops, bytes_accessed=nbytes, transcendentals=trans)


def rows_spec(width):
    return pl.BlockSpec((ROWS, width), lambda i, *_: (i, 0))


def fixed(shape, at=0):
    return pl.BlockSpec(shape, lambda i, *_: (at,) + (0,) * (len(shape) - 1))


def vec_piece(vec_ref, layer, name):
    start, length = VEC_AT[layer][name]
    return vec_ref[:, start : start + length]


def dot(left, right):
    return jnp.dot(left, right, preferred_element_type=f32)


def dot_nt(left, right, precision=None):
    return lax.dot_general(
        left, right, (((1,), (1,)), ((), ())), precision=precision, preferred_element_type=f32
    )


def dot_tn(left, right):
    return lax.dot_general(left, right, (((0,), (0,)), ((), ())), preferred_element_type=f32)


def joined(ref, start, rows_n, panels):
    return jnp.concatenate(
        [ref[start + p * rows_n : start + (p + 1) * rows_n, :] for p in range(panels)], axis=1
    )


def norm_stats(values):
    mean_val = jnp.mean(values, axis=-1, keepdims=True)
    centered = values - mean_val
    inv_std = lax.rsqrt(jnp.mean(centered * centered, axis=-1, keepdims=True) + norm_eps)
    return centered * inv_std, inv_std


def norm_back(values, gain, grad):
    unit, inv_std = norm_stats(values)
    scaled = grad * gain
    mean_s = jnp.mean(scaled, axis=-1, keepdims=True)
    mean_u = jnp.mean(scaled * unit, axis=-1, keepdims=True)
    back = inv_std * (scaled - mean_s - unit * mean_u)
    return (
        back,
        jnp.sum(grad * unit, axis=0, keepdims=True),
        jnp.sum(grad, axis=0, keepdims=True),
    )


def accumulate(ref, value):
    first = pl.program_id(0) == 0

    @pl.when(first)
    def _():
        ref[...] = value

    @pl.when(jnp.logical_not(first))
    def _():
        ref[...] += value


def stay(value):
    return pltpu.with_memory_space_constraint(value, pltpu.HBM)


def fence(*arrays):
    def nothing(*refs):
        pass

    anywhere = pl.BlockSpec(memory_space=pl.ANY)
    return pl.pallas_call(
        nothing,
        out_shape=[jax.ShapeDtypeStruct(a.shape, a.dtype) for a in arrays],
        in_specs=[anywhere] * len(arrays),
        out_specs=[anywhere] * len(arrays),
        input_output_aliases={i: i for i in range(len(arrays))},
        compiler_params=pltpu.CompilerParams(vmem_limit_bytes=MIB),
    )(*[stay(a) if a.size > 32 * 1024 else a for a in arrays])


def gather_kernel(slots, count_a, count_b, owner, drow, dcol, flag, *refs):
    first = refs[:count_a]
    second = refs[count_a : count_a + count_b]
    *panels, vectors, held, sem, vec_sem = refs[count_a + count_b :]

    def copy_all(sources):
        at = 0
        for src in sources:
            for n in range(src.shape[0]):
                who = owner[at]
                at += 1

                def body(i, carried, src=src, n=n, who=who):
                    slot = who * slots + i
                    row = drow[slot]

                    @pl.when(row >= 0)
                    def _():
                        start = pl.multiple_of(i * BS, BS)
                        pltpu.make_async_copy(
                            src.at[n, pl.ds(start, BS), :],
                            held.at[
                                pl.ds(pl.multiple_of(row, BS), BS),
                                pl.ds(pl.multiple_of(dcol[slot], BS), BS),
                            ],
                            sem,
                        ).start()

                    return carried

                lax.fori_loop(0, slots, body, 0)
                pltpu.make_async_copy(
                    src.at[n, pl.ds(slots * BS, VEC_ROWS), :], vectors.at[who], vec_sem
                ).start()

    if count_b:

        @pl.when(flag[0] == 1)
        def _():
            copy_all(first)

        @pl.when(flag[0] == 0)
        def _():
            copy_all(second)
    else:
        copy_all(first)
    pltpu.make_async_copy(held, held, sem).wait()
    at = 0
    for panel in panels:
        size = panel.shape[0]
        pltpu.make_async_copy(held.at[pl.ds(at, size), :], panel, sem).start()
        at += size
    pltpu.make_async_copy(vectors, vectors, vec_sem).wait()
    pltpu.make_async_copy(held, held, sem).wait()


def gather_tiles(first, second, owner, drow, dcol, flag, slots, owners):
    anywhere = pl.BlockSpec(memory_space=pl.ANY)
    *panels, vectors = pl.pallas_call(
        functools.partial(gather_kernel, slots, len(first), len(second)),
        out_shape=[pltpu.HBM((size, HALF), bf16) for unused, unused2, size in WEIGHTS]
        + [jax.ShapeDtypeStruct((owners, VEC_ROWS, BS), bf16)],
        grid_spec=pltpu.PrefetchScalarGridSpec(
            num_scalar_prefetch=4,
            grid=(1,),
            in_specs=[anywhere] * (len(first) + len(second)),
            out_specs=[anywhere] * len(WEIGHTS) + [fixed((owners, VEC_ROWS, BS))],
            scratch_shapes=[
                pltpu.VMEM((PANEL_ROWS, HALF), bf16),
                pltpu.SemaphoreType.DMA,
                pltpu.SemaphoreType.DMA,
            ],
        ),
        compiler_params=params(),
        cost_estimate=cost(0, 4 * PANEL_ROWS * HALF),
    )(owner, drow, dcol, flag, *[stay(v) for v in first], *[stay(v) for v in second])
    return {(name, layer): p for (name, layer, unused), p in zip(WEIGHTS, panels)}, vectors


def scatter_kernel(rows_n, cols_n, steps, paired, parts, pos, part, own, *refs):
    @pl.when(part[1] > 0)
    def _():
        scatter_body(rows_n, cols_n, steps, paired, parts, pos, part, own, *refs)


def scatter_body(rows_n, cols_n, steps, paired, parts, pos, part, own, *refs):
    if paired:
        recv, *refs = refs
        span = pl.num_programs(0) // parts
        here = jnp.logical_or(parts == 1, pl.program_id(0) // span == part[0])
    target, buf, sems = refs[-3:]
    step = pl.program_id(0)
    slot = lax.rem(step, 2)
    per = rows_n // BS * (cols_n // BS)

    def wait(at):
        pltpu.make_async_copy(buf.at[at], buf.at[at], sems.at[at]).wait()

    @pl.when(step >= 2)
    def _():
        wait(slot)

    for i in range(rows_n // BS):
        for j in range(cols_n // BS):
            area = (slice(i * BS, (i + 1) * BS), slice(j * BS, (j + 1) * BS))
            value = own[area]
            if paired:
                more = jnp.where(here, recv[area].astype(f32), 0.0)
                value = (value.astype(f32) + more).astype(bf16)
            buf[slot, i * (cols_n // BS) + j] = value
    for n in range(per):
        pltpu.make_async_copy(
            buf.at[slot, n],
            target.at[pl.ds(pl.multiple_of(pos[step * per + n], 16), BS), :],
            sems.at[slot],
        ).start()

    @pl.when(step == pl.num_programs(0) - 1)
    def _():
        if steps > 1:
            wait(1 - slot)
        wait(slot)


def scatter_matrix(pos, own, recv, part, target, total_rows, rows_n):
    cols_n = own.shape[1]
    steps = own.shape[0] // rows_n
    anywhere = pl.BlockSpec(memory_space=pl.ANY)
    block = pl.BlockSpec((rows_n, cols_n), lambda i, *_: (i, 0))
    paired = recv is not None
    parts = own.shape[0] // recv.shape[0] if paired else 1
    span = steps // parts
    arrived = pl.BlockSpec(
        (rows_n, cols_n), lambda i, pos, part: (jnp.clip(i - part[0] * span, 0, span - 1), 0)
    )
    operands = [stay(own)] + ([stay(recv)] if paired else []) + ([] if target is None else [stay(target)])
    specs = [block] + ([block if parts == 1 else arrived] if paired else [])
    specs += [] if target is None else [anywhere]
    return pl.pallas_call(
        functools.partial(scatter_kernel, rows_n, cols_n, steps, paired, parts),
        out_shape=pltpu.HBM((total_rows, BS), bf16),
        grid_spec=pltpu.PrefetchScalarGridSpec(
            num_scalar_prefetch=2,
            grid=(steps,),
            in_specs=specs,
            out_specs=anywhere,
            scratch_shapes=[
                pltpu.VMEM((2, rows_n // BS * (cols_n // BS), BS, BS), bf16),
                pltpu.SemaphoreType.DMA((2,)),
            ],
        ),
        input_output_aliases={} if target is None else {len(operands) + 1: 0},
        compiler_params=params(12),
        cost_estimate=cost(own.size, own.size * 6),
    )(pos, part, *operands)


def half_sum_kernel(part, own, arrived, out):
    out[...] = (own[...].astype(f32) + arrived[...].astype(f32)).astype(bf16)


def half_sum(part, own, arrived):
    block = arrived.shape
    return pl.pallas_call(
        half_sum_kernel,
        out_shape=pltpu.HBM(block, bf16),
        grid_spec=pltpu.PrefetchScalarGridSpec(
            num_scalar_prefetch=1,
            grid=(1,),
            in_specs=[pl.BlockSpec(block, lambda i, part: (part[0], 0)), fixed(block)],
            out_specs=fixed(block),
        ),
        compiler_params=params(8),
        cost_estimate=cost(arrived.size, arrived.size * 6),
    )(part, stay(own), stay(arrived))


def half_copy_kernel(part, own, out):
    out[...] = own[...]


def other_half(part, own):
    block = (own.shape[0] // 2, own.shape[1])
    return pl.pallas_call(
        half_copy_kernel,
        out_shape=pltpu.HBM(block, bf16),
        grid_spec=pltpu.PrefetchScalarGridSpec(
            num_scalar_prefetch=1,
            grid=(1,),
            in_specs=[pl.BlockSpec(block, lambda i, part: (1 - part[0], 0))],
            out_specs=fixed(block),
        ),
        compiler_params=params(8),
        cost_estimate=cost(0, own.size * 2),
    )(part, stay(own))


def scatter_vec_kernel(paired, pos, own, *refs):
    if paired:
        recv, *refs = refs
    target, buf, sem = refs[-3:]
    value = own[...]
    if paired:
        value = (value.astype(f32) + recv[...].astype(f32)).astype(bf16)
    buf[...] = value

    def body(n, carried):
        pltpu.make_async_copy(
            buf.at[n], target.at[pl.ds(pl.multiple_of(pos[n], 16), VEC_ROWS), :], sem
        ).start()
        return carried

    lax.fori_loop(0, own.shape[0], body, 0)
    pltpu.make_async_copy(buf, buf, sem).wait()


def scatter_vec(pos, own, recv, target):
    anywhere = pl.BlockSpec(memory_space=pl.ANY)
    block = fixed(own.shape)
    paired = recv is not None
    operands = [own] + ([recv] if paired else []) + [stay(target)]
    return pl.pallas_call(
        functools.partial(scatter_vec_kernel, paired),
        out_shape=pltpu.HBM(target.shape, bf16),
        grid_spec=pltpu.PrefetchScalarGridSpec(
            num_scalar_prefetch=1,
            grid=(1,),
            in_specs=[block] * (len(operands) - 1) + [anywhere],
            out_specs=anywhere,
            scratch_shapes=[pltpu.VMEM(own.shape, bf16), pltpu.SemaphoreType.DMA],
        ),
        input_output_aliases={len(operands): 0},
        compiler_params=params(4),
    )(pos, *operands)


def expand_kernel(present, half, patch_ref, class_ref, pinv_ref, out, total):
    for block in range(patch_ref.shape[0] // ROWS):
        rows = slice(block * ROWS, (block + 1) * ROWS)
        total[...] = jnp.zeros_like(total)
        for which in range(3):

            @pl.when(present[block, which] > 0)
            def _(which=which, rows=rows):
                chosen = jnp.where(class_ref[rows, :] == which, patch_ref[rows, :].astype(f32), 0.0)
                total[...] += dot_nt(chosen.astype(bf16), pinv_ref[which])

        out[rows, :] = total[...].astype(bf16)


def expand_call(which, present, half, patches, class_col, pinv):
    tokens = patches.shape[0]
    size = BASE_PIX // CHUNKS
    step = size
    return pl.pallas_call(
        expand_kernel,
        out_shape=jax.ShapeDtypeStruct((tokens, size), bf16),
        grid_spec=pltpu.PrefetchScalarGridSpec(
            num_scalar_prefetch=2,
            grid=(1,),
            in_specs=[
                fixed(patches.shape),
                fixed(class_col.shape),
                pl.BlockSpec(
                    (3, step, pinv.shape[2]),
                    lambda i, present, half: (0, (which + half[0] * (CHUNKS // 2)) % CHUNKS, 0),
                ),
            ],
            out_specs=pl.BlockSpec((tokens, step), lambda i, *_: (0, i)),
            scratch_shapes=[pltpu.VMEM((ROWS, step), f32)],
        ),
        compiler_params=params(),
        cost_estimate=cost(3 * tokens * size * D, tokens * size * 4 + size * D * 6),
    )(present, half, stay(patches), class_col, stay(pinv))


def resize_kernel(base, pinv_ref, out, turned):
    @pl.when(pl.program_id(0) == 0)
    def _():
        turned[...] = base[...].T

    out[0] = dot(turned[...], pinv_ref[0]).astype(bf16)


def resize_call(weights, pinv):
    return pl.pallas_call(
        resize_kernel,
        out_shape=jax.ShapeDtypeStruct((3, HALF, pinv.shape[2]), bf16),
        grid=(3,),
        in_specs=[
            fixed((BASE_PIX, HALF)),
            pl.BlockSpec((1, BASE_PIX, pinv.shape[2]), lambda i: (i, 0, 0)),
        ],
        out_specs=pl.BlockSpec((1, HALF, pinv.shape[2]), lambda i: (i, 0, 0)),
        scratch_shapes=[pltpu.VMEM((HALF, BASE_PIX), bf16)],
        compiler_params=params(),
        cost_estimate=cost(6 * D * BASE_PIX * HALF, 6 * D * BASE_PIX),
    )(stay(weights["base", 0]), stay(pinv))


def embed_back_kernel(core, base, own, recv, out, bias):
    low = (base[...] + (own[...].astype(f32) + recv[...].astype(f32))).astype(bf16)
    out[...] = low
    accumulate(bias, jnp.sum(low.astype(f32), axis=0, keepdims=True))


def embed_back_call(core, base, own, recv):
    tokens = base.shape[0]
    half = pl.BlockSpec((ROWS, HALF), lambda i, core: (i, core[0]))
    return pl.pallas_call(
        embed_back_kernel,
        out_shape=[
            jax.ShapeDtypeStruct((tokens, HALF), bf16),
            jax.ShapeDtypeStruct((1, HALF), f32),
        ],
        grid_spec=pltpu.PrefetchScalarGridSpec(
            num_scalar_prefetch=1,
            grid=(tokens // ROWS,),
            in_specs=[half] * 3,
            out_specs=[rows_spec(HALF), fixed((1, HALF))],
        ),
        compiler_params=params(8),
        cost_estimate=cost(tokens * D, tokens * D * 5),
    )(core, base, own, recv)


def pack_kernel(vec_per, *refs):
    *pieces, out = refs
    out[...] = jnp.zeros_like(out)
    at = 0
    for piece in pieces:
        for k in range(piece.shape[1] // BS):
            owner, row = divmod(at, vec_per // BS)
            out[owner, row : row + 1, :] = piece[:, k * BS : (k + 1) * BS]
            at += 1


def pack_call(pieces, owners, vec_per):
    if vec_per % BS:
        joined = jnp.concatenate(pieces, axis=1)[0]
        joined = jnp.pad(joined, (0, owners * vec_per - joined.shape[0])).reshape(owners, vec_per)
        joined = jnp.pad(joined, ((0, 0), (0, VEC_ROWS * BS - vec_per)))
        return joined.astype(bf16).reshape(owners, VEC_ROWS, BS)
    return pl.pallas_call(
        functools.partial(pack_kernel, vec_per),
        out_shape=jax.ShapeDtypeStruct((owners, VEC_ROWS, BS), f32),
        grid=(1,),
        in_specs=[fixed(p.shape) for p in pieces],
        out_specs=fixed((owners, VEC_ROWS, BS)),
        compiler_params=params(4),
        cost_estimate=cost(0, owners * vec_per * 8),
    )(*pieces).astype(bf16)


def embed_kernel(half, *refs):
    *parts, vec, weight, out = refs
    size = BASE_PIX // CHUNKS
    total = vec[:, :HALF]
    for c in range(CHUNKS):
        at = lax.rem(c + half[0] * (CHUNKS // 2), CHUNKS)
        rows = pl.ds(pl.multiple_of(at * size, size), size)
        total = total + dot(parts[c][...], weight[rows, :])
    out[...] = total.astype(bf16)


def embed_call(half, chunks, vec, weights):
    tokens = chunks[0].shape[0]
    return pl.pallas_call(
        embed_kernel,
        out_shape=jax.ShapeDtypeStruct((tokens, HALF), bf16),
        grid_spec=pltpu.PrefetchScalarGridSpec(
            num_scalar_prefetch=1,
            grid=(tokens // ROWS,),
            in_specs=[rows_spec(BASE_PIX // CHUNKS)] * CHUNKS
            + [fixed(vec.shape), fixed((BASE_PIX, HALF))],
            out_specs=rows_spec(HALF),
        ),
        compiler_params=params(),
        cost_estimate=cost(2 * tokens * BASE_PIX * HALF, tokens * BASE_PIX * 3),
    )(half, *[stay(c) for c in chunks], vec, stay(weights["base", 0]))


def qkv_kernel(layer, first, core, *refs):
    if first:
        own, recv, vec, weight, hid, normed, q_ref, k_ref, v_ref = refs
        mine, theirs = own[...].astype(f32), recv[...].astype(f32)
        low = core[0] == 0
        values = jnp.concatenate(
            [jnp.where(low, mine, theirs), jnp.where(low, theirs, mine)], axis=1
        )
    else:
        base, own, recv, vec, weight, hid, normed, q_ref, k_ref, v_ref = refs
        values = base[...] + (own[...].astype(f32) + recv[...].astype(f32))
    hid[...] = values
    unit, unused = norm_stats(values)
    low = (unit * vec_piece(vec, layer, "g1") + vec_piece(vec, layer, "s1")).astype(bf16)
    normed[...] = low
    made = dot(low, joined(weight, 0, D, 3))
    q_ref[...] = (made[:, :HALF] + vec_piece(vec, layer, "bq")).astype(bf16)
    k_ref[...] = made[:, HALF : 2 * HALF].astype(bf16)
    v_ref[...] = (made[:, 2 * HALF :] + vec_piece(vec, layer, "bv")).astype(bf16)


def qkv_call(layer, base, own, recv, core, vec, weights):
    tokens = own.shape[0]
    shape = lambda width, kind: jax.ShapeDtypeStruct((tokens, width), kind)
    outs = [shape(D, f32), pltpu.HBM((tokens, D), bf16)] + [shape(HALF, bf16)] * 3
    operands = ([] if base is None else [base]) + [own, recv]
    return pl.pallas_call(
        functools.partial(qkv_kernel, layer, base is None),
        out_shape=outs,
        grid_spec=pltpu.PrefetchScalarGridSpec(
            num_scalar_prefetch=1,
            grid=(tokens // ROWS,),
            in_specs=[rows_spec(o.shape[1]) for o in operands]
            + [fixed(vec.shape), fixed((3 * D, HALF))],
            out_specs=[rows_spec(o.shape[1]) for o in outs],
        ),
        compiler_params=params(),
        cost_estimate=cost(2 * tokens * D * 3 * HALF, tokens * D * 14),
    )(core, *operands, vec, weights["qkv", layer])


def head_masks():
    lane = lax.broadcasted_iota(jnp.int32, (1, 2 * HEAD_DIM), 1)
    low = (lane < HEAD_DIM).astype(f32).astype(bf16)
    high = (lane >= HEAD_DIM).astype(f32).astype(bf16)
    return low, high


def attend_kernel(
    layer, low_ref, high_ref, q_ref, k_ref, v_ref, seg_q, seg_k, vec, w_out, o_ref, lse_ref, part,
    scores_ref, top_ref, acc_ref,
):
    step = pl.program_id(0)
    first, last = low_ref[step], high_ref[step]
    masks = head_masks()
    scale = jnp.asarray(HEAD_DIM ** (-0.5), bf16)
    lane = lax.broadcasted_iota(jnp.int32, (1, BS), 1)
    sums = [(lane == HEAD_DIM).astype(f32).astype(bf16), (lane == 0).astype(f32).astype(bf16)]
    top_ref[...] = jnp.full(top_ref.shape, masked_score, f32)
    acc_ref[...] = jnp.zeros_like(acc_ref)
    seg_col = seg_q[...]

    def score_block(block, carried):
        rows = pl.ds(pl.multiple_of(block * ROWS, ROWS), ROWS)
        same = seg_col == seg_k[:, rows]
        for pair in range(HEADS // 2):
            cols = slice(pair * BS, (pair + 1) * BS)
            q_two = q_ref[:, cols] * scale
            k_two = k_ref[rows, cols]
            for side in range(2):
                head = 2 * pair + side
                scores = jnp.where(same, dot_nt(q_two * masks[side], k_two), masked_score)
                scores_ref[head, block] = scores
                top = top_ref[head]
                for piece in range(ROWS // BS):
                    top = jnp.maximum(top, scores[:, piece * BS : (piece + 1) * BS])
                top_ref[head] = top
        return carried

    lax.fori_loop(first, last, score_block, 0)
    tops = [jnp.max(top_ref[head], axis=1, keepdims=True) for head in range(HEADS)]

    def mix_block(block, carried):
        rows = pl.ds(pl.multiple_of(block * ROWS, ROWS), ROWS)
        for pair in range(HEADS // 2):
            v_two = v_ref[rows, pair * BS : (pair + 1) * BS]
            for side in range(2):
                head = 2 * pair + side
                expo = jnp.exp(scores_ref[head, block] - tops[head]).astype(bf16)
                acc_ref[head] += dot(expo, v_two * masks[side] + sums[side])
        return carried

    lax.fori_loop(first, last, mix_block, 0)
    totals = jnp.zeros((ROWS, BS), f32)
    for pair in range(HEADS // 2):
        sides = []
        for side in range(2):
            head = 2 * pair + side
            mixed = acc_ref[head]
            at = HEAD_DIM * (1 - side)
            total = mixed[:, at : at + 1]
            totals = jnp.where(lane == head, tops[head] + jnp.log(total), totals)
            sides.append(mixed * (1.0 / total))
        o_ref[:, pair * BS : (pair + 1) * BS] = jnp.where(lane < HEAD_DIM, *sides).astype(bf16)
    lse_ref[...] = totals.T[0:8, :]
    low = o_ref[...]
    bias = vec_piece(vec, layer, "bo")
    part[...] = (dot(low, joined(w_out, 0, HALF, TENSOR)) + bias).astype(bf16)


def attend_call(layer, first, last, queries, keys, values, seg_col, seg_row, vec, weights):
    tokens = queries.shape[0]
    return pl.pallas_call(
        functools.partial(attend_kernel, layer),
        out_shape=[
            jax.ShapeDtypeStruct((tokens, HALF), bf16),
            jax.ShapeDtypeStruct((8, tokens), f32),
            jax.ShapeDtypeStruct((tokens, D), bf16),
        ],
        grid_spec=pltpu.PrefetchScalarGridSpec(
            num_scalar_prefetch=2,
            grid=(tokens // ROWS,),
            in_specs=[
                rows_spec(HALF),
                fixed(keys.shape),
                fixed(values.shape),
                rows_spec(1),
                fixed(seg_row.shape),
                fixed(vec.shape),
                fixed((D, HALF)),
            ],
            out_specs=[
                rows_spec(HALF),
                pl.BlockSpec((8, ROWS), lambda i, *_: (0, i)),
                rows_spec(D),
            ],
            scratch_shapes=[
                pltpu.VMEM((HEADS, tokens // ROWS, ROWS, ROWS), f32),
                pltpu.VMEM((HEADS, ROWS, BS), f32),
                pltpu.VMEM((HEADS, ROWS, BS), f32),
            ],
        ),
        compiler_params=params(),
        cost_estimate=cost(8 * HEADS * tokens * tokens * BS, tokens * D * 8, HEADS * tokens * tokens),
    )(first, last, queries, keys, values, seg_col, seg_row, vec, weights["out", layer])


def gelu_parts(values):
    cdf = 0.5 * (1.0 + lax.erf(values * 0.7071067811865476))
    pdf = 0.3989422804014327 * jnp.exp(-0.5 * values * values)
    return values * cdf, cdf + values * pdf


def mlp_kernel(layer, base, own, recv, vec, w_up, w_down, hid, normed, act, slope, part):
    values = base[...] + (own[...].astype(f32) + recv[...].astype(f32))
    hid[...] = values
    unit, unused = norm_stats(values)
    low = (unit * vec_piece(vec, layer, "g2") + vec_piece(vec, layer, "s2")).astype(bf16)
    normed[...] = low
    bias_up = vec_piece(vec, layer, "b1")
    for pair in range(HALF_FF // D):
        area = slice(pair * D, (pair + 1) * D)
        up = dot(low, joined(w_up, pair * 2 * D, D, 2)) + bias_up[:, area]
        gelu, grad = gelu_parts(up)
        act[:, area] = gelu.astype(bf16)
        slope[:, area] = grad.astype(bf16)
    bias_down = vec_piece(vec, layer, "b2")
    part[...] = (dot(act[...], joined(w_down, 0, HALF_FF, TENSOR)) + bias_down).astype(bf16)


def mlp_call(layer, base, own, recv, vec, weights):
    tokens = base.shape[0]
    shape = lambda width, kind: jax.ShapeDtypeStruct((tokens, width), kind)
    kept = lambda width: pltpu.HBM((tokens, width), bf16)
    outs = [shape(D, f32), kept(D), kept(HALF_FF), kept(HALF_FF), shape(D, bf16)]
    return pl.pallas_call(
        functools.partial(mlp_kernel, layer),
        out_shape=outs,
        grid=(tokens // ROWS,),
        in_specs=[rows_spec(D)] * 3
        + [
            fixed(vec.shape),
            fixed((2 * HALF_FF, HALF)),
            fixed((2 * HALF_FF, HALF)),
        ],
        out_specs=[rows_spec(o.shape[1]) for o in outs],
        compiler_params=params(),
        cost_estimate=cost(4 * tokens * D * HALF_FF, tokens * D * 24, 2 * tokens * HALF_FF),
    )(base, own, recv, vec, weights["up", layer], weights["down", layer])


def mlp_back_kernel(layer, summed, *refs):
    if summed:
        base, own, recv, *refs = refs
        (hid, slope, vec, w_up, w_down, grad_full, grad_low, du_ref, back, dgain, dshift, db1, db2) = refs
        values = base[...].astype(f32) + (own[...].astype(f32) + recv[...].astype(f32))
        grad_full[...] = values
        low = values.astype(bf16)
    else:
        base, valid, *refs = refs
        (hid, slope, vec, w_up, w_down, grad_low, du_ref, back, dgain, dshift, db1, db2) = refs
        low = (base[...].astype(f32) * valid[...]).astype(bf16)
    grad_low[...] = low
    accumulate(db2, jnp.sum(low.astype(f32), axis=0, keepdims=True))
    for part in range(HALF_FF // D):
        area = slice(part * D, (part + 1) * D)
        rows = jnp.concatenate(
            [w_down[p * HALF_FF + part * D : p * HALF_FF + (part + 1) * D, :] for p in range(TENSOR)],
            axis=1,
        )
        du_ref[:, area] = (dot_nt(low, rows) * slope[:, area].astype(f32)).astype(bf16)
    grad_normed = dot_nt(du_ref[...], joined(w_up, 0, D, HALF_FF // HALF))
    accumulate(db1, jnp.sum(du_ref[...].astype(f32), axis=0, keepdims=True))
    part_back, gain_grad, shift_grad = norm_back(hid[...], vec_piece(vec, layer, "g2"), grad_normed)
    back[...] = part_back.astype(bf16)
    accumulate(dgain, gain_grad)
    accumulate(dshift, shift_grad)


def mlp_back_call(layer, base, own, recv, valid, hid, slope, vec, weights):
    tokens = base.shape[0]
    summed = own is not None
    shape = lambda width, kind: jax.ShapeDtypeStruct((tokens, width), kind)
    line = lambda width: jax.ShapeDtypeStruct((1, width), f32)
    outs = ([shape(D, f32)] if summed else []) + [shape(D, bf16), shape(HALF_FF, bf16), shape(D, bf16)]
    lines = [line(D), line(D), line(HALF_FF), line(D)]
    extra = [own, recv] if summed else [valid]
    return pl.pallas_call(
        functools.partial(mlp_back_kernel, layer, summed),
        out_shape=outs + lines,
        grid=(tokens // ROWS,),
        in_specs=[rows_spec(D)]
        + [rows_spec(e.shape[1]) for e in extra]
        + [
            rows_spec(D),
            rows_spec(HALF_FF),
            fixed(vec.shape),
            fixed((2 * HALF_FF, HALF)),
            fixed((2 * HALF_FF, HALF)),
        ],
        out_specs=[rows_spec(o.shape[1]) for o in outs] + [fixed(o.shape) for o in lines],
        compiler_params=params(),
        cost_estimate=cost(4 * tokens * D * HALF_FF, tokens * D * 24),
    )(base, *extra, stay(hid), stay(slope), vec, weights["up", layer], weights["down", layer])


def attend_back_kernel(
    low_ref, high_ref, base, own, recv, q_ref, k_ref, v_ref, o_ref, lse_ref, seg_k, seg_q, w_out,
    full_ref, grad_low, dq_ref, dk_ref, dv_ref, dbo, dk_acc, dv_acc, dq_acc, do_ref,
):
    step = pl.program_id(0)

    @pl.when(step == 0)
    def _():
        dk_acc[...] = jnp.zeros_like(dk_acc)
        dv_acc[...] = jnp.zeros_like(dv_acc)

    values = base[...].astype(f32) + (own[...].astype(f32) + recv[...].astype(f32))
    full_ref[...] = values
    low = values.astype(bf16)
    grad_low[...] = low
    accumulate(dbo, jnp.sum(low.astype(f32), axis=0, keepdims=True))
    do_ref[...] = dot_nt(low, joined(w_out, 0, HALF, TENSOR)).astype(bf16)
    product = do_ref[...].astype(f32) * o_ref[...].astype(f32)
    head = lax.broadcasted_iota(jnp.int32, (8, HALF), 0)
    lane = lax.broadcasted_iota(jnp.int32, (8, HALF), 1)
    pick = ((lane >= head * HEAD_DIM) & (lane < (head + 1) * HEAD_DIM)).astype(f32)
    high, rest = split(product)
    pick = pick.astype(bf16)
    inner = dot_nt(pick, high) + dot_nt(pick, rest)
    dq_acc[...] = jnp.zeros_like(dq_acc)
    masks = head_masks()
    scale = jnp.asarray(HEAD_DIM ** (-0.5), bf16)
    seg_row = seg_q[...]

    def one_block(block, carried):
        rows = pl.ds(pl.multiple_of(block * KEYS, KEYS), KEYS)
        same = seg_k[rows, :] == seg_row
        for pair in range(HEADS // 2):
            cols = slice(pair * BS, (pair + 1) * BS)
            q_two = q_ref[:, cols] * scale
            do_two = do_ref[:, cols]
            k_two = k_ref[rows, cols]
            v_two = v_ref[rows, cols]
            dv_two = dk_two = dq_two = None
            for side in range(2):
                at = 2 * pair + side
                q_one = q_two * masks[side]
                do_one = do_two * masks[side]
                scores = dot_nt(k_two, q_one)
                prob = jnp.where(same, jnp.exp(scores - lse_ref[at : at + 1, :]), 0.0)
                grad_prob = dot_nt(v_two, do_one)
                grad_scores = (prob * (grad_prob - inner[at : at + 1, :])).astype(bf16)
                dv_one = dot(prob.astype(bf16), do_one)
                dk_one = dot(grad_scores, q_one)
                dq_one = dot_tn(grad_scores, k_two * masks[side])
                dq_two = dq_one if dq_two is None else dq_two + dq_one
                dv_two = dv_one if dv_two is None else dv_two + dv_one
                dk_two = dk_one if dk_two is None else dk_two + dk_one
            dv_acc[rows, cols] += dv_two
            dk_acc[rows, cols] += dk_two
            dq_acc[:, cols] += dq_two
        return carried

    lax.fori_loop(low_ref[step], high_ref[step], one_block, 0)
    dq_ref[...] = (dq_acc[...] * HEAD_DIM ** (-0.5)).astype(bf16)

    @pl.when(step == pl.num_programs(0) - 1)
    def _():
        dk_ref[...] = dk_acc[...].astype(bf16)
        dv_ref[...] = dv_acc[...].astype(bf16)


def attend_back_call(
    layer, first, last, base, own, recv, queries, keys, values, mixed, lse, seg_col, seg_row, weights
):
    tokens = base.shape[0]
    shape = lambda width, kind: jax.ShapeDtypeStruct((tokens, width), kind)
    whole = (tokens, HALF)
    return pl.pallas_call(
        attend_back_kernel,
        out_shape=[
            shape(D, f32),
            shape(D, bf16),
            shape(HALF, bf16),
            shape(HALF, bf16),
            shape(HALF, bf16),
            jax.ShapeDtypeStruct((1, D), f32),
        ],
        grid_spec=pltpu.PrefetchScalarGridSpec(
            num_scalar_prefetch=2,
            grid=(tokens // ROWS,),
            in_specs=[
                rows_spec(D),
                rows_spec(D),
                rows_spec(D),
                rows_spec(HALF),
                fixed(whole),
                fixed(whole),
                rows_spec(HALF),
                pl.BlockSpec((8, ROWS), lambda i, *_: (0, i)),
                fixed(seg_col.shape),
                pl.BlockSpec((1, ROWS), lambda i, *_: (0, i)),
                fixed((D, HALF)),
            ],
            out_specs=[
                rows_spec(D),
                rows_spec(D),
                rows_spec(HALF),
                fixed(whole),
                fixed(whole),
                fixed((1, D)),
            ],
            scratch_shapes=[
                pltpu.VMEM(whole, f32),
                pltpu.VMEM(whole, f32),
                pltpu.VMEM((ROWS, HALF), f32),
                pltpu.VMEM((ROWS, HALF), bf16),
            ],
        ),
        compiler_params=params(),
        cost_estimate=cost(14 * HEADS * tokens * tokens * BS, tokens * D * 20, HEADS * tokens * tokens),
    )(
        first, last, base, own, recv, stay(queries), stay(keys), stay(values), stay(mixed), lse,
        seg_col, seg_row, weights["out", layer],
    )


def qkv_back_kernel(layer, dq, dk, dv, hid, vec, weight, back, dgain, dshift, dbq, dbv):
    grad_three = jnp.concatenate([dq[...], dk[...], dv[...]], axis=1)
    grad_normed = dot_nt(grad_three, joined(weight, 0, D, 3))
    part_back, gain_grad, shift_grad = norm_back(hid[...], vec_piece(vec, layer, "g1"), grad_normed)
    back[...] = part_back.astype(bf16)
    accumulate(dgain, gain_grad)
    accumulate(dshift, shift_grad)
    accumulate(dbq, jnp.sum(dq[...].astype(f32), axis=0, keepdims=True))
    accumulate(dbv, jnp.sum(dv[...].astype(f32), axis=0, keepdims=True))


def qkv_back_call(layer, dq, dk, dv, hid, vec, weights):
    tokens = dq.shape[0]
    line = lambda width: jax.ShapeDtypeStruct((1, width), f32)
    lines = [line(D), line(D), line(HALF), line(HALF)]
    return pl.pallas_call(
        functools.partial(qkv_back_kernel, layer),
        out_shape=[jax.ShapeDtypeStruct((tokens, D), bf16)] + lines,
        grid=(tokens // ROWS,),
        in_specs=[rows_spec(HALF)] * 3
        + [
            rows_spec(D),
            fixed(vec.shape),
            fixed((3 * D, HALF)),
        ],
        out_specs=[rows_spec(D)] + [fixed(o.shape) for o in lines],
        compiler_params=params(),
        cost_estimate=cost(2 * tokens * D * 3 * HALF, tokens * D * 10),
    )(dq, dk, dv, stay(hid), vec, weights["qkv", layer])


def split(values):
    high = values.astype(bf16)
    return high, (values - high.astype(f32)).astype(bf16)


def product(left, right, left_dim, right_dim):
    def one(a, b):
        return lax.dot_general(
            a, b, (((left_dim,), (right_dim,)), ((), ())), preferred_element_type=f32
        )

    return one(left[0], right[0]) + (one(left[0], right[1]) + one(left[1], right[0]))


def owner_kernel(per, used, home, near, far, master, left, right, moment, variance, grad, out, out_mom, out_var):
    here = range(per)
    first = pl.program_id(0) * per
    lefts = [split(left[i]) for i in here]
    rights = [split(right[i]) for i in here]
    rotated = []
    for i in here:
        rows = slice(i * BS, (i + 1) * BS)
        tile = jnp.where(home[0] > 0, near[rows, :].astype(f32), far[rows, :].astype(f32))
        tile = jnp.where(used[first + i] > 0, tile, 0.0)
        grad[i] = tile
        tile = tile.astype(bf16)
        rotated.append(split(dot_tn(lefts[i][0], tile) + dot_tn(lefts[i][1], tile)))
    rotated = [product(rotated[i], rights[i], 1, 0) for i in here]
    steps = []
    for i in here:
        new_moment = decay * moment[i] + (1.0 - decay) * rotated[i]
        new_variance = decay * variance[i] + (1.0 - decay) * rotated[i] * rotated[i]
        out_mom[i] = new_moment
        out_var[i] = new_variance
        steps.append(split(new_moment / (jnp.sqrt(new_variance) + adam_eps)))
    returned = [split(product(lefts[i], steps[i], 1, 0)) for i in here]
    returned = [product(returned[i], rights[i], 1, 1) for i in here]
    for i in here:
        out[i] = master[i] - matrix_rate * returned[i]


def owner_call(used, home, near, far, *arrays):
    count = arrays[0].shape[0]
    per = min(8, count)
    block = pl.BlockSpec((per, BS, BS), lambda i, *_: (i, 0, 0))
    return pl.pallas_call(
        functools.partial(owner_kernel, per),
        out_shape=[jax.ShapeDtypeStruct(arrays[0].shape, f32)] * 4,
        grid_spec=pltpu.PrefetchScalarGridSpec(
            num_scalar_prefetch=2,
            grid=(count // per,),
            in_specs=[pl.BlockSpec((per * BS, BS), lambda i, *_: (i, 0))] * 2 + [block] * 5,
            out_specs=[block] * 4,
        ),
        compiler_params=params(),
        cost_estimate=cost(count * 88 * BS**3, count * BS * BS * 38),
    )(used, home, stay(near), stay(far), *arrays)


def reduce_kernel(carrying, last, *refs):
    block, arrived, *refs = refs
    total = block[...].astype(f32) + arrived[...].astype(f32)
    if carrying:
        carried, *refs = refs
        total = total + carried[...].astype(f32)
    if last:
        [out] = refs
    else:
        following, out, later = refs
        later[...] = following[...]
    out[...] = total.astype(bf16)


def reduce_call(j, n, buffer, arrived, carried, payload):
    last = j >= 2
    at = lambda j, x_rel: pl.BlockSpec((payload, BS), lambda i: ((j * 2 + x_rel) * 2 + n, 0))
    whole = fixed((payload, BS))
    operands = [stay(buffer), stay(arrived)] + ([] if carried is None else [stay(carried)])
    specs = [at(j, 0)] + [whole] * (len(operands) - 1)
    if not last:
        operands.append(stay(buffer))
        specs.append(at(j + 2, 1))
    outs = [pltpu.HBM((payload, BS), bf16)] * (1 if last else 2)
    made = pl.pallas_call(
        functools.partial(reduce_kernel, carried is not None, last),
        out_shape=outs,
        grid=(1,),
        in_specs=specs,
        out_specs=[whole] * len(outs),
        compiler_params=params(8),
        cost_estimate=cost(payload * BS * 3, payload * BS * 12),
    )(*operands)
    return (made[0], None) if last else made


class Routes:
    def __init__(self, dp_n):
        pairs = [(d, t) for d in range(dp_n) for t in range(TENSOR)]
        at = lambda d, t: d * TENSOR + t
        home = [(d, t) for d, t in pairs if d % 2 == t]
        away = [(d, t) for d, t in pairs if d % 2 != t]
        self.core_all = [(at(d, t), at(d ^ 1, t)) for d, t in pairs]
        self.core_out = [(at(d, t), at(d ^ 1, t)) for d, t in home]
        self.core_in = [(at(d, t), at(d ^ 1, t)) for d, t in away]
        self.y_all = [(at(d, t), at(d, 1 - t)) for d, t in pairs]
        self.y_out = [(at(d, t), at(d, 1 - t)) for d, t in home]
        self.y_in = [(at(d, t), at(d, 1 - t)) for d, t in away]
        self.x_home = [(at(d, t), at(d ^ 2, t)) for d, t in home]
        self.x_away = [(at(d, t), at(d ^ 2, t)) for d, t in away]
        self.x_all = [(at(d, t), at(d ^ 2, t)) for d, t in pairs]
        self.z_all = [(at(d, t), at((d + 4) % dp_n, t)) for d, t in pairs]
        self.z_home = [(at(d, t), at((d + 4) % dp_n, t)) for d, t in home]


def send(value, route):
    return lax.ppermute(value, AXES, route)


def shards(
    patches,
    cotangent,
    image_size,
    block_slot,
    pinv,
    master_slots,
    left_basis,
    right_basis,
    mom_slots,
    var_slots,
    vec_master,
    vec_mom,
    vec_var,
):
    dp_n = lax.axis_size("dp")
    dp_pos = lax.axis_index("dp")
    y_pos = lax.axis_index("tensor")
    core = dp_pos % 2
    home = core == y_pos
    routes = Routes(dp_n)
    grid3 = dp_n == 16
    x_pos = (dp_pos // 2) % 2
    half_at = (x_pos if grid3 else x_pos * 0).astype(jnp.int32).reshape(1)
    tokens_n = patches.shape[0]
    slots_per = master_slots.shape[1]
    vec_per = vec_master.shape[1]
    slots_n = slots_per * dp_n
    payload = slots_per * BS + VEC_ROWS

    patches = jnp.where(home, patches, send(patches, routes.core_out))
    cotangent = jnp.where(home, cotangent, send(cotangent, routes.core_out))
    size_row = jnp.where(home, image_size, send(image_size, routes.core_out))[0]
    own_slots = block_slot[0]
    slot_other = send(block_slot, routes.y_all)

    lengths = jnp.where(
        size_row == 0, LEN_A, jnp.where(size_row == 1, LEN_B, jnp.where(size_row == 2, LEN_C, 0))
    )
    order = jnp.arange(IMG_DEV)
    ends_at = jnp.sum(jnp.where(order[None, :] <= order[:, None], lengths[None, :], 0), axis=1)
    places = jnp.arange(tokens_n)
    segment = jnp.sum((places[:, None] >= ends_at[None, :]).astype(jnp.int32), axis=1)
    in_image = segment[:, None] == order[None, :]
    select = jnp.stack(
        [jnp.any(in_image & (size_row == s)[None, :], axis=1) for s in range(3)], axis=1
    )
    valid_col = (segment < IMG_DEV).astype(f32)[:, None]
    seg_col = segment[:, None]
    seg_row = segment[None, :]
    blocks_n = tokens_n // ROWS
    starts = jnp.arange(blocks_n) * ROWS
    begun = ends_at[None, :] <= starts[:, None]
    first_tok = jnp.max(jnp.where(begun, ends_at[None, :], 0), axis=1)
    after = ends_at[None, :] > (starts + ROWS - 1)[:, None]
    last_tok = jnp.min(jnp.where(after, ends_at[None, :], tokens_n), axis=1)
    first_blk = (first_tok // ROWS).astype(jnp.int32)
    last_blk = ((last_tok + ROWS - 1) // ROWS).astype(jnp.int32)
    first_key = (first_tok // KEYS).astype(jnp.int32)
    last_key = ((last_tok + KEYS - 1) // KEYS).astype(jnp.int32)

    select_low = select.astype(bf16)
    class_col = jnp.sum(jnp.where(select, jnp.arange(1, 4)[None, :], 0), axis=1, keepdims=True) - 1
    present = jnp.any(select.reshape(blocks_n, ROWS, 3), axis=1).astype(jnp.int32)

    def expand(which, rows):
        return expand_call(which, present, half_at, rows, class_col, pinv)

    vec_low = jnp.pad(vec_master[0].astype(bf16), (0, VEC_ROWS * BS - vec_per))
    own_pack = jnp.concatenate(
        [
            master_slots[0].astype(bf16).reshape(slots_per * BS, BS),
            vec_low.reshape(VEC_ROWS, BS),
        ],
        axis=0,
    )
    flag = home.astype(jnp.int32).reshape(1)
    if grid3:
        z_pos = dp_pos // 4
        pack = own_pack
        chunks, first, second, owner = [], [], [], []
        middle_row = slots_per * BS // 2
        for j in range(4):
            beside_x, beside_y = send(pack, routes.x_all), send(pack, routes.y_all)
            if j < 3:
                further = send(pack, routes.z_all)
            work = [expand(j, patches)] + ([slot_other] if j == 0 else [])
            beside_x, patches, chunk, *work = fence(beside_x, patches, *work)
            chunks.append(chunk)
            if j == 0:
                [slot_other] = work
            corner = jnp.concatenate(
                [send(beside_x[:middle_row], routes.y_all), send(beside_y[middle_row:], routes.x_all)],
                axis=0,
            )
            near_two = send(jnp.where(home, beside_y, pack), routes.core_all)
            far_two = send(jnp.where(home, corner, beside_x), routes.core_all)
            first += [pack, near_two, beside_x, far_two]
            second += [beside_y, near_two, corner, far_two]
            for x_rel in range(2):
                for n in range(2):
                    owner.append(((z_pos - j) % 4) * 4 + (x_pos ^ x_rel) * 2 + (core ^ n))
            if j < 3:
                pack = further
        first = [v[None] for v in first]
        second = [v[None] for v in second]
        owner = jnp.stack(owner).astype(jnp.int32)
    else:
        everything = lax.all_gather(own_pack, AXES, axis=0)
        everything = everything.reshape(dp_n, TENSOR, payload, BS)
        first = [jnp.where(core == 0, everything[:, 0], everything[:, 1])]
        second = []
        owner = jnp.arange(dp_n, dtype=jnp.int32)
        chunks = [expand(c, patches) for c in range(CHUNKS)]
    slot_list = jnp.where(home, block_slot, slot_other)[0]
    named = slot_list[None, :] == jnp.arange(slots_n)[:, None]
    used = jnp.any(named, axis=1)
    drow = jnp.where(used, jnp.sum(jnp.where(named, TARGET_ROW[None, :], 0), axis=1), -1)
    dcol = jnp.sum(jnp.where(named, TARGET_COL[None, :], 0), axis=1)
    weights, vec_rows = gather_tiles(first, second, owner, drow, dcol, flag, slots_per, dp_n)
    vec = vec_rows.reshape(dp_n, VEC_ROWS * BS)[:, :vec_per].astype(f32).reshape(1, dp_n * vec_per)

    embedded = embed_call(half_at, chunks, vec, weights)
    embedded_other = send(embedded, routes.core_all)
    core_flag = core.astype(jnp.int32).reshape(1)

    caches = []
    hidden, own, recv = None, embedded, embedded_other
    for layer in range(LAYERS):
        hidden, normed, queries, keys, values = qkv_call(
            layer, hidden, own, recv, core_flag, vec, weights
        )
        mixed, lse, part = attend_call(
            layer, first_blk, last_blk, queries, keys, values, seg_col, seg_row, vec, weights
        )
        other = send(part, routes.core_all)
        middle, normed2, act, slope, own = mlp_call(layer, hidden, part, other, vec, weights)
        recv = send(own, routes.core_all)
        caches.append((hidden, normed, queries, keys, values, mixed, lse, middle, normed2, act, slope))
        hidden = middle
    out_low = ((hidden + (own.astype(f32) + recv.astype(f32))) * valid_col).astype(bf16)

    owners = jnp.arange(dp_n)
    if grid3:
        place = (
            ((z_pos - 1 - owners // 4) % 4) * 4
            + (x_pos ^ ((owners // 2) % 2)) * 2
            + (core ^ (owners % 2))
        ).astype(jnp.int32)
    else:
        place = owners.astype(jnp.int32)
    slot_owner = slot_list // slots_per
    owner_place = jnp.sum(
        jnp.where(slot_owner[:, None] == owners[None, :], place[None, :], 0), axis=1
    )
    tile_pos = (owner_place * payload + (slot_list % slots_per) * BS).astype(jnp.int32)
    vec_pos = (place * payload + slots_per * BS).astype(jnp.int32)
    total_rows = dp_n * payload
    where_to = jnp.concatenate([half_at, flag if grid3 else flag * 0 + 1])
    offsets = {"base": 0}
    count = BASE_PIX // BS * (HALF // BS)
    for layer in range(LAYERS):
        for name, size in (("qkv", 3 * D * HALF), ("out", D * HALF), ("up", D * HALF_FF), ("down", D * HALF_FF)):
            offsets[name, layer] = count
            count += size // (BS * BS)

    def place_tiles(key, matrix, arrived, buffer):
        tiles = matrix.size // (BS * BS)
        pos = tile_pos[offsets[key] : offsets[key] + tiles]
        rows_n = matrix.shape[0] // 2 if matrix.shape[0] > HALF else HALF
        return scatter_matrix(pos, matrix, arrived, where_to, buffer, total_rows, rows_n)

    def place_base(rel, matrix, arrived, buffer):
        size = BASE_PIX * HALF // (BS * BS) // 2
        low_pos, high_pos = tile_pos[:size], tile_pos[size : 2 * size]
        pos = jnp.where(half_at[0] == rel, low_pos, high_pos)
        return scatter_matrix(pos, matrix, arrived, where_to, buffer, total_rows, D)

    def over(matrix):
        return send(matrix, routes.y_in) if grid3 else None

    def beside(matrix):
        return send(other_half(half_at, matrix), routes.x_away) if grid3 else None

    def summed(matrix, arrived):
        return half_sum(half_at, matrix, arrived) if grid3 else None

    def hold(*arrays):
        kept = [a for a in arrays if a is not None]
        done = iter(fence(*kept))
        return [None if a is None else next(done) for a in arrays]

    top, low = 1, 0
    vec_grads = [None] * LAYERS

    def mlp_step(layer, grad, own, recv):
        middle, normed2, act, slope = caches[layer][7:11]
        made = mlp_back_call(layer, grad, own, recv, valid_col, middle, slope, vec, weights)
        if own is not None:
            return made
        return [made[0]] + list(made)

    def attend_step(layer, grad, part, other, lse):
        hid_in, normed, queries, keys, values, mixed = caches[layer][:6]
        return attend_back_call(
            layer, first_key, last_key, grad, part, other, queries, keys, values, mixed, lse,
            seg_col, seg_row, weights,
        )

    grad, grad_low, du, part, dg2, ds2, db1, db2 = mlp_step(top, cotangent, None, None)
    other = send(part, routes.core_all)
    gd1 = dot_tn(caches[top][9], grad_low).astype(bf16)
    gu1 = dot_tn(caches[top][8], du).astype(bf16)
    lse, gd1, gu1, out_low = fence(caches[top][6], gd1, gu1, out_low)
    ad1 = over(gd1)
    grad, grad_low, dq, dk, dv, dbo = attend_step(top, grad, part, other, lse)
    vec, dbo, ad1, gu1 = hold(vec, dbo, ad1, gu1)
    au1 = over(gu1)
    own, dg1, ds1, dbq, dbv = qkv_back_call(top, dq, dk, dv, caches[top][0], vec, weights)
    recv = send(own, routes.core_all)
    go1 = dot_tn(caches[top][5], grad_low).astype(bf16)
    gq1 = dot_tn(caches[top][1], jnp.concatenate([dq, dk, dv], axis=1)).astype(bf16)
    vec_grads[top] = [dg1, ds1, dbq, dbv, dbo, dg2, ds2, db1, db2]
    grad, grad_low, du, part, dg2, ds2, db1, db2 = mlp_step(low, grad, own, recv)
    other = send(part, routes.core_all)
    db2, au1, go1, gq1 = hold(db2, au1, go1, gq1)
    xq1, ao1 = beside(gq1), over(go1)
    gd0 = dot_tn(caches[low][9], grad_low).astype(bf16)
    gu0 = dot_tn(caches[low][8], du).astype(bf16)
    lse, gd0, gu0, xq1, ao1 = hold(caches[low][6], gd0, gu0, xq1, ao1)
    hq1 = summed(gq1, xq1)
    ad0 = over(gd0)
    xu0 = beside(gu0)
    buffer = place_tiles(("down", top), gd1, ad1, None)
    buffer = place_tiles(("up", top), gu1, au1, buffer)
    grad, grad_low, dq, dk, dv, dbo = attend_step(low, grad, part, other, lse)
    vec, dbo, ad0, xu0, hq1, buffer = hold(vec, dbo, ad0, xu0, hq1, buffer)
    au0 = over(summed(gu0, xu0))
    aq1 = over(hq1)
    own, dg1, ds1, dbq, dbv = qkv_back_call(low, dq, dk, dv, caches[low][0], vec, weights)
    recv = send(own, routes.core_all)
    gq0 = dot_tn(caches[low][1], jnp.concatenate([dq, dk, dv], axis=1)).astype(bf16)
    vec_grads[low] = [dg1, ds1, dbq, dbv, dbo, dg2, ds2, db1, db2]
    xq0 = beside(gq0)
    grad_emb, grad_emb_bias = embed_back_call(core_flag, grad, own, recv)
    middle = CHUNKS // 2

    def base_grad(parts):
        return jnp.concatenate([dot_tn(c, grad_emb).astype(bf16) for c in parts], axis=0)

    gbt = base_grad(chunks[middle:])
    gbt, au0, xq0, aq1 = hold(gbt, au0, xq0, aq1)
    xb = send(gbt, routes.x_away) if grid3 else None
    aq0 = over(summed(gq0, xq0))
    gbm = base_grad(chunks[:middle])
    vec_grad = pack_call([grad_emb_bias] + vec_grads[0] + vec_grads[1], dp_n, vec_per)
    go0 = dot_tn(caches[low][5], grad_low).astype(bf16)
    ao0, av = over(go0), over(vec_grad)
    buffer = place_tiles(("out", top), go1, ao1, buffer)
    buffer = place_tiles(("qkv", top), gq1, aq1, buffer)
    buffer = place_tiles(("down", low), gd0, ad0, buffer)
    buffer = place_tiles(("up", low), gu0, au0, buffer)
    buffer = place_base(1, gbt, None, buffer)
    gbm, xb, aq0, ao0, av, buffer = hold(gbm, xb, aq0, ao0, av, buffer)
    ab = over(half_sum(half_at * 0, gbm, xb)) if grid3 else None
    buffer = place_tiles(("out", low), go0, ao0, buffer)
    buffer = scatter_vec(vec_pos, vec_grad, av, buffer)
    buffer = place_tiles(("qkv", low), gq0, aq0, buffer)
    base_weight = weights["base", 0]
    ab, buffer, base_weight, out_low = hold(ab, buffer, base_weight, out_low)
    weights["base", 0] = base_weight
    buffer = place_base(0, gbm, ab, buffer)

    if grid3:
        token = jnp.zeros((8, BS), f32)
        order = (1, 0)
        resized = resize_call(weights, pinv)
        carried = {n: None for n in order}
        blocks = buffer.reshape(4, 2, 2, payload, BS)
        across = {n: send(blocks[0, 1, n], routes.x_home) for n in order}
        following = {n: blocks[1, 1, n] for n in order}
        rounded = {}
        for j in range(4):
            for n in order:
                extra = None
                if j == 0 and n == order[0]:
                    extra = resized
                token, across[n], carried[n], extra = hold(token, across[n], carried[n], extra)
                if extra is not None:
                    resized = extra
                arrived = across[n]
                if j < 3:
                    across[n] = send(following[n], routes.x_home)
                total, following[n] = reduce_call(j, n, buffer, arrived, carried[n], payload)
                if j < 3:
                    carried[n] = send(total, routes.z_home)
                else:
                    rounded[n] = total
        near_grad, far_grad = rounded[0], send(rounded[1], routes.core_out)
    else:
        held = buffer.reshape(dp_n, 1, payload, BS).astype(f32)
        nothing = jnp.zeros_like(held)
        both = jnp.concatenate(
            [jnp.where(core == 0, held, nothing), jnp.where(core == 0, nothing, held)], axis=1
        )
        used_rows = jnp.repeat(used, BS).reshape(dp_n, 1, slots_per * BS, 1)
        used_rows = jnp.concatenate(
            [used_rows, jnp.ones((dp_n, 1, VEC_ROWS, 1), bool)], axis=2
        )
        both = jnp.where(used_rows, both, 0.0).reshape(dp_n * TENSOR * payload, BS)
        near_grad = lax.psum_scatter(both, AXES, scatter_dimension=0, tiled=True).astype(bf16)
        far_grad = near_grad
        resized = resize_call(weights, pinv)

    output = jnp.where(home, out_low, send(out_low, routes.y_out)).astype(f32)
    grad_pixels = sum(
        dot(grad_emb * select_low[:, s : s + 1], resized[s]) for s in range(3)
    ).astype(bf16)
    pixels_other = send(grad_pixels, routes.core_all)
    pixel_sides = [
        grad_pixels[:, s * HALF : (s + 1) * HALF].astype(f32)
        + pixels_other[:, s * HALF : (s + 1) * HALF].astype(f32)
        for s in range(TENSOR)
    ]
    near = jnp.where(core == 0, pixel_sides[0], pixel_sides[1])
    far = jnp.where(core == 0, pixel_sides[1], pixel_sides[0]).astype(bf16)
    patch_grad = jnp.where(home, near, send(far, routes.y_out).astype(f32))

    my_slots = dp_pos * slots_per + jnp.arange(slots_per)
    mine_used = jnp.any(own_slots[None, :] == my_slots[:, None], axis=1).astype(jnp.int32)
    owned_grad, new_master, new_mom, new_var = owner_call(
        mine_used, flag, near_grad, far_grad, master_slots[0], left_basis[0], right_basis[0], mom_slots[0], var_slots[0]
    )
    vec_rows = jnp.where(home, near_grad[slots_per * BS :], far_grad[slots_per * BS :])
    owned_vec_grad = vec_rows.astype(f32).reshape(VEC_ROWS * BS)[:vec_per]
    new_vec_mom = decay * vec_mom[0] + (1.0 - decay) * owned_vec_grad
    new_vec_var = decay * vec_var[0] + (1.0 - decay) * owned_vec_grad * owned_vec_grad
    new_vec = vec_master[0] - vector_rate * new_vec_mom / (jnp.sqrt(new_vec_var) + adam_eps)
    return (
        output,
        patch_grad,
        owned_grad[None],
        new_master[None],
        new_mom[None],
        new_var[None],
        owned_vec_grad[None],
        new_vec[None],
        new_vec_mom[None],
        new_vec_var[None],
    )


def solution(mesh):
    slots = P("tensor", "dp", None, None)
    vectors = P("tensor", "dp")
    tokens = P("dp", None)
    in_specs = (tokens, tokens, tokens, P("tensor", None), P()) + (slots,) * 5 + (vectors,) * 3
    out_specs = (tokens, P("dp", "tensor")) + (slots,) * 4 + (vectors,) * 4
    return jax.shard_map(shards, mesh=mesh, in_specs=in_specs, out_specs=out_specs, check_vma=False)
```

```python
import functools

import jax
import jax.numpy as jnp
import numpy as np
from jax import lax
from jax.experimental import pallas as pl
from jax.experimental.pallas import tpu as pltpu
from jax.sharding import PartitionSpec as P

D = 768
HEAD_DIM = 64
FF = 3072
BASE_PIX = 3072
LAYERS = 2
LEN_A = 196
LEN_B = 225
LEN_C = 576
IMG_DEV = 5
BS = 128
TENSOR = 2
HALF = D // TENSOR
HALF_FF = FF // TENSOR
HEADS = HALF // HEAD_DIM
ROWS = 256
KEYS = 512
VEC_ROWS = 16
CHUNKS = 4

AXES = ("dp", "tensor")
precise = lax.Precision.HIGHEST
masked_score = -1e30
norm_eps = 1e-06
adam_eps = 1e-08
decay = 0.5
matrix_rate = 0.05
vector_rate = 0.3
f32 = jnp.float32
bf16 = jnp.bfloat16
MIB = 1024 * 1024

WEIGHTS = [("base", 0, BASE_PIX)]
for layer in range(LAYERS):
    WEIGHTS += [("qkv", layer, 3 * D), ("out", layer, D), ("up", layer, FF), ("down", layer, FF)]
STARTS = {}
PANEL_ROWS = 0
for name, layer, size in WEIGHTS:
    STARTS[name, layer] = PANEL_ROWS
    PANEL_ROWS += size


def tile_targets():
    rows, cols = [], []

    def add(start, rows_n, cols_n):
        for i in range(rows_n // BS):
            for j in range(cols_n // BS):
                panel, inner = divmod(j * BS, HALF)
                rows.append(start + panel * rows_n + i * BS)
                cols.append(inner)

    add(STARTS["base", 0], BASE_PIX, HALF)
    for layer in range(LAYERS):
        add(STARTS["qkv", layer], D, 3 * HALF)
        add(STARTS["out", layer], HALF, D)
        add(STARTS["up", layer], D, HALF_FF)
        add(STARTS["down", layer], HALF_FF, D)
    return np.array(rows, np.int32), np.array(cols, np.int32)


TARGET_ROW, TARGET_COL = tile_targets()
LAYER_VECS = (D, D, HALF, HALF, D, D, D, HALF_FF, D)
VEC_NAMES = ("g1", "s1", "bq", "bv", "bo", "g2", "s2", "b1", "b2")


def vec_offsets():
    offset = HALF
    found = []
    for layer in range(LAYERS):
        here = {}
        for name, length in zip(VEC_NAMES, LAYER_VECS):
            here[name] = (offset, length)
            offset += length
        found.append(here)
    return found


VEC_AT = vec_offsets()


def params(limit=24):
    return pltpu.CompilerParams(
        dimension_semantics=("arbitrary",), vmem_limit_bytes=limit * MIB
    )


def cost(flops, nbytes, trans=0):
    return pl.CostEstimate(flops=flops, bytes_accessed=nbytes, transcendentals=trans)


def rows_spec(width):
    return pl.BlockSpec((ROWS, width), lambda i, *_: (i, 0))


def fixed(shape, at=0):
    return pl.BlockSpec(shape, lambda i, *_: (at,) + (0,) * (len(shape) - 1))


def vec_piece(vec_ref, layer, name):
    start, length = VEC_AT[layer][name]
    return vec_ref[:, start : start + length]


def dot(left, right):
    return jnp.dot(left, right, preferred_element_type=f32)


def dot_nt(left, right, precision=None):
    return lax.dot_general(
        left, right, (((1,), (1,)), ((), ())), precision=precision, preferred_element_type=f32
    )


def dot_tn(left, right):
    return lax.dot_general(left, right, (((0,), (0,)), ((), ())), preferred_element_type=f32)


def joined(ref, start, rows_n, panels):
    return jnp.concatenate(
        [ref[start + p * rows_n : start + (p + 1) * rows_n, :] for p in range(panels)], axis=1
    )


def norm_stats(values):
    mean_val = jnp.mean(values, axis=-1, keepdims=True)
    centered = values - mean_val
    inv_std = lax.rsqrt(jnp.mean(centered * centered, axis=-1, keepdims=True) + norm_eps)
    return centered * inv_std, inv_std


def norm_back(values, gain, grad):
    unit, inv_std = norm_stats(values)
    scaled = grad * gain
    mean_s = jnp.mean(scaled, axis=-1, keepdims=True)
    mean_u = jnp.mean(scaled * unit, axis=-1, keepdims=True)
    back = inv_std * (scaled - mean_s - unit * mean_u)
    return (
        back,
        jnp.sum(grad * unit, axis=0, keepdims=True),
        jnp.sum(grad, axis=0, keepdims=True),
    )


def accumulate(ref, value):
    first = pl.program_id(0) == 0

    @pl.when(first)
    def _():
        ref[...] = value

    @pl.when(jnp.logical_not(first))
    def _():
        ref[...] += value


def stay(value):
    return pltpu.with_memory_space_constraint(value, pltpu.HBM)


def fence(*arrays):
    def nothing(*refs):
        pass

    anywhere = pl.BlockSpec(memory_space=pl.ANY)
    return pl.pallas_call(
        nothing,
        out_shape=[jax.ShapeDtypeStruct(a.shape, a.dtype) for a in arrays],
        in_specs=[anywhere] * len(arrays),
        out_specs=[anywhere] * len(arrays),
        input_output_aliases={i: i for i in range(len(arrays))},
        compiler_params=pltpu.CompilerParams(vmem_limit_bytes=MIB),
    )(*[stay(a) if a.size > 32 * 1024 else a for a in arrays])


def gather_kernel(slots, count_a, count_b, owner, drow, dcol, flag, *refs):
    first = refs[:count_a]
    second = refs[count_a : count_a + count_b]
    *panels, vectors, held, sem, vec_sem = refs[count_a + count_b :]

    def copy_all(sources):
        at = 0
        for src in sources:
            for n in range(src.shape[0]):
                who = owner[at]
                at += 1

                def body(i, carried, src=src, n=n, who=who):
                    slot = who * slots + i
                    row = drow[slot]

                    @pl.when(row >= 0)
                    def _():
                        start = pl.multiple_of(i * BS, BS)
                        pltpu.make_async_copy(
                            src.at[n, pl.ds(start, BS), :],
                            held.at[
                                pl.ds(pl.multiple_of(row, BS), BS),
                                pl.ds(pl.multiple_of(dcol[slot], BS), BS),
                            ],
                            sem,
                        ).start()

                    return carried

                lax.fori_loop(0, slots, body, 0)
                pltpu.make_async_copy(
                    src.at[n, pl.ds(slots * BS, VEC_ROWS), :], vectors.at[who], vec_sem
                ).start()

    if count_b:

        @pl.when(flag[0] == 1)
        def _():
            copy_all(first)

        @pl.when(flag[0] == 0)
        def _():
            copy_all(second)
    else:
        copy_all(first)
    pltpu.make_async_copy(held, held, sem).wait()
    at = 0
    for panel in panels:
        size = panel.shape[0]
        pltpu.make_async_copy(held.at[pl.ds(at, size), :], panel, sem).start()
        at += size
    pltpu.make_async_copy(vectors, vectors, vec_sem).wait()
    pltpu.make_async_copy(held, held, sem).wait()


def gather_tiles(first, second, owner, drow, dcol, flag, slots, owners):
    anywhere = pl.BlockSpec(memory_space=pl.ANY)
    *panels, vectors = pl.pallas_call(
        functools.partial(gather_kernel, slots, len(first), len(second)),
        out_shape=[pltpu.HBM((size, HALF), bf16) for unused, unused2, size in WEIGHTS]
        + [jax.ShapeDtypeStruct((owners, VEC_ROWS, BS), bf16)],
        grid_spec=pltpu.PrefetchScalarGridSpec(
            num_scalar_prefetch=4,
            grid=(1,),
            in_specs=[anywhere] * (len(first) + len(second)),
            out_specs=[anywhere] * len(WEIGHTS) + [fixed((owners, VEC_ROWS, BS))],
            scratch_shapes=[
                pltpu.VMEM((PANEL_ROWS, HALF), bf16),
                pltpu.SemaphoreType.DMA,
                pltpu.SemaphoreType.DMA,
            ],
        ),
        compiler_params=params(),
        cost_estimate=cost(0, 4 * PANEL_ROWS * HALF),
    )(owner, drow, dcol, flag, *[stay(v) for v in first], *[stay(v) for v in second])
    return {(name, layer): p for (name, layer, unused), p in zip(WEIGHTS, panels)}, vectors


def scatter_kernel(rows_n, cols_n, steps, paired, parts, pos, part, own, *refs):
    @pl.when(part[1] > 0)
    def _():
        scatter_body(rows_n, cols_n, steps, paired, parts, pos, part, own, *refs)


def scatter_body(rows_n, cols_n, steps, paired, parts, pos, part, own, *refs):
    if paired:
        recv, *refs = refs
        span = pl.num_programs(0) // parts
        here = jnp.logical_or(parts == 1, pl.program_id(0) // span == part[0])
    target, buf, sems = refs[-3:]
    step = pl.program_id(0)
    slot = lax.rem(step, 2)
    per = rows_n // BS * (cols_n // BS)

    def wait(at):
        pltpu.make_async_copy(buf.at[at], buf.at[at], sems.at[at]).wait()

    @pl.when(step >= 2)
    def _():
        wait(slot)

    for i in range(rows_n // BS):
        for j in range(cols_n // BS):
            area = (slice(i * BS, (i + 1) * BS), slice(j * BS, (j + 1) * BS))
            value = own[area]
            if paired:
                more = jnp.where(here, recv[area].astype(f32), 0.0)
                value = (value.astype(f32) + more).astype(bf16)
            buf[slot, i * (cols_n // BS) + j] = value
    for n in range(per):
        pltpu.make_async_copy(
            buf.at[slot, n],
            target.at[pl.ds(pl.multiple_of(pos[step * per + n], 16), BS), :],
            sems.at[slot],
        ).start()

    @pl.when(step == pl.num_programs(0) - 1)
    def _():
        if steps > 1:
            wait(1 - slot)
        wait(slot)


def scatter_matrix(pos, own, recv, part, target, total_rows, rows_n):
    cols_n = own.shape[1]
    steps = own.shape[0] // rows_n
    anywhere = pl.BlockSpec(memory_space=pl.ANY)
    block = pl.BlockSpec((rows_n, cols_n), lambda i, *_: (i, 0))
    paired = recv is not None
    parts = own.shape[0] // recv.shape[0] if paired else 1
    span = steps // parts
    arrived = pl.BlockSpec(
        (rows_n, cols_n), lambda i, pos, part: (jnp.clip(i - part[0] * span, 0, span - 1), 0)
    )
    operands = [stay(own)] + ([stay(recv)] if paired else []) + ([] if target is None else [stay(target)])
    specs = [block] + ([block if parts == 1 else arrived] if paired else [])
    specs += [] if target is None else [anywhere]
    return pl.pallas_call(
        functools.partial(scatter_kernel, rows_n, cols_n, steps, paired, parts),
        out_shape=pltpu.HBM((total_rows, BS), bf16),
        grid_spec=pltpu.PrefetchScalarGridSpec(
            num_scalar_prefetch=2,
            grid=(steps,),
            in_specs=specs,
            out_specs=anywhere,
            scratch_shapes=[
                pltpu.VMEM((2, rows_n // BS * (cols_n // BS), BS, BS), bf16),
                pltpu.SemaphoreType.DMA((2,)),
            ],
        ),
        input_output_aliases={} if target is None else {len(operands) + 1: 0},
        compiler_params=params(12),
        cost_estimate=cost(own.size, own.size * 6),
    )(pos, part, *operands)


def half_sum_kernel(part, own, arrived, out):
    out[...] = (own[...].astype(f32) + arrived[...].astype(f32)).astype(bf16)


def half_sum(part, own, arrived):
    block = arrived.shape
    return pl.pallas_call(
        half_sum_kernel,
        out_shape=pltpu.HBM(block, bf16),
        grid_spec=pltpu.PrefetchScalarGridSpec(
            num_scalar_prefetch=1,
            grid=(1,),
            in_specs=[pl.BlockSpec(block, lambda i, part: (part[0], 0)), fixed(block)],
            out_specs=fixed(block),
        ),
        compiler_params=params(8),
        cost_estimate=cost(arrived.size, arrived.size * 6),
    )(part, stay(own), stay(arrived))


def half_copy_kernel(part, own, out):
    out[...] = own[...]


def other_half(part, own):
    block = (own.shape[0] // 2, own.shape[1])
    return pl.pallas_call(
        half_copy_kernel,
        out_shape=pltpu.HBM(block, bf16),
        grid_spec=pltpu.PrefetchScalarGridSpec(
            num_scalar_prefetch=1,
            grid=(1,),
            in_specs=[pl.BlockSpec(block, lambda i, part: (1 - part[0], 0))],
            out_specs=fixed(block),
        ),
        compiler_params=params(8),
        cost_estimate=cost(0, own.size * 2),
    )(part, stay(own))


def scatter_vec_kernel(paired, pos, own, *refs):
    if paired:
        recv, *refs = refs
    target, buf, sem = refs[-3:]
    value = own[...]
    if paired:
        value = (value.astype(f32) + recv[...].astype(f32)).astype(bf16)
    buf[...] = value

    def body(n, carried):
        pltpu.make_async_copy(
            buf.at[n], target.at[pl.ds(pl.multiple_of(pos[n], 16), VEC_ROWS), :], sem
        ).start()
        return carried

    lax.fori_loop(0, own.shape[0], body, 0)
    pltpu.make_async_copy(buf, buf, sem).wait()


def scatter_vec(pos, own, recv, target):
    anywhere = pl.BlockSpec(memory_space=pl.ANY)
    block = fixed(own.shape)
    paired = recv is not None
    operands = [own] + ([recv] if paired else []) + [stay(target)]
    return pl.pallas_call(
        functools.partial(scatter_vec_kernel, paired),
        out_shape=pltpu.HBM(target.shape, bf16),
        grid_spec=pltpu.PrefetchScalarGridSpec(
            num_scalar_prefetch=1,
            grid=(1,),
            in_specs=[block] * (len(operands) - 1) + [anywhere],
            out_specs=anywhere,
            scratch_shapes=[pltpu.VMEM(own.shape, bf16), pltpu.SemaphoreType.DMA],
        ),
        input_output_aliases={len(operands): 0},
        compiler_params=params(4),
    )(pos, *operands)


def expand_kernel(present, half, patch_ref, class_ref, pinv_ref, out, total):
    for block in range(patch_ref.shape[0] // ROWS):
        rows = slice(block * ROWS, (block + 1) * ROWS)
        total[...] = jnp.zeros_like(total)
        for which in range(3):

            @pl.when(present[block, which] > 0)
            def _(which=which, rows=rows):
                chosen = jnp.where(class_ref[rows, :] == which, patch_ref[rows, :].astype(f32), 0.0)
                total[...] += dot_nt(chosen.astype(bf16), pinv_ref[which])

        out[rows, :] = total[...].astype(bf16)


def expand_call(which, present, half, patches, class_col, pinv):
    tokens = patches.shape[0]
    size = BASE_PIX // CHUNKS
    step = size
    return pl.pallas_call(
        expand_kernel,
        out_shape=jax.ShapeDtypeStruct((tokens, size), bf16),
        grid_spec=pltpu.PrefetchScalarGridSpec(
            num_scalar_prefetch=2,
            grid=(1,),
            in_specs=[
                fixed(patches.shape),
                fixed(class_col.shape),
                pl.BlockSpec(
                    (3, step, pinv.shape[2]),
                    lambda i, present, half: (0, (which + half[0] * (CHUNKS // 2)) % CHUNKS, 0),
                ),
            ],
            out_specs=pl.BlockSpec((tokens, step), lambda i, *_: (0, i)),
            scratch_shapes=[pltpu.VMEM((ROWS, step), f32)],
        ),
        compiler_params=params(),
        cost_estimate=cost(3 * tokens * size * D, tokens * size * 4 + size * D * 6),
    )(present, half, patches, class_col, stay(pinv))


def resize_kernel(base, pinv_ref, out, turned):
    @pl.when(pl.program_id(0) == 0)
    def _():
        turned[...] = base[...].T

    out[0] = dot(turned[...], pinv_ref[0]).astype(bf16)


def resize_call(weights, pinv):
    return pl.pallas_call(
        resize_kernel,
        out_shape=jax.ShapeDtypeStruct((3, HALF, pinv.shape[2]), bf16),
        grid=(3,),
        in_specs=[
            fixed((BASE_PIX, HALF)),
            pl.BlockSpec((1, BASE_PIX, pinv.shape[2]), lambda i: (i, 0, 0)),
        ],
        out_specs=pl.BlockSpec((1, HALF, pinv.shape[2]), lambda i: (i, 0, 0)),
        scratch_shapes=[pltpu.VMEM((HALF, BASE_PIX), bf16)],
        compiler_params=params(),
        cost_estimate=cost(6 * D * BASE_PIX * HALF, 6 * D * BASE_PIX),
    )(stay(weights["base", 0]), stay(pinv))


def embed_back_kernel(core, base, own, recv, out, bias):
    low = (base[...] + (own[...].astype(f32) + recv[...].astype(f32))).astype(bf16)
    out[...] = low
    accumulate(bias, jnp.sum(low.astype(f32), axis=0, keepdims=True))


def embed_back_call(core, base, own, recv):
    tokens = base.shape[0]
    half = pl.BlockSpec((ROWS, HALF), lambda i, core: (i, core[0]))
    return pl.pallas_call(
        embed_back_kernel,
        out_shape=[
            jax.ShapeDtypeStruct((tokens, HALF), bf16),
            jax.ShapeDtypeStruct((1, HALF), f32),
        ],
        grid_spec=pltpu.PrefetchScalarGridSpec(
            num_scalar_prefetch=1,
            grid=(tokens // ROWS,),
            in_specs=[half] * 3,
            out_specs=[rows_spec(HALF), fixed((1, HALF))],
        ),
        compiler_params=params(8),
        cost_estimate=cost(tokens * D, tokens * D * 5),
    )(core, base, own, recv)


def pack_kernel(vec_per, *refs):
    *pieces, out = refs
    out[...] = jnp.zeros_like(out)
    at = 0
    for piece in pieces:
        for k in range(piece.shape[1] // BS):
            owner, row = divmod(at, vec_per // BS)
            out[owner, row : row + 1, :] = piece[:, k * BS : (k + 1) * BS]
            at += 1


def pack_call(pieces, owners, vec_per):
    if vec_per % BS:
        joined = jnp.concatenate(pieces, axis=1)[0]
        joined = jnp.pad(joined, (0, owners * vec_per - joined.shape[0])).reshape(owners, vec_per)
        joined = jnp.pad(joined, ((0, 0), (0, VEC_ROWS * BS - vec_per)))
        return joined.astype(bf16).reshape(owners, VEC_ROWS, BS)
    return pl.pallas_call(
        functools.partial(pack_kernel, vec_per),
        out_shape=jax.ShapeDtypeStruct((owners, VEC_ROWS, BS), f32),
        grid=(1,),
        in_specs=[fixed(p.shape) for p in pieces],
        out_specs=fixed((owners, VEC_ROWS, BS)),
        compiler_params=params(4),
        cost_estimate=cost(0, owners * vec_per * 8),
    )(*pieces).astype(bf16)


def embed_kernel(half, *refs):
    *parts, vec, weight, out = refs
    size = BASE_PIX // CHUNKS
    total = vec[:, :HALF]
    for c in range(CHUNKS):
        at = lax.rem(c + half[0] * (CHUNKS // 2), CHUNKS)
        rows = pl.ds(pl.multiple_of(at * size, size), size)
        total = total + dot(parts[c][...], weight[rows, :])
    out[...] = total.astype(bf16)


def embed_call(half, chunks, vec, weights):
    tokens = chunks[0].shape[0]
    return pl.pallas_call(
        embed_kernel,
        out_shape=jax.ShapeDtypeStruct((tokens, HALF), bf16),
        grid_spec=pltpu.PrefetchScalarGridSpec(
            num_scalar_prefetch=1,
            grid=(tokens // ROWS,),
            in_specs=[rows_spec(BASE_PIX // CHUNKS)] * CHUNKS
            + [fixed(vec.shape), fixed((BASE_PIX, HALF))],
            out_specs=rows_spec(HALF),
        ),
        compiler_params=params(),
        cost_estimate=cost(2 * tokens * BASE_PIX * HALF, tokens * BASE_PIX * 3),
    )(half, *[stay(c) for c in chunks], vec, stay(weights["base", 0]))


def qkv_kernel(layer, first, core, *refs):
    if first:
        own, recv, vec, weight, hid, normed, q_ref, k_ref, v_ref = refs
        mine, theirs = own[...].astype(f32), recv[...].astype(f32)
        low = core[0] == 0
        values = jnp.concatenate(
            [jnp.where(low, mine, theirs), jnp.where(low, theirs, mine)], axis=1
        )
    else:
        base, own, recv, vec, weight, hid, normed, q_ref, k_ref, v_ref = refs
        values = base[...] + (own[...].astype(f32) + recv[...].astype(f32))
    hid[...] = values
    unit, unused = norm_stats(values)
    low = (unit * vec_piece(vec, layer, "g1") + vec_piece(vec, layer, "s1")).astype(bf16)
    normed[...] = low
    made = dot(low, joined(weight, 0, D, 3))
    q_ref[...] = (made[:, :HALF] + vec_piece(vec, layer, "bq")).astype(bf16)
    k_ref[...] = made[:, HALF : 2 * HALF].astype(bf16)
    v_ref[...] = (made[:, 2 * HALF :] + vec_piece(vec, layer, "bv")).astype(bf16)


def qkv_call(layer, base, own, recv, core, vec, weights):
    tokens = own.shape[0]
    shape = lambda width, kind: jax.ShapeDtypeStruct((tokens, width), kind)
    outs = [shape(D, f32), pltpu.HBM((tokens, D), bf16)] + [shape(HALF, bf16)] * 3
    operands = ([] if base is None else [base]) + [own, recv]
    return pl.pallas_call(
        functools.partial(qkv_kernel, layer, base is None),
        out_shape=outs,
        grid_spec=pltpu.PrefetchScalarGridSpec(
            num_scalar_prefetch=1,
            grid=(tokens // ROWS,),
            in_specs=[rows_spec(o.shape[1]) for o in operands]
            + [fixed(vec.shape), fixed((3 * D, HALF))],
            out_specs=[rows_spec(o.shape[1]) for o in outs],
        ),
        compiler_params=params(),
        cost_estimate=cost(2 * tokens * D * 3 * HALF, tokens * D * 14),
    )(core, *operands, vec, weights["qkv", layer])


def head_masks():
    lane = lax.broadcasted_iota(jnp.int32, (1, 2 * HEAD_DIM), 1)
    low = (lane < HEAD_DIM).astype(f32).astype(bf16)
    high = (lane >= HEAD_DIM).astype(f32).astype(bf16)
    return low, high


def attend_kernel(
    layer, low_ref, high_ref, q_ref, k_ref, v_ref, seg_q, seg_k, vec, w_out, o_ref, lse_ref, part,
    scores_ref, top_ref, acc_ref,
):
    step = pl.program_id(0)
    first, last = low_ref[step], high_ref[step]
    masks = head_masks()
    scale = jnp.asarray(HEAD_DIM ** (-0.5), bf16)
    lane = lax.broadcasted_iota(jnp.int32, (1, BS), 1)
    sums = [(lane == HEAD_DIM).astype(f32).astype(bf16), (lane == 0).astype(f32).astype(bf16)]
    top_ref[...] = jnp.full(top_ref.shape, masked_score, f32)
    acc_ref[...] = jnp.zeros_like(acc_ref)
    seg_col = seg_q[...]

    def score_block(block, carried):
        rows = pl.ds(pl.multiple_of(block * ROWS, ROWS), ROWS)
        same = seg_col == seg_k[:, rows]
        for pair in range(HEADS // 2):
            cols = slice(pair * BS, (pair + 1) * BS)
            q_two = q_ref[:, cols] * scale
            k_two = k_ref[rows, cols]
            for side in range(2):
                head = 2 * pair + side
                scores = jnp.where(same, dot_nt(q_two * masks[side], k_two), masked_score)
                scores_ref[head, block] = scores
                top = top_ref[head]
                for piece in range(ROWS // BS):
                    top = jnp.maximum(top, scores[:, piece * BS : (piece + 1) * BS])
                top_ref[head] = top
        return carried

    lax.fori_loop(first, last, score_block, 0)
    tops = [jnp.max(top_ref[head], axis=1, keepdims=True) for head in range(HEADS)]

    def mix_block(block, carried):
        rows = pl.ds(pl.multiple_of(block * ROWS, ROWS), ROWS)
        for pair in range(HEADS // 2):
            v_two = v_ref[rows, pair * BS : (pair + 1) * BS]
            for side in range(2):
                head = 2 * pair + side
                expo = jnp.exp(scores_ref[head, block] - tops[head]).astype(bf16)
                acc_ref[head] += dot(expo, v_two * masks[side] + sums[side])
        return carried

    lax.fori_loop(first, last, mix_block, 0)
    totals = jnp.zeros((ROWS, BS), f32)
    for pair in range(HEADS // 2):
        sides = []
        for side in range(2):
            head = 2 * pair + side
            mixed = acc_ref[head]
            at = HEAD_DIM * (1 - side)
            total = mixed[:, at : at + 1]
            totals = jnp.where(lane == head, tops[head] + jnp.log(total), totals)
            sides.append(mixed * (1.0 / total))
        o_ref[:, pair * BS : (pair + 1) * BS] = jnp.where(lane < HEAD_DIM, *sides).astype(bf16)
    lse_ref[...] = totals.T[0:8, :]
    low = o_ref[...]
    bias = vec_piece(vec, layer, "bo")
    part[...] = (dot(low, joined(w_out, 0, HALF, TENSOR)) + bias).astype(bf16)


def attend_call(layer, first, last, queries, keys, values, seg_col, seg_row, vec, weights):
    tokens = queries.shape[0]
    return pl.pallas_call(
        functools.partial(attend_kernel, layer),
        out_shape=[
            jax.ShapeDtypeStruct((tokens, HALF), bf16),
            jax.ShapeDtypeStruct((8, tokens), f32),
            jax.ShapeDtypeStruct((tokens, D), bf16),
        ],
        grid_spec=pltpu.PrefetchScalarGridSpec(
            num_scalar_prefetch=2,
            grid=(tokens // ROWS,),
            in_specs=[
                rows_spec(HALF),
                fixed(keys.shape),
                fixed(values.shape),
                rows_spec(1),
                fixed(seg_row.shape),
                fixed(vec.shape),
                fixed((D, HALF)),
            ],
            out_specs=[
                rows_spec(HALF),
                pl.BlockSpec((8, ROWS), lambda i, *_: (0, i)),
                rows_spec(D),
            ],
            scratch_shapes=[
                pltpu.VMEM((HEADS, tokens // ROWS, ROWS, ROWS), f32),
                pltpu.VMEM((HEADS, ROWS, BS), f32),
                pltpu.VMEM((HEADS, ROWS, BS), f32),
            ],
        ),
        compiler_params=params(),
        cost_estimate=cost(8 * HEADS * tokens * tokens * BS, tokens * D * 8, HEADS * tokens * tokens),
    )(first, last, queries, keys, values, seg_col, seg_row, vec, weights["out", layer])


def gelu_parts(values):
    cdf = 0.5 * (1.0 + lax.erf(values * 0.7071067811865476))
    pdf = 0.3989422804014327 * jnp.exp(-0.5 * values * values)
    return values * cdf, cdf + values * pdf


def mlp_kernel(layer, base, own, recv, vec, w_up, w_down, hid, normed, act, slope, part):
    values = base[...] + (own[...].astype(f32) + recv[...].astype(f32))
    hid[...] = values
    unit, unused = norm_stats(values)
    low = (unit * vec_piece(vec, layer, "g2") + vec_piece(vec, layer, "s2")).astype(bf16)
    normed[...] = low
    bias_up = vec_piece(vec, layer, "b1")
    for pair in range(HALF_FF // D):
        area = slice(pair * D, (pair + 1) * D)
        up = dot(low, joined(w_up, pair * 2 * D, D, 2)) + bias_up[:, area]
        gelu, grad = gelu_parts(up)
        act[:, area] = gelu.astype(bf16)
        slope[:, area] = grad.astype(bf16)
    bias_down = vec_piece(vec, layer, "b2")
    part[...] = (dot(act[...], joined(w_down, 0, HALF_FF, TENSOR)) + bias_down).astype(bf16)


def mlp_call(layer, base, own, recv, vec, weights):
    tokens = base.shape[0]
    shape = lambda width, kind: jax.ShapeDtypeStruct((tokens, width), kind)
    kept = lambda width: pltpu.HBM((tokens, width), bf16)
    outs = [shape(D, f32), kept(D), kept(HALF_FF), kept(HALF_FF), shape(D, bf16)]
    return pl.pallas_call(
        functools.partial(mlp_kernel, layer),
        out_shape=outs,
        grid=(tokens // ROWS,),
        in_specs=[rows_spec(D)] * 3
        + [
            fixed(vec.shape),
            fixed((2 * HALF_FF, HALF)),
            fixed((2 * HALF_FF, HALF)),
        ],
        out_specs=[rows_spec(o.shape[1]) for o in outs],
        compiler_params=params(),
        cost_estimate=cost(4 * tokens * D * HALF_FF, tokens * D * 24, 2 * tokens * HALF_FF),
    )(base, own, recv, vec, weights["up", layer], weights["down", layer])


def mlp_back_kernel(layer, summed, *refs):
    if summed:
        base, own, recv, *refs = refs
        (hid, slope, vec, w_up, w_down, grad_full, grad_low, du_ref, back, dgain, dshift, db1, db2) = refs
        values = base[...].astype(f32) + (own[...].astype(f32) + recv[...].astype(f32))
        grad_full[...] = values
        low = values.astype(bf16)
    else:
        base, valid, *refs = refs
        (hid, slope, vec, w_up, w_down, grad_low, du_ref, back, dgain, dshift, db1, db2) = refs
        low = (base[...].astype(f32) * valid[...]).astype(bf16)
    grad_low[...] = low
    accumulate(db2, jnp.sum(low.astype(f32), axis=0, keepdims=True))
    for part in range(HALF_FF // D):
        area = slice(part * D, (part + 1) * D)
        rows = jnp.concatenate(
            [w_down[p * HALF_FF + part * D : p * HALF_FF + (part + 1) * D, :] for p in range(TENSOR)],
            axis=1,
        )
        du_ref[:, area] = (dot_nt(low, rows) * slope[:, area].astype(f32)).astype(bf16)
    grad_normed = dot_nt(du_ref[...], joined(w_up, 0, D, HALF_FF // HALF))
    accumulate(db1, jnp.sum(du_ref[...].astype(f32), axis=0, keepdims=True))
    part_back, gain_grad, shift_grad = norm_back(hid[...], vec_piece(vec, layer, "g2"), grad_normed)
    back[...] = part_back.astype(bf16)
    accumulate(dgain, gain_grad)
    accumulate(dshift, shift_grad)


def mlp_back_call(layer, base, own, recv, valid, hid, slope, vec, weights):
    tokens = base.shape[0]
    summed = own is not None
    shape = lambda width, kind: jax.ShapeDtypeStruct((tokens, width), kind)
    line = lambda width: jax.ShapeDtypeStruct((1, width), f32)
    outs = ([shape(D, f32)] if summed else []) + [shape(D, bf16), shape(HALF_FF, bf16), shape(D, bf16)]
    lines = [line(D), line(D), line(HALF_FF), line(D)]
    extra = [own, recv] if summed else [valid]
    return pl.pallas_call(
        functools.partial(mlp_back_kernel, layer, summed),
        out_shape=outs + lines,
        grid=(tokens // ROWS,),
        in_specs=[rows_spec(D)]
        + [rows_spec(e.shape[1]) for e in extra]
        + [
            rows_spec(D),
            rows_spec(HALF_FF),
            fixed(vec.shape),
            fixed((2 * HALF_FF, HALF)),
            fixed((2 * HALF_FF, HALF)),
        ],
        out_specs=[rows_spec(o.shape[1]) for o in outs] + [fixed(o.shape) for o in lines],
        compiler_params=params(),
        cost_estimate=cost(4 * tokens * D * HALF_FF, tokens * D * 24),
    )(base, *extra, stay(hid), stay(slope), vec, weights["up", layer], weights["down", layer])


def attend_back_kernel(
    low_ref, high_ref, base, own, recv, q_ref, k_ref, v_ref, o_ref, lse_ref, seg_k, seg_q, w_out,
    full_ref, grad_low, dq_ref, dk_ref, dv_ref, dbo, dk_acc, dv_acc, dq_acc, do_ref,
):
    step = pl.program_id(0)

    @pl.when(step == 0)
    def _():
        dk_acc[...] = jnp.zeros_like(dk_acc)
        dv_acc[...] = jnp.zeros_like(dv_acc)

    values = base[...].astype(f32) + (own[...].astype(f32) + recv[...].astype(f32))
    full_ref[...] = values
    low = values.astype(bf16)
    grad_low[...] = low
    accumulate(dbo, jnp.sum(low.astype(f32), axis=0, keepdims=True))
    do_ref[...] = dot_nt(low, joined(w_out, 0, HALF, TENSOR)).astype(bf16)
    product = do_ref[...].astype(f32) * o_ref[...].astype(f32)
    head = lax.broadcasted_iota(jnp.int32, (8, HALF), 0)
    lane = lax.broadcasted_iota(jnp.int32, (8, HALF), 1)
    pick = ((lane >= head * HEAD_DIM) & (lane < (head + 1) * HEAD_DIM)).astype(f32)
    high, rest = split(product)
    pick = pick.astype(bf16)
    inner = dot_nt(pick, high) + dot_nt(pick, rest)
    dq_acc[...] = jnp.zeros_like(dq_acc)
    masks = head_masks()
    scale = jnp.asarray(HEAD_DIM ** (-0.5), bf16)
    seg_row = seg_q[...]

    def one_block(block, carried):
        rows = pl.ds(pl.multiple_of(block * KEYS, KEYS), KEYS)
        same = seg_k[rows, :] == seg_row
        for pair in range(HEADS // 2):
            cols = slice(pair * BS, (pair + 1) * BS)
            q_two = q_ref[:, cols] * scale
            do_two = do_ref[:, cols]
            k_two = k_ref[rows, cols]
            v_two = v_ref[rows, cols]
            dv_two = dk_two = dq_two = None
            for side in range(2):
                at = 2 * pair + side
                q_one = q_two * masks[side]
                do_one = do_two * masks[side]
                scores = dot_nt(k_two, q_one)
                prob = jnp.where(same, jnp.exp(scores - lse_ref[at : at + 1, :]), 0.0)
                grad_prob = dot_nt(v_two, do_one)
                grad_scores = (prob * (grad_prob - inner[at : at + 1, :])).astype(bf16)
                dv_one = dot(prob.astype(bf16), do_one)
                dk_one = dot(grad_scores, q_one)
                dq_one = dot_tn(grad_scores, k_two * masks[side])
                dq_two = dq_one if dq_two is None else dq_two + dq_one
                dv_two = dv_one if dv_two is None else dv_two + dv_one
                dk_two = dk_one if dk_two is None else dk_two + dk_one
            dv_acc[rows, cols] += dv_two
            dk_acc[rows, cols] += dk_two
            dq_acc[:, cols] += dq_two
        return carried

    lax.fori_loop(low_ref[step], high_ref[step], one_block, 0)
    dq_ref[...] = (dq_acc[...] * HEAD_DIM ** (-0.5)).astype(bf16)

    @pl.when(step == pl.num_programs(0) - 1)
    def _():
        dk_ref[...] = dk_acc[...].astype(bf16)
        dv_ref[...] = dv_acc[...].astype(bf16)


def attend_back_call(
    layer, first, last, base, own, recv, queries, keys, values, mixed, lse, seg_col, seg_row, weights
):
    tokens = base.shape[0]
    shape = lambda width, kind: jax.ShapeDtypeStruct((tokens, width), kind)
    whole = (tokens, HALF)
    return pl.pallas_call(
        attend_back_kernel,
        out_shape=[
            shape(D, f32),
            shape(D, bf16),
            shape(HALF, bf16),
            shape(HALF, bf16),
            shape(HALF, bf16),
            jax.ShapeDtypeStruct((1, D), f32),
        ],
        grid_spec=pltpu.PrefetchScalarGridSpec(
            num_scalar_prefetch=2,
            grid=(tokens // ROWS,),
            in_specs=[
                rows_spec(D),
                rows_spec(D),
                rows_spec(D),
                rows_spec(HALF),
                fixed(whole),
                fixed(whole),
                rows_spec(HALF),
                pl.BlockSpec((8, ROWS), lambda i, *_: (0, i)),
                fixed(seg_col.shape),
                pl.BlockSpec((1, ROWS), lambda i, *_: (0, i)),
                fixed((D, HALF)),
            ],
            out_specs=[
                rows_spec(D),
                rows_spec(D),
                rows_spec(HALF),
                fixed(whole),
                fixed(whole),
                fixed((1, D)),
            ],
            scratch_shapes=[
                pltpu.VMEM(whole, f32),
                pltpu.VMEM(whole, f32),
                pltpu.VMEM((ROWS, HALF), f32),
                pltpu.VMEM((ROWS, HALF), bf16),
            ],
        ),
        compiler_params=params(),
        cost_estimate=cost(14 * HEADS * tokens * tokens * BS, tokens * D * 20, HEADS * tokens * tokens),
    )(
        first, last, base, own, recv, stay(queries), stay(keys), stay(values), stay(mixed), lse,
        seg_col, seg_row, weights["out", layer],
    )


def qkv_back_kernel(layer, dq, dk, dv, hid, vec, weight, back, dgain, dshift, dbq, dbv):
    grad_three = jnp.concatenate([dq[...], dk[...], dv[...]], axis=1)
    grad_normed = dot_nt(grad_three, joined(weight, 0, D, 3))
    part_back, gain_grad, shift_grad = norm_back(hid[...], vec_piece(vec, layer, "g1"), grad_normed)
    back[...] = part_back.astype(bf16)
    accumulate(dgain, gain_grad)
    accumulate(dshift, shift_grad)
    accumulate(dbq, jnp.sum(dq[...].astype(f32), axis=0, keepdims=True))
    accumulate(dbv, jnp.sum(dv[...].astype(f32), axis=0, keepdims=True))


def qkv_back_call(layer, dq, dk, dv, hid, vec, weights):
    tokens = dq.shape[0]
    line = lambda width: jax.ShapeDtypeStruct((1, width), f32)
    lines = [line(D), line(D), line(HALF), line(HALF)]
    return pl.pallas_call(
        functools.partial(qkv_back_kernel, layer),
        out_shape=[jax.ShapeDtypeStruct((tokens, D), bf16)] + lines,
        grid=(tokens // ROWS,),
        in_specs=[rows_spec(HALF)] * 3
        + [
            rows_spec(D),
            fixed(vec.shape),
            fixed((3 * D, HALF)),
        ],
        out_specs=[rows_spec(D)] + [fixed(o.shape) for o in lines],
        compiler_params=params(),
        cost_estimate=cost(2 * tokens * D * 3 * HALF, tokens * D * 10),
    )(dq, dk, dv, stay(hid), vec, weights["qkv", layer])


def split(values):
    high = values.astype(bf16)
    return high, (values - high.astype(f32)).astype(bf16)


def product(left, right, left_dim, right_dim):
    def one(a, b):
        return lax.dot_general(
            a, b, (((left_dim,), (right_dim,)), ((), ())), preferred_element_type=f32
        )

    return one(left[0], right[0]) + (one(left[0], right[1]) + one(left[1], right[0]))


def owner_kernel(per, used, home, near, far, master, left, right, moment, variance, grad, out, out_mom, out_var):
    here = range(per)
    first = pl.program_id(0) * per
    lefts = [split(left[i]) for i in here]
    rights = [split(right[i]) for i in here]
    rotated = []
    for i in here:
        rows = slice(i * BS, (i + 1) * BS)
        tile = jnp.where(home[0] > 0, near[rows, :].astype(f32), far[rows, :].astype(f32))
        tile = jnp.where(used[first + i] > 0, tile, 0.0)
        grad[i] = tile
        tile = tile.astype(bf16)
        rotated.append(split(dot_tn(lefts[i][0], tile) + dot_tn(lefts[i][1], tile)))
    rotated = [product(rotated[i], rights[i], 1, 0) for i in here]
    steps = []
    for i in here:
        new_moment = decay * moment[i] + (1.0 - decay) * rotated[i]
        new_variance = decay * variance[i] + (1.0 - decay) * rotated[i] * rotated[i]
        out_mom[i] = new_moment
        out_var[i] = new_variance
        steps.append(split(new_moment / (jnp.sqrt(new_variance) + adam_eps)))
    returned = [split(product(lefts[i], steps[i], 1, 0)) for i in here]
    returned = [product(returned[i], rights[i], 1, 1) for i in here]
    for i in here:
        out[i] = master[i] - matrix_rate * returned[i]


def owner_call(used, home, near, far, *arrays):
    count = arrays[0].shape[0]
    per = min(8, count)
    block = pl.BlockSpec((per, BS, BS), lambda i, *_: (i, 0, 0))
    return pl.pallas_call(
        functools.partial(owner_kernel, per),
        out_shape=[jax.ShapeDtypeStruct(arrays[0].shape, f32)] * 4,
        grid_spec=pltpu.PrefetchScalarGridSpec(
            num_scalar_prefetch=2,
            grid=(count // per,),
            in_specs=[pl.BlockSpec((per * BS, BS), lambda i, *_: (i, 0))] * 2 + [block] * 5,
            out_specs=[block] * 4,
        ),
        compiler_params=params(),
        cost_estimate=cost(count * 88 * BS**3, count * BS * BS * 38),
    )(used, home, stay(near), stay(far), *arrays)


def reduce_kernel(carrying, last, *refs):
    block, arrived, *refs = refs
    total = block[...].astype(f32) + arrived[...].astype(f32)
    if carrying:
        carried, *refs = refs
        total = total + carried[...].astype(f32)
    if last:
        [out] = refs
    else:
        following, out, later = refs
        later[...] = following[...]
    out[...] = total.astype(bf16)


def reduce_call(j, n, buffer, arrived, carried, payload):
    last = j >= 2
    at = lambda j, x_rel: pl.BlockSpec((payload, BS), lambda i: ((j * 2 + x_rel) * 2 + n, 0))
    whole = fixed((payload, BS))
    operands = [stay(buffer), stay(arrived)] + ([] if carried is None else [stay(carried)])
    specs = [at(j, 0)] + [whole] * (len(operands) - 1)
    if not last:
        operands.append(stay(buffer))
        specs.append(at(j + 2, 1))
    outs = [pltpu.HBM((payload, BS), bf16)] * (1 if last else 2)
    made = pl.pallas_call(
        functools.partial(reduce_kernel, carried is not None, last),
        out_shape=outs,
        grid=(1,),
        in_specs=specs,
        out_specs=[whole] * len(outs),
        compiler_params=params(8),
        cost_estimate=cost(payload * BS * 3, payload * BS * 12),
    )(*operands)
    return (made[0], None) if last else made


class Routes:
    def __init__(self, dp_n):
        pairs = [(d, t) for d in range(dp_n) for t in range(TENSOR)]
        at = lambda d, t: d * TENSOR + t
        home = [(d, t) for d, t in pairs if d % 2 == t]
        away = [(d, t) for d, t in pairs if d % 2 != t]
        self.core_all = [(at(d, t), at(d ^ 1, t)) for d, t in pairs]
        self.core_out = [(at(d, t), at(d ^ 1, t)) for d, t in home]
        self.core_in = [(at(d, t), at(d ^ 1, t)) for d, t in away]
        self.y_all = [(at(d, t), at(d, 1 - t)) for d, t in pairs]
        self.y_out = [(at(d, t), at(d, 1 - t)) for d, t in home]
        self.y_in = [(at(d, t), at(d, 1 - t)) for d, t in away]
        self.x_home = [(at(d, t), at(d ^ 2, t)) for d, t in home]
        self.x_away = [(at(d, t), at(d ^ 2, t)) for d, t in away]
        self.x_all = [(at(d, t), at(d ^ 2, t)) for d, t in pairs]
        self.z_all = [(at(d, t), at((d + 4) % dp_n, t)) for d, t in pairs]
        self.z_home = [(at(d, t), at((d + 4) % dp_n, t)) for d, t in home]


def send(value, route):
    return lax.ppermute(value, AXES, route)


def shards(
    patches,
    cotangent,
    image_size,
    block_slot,
    pinv,
    master_slots,
    left_basis,
    right_basis,
    mom_slots,
    var_slots,
    vec_master,
    vec_mom,
    vec_var,
):
    dp_n = lax.axis_size("dp")
    dp_pos = lax.axis_index("dp")
    y_pos = lax.axis_index("tensor")
    core = dp_pos % 2
    home = core == y_pos
    routes = Routes(dp_n)
    grid3 = dp_n == 16
    x_pos = (dp_pos // 2) % 2
    half_at = (x_pos if grid3 else x_pos * 0).astype(jnp.int32).reshape(1)
    tokens_n = patches.shape[0]
    slots_per = master_slots.shape[1]
    vec_per = vec_master.shape[1]
    slots_n = slots_per * dp_n
    payload = slots_per * BS + VEC_ROWS

    patches = jnp.where(home, patches, send(patches, routes.core_out))
    cotangent = jnp.where(home, cotangent, send(cotangent, routes.core_out))
    size_row = jnp.where(home, image_size, send(image_size, routes.core_out))[0]
    own_slots = block_slot[0]
    slot_other = send(block_slot, routes.y_all)

    lengths = jnp.where(
        size_row == 0, LEN_A, jnp.where(size_row == 1, LEN_B, jnp.where(size_row == 2, LEN_C, 0))
    )
    order = jnp.arange(IMG_DEV)
    ends_at = jnp.sum(jnp.where(order[None, :] <= order[:, None], lengths[None, :], 0), axis=1)
    places = jnp.arange(tokens_n)
    segment = jnp.sum((places[:, None] >= ends_at[None, :]).astype(jnp.int32), axis=1)
    in_image = segment[:, None] == order[None, :]
    select = jnp.stack(
        [jnp.any(in_image & (size_row == s)[None, :], axis=1) for s in range(3)], axis=1
    )
    valid_col = (segment < IMG_DEV).astype(f32)[:, None]
    seg_col = segment[:, None]
    seg_row = segment[None, :]
    blocks_n = tokens_n // ROWS
    starts = jnp.arange(blocks_n) * ROWS
    begun = ends_at[None, :] <= starts[:, None]
    first_tok = jnp.max(jnp.where(begun, ends_at[None, :], 0), axis=1)
    after = ends_at[None, :] > (starts + ROWS - 1)[:, None]
    last_tok = jnp.min(jnp.where(after, ends_at[None, :], tokens_n), axis=1)
    first_blk = (first_tok // ROWS).astype(jnp.int32)
    last_blk = ((last_tok + ROWS - 1) // ROWS).astype(jnp.int32)
    first_key = (first_tok // KEYS).astype(jnp.int32)
    last_key = ((last_tok + KEYS - 1) // KEYS).astype(jnp.int32)

    select_low = select.astype(bf16)
    class_col = jnp.sum(jnp.where(select, jnp.arange(1, 4)[None, :], 0), axis=1, keepdims=True) - 1
    present = jnp.any(select.reshape(blocks_n, ROWS, 3), axis=1).astype(jnp.int32)

    def expand(which):
        return expand_call(which, present, half_at, patches, class_col, pinv)

    vec_low = jnp.pad(vec_master[0].astype(bf16), (0, VEC_ROWS * BS - vec_per))
    own_pack = jnp.concatenate(
        [
            master_slots[0].astype(bf16).reshape(slots_per * BS, BS),
            vec_low.reshape(VEC_ROWS, BS),
        ],
        axis=0,
    )
    flag = home.astype(jnp.int32).reshape(1)
    if grid3:
        z_pos = dp_pos // 4
        pack = own_pack
        chunks, first, second, owner = [], [], [], []
        middle_row = slots_per * BS // 2
        for j in range(4):
            beside_x, beside_y = send(pack, routes.x_all), send(pack, routes.y_all)
            if j < 3:
                further = send(pack, routes.z_all)
                work = [expand(j)] + ([slot_other] if j == 0 else [])
                further, chunk, *work = fence(further, *work)
                chunks.append(chunk)
                if j == 0:
                    [slot_other] = work
            else:
                beside_x, chunk = fence(beside_x, expand(j))
                chunks.append(chunk)
            corner = jnp.concatenate(
                [send(beside_x[:middle_row], routes.y_all), send(beside_y[middle_row:], routes.x_all)],
                axis=0,
            )
            near_two = send(jnp.where(home, beside_y, pack), routes.core_all)
            far_two = send(jnp.where(home, corner, beside_x), routes.core_all)
            first += [pack, near_two, beside_x, far_two]
            second += [beside_y, near_two, corner, far_two]
            for x_rel in range(2):
                for n in range(2):
                    owner.append(((z_pos - j) % 4) * 4 + (x_pos ^ x_rel) * 2 + (core ^ n))
            if j < 3:
                pack = further
        first = [v[None] for v in first]
        second = [v[None] for v in second]
        owner = jnp.stack(owner).astype(jnp.int32)
    else:
        everything = lax.all_gather(own_pack, AXES, axis=0)
        everything = everything.reshape(dp_n, TENSOR, payload, BS)
        first = [jnp.where(core == 0, everything[:, 0], everything[:, 1])]
        second = []
        owner = jnp.arange(dp_n, dtype=jnp.int32)
        chunks = [expand(c) for c in range(CHUNKS)]
    slot_list = jnp.where(home, block_slot, slot_other)[0]
    named = slot_list[None, :] == jnp.arange(slots_n)[:, None]
    used = jnp.any(named, axis=1)
    drow = jnp.where(used, jnp.sum(jnp.where(named, TARGET_ROW[None, :], 0), axis=1), -1)
    dcol = jnp.sum(jnp.where(named, TARGET_COL[None, :], 0), axis=1)
    weights, vec_rows = gather_tiles(first, second, owner, drow, dcol, flag, slots_per, dp_n)
    vec = vec_rows.reshape(dp_n, VEC_ROWS * BS)[:, :vec_per].astype(f32).reshape(1, dp_n * vec_per)

    embedded = embed_call(half_at, chunks, vec, weights)
    embedded_other = send(embedded, routes.core_all)
    core_flag = core.astype(jnp.int32).reshape(1)

    caches = []
    hidden, own, recv = None, embedded, embedded_other
    for layer in range(LAYERS):
        hidden, normed, queries, keys, values = qkv_call(
            layer, hidden, own, recv, core_flag, vec, weights
        )
        mixed, lse, part = attend_call(
            layer, first_blk, last_blk, queries, keys, values, seg_col, seg_row, vec, weights
        )
        other = send(part, routes.core_all)
        middle, normed2, act, slope, own = mlp_call(layer, hidden, part, other, vec, weights)
        recv = send(own, routes.core_all)
        caches.append((hidden, normed, queries, keys, values, mixed, lse, middle, normed2, act, slope))
        hidden = middle
    out_low = ((hidden + (own.astype(f32) + recv.astype(f32))) * valid_col).astype(bf16)

    owners = jnp.arange(dp_n)
    if grid3:
        place = (
            ((z_pos - 1 - owners // 4) % 4) * 4
            + (x_pos ^ ((owners // 2) % 2)) * 2
            + (core ^ (owners % 2))
        ).astype(jnp.int32)
    else:
        place = owners.astype(jnp.int32)
    slot_owner = slot_list // slots_per
    owner_place = jnp.sum(
        jnp.where(slot_owner[:, None] == owners[None, :], place[None, :], 0), axis=1
    )
    tile_pos = (owner_place * payload + (slot_list % slots_per) * BS).astype(jnp.int32)
    vec_pos = (place * payload + slots_per * BS).astype(jnp.int32)
    total_rows = dp_n * payload
    where_to = jnp.concatenate([half_at, flag if grid3 else flag * 0 + 1])
    offsets = {"base": 0}
    count = BASE_PIX // BS * (HALF // BS)
    for layer in range(LAYERS):
        for name, size in (("qkv", 3 * D * HALF), ("out", D * HALF), ("up", D * HALF_FF), ("down", D * HALF_FF)):
            offsets[name, layer] = count
            count += size // (BS * BS)

    def place_tiles(key, matrix, arrived, buffer):
        tiles = matrix.size // (BS * BS)
        pos = tile_pos[offsets[key] : offsets[key] + tiles]
        rows_n = matrix.shape[0] // 2 if matrix.shape[0] > HALF else HALF
        return scatter_matrix(pos, matrix, arrived, where_to, buffer, total_rows, rows_n)

    def place_base(rel, matrix, arrived, buffer):
        size = BASE_PIX * HALF // (BS * BS) // 2
        low_pos, high_pos = tile_pos[:size], tile_pos[size : 2 * size]
        pos = jnp.where(half_at[0] == rel, low_pos, high_pos)
        return scatter_matrix(pos, matrix, arrived, where_to, buffer, total_rows, D)

    def over(matrix):
        return send(matrix, routes.y_in) if grid3 else None

    def beside(matrix):
        return send(other_half(half_at, matrix), routes.x_away) if grid3 else None

    def summed(matrix, arrived):
        return half_sum(half_at, matrix, arrived) if grid3 else None

    def hold(*arrays):
        kept = [a for a in arrays if a is not None]
        done = iter(fence(*kept))
        return [None if a is None else next(done) for a in arrays]

    top, low = 1, 0
    vec_grads = [None] * LAYERS

    def mlp_step(layer, grad, own, recv):
        middle, normed2, act, slope = caches[layer][7:11]
        made = mlp_back_call(layer, grad, own, recv, valid_col, middle, slope, vec, weights)
        if own is not None:
            return made
        return [made[0]] + list(made)

    def attend_step(layer, grad, part, other, lse):
        hid_in, normed, queries, keys, values, mixed = caches[layer][:6]
        return attend_back_call(
            layer, first_key, last_key, grad, part, other, queries, keys, values, mixed, lse,
            seg_col, seg_row, weights,
        )

    grad, grad_low, du, part, dg2, ds2, db1, db2 = mlp_step(top, cotangent, None, None)
    other = send(part, routes.core_all)
    gd1 = dot_tn(caches[top][9], grad_low).astype(bf16)
    gu1 = dot_tn(caches[top][8], du).astype(bf16)
    ad1 = over(gd1)
    lse, gu1 = fence(caches[top][6], gu1)
    grad, grad_low, dq, dk, dv, dbo = attend_step(top, grad, part, other, lse)
    vec, dbo, ad1, gu1, out_low = hold(vec, dbo, ad1, gu1, out_low)
    au1 = over(gu1)
    own, dg1, ds1, dbq, dbv = qkv_back_call(top, dq, dk, dv, caches[top][0], vec, weights)
    recv = send(own, routes.core_all)
    go1 = dot_tn(caches[top][5], grad_low).astype(bf16)
    gq1 = dot_tn(caches[top][1], jnp.concatenate([dq, dk, dv], axis=1)).astype(bf16)
    vec_grads[top] = [dg1, ds1, dbq, dbv, dbo, dg2, ds2, db1, db2]
    grad, grad_low, du, part, dg2, ds2, db1, db2 = mlp_step(low, grad, own, recv)
    other = send(part, routes.core_all)
    db2, go1, gq1 = hold(db2, go1, gq1)
    xq1, ao1 = beside(gq1), over(go1)
    gd0 = dot_tn(caches[low][9], grad_low).astype(bf16)
    gu0 = dot_tn(caches[low][8], du).astype(bf16)
    lse, gd0, gu0, xq1, au1 = hold(caches[low][6], gd0, gu0, xq1, au1)
    hq1 = summed(gq1, xq1)
    ad0 = over(gd0)
    xu0 = beside(gu0)
    buffer = place_tiles(("down", top), gd1, ad1, None)
    buffer = place_tiles(("up", top), gu1, au1, buffer)
    grad, grad_low, dq, dk, dv, dbo = attend_step(low, grad, part, other, lse)
    vec, dbo, ad0, ao1, xu0, hq1, buffer = hold(vec, dbo, ad0, ao1, xu0, hq1, buffer)
    au0 = over(summed(gu0, xu0))
    aq1 = over(hq1)
    own, dg1, ds1, dbq, dbv = qkv_back_call(low, dq, dk, dv, caches[low][0], vec, weights)
    recv = send(own, routes.core_all)
    gq0 = dot_tn(caches[low][1], jnp.concatenate([dq, dk, dv], axis=1)).astype(bf16)
    vec_grads[low] = [dg1, ds1, dbq, dbv, dbo, dg2, ds2, db1, db2]
    xq0 = beside(gq0)
    grad_emb, grad_emb_bias = embed_back_call(core_flag, grad, own, recv)
    middle = CHUNKS // 2

    def base_grad(parts):
        return jnp.concatenate([dot_tn(c, grad_emb).astype(bf16) for c in parts], axis=0)

    gbt = base_grad(chunks[middle:])
    gbt, au0, xq0 = hold(gbt, au0, xq0)
    xb = send(gbt, routes.x_away) if grid3 else None
    aq0 = over(summed(gq0, xq0))
    gbm = base_grad(chunks[:middle])
    vec_grad = pack_call([grad_emb_bias] + vec_grads[0] + vec_grads[1], dp_n, vec_per)
    go0 = dot_tn(caches[low][5], grad_low).astype(bf16)
    ao0, av = over(go0), over(vec_grad)
    buffer = place_tiles(("out", top), go1, ao1, buffer)
    buffer = place_tiles(("down", low), gd0, ad0, buffer)
    buffer = place_tiles(("up", low), gu0, au0, buffer)
    buffer = place_base(1, gbt, None, buffer)
    gbm, xb, aq0, ao0, av, aq1, buffer = hold(gbm, xb, aq0, ao0, av, aq1, buffer)
    ab = over(half_sum(half_at * 0, gbm, xb)) if grid3 else None
    buffer = place_tiles(("qkv", top), gq1, aq1, buffer)
    buffer = place_tiles(("out", low), go0, ao0, buffer)
    buffer = scatter_vec(vec_pos, vec_grad, av, buffer)
    buffer = place_tiles(("qkv", low), gq0, aq0, buffer)
    base_weight = weights["base", 0]
    ab, buffer, base_weight, out_low = hold(ab, buffer, base_weight, out_low)
    weights["base", 0] = base_weight
    buffer = place_base(0, gbm, ab, buffer)

    if grid3:
        token = jnp.zeros((8, BS), f32)
        order = (1, 0)
        resized = resize_call(weights, pinv)
        carried = {n: None for n in order}
        blocks = buffer.reshape(4, 2, 2, payload, BS)
        across = {n: send(blocks[0, 1, n], routes.x_home) for n in order}
        following = {n: blocks[1, 1, n] for n in order}
        rounded = {}
        for j in range(4):
            for n in order:
                extra = None
                if j == 0 and n == order[0]:
                    extra = resized
                token, across[n], carried[n], extra = hold(token, across[n], carried[n], extra)
                if extra is not None:
                    resized = extra
                arrived = across[n]
                if j < 3:
                    across[n] = send(following[n], routes.x_home)
                total, following[n] = reduce_call(j, n, buffer, arrived, carried[n], payload)
                if j < 3:
                    carried[n] = send(total, routes.z_home)
                else:
                    rounded[n] = total
        near_grad, far_grad = rounded[0], send(rounded[1], routes.core_out)
    else:
        held = buffer.reshape(dp_n, 1, payload, BS).astype(f32)
        nothing = jnp.zeros_like(held)
        both = jnp.concatenate(
            [jnp.where(core == 0, held, nothing), jnp.where(core == 0, nothing, held)], axis=1
        )
        used_rows = jnp.repeat(used, BS).reshape(dp_n, 1, slots_per * BS, 1)
        used_rows = jnp.concatenate(
            [used_rows, jnp.ones((dp_n, 1, VEC_ROWS, 1), bool)], axis=2
        )
        both = jnp.where(used_rows, both, 0.0).reshape(dp_n * TENSOR * payload, BS)
        near_grad = lax.psum_scatter(both, AXES, scatter_dimension=0, tiled=True).astype(bf16)
        far_grad = near_grad
        resized = resize_call(weights, pinv)

    output = jnp.where(home, out_low, send(out_low, routes.y_out)).astype(f32)
    grad_pixels = sum(
        dot(grad_emb * select_low[:, s : s + 1], resized[s]) for s in range(3)
    ).astype(bf16)
    pixels_other = send(grad_pixels, routes.core_all)
    pixel_sides = [
        grad_pixels[:, s * HALF : (s + 1) * HALF].astype(f32)
        + pixels_other[:, s * HALF : (s + 1) * HALF].astype(f32)
        for s in range(TENSOR)
    ]
    near = jnp.where(core == 0, pixel_sides[0], pixel_sides[1])
    far = jnp.where(core == 0, pixel_sides[1], pixel_sides[0]).astype(bf16)
    patch_grad = jnp.where(home, near, send(far, routes.y_out).astype(f32))

    my_slots = dp_pos * slots_per + jnp.arange(slots_per)
    mine_used = jnp.any(own_slots[None, :] == my_slots[:, None], axis=1).astype(jnp.int32)
    owned_grad, new_master, new_mom, new_var = owner_call(
        mine_used, flag, near_grad, far_grad, master_slots[0], left_basis[0], right_basis[0], mom_slots[0], var_slots[0]
    )
    vec_rows = jnp.where(home, near_grad[slots_per * BS :], far_grad[slots_per * BS :])
    owned_vec_grad = vec_rows.astype(f32).reshape(VEC_ROWS * BS)[:vec_per]
    new_vec_mom = decay * vec_mom[0] + (1.0 - decay) * owned_vec_grad
    new_vec_var = decay * vec_var[0] + (1.0 - decay) * owned_vec_grad * owned_vec_grad
    new_vec = vec_master[0] - vector_rate * new_vec_mom / (jnp.sqrt(new_vec_var) + adam_eps)
    return (
        output,
        patch_grad,
        owned_grad[None],
        new_master[None],
        new_mom[None],
        new_var[None],
        owned_vec_grad[None],
        new_vec[None],
        new_vec_mom[None],
        new_vec_var[None],
    )


def solution(mesh):
    slots = P("tensor", "dp", None, None)
    vectors = P("tensor", "dp")
    tokens = P("dp", None)
    in_specs = (tokens, tokens, tokens, P("tensor", None), P()) + (slots,) * 5 + (vectors,) * 3
    out_specs = (tokens, P("dp", "tensor")) + (slots,) * 4 + (vectors,) * 4
    return jax.shard_map(shards, mesh=mesh, in_specs=in_specs, out_specs=out_specs, check_vma=False)
```

```python
import functools

import jax
import jax.numpy as jnp
import numpy as np
from jax import lax
from jax.experimental import pallas as pl
from jax.experimental.pallas import tpu as pltpu
from jax.sharding import PartitionSpec as P

D = 768
HEAD_DIM = 64
FF = 3072
BASE_PIX = 3072
LAYERS = 2
LEN_A = 196
LEN_B = 225
LEN_C = 576
IMG_DEV = 5
BS = 128
TENSOR = 2
HALF = D // TENSOR
HALF_FF = FF // TENSOR
HEADS = HALF // HEAD_DIM
ROWS = 256
KEYS = 512
VEC_ROWS = 16
CHUNKS = 4

AXES = ("dp", "tensor")
precise = lax.Precision.HIGHEST
masked_score = -1e30
norm_eps = 1e-06
adam_eps = 1e-08
decay = 0.5
matrix_rate = 0.05
vector_rate = 0.3
f32 = jnp.float32
bf16 = jnp.bfloat16
MIB = 1024 * 1024

WEIGHTS = [("base", 0, BASE_PIX)]
for layer in range(LAYERS):
    WEIGHTS += [("qkv", layer, 3 * D), ("out", layer, D), ("up", layer, FF), ("down", layer, FF)]
STARTS = {}
PANEL_ROWS = 0
for name, layer, size in WEIGHTS:
    STARTS[name, layer] = PANEL_ROWS
    PANEL_ROWS += size


def tile_targets():
    rows, cols = [], []

    def add(start, rows_n, cols_n):
        for i in range(rows_n // BS):
            for j in range(cols_n // BS):
                panel, inner = divmod(j * BS, HALF)
                rows.append(start + panel * rows_n + i * BS)
                cols.append(inner)

    add(STARTS["base", 0], BASE_PIX, HALF)
    for layer in range(LAYERS):
        add(STARTS["qkv", layer], D, 3 * HALF)
        add(STARTS["out", layer], HALF, D)
        add(STARTS["up", layer], D, HALF_FF)
        add(STARTS["down", layer], HALF_FF, D)
    return np.array(rows, np.int32), np.array(cols, np.int32)


TARGET_ROW, TARGET_COL = tile_targets()
LAYER_VECS = (D, D, HALF, HALF, D, D, D, HALF_FF, D)
VEC_NAMES = ("g1", "s1", "bq", "bv", "bo", "g2", "s2", "b1", "b2")


def vec_offsets():
    offset = HALF
    found = []
    for layer in range(LAYERS):
        here = {}
        for name, length in zip(VEC_NAMES, LAYER_VECS):
            here[name] = (offset, length)
            offset += length
        found.append(here)
    return found


VEC_AT = vec_offsets()


def params(limit=24):
    return pltpu.CompilerParams(
        dimension_semantics=("arbitrary",), vmem_limit_bytes=limit * MIB
    )


def cost(flops, nbytes, trans=0):
    return pl.CostEstimate(flops=flops, bytes_accessed=nbytes, transcendentals=trans)


def rows_spec(width):
    return pl.BlockSpec((ROWS, width), lambda i, *_: (i, 0))


def fixed(shape, at=0):
    return pl.BlockSpec(shape, lambda i, *_: (at,) + (0,) * (len(shape) - 1))


def vec_piece(vec_ref, layer, name):
    start, length = VEC_AT[layer][name]
    return vec_ref[:, start : start + length]


def dot(left, right):
    return jnp.dot(left, right, preferred_element_type=f32)


def dot_nt(left, right, precision=None):
    return lax.dot_general(
        left, right, (((1,), (1,)), ((), ())), precision=precision, preferred_element_type=f32
    )


def dot_tn(left, right):
    return lax.dot_general(left, right, (((0,), (0,)), ((), ())), preferred_element_type=f32)


def joined(ref, start, rows_n, panels):
    return jnp.concatenate(
        [ref[start + p * rows_n : start + (p + 1) * rows_n, :] for p in range(panels)], axis=1
    )


def norm_stats(values):
    mean_val = jnp.mean(values, axis=-1, keepdims=True)
    centered = values - mean_val
    inv_std = lax.rsqrt(jnp.mean(centered * centered, axis=-1, keepdims=True) + norm_eps)
    return centered * inv_std, inv_std


def norm_back(values, gain, grad):
    unit, inv_std = norm_stats(values)
    scaled = grad * gain
    mean_s = jnp.mean(scaled, axis=-1, keepdims=True)
    mean_u = jnp.mean(scaled * unit, axis=-1, keepdims=True)
    back = inv_std * (scaled - mean_s - unit * mean_u)
    return (
        back,
        jnp.sum(grad * unit, axis=0, keepdims=True),
        jnp.sum(grad, axis=0, keepdims=True),
    )


def accumulate(ref, value):
    first = pl.program_id(0) == 0

    @pl.when(first)
    def _():
        ref[...] = value

    @pl.when(jnp.logical_not(first))
    def _():
        ref[...] += value


def stay(value):
    return pltpu.with_memory_space_constraint(value, pltpu.HBM)


def fence(*arrays):
    def nothing(*refs):
        pass

    anywhere = pl.BlockSpec(memory_space=pl.ANY)
    return pl.pallas_call(
        nothing,
        out_shape=[jax.ShapeDtypeStruct(a.shape, a.dtype) for a in arrays],
        in_specs=[anywhere] * len(arrays),
        out_specs=[anywhere] * len(arrays),
        input_output_aliases={i: i for i in range(len(arrays))},
        compiler_params=pltpu.CompilerParams(vmem_limit_bytes=MIB),
    )(*[stay(a) if a.size > 32 * 1024 else a for a in arrays])


def gather_kernel(slots, count_a, count_b, owner, drow, dcol, flag, *refs):
    first = refs[:count_a]
    second = refs[count_a : count_a + count_b]
    *panels, vectors, held, sem, vec_sem = refs[count_a + count_b :]

    def copy_all(sources):
        at = 0
        for src in sources:
            for n in range(src.shape[0]):
                who = owner[at]
                at += 1

                def body(i, carried, src=src, n=n, who=who):
                    slot = who * slots + i
                    row = drow[slot]

                    @pl.when(row >= 0)
                    def _():
                        start = pl.multiple_of(i * BS, BS)
                        pltpu.make_async_copy(
                            src.at[n, pl.ds(start, BS), :],
                            held.at[
                                pl.ds(pl.multiple_of(row, BS), BS),
                                pl.ds(pl.multiple_of(dcol[slot], BS), BS),
                            ],
                            sem,
                        ).start()

                    return carried

                lax.fori_loop(0, slots, body, 0)
                pltpu.make_async_copy(
                    src.at[n, pl.ds(slots * BS, VEC_ROWS), :], vectors.at[who], vec_sem
                ).start()

    if count_b:

        @pl.when(flag[0] == 1)
        def _():
            copy_all(first)

        @pl.when(flag[0] == 0)
        def _():
            copy_all(second)
    else:
        copy_all(first)
    pltpu.make_async_copy(held, held, sem).wait()
    at = 0
    for panel in panels:
        size = panel.shape[0]
        pltpu.make_async_copy(held.at[pl.ds(at, size), :], panel, sem).start()
        at += size
    pltpu.make_async_copy(vectors, vectors, vec_sem).wait()
    pltpu.make_async_copy(held, held, sem).wait()


def gather_tiles(first, second, owner, drow, dcol, flag, slots, owners):
    anywhere = pl.BlockSpec(memory_space=pl.ANY)
    *panels, vectors = pl.pallas_call(
        functools.partial(gather_kernel, slots, len(first), len(second)),
        out_shape=[pltpu.HBM((size, HALF), bf16) for unused, unused2, size in WEIGHTS]
        + [jax.ShapeDtypeStruct((owners, VEC_ROWS, BS), bf16)],
        grid_spec=pltpu.PrefetchScalarGridSpec(
            num_scalar_prefetch=4,
            grid=(1,),
            in_specs=[anywhere] * (len(first) + len(second)),
            out_specs=[anywhere] * len(WEIGHTS) + [fixed((owners, VEC_ROWS, BS))],
            scratch_shapes=[
                pltpu.VMEM((PANEL_ROWS, HALF), bf16),
                pltpu.SemaphoreType.DMA,
                pltpu.SemaphoreType.DMA,
            ],
        ),
        compiler_params=params(),
        cost_estimate=cost(0, 4 * PANEL_ROWS * HALF),
    )(owner, drow, dcol, flag, *[stay(v) for v in first], *[stay(v) for v in second])
    return {(name, layer): p for (name, layer, unused), p in zip(WEIGHTS, panels)}, vectors


def scatter_kernel(rows_n, cols_n, steps, paired, parts, pos, part, own, *refs):
    @pl.when(part[1] > 0)
    def _():
        scatter_body(rows_n, cols_n, steps, paired, parts, pos, part, own, *refs)


def scatter_body(rows_n, cols_n, steps, paired, parts, pos, part, own, *refs):
    if paired:
        recv, *refs = refs
        span = pl.num_programs(0) // parts
        here = jnp.logical_or(parts == 1, pl.program_id(0) // span == part[0])
    target, buf, sems = refs[-3:]
    step = pl.program_id(0)
    slot = lax.rem(step, 2)
    per = rows_n // BS * (cols_n // BS)

    def wait(at):
        pltpu.make_async_copy(buf.at[at], buf.at[at], sems.at[at]).wait()

    @pl.when(step >= 2)
    def _():
        wait(slot)

    for i in range(rows_n // BS):
        for j in range(cols_n // BS):
            area = (slice(i * BS, (i + 1) * BS), slice(j * BS, (j + 1) * BS))
            value = own[area]
            if paired:
                more = jnp.where(here, recv[area].astype(f32), 0.0)
                value = (value.astype(f32) + more).astype(bf16)
            buf[slot, i * (cols_n // BS) + j] = value
    for n in range(per):
        pltpu.make_async_copy(
            buf.at[slot, n],
            target.at[pl.ds(pl.multiple_of(pos[step * per + n], 16), BS), :],
            sems.at[slot],
        ).start()

    @pl.when(step == pl.num_programs(0) - 1)
    def _():
        if steps > 1:
            wait(1 - slot)
        wait(slot)


def scatter_matrix(pos, own, recv, part, target, total_rows, rows_n):
    cols_n = own.shape[1]
    steps = own.shape[0] // rows_n
    anywhere = pl.BlockSpec(memory_space=pl.ANY)
    block = pl.BlockSpec((rows_n, cols_n), lambda i, *_: (i, 0))
    paired = recv is not None
    parts = own.shape[0] // recv.shape[0] if paired else 1
    span = steps // parts
    arrived = pl.BlockSpec(
        (rows_n, cols_n), lambda i, pos, part: (jnp.clip(i - part[0] * span, 0, span - 1), 0)
    )
    operands = [stay(own)] + ([stay(recv)] if paired else []) + ([] if target is None else [stay(target)])
    specs = [block] + ([block if parts == 1 else arrived] if paired else [])
    specs += [] if target is None else [anywhere]
    return pl.pallas_call(
        functools.partial(scatter_kernel, rows_n, cols_n, steps, paired, parts),
        out_shape=pltpu.HBM((total_rows, BS), bf16),
        grid_spec=pltpu.PrefetchScalarGridSpec(
            num_scalar_prefetch=2,
            grid=(steps,),
            in_specs=specs,
            out_specs=anywhere,
            scratch_shapes=[
                pltpu.VMEM((2, rows_n // BS * (cols_n // BS), BS, BS), bf16),
                pltpu.SemaphoreType.DMA((2,)),
            ],
        ),
        input_output_aliases={} if target is None else {len(operands) + 1: 0},
        compiler_params=params(12),
        cost_estimate=cost(own.size, own.size * 6),
    )(pos, part, *operands)


def half_sum_kernel(part, own, arrived, out):
    out[...] = (own[...].astype(f32) + arrived[...].astype(f32)).astype(bf16)


def half_sum(part, own, arrived):
    block = arrived.shape
    return pl.pallas_call(
        half_sum_kernel,
        out_shape=pltpu.HBM(block, bf16),
        grid_spec=pltpu.PrefetchScalarGridSpec(
            num_scalar_prefetch=1,
            grid=(1,),
            in_specs=[pl.BlockSpec(block, lambda i, part: (part[0], 0)), fixed(block)],
            out_specs=fixed(block),
        ),
        compiler_params=params(8),
        cost_estimate=cost(arrived.size, arrived.size * 6),
    )(part, stay(own), stay(arrived))


def half_copy_kernel(part, own, out):
    out[...] = own[...]


def other_half(part, own):
    block = (own.shape[0] // 2, own.shape[1])
    return pl.pallas_call(
        half_copy_kernel,
        out_shape=pltpu.HBM(block, bf16),
        grid_spec=pltpu.PrefetchScalarGridSpec(
            num_scalar_prefetch=1,
            grid=(1,),
            in_specs=[pl.BlockSpec(block, lambda i, part: (1 - part[0], 0))],
            out_specs=fixed(block),
        ),
        compiler_params=params(8),
        cost_estimate=cost(0, own.size * 2),
    )(part, stay(own))


def scatter_vec_kernel(paired, pos, own, *refs):
    if paired:
        recv, *refs = refs
    target, buf, sem = refs[-3:]
    value = own[...]
    if paired:
        value = (value.astype(f32) + recv[...].astype(f32)).astype(bf16)
    buf[...] = value

    def body(n, carried):
        pltpu.make_async_copy(
            buf.at[n], target.at[pl.ds(pl.multiple_of(pos[n], 16), VEC_ROWS), :], sem
        ).start()
        return carried

    lax.fori_loop(0, own.shape[0], body, 0)
    pltpu.make_async_copy(buf, buf, sem).wait()


def scatter_vec(pos, own, recv, target):
    anywhere = pl.BlockSpec(memory_space=pl.ANY)
    block = fixed(own.shape)
    paired = recv is not None
    operands = [own] + ([recv] if paired else []) + [stay(target)]
    return pl.pallas_call(
        functools.partial(scatter_vec_kernel, paired),
        out_shape=pltpu.HBM(target.shape, bf16),
        grid_spec=pltpu.PrefetchScalarGridSpec(
            num_scalar_prefetch=1,
            grid=(1,),
            in_specs=[block] * (len(operands) - 1) + [anywhere],
            out_specs=anywhere,
            scratch_shapes=[pltpu.VMEM(own.shape, bf16), pltpu.SemaphoreType.DMA],
        ),
        input_output_aliases={len(operands): 0},
        compiler_params=params(4),
    )(pos, *operands)


def expand_kernel(present, half, patch_ref, class_ref, pinv_ref, out, total):
    for block in range(patch_ref.shape[0] // ROWS):
        rows = slice(block * ROWS, (block + 1) * ROWS)
        total[...] = jnp.zeros_like(total)
        for which in range(3):

            @pl.when(present[block, which] > 0)
            def _(which=which, rows=rows):
                chosen = jnp.where(class_ref[rows, :] == which, patch_ref[rows, :].astype(f32), 0.0)
                total[...] += dot_nt(chosen.astype(bf16), pinv_ref[which])

        out[rows, :] = total[...].astype(bf16)


def expand_call(which, present, half, patches, class_col, pinv):
    tokens = patches.shape[0]
    size = BASE_PIX // CHUNKS
    step = size
    return pl.pallas_call(
        expand_kernel,
        out_shape=jax.ShapeDtypeStruct((tokens, size), bf16),
        grid_spec=pltpu.PrefetchScalarGridSpec(
            num_scalar_prefetch=2,
            grid=(1,),
            in_specs=[
                fixed(patches.shape),
                fixed(class_col.shape),
                pl.BlockSpec(
                    (3, step, pinv.shape[2]),
                    lambda i, present, half: (0, (which + half[0] * (CHUNKS // 2)) % CHUNKS, 0),
                ),
            ],
            out_specs=pl.BlockSpec((tokens, step), lambda i, *_: (0, i)),
            scratch_shapes=[pltpu.VMEM((ROWS, step), f32)],
        ),
        compiler_params=params(),
        cost_estimate=cost(3 * tokens * size * D, tokens * size * 4 + size * D * 6),
    )(present, half, stay(patches), class_col, stay(pinv))


def resize_kernel(base, pinv_ref, out, turned):
    @pl.when(pl.program_id(0) == 0)
    def _():
        turned[...] = base[...].T

    out[0] = dot(turned[...], pinv_ref[0]).astype(bf16)


def resize_call(weights, pinv):
    return pl.pallas_call(
        resize_kernel,
        out_shape=jax.ShapeDtypeStruct((3, HALF, pinv.shape[2]), bf16),
        grid=(3,),
        in_specs=[
            fixed((BASE_PIX, HALF)),
            pl.BlockSpec((1, BASE_PIX, pinv.shape[2]), lambda i: (i, 0, 0)),
        ],
        out_specs=pl.BlockSpec((1, HALF, pinv.shape[2]), lambda i: (i, 0, 0)),
        scratch_shapes=[pltpu.VMEM((HALF, BASE_PIX), bf16)],
        compiler_params=params(),
        cost_estimate=cost(6 * D * BASE_PIX * HALF, 6 * D * BASE_PIX),
    )(stay(weights["base", 0]), stay(pinv))


def embed_back_kernel(core, token, base, own, recv, out, bias):
    low = (base[...] + (own[...].astype(f32) + recv[...].astype(f32))).astype(bf16)
    out[...] = low
    accumulate(bias, jnp.sum(low.astype(f32), axis=0, keepdims=True))


def embed_back_call(core, token, base, own, recv):
    tokens = base.shape[0]
    half = pl.BlockSpec((ROWS, HALF), lambda i, core: (i, core[0]))
    return pl.pallas_call(
        embed_back_kernel,
        out_shape=[
            jax.ShapeDtypeStruct((tokens, HALF), bf16),
            jax.ShapeDtypeStruct((1, HALF), f32),
        ],
        grid_spec=pltpu.PrefetchScalarGridSpec(
            num_scalar_prefetch=1,
            grid=(tokens // ROWS,),
            in_specs=[fixed(token.shape)] + [half] * 3,
            out_specs=[rows_spec(HALF), fixed((1, HALF))],
        ),
        compiler_params=params(8),
        cost_estimate=cost(tokens * D, tokens * D * 5),
    )(core, token, base, own, recv)


def pack_kernel(vec_per, *refs):
    *pieces, out = refs
    out[...] = jnp.zeros_like(out)
    at = 0
    for piece in pieces:
        for k in range(piece.shape[1] // BS):
            owner, row = divmod(at, vec_per // BS)
            out[owner, row : row + 1, :] = piece[:, k * BS : (k + 1) * BS]
            at += 1


def pack_call(pieces, owners, vec_per):
    if vec_per % BS:
        joined = jnp.concatenate(pieces, axis=1)[0]
        joined = jnp.pad(joined, (0, owners * vec_per - joined.shape[0])).reshape(owners, vec_per)
        joined = jnp.pad(joined, ((0, 0), (0, VEC_ROWS * BS - vec_per)))
        return joined.astype(bf16).reshape(owners, VEC_ROWS, BS)
    return pl.pallas_call(
        functools.partial(pack_kernel, vec_per),
        out_shape=jax.ShapeDtypeStruct((owners, VEC_ROWS, BS), f32),
        grid=(1,),
        in_specs=[fixed(p.shape) for p in pieces],
        out_specs=fixed((owners, VEC_ROWS, BS)),
        compiler_params=params(4),
        cost_estimate=cost(0, owners * vec_per * 8),
    )(*pieces).astype(bf16)


def embed_kernel(half, *refs):
    *parts, vec, weight, out = refs
    size = BASE_PIX // CHUNKS
    total = vec[:, :HALF]
    for c in range(CHUNKS):
        at = lax.rem(c + half[0] * (CHUNKS // 2), CHUNKS)
        rows = pl.ds(pl.multiple_of(at * size, size), size)
        total = total + dot(parts[c][...], weight[rows, :])
    out[...] = total.astype(bf16)


def embed_call(half, chunks, vec, weights):
    tokens = chunks[0].shape[0]
    return pl.pallas_call(
        embed_kernel,
        out_shape=jax.ShapeDtypeStruct((tokens, HALF), bf16),
        grid_spec=pltpu.PrefetchScalarGridSpec(
            num_scalar_prefetch=1,
            grid=(tokens // ROWS,),
            in_specs=[rows_spec(BASE_PIX // CHUNKS)] * CHUNKS
            + [fixed(vec.shape), fixed((BASE_PIX, HALF))],
            out_specs=rows_spec(HALF),
        ),
        compiler_params=params(),
        cost_estimate=cost(2 * tokens * BASE_PIX * HALF, tokens * BASE_PIX * 3),
    )(half, *[stay(c) for c in chunks], vec, stay(weights["base", 0]))


def qkv_kernel(layer, first, core, *refs):
    if first:
        own, recv, vec, weight, hid, normed, q_ref, k_ref, v_ref = refs
        mine, theirs = own[...].astype(f32), recv[...].astype(f32)
        low = core[0] == 0
        values = jnp.concatenate(
            [jnp.where(low, mine, theirs), jnp.where(low, theirs, mine)], axis=1
        )
    else:
        base, own, recv, vec, weight, hid, normed, q_ref, k_ref, v_ref = refs
        values = base[...] + (own[...].astype(f32) + recv[...].astype(f32))
    hid[...] = values
    unit, unused = norm_stats(values)
    low = (unit * vec_piece(vec, layer, "g1") + vec_piece(vec, layer, "s1")).astype(bf16)
    normed[...] = low
    made = dot(low, joined(weight, 0, D, 3))
    q_ref[...] = (made[:, :HALF] + vec_piece(vec, layer, "bq")).astype(bf16)
    k_ref[...] = made[:, HALF : 2 * HALF].astype(bf16)
    v_ref[...] = (made[:, 2 * HALF :] + vec_piece(vec, layer, "bv")).astype(bf16)


def qkv_call(layer, base, own, recv, core, vec, weights):
    tokens = own.shape[0]
    shape = lambda width, kind: jax.ShapeDtypeStruct((tokens, width), kind)
    outs = [shape(D, f32), pltpu.HBM((tokens, D), bf16)] + [shape(HALF, bf16)] * 3
    operands = ([] if base is None else [base]) + [own, recv]
    return pl.pallas_call(
        functools.partial(qkv_kernel, layer, base is None),
        out_shape=outs,
        grid_spec=pltpu.PrefetchScalarGridSpec(
            num_scalar_prefetch=1,
            grid=(tokens // ROWS,),
            in_specs=[rows_spec(o.shape[1]) for o in operands]
            + [fixed(vec.shape), fixed((3 * D, HALF))],
            out_specs=[rows_spec(o.shape[1]) for o in outs],
        ),
        compiler_params=params(),
        cost_estimate=cost(2 * tokens * D * 3 * HALF, tokens * D * 14),
    )(core, *operands, vec, weights["qkv", layer])


def head_masks():
    lane = lax.broadcasted_iota(jnp.int32, (1, 2 * HEAD_DIM), 1)
    low = (lane < HEAD_DIM).astype(f32).astype(bf16)
    high = (lane >= HEAD_DIM).astype(f32).astype(bf16)
    return low, high


def attend_kernel(
    layer, low_ref, high_ref, q_ref, k_ref, v_ref, seg_q, seg_k, vec, w_out, o_ref, lse_ref, part,
    scores_ref, top_ref, acc_ref,
):
    step = pl.program_id(0)
    first, last = low_ref[step], high_ref[step]
    masks = head_masks()
    scale = jnp.asarray(HEAD_DIM ** (-0.5), bf16)
    lane = lax.broadcasted_iota(jnp.int32, (1, BS), 1)
    sums = [(lane == HEAD_DIM).astype(f32).astype(bf16), (lane == 0).astype(f32).astype(bf16)]
    top_ref[...] = jnp.full(top_ref.shape, masked_score, f32)
    acc_ref[...] = jnp.zeros_like(acc_ref)
    seg_col = seg_q[...]

    def score_block(block, carried):
        rows = pl.ds(pl.multiple_of(block * ROWS, ROWS), ROWS)
        same = seg_col == seg_k[:, rows]
        for pair in range(HEADS // 2):
            cols = slice(pair * BS, (pair + 1) * BS)
            q_two = q_ref[:, cols] * scale
            k_two = k_ref[rows, cols]
            for side in range(2):
                head = 2 * pair + side
                scores = jnp.where(same, dot_nt(q_two * masks[side], k_two), masked_score)
                scores_ref[head, block] = scores
                top = top_ref[head]
                for piece in range(ROWS // BS):
                    top = jnp.maximum(top, scores[:, piece * BS : (piece + 1) * BS])
                top_ref[head] = top
        return carried

    lax.fori_loop(first, last, score_block, 0)
    tops = [jnp.max(top_ref[head], axis=1, keepdims=True) for head in range(HEADS)]

    def mix_block(block, carried):
        rows = pl.ds(pl.multiple_of(block * ROWS, ROWS), ROWS)
        for pair in range(HEADS // 2):
            v_two = v_ref[rows, pair * BS : (pair + 1) * BS]
            for side in range(2):
                head = 2 * pair + side
                expo = jnp.exp(scores_ref[head, block] - tops[head]).astype(bf16)
                acc_ref[head] += dot(expo, v_two * masks[side] + sums[side])
        return carried

    lax.fori_loop(first, last, mix_block, 0)
    totals = jnp.zeros((ROWS, BS), f32)
    for pair in range(HEADS // 2):
        sides = []
        for side in range(2):
            head = 2 * pair + side
            mixed = acc_ref[head]
            at = HEAD_DIM * (1 - side)
            total = mixed[:, at : at + 1]
            totals = jnp.where(lane == head, tops[head] + jnp.log(total), totals)
            sides.append(mixed * (1.0 / total))
        o_ref[:, pair * BS : (pair + 1) * BS] = jnp.where(lane < HEAD_DIM, *sides).astype(bf16)
    lse_ref[...] = totals.T[0:8, :]
    low = o_ref[...]
    bias = vec_piece(vec, layer, "bo")
    part[...] = (dot(low, joined(w_out, 0, HALF, TENSOR)) + bias).astype(bf16)


def attend_call(layer, first, last, queries, keys, values, seg_col, seg_row, vec, weights):
    tokens = queries.shape[0]
    return pl.pallas_call(
        functools.partial(attend_kernel, layer),
        out_shape=[
            jax.ShapeDtypeStruct((tokens, HALF), bf16),
            jax.ShapeDtypeStruct((8, tokens), f32),
            jax.ShapeDtypeStruct((tokens, D), bf16),
        ],
        grid_spec=pltpu.PrefetchScalarGridSpec(
            num_scalar_prefetch=2,
            grid=(tokens // ROWS,),
            in_specs=[
                rows_spec(HALF),
                fixed(keys.shape),
                fixed(values.shape),
                rows_spec(1),
                fixed(seg_row.shape),
                fixed(vec.shape),
                fixed((D, HALF)),
            ],
            out_specs=[
                rows_spec(HALF),
                pl.BlockSpec((8, ROWS), lambda i, *_: (0, i)),
                rows_spec(D),
            ],
            scratch_shapes=[
                pltpu.VMEM((HEADS, tokens // ROWS, ROWS, ROWS), f32),
                pltpu.VMEM((HEADS, ROWS, BS), f32),
                pltpu.VMEM((HEADS, ROWS, BS), f32),
            ],
        ),
        compiler_params=params(),
        cost_estimate=cost(8 * HEADS * tokens * tokens * BS, tokens * D * 8, HEADS * tokens * tokens),
    )(first, last, queries, keys, values, seg_col, seg_row, vec, weights["out", layer])


def gelu_parts(values):
    cdf = 0.5 * (1.0 + lax.erf(values * 0.7071067811865476))
    pdf = 0.3989422804014327 * jnp.exp(-0.5 * values * values)
    return values * cdf, cdf + values * pdf


def mlp_kernel(layer, base, own, recv, vec, w_up, w_down, hid, normed, act, slope, part):
    values = base[...] + (own[...].astype(f32) + recv[...].astype(f32))
    hid[...] = values
    unit, unused = norm_stats(values)
    low = (unit * vec_piece(vec, layer, "g2") + vec_piece(vec, layer, "s2")).astype(bf16)
    normed[...] = low
    bias_up = vec_piece(vec, layer, "b1")
    for pair in range(HALF_FF // D):
        area = slice(pair * D, (pair + 1) * D)
        up = dot(low, joined(w_up, pair * 2 * D, D, 2)) + bias_up[:, area]
        gelu, grad = gelu_parts(up)
        act[:, area] = gelu.astype(bf16)
        slope[:, area] = grad.astype(bf16)
    bias_down = vec_piece(vec, layer, "b2")
    part[...] = (dot(act[...], joined(w_down, 0, HALF_FF, TENSOR)) + bias_down).astype(bf16)


def mlp_call(layer, base, own, recv, vec, weights):
    tokens = base.shape[0]
    shape = lambda width, kind: jax.ShapeDtypeStruct((tokens, width), kind)
    kept = lambda width: pltpu.HBM((tokens, width), bf16)
    outs = [shape(D, f32), kept(D), kept(HALF_FF), kept(HALF_FF), shape(D, bf16)]
    return pl.pallas_call(
        functools.partial(mlp_kernel, layer),
        out_shape=outs,
        grid=(tokens // ROWS,),
        in_specs=[rows_spec(D)] * 3
        + [
            fixed(vec.shape),
            fixed((2 * HALF_FF, HALF)),
            fixed((2 * HALF_FF, HALF)),
        ],
        out_specs=[rows_spec(o.shape[1]) for o in outs],
        compiler_params=params(),
        cost_estimate=cost(4 * tokens * D * HALF_FF, tokens * D * 24, 2 * tokens * HALF_FF),
    )(base, own, recv, vec, weights["up", layer], weights["down", layer])


def mlp_back_kernel(layer, summed, *refs):
    if summed:
        base, own, recv, *refs = refs
        (hid, slope, vec, w_up, w_down, grad_full, grad_low, du_ref, back, dgain, dshift, db1, db2) = refs
        values = base[...].astype(f32) + (own[...].astype(f32) + recv[...].astype(f32))
        grad_full[...] = values
        low = values.astype(bf16)
    else:
        base, valid, *refs = refs
        (hid, slope, vec, w_up, w_down, grad_low, du_ref, back, dgain, dshift, db1, db2) = refs
        low = (base[...].astype(f32) * valid[...]).astype(bf16)
    grad_low[...] = low
    accumulate(db2, jnp.sum(low.astype(f32), axis=0, keepdims=True))
    for part in range(HALF_FF // D):
        area = slice(part * D, (part + 1) * D)
        rows = jnp.concatenate(
            [w_down[p * HALF_FF + part * D : p * HALF_FF + (part + 1) * D, :] for p in range(TENSOR)],
            axis=1,
        )
        du_ref[:, area] = (dot_nt(low, rows) * slope[:, area].astype(f32)).astype(bf16)
    grad_normed = dot_nt(du_ref[...], joined(w_up, 0, D, HALF_FF // HALF))
    accumulate(db1, jnp.sum(du_ref[...].astype(f32), axis=0, keepdims=True))
    part_back, gain_grad, shift_grad = norm_back(hid[...], vec_piece(vec, layer, "g2"), grad_normed)
    back[...] = part_back.astype(bf16)
    accumulate(dgain, gain_grad)
    accumulate(dshift, shift_grad)


def mlp_back_call(layer, base, own, recv, valid, hid, slope, vec, weights):
    tokens = base.shape[0]
    summed = own is not None
    shape = lambda width, kind: jax.ShapeDtypeStruct((tokens, width), kind)
    line = lambda width: jax.ShapeDtypeStruct((1, width), f32)
    outs = ([shape(D, f32)] if summed else []) + [shape(D, bf16), shape(HALF_FF, bf16), shape(D, bf16)]
    lines = [line(D), line(D), line(HALF_FF), line(D)]
    extra = [own, recv] if summed else [valid]
    return pl.pallas_call(
        functools.partial(mlp_back_kernel, layer, summed),
        out_shape=outs + lines,
        grid=(tokens // ROWS,),
        in_specs=[rows_spec(D)]
        + [rows_spec(e.shape[1]) for e in extra]
        + [
            rows_spec(D),
            rows_spec(HALF_FF),
            fixed(vec.shape),
            fixed((2 * HALF_FF, HALF)),
            fixed((2 * HALF_FF, HALF)),
        ],
        out_specs=[rows_spec(o.shape[1]) for o in outs] + [fixed(o.shape) for o in lines],
        compiler_params=params(),
        cost_estimate=cost(4 * tokens * D * HALF_FF, tokens * D * 24),
    )(base, *extra, stay(hid), stay(slope), vec, weights["up", layer], weights["down", layer])


def attend_back_kernel(
    low_ref, high_ref, base, own, recv, q_ref, k_ref, v_ref, o_ref, lse_ref, seg_k, seg_q, w_out,
    full_ref, grad_low, dq_ref, dk_ref, dv_ref, dbo, dk_acc, dv_acc, dq_acc, do_ref,
):
    step = pl.program_id(0)

    @pl.when(step == 0)
    def _():
        dk_acc[...] = jnp.zeros_like(dk_acc)
        dv_acc[...] = jnp.zeros_like(dv_acc)

    values = base[...].astype(f32) + (own[...].astype(f32) + recv[...].astype(f32))
    full_ref[...] = values
    low = values.astype(bf16)
    grad_low[...] = low
    accumulate(dbo, jnp.sum(low.astype(f32), axis=0, keepdims=True))
    do_ref[...] = dot_nt(low, joined(w_out, 0, HALF, TENSOR)).astype(bf16)
    product = do_ref[...].astype(f32) * o_ref[...].astype(f32)
    head = lax.broadcasted_iota(jnp.int32, (8, HALF), 0)
    lane = lax.broadcasted_iota(jnp.int32, (8, HALF), 1)
    pick = ((lane >= head * HEAD_DIM) & (lane < (head + 1) * HEAD_DIM)).astype(f32)
    high, rest = split(product)
    pick = pick.astype(bf16)
    inner = dot_nt(pick, high) + dot_nt(pick, rest)
    dq_acc[...] = jnp.zeros_like(dq_acc)
    masks = head_masks()
    scale = jnp.asarray(HEAD_DIM ** (-0.5), bf16)
    seg_row = seg_q[...]

    def one_block(block, carried):
        rows = pl.ds(pl.multiple_of(block * KEYS, KEYS), KEYS)
        same = seg_k[rows, :] == seg_row
        for pair in range(HEADS // 2):
            cols = slice(pair * BS, (pair + 1) * BS)
            q_two = q_ref[:, cols] * scale
            do_two = do_ref[:, cols]
            k_two = k_ref[rows, cols]
            v_two = v_ref[rows, cols]
            dv_two = dk_two = dq_two = None
            for side in range(2):
                at = 2 * pair + side
                q_one = q_two * masks[side]
                do_one = do_two * masks[side]
                scores = dot_nt(k_two, q_one)
                prob = jnp.where(same, jnp.exp(scores - lse_ref[at : at + 1, :]), 0.0)
                grad_prob = dot_nt(v_two, do_one)
                grad_scores = (prob * (grad_prob - inner[at : at + 1, :])).astype(bf16)
                dv_one = dot(prob.astype(bf16), do_one)
                dk_one = dot(grad_scores, q_one)
                dq_one = dot_tn(grad_scores, k_two * masks[side])
                dq_two = dq_one if dq_two is None else dq_two + dq_one
                dv_two = dv_one if dv_two is None else dv_two + dv_one
                dk_two = dk_one if dk_two is None else dk_two + dk_one
            dv_acc[rows, cols] += dv_two
            dk_acc[rows, cols] += dk_two
            dq_acc[:, cols] += dq_two
        return carried

    lax.fori_loop(low_ref[step], high_ref[step], one_block, 0)
    dq_ref[...] = (dq_acc[...] * HEAD_DIM ** (-0.5)).astype(bf16)

    @pl.when(step == pl.num_programs(0) - 1)
    def _():
        dk_ref[...] = dk_acc[...].astype(bf16)
        dv_ref[...] = dv_acc[...].astype(bf16)


def attend_back_call(
    layer, first, last, base, own, recv, queries, keys, values, mixed, lse, seg_col, seg_row, weights
):
    tokens = base.shape[0]
    shape = lambda width, kind: jax.ShapeDtypeStruct((tokens, width), kind)
    whole = (tokens, HALF)
    return pl.pallas_call(
        attend_back_kernel,
        out_shape=[
            shape(D, f32),
            shape(D, bf16),
            shape(HALF, bf16),
            shape(HALF, bf16),
            shape(HALF, bf16),
            jax.ShapeDtypeStruct((1, D), f32),
        ],
        grid_spec=pltpu.PrefetchScalarGridSpec(
            num_scalar_prefetch=2,
            grid=(tokens // ROWS,),
            in_specs=[
                rows_spec(D),
                rows_spec(D),
                rows_spec(D),
                rows_spec(HALF),
                fixed(whole),
                fixed(whole),
                rows_spec(HALF),
                pl.BlockSpec((8, ROWS), lambda i, *_: (0, i)),
                fixed(seg_col.shape),
                pl.BlockSpec((1, ROWS), lambda i, *_: (0, i)),
                fixed((D, HALF)),
            ],
            out_specs=[
                rows_spec(D),
                rows_spec(D),
                rows_spec(HALF),
                fixed(whole),
                fixed(whole),
                fixed((1, D)),
            ],
            scratch_shapes=[
                pltpu.VMEM(whole, f32),
                pltpu.VMEM(whole, f32),
                pltpu.VMEM((ROWS, HALF), f32),
                pltpu.VMEM((ROWS, HALF), bf16),
            ],
        ),
        compiler_params=params(),
        cost_estimate=cost(14 * HEADS * tokens * tokens * BS, tokens * D * 20, HEADS * tokens * tokens),
    )(
        first, last, base, own, recv, stay(queries), stay(keys), stay(values), stay(mixed), lse,
        seg_col, seg_row, weights["out", layer],
    )


def qkv_back_kernel(layer, dq, dk, dv, hid, vec, weight, back, dgain, dshift, dbq, dbv):
    grad_three = jnp.concatenate([dq[...], dk[...], dv[...]], axis=1)
    grad_normed = dot_nt(grad_three, joined(weight, 0, D, 3))
    part_back, gain_grad, shift_grad = norm_back(hid[...], vec_piece(vec, layer, "g1"), grad_normed)
    back[...] = part_back.astype(bf16)
    accumulate(dgain, gain_grad)
    accumulate(dshift, shift_grad)
    accumulate(dbq, jnp.sum(dq[...].astype(f32), axis=0, keepdims=True))
    accumulate(dbv, jnp.sum(dv[...].astype(f32), axis=0, keepdims=True))


def qkv_back_call(layer, dq, dk, dv, hid, vec, weights):
    tokens = dq.shape[0]
    line = lambda width: jax.ShapeDtypeStruct((1, width), f32)
    lines = [line(D), line(D), line(HALF), line(HALF)]
    return pl.pallas_call(
        functools.partial(qkv_back_kernel, layer),
        out_shape=[jax.ShapeDtypeStruct((tokens, D), bf16)] + lines,
        grid=(tokens // ROWS,),
        in_specs=[rows_spec(HALF)] * 3
        + [
            rows_spec(D),
            fixed(vec.shape),
            fixed((3 * D, HALF)),
        ],
        out_specs=[rows_spec(D)] + [fixed(o.shape) for o in lines],
        compiler_params=params(),
        cost_estimate=cost(2 * tokens * D * 3 * HALF, tokens * D * 10),
    )(dq, dk, dv, stay(hid), vec, weights["qkv", layer])


def split(values):
    high = values.astype(bf16)
    return high, (values - high.astype(f32)).astype(bf16)


def product(left, right, left_dim, right_dim):
    def one(a, b):
        return lax.dot_general(
            a, b, (((left_dim,), (right_dim,)), ((), ())), preferred_element_type=f32
        )

    return one(left[0], right[0]) + (one(left[0], right[1]) + one(left[1], right[0]))


def owner_kernel(per, used, home, near, far, master, left, right, moment, variance, grad, out, out_mom, out_var):
    here = range(per)
    first = pl.program_id(0) * per
    lefts = [split(left[i]) for i in here]
    rights = [split(right[i]) for i in here]
    rotated = []
    for i in here:
        rows = slice(i * BS, (i + 1) * BS)
        tile = jnp.where(home[0] > 0, near[rows, :].astype(f32), far[rows, :].astype(f32))
        tile = jnp.where(used[first + i] > 0, tile, 0.0)
        grad[i] = tile
        tile = tile.astype(bf16)
        rotated.append(split(dot_tn(lefts[i][0], tile) + dot_tn(lefts[i][1], tile)))
    rotated = [product(rotated[i], rights[i], 1, 0) for i in here]
    steps = []
    for i in here:
        new_moment = decay * moment[i] + (1.0 - decay) * rotated[i]
        new_variance = decay * variance[i] + (1.0 - decay) * rotated[i] * rotated[i]
        out_mom[i] = new_moment
        out_var[i] = new_variance
        steps.append(split(new_moment / (jnp.sqrt(new_variance) + adam_eps)))
    returned = [split(product(lefts[i], steps[i], 1, 0)) for i in here]
    returned = [product(returned[i], rights[i], 1, 1) for i in here]
    for i in here:
        out[i] = master[i] - matrix_rate * returned[i]


def owner_call(used, home, near, far, *arrays):
    count = arrays[0].shape[0]
    per = min(8, count)
    block = pl.BlockSpec((per, BS, BS), lambda i, *_: (i, 0, 0))
    return pl.pallas_call(
        functools.partial(owner_kernel, per),
        out_shape=[jax.ShapeDtypeStruct(arrays[0].shape, f32)] * 4,
        grid_spec=pltpu.PrefetchScalarGridSpec(
            num_scalar_prefetch=2,
            grid=(count // per,),
            in_specs=[pl.BlockSpec((per * BS, BS), lambda i, *_: (i, 0))] * 2 + [block] * 5,
            out_specs=[block] * 4,
        ),
        compiler_params=params(),
        cost_estimate=cost(count * 88 * BS**3, count * BS * BS * 38),
    )(used, home, stay(near), stay(far), *arrays)


def reduce_kernel(carrying, last, *refs):
    block, arrived, *refs = refs
    total = block[...].astype(f32) + arrived[...].astype(f32)
    if carrying:
        carried, *refs = refs
        total = total + carried[...].astype(f32)
    if last:
        [out] = refs
    else:
        following, out, later = refs
        later[...] = following[...]
    out[...] = total.astype(bf16)


def reduce_call(j, n, buffer, arrived, carried, payload):
    last = j >= 2
    at = lambda j, x_rel: pl.BlockSpec((payload, BS), lambda i: ((j * 2 + x_rel) * 2 + n, 0))
    whole = fixed((payload, BS))
    operands = [stay(buffer), stay(arrived)] + ([] if carried is None else [stay(carried)])
    specs = [at(j, 0)] + [whole] * (len(operands) - 1)
    if not last:
        operands.append(stay(buffer))
        specs.append(at(j + 2, 1))
    outs = [pltpu.HBM((payload, BS), bf16)] * (1 if last else 2)
    made = pl.pallas_call(
        functools.partial(reduce_kernel, carried is not None, last),
        out_shape=outs,
        grid=(1,),
        in_specs=specs,
        out_specs=[whole] * len(outs),
        compiler_params=params(8),
        cost_estimate=cost(payload * BS * 3, payload * BS * 12),
    )(*operands)
    return (made[0], None) if last else made


class Routes:
    def __init__(self, dp_n):
        pairs = [(d, t) for d in range(dp_n) for t in range(TENSOR)]
        at = lambda d, t: d * TENSOR + t
        home = [(d, t) for d, t in pairs if d % 2 == t]
        away = [(d, t) for d, t in pairs if d % 2 != t]
        self.core_all = [(at(d, t), at(d ^ 1, t)) for d, t in pairs]
        self.core_out = [(at(d, t), at(d ^ 1, t)) for d, t in home]
        self.core_in = [(at(d, t), at(d ^ 1, t)) for d, t in away]
        self.y_all = [(at(d, t), at(d, 1 - t)) for d, t in pairs]
        self.y_out = [(at(d, t), at(d, 1 - t)) for d, t in home]
        self.y_in = [(at(d, t), at(d, 1 - t)) for d, t in away]
        self.x_home = [(at(d, t), at(d ^ 2, t)) for d, t in home]
        self.x_away = [(at(d, t), at(d ^ 2, t)) for d, t in away]
        self.x_all = [(at(d, t), at(d ^ 2, t)) for d, t in pairs]
        self.z_all = [(at(d, t), at((d + 4) % dp_n, t)) for d, t in pairs]
        self.z_home = [(at(d, t), at((d + 4) % dp_n, t)) for d, t in home]


def send(value, route):
    return lax.ppermute(value, AXES, route)


def shards(
    patches,
    cotangent,
    image_size,
    block_slot,
    pinv,
    master_slots,
    left_basis,
    right_basis,
    mom_slots,
    var_slots,
    vec_master,
    vec_mom,
    vec_var,
):
    dp_n = lax.axis_size("dp")
    dp_pos = lax.axis_index("dp")
    y_pos = lax.axis_index("tensor")
    core = dp_pos % 2
    home = core == y_pos
    routes = Routes(dp_n)
    grid3 = dp_n == 16
    x_pos = (dp_pos // 2) % 2
    half_at = (x_pos if grid3 else x_pos * 0).astype(jnp.int32).reshape(1)
    tokens_n = patches.shape[0]
    slots_per = master_slots.shape[1]
    vec_per = vec_master.shape[1]
    slots_n = slots_per * dp_n
    payload = slots_per * BS + VEC_ROWS

    patches = jnp.where(home, patches, send(patches, routes.core_out))
    cotangent = jnp.where(home, cotangent, send(cotangent, routes.core_out))
    size_row = jnp.where(home, image_size, send(image_size, routes.core_out))[0]
    own_slots = block_slot[0]
    slot_other = send(block_slot, routes.y_all)

    lengths = jnp.where(
        size_row == 0, LEN_A, jnp.where(size_row == 1, LEN_B, jnp.where(size_row == 2, LEN_C, 0))
    )
    order = jnp.arange(IMG_DEV)
    ends_at = jnp.sum(jnp.where(order[None, :] <= order[:, None], lengths[None, :], 0), axis=1)
    places = jnp.arange(tokens_n)
    segment = jnp.sum((places[:, None] >= ends_at[None, :]).astype(jnp.int32), axis=1)
    in_image = segment[:, None] == order[None, :]
    select = jnp.stack(
        [jnp.any(in_image & (size_row == s)[None, :], axis=1) for s in range(3)], axis=1
    )
    valid_col = (segment < IMG_DEV).astype(f32)[:, None]
    seg_col = segment[:, None]
    seg_row = segment[None, :]
    blocks_n = tokens_n // ROWS
    starts = jnp.arange(blocks_n) * ROWS
    begun = ends_at[None, :] <= starts[:, None]
    first_tok = jnp.max(jnp.where(begun, ends_at[None, :], 0), axis=1)
    after = ends_at[None, :] > (starts + ROWS - 1)[:, None]
    last_tok = jnp.min(jnp.where(after, ends_at[None, :], tokens_n), axis=1)
    first_blk = (first_tok // ROWS).astype(jnp.int32)
    last_blk = ((last_tok + ROWS - 1) // ROWS).astype(jnp.int32)
    first_key = (first_tok // KEYS).astype(jnp.int32)
    last_key = ((last_tok + KEYS - 1) // KEYS).astype(jnp.int32)

    select_low = select.astype(bf16)
    class_col = jnp.sum(jnp.where(select, jnp.arange(1, 4)[None, :], 0), axis=1, keepdims=True) - 1
    present = jnp.any(select.reshape(blocks_n, ROWS, 3), axis=1).astype(jnp.int32)

    def expand(which, rows):
        return expand_call(which, present, half_at, rows, class_col, pinv)

    vec_low = jnp.pad(vec_master[0].astype(bf16), (0, VEC_ROWS * BS - vec_per))
    own_pack = jnp.concatenate(
        [
            master_slots[0].astype(bf16).reshape(slots_per * BS, BS),
            vec_low.reshape(VEC_ROWS, BS),
        ],
        axis=0,
    )
    flag = home.astype(jnp.int32).reshape(1)
    if grid3:
        z_pos = dp_pos // 4
        pack = own_pack
        chunks, first, second, owner = [], [], [], []
        middle_row = slots_per * BS // 2
        for j in range(4):
            beside_x, beside_y = send(pack, routes.x_all), send(pack, routes.y_all)
            further = [send(pack, routes.z_all)] if j < 3 else []
            work = [slot_other] if j == 0 else []
            beside_x, beside_y, patches, chunk, *more = fence(
                beside_x, beside_y, patches, expand(j, patches), *further, *work
            )
            chunks.append(chunk)
            if j < 3:
                further = more.pop(0)
            if j == 0:
                [slot_other] = more
            corner = jnp.concatenate(
                [send(beside_x[:middle_row], routes.y_all), send(beside_y[middle_row:], routes.x_all)],
                axis=0,
            )
            near_two = send(jnp.where(home, beside_y, pack), routes.core_all)
            far_two = send(jnp.where(home, corner, beside_x), routes.core_all)
            first += [pack, near_two, beside_x, far_two]
            second += [beside_y, near_two, corner, far_two]
            for x_rel in range(2):
                for n in range(2):
                    owner.append(((z_pos - j) % 4) * 4 + (x_pos ^ x_rel) * 2 + (core ^ n))
            if j < 3:
                pack = further
        first = [v[None] for v in first]
        second = [v[None] for v in second]
        owner = jnp.stack(owner).astype(jnp.int32)
    else:
        everything = lax.all_gather(own_pack, AXES, axis=0)
        everything = everything.reshape(dp_n, TENSOR, payload, BS)
        first = [jnp.where(core == 0, everything[:, 0], everything[:, 1])]
        second = []
        owner = jnp.arange(dp_n, dtype=jnp.int32)
        chunks = [expand(c, patches) for c in range(CHUNKS)]
    slot_list = jnp.where(home, block_slot, slot_other)[0]
    named = slot_list[None, :] == jnp.arange(slots_n)[:, None]
    used = jnp.any(named, axis=1)
    drow = jnp.where(used, jnp.sum(jnp.where(named, TARGET_ROW[None, :], 0), axis=1), -1)
    dcol = jnp.sum(jnp.where(named, TARGET_COL[None, :], 0), axis=1)
    weights, vec_rows = gather_tiles(first, second, owner, drow, dcol, flag, slots_per, dp_n)
    vec = vec_rows.reshape(dp_n, VEC_ROWS * BS)[:, :vec_per].astype(f32).reshape(1, dp_n * vec_per)

    embedded = embed_call(half_at, chunks, vec, weights)
    embedded_other = send(embedded, routes.core_all)
    core_flag = core.astype(jnp.int32).reshape(1)

    caches = []
    hidden, own, recv = None, embedded, embedded_other
    for layer in range(LAYERS):
        hidden, normed, queries, keys, values = qkv_call(
            layer, hidden, own, recv, core_flag, vec, weights
        )
        mixed, lse, part = attend_call(
            layer, first_blk, last_blk, queries, keys, values, seg_col, seg_row, vec, weights
        )
        other = send(part, routes.core_all)
        middle, normed2, act, slope, own = mlp_call(layer, hidden, part, other, vec, weights)
        recv = send(own, routes.core_all)
        caches.append((hidden, normed, queries, keys, values, mixed, lse, middle, normed2, act, slope))
        hidden = middle
    out_low = ((hidden + (own.astype(f32) + recv.astype(f32))) * valid_col).astype(bf16)

    owners = jnp.arange(dp_n)
    if grid3:
        place = (
            ((z_pos - 1 - owners // 4) % 4) * 4
            + (x_pos ^ ((owners // 2) % 2)) * 2
            + (core ^ (owners % 2))
        ).astype(jnp.int32)
    else:
        place = owners.astype(jnp.int32)
    slot_owner = slot_list // slots_per
    owner_place = jnp.sum(
        jnp.where(slot_owner[:, None] == owners[None, :], place[None, :], 0), axis=1
    )
    tile_pos = (owner_place * payload + (slot_list % slots_per) * BS).astype(jnp.int32)
    vec_pos = (place * payload + slots_per * BS).astype(jnp.int32)
    total_rows = dp_n * payload
    where_to = jnp.concatenate([half_at, flag if grid3 else flag * 0 + 1])
    offsets = {"base": 0}
    count = BASE_PIX // BS * (HALF // BS)
    for layer in range(LAYERS):
        for name, size in (("qkv", 3 * D * HALF), ("out", D * HALF), ("up", D * HALF_FF), ("down", D * HALF_FF)):
            offsets[name, layer] = count
            count += size // (BS * BS)

    def place_tiles(key, matrix, arrived, buffer):
        tiles = matrix.size // (BS * BS)
        pos = tile_pos[offsets[key] : offsets[key] + tiles]
        rows_n = matrix.shape[0] // 2 if matrix.shape[0] > HALF else HALF
        return scatter_matrix(pos, matrix, arrived, where_to, buffer, total_rows, rows_n)

    def place_base(rel, matrix, arrived, buffer):
        size = BASE_PIX * HALF // (BS * BS) // 2
        low_pos, high_pos = tile_pos[:size], tile_pos[size : 2 * size]
        pos = jnp.where(half_at[0] == rel, low_pos, high_pos)
        return scatter_matrix(pos, matrix, arrived, where_to, buffer, total_rows, D)

    def over(matrix):
        return send(matrix, routes.y_in) if grid3 else None

    def beside(matrix):
        return send(other_half(half_at, matrix), routes.x_away) if grid3 else None

    def summed(matrix, arrived):
        return half_sum(half_at, matrix, arrived) if grid3 else None

    def hold(*arrays):
        kept = [a for a in arrays if a is not None]
        done = iter(fence(*kept))
        return [None if a is None else next(done) for a in arrays]

    top, low = 1, 0
    vec_grads = [None] * LAYERS

    def mlp_step(layer, grad, own, recv):
        middle, normed2, act, slope = caches[layer][7:11]
        made = mlp_back_call(layer, grad, own, recv, valid_col, middle, slope, vec, weights)
        if own is not None:
            return made
        return [made[0]] + list(made)

    def attend_step(layer, grad, part, other, lse):
        hid_in, normed, queries, keys, values, mixed = caches[layer][:6]
        return attend_back_call(
            layer, first_key, last_key, grad, part, other, queries, keys, values, mixed, lse,
            seg_col, seg_row, weights,
        )

    grad, grad_low, du, part, dg2, ds2, db1, db2 = mlp_step(top, cotangent, None, None)
    other = send(part, routes.core_all)
    gd1 = dot_tn(caches[top][9], grad_low).astype(bf16)
    gu1 = dot_tn(caches[top][8], du).astype(bf16)
    ad1 = over(gd1)
    lse, gu1 = fence(caches[top][6], gu1)
    grad, grad_low, dq, dk, dv, dbo = attend_step(top, grad, part, other, lse)
    vec, dbo, ad1, gu1, out_low = hold(vec, dbo, ad1, gu1, out_low)
    au1 = over(gu1)
    own, dg1, ds1, dbq, dbv = qkv_back_call(top, dq, dk, dv, caches[top][0], vec, weights)
    recv = send(own, routes.core_all)
    go1 = dot_tn(caches[top][5], grad_low).astype(bf16)
    gq1 = dot_tn(caches[top][1], jnp.concatenate([dq, dk, dv], axis=1)).astype(bf16)
    vec_grads[top] = [dg1, ds1, dbq, dbv, dbo, dg2, ds2, db1, db2]
    grad, grad_low, du, part, dg2, ds2, db1, db2 = mlp_step(low, grad, own, recv)
    other = send(part, routes.core_all)
    db2, go1, gq1 = hold(db2, go1, gq1)
    xq1, ao1 = beside(gq1), over(go1)
    gd0 = dot_tn(caches[low][9], grad_low).astype(bf16)
    gu0 = dot_tn(caches[low][8], du).astype(bf16)
    lse, gd0, gu0, xq1, au1 = hold(caches[low][6], gd0, gu0, xq1, au1)
    hq1 = summed(gq1, xq1)
    ad0 = over(gd0)
    xu0 = beside(gu0)
    buffer = place_tiles(("down", top), gd1, ad1, None)
    buffer = place_tiles(("up", top), gu1, au1, buffer)
    grad, grad_low, dq, dk, dv, dbo = attend_step(low, grad, part, other, lse)
    vec, dbo, ad0, ao1, xu0, hq1, buffer = hold(vec, dbo, ad0, ao1, xu0, hq1, buffer)
    au0 = over(summed(gu0, xu0))
    aq1 = over(hq1)
    own, dg1, ds1, dbq, dbv = qkv_back_call(low, dq, dk, dv, caches[low][0], vec, weights)
    recv = send(own, routes.core_all)
    gq0 = dot_tn(caches[low][1], jnp.concatenate([dq, dk, dv], axis=1)).astype(bf16)
    vec_grads[low] = [dg1, ds1, dbq, dbv, dbo, dg2, ds2, db1, db2]
    xq0 = beside(gq0)
    turn, aq1 = hold(jnp.zeros((8, BS), f32), aq1)
    grad_emb, grad_emb_bias = embed_back_call(core_flag, turn, grad, own, recv)
    middle = CHUNKS // 2

    def base_grad(parts):
        return jnp.concatenate([dot_tn(c, grad_emb).astype(bf16) for c in parts], axis=0)

    gbt = base_grad(chunks[middle:])
    gbt, au0, xq0 = hold(gbt, au0, xq0)
    xb = send(gbt, routes.x_away) if grid3 else None
    aq0 = over(summed(gq0, xq0))
    gbm = base_grad(chunks[:middle])
    vec_grad = pack_call([grad_emb_bias] + vec_grads[0] + vec_grads[1], dp_n, vec_per)
    go0 = dot_tn(caches[low][5], grad_low).astype(bf16)
    ao0, av = over(go0), over(vec_grad)
    buffer = place_tiles(("out", top), go1, ao1, buffer)
    buffer = place_tiles(("qkv", top), gq1, aq1, buffer)
    buffer = place_tiles(("down", low), gd0, ad0, buffer)
    buffer = place_tiles(("up", low), gu0, au0, buffer)
    buffer = place_base(1, gbt, None, buffer)
    gbm, xb, aq0, ao0, av, buffer = hold(gbm, xb, aq0, ao0, av, buffer)
    ab = over(half_sum(half_at * 0, gbm, xb)) if grid3 else None
    buffer = place_tiles(("out", low), go0, ao0, buffer)
    buffer = scatter_vec(vec_pos, vec_grad, av, buffer)
    buffer = place_tiles(("qkv", low), gq0, aq0, buffer)
    base_weight = weights["base", 0]
    ab, buffer, base_weight, out_low = hold(ab, buffer, base_weight, out_low)
    weights["base", 0] = base_weight
    buffer = place_base(0, gbm, ab, buffer)

    if grid3:
        token = jnp.zeros((8, BS), f32)
        order = (1, 0)
        resized = resize_call(weights, pinv)
        carried = {n: None for n in order}
        blocks = buffer.reshape(4, 2, 2, payload, BS)
        across = {n: send(blocks[0, 1, n], routes.x_home) for n in order}
        following = {n: blocks[1, 1, n] for n in order}
        rounded = {}
        for j in range(4):
            for n in order:
                extra = None
                if j == 0 and n == order[0]:
                    extra = resized
                token, across[n], carried[n], extra = hold(token, across[n], carried[n], extra)
                if extra is not None:
                    resized = extra
                arrived = across[n]
                if j < 3:
                    across[n] = send(following[n], routes.x_home)
                total, following[n] = reduce_call(j, n, buffer, arrived, carried[n], payload)
                if j < 3:
                    carried[n] = send(total, routes.z_home)
                else:
                    rounded[n] = total
        near_grad, far_grad = rounded[0], send(rounded[1], routes.core_out)
    else:
        held = buffer.reshape(dp_n, 1, payload, BS).astype(f32)
        nothing = jnp.zeros_like(held)
        both = jnp.concatenate(
            [jnp.where(core == 0, held, nothing), jnp.where(core == 0, nothing, held)], axis=1
        )
        used_rows = jnp.repeat(used, BS).reshape(dp_n, 1, slots_per * BS, 1)
        used_rows = jnp.concatenate(
            [used_rows, jnp.ones((dp_n, 1, VEC_ROWS, 1), bool)], axis=2
        )
        both = jnp.where(used_rows, both, 0.0).reshape(dp_n * TENSOR * payload, BS)
        near_grad = lax.psum_scatter(both, AXES, scatter_dimension=0, tiled=True).astype(bf16)
        far_grad = near_grad
        resized = resize_call(weights, pinv)

    output = jnp.where(home, out_low, send(out_low, routes.y_out)).astype(f32)
    grad_pixels = sum(
        dot(grad_emb * select_low[:, s : s + 1], resized[s]) for s in range(3)
    ).astype(bf16)
    pixels_other = send(grad_pixels, routes.core_all)
    pixel_sides = [
        grad_pixels[:, s * HALF : (s + 1) * HALF].astype(f32)
        + pixels_other[:, s * HALF : (s + 1) * HALF].astype(f32)
        for s in range(TENSOR)
    ]
    near = jnp.where(core == 0, pixel_sides[0], pixel_sides[1])
    far = jnp.where(core == 0, pixel_sides[1], pixel_sides[0]).astype(bf16)
    patch_grad = jnp.where(home, near, send(far, routes.y_out).astype(f32))

    my_slots = dp_pos * slots_per + jnp.arange(slots_per)
    mine_used = jnp.any(own_slots[None, :] == my_slots[:, None], axis=1).astype(jnp.int32)
    owned_grad, new_master, new_mom, new_var = owner_call(
        mine_used, flag, near_grad, far_grad, master_slots[0], left_basis[0], right_basis[0], mom_slots[0], var_slots[0]
    )
    vec_rows = jnp.where(home, near_grad[slots_per * BS :], far_grad[slots_per * BS :])
    owned_vec_grad = vec_rows.astype(f32).reshape(VEC_ROWS * BS)[:vec_per]
    new_vec_mom = decay * vec_mom[0] + (1.0 - decay) * owned_vec_grad
    new_vec_var = decay * vec_var[0] + (1.0 - decay) * owned_vec_grad * owned_vec_grad
    new_vec = vec_master[0] - vector_rate * new_vec_mom / (jnp.sqrt(new_vec_var) + adam_eps)
    return (
        output,
        patch_grad,
        owned_grad[None],
        new_master[None],
        new_mom[None],
        new_var[None],
        owned_vec_grad[None],
        new_vec[None],
        new_vec_mom[None],
        new_vec_var[None],
    )


def solution(mesh):
    slots = P("tensor", "dp", None, None)
    vectors = P("tensor", "dp")
    tokens = P("dp", None)
    in_specs = (tokens, tokens, tokens, P("tensor", None), P()) + (slots,) * 5 + (vectors,) * 3
    out_specs = (tokens, P("dp", "tensor")) + (slots,) * 4 + (vectors,) * 4
    return jax.shard_map(shards, mesh=mesh, in_specs=in_specs, out_specs=out_specs, check_vma=False)
```

```python
import functools

import jax
import jax.numpy as jnp
import numpy as np
from jax import lax
from jax.experimental import pallas as pl
from jax.experimental.pallas import tpu as pltpu
from jax.sharding import PartitionSpec as P

D = 768
HEAD_DIM = 64
FF = 3072
BASE_PIX = 3072
LAYERS = 2
LEN_A = 196
LEN_B = 225
LEN_C = 576
IMG_DEV = 5
BS = 128
TENSOR = 2
HALF = D // TENSOR
HALF_FF = FF // TENSOR
HEADS = HALF // HEAD_DIM
ROWS = 256
KEYS = 512
VEC_ROWS = 16
CHUNKS = 4

AXES = ("dp", "tensor")
precise = lax.Precision.HIGHEST
masked_score = -1e30
norm_eps = 1e-06
adam_eps = 1e-08
decay = 0.5
matrix_rate = 0.05
vector_rate = 0.3
f32 = jnp.float32
bf16 = jnp.bfloat16
MIB = 1024 * 1024

WEIGHTS = [("base", 0, BASE_PIX)]
for layer in range(LAYERS):
    WEIGHTS += [("qkv", layer, 3 * D), ("out", layer, D), ("up", layer, FF), ("down", layer, FF)]
STARTS = {}
PANEL_ROWS = 0
for name, layer, size in WEIGHTS:
    STARTS[name, layer] = PANEL_ROWS
    PANEL_ROWS += size


def tile_targets():
    rows, cols = [], []

    def add(start, rows_n, cols_n):
        for i in range(rows_n // BS):
            for j in range(cols_n // BS):
                panel, inner = divmod(j * BS, HALF)
                rows.append(start + panel * rows_n + i * BS)
                cols.append(inner)

    add(STARTS["base", 0], BASE_PIX, HALF)
    for layer in range(LAYERS):
        add(STARTS["qkv", layer], D, 3 * HALF)
        add(STARTS["out", layer], HALF, D)
        add(STARTS["up", layer], D, HALF_FF)
        add(STARTS["down", layer], HALF_FF, D)
    return np.array(rows, np.int32), np.array(cols, np.int32)


TARGET_ROW, TARGET_COL = tile_targets()
LAYER_VECS = (D, D, HALF, HALF, D, D, D, HALF_FF, D)
VEC_NAMES = ("g1", "s1", "bq", "bv", "bo", "g2", "s2", "b1", "b2")


def vec_offsets():
    offset = HALF
    found = []
    for layer in range(LAYERS):
        here = {}
        for name, length in zip(VEC_NAMES, LAYER_VECS):
            here[name] = (offset, length)
            offset += length
        found.append(here)
    return found


VEC_AT = vec_offsets()


def params(limit=24):
    return pltpu.CompilerParams(
        dimension_semantics=("arbitrary",), vmem_limit_bytes=limit * MIB
    )


def cost(flops, nbytes, trans=0):
    return pl.CostEstimate(flops=flops, bytes_accessed=nbytes, transcendentals=trans)


def rows_spec(width):
    return pl.BlockSpec((ROWS, width), lambda i, *_: (i, 0))


def fixed(shape, at=0):
    return pl.BlockSpec(shape, lambda i, *_: (at,) + (0,) * (len(shape) - 1))


def vec_piece(vec_ref, layer, name):
    start, length = VEC_AT[layer][name]
    return vec_ref[:, start : start + length]


def dot(left, right):
    return jnp.dot(left, right, preferred_element_type=f32)


def dot_nt(left, right, precision=None):
    return lax.dot_general(
        left, right, (((1,), (1,)), ((), ())), precision=precision, preferred_element_type=f32
    )


def dot_tn(left, right):
    return lax.dot_general(left, right, (((0,), (0,)), ((), ())), preferred_element_type=f32)


def joined(ref, start, rows_n, panels):
    return jnp.concatenate(
        [ref[start + p * rows_n : start + (p + 1) * rows_n, :] for p in range(panels)], axis=1
    )


def norm_stats(values):
    mean_val = jnp.mean(values, axis=-1, keepdims=True)
    centered = values - mean_val
    inv_std = lax.rsqrt(jnp.mean(centered * centered, axis=-1, keepdims=True) + norm_eps)
    return centered * inv_std, inv_std


def norm_back(values, gain, grad):
    unit, inv_std = norm_stats(values)
    scaled = grad * gain
    mean_s = jnp.mean(scaled, axis=-1, keepdims=True)
    mean_u = jnp.mean(scaled * unit, axis=-1, keepdims=True)
    back = inv_std * (scaled - mean_s - unit * mean_u)
    return (
        back,
        jnp.sum(grad * unit, axis=0, keepdims=True),
        jnp.sum(grad, axis=0, keepdims=True),
    )


def accumulate(ref, value):
    first = pl.program_id(0) == 0

    @pl.when(first)
    def _():
        ref[...] = value

    @pl.when(jnp.logical_not(first))
    def _():
        ref[...] += value


def stay(value):
    return pltpu.with_memory_space_constraint(value, pltpu.HBM)


def fence(*arrays):
    def nothing(*refs):
        pass

    anywhere = pl.BlockSpec(memory_space=pl.ANY)
    return pl.pallas_call(
        nothing,
        out_shape=[jax.ShapeDtypeStruct(a.shape, a.dtype) for a in arrays],
        in_specs=[anywhere] * len(arrays),
        out_specs=[anywhere] * len(arrays),
        input_output_aliases={i: i for i in range(len(arrays))},
        compiler_params=pltpu.CompilerParams(vmem_limit_bytes=MIB),
    )(*[stay(a) if a.size > 32 * 1024 else a for a in arrays])


def gather_kernel(slots, count_a, count_b, owner, drow, dcol, flag, *refs):
    first = refs[:count_a]
    second = refs[count_a : count_a + count_b]
    *panels, vectors, held, sem, vec_sem = refs[count_a + count_b :]

    def copy_all(sources):
        at = 0
        for src in sources:
            for n in range(src.shape[0]):
                who = owner[at]
                at += 1

                def body(i, carried, src=src, n=n, who=who):
                    slot = who * slots + i
                    row = drow[slot]

                    @pl.when(row >= 0)
                    def _():
                        start = pl.multiple_of(i * BS, BS)
                        pltpu.make_async_copy(
                            src.at[n, pl.ds(start, BS), :],
                            held.at[
                                pl.ds(pl.multiple_of(row, BS), BS),
                                pl.ds(pl.multiple_of(dcol[slot], BS), BS),
                            ],
                            sem,
                        ).start()

                    return carried

                lax.fori_loop(0, slots, body, 0)
                pltpu.make_async_copy(
                    src.at[n, pl.ds(slots * BS, VEC_ROWS), :], vectors.at[who], vec_sem
                ).start()

    if count_b:

        @pl.when(flag[0] == 1)
        def _():
            copy_all(first)

        @pl.when(flag[0] == 0)
        def _():
            copy_all(second)
    else:
        copy_all(first)
    pltpu.make_async_copy(held, held, sem).wait()
    at = 0
    for panel in panels:
        size = panel.shape[0]
        pltpu.make_async_copy(held.at[pl.ds(at, size), :], panel, sem).start()
        at += size
    pltpu.make_async_copy(vectors, vectors, vec_sem).wait()
    pltpu.make_async_copy(held, held, sem).wait()


def gather_tiles(first, second, owner, drow, dcol, flag, slots, owners):
    anywhere = pl.BlockSpec(memory_space=pl.ANY)
    *panels, vectors = pl.pallas_call(
        functools.partial(gather_kernel, slots, len(first), len(second)),
        out_shape=[pltpu.HBM((size, HALF), bf16) for unused, unused2, size in WEIGHTS]
        + [jax.ShapeDtypeStruct((owners, VEC_ROWS, BS), bf16)],
        grid_spec=pltpu.PrefetchScalarGridSpec(
            num_scalar_prefetch=4,
            grid=(1,),
            in_specs=[anywhere] * (len(first) + len(second)),
            out_specs=[anywhere] * len(WEIGHTS) + [fixed((owners, VEC_ROWS, BS))],
            scratch_shapes=[
                pltpu.VMEM((PANEL_ROWS, HALF), bf16),
                pltpu.SemaphoreType.DMA,
                pltpu.SemaphoreType.DMA,
            ],
        ),
        compiler_params=params(),
        cost_estimate=cost(0, 4 * PANEL_ROWS * HALF),
    )(owner, drow, dcol, flag, *[stay(v) for v in first], *[stay(v) for v in second])
    return {(name, layer): p for (name, layer, unused), p in zip(WEIGHTS, panels)}, vectors


def scatter_kernel(rows_n, cols_n, steps, paired, parts, pos, part, own, *refs):
    @pl.when(part[1] > 0)
    def _():
        scatter_body(rows_n, cols_n, steps, paired, parts, pos, part, own, *refs)


def scatter_body(rows_n, cols_n, steps, paired, parts, pos, part, own, *refs):
    if paired:
        recv, *refs = refs
        span = pl.num_programs(0) // parts
        here = jnp.logical_or(parts == 1, pl.program_id(0) // span == part[0])
    target, buf, sems = refs[-3:]
    step = pl.program_id(0)
    slot = lax.rem(step, 2)
    per = rows_n // BS * (cols_n // BS)

    def wait(at):
        pltpu.make_async_copy(buf.at[at], buf.at[at], sems.at[at]).wait()

    @pl.when(step >= 2)
    def _():
        wait(slot)

    for i in range(rows_n // BS):
        for j in range(cols_n // BS):
            area = (slice(i * BS, (i + 1) * BS), slice(j * BS, (j + 1) * BS))
            value = own[area]
            if paired:
                more = jnp.where(here, recv[area].astype(f32), 0.0)
                value = (value.astype(f32) + more).astype(bf16)
            buf[slot, i * (cols_n // BS) + j] = value
    for n in range(per):
        pltpu.make_async_copy(
            buf.at[slot, n],
            target.at[pl.ds(pl.multiple_of(pos[step * per + n], 16), BS), :],
            sems.at[slot],
        ).start()

    @pl.when(step == pl.num_programs(0) - 1)
    def _():
        if steps > 1:
            wait(1 - slot)
        wait(slot)


def scatter_matrix(pos, own, recv, part, target, total_rows, rows_n):
    cols_n = own.shape[1]
    steps = own.shape[0] // rows_n
    anywhere = pl.BlockSpec(memory_space=pl.ANY)
    block = pl.BlockSpec((rows_n, cols_n), lambda i, *_: (i, 0))
    paired = recv is not None
    parts = own.shape[0] // recv.shape[0] if paired else 1
    span = steps // parts
    arrived = pl.BlockSpec(
        (rows_n, cols_n), lambda i, pos, part: (jnp.clip(i - part[0] * span, 0, span - 1), 0)
    )
    operands = [stay(own)] + ([stay(recv)] if paired else []) + ([] if target is None else [stay(target)])
    specs = [block] + ([block if parts == 1 else arrived] if paired else [])
    specs += [] if target is None else [anywhere]
    return pl.pallas_call(
        functools.partial(scatter_kernel, rows_n, cols_n, steps, paired, parts),
        out_shape=pltpu.HBM((total_rows, BS), bf16),
        grid_spec=pltpu.PrefetchScalarGridSpec(
            num_scalar_prefetch=2,
            grid=(steps,),
            in_specs=specs,
            out_specs=anywhere,
            scratch_shapes=[
                pltpu.VMEM((2, rows_n // BS * (cols_n // BS), BS, BS), bf16),
                pltpu.SemaphoreType.DMA((2,)),
            ],
        ),
        input_output_aliases={} if target is None else {len(operands) + 1: 0},
        compiler_params=params(12),
        cost_estimate=cost(own.size, own.size * 6),
    )(pos, part, *operands)


def half_sum_kernel(part, own, arrived, out):
    out[...] = (own[...].astype(f32) + arrived[...].astype(f32)).astype(bf16)


def half_sum(part, own, arrived):
    block = arrived.shape
    return pl.pallas_call(
        half_sum_kernel,
        out_shape=pltpu.HBM(block, bf16),
        grid_spec=pltpu.PrefetchScalarGridSpec(
            num_scalar_prefetch=1,
            grid=(1,),
            in_specs=[pl.BlockSpec(block, lambda i, part: (part[0], 0)), fixed(block)],
            out_specs=fixed(block),
        ),
        compiler_params=params(8),
        cost_estimate=cost(arrived.size, arrived.size * 6),
    )(part, stay(own), stay(arrived))


def half_copy_kernel(part, own, out):
    out[...] = own[...]


def other_half(part, own):
    block = (own.shape[0] // 2, own.shape[1])
    return pl.pallas_call(
        half_copy_kernel,
        out_shape=pltpu.HBM(block, bf16),
        grid_spec=pltpu.PrefetchScalarGridSpec(
            num_scalar_prefetch=1,
            grid=(1,),
            in_specs=[pl.BlockSpec(block, lambda i, part: (1 - part[0], 0))],
            out_specs=fixed(block),
        ),
        compiler_params=params(8),
        cost_estimate=cost(0, own.size * 2),
    )(part, stay(own))


def scatter_vec_kernel(paired, pos, own, *refs):
    if paired:
        recv, *refs = refs
    target, buf, sem = refs[-3:]
    value = own[...]
    if paired:
        value = (value.astype(f32) + recv[...].astype(f32)).astype(bf16)
    buf[...] = value

    def body(n, carried):
        pltpu.make_async_copy(
            buf.at[n], target.at[pl.ds(pl.multiple_of(pos[n], 16), VEC_ROWS), :], sem
        ).start()
        return carried

    lax.fori_loop(0, own.shape[0], body, 0)
    pltpu.make_async_copy(buf, buf, sem).wait()


def scatter_vec(pos, own, recv, target):
    anywhere = pl.BlockSpec(memory_space=pl.ANY)
    block = fixed(own.shape)
    paired = recv is not None
    operands = [own] + ([recv] if paired else []) + [stay(target)]
    return pl.pallas_call(
        functools.partial(scatter_vec_kernel, paired),
        out_shape=pltpu.HBM(target.shape, bf16),
        grid_spec=pltpu.PrefetchScalarGridSpec(
            num_scalar_prefetch=1,
            grid=(1,),
            in_specs=[block] * (len(operands) - 1) + [anywhere],
            out_specs=anywhere,
            scratch_shapes=[pltpu.VMEM(own.shape, bf16), pltpu.SemaphoreType.DMA],
        ),
        input_output_aliases={len(operands): 0},
        compiler_params=params(4),
    )(pos, *operands)


def expand_kernel(present, half, patch_ref, class_ref, pinv_ref, out, total):
    for block in range(patch_ref.shape[0] // ROWS):
        rows = slice(block * ROWS, (block + 1) * ROWS)
        total[...] = jnp.zeros_like(total)
        for which in range(3):

            @pl.when(present[block, which] > 0)
            def _(which=which, rows=rows):
                chosen = jnp.where(class_ref[rows, :] == which, patch_ref[rows, :].astype(f32), 0.0)
                total[...] += dot_nt(chosen.astype(bf16), pinv_ref[which])

        out[rows, :] = total[...].astype(bf16)


def expand_call(which, present, half, patches, class_col, pinv):
    tokens = patches.shape[0]
    size = BASE_PIX // CHUNKS
    step = size
    return pl.pallas_call(
        expand_kernel,
        out_shape=jax.ShapeDtypeStruct((tokens, size), bf16),
        grid_spec=pltpu.PrefetchScalarGridSpec(
            num_scalar_prefetch=2,
            grid=(1,),
            in_specs=[
                fixed(patches.shape),
                fixed(class_col.shape),
                pl.BlockSpec(
                    (3, step, pinv.shape[2]),
                    lambda i, present, half: (0, (which + half[0] * (CHUNKS // 2)) % CHUNKS, 0),
                ),
            ],
            out_specs=pl.BlockSpec((tokens, step), lambda i, *_: (0, i)),
            scratch_shapes=[pltpu.VMEM((ROWS, step), f32)],
        ),
        compiler_params=params(),
        cost_estimate=cost(3 * tokens * size * D, tokens * size * 4 + size * D * 6),
    )(present, half, stay(patches), class_col, stay(pinv))


def resize_kernel(base, pinv_ref, out, turned):
    @pl.when(pl.program_id(0) == 0)
    def _():
        turned[...] = base[...].T

    out[0] = dot(turned[...], pinv_ref[0]).astype(bf16)


def resize_call(weights, pinv):
    return pl.pallas_call(
        resize_kernel,
        out_shape=jax.ShapeDtypeStruct((3, HALF, pinv.shape[2]), bf16),
        grid=(3,),
        in_specs=[
            fixed((BASE_PIX, HALF)),
            pl.BlockSpec((1, BASE_PIX, pinv.shape[2]), lambda i: (i, 0, 0)),
        ],
        out_specs=pl.BlockSpec((1, HALF, pinv.shape[2]), lambda i: (i, 0, 0)),
        scratch_shapes=[pltpu.VMEM((HALF, BASE_PIX), bf16)],
        compiler_params=params(),
        cost_estimate=cost(6 * D * BASE_PIX * HALF, 6 * D * BASE_PIX),
    )(stay(weights["base", 0]), stay(pinv))


def embed_back_kernel(core, token, base, own, recv, out, bias):
    low = (base[...] + (own[...].astype(f32) + recv[...].astype(f32))).astype(bf16)
    out[...] = low
    accumulate(bias, jnp.sum(low.astype(f32), axis=0, keepdims=True))


def embed_back_call(core, token, base, own, recv):
    tokens = base.shape[0]
    half = pl.BlockSpec((ROWS, HALF), lambda i, core: (i, core[0]))
    return pl.pallas_call(
        embed_back_kernel,
        out_shape=[
            jax.ShapeDtypeStruct((tokens, HALF), bf16),
            jax.ShapeDtypeStruct((1, HALF), f32),
        ],
        grid_spec=pltpu.PrefetchScalarGridSpec(
            num_scalar_prefetch=1,
            grid=(tokens // ROWS,),
            in_specs=[fixed(token.shape)] + [half] * 3,
            out_specs=[rows_spec(HALF), fixed((1, HALF))],
        ),
        compiler_params=params(8),
        cost_estimate=cost(tokens * D, tokens * D * 5),
    )(core, token, base, own, recv)


def pack_kernel(vec_per, *refs):
    *pieces, out = refs
    out[...] = jnp.zeros_like(out)
    at = 0
    for piece in pieces:
        for k in range(piece.shape[1] // BS):
            owner, row = divmod(at, vec_per // BS)
            out[owner, row : row + 1, :] = piece[:, k * BS : (k + 1) * BS]
            at += 1


def pack_call(pieces, owners, vec_per):
    if vec_per % BS:
        joined = jnp.concatenate(pieces, axis=1)[0]
        joined = jnp.pad(joined, (0, owners * vec_per - joined.shape[0])).reshape(owners, vec_per)
        joined = jnp.pad(joined, ((0, 0), (0, VEC_ROWS * BS - vec_per)))
        return joined.astype(bf16).reshape(owners, VEC_ROWS, BS)
    return pl.pallas_call(
        functools.partial(pack_kernel, vec_per),
        out_shape=jax.ShapeDtypeStruct((owners, VEC_ROWS, BS), f32),
        grid=(1,),
        in_specs=[fixed(p.shape) for p in pieces],
        out_specs=fixed((owners, VEC_ROWS, BS)),
        compiler_params=params(4),
        cost_estimate=cost(0, owners * vec_per * 8),
    )(*pieces).astype(bf16)


def embed_kernel(half, *refs):
    *parts, vec, weight, out = refs
    size = BASE_PIX // CHUNKS
    total = vec[:, :HALF]
    for c in range(CHUNKS):
        at = lax.rem(c + half[0] * (CHUNKS // 2), CHUNKS)
        rows = pl.ds(pl.multiple_of(at * size, size), size)
        total = total + dot(parts[c][...], weight[rows, :])
    out[...] = total.astype(bf16)


def embed_call(half, chunks, vec, weights):
    tokens = chunks[0].shape[0]
    return pl.pallas_call(
        embed_kernel,
        out_shape=jax.ShapeDtypeStruct((tokens, HALF), bf16),
        grid_spec=pltpu.PrefetchScalarGridSpec(
            num_scalar_prefetch=1,
            grid=(tokens // ROWS,),
            in_specs=[rows_spec(BASE_PIX // CHUNKS)] * CHUNKS
            + [fixed(vec.shape), fixed((BASE_PIX, HALF))],
            out_specs=rows_spec(HALF),
        ),
        compiler_params=params(),
        cost_estimate=cost(2 * tokens * BASE_PIX * HALF, tokens * BASE_PIX * 3),
    )(half, *[stay(c) for c in chunks], vec, stay(weights["base", 0]))


def qkv_kernel(layer, first, core, *refs):
    if first:
        own, recv, vec, weight, hid, normed, q_ref, k_ref, v_ref = refs
        mine, theirs = own[...].astype(f32), recv[...].astype(f32)
        low = core[0] == 0
        values = jnp.concatenate(
            [jnp.where(low, mine, theirs), jnp.where(low, theirs, mine)], axis=1
        )
    else:
        base, own, recv, vec, weight, hid, normed, q_ref, k_ref, v_ref = refs
        values = base[...] + (own[...].astype(f32) + recv[...].astype(f32))
    hid[...] = values
    unit, unused = norm_stats(values)
    low = (unit * vec_piece(vec, layer, "g1") + vec_piece(vec, layer, "s1")).astype(bf16)
    normed[...] = low
    made = dot(low, joined(weight, 0, D, 3))
    q_ref[...] = (made[:, :HALF] + vec_piece(vec, layer, "bq")).astype(bf16)
    k_ref[...] = made[:, HALF : 2 * HALF].astype(bf16)
    v_ref[...] = (made[:, 2 * HALF :] + vec_piece(vec, layer, "bv")).astype(bf16)


def qkv_call(layer, base, own, recv, core, vec, weights):
    tokens = own.shape[0]
    shape = lambda width, kind: jax.ShapeDtypeStruct((tokens, width), kind)
    outs = [shape(D, f32), pltpu.HBM((tokens, D), bf16)] + [shape(HALF, bf16)] * 3
    operands = ([] if base is None else [base]) + [own, recv]
    return pl.pallas_call(
        functools.partial(qkv_kernel, layer, base is None),
        out_shape=outs,
        grid_spec=pltpu.PrefetchScalarGridSpec(
            num_scalar_prefetch=1,
            grid=(tokens // ROWS,),
            in_specs=[rows_spec(o.shape[1]) for o in operands]
            + [fixed(vec.shape), fixed((3 * D, HALF))],
            out_specs=[rows_spec(o.shape[1]) for o in outs],
        ),
        compiler_params=params(),
        cost_estimate=cost(2 * tokens * D * 3 * HALF, tokens * D * 14),
    )(core, *operands, vec, weights["qkv", layer])


def head_masks():
    lane = lax.broadcasted_iota(jnp.int32, (1, 2 * HEAD_DIM), 1)
    low = (lane < HEAD_DIM).astype(f32).astype(bf16)
    high = (lane >= HEAD_DIM).astype(f32).astype(bf16)
    return low, high


def attend_kernel(
    layer, low_ref, high_ref, q_ref, k_ref, v_ref, seg_q, seg_k, vec, w_out, o_ref, lse_ref, part,
    scores_ref, top_ref, acc_ref,
):
    step = pl.program_id(0)
    first, last = low_ref[step], high_ref[step]
    masks = head_masks()
    scale = jnp.asarray(HEAD_DIM ** (-0.5), bf16)
    lane = lax.broadcasted_iota(jnp.int32, (1, BS), 1)
    sums = [(lane == HEAD_DIM).astype(f32).astype(bf16), (lane == 0).astype(f32).astype(bf16)]
    top_ref[...] = jnp.full(top_ref.shape, masked_score, f32)
    acc_ref[...] = jnp.zeros_like(acc_ref)
    seg_col = seg_q[...]

    def score_block(block, carried):
        rows = pl.ds(pl.multiple_of(block * ROWS, ROWS), ROWS)
        same = seg_col == seg_k[:, rows]
        for pair in range(HEADS // 2):
            cols = slice(pair * BS, (pair + 1) * BS)
            q_two = q_ref[:, cols] * scale
            k_two = k_ref[rows, cols]
            for side in range(2):
                head = 2 * pair + side
                scores = jnp.where(same, dot_nt(q_two * masks[side], k_two), masked_score)
                scores_ref[head, block] = scores
                top = top_ref[head]
                for piece in range(ROWS // BS):
                    top = jnp.maximum(top, scores[:, piece * BS : (piece + 1) * BS])
                top_ref[head] = top
        return carried

    lax.fori_loop(first, last, score_block, 0)
    tops = [jnp.max(top_ref[head], axis=1, keepdims=True) for head in range(HEADS)]

    def mix_block(block, carried):
        rows = pl.ds(pl.multiple_of(block * ROWS, ROWS), ROWS)
        for pair in range(HEADS // 2):
            v_two = v_ref[rows, pair * BS : (pair + 1) * BS]
            for side in range(2):
                head = 2 * pair + side
                expo = jnp.exp(scores_ref[head, block] - tops[head]).astype(bf16)
                acc_ref[head] += dot(expo, v_two * masks[side] + sums[side])
        return carried

    lax.fori_loop(first, last, mix_block, 0)
    totals = jnp.zeros((ROWS, BS), f32)
    for pair in range(HEADS // 2):
        sides = []
        for side in range(2):
            head = 2 * pair + side
            mixed = acc_ref[head]
            at = HEAD_DIM * (1 - side)
            total = mixed[:, at : at + 1]
            totals = jnp.where(lane == head, tops[head] + jnp.log(total), totals)
            sides.append(mixed * (1.0 / total))
        o_ref[:, pair * BS : (pair + 1) * BS] = jnp.where(lane < HEAD_DIM, *sides).astype(bf16)
    lse_ref[...] = totals.T[0:8, :]
    low = o_ref[...]
    bias = vec_piece(vec, layer, "bo")
    part[...] = (dot(low, joined(w_out, 0, HALF, TENSOR)) + bias).astype(bf16)


def attend_call(layer, first, last, queries, keys, values, seg_col, seg_row, vec, weights):
    tokens = queries.shape[0]
    return pl.pallas_call(
        functools.partial(attend_kernel, layer),
        out_shape=[
            jax.ShapeDtypeStruct((tokens, HALF), bf16),
            jax.ShapeDtypeStruct((8, tokens), f32),
            jax.ShapeDtypeStruct((tokens, D), bf16),
        ],
        grid_spec=pltpu.PrefetchScalarGridSpec(
            num_scalar_prefetch=2,
            grid=(tokens // ROWS,),
            in_specs=[
                rows_spec(HALF),
                fixed(keys.shape),
                fixed(values.shape),
                rows_spec(1),
                fixed(seg_row.shape),
                fixed(vec.shape),
                fixed((D, HALF)),
            ],
            out_specs=[
                rows_spec(HALF),
                pl.BlockSpec((8, ROWS), lambda i, *_: (0, i)),
                rows_spec(D),
            ],
            scratch_shapes=[
                pltpu.VMEM((HEADS, tokens // ROWS, ROWS, ROWS), f32),
                pltpu.VMEM((HEADS, ROWS, BS), f32),
                pltpu.VMEM((HEADS, ROWS, BS), f32),
            ],
        ),
        compiler_params=params(),
        cost_estimate=cost(8 * HEADS * tokens * tokens * BS, tokens * D * 8, HEADS * tokens * tokens),
    )(first, last, queries, keys, values, seg_col, seg_row, vec, weights["out", layer])


def gelu_parts(values):
    cdf = 0.5 * (1.0 + lax.erf(values * 0.7071067811865476))
    pdf = 0.3989422804014327 * jnp.exp(-0.5 * values * values)
    return values * cdf, cdf + values * pdf


def mlp_kernel(layer, base, own, recv, vec, w_up, w_down, hid, normed, act, slope, part):
    values = base[...] + (own[...].astype(f32) + recv[...].astype(f32))
    hid[...] = values
    unit, unused = norm_stats(values)
    low = (unit * vec_piece(vec, layer, "g2") + vec_piece(vec, layer, "s2")).astype(bf16)
    normed[...] = low
    bias_up = vec_piece(vec, layer, "b1")
    for pair in range(HALF_FF // D):
        area = slice(pair * D, (pair + 1) * D)
        up = dot(low, joined(w_up, pair * 2 * D, D, 2)) + bias_up[:, area]
        gelu, grad = gelu_parts(up)
        act[:, area] = gelu.astype(bf16)
        slope[:, area] = grad.astype(bf16)
    bias_down = vec_piece(vec, layer, "b2")
    part[...] = (dot(act[...], joined(w_down, 0, HALF_FF, TENSOR)) + bias_down).astype(bf16)


def mlp_call(layer, base, own, recv, vec, weights):
    tokens = base.shape[0]
    shape = lambda width, kind: jax.ShapeDtypeStruct((tokens, width), kind)
    kept = lambda width: pltpu.HBM((tokens, width), bf16)
    outs = [shape(D, f32), kept(D), kept(HALF_FF), kept(HALF_FF), shape(D, bf16)]
    return pl.pallas_call(
        functools.partial(mlp_kernel, layer),
        out_shape=outs,
        grid=(tokens // ROWS,),
        in_specs=[rows_spec(D)] * 3
        + [
            fixed(vec.shape),
            fixed((2 * HALF_FF, HALF)),
            fixed((2 * HALF_FF, HALF)),
        ],
        out_specs=[rows_spec(o.shape[1]) for o in outs],
        compiler_params=params(),
        cost_estimate=cost(4 * tokens * D * HALF_FF, tokens * D * 24, 2 * tokens * HALF_FF),
    )(base, own, recv, vec, weights["up", layer], weights["down", layer])


def mlp_back_kernel(layer, summed, *refs):
    if summed:
        base, own, recv, *refs = refs
        (hid, slope, vec, w_up, w_down, grad_full, grad_low, du_ref, back, dgain, dshift, db1, db2) = refs
        values = base[...].astype(f32) + (own[...].astype(f32) + recv[...].astype(f32))
        grad_full[...] = values
        low = values.astype(bf16)
    else:
        base, valid, *refs = refs
        (hid, slope, vec, w_up, w_down, grad_low, du_ref, back, dgain, dshift, db1, db2) = refs
        low = (base[...].astype(f32) * valid[...]).astype(bf16)
    grad_low[...] = low
    accumulate(db2, jnp.sum(low.astype(f32), axis=0, keepdims=True))
    for part in range(HALF_FF // D):
        area = slice(part * D, (part + 1) * D)
        rows = jnp.concatenate(
            [w_down[p * HALF_FF + part * D : p * HALF_FF + (part + 1) * D, :] for p in range(TENSOR)],
            axis=1,
        )
        du_ref[:, area] = (dot_nt(low, rows) * slope[:, area].astype(f32)).astype(bf16)
    grad_normed = dot_nt(du_ref[...], joined(w_up, 0, D, HALF_FF // HALF))
    accumulate(db1, jnp.sum(du_ref[...].astype(f32), axis=0, keepdims=True))
    part_back, gain_grad, shift_grad = norm_back(hid[...], vec_piece(vec, layer, "g2"), grad_normed)
    back[...] = part_back.astype(bf16)
    accumulate(dgain, gain_grad)
    accumulate(dshift, shift_grad)


def mlp_back_call(layer, base, own, recv, valid, hid, slope, vec, weights):
    tokens = base.shape[0]
    summed = own is not None
    shape = lambda width, kind: jax.ShapeDtypeStruct((tokens, width), kind)
    line = lambda width: jax.ShapeDtypeStruct((1, width), f32)
    outs = ([shape(D, f32)] if summed else []) + [shape(D, bf16), shape(HALF_FF, bf16), shape(D, bf16)]
    lines = [line(D), line(D), line(HALF_FF), line(D)]
    extra = [own, recv] if summed else [valid]
    return pl.pallas_call(
        functools.partial(mlp_back_kernel, layer, summed),
        out_shape=outs + lines,
        grid=(tokens // ROWS,),
        in_specs=[rows_spec(D)]
        + [rows_spec(e.shape[1]) for e in extra]
        + [
            rows_spec(D),
            rows_spec(HALF_FF),
            fixed(vec.shape),
            fixed((2 * HALF_FF, HALF)),
            fixed((2 * HALF_FF, HALF)),
        ],
        out_specs=[rows_spec(o.shape[1]) for o in outs] + [fixed(o.shape) for o in lines],
        compiler_params=params(),
        cost_estimate=cost(4 * tokens * D * HALF_FF, tokens * D * 24),
    )(base, *extra, stay(hid), stay(slope), vec, weights["up", layer], weights["down", layer])


def attend_back_kernel(
    low_ref, high_ref, base, own, recv, q_ref, k_ref, v_ref, o_ref, lse_ref, seg_k, seg_q, w_out,
    full_ref, grad_low, dq_ref, dk_ref, dv_ref, dbo, dk_acc, dv_acc, dq_acc, do_ref,
):
    step = pl.program_id(0)

    @pl.when(step == 0)
    def _():
        dk_acc[...] = jnp.zeros_like(dk_acc)
        dv_acc[...] = jnp.zeros_like(dv_acc)

    values = base[...].astype(f32) + (own[...].astype(f32) + recv[...].astype(f32))
    full_ref[...] = values
    low = values.astype(bf16)
    grad_low[...] = low
    accumulate(dbo, jnp.sum(low.astype(f32), axis=0, keepdims=True))
    do_ref[...] = dot_nt(low, joined(w_out, 0, HALF, TENSOR)).astype(bf16)
    product = do_ref[...].astype(f32) * o_ref[...].astype(f32)
    head = lax.broadcasted_iota(jnp.int32, (8, HALF), 0)
    lane = lax.broadcasted_iota(jnp.int32, (8, HALF), 1)
    pick = ((lane >= head * HEAD_DIM) & (lane < (head + 1) * HEAD_DIM)).astype(f32)
    high, rest = split(product)
    pick = pick.astype(bf16)
    inner = dot_nt(pick, high) + dot_nt(pick, rest)
    dq_acc[...] = jnp.zeros_like(dq_acc)
    masks = head_masks()
    scale = jnp.asarray(HEAD_DIM ** (-0.5), bf16)
    seg_row = seg_q[...]

    def one_block(block, carried):
        rows = pl.ds(pl.multiple_of(block * KEYS, KEYS), KEYS)
        same = seg_k[rows, :] == seg_row
        for pair in range(HEADS // 2):
            cols = slice(pair * BS, (pair + 1) * BS)
            q_two = q_ref[:, cols] * scale
            do_two = do_ref[:, cols]
            k_two = k_ref[rows, cols]
            v_two = v_ref[rows, cols]
            dv_two = dk_two = dq_two = None
            for side in range(2):
                at = 2 * pair + side
                q_one = q_two * masks[side]
                do_one = do_two * masks[side]
                scores = dot_nt(k_two, q_one)
                prob = jnp.where(same, jnp.exp(scores - lse_ref[at : at + 1, :]), 0.0)
                grad_prob = dot_nt(v_two, do_one)
                grad_scores = (prob * (grad_prob - inner[at : at + 1, :])).astype(bf16)
                dv_one = dot(prob.astype(bf16), do_one)
                dk_one = dot(grad_scores, q_one)
                dq_one = dot_tn(grad_scores, k_two * masks[side])
                dq_two = dq_one if dq_two is None else dq_two + dq_one
                dv_two = dv_one if dv_two is None else dv_two + dv_one
                dk_two = dk_one if dk_two is None else dk_two + dk_one
            dv_acc[rows, cols] += dv_two
            dk_acc[rows, cols] += dk_two
            dq_acc[:, cols] += dq_two
        return carried

    lax.fori_loop(low_ref[step], high_ref[step], one_block, 0)
    dq_ref[...] = (dq_acc[...] * HEAD_DIM ** (-0.5)).astype(bf16)

    @pl.when(step == pl.num_programs(0) - 1)
    def _():
        dk_ref[...] = dk_acc[...].astype(bf16)
        dv_ref[...] = dv_acc[...].astype(bf16)


def attend_back_call(
    layer, first, last, base, own, recv, queries, keys, values, mixed, lse, seg_col, seg_row, weights
):
    tokens = base.shape[0]
    shape = lambda width, kind: jax.ShapeDtypeStruct((tokens, width), kind)
    whole = (tokens, HALF)
    return pl.pallas_call(
        attend_back_kernel,
        out_shape=[
            shape(D, f32),
            shape(D, bf16),
            shape(HALF, bf16),
            shape(HALF, bf16),
            shape(HALF, bf16),
            jax.ShapeDtypeStruct((1, D), f32),
        ],
        grid_spec=pltpu.PrefetchScalarGridSpec(
            num_scalar_prefetch=2,
            grid=(tokens // ROWS,),
            in_specs=[
                rows_spec(D),
                rows_spec(D),
                rows_spec(D),
                rows_spec(HALF),
                fixed(whole),
                fixed(whole),
                rows_spec(HALF),
                pl.BlockSpec((8, ROWS), lambda i, *_: (0, i)),
                fixed(seg_col.shape),
                pl.BlockSpec((1, ROWS), lambda i, *_: (0, i)),
                fixed((D, HALF)),
            ],
            out_specs=[
                rows_spec(D),
                rows_spec(D),
                rows_spec(HALF),
                fixed(whole),
                fixed(whole),
                fixed((1, D)),
            ],
            scratch_shapes=[
                pltpu.VMEM(whole, f32),
                pltpu.VMEM(whole, f32),
                pltpu.VMEM((ROWS, HALF), f32),
                pltpu.VMEM((ROWS, HALF), bf16),
            ],
        ),
        compiler_params=params(),
        cost_estimate=cost(14 * HEADS * tokens * tokens * BS, tokens * D * 20, HEADS * tokens * tokens),
    )(
        first, last, base, own, recv, stay(queries), stay(keys), stay(values), stay(mixed), lse,
        seg_col, seg_row, weights["out", layer],
    )


def qkv_back_kernel(layer, dq, dk, dv, hid, vec, weight, back, dgain, dshift, dbq, dbv):
    grad_three = jnp.concatenate([dq[...], dk[...], dv[...]], axis=1)
    grad_normed = dot_nt(grad_three, joined(weight, 0, D, 3))
    part_back, gain_grad, shift_grad = norm_back(hid[...], vec_piece(vec, layer, "g1"), grad_normed)
    back[...] = part_back.astype(bf16)
    accumulate(dgain, gain_grad)
    accumulate(dshift, shift_grad)
    accumulate(dbq, jnp.sum(dq[...].astype(f32), axis=0, keepdims=True))
    accumulate(dbv, jnp.sum(dv[...].astype(f32), axis=0, keepdims=True))


def qkv_back_call(layer, dq, dk, dv, hid, vec, weights):
    tokens = dq.shape[0]
    line = lambda width: jax.ShapeDtypeStruct((1, width), f32)
    lines = [line(D), line(D), line(HALF), line(HALF)]
    return pl.pallas_call(
        functools.partial(qkv_back_kernel, layer),
        out_shape=[jax.ShapeDtypeStruct((tokens, D), bf16)] + lines,
        grid=(tokens // ROWS,),
        in_specs=[rows_spec(HALF)] * 3
        + [
            rows_spec(D),
            fixed(vec.shape),
            fixed((3 * D, HALF)),
        ],
        out_specs=[rows_spec(D)] + [fixed(o.shape) for o in lines],
        compiler_params=params(),
        cost_estimate=cost(2 * tokens * D * 3 * HALF, tokens * D * 10),
    )(dq, dk, dv, stay(hid), vec, weights["qkv", layer])


def split(values):
    high = values.astype(bf16)
    return high, (values - high.astype(f32)).astype(bf16)


def product(left, right, left_dim, right_dim):
    def one(a, b):
        return lax.dot_general(
            a, b, (((left_dim,), (right_dim,)), ((), ())), preferred_element_type=f32
        )

    return one(left[0], right[0]) + (one(left[0], right[1]) + one(left[1], right[0]))


def owner_kernel(per, used, home, near, far, master, left, right, moment, variance, grad, out, out_mom, out_var):
    here = range(per)
    first = pl.program_id(0) * per
    lefts = [split(left[i]) for i in here]
    rights = [split(right[i]) for i in here]
    rotated = []
    for i in here:
        rows = slice(i * BS, (i + 1) * BS)
        tile = jnp.where(home[0] > 0, near[rows, :].astype(f32), far[rows, :].astype(f32))
        tile = jnp.where(used[first + i] > 0, tile, 0.0)
        grad[i] = tile
        tile = tile.astype(bf16)
        rotated.append(split(dot_tn(lefts[i][0], tile) + dot_tn(lefts[i][1], tile)))
    rotated = [product(rotated[i], rights[i], 1, 0) for i in here]
    steps = []
    for i in here:
        new_moment = decay * moment[i] + (1.0 - decay) * rotated[i]
        new_variance = decay * variance[i] + (1.0 - decay) * rotated[i] * rotated[i]
        out_mom[i] = new_moment
        out_var[i] = new_variance
        steps.append(split(new_moment / (jnp.sqrt(new_variance) + adam_eps)))
    returned = [split(product(lefts[i], steps[i], 1, 0)) for i in here]
    returned = [product(returned[i], rights[i], 1, 1) for i in here]
    for i in here:
        out[i] = master[i] - matrix_rate * returned[i]


def owner_call(used, home, near, far, *arrays):
    count = arrays[0].shape[0]
    per = min(8, count)
    block = pl.BlockSpec((per, BS, BS), lambda i, *_: (i, 0, 0))
    return pl.pallas_call(
        functools.partial(owner_kernel, per),
        out_shape=[jax.ShapeDtypeStruct(arrays[0].shape, f32)] * 4,
        grid_spec=pltpu.PrefetchScalarGridSpec(
            num_scalar_prefetch=2,
            grid=(count // per,),
            in_specs=[pl.BlockSpec((per * BS, BS), lambda i, *_: (i, 0))] * 2 + [block] * 5,
            out_specs=[block] * 4,
        ),
        compiler_params=params(),
        cost_estimate=cost(count * 88 * BS**3, count * BS * BS * 38),
    )(used, home, stay(near), stay(far), *arrays)


def reduce_kernel(carrying, last, *refs):
    block, arrived, *refs = refs
    total = block[...].astype(f32) + arrived[...].astype(f32)
    if carrying:
        carried, *refs = refs
        total = total + carried[...].astype(f32)
    if last:
        [out] = refs
    else:
        following, out, later = refs
        later[...] = following[...]
    out[...] = total.astype(bf16)


def reduce_call(j, n, buffer, arrived, carried, payload):
    last = j >= 2
    at = lambda j, x_rel: pl.BlockSpec((payload, BS), lambda i: ((j * 2 + x_rel) * 2 + n, 0))
    whole = fixed((payload, BS))
    operands = [stay(buffer), stay(arrived)] + ([] if carried is None else [stay(carried)])
    specs = [at(j, 0)] + [whole] * (len(operands) - 1)
    if not last:
        operands.append(stay(buffer))
        specs.append(at(j + 2, 1))
    outs = [pltpu.HBM((payload, BS), bf16)] * (1 if last else 2)
    made = pl.pallas_call(
        functools.partial(reduce_kernel, carried is not None, last),
        out_shape=outs,
        grid=(1,),
        in_specs=specs,
        out_specs=[whole] * len(outs),
        compiler_params=params(8),
        cost_estimate=cost(payload * BS * 3, payload * BS * 12),
    )(*operands)
    return (made[0], None) if last else made


class Routes:
    def __init__(self, dp_n):
        pairs = [(d, t) for d in range(dp_n) for t in range(TENSOR)]
        at = lambda d, t: d * TENSOR + t
        home = [(d, t) for d, t in pairs if d % 2 == t]
        away = [(d, t) for d, t in pairs if d % 2 != t]
        self.core_all = [(at(d, t), at(d ^ 1, t)) for d, t in pairs]
        self.core_out = [(at(d, t), at(d ^ 1, t)) for d, t in home]
        self.core_in = [(at(d, t), at(d ^ 1, t)) for d, t in away]
        self.y_all = [(at(d, t), at(d, 1 - t)) for d, t in pairs]
        self.y_out = [(at(d, t), at(d, 1 - t)) for d, t in home]
        self.y_in = [(at(d, t), at(d, 1 - t)) for d, t in away]
        self.x_home = [(at(d, t), at(d ^ 2, t)) for d, t in home]
        self.x_away = [(at(d, t), at(d ^ 2, t)) for d, t in away]
        self.x_all = [(at(d, t), at(d ^ 2, t)) for d, t in pairs]
        self.z_all = [(at(d, t), at((d + 4) % dp_n, t)) for d, t in pairs]
        self.z_home = [(at(d, t), at((d + 4) % dp_n, t)) for d, t in home]


def send(value, route):
    return lax.ppermute(value, AXES, route)


def shards(
    patches,
    cotangent,
    image_size,
    block_slot,
    pinv,
    master_slots,
    left_basis,
    right_basis,
    mom_slots,
    var_slots,
    vec_master,
    vec_mom,
    vec_var,
):
    dp_n = lax.axis_size("dp")
    dp_pos = lax.axis_index("dp")
    y_pos = lax.axis_index("tensor")
    core = dp_pos % 2
    home = core == y_pos
    routes = Routes(dp_n)
    grid3 = dp_n == 16
    x_pos = (dp_pos // 2) % 2
    half_at = (x_pos if grid3 else x_pos * 0).astype(jnp.int32).reshape(1)
    tokens_n = patches.shape[0]
    slots_per = master_slots.shape[1]
    vec_per = vec_master.shape[1]
    slots_n = slots_per * dp_n
    payload = slots_per * BS + VEC_ROWS

    patches = jnp.where(home, patches, send(patches, routes.core_out))
    cotangent = jnp.where(home, cotangent, send(cotangent, routes.core_out))
    size_row = jnp.where(home, image_size, send(image_size, routes.core_out))[0]
    own_slots = block_slot[0]
    slot_other = send(block_slot, routes.y_all)

    lengths = jnp.where(
        size_row == 0, LEN_A, jnp.where(size_row == 1, LEN_B, jnp.where(size_row == 2, LEN_C, 0))
    )
    order = jnp.arange(IMG_DEV)
    ends_at = jnp.sum(jnp.where(order[None, :] <= order[:, None], lengths[None, :], 0), axis=1)
    places = jnp.arange(tokens_n)
    segment = jnp.sum((places[:, None] >= ends_at[None, :]).astype(jnp.int32), axis=1)
    in_image = segment[:, None] == order[None, :]
    select = jnp.stack(
        [jnp.any(in_image & (size_row == s)[None, :], axis=1) for s in range(3)], axis=1
    )
    valid_col = (segment < IMG_DEV).astype(f32)[:, None]
    seg_col = segment[:, None]
    seg_row = segment[None, :]
    blocks_n = tokens_n // ROWS
    starts = jnp.arange(blocks_n) * ROWS
    begun = ends_at[None, :] <= starts[:, None]
    first_tok = jnp.max(jnp.where(begun, ends_at[None, :], 0), axis=1)
    after = ends_at[None, :] > (starts + ROWS - 1)[:, None]
    last_tok = jnp.min(jnp.where(after, ends_at[None, :], tokens_n), axis=1)
    first_blk = (first_tok // ROWS).astype(jnp.int32)
    last_blk = ((last_tok + ROWS - 1) // ROWS).astype(jnp.int32)
    first_key = (first_tok // KEYS).astype(jnp.int32)
    last_key = ((last_tok + KEYS - 1) // KEYS).astype(jnp.int32)

    select_low = select.astype(bf16)
    class_col = jnp.sum(jnp.where(select, jnp.arange(1, 4)[None, :], 0), axis=1, keepdims=True) - 1
    present = jnp.any(select.reshape(blocks_n, ROWS, 3), axis=1).astype(jnp.int32)

    def expand(which, rows):
        return expand_call(which, present, half_at, rows, class_col, pinv)

    vec_low = jnp.pad(vec_master[0].astype(bf16), (0, VEC_ROWS * BS - vec_per))
    own_pack = jnp.concatenate(
        [
            master_slots[0].astype(bf16).reshape(slots_per * BS, BS),
            vec_low.reshape(VEC_ROWS, BS),
        ],
        axis=0,
    )
    flag = home.astype(jnp.int32).reshape(1)
    if grid3:
        z_pos = dp_pos // 4
        pack = own_pack
        chunks, first, second, owner = [], [], [], []
        middle_row = slots_per * BS // 2
        for j in range(4):
            beside_x, beside_y = send(pack, routes.x_all), send(pack, routes.y_all)
            further = [send(pack, routes.z_all)] if j < 3 else []
            work = [slot_other] if j == 0 else []
            beside_x, beside_y, patches, chunk, *more = fence(
                beside_x, beside_y, patches, expand(j, patches), *further, *work
            )
            chunks.append(chunk)
            if j < 3:
                further = more.pop(0)
            if j == 0:
                [slot_other] = more
            corner = jnp.concatenate(
                [send(beside_x[:middle_row], routes.y_all), send(beside_y[middle_row:], routes.x_all)],
                axis=0,
            )
            near_two = send(jnp.where(home, beside_y, pack), routes.core_all)
            far_two = send(jnp.where(home, corner, beside_x), routes.core_all)
            first += [pack, near_two, beside_x, far_two]
            second += [beside_y, near_two, corner, far_two]
            for x_rel in range(2):
                for n in range(2):
                    owner.append(((z_pos - j) % 4) * 4 + (x_pos ^ x_rel) * 2 + (core ^ n))
            if j < 3:
                pack = further
        first = [v[None] for v in first]
        second = [v[None] for v in second]
        owner = jnp.stack(owner).astype(jnp.int32)
    else:
        everything = lax.all_gather(own_pack, AXES, axis=0)
        everything = everything.reshape(dp_n, TENSOR, payload, BS)
        first = [jnp.where(core == 0, everything[:, 0], everything[:, 1])]
        second = []
        owner = jnp.arange(dp_n, dtype=jnp.int32)
        chunks = [expand(c, patches) for c in range(CHUNKS)]
    slot_list = jnp.where(home, block_slot, slot_other)[0]
    named = slot_list[None, :] == jnp.arange(slots_n)[:, None]
    used = jnp.any(named, axis=1)
    drow = jnp.where(used, jnp.sum(jnp.where(named, TARGET_ROW[None, :], 0), axis=1), -1)
    dcol = jnp.sum(jnp.where(named, TARGET_COL[None, :], 0), axis=1)
    weights, vec_rows = gather_tiles(first, second, owner, drow, dcol, flag, slots_per, dp_n)
    vec = vec_rows.reshape(dp_n, VEC_ROWS * BS)[:, :vec_per].astype(f32).reshape(1, dp_n * vec_per)

    embedded = embed_call(half_at, chunks, vec, weights)
    embedded_other = send(embedded, routes.core_all)
    core_flag = core.astype(jnp.int32).reshape(1)

    caches = []
    hidden, own, recv = None, embedded, embedded_other
    for layer in range(LAYERS):
        hidden, normed, queries, keys, values = qkv_call(
            layer, hidden, own, recv, core_flag, vec, weights
        )
        mixed, lse, part = attend_call(
            layer, first_blk, last_blk, queries, keys, values, seg_col, seg_row, vec, weights
        )
        other = send(part, routes.core_all)
        middle, normed2, act, slope, own = mlp_call(layer, hidden, part, other, vec, weights)
        recv = send(own, routes.core_all)
        caches.append((hidden, normed, queries, keys, values, mixed, lse, middle, normed2, act, slope))
        hidden = middle
    out_low = ((hidden + (own.astype(f32) + recv.astype(f32))) * valid_col).astype(bf16)

    owners = jnp.arange(dp_n)
    if grid3:
        place = (
            ((z_pos - 1 - owners // 4) % 4) * 4
            + (x_pos ^ ((owners // 2) % 2)) * 2
            + (core ^ (owners % 2))
        ).astype(jnp.int32)
    else:
        place = owners.astype(jnp.int32)
    slot_owner = slot_list // slots_per
    owner_place = jnp.sum(
        jnp.where(slot_owner[:, None] == owners[None, :], place[None, :], 0), axis=1
    )
    tile_pos = (owner_place * payload + (slot_list % slots_per) * BS).astype(jnp.int32)
    vec_pos = (place * payload + slots_per * BS).astype(jnp.int32)
    total_rows = dp_n * payload
    where_to = jnp.concatenate([half_at, flag if grid3 else flag * 0 + 1])
    offsets = {"base": 0}
    count = BASE_PIX // BS * (HALF // BS)
    for layer in range(LAYERS):
        for name, size in (("qkv", 3 * D * HALF), ("out", D * HALF), ("up", D * HALF_FF), ("down", D * HALF_FF)):
            offsets[name, layer] = count
            count += size // (BS * BS)

    def place_tiles(key, matrix, arrived, buffer):
        tiles = matrix.size // (BS * BS)
        pos = tile_pos[offsets[key] : offsets[key] + tiles]
        rows_n = matrix.shape[0] // 2 if matrix.shape[0] > HALF else HALF
        return scatter_matrix(pos, matrix, arrived, where_to, buffer, total_rows, rows_n)

    def place_base(rel, matrix, arrived, buffer):
        size = BASE_PIX * HALF // (BS * BS) // 2
        low_pos, high_pos = tile_pos[:size], tile_pos[size : 2 * size]
        pos = jnp.where(half_at[0] == rel, low_pos, high_pos)
        return scatter_matrix(pos, matrix, arrived, where_to, buffer, total_rows, D)

    def over(matrix):
        return send(matrix, routes.y_in) if grid3 else None

    def beside(matrix):
        return send(other_half(half_at, matrix), routes.x_away) if grid3 else None

    def summed(matrix, arrived):
        return half_sum(half_at, matrix, arrived) if grid3 else None

    def hold(*arrays):
        kept = [a for a in arrays if a is not None]
        done = iter(fence(*kept))
        return [None if a is None else next(done) for a in arrays]

    top, low = 1, 0
    vec_grads = [None] * LAYERS

    def mlp_step(layer, grad, own, recv):
        middle, normed2, act, slope = caches[layer][7:11]
        made = mlp_back_call(layer, grad, own, recv, valid_col, middle, slope, vec, weights)
        if own is not None:
            return made
        return [made[0]] + list(made)

    def attend_step(layer, grad, part, other, lse):
        hid_in, normed, queries, keys, values, mixed = caches[layer][:6]
        return attend_back_call(
            layer, first_key, last_key, grad, part, other, queries, keys, values, mixed, lse,
            seg_col, seg_row, weights,
        )

    grad, grad_low, du, part, dg2, ds2, db1, db2 = mlp_step(top, cotangent, None, None)
    other = send(part, routes.core_all)
    gd1 = dot_tn(caches[top][9], grad_low).astype(bf16)
    gu1 = dot_tn(caches[top][8], du).astype(bf16)
    ad1 = over(gd1)
    lse, gu1 = fence(caches[top][6], gu1)
    xu1 = beside(gu1)
    grad, grad_low, dq, dk, dv, dbo = attend_step(top, grad, part, other, lse)
    vec, dbo, ad1, xu1, out_low = hold(vec, dbo, ad1, xu1, out_low)
    au1 = over(summed(gu1, xu1))
    own, dg1, ds1, dbq, dbv = qkv_back_call(top, dq, dk, dv, caches[top][0], vec, weights)
    recv = send(own, routes.core_all)
    go1 = dot_tn(caches[top][5], grad_low).astype(bf16)
    gq1 = dot_tn(caches[top][1], jnp.concatenate([dq, dk, dv], axis=1)).astype(bf16)
    vec_grads[top] = [dg1, ds1, dbq, dbv, dbo, dg2, ds2, db1, db2]
    xq1, ao1 = beside(gq1), over(go1)
    grad, grad_low, du, part, dg2, ds2, db1, db2 = mlp_step(low, grad, own, recv)
    other = send(part, routes.core_all)
    db2, xq1, au1 = hold(db2, xq1, au1)
    aq1 = over(summed(gq1, xq1))
    gd0 = dot_tn(caches[low][9], grad_low).astype(bf16)
    gu0 = dot_tn(caches[low][8], du).astype(bf16)
    lse, gd0, gu0, ao1, aq1 = hold(caches[low][6], gd0, gu0, ao1, aq1)
    ad0 = over(gd0)
    xu0 = beside(gu0)
    buffer = place_tiles(("down", top), gd1, ad1, None)
    buffer = place_tiles(("up", top), gu1, au1, buffer)
    grad, grad_low, dq, dk, dv, dbo = attend_step(low, grad, part, other, lse)
    vec, dbo, ad0, xu0, buffer = hold(vec, dbo, ad0, xu0, buffer)
    au0 = over(summed(gu0, xu0))
    own, dg1, ds1, dbq, dbv = qkv_back_call(low, dq, dk, dv, caches[low][0], vec, weights)
    recv = send(own, routes.core_all)
    gq0 = dot_tn(caches[low][1], jnp.concatenate([dq, dk, dv], axis=1)).astype(bf16)
    vec_grads[low] = [dg1, ds1, dbq, dbv, dbo, dg2, ds2, db1, db2]
    xq0 = beside(gq0)
    turn = jnp.zeros((8, BS), f32)
    grad_emb, grad_emb_bias = embed_back_call(core_flag, turn, grad, own, recv)
    middle = CHUNKS // 2

    def base_grad(parts):
        return jnp.concatenate([dot_tn(c, grad_emb).astype(bf16) for c in parts], axis=0)

    gbt = base_grad(chunks[middle:])
    gbt, au0, xq0 = hold(gbt, au0, xq0)
    xb = send(gbt, routes.x_away) if grid3 else None
    aq0 = over(summed(gq0, xq0))
    gbm = base_grad(chunks[:middle])
    vec_grad = pack_call([grad_emb_bias] + vec_grads[0] + vec_grads[1], dp_n, vec_per)
    go0 = dot_tn(caches[low][5], grad_low).astype(bf16)
    ao0, av = over(go0), over(vec_grad)
    buffer = place_tiles(("out", top), go1, ao1, buffer)
    buffer = place_tiles(("qkv", top), gq1, aq1, buffer)
    buffer = place_tiles(("down", low), gd0, ad0, buffer)
    gbm, xb, aq0, ao0, av, buffer = hold(gbm, xb, aq0, ao0, av, buffer)
    ab = over(half_sum(half_at * 0, gbm, xb)) if grid3 else None
    buffer = place_tiles(("up", low), gu0, au0, buffer)
    buffer = place_base(1, gbt, None, buffer)
    buffer = place_tiles(("out", low), go0, ao0, buffer)
    buffer = scatter_vec(vec_pos, vec_grad, av, buffer)
    buffer = place_tiles(("qkv", low), gq0, aq0, buffer)
    base_weight = weights["base", 0]
    ab, buffer, base_weight, out_low = hold(ab, buffer, base_weight, out_low)
    weights["base", 0] = base_weight
    buffer = place_base(0, gbm, ab, buffer)

    if grid3:
        token = jnp.zeros((8, BS), f32)
        order = (1, 0)
        resized = resize_call(weights, pinv)
        carried = {n: None for n in order}
        blocks = buffer.reshape(4, 2, 2, payload, BS)
        across = {n: send(blocks[0, 1, n], routes.x_home) for n in order}
        following = {n: blocks[1, 1, n] for n in order}
        rounded = {}
        for j in range(4):
            for n in order:
                extra = None
                if j == 0 and n == order[0]:
                    extra = resized
                token, across[n], carried[n], extra = hold(token, across[n], carried[n], extra)
                if extra is not None:
                    resized = extra
                arrived = across[n]
                if j < 3:
                    across[n] = send(following[n], routes.x_home)
                total, following[n] = reduce_call(j, n, buffer, arrived, carried[n], payload)
                if j < 3:
                    carried[n] = send(total, routes.z_home)
                else:
                    rounded[n] = total
        near_grad, far_grad = rounded[0], send(rounded[1], routes.core_out)
    else:
        held = buffer.reshape(dp_n, 1, payload, BS).astype(f32)
        nothing = jnp.zeros_like(held)
        both = jnp.concatenate(
            [jnp.where(core == 0, held, nothing), jnp.where(core == 0, nothing, held)], axis=1
        )
        used_rows = jnp.repeat(used, BS).reshape(dp_n, 1, slots_per * BS, 1)
        used_rows = jnp.concatenate(
            [used_rows, jnp.ones((dp_n, 1, VEC_ROWS, 1), bool)], axis=2
        )
        both = jnp.where(used_rows, both, 0.0).reshape(dp_n * TENSOR * payload, BS)
        near_grad = lax.psum_scatter(both, AXES, scatter_dimension=0, tiled=True).astype(bf16)
        far_grad = near_grad
        resized = resize_call(weights, pinv)

    output = jnp.where(home, out_low, send(out_low, routes.y_out)).astype(f32)
    grad_pixels = sum(
        dot(grad_emb * select_low[:, s : s + 1], resized[s]) for s in range(3)
    ).astype(bf16)
    pixels_other = send(grad_pixels, routes.core_all)
    pixel_sides = [
        grad_pixels[:, s * HALF : (s + 1) * HALF].astype(f32)
        + pixels_other[:, s * HALF : (s + 1) * HALF].astype(f32)
        for s in range(TENSOR)
    ]
    near = jnp.where(core == 0, pixel_sides[0], pixel_sides[1])
    far = jnp.where(core == 0, pixel_sides[1], pixel_sides[0]).astype(bf16)
    patch_grad = jnp.where(home, near, send(far, routes.y_out).astype(f32))

    my_slots = dp_pos * slots_per + jnp.arange(slots_per)
    mine_used = jnp.any(own_slots[None, :] == my_slots[:, None], axis=1).astype(jnp.int32)
    owned_grad, new_master, new_mom, new_var = owner_call(
        mine_used, flag, near_grad, far_grad, master_slots[0], left_basis[0], right_basis[0], mom_slots[0], var_slots[0]
    )
    vec_rows = jnp.where(home, near_grad[slots_per * BS :], far_grad[slots_per * BS :])
    owned_vec_grad = vec_rows.astype(f32).reshape(VEC_ROWS * BS)[:vec_per]
    new_vec_mom = decay * vec_mom[0] + (1.0 - decay) * owned_vec_grad
    new_vec_var = decay * vec_var[0] + (1.0 - decay) * owned_vec_grad * owned_vec_grad
    new_vec = vec_master[0] - vector_rate * new_vec_mom / (jnp.sqrt(new_vec_var) + adam_eps)
    return (
        output,
        patch_grad,
        owned_grad[None],
        new_master[None],
        new_mom[None],
        new_var[None],
        owned_vec_grad[None],
        new_vec[None],
        new_vec_mom[None],
        new_vec_var[None],
    )


def solution(mesh):
    slots = P("tensor", "dp", None, None)
    vectors = P("tensor", "dp")
    tokens = P("dp", None)
    in_specs = (tokens, tokens, tokens, P("tensor", None), P()) + (slots,) * 5 + (vectors,) * 3
    out_specs = (tokens, P("dp", "tensor")) + (slots,) * 4 + (vectors,) * 4
    return jax.shard_map(shards, mesh=mesh, in_specs=in_specs, out_specs=out_specs, check_vma=False)
```

```python
import functools

import jax
import jax.numpy as jnp
import numpy as np
from jax import lax
from jax.experimental import pallas as pl
from jax.experimental.pallas import tpu as pltpu
from jax.sharding import PartitionSpec as P

D = 768
HEAD_DIM = 64
FF = 3072
BASE_PIX = 3072
LAYERS = 2
LEN_A = 196
LEN_B = 225
LEN_C = 576
IMG_DEV = 5
BS = 128
TENSOR = 2
HALF = D // TENSOR
HALF_FF = FF // TENSOR
HEADS = HALF // HEAD_DIM
ROWS = 256
KEYS = 512
VEC_ROWS = 16
CHUNKS = 4

AXES = ("dp", "tensor")
precise = lax.Precision.HIGHEST
masked_score = -1e30
norm_eps = 1e-06
adam_eps = 1e-08
decay = 0.5
matrix_rate = 0.05
vector_rate = 0.3
f32 = jnp.float32
bf16 = jnp.bfloat16
MIB = 1024 * 1024

WEIGHTS = [("base", 0, BASE_PIX)]
for layer in range(LAYERS):
    WEIGHTS += [("qkv", layer, 3 * D), ("out", layer, D), ("up", layer, FF), ("down", layer, FF)]
STARTS = {}
PANEL_ROWS = 0
for name, layer, size in WEIGHTS:
    STARTS[name, layer] = PANEL_ROWS
    PANEL_ROWS += size


def tile_targets():
    rows, cols = [], []

    def add(start, rows_n, cols_n):
        for i in range(rows_n // BS):
            for j in range(cols_n // BS):
                panel, inner = divmod(j * BS, HALF)
                rows.append(start + panel * rows_n + i * BS)
                cols.append(inner)

    add(STARTS["base", 0], BASE_PIX, HALF)
    for layer in range(LAYERS):
        add(STARTS["qkv", layer], D, 3 * HALF)
        add(STARTS["out", layer], HALF, D)
        add(STARTS["up", layer], D, HALF_FF)
        add(STARTS["down", layer], HALF_FF, D)
    return np.array(rows, np.int32), np.array(cols, np.int32)


TARGET_ROW, TARGET_COL = tile_targets()
LAYER_VECS = (D, D, HALF, HALF, D, D, D, HALF_FF, D)
VEC_NAMES = ("g1", "s1", "bq", "bv", "bo", "g2", "s2", "b1", "b2")


def vec_offsets():
    offset = HALF
    found = []
    for layer in range(LAYERS):
        here = {}
        for name, length in zip(VEC_NAMES, LAYER_VECS):
            here[name] = (offset, length)
            offset += length
        found.append(here)
    return found


VEC_AT = vec_offsets()


def params(limit=24):
    return pltpu.CompilerParams(
        dimension_semantics=("arbitrary",), vmem_limit_bytes=limit * MIB
    )


def cost(flops, nbytes, trans=0):
    return pl.CostEstimate(flops=flops, bytes_accessed=nbytes, transcendentals=trans)


def rows_spec(width):
    return pl.BlockSpec((ROWS, width), lambda i, *_: (i, 0))


def fixed(shape, at=0):
    return pl.BlockSpec(shape, lambda i, *_: (at,) + (0,) * (len(shape) - 1))


def vec_piece(vec_ref, layer, name):
    start, length = VEC_AT[layer][name]
    return vec_ref[:, start : start + length]


def dot(left, right):
    return jnp.dot(left, right, preferred_element_type=f32)


def dot_nt(left, right, precision=None):
    return lax.dot_general(
        left, right, (((1,), (1,)), ((), ())), precision=precision, preferred_element_type=f32
    )


def dot_tn(left, right):
    return lax.dot_general(left, right, (((0,), (0,)), ((), ())), preferred_element_type=f32)


def joined(ref, start, rows_n, panels):
    return jnp.concatenate(
        [ref[start + p * rows_n : start + (p + 1) * rows_n, :] for p in range(panels)], axis=1
    )


def norm_stats(values):
    mean_val = jnp.mean(values, axis=-1, keepdims=True)
    centered = values - mean_val
    inv_std = lax.rsqrt(jnp.mean(centered * centered, axis=-1, keepdims=True) + norm_eps)
    return centered * inv_std, inv_std


def norm_back(values, gain, grad):
    unit, inv_std = norm_stats(values)
    scaled = grad * gain
    mean_s = jnp.mean(scaled, axis=-1, keepdims=True)
    mean_u = jnp.mean(scaled * unit, axis=-1, keepdims=True)
    back = inv_std * (scaled - mean_s - unit * mean_u)
    return (
        back,
        jnp.sum(grad * unit, axis=0, keepdims=True),
        jnp.sum(grad, axis=0, keepdims=True),
    )


def accumulate(ref, value):
    first = pl.program_id(0) == 0

    @pl.when(first)
    def _():
        ref[...] = value

    @pl.when(jnp.logical_not(first))
    def _():
        ref[...] += value


def stay(value):
    return pltpu.with_memory_space_constraint(value, pltpu.HBM)


def fence(*arrays):
    def nothing(*refs):
        pass

    anywhere = pl.BlockSpec(memory_space=pl.ANY)
    return pl.pallas_call(
        nothing,
        out_shape=[jax.ShapeDtypeStruct(a.shape, a.dtype) for a in arrays],
        in_specs=[anywhere] * len(arrays),
        out_specs=[anywhere] * len(arrays),
        input_output_aliases={i: i for i in range(len(arrays))},
        compiler_params=pltpu.CompilerParams(vmem_limit_bytes=MIB),
    )(*[stay(a) if a.size > 32 * 1024 else a for a in arrays])


def gather_kernel(slots, count_a, count_b, owner, drow, dcol, flag, *refs):
    first = refs[:count_a]
    second = refs[count_a : count_a + count_b]
    *panels, vectors, held, sem, vec_sem = refs[count_a + count_b :]

    def copy_all(sources):
        at = 0
        for src in sources:
            for n in range(src.shape[0]):
                who = owner[at]
                at += 1

                def body(i, carried, src=src, n=n, who=who):
                    slot = who * slots + i
                    row = drow[slot]

                    @pl.when(row >= 0)
                    def _():
                        start = pl.multiple_of(i * BS, BS)
                        pltpu.make_async_copy(
                            src.at[n, pl.ds(start, BS), :],
                            held.at[
                                pl.ds(pl.multiple_of(row, BS), BS),
                                pl.ds(pl.multiple_of(dcol[slot], BS), BS),
                            ],
                            sem,
                        ).start()

                    return carried

                lax.fori_loop(0, slots, body, 0)
                pltpu.make_async_copy(
                    src.at[n, pl.ds(slots * BS, VEC_ROWS), :], vectors.at[who], vec_sem
                ).start()

    if count_b:

        @pl.when(flag[0] == 1)
        def _():
            copy_all(first)

        @pl.when(flag[0] == 0)
        def _():
            copy_all(second)
    else:
        copy_all(first)
    pltpu.make_async_copy(held, held, sem).wait()
    at = 0
    for panel in panels:
        size = panel.shape[0]
        pltpu.make_async_copy(held.at[pl.ds(at, size), :], panel, sem).start()
        at += size
    pltpu.make_async_copy(vectors, vectors, vec_sem).wait()
    pltpu.make_async_copy(held, held, sem).wait()


def gather_tiles(first, second, owner, drow, dcol, flag, slots, owners):
    anywhere = pl.BlockSpec(memory_space=pl.ANY)
    *panels, vectors = pl.pallas_call(
        functools.partial(gather_kernel, slots, len(first), len(second)),
        out_shape=[pltpu.HBM((size, HALF), bf16) for unused, unused2, size in WEIGHTS]
        + [jax.ShapeDtypeStruct((owners, VEC_ROWS, BS), bf16)],
        grid_spec=pltpu.PrefetchScalarGridSpec(
            num_scalar_prefetch=4,
            grid=(1,),
            in_specs=[anywhere] * (len(first) + len(second)),
            out_specs=[anywhere] * len(WEIGHTS) + [fixed((owners, VEC_ROWS, BS))],
            scratch_shapes=[
                pltpu.VMEM((PANEL_ROWS, HALF), bf16),
                pltpu.SemaphoreType.DMA,
                pltpu.SemaphoreType.DMA,
            ],
        ),
        compiler_params=params(),
        cost_estimate=cost(0, 4 * PANEL_ROWS * HALF),
    )(owner, drow, dcol, flag, *[stay(v) for v in first], *[stay(v) for v in second])
    return {(name, layer): p for (name, layer, unused), p in zip(WEIGHTS, panels)}, vectors


def scatter_kernel(rows_n, cols_n, steps, paired, parts, pos, part, own, *refs):
    @pl.when(part[1] > 0)
    def _():
        scatter_body(rows_n, cols_n, steps, paired, parts, pos, part, own, *refs)


def scatter_body(rows_n, cols_n, steps, paired, parts, pos, part, own, *refs):
    if paired:
        recv, *refs = refs
        span = pl.num_programs(0) // parts
        here = jnp.logical_or(parts == 1, pl.program_id(0) // span == part[0])
    target, buf, sems = refs[-3:]
    step = pl.program_id(0)
    slot = lax.rem(step, 2)
    per = rows_n // BS * (cols_n // BS)

    def wait(at):
        pltpu.make_async_copy(buf.at[at], buf.at[at], sems.at[at]).wait()

    @pl.when(step >= 2)
    def _():
        wait(slot)

    for i in range(rows_n // BS):
        for j in range(cols_n // BS):
            area = (slice(i * BS, (i + 1) * BS), slice(j * BS, (j + 1) * BS))
            value = own[area]
            if paired:
                more = jnp.where(here, recv[area].astype(f32), 0.0)
                value = (value.astype(f32) + more).astype(bf16)
            buf[slot, i * (cols_n // BS) + j] = value
    for n in range(per):
        pltpu.make_async_copy(
            buf.at[slot, n],
            target.at[pl.ds(pl.multiple_of(pos[step * per + n], 16), BS), :],
            sems.at[slot],
        ).start()

    @pl.when(step == pl.num_programs(0) - 1)
    def _():
        if steps > 1:
            wait(1 - slot)
        wait(slot)


def scatter_matrix(pos, own, recv, part, target, total_rows, rows_n):
    cols_n = own.shape[1]
    steps = own.shape[0] // rows_n
    anywhere = pl.BlockSpec(memory_space=pl.ANY)
    block = pl.BlockSpec((rows_n, cols_n), lambda i, *_: (i, 0))
    paired = recv is not None
    parts = own.shape[0] // recv.shape[0] if paired else 1
    span = steps // parts
    arrived = pl.BlockSpec(
        (rows_n, cols_n), lambda i, pos, part: (jnp.clip(i - part[0] * span, 0, span - 1), 0)
    )
    operands = [stay(own)] + ([stay(recv)] if paired else []) + ([] if target is None else [stay(target)])
    specs = [block] + ([block if parts == 1 else arrived] if paired else [])
    specs += [] if target is None else [anywhere]
    return pl.pallas_call(
        functools.partial(scatter_kernel, rows_n, cols_n, steps, paired, parts),
        out_shape=pltpu.HBM((total_rows, BS), bf16),
        grid_spec=pltpu.PrefetchScalarGridSpec(
            num_scalar_prefetch=2,
            grid=(steps,),
            in_specs=specs,
            out_specs=anywhere,
            scratch_shapes=[
                pltpu.VMEM((2, rows_n // BS * (cols_n // BS), BS, BS), bf16),
                pltpu.SemaphoreType.DMA((2,)),
            ],
        ),
        input_output_aliases={} if target is None else {len(operands) + 1: 0},
        compiler_params=params(12),
        cost_estimate=cost(own.size, own.size * 6),
    )(pos, part, *operands)


def half_sum_kernel(part, own, arrived, out):
    out[...] = (own[...].astype(f32) + arrived[...].astype(f32)).astype(bf16)


def half_sum(part, own, arrived):
    block = arrived.shape
    return pl.pallas_call(
        half_sum_kernel,
        out_shape=pltpu.HBM(block, bf16),
        grid_spec=pltpu.PrefetchScalarGridSpec(
            num_scalar_prefetch=1,
            grid=(1,),
            in_specs=[pl.BlockSpec(block, lambda i, part: (part[0], 0)), fixed(block)],
            out_specs=fixed(block),
        ),
        compiler_params=params(8),
        cost_estimate=cost(arrived.size, arrived.size * 6),
    )(part, stay(own), stay(arrived))


def half_copy_kernel(part, own, out):
    out[...] = own[...]


def other_half(part, own):
    block = (own.shape[0] // 2, own.shape[1])
    return pl.pallas_call(
        half_copy_kernel,
        out_shape=pltpu.HBM(block, bf16),
        grid_spec=pltpu.PrefetchScalarGridSpec(
            num_scalar_prefetch=1,
            grid=(1,),
            in_specs=[pl.BlockSpec(block, lambda i, part: (1 - part[0], 0))],
            out_specs=fixed(block),
        ),
        compiler_params=params(8),
        cost_estimate=cost(0, own.size * 2),
    )(part, stay(own))


def scatter_vec_kernel(paired, pos, own, *refs):
    if paired:
        recv, *refs = refs
    target, buf, sem = refs[-3:]
    value = own[...]
    if paired:
        value = (value.astype(f32) + recv[...].astype(f32)).astype(bf16)
    buf[...] = value

    def body(n, carried):
        pltpu.make_async_copy(
            buf.at[n], target.at[pl.ds(pl.multiple_of(pos[n], 16), VEC_ROWS), :], sem
        ).start()
        return carried

    lax.fori_loop(0, own.shape[0], body, 0)
    pltpu.make_async_copy(buf, buf, sem).wait()


def scatter_vec(pos, own, recv, target):
    anywhere = pl.BlockSpec(memory_space=pl.ANY)
    block = fixed(own.shape)
    paired = recv is not None
    operands = [own] + ([recv] if paired else []) + [stay(target)]
    return pl.pallas_call(
        functools.partial(scatter_vec_kernel, paired),
        out_shape=pltpu.HBM(target.shape, bf16),
        grid_spec=pltpu.PrefetchScalarGridSpec(
            num_scalar_prefetch=1,
            grid=(1,),
            in_specs=[block] * (len(operands) - 1) + [anywhere],
            out_specs=anywhere,
            scratch_shapes=[pltpu.VMEM(own.shape, bf16), pltpu.SemaphoreType.DMA],
        ),
        input_output_aliases={len(operands): 0},
        compiler_params=params(4),
    )(pos, *operands)


def expand_kernel(present, half, patch_ref, class_ref, pinv_ref, out, total):
    for block in range(patch_ref.shape[0] // ROWS):
        rows = slice(block * ROWS, (block + 1) * ROWS)
        total[...] = jnp.zeros_like(total)
        for which in range(3):

            @pl.when(present[block, which] > 0)
            def _(which=which, rows=rows):
                chosen = jnp.where(class_ref[rows, :] == which, patch_ref[rows, :].astype(f32), 0.0)
                total[...] += dot_nt(chosen.astype(bf16), pinv_ref[which])

        out[rows, :] = total[...].astype(bf16)


def expand_call(which, present, half, patches, class_col, pinv):
    tokens = patches.shape[0]
    size = BASE_PIX // CHUNKS
    step = size
    return pl.pallas_call(
        expand_kernel,
        out_shape=jax.ShapeDtypeStruct((tokens, size), bf16),
        grid_spec=pltpu.PrefetchScalarGridSpec(
            num_scalar_prefetch=2,
            grid=(1,),
            in_specs=[
                fixed(patches.shape),
                fixed(class_col.shape),
                pl.BlockSpec(
                    (3, step, pinv.shape[2]),
                    lambda i, present, half: (0, (which + half[0] * (CHUNKS // 2)) % CHUNKS, 0),
                ),
            ],
            out_specs=pl.BlockSpec((tokens, step), lambda i, *_: (0, i)),
            scratch_shapes=[pltpu.VMEM((ROWS, step), f32)],
        ),
        compiler_params=params(),
        cost_estimate=cost(3 * tokens * size * D, tokens * size * 4 + size * D * 6),
    )(present, half, stay(patches), class_col, stay(pinv))


def resize_kernel(base, pinv_ref, out, turned):
    @pl.when(pl.program_id(0) == 0)
    def _():
        turned[...] = base[...].T

    out[0] = dot(turned[...], pinv_ref[0]).astype(bf16)


def resize_call(weights, pinv):
    return pl.pallas_call(
        resize_kernel,
        out_shape=jax.ShapeDtypeStruct((3, HALF, pinv.shape[2]), bf16),
        grid=(3,),
        in_specs=[
            fixed((BASE_PIX, HALF)),
            pl.BlockSpec((1, BASE_PIX, pinv.shape[2]), lambda i: (i, 0, 0)),
        ],
        out_specs=pl.BlockSpec((1, HALF, pinv.shape[2]), lambda i: (i, 0, 0)),
        scratch_shapes=[pltpu.VMEM((HALF, BASE_PIX), bf16)],
        compiler_params=params(),
        cost_estimate=cost(6 * D * BASE_PIX * HALF, 6 * D * BASE_PIX),
    )(stay(weights["base", 0]), stay(pinv))


def embed_back_kernel(core, token, base, own, recv, out, bias):
    low = (base[...] + (own[...].astype(f32) + recv[...].astype(f32))).astype(bf16)
    out[...] = low
    accumulate(bias, jnp.sum(low.astype(f32), axis=0, keepdims=True))


def embed_back_call(core, token, base, own, recv):
    tokens = base.shape[0]
    half = pl.BlockSpec((ROWS, HALF), lambda i, core: (i, core[0]))
    return pl.pallas_call(
        embed_back_kernel,
        out_shape=[
            jax.ShapeDtypeStruct((tokens, HALF), bf16),
            jax.ShapeDtypeStruct((1, HALF), f32),
        ],
        grid_spec=pltpu.PrefetchScalarGridSpec(
            num_scalar_prefetch=1,
            grid=(tokens // ROWS,),
            in_specs=[fixed(token.shape)] + [half] * 3,
            out_specs=[rows_spec(HALF), fixed((1, HALF))],
        ),
        compiler_params=params(8),
        cost_estimate=cost(tokens * D, tokens * D * 5),
    )(core, token, base, own, recv)


def pack_kernel(vec_per, *refs):
    *pieces, out = refs
    out[...] = jnp.zeros_like(out)
    at = 0
    for piece in pieces:
        for k in range(piece.shape[1] // BS):
            owner, row = divmod(at, vec_per // BS)
            out[owner, row : row + 1, :] = piece[:, k * BS : (k + 1) * BS]
            at += 1


def pack_call(pieces, owners, vec_per):
    if vec_per % BS:
        joined = jnp.concatenate(pieces, axis=1)[0]
        joined = jnp.pad(joined, (0, owners * vec_per - joined.shape[0])).reshape(owners, vec_per)
        joined = jnp.pad(joined, ((0, 0), (0, VEC_ROWS * BS - vec_per)))
        return joined.astype(bf16).reshape(owners, VEC_ROWS, BS)
    return pl.pallas_call(
        functools.partial(pack_kernel, vec_per),
        out_shape=jax.ShapeDtypeStruct((owners, VEC_ROWS, BS), f32),
        grid=(1,),
        in_specs=[fixed(p.shape) for p in pieces],
        out_specs=fixed((owners, VEC_ROWS, BS)),
        compiler_params=params(4),
        cost_estimate=cost(0, owners * vec_per * 8),
    )(*pieces).astype(bf16)


def embed_kernel(half, *refs):
    *parts, vec, weight, out = refs
    size = BASE_PIX // CHUNKS
    total = vec[:, :HALF]
    for c in range(CHUNKS):
        at = lax.rem(c + half[0] * (CHUNKS // 2), CHUNKS)
        rows = pl.ds(pl.multiple_of(at * size, size), size)
        total = total + dot(parts[c][...], weight[rows, :])
    out[...] = total.astype(bf16)


def embed_call(half, chunks, vec, weights):
    tokens = chunks[0].shape[0]
    return pl.pallas_call(
        embed_kernel,
        out_shape=jax.ShapeDtypeStruct((tokens, HALF), bf16),
        grid_spec=pltpu.PrefetchScalarGridSpec(
            num_scalar_prefetch=1,
            grid=(tokens // ROWS,),
            in_specs=[rows_spec(BASE_PIX // CHUNKS)] * CHUNKS
            + [fixed(vec.shape), fixed((BASE_PIX, HALF))],
            out_specs=rows_spec(HALF),
        ),
        compiler_params=params(),
        cost_estimate=cost(2 * tokens * BASE_PIX * HALF, tokens * BASE_PIX * 3),
    )(half, *[stay(c) for c in chunks], vec, stay(weights["base", 0]))


def qkv_kernel(layer, first, core, *refs):
    if first:
        own, recv, vec, weight, hid, normed, q_ref, k_ref, v_ref = refs
        mine, theirs = own[...].astype(f32), recv[...].astype(f32)
        low = core[0] == 0
        values = jnp.concatenate(
            [jnp.where(low, mine, theirs), jnp.where(low, theirs, mine)], axis=1
        )
    else:
        base, own, recv, vec, weight, hid, normed, q_ref, k_ref, v_ref = refs
        values = base[...] + (own[...].astype(f32) + recv[...].astype(f32))
    hid[...] = values
    unit, unused = norm_stats(values)
    low = (unit * vec_piece(vec, layer, "g1") + vec_piece(vec, layer, "s1")).astype(bf16)
    normed[...] = low
    made = dot(low, joined(weight, 0, D, 3))
    q_ref[...] = (made[:, :HALF] + vec_piece(vec, layer, "bq")).astype(bf16)
    k_ref[...] = made[:, HALF : 2 * HALF].astype(bf16)
    v_ref[...] = (made[:, 2 * HALF :] + vec_piece(vec, layer, "bv")).astype(bf16)


def qkv_call(layer, base, own, recv, core, vec, weights):
    tokens = own.shape[0]
    shape = lambda width, kind: jax.ShapeDtypeStruct((tokens, width), kind)
    outs = [shape(D, f32), pltpu.HBM((tokens, D), bf16)] + [shape(HALF, bf16)] * 3
    operands = ([] if base is None else [base]) + [own, recv]
    return pl.pallas_call(
        functools.partial(qkv_kernel, layer, base is None),
        out_shape=outs,
        grid_spec=pltpu.PrefetchScalarGridSpec(
            num_scalar_prefetch=1,
            grid=(tokens // ROWS,),
            in_specs=[rows_spec(o.shape[1]) for o in operands]
            + [fixed(vec.shape), fixed((3 * D, HALF))],
            out_specs=[rows_spec(o.shape[1]) for o in outs],
        ),
        compiler_params=params(),
        cost_estimate=cost(2 * tokens * D * 3 * HALF, tokens * D * 14),
    )(core, *operands, vec, weights["qkv", layer])


def head_masks():
    lane = lax.broadcasted_iota(jnp.int32, (1, 2 * HEAD_DIM), 1)
    low = (lane < HEAD_DIM).astype(f32).astype(bf16)
    high = (lane >= HEAD_DIM).astype(f32).astype(bf16)
    return low, high


def attend_kernel(
    layer, low_ref, high_ref, q_ref, k_ref, v_ref, seg_q, seg_k, vec, w_out, o_ref, lse_ref, part,
    scores_ref, top_ref, acc_ref,
):
    step = pl.program_id(0)
    first, last = low_ref[step], high_ref[step]
    masks = head_masks()
    scale = jnp.asarray(HEAD_DIM ** (-0.5), bf16)
    lane = lax.broadcasted_iota(jnp.int32, (1, BS), 1)
    sums = [(lane == HEAD_DIM).astype(f32).astype(bf16), (lane == 0).astype(f32).astype(bf16)]
    top_ref[...] = jnp.full(top_ref.shape, masked_score, f32)
    acc_ref[...] = jnp.zeros_like(acc_ref)
    seg_col = seg_q[...]

    def score_block(block, carried):
        rows = pl.ds(pl.multiple_of(block * ROWS, ROWS), ROWS)
        same = seg_col == seg_k[:, rows]
        for pair in range(HEADS // 2):
            cols = slice(pair * BS, (pair + 1) * BS)
            q_two = q_ref[:, cols] * scale
            k_two = k_ref[rows, cols]
            for side in range(2):
                head = 2 * pair + side
                scores = jnp.where(same, dot_nt(q_two * masks[side], k_two), masked_score)
                scores_ref[head, block] = scores
                top = top_ref[head]
                for piece in range(ROWS // BS):
                    top = jnp.maximum(top, scores[:, piece * BS : (piece + 1) * BS])
                top_ref[head] = top
        return carried

    lax.fori_loop(first, last, score_block, 0)
    tops = [jnp.max(top_ref[head], axis=1, keepdims=True) for head in range(HEADS)]

    def mix_block(block, carried):
        rows = pl.ds(pl.multiple_of(block * ROWS, ROWS), ROWS)
        for pair in range(HEADS // 2):
            v_two = v_ref[rows, pair * BS : (pair + 1) * BS]
            for side in range(2):
                head = 2 * pair + side
                expo = jnp.exp(scores_ref[head, block] - tops[head]).astype(bf16)
                acc_ref[head] += dot(expo, v_two * masks[side] + sums[side])
        return carried

    lax.fori_loop(first, last, mix_block, 0)
    totals = jnp.zeros((ROWS, BS), f32)
    for pair in range(HEADS // 2):
        sides = []
        for side in range(2):
            head = 2 * pair + side
            mixed = acc_ref[head]
            at = HEAD_DIM * (1 - side)
            total = mixed[:, at : at + 1]
            totals = jnp.where(lane == head, tops[head] + jnp.log(total), totals)
            sides.append(mixed * (1.0 / total))
        o_ref[:, pair * BS : (pair + 1) * BS] = jnp.where(lane < HEAD_DIM, *sides).astype(bf16)
    lse_ref[...] = totals.T[0:8, :]
    low = o_ref[...]
    bias = vec_piece(vec, layer, "bo")
    part[...] = (dot(low, joined(w_out, 0, HALF, TENSOR)) + bias).astype(bf16)


def attend_call(layer, first, last, queries, keys, values, seg_col, seg_row, vec, weights):
    tokens = queries.shape[0]
    return pl.pallas_call(
        functools.partial(attend_kernel, layer),
        out_shape=[
            jax.ShapeDtypeStruct((tokens, HALF), bf16),
            jax.ShapeDtypeStruct((8, tokens), f32),
            jax.ShapeDtypeStruct((tokens, D), bf16),
        ],
        grid_spec=pltpu.PrefetchScalarGridSpec(
            num_scalar_prefetch=2,
            grid=(tokens // ROWS,),
            in_specs=[
                rows_spec(HALF),
                fixed(keys.shape),
                fixed(values.shape),
                rows_spec(1),
                fixed(seg_row.shape),
                fixed(vec.shape),
                fixed((D, HALF)),
            ],
            out_specs=[
                rows_spec(HALF),
                pl.BlockSpec((8, ROWS), lambda i, *_: (0, i)),
                rows_spec(D),
            ],
            scratch_shapes=[
                pltpu.VMEM((HEADS, tokens // ROWS, ROWS, ROWS), f32),
                pltpu.VMEM((HEADS, ROWS, BS), f32),
                pltpu.VMEM((HEADS, ROWS, BS), f32),
            ],
        ),
        compiler_params=params(),
        cost_estimate=cost(8 * HEADS * tokens * tokens * BS, tokens * D * 8, HEADS * tokens * tokens),
    )(first, last, queries, keys, values, seg_col, seg_row, vec, weights["out", layer])


def gelu_parts(values):
    cdf = 0.5 * (1.0 + lax.erf(values * 0.7071067811865476))
    pdf = 0.3989422804014327 * jnp.exp(-0.5 * values * values)
    return values * cdf, cdf + values * pdf


def mlp_kernel(layer, base, own, recv, vec, w_up, w_down, hid, normed, act, slope, part):
    values = base[...] + (own[...].astype(f32) + recv[...].astype(f32))
    hid[...] = values
    unit, unused = norm_stats(values)
    low = (unit * vec_piece(vec, layer, "g2") + vec_piece(vec, layer, "s2")).astype(bf16)
    normed[...] = low
    bias_up = vec_piece(vec, layer, "b1")
    for pair in range(HALF_FF // D):
        area = slice(pair * D, (pair + 1) * D)
        up = dot(low, joined(w_up, pair * 2 * D, D, 2)) + bias_up[:, area]
        gelu, grad = gelu_parts(up)
        act[:, area] = gelu.astype(bf16)
        slope[:, area] = grad.astype(bf16)
    bias_down = vec_piece(vec, layer, "b2")
    part[...] = (dot(act[...], joined(w_down, 0, HALF_FF, TENSOR)) + bias_down).astype(bf16)


def mlp_call(layer, base, own, recv, vec, weights):
    tokens = base.shape[0]
    shape = lambda width, kind: jax.ShapeDtypeStruct((tokens, width), kind)
    kept = lambda width: pltpu.HBM((tokens, width), bf16)
    outs = [shape(D, f32), kept(D), kept(HALF_FF), kept(HALF_FF), shape(D, bf16)]
    return pl.pallas_call(
        functools.partial(mlp_kernel, layer),
        out_shape=outs,
        grid=(tokens // ROWS,),
        in_specs=[rows_spec(D)] * 3
        + [
            fixed(vec.shape),
            fixed((2 * HALF_FF, HALF)),
            fixed((2 * HALF_FF, HALF)),
        ],
        out_specs=[rows_spec(o.shape[1]) for o in outs],
        compiler_params=params(),
        cost_estimate=cost(4 * tokens * D * HALF_FF, tokens * D * 24, 2 * tokens * HALF_FF),
    )(base, own, recv, vec, weights["up", layer], weights["down", layer])


def mlp_back_kernel(layer, summed, *refs):
    if summed:
        base, own, recv, *refs = refs
        (hid, slope, vec, w_up, w_down, grad_full, grad_low, du_ref, back, dgain, dshift, db1, db2) = refs
        values = base[...].astype(f32) + (own[...].astype(f32) + recv[...].astype(f32))
        grad_full[...] = values
        low = values.astype(bf16)
    else:
        base, valid, *refs = refs
        (hid, slope, vec, w_up, w_down, grad_low, du_ref, back, dgain, dshift, db1, db2) = refs
        low = (base[...].astype(f32) * valid[...]).astype(bf16)
    grad_low[...] = low
    accumulate(db2, jnp.sum(low.astype(f32), axis=0, keepdims=True))
    for part in range(HALF_FF // D):
        area = slice(part * D, (part + 1) * D)
        rows = jnp.concatenate(
            [w_down[p * HALF_FF + part * D : p * HALF_FF + (part + 1) * D, :] for p in range(TENSOR)],
            axis=1,
        )
        du_ref[:, area] = (dot_nt(low, rows) * slope[:, area].astype(f32)).astype(bf16)
    grad_normed = dot_nt(du_ref[...], joined(w_up, 0, D, HALF_FF // HALF))
    accumulate(db1, jnp.sum(du_ref[...].astype(f32), axis=0, keepdims=True))
    part_back, gain_grad, shift_grad = norm_back(hid[...], vec_piece(vec, layer, "g2"), grad_normed)
    back[...] = part_back.astype(bf16)
    accumulate(dgain, gain_grad)
    accumulate(dshift, shift_grad)


def mlp_back_call(layer, base, own, recv, valid, hid, slope, vec, weights):
    tokens = base.shape[0]
    summed = own is not None
    shape = lambda width, kind: jax.ShapeDtypeStruct((tokens, width), kind)
    line = lambda width: jax.ShapeDtypeStruct((1, width), f32)
    outs = ([shape(D, f32)] if summed else []) + [shape(D, bf16), shape(HALF_FF, bf16), shape(D, bf16)]
    lines = [line(D), line(D), line(HALF_FF), line(D)]
    extra = [own, recv] if summed else [valid]
    return pl.pallas_call(
        functools.partial(mlp_back_kernel, layer, summed),
        out_shape=outs + lines,
        grid=(tokens // ROWS,),
        in_specs=[rows_spec(D)]
        + [rows_spec(e.shape[1]) for e in extra]
        + [
            rows_spec(D),
            rows_spec(HALF_FF),
            fixed(vec.shape),
            fixed((2 * HALF_FF, HALF)),
            fixed((2 * HALF_FF, HALF)),
        ],
        out_specs=[rows_spec(o.shape[1]) for o in outs] + [fixed(o.shape) for o in lines],
        compiler_params=params(),
        cost_estimate=cost(4 * tokens * D * HALF_FF, tokens * D * 24),
    )(base, *extra, stay(hid), stay(slope), vec, weights["up", layer], weights["down", layer])


def attend_back_kernel(
    low_ref, high_ref, base, own, recv, q_ref, k_ref, v_ref, o_ref, lse_ref, seg_k, seg_q, w_out,
    full_ref, grad_low, dq_ref, dk_ref, dv_ref, dbo, dk_acc, dv_acc, dq_acc, do_ref,
):
    step = pl.program_id(0)

    @pl.when(step == 0)
    def _():
        dk_acc[...] = jnp.zeros_like(dk_acc)
        dv_acc[...] = jnp.zeros_like(dv_acc)

    values = base[...].astype(f32) + (own[...].astype(f32) + recv[...].astype(f32))
    full_ref[...] = values
    low = values.astype(bf16)
    grad_low[...] = low
    accumulate(dbo, jnp.sum(low.astype(f32), axis=0, keepdims=True))
    do_ref[...] = dot_nt(low, joined(w_out, 0, HALF, TENSOR)).astype(bf16)
    product = do_ref[...].astype(f32) * o_ref[...].astype(f32)
    head = lax.broadcasted_iota(jnp.int32, (8, HALF), 0)
    lane = lax.broadcasted_iota(jnp.int32, (8, HALF), 1)
    pick = ((lane >= head * HEAD_DIM) & (lane < (head + 1) * HEAD_DIM)).astype(f32)
    high, rest = split(product)
    pick = pick.astype(bf16)
    inner = dot_nt(pick, high) + dot_nt(pick, rest)
    dq_acc[...] = jnp.zeros_like(dq_acc)
    masks = head_masks()
    scale = jnp.asarray(HEAD_DIM ** (-0.5), bf16)
    seg_row = seg_q[...]

    def one_block(block, carried):
        rows = pl.ds(pl.multiple_of(block * KEYS, KEYS), KEYS)
        same = seg_k[rows, :] == seg_row
        for pair in range(HEADS // 2):
            cols = slice(pair * BS, (pair + 1) * BS)
            q_two = q_ref[:, cols] * scale
            do_two = do_ref[:, cols]
            k_two = k_ref[rows, cols]
            v_two = v_ref[rows, cols]
            dv_two = dk_two = dq_two = None
            for side in range(2):
                at = 2 * pair + side
                q_one = q_two * masks[side]
                do_one = do_two * masks[side]
                scores = dot_nt(k_two, q_one)
                prob = jnp.where(same, jnp.exp(scores - lse_ref[at : at + 1, :]), 0.0)
                grad_prob = dot_nt(v_two, do_one)
                grad_scores = (prob * (grad_prob - inner[at : at + 1, :])).astype(bf16)
                dv_one = dot(prob.astype(bf16), do_one)
                dk_one = dot(grad_scores, q_one)
                dq_one = dot_tn(grad_scores, k_two * masks[side])
                dq_two = dq_one if dq_two is None else dq_two + dq_one
                dv_two = dv_one if dv_two is None else dv_two + dv_one
                dk_two = dk_one if dk_two is None else dk_two + dk_one
            dv_acc[rows, cols] += dv_two
            dk_acc[rows, cols] += dk_two
            dq_acc[:, cols] += dq_two
        return carried

    lax.fori_loop(low_ref[step], high_ref[step], one_block, 0)
    dq_ref[...] = (dq_acc[...] * HEAD_DIM ** (-0.5)).astype(bf16)

    @pl.when(step == pl.num_programs(0) - 1)
    def _():
        dk_ref[...] = dk_acc[...].astype(bf16)
        dv_ref[...] = dv_acc[...].astype(bf16)


def attend_back_call(
    layer, first, last, base, own, recv, queries, keys, values, mixed, lse, seg_col, seg_row, weights
):
    tokens = base.shape[0]
    shape = lambda width, kind: jax.ShapeDtypeStruct((tokens, width), kind)
    whole = (tokens, HALF)
    return pl.pallas_call(
        attend_back_kernel,
        out_shape=[
            shape(D, f32),
            shape(D, bf16),
            shape(HALF, bf16),
            shape(HALF, bf16),
            shape(HALF, bf16),
            jax.ShapeDtypeStruct((1, D), f32),
        ],
        grid_spec=pltpu.PrefetchScalarGridSpec(
            num_scalar_prefetch=2,
            grid=(tokens // ROWS,),
            in_specs=[
                rows_spec(D),
                rows_spec(D),
                rows_spec(D),
                rows_spec(HALF),
                fixed(whole),
                fixed(whole),
                rows_spec(HALF),
                pl.BlockSpec((8, ROWS), lambda i, *_: (0, i)),
                fixed(seg_col.shape),
                pl.BlockSpec((1, ROWS), lambda i, *_: (0, i)),
                fixed((D, HALF)),
            ],
            out_specs=[
                rows_spec(D),
                rows_spec(D),
                rows_spec(HALF),
                fixed(whole),
                fixed(whole),
                fixed((1, D)),
            ],
            scratch_shapes=[
                pltpu.VMEM(whole, f32),
                pltpu.VMEM(whole, f32),
                pltpu.VMEM((ROWS, HALF), f32),
                pltpu.VMEM((ROWS, HALF), bf16),
            ],
        ),
        compiler_params=params(),
        cost_estimate=cost(14 * HEADS * tokens * tokens * BS, tokens * D * 20, HEADS * tokens * tokens),
    )(
        first, last, base, own, recv, stay(queries), stay(keys), stay(values), stay(mixed), lse,
        seg_col, seg_row, weights["out", layer],
    )


def qkv_back_kernel(layer, dq, dk, dv, hid, vec, weight, back, dgain, dshift, dbq, dbv):
    grad_three = jnp.concatenate([dq[...], dk[...], dv[...]], axis=1)
    grad_normed = dot_nt(grad_three, joined(weight, 0, D, 3))
    part_back, gain_grad, shift_grad = norm_back(hid[...], vec_piece(vec, layer, "g1"), grad_normed)
    back[...] = part_back.astype(bf16)
    accumulate(dgain, gain_grad)
    accumulate(dshift, shift_grad)
    accumulate(dbq, jnp.sum(dq[...].astype(f32), axis=0, keepdims=True))
    accumulate(dbv, jnp.sum(dv[...].astype(f32), axis=0, keepdims=True))


def qkv_back_call(layer, dq, dk, dv, hid, vec, weights):
    tokens = dq.shape[0]
    line = lambda width: jax.ShapeDtypeStruct((1, width), f32)
    lines = [line(D), line(D), line(HALF), line(HALF)]
    return pl.pallas_call(
        functools.partial(qkv_back_kernel, layer),
        out_shape=[jax.ShapeDtypeStruct((tokens, D), bf16)] + lines,
        grid=(tokens // ROWS,),
        in_specs=[rows_spec(HALF)] * 3
        + [
            rows_spec(D),
            fixed(vec.shape),
            fixed((3 * D, HALF)),
        ],
        out_specs=[rows_spec(D)] + [fixed(o.shape) for o in lines],
        compiler_params=params(),
        cost_estimate=cost(2 * tokens * D * 3 * HALF, tokens * D * 10),
    )(dq, dk, dv, stay(hid), vec, weights["qkv", layer])


def split(values):
    high = values.astype(bf16)
    return high, (values - high.astype(f32)).astype(bf16)


def product(left, right, left_dim, right_dim):
    def one(a, b):
        return lax.dot_general(
            a, b, (((left_dim,), (right_dim,)), ((), ())), preferred_element_type=f32
        )

    return one(left[0], right[0]) + (one(left[0], right[1]) + one(left[1], right[0]))


def owner_kernel(per, used, home, near, far, master, left, right, moment, variance, grad, out, out_mom, out_var):
    here = range(per)
    first = pl.program_id(0) * per
    lefts = [split(left[i]) for i in here]
    rights = [split(right[i]) for i in here]
    rotated = []
    for i in here:
        rows = slice(i * BS, (i + 1) * BS)
        tile = jnp.where(home[0] > 0, near[rows, :].astype(f32), far[rows, :].astype(f32))
        tile = jnp.where(used[first + i] > 0, tile, 0.0)
        grad[i] = tile
        tile = tile.astype(bf16)
        rotated.append(split(dot_tn(lefts[i][0], tile) + dot_tn(lefts[i][1], tile)))
    rotated = [product(rotated[i], rights[i], 1, 0) for i in here]
    steps = []
    for i in here:
        new_moment = decay * moment[i] + (1.0 - decay) * rotated[i]
        new_variance = decay * variance[i] + (1.0 - decay) * rotated[i] * rotated[i]
        out_mom[i] = new_moment
        out_var[i] = new_variance
        steps.append(split(new_moment / (jnp.sqrt(new_variance) + adam_eps)))
    returned = [split(product(lefts[i], steps[i], 1, 0)) for i in here]
    returned = [product(returned[i], rights[i], 1, 1) for i in here]
    for i in here:
        out[i] = master[i] - matrix_rate * returned[i]


def owner_call(used, home, near, far, *arrays):
    count = arrays[0].shape[0]
    per = min(8, count)
    block = pl.BlockSpec((per, BS, BS), lambda i, *_: (i, 0, 0))
    return pl.pallas_call(
        functools.partial(owner_kernel, per),
        out_shape=[jax.ShapeDtypeStruct(arrays[0].shape, f32)] * 4,
        grid_spec=pltpu.PrefetchScalarGridSpec(
            num_scalar_prefetch=2,
            grid=(count // per,),
            in_specs=[pl.BlockSpec((per * BS, BS), lambda i, *_: (i, 0))] * 2 + [block] * 5,
            out_specs=[block] * 4,
        ),
        compiler_params=params(),
        cost_estimate=cost(count * 88 * BS**3, count * BS * BS * 38),
    )(used, home, stay(near), stay(far), *arrays)


def reduce_kernel(carrying, last, *refs):
    block, arrived, *refs = refs
    total = block[...].astype(f32) + arrived[...].astype(f32)
    if carrying:
        carried, *refs = refs
        total = total + carried[...].astype(f32)
    if last:
        [out] = refs
    else:
        following, out, later = refs
        later[...] = following[...]
    out[...] = total.astype(bf16)


def reduce_call(j, n, buffer, arrived, carried, payload, x_rel=0):
    last = j >= 2 or x_rel == 1
    at = lambda j, x_rel: pl.BlockSpec((payload, BS), lambda i: ((j * 2 + x_rel) * 2 + n, 0))
    whole = fixed((payload, BS))
    operands = [stay(buffer), stay(arrived)] + ([] if carried is None else [stay(carried)])
    specs = [at(j, x_rel)] + [whole] * (len(operands) - 1)
    if not last:
        operands.append(stay(buffer))
        specs.append(at(j + 2, 1))
    outs = [pltpu.HBM((payload, BS), bf16)] * (1 if last else 2)
    made = pl.pallas_call(
        functools.partial(reduce_kernel, carried is not None, last),
        out_shape=outs,
        grid=(1,),
        in_specs=specs,
        out_specs=[whole] * len(outs),
        compiler_params=params(8),
        cost_estimate=cost(payload * BS * 3, payload * BS * 12),
    )(*operands)
    return (made[0], None) if last else made


class Routes:
    def __init__(self, dp_n):
        pairs = [(d, t) for d in range(dp_n) for t in range(TENSOR)]
        at = lambda d, t: d * TENSOR + t
        home = [(d, t) for d, t in pairs if d % 2 == t]
        away = [(d, t) for d, t in pairs if d % 2 != t]
        self.core_all = [(at(d, t), at(d ^ 1, t)) for d, t in pairs]
        self.core_out = [(at(d, t), at(d ^ 1, t)) for d, t in home]
        self.core_in = [(at(d, t), at(d ^ 1, t)) for d, t in away]
        self.y_all = [(at(d, t), at(d, 1 - t)) for d, t in pairs]
        self.y_out = [(at(d, t), at(d, 1 - t)) for d, t in home]
        self.y_in = [(at(d, t), at(d, 1 - t)) for d, t in away]
        self.x_home = [(at(d, t), at(d ^ 2, t)) for d, t in home]
        self.x_away = [(at(d, t), at(d ^ 2, t)) for d, t in away]
        self.x_all = [(at(d, t), at(d ^ 2, t)) for d, t in pairs]
        self.z_all = [(at(d, t), at((d + 4) % dp_n, t)) for d, t in pairs]
        self.z_home = [(at(d, t), at((d + 4) % dp_n, t)) for d, t in home]


def send(value, route):
    return lax.ppermute(value, AXES, route)


def shards(
    patches,
    cotangent,
    image_size,
    block_slot,
    pinv,
    master_slots,
    left_basis,
    right_basis,
    mom_slots,
    var_slots,
    vec_master,
    vec_mom,
    vec_var,
):
    dp_n = lax.axis_size("dp")
    dp_pos = lax.axis_index("dp")
    y_pos = lax.axis_index("tensor")
    core = dp_pos % 2
    home = core == y_pos
    routes = Routes(dp_n)
    grid3 = dp_n == 16
    x_pos = (dp_pos // 2) % 2
    half_at = (x_pos if grid3 else x_pos * 0).astype(jnp.int32).reshape(1)
    tokens_n = patches.shape[0]
    slots_per = master_slots.shape[1]
    vec_per = vec_master.shape[1]
    slots_n = slots_per * dp_n
    payload = slots_per * BS + VEC_ROWS

    patches = jnp.where(home, patches, send(patches, routes.core_out))
    cotangent = jnp.where(home, cotangent, send(cotangent, routes.core_out))
    size_row = jnp.where(home, image_size, send(image_size, routes.core_out))[0]
    own_slots = block_slot[0]
    slot_other = send(block_slot, routes.y_all)

    lengths = jnp.where(
        size_row == 0, LEN_A, jnp.where(size_row == 1, LEN_B, jnp.where(size_row == 2, LEN_C, 0))
    )
    order = jnp.arange(IMG_DEV)
    ends_at = jnp.sum(jnp.where(order[None, :] <= order[:, None], lengths[None, :], 0), axis=1)
    places = jnp.arange(tokens_n)
    segment = jnp.sum((places[:, None] >= ends_at[None, :]).astype(jnp.int32), axis=1)
    in_image = segment[:, None] == order[None, :]
    select = jnp.stack(
        [jnp.any(in_image & (size_row == s)[None, :], axis=1) for s in range(3)], axis=1
    )
    valid_col = (segment < IMG_DEV).astype(f32)[:, None]
    seg_col = segment[:, None]
    seg_row = segment[None, :]
    blocks_n = tokens_n // ROWS
    starts = jnp.arange(blocks_n) * ROWS
    begun = ends_at[None, :] <= starts[:, None]
    first_tok = jnp.max(jnp.where(begun, ends_at[None, :], 0), axis=1)
    after = ends_at[None, :] > (starts + ROWS - 1)[:, None]
    last_tok = jnp.min(jnp.where(after, ends_at[None, :], tokens_n), axis=1)
    first_blk = (first_tok // ROWS).astype(jnp.int32)
    last_blk = ((last_tok + ROWS - 1) // ROWS).astype(jnp.int32)
    first_key = (first_tok // KEYS).astype(jnp.int32)
    last_key = ((last_tok + KEYS - 1) // KEYS).astype(jnp.int32)

    select_low = select.astype(bf16)
    class_col = jnp.sum(jnp.where(select, jnp.arange(1, 4)[None, :], 0), axis=1, keepdims=True) - 1
    present = jnp.any(select.reshape(blocks_n, ROWS, 3), axis=1).astype(jnp.int32)

    def expand(which, rows):
        return expand_call(which, present, half_at, rows, class_col, pinv)

    vec_low = jnp.pad(vec_master[0].astype(bf16), (0, VEC_ROWS * BS - vec_per))
    own_pack = jnp.concatenate(
        [
            master_slots[0].astype(bf16).reshape(slots_per * BS, BS),
            vec_low.reshape(VEC_ROWS, BS),
        ],
        axis=0,
    )
    flag = home.astype(jnp.int32).reshape(1)
    if grid3:
        z_pos = dp_pos // 4
        pack = own_pack
        chunks, first, second, owner = [], [], [], []
        middle_row = slots_per * BS // 2
        for j in range(4):
            beside_x, beside_y = send(pack, routes.x_all), send(pack, routes.y_all)
            further = [send(pack, routes.z_all)] if j < 3 else []
            work = [slot_other] if j == 0 else []
            beside_x, beside_y, patches, chunk, *more = fence(
                beside_x, beside_y, patches, expand(j, patches), *further, *work
            )
            chunks.append(chunk)
            if j < 3:
                further = more.pop(0)
            if j == 0:
                [slot_other] = more
            corner = jnp.concatenate(
                [send(beside_x[:middle_row], routes.y_all), send(beside_y[middle_row:], routes.x_all)],
                axis=0,
            )
            near_two = send(jnp.where(home, beside_y, pack), routes.core_all)
            far_two = send(jnp.where(home, corner, beside_x), routes.core_all)
            first += [pack, near_two, beside_x, far_two]
            second += [beside_y, near_two, corner, far_two]
            for x_rel in range(2):
                for n in range(2):
                    owner.append(((z_pos - j) % 4) * 4 + (x_pos ^ x_rel) * 2 + (core ^ n))
            if j < 3:
                pack = further
        first = [v[None] for v in first]
        second = [v[None] for v in second]
        owner = jnp.stack(owner).astype(jnp.int32)
    else:
        everything = lax.all_gather(own_pack, AXES, axis=0)
        everything = everything.reshape(dp_n, TENSOR, payload, BS)
        first = [jnp.where(core == 0, everything[:, 0], everything[:, 1])]
        second = []
        owner = jnp.arange(dp_n, dtype=jnp.int32)
        chunks = [expand(c, patches) for c in range(CHUNKS)]
    slot_list = jnp.where(home, block_slot, slot_other)[0]
    named = slot_list[None, :] == jnp.arange(slots_n)[:, None]
    used = jnp.any(named, axis=1)
    drow = jnp.where(used, jnp.sum(jnp.where(named, TARGET_ROW[None, :], 0), axis=1), -1)
    dcol = jnp.sum(jnp.where(named, TARGET_COL[None, :], 0), axis=1)
    weights, vec_rows = gather_tiles(first, second, owner, drow, dcol, flag, slots_per, dp_n)
    vec = vec_rows.reshape(dp_n, VEC_ROWS * BS)[:, :vec_per].astype(f32).reshape(1, dp_n * vec_per)

    embedded = embed_call(half_at, chunks, vec, weights)
    embedded_other = send(embedded, routes.core_all)
    core_flag = core.astype(jnp.int32).reshape(1)

    caches = []
    hidden, own, recv = None, embedded, embedded_other
    for layer in range(LAYERS):
        hidden, normed, queries, keys, values = qkv_call(
            layer, hidden, own, recv, core_flag, vec, weights
        )
        mixed, lse, part = attend_call(
            layer, first_blk, last_blk, queries, keys, values, seg_col, seg_row, vec, weights
        )
        other = send(part, routes.core_all)
        middle, normed2, act, slope, own = mlp_call(layer, hidden, part, other, vec, weights)
        recv = send(own, routes.core_all)
        caches.append((hidden, normed, queries, keys, values, mixed, lse, middle, normed2, act, slope))
        hidden = middle
    out_low = ((hidden + (own.astype(f32) + recv.astype(f32))) * valid_col).astype(bf16)

    owners = jnp.arange(dp_n)
    if grid3:
        place = (
            ((z_pos - 1 - owners // 4) % 4) * 4
            + (x_pos ^ ((owners // 2) % 2)) * 2
            + (core ^ (owners % 2))
        ).astype(jnp.int32)
    else:
        place = owners.astype(jnp.int32)
    slot_owner = slot_list // slots_per
    owner_place = jnp.sum(
        jnp.where(slot_owner[:, None] == owners[None, :], place[None, :], 0), axis=1
    )
    tile_pos = (owner_place * payload + (slot_list % slots_per) * BS).astype(jnp.int32)
    vec_pos = (place * payload + slots_per * BS).astype(jnp.int32)
    total_rows = dp_n * payload
    where_to = jnp.concatenate([half_at, flag if grid3 else flag * 0 + 1])
    offsets = {"base": 0}
    count = BASE_PIX // BS * (HALF // BS)
    for layer in range(LAYERS):
        for name, size in (("qkv", 3 * D * HALF), ("out", D * HALF), ("up", D * HALF_FF), ("down", D * HALF_FF)):
            offsets[name, layer] = count
            count += size // (BS * BS)

    def place_tiles(key, matrix, arrived, buffer):
        tiles = matrix.size // (BS * BS)
        pos = tile_pos[offsets[key] : offsets[key] + tiles]
        rows_n = matrix.shape[0] // 2 if matrix.shape[0] > HALF else HALF
        return scatter_matrix(pos, matrix, arrived, where_to, buffer, total_rows, rows_n)

    def place_base(rel, matrix, arrived, buffer):
        size = BASE_PIX * HALF // (BS * BS) // 2
        low_pos, high_pos = tile_pos[:size], tile_pos[size : 2 * size]
        pos = jnp.where(half_at[0] == rel, low_pos, high_pos)
        return scatter_matrix(pos, matrix, arrived, where_to, buffer, total_rows, D)

    def over(matrix):
        return send(matrix, routes.y_in) if grid3 else None

    def beside(matrix):
        return send(other_half(half_at, matrix), routes.x_away) if grid3 else None

    def summed(matrix, arrived):
        return half_sum(half_at, matrix, arrived) if grid3 else None

    def hold(*arrays):
        kept = [a for a in arrays if a is not None]
        done = iter(fence(*kept))
        return [None if a is None else next(done) for a in arrays]

    top, low = 1, 0
    vec_grads = [None] * LAYERS

    def mlp_step(layer, grad, own, recv):
        middle, normed2, act, slope = caches[layer][7:11]
        made = mlp_back_call(layer, grad, own, recv, valid_col, middle, slope, vec, weights)
        if own is not None:
            return made
        return [made[0]] + list(made)

    def attend_step(layer, grad, part, other, lse):
        hid_in, normed, queries, keys, values, mixed = caches[layer][:6]
        return attend_back_call(
            layer, first_key, last_key, grad, part, other, queries, keys, values, mixed, lse,
            seg_col, seg_row, weights,
        )

    grad, grad_low, du, part, dg2, ds2, db1, db2 = mlp_step(top, cotangent, None, None)
    other = send(part, routes.core_all)
    gd1 = dot_tn(caches[top][9], grad_low).astype(bf16)
    gu1 = dot_tn(caches[top][8], du).astype(bf16)
    ad1 = over(gd1)
    lse, gu1 = fence(caches[top][6], gu1)
    xu1 = beside(gu1)
    grad, grad_low, dq, dk, dv, dbo = attend_step(top, grad, part, other, lse)
    vec, dbo, ad1, xu1, out_low = hold(vec, dbo, ad1, xu1, out_low)
    au1 = over(summed(gu1, xu1))
    own, dg1, ds1, dbq, dbv = qkv_back_call(top, dq, dk, dv, caches[top][0], vec, weights)
    recv = send(own, routes.core_all)
    go1 = dot_tn(caches[top][5], grad_low).astype(bf16)
    gq1 = dot_tn(caches[top][1], jnp.concatenate([dq, dk, dv], axis=1)).astype(bf16)
    vec_grads[top] = [dg1, ds1, dbq, dbv, dbo, dg2, ds2, db1, db2]
    xq1, ao1 = beside(gq1), over(go1)
    grad, grad_low, du, part, dg2, ds2, db1, db2 = mlp_step(low, grad, own, recv)
    other = send(part, routes.core_all)
    db2, xq1, au1 = hold(db2, xq1, au1)
    aq1 = over(summed(gq1, xq1))
    gd0 = dot_tn(caches[low][9], grad_low).astype(bf16)
    gu0 = dot_tn(caches[low][8], du).astype(bf16)
    lse, gd0, gu0, ao1, aq1 = hold(caches[low][6], gd0, gu0, ao1, aq1)
    ad0 = over(gd0)
    xu0 = beside(gu0)
    buffer = place_tiles(("down", top), gd1, ad1, None)
    buffer = place_tiles(("up", top), gu1, au1, buffer)
    grad, grad_low, dq, dk, dv, dbo = attend_step(low, grad, part, other, lse)
    vec, dbo, ad0, xu0, buffer = hold(vec, dbo, ad0, xu0, buffer)
    au0 = over(summed(gu0, xu0))
    own, dg1, ds1, dbq, dbv = qkv_back_call(low, dq, dk, dv, caches[low][0], vec, weights)
    recv = send(own, routes.core_all)
    gq0 = dot_tn(caches[low][1], jnp.concatenate([dq, dk, dv], axis=1)).astype(bf16)
    vec_grads[low] = [dg1, ds1, dbq, dbv, dbo, dg2, ds2, db1, db2]
    xq0 = beside(gq0)
    turn = jnp.zeros((8, BS), f32)
    grad_emb, grad_emb_bias = embed_back_call(core_flag, turn, grad, own, recv)
    middle = CHUNKS // 2

    def base_grad(parts):
        return jnp.concatenate([dot_tn(c, grad_emb).astype(bf16) for c in parts], axis=0)

    gbt = base_grad(chunks[middle:])
    gbt, au0, xq0 = hold(gbt, au0, xq0)
    xb = send(gbt, routes.x_away) if grid3 else None
    aq0 = over(summed(gq0, xq0))
    gbm = base_grad(chunks[:middle])
    vec_grad = pack_call([grad_emb_bias] + vec_grads[0] + vec_grads[1], dp_n, vec_per)
    go0 = dot_tn(caches[low][5], grad_low).astype(bf16)
    ao0, av = over(go0), over(vec_grad)
    buffer = place_tiles(("out", top), go1, ao1, buffer)
    buffer = place_tiles(("qkv", top), gq1, aq1, buffer)
    buffer = place_tiles(("down", low), gd0, ad0, buffer)
    gbm, xb, aq0, av, buffer = hold(gbm, xb, aq0, av, buffer)
    ab = over(half_sum(half_at * 0, gbm, xb)) if grid3 else None
    buffer = place_tiles(("up", low), gu0, au0, buffer)
    buffer = place_base(1, gbt, None, buffer)
    buffer = scatter_vec(vec_pos, vec_grad, av, buffer)
    buffer = place_tiles(("qkv", low), gq0, aq0, buffer)
    buffer = place_tiles(("out", low), go0, ao0, buffer)
    base_weight = weights["base", 0]
    ab, buffer, base_weight, out_low = hold(ab, buffer, base_weight, out_low)
    weights["base", 0] = base_weight
    buffer = place_base(0, gbm, ab, buffer)

    if grid3:
        token = jnp.zeros((8, BS), f32)
        order = (1, 0)
        resized = resize_call(weights, pinv)
        carried = {n: None for n in order}
        blocks = buffer.reshape(4, 2, 2, payload, BS)
        across = {order[1]: send(blocks[0, 1, order[1]], routes.x_home), order[0]: None}
        following = {order[1]: blocks[1, 1, order[1]], order[0]: blocks[2, 1, order[0]]}
        far_side = send(blocks[0, 1, order[0]], routes.z_home)
        carried[order[0]] = send(blocks[0, 0, order[0]], routes.z_home)
        rounded = {}
        for j in range(4):
            for n in order:
                extra = None
                if j == 0 and n == order[0]:
                    token, far_side, resized = hold(token, far_side, resized)
                    later, unused = reduce_call(1, n, buffer, far_side, None, payload, 1)
                    across[n] = send(later, routes.x_home)
                    continue
                token, across[n], carried[n], extra = hold(token, across[n], carried[n], extra)
                if extra is not None:
                    resized = extra
                arrived = across[n]
                if j < 3:
                    across[n] = send(following[n], routes.x_home)
                total, following[n] = reduce_call(j, n, buffer, arrived, carried[n], payload)
                if j < 3:
                    carried[n] = send(total, routes.z_home)
                else:
                    rounded[n] = total
        near_grad, far_grad = rounded[0], send(rounded[1], routes.core_out)
    else:
        held = buffer.reshape(dp_n, 1, payload, BS).astype(f32)
        nothing = jnp.zeros_like(held)
        both = jnp.concatenate(
            [jnp.where(core == 0, held, nothing), jnp.where(core == 0, nothing, held)], axis=1
        )
        used_rows = jnp.repeat(used, BS).reshape(dp_n, 1, slots_per * BS, 1)
        used_rows = jnp.concatenate(
            [used_rows, jnp.ones((dp_n, 1, VEC_ROWS, 1), bool)], axis=2
        )
        both = jnp.where(used_rows, both, 0.0).reshape(dp_n * TENSOR * payload, BS)
        near_grad = lax.psum_scatter(both, AXES, scatter_dimension=0, tiled=True).astype(bf16)
        far_grad = near_grad
        resized = resize_call(weights, pinv)

    output = jnp.where(home, out_low, send(out_low, routes.y_out)).astype(f32)
    grad_pixels = sum(
        dot(grad_emb * select_low[:, s : s + 1], resized[s]) for s in range(3)
    ).astype(bf16)
    pixels_other = send(grad_pixels, routes.core_all)
    pixel_sides = [
        grad_pixels[:, s * HALF : (s + 1) * HALF].astype(f32)
        + pixels_other[:, s * HALF : (s + 1) * HALF].astype(f32)
        for s in range(TENSOR)
    ]
    near = jnp.where(core == 0, pixel_sides[0], pixel_sides[1])
    far = jnp.where(core == 0, pixel_sides[1], pixel_sides[0]).astype(bf16)
    patch_grad = jnp.where(home, near, send(far, routes.y_out).astype(f32))

    my_slots = dp_pos * slots_per + jnp.arange(slots_per)
    mine_used = jnp.any(own_slots[None, :] == my_slots[:, None], axis=1).astype(jnp.int32)
    owned_grad, new_master, new_mom, new_var = owner_call(
        mine_used, flag, near_grad, far_grad, master_slots[0], left_basis[0], right_basis[0], mom_slots[0], var_slots[0]
    )
    vec_rows = jnp.where(home, near_grad[slots_per * BS :], far_grad[slots_per * BS :])
    owned_vec_grad = vec_rows.astype(f32).reshape(VEC_ROWS * BS)[:vec_per]
    new_vec_mom = decay * vec_mom[0] + (1.0 - decay) * owned_vec_grad
    new_vec_var = decay * vec_var[0] + (1.0 - decay) * owned_vec_grad * owned_vec_grad
    new_vec = vec_master[0] - vector_rate * new_vec_mom / (jnp.sqrt(new_vec_var) + adam_eps)
    return (
        output,
        patch_grad,
        owned_grad[None],
        new_master[None],
        new_mom[None],
        new_var[None],
        owned_vec_grad[None],
        new_vec[None],
        new_vec_mom[None],
        new_vec_var[None],
    )


def solution(mesh):
    slots = P("tensor", "dp", None, None)
    vectors = P("tensor", "dp")
    tokens = P("dp", None)
    in_specs = (tokens, tokens, tokens, P("tensor", None), P()) + (slots,) * 5 + (vectors,) * 3
    out_specs = (tokens, P("dp", "tensor")) + (slots,) * 4 + (vectors,) * 4
    return jax.shard_map(shards, mesh=mesh, in_specs=in_specs, out_specs=out_specs, check_vma=False)
```

```python
import functools

import jax
import jax.numpy as jnp
import numpy as np
from jax import lax
from jax.experimental import pallas as pl
from jax.experimental.pallas import tpu as pltpu
from jax.sharding import PartitionSpec as P

D = 768
HEAD_DIM = 64
FF = 3072
BASE_PIX = 3072
LAYERS = 2
LEN_A = 196
LEN_B = 225
LEN_C = 576
IMG_DEV = 5
BS = 128
TENSOR = 2
HALF = D // TENSOR
HALF_FF = FF // TENSOR
HEADS = HALF // HEAD_DIM
ROWS = 256
KEYS = 512
VEC_ROWS = 32
CHUNKS = 4

AXES = ("dp", "tensor")
precise = lax.Precision.HIGHEST
masked_score = -1e30
norm_eps = 1e-06
adam_eps = 1e-08
decay = 0.5
matrix_rate = 0.05
vector_rate = 0.3
f32 = jnp.float32
bf16 = jnp.bfloat16
MIB = 1024 * 1024

WEIGHTS = [("base", 0, BASE_PIX)]
for layer in range(LAYERS):
    WEIGHTS += [("qkv", layer, 3 * D), ("out", layer, D), ("up", layer, FF), ("down", layer, FF)]
STARTS = {}
PANEL_ROWS = 0
for name, layer, size in WEIGHTS:
    STARTS[name, layer] = PANEL_ROWS
    PANEL_ROWS += size


def tile_targets():
    rows, cols = [], []

    def add(start, rows_n, cols_n):
        for i in range(rows_n // BS):
            for j in range(cols_n // BS):
                panel, inner = divmod(j * BS, HALF)
                rows.append(start + panel * rows_n + i * BS)
                cols.append(inner)

    add(STARTS["base", 0], BASE_PIX, HALF)
    for layer in range(LAYERS):
        add(STARTS["qkv", layer], D, 3 * HALF)
        add(STARTS["out", layer], HALF, D)
        add(STARTS["up", layer], D, HALF_FF)
        add(STARTS["down", layer], HALF_FF, D)
    return np.array(rows, np.int32), np.array(cols, np.int32)


TARGET_ROW, TARGET_COL = tile_targets()
LAYER_VECS = (D, D, HALF, HALF, D, D, D, HALF_FF, D)
VEC_NAMES = ("g1", "s1", "bq", "bv", "bo", "g2", "s2", "b1", "b2")


def vec_offsets():
    offset = HALF
    found = []
    for layer in range(LAYERS):
        here = {}
        for name, length in zip(VEC_NAMES, LAYER_VECS):
            here[name] = (offset, length)
            offset += length
        found.append(here)
    return found


VEC_AT = vec_offsets()


def params(limit=24):
    return pltpu.CompilerParams(
        dimension_semantics=("arbitrary",), vmem_limit_bytes=limit * MIB
    )


def cost(flops, nbytes, trans=0):
    return pl.CostEstimate(flops=flops, bytes_accessed=nbytes, transcendentals=trans)


def rows_spec(width):
    return pl.BlockSpec((ROWS, width), lambda i, *_: (i, 0))


def fixed(shape, at=0):
    return pl.BlockSpec(shape, lambda i, *_: (at,) + (0,) * (len(shape) - 1))


def vec_piece(vec_ref, layer, name):
    start, length = VEC_AT[layer][name]
    return vec_ref[:, start : start + length]


def dot(left, right):
    return jnp.dot(left, right, preferred_element_type=f32)


def dot_nt(left, right, precision=None):
    return lax.dot_general(
        left, right, (((1,), (1,)), ((), ())), precision=precision, preferred_element_type=f32
    )


def dot_tn(left, right):
    return lax.dot_general(left, right, (((0,), (0,)), ((), ())), preferred_element_type=f32)


def joined(ref, start, rows_n, panels):
    return jnp.concatenate(
        [ref[start + p * rows_n : start + (p + 1) * rows_n, :] for p in range(panels)], axis=1
    )


def norm_stats(values):
    mean_val = jnp.mean(values, axis=-1, keepdims=True)
    centered = values - mean_val
    inv_std = lax.rsqrt(jnp.mean(centered * centered, axis=-1, keepdims=True) + norm_eps)
    return centered * inv_std, inv_std


def norm_back(values, gain, grad):
    unit, inv_std = norm_stats(values)
    scaled = grad * gain
    mean_s = jnp.mean(scaled, axis=-1, keepdims=True)
    mean_u = jnp.mean(scaled * unit, axis=-1, keepdims=True)
    back = inv_std * (scaled - mean_s - unit * mean_u)
    return (
        back,
        jnp.sum(grad * unit, axis=0, keepdims=True),
        jnp.sum(grad, axis=0, keepdims=True),
    )


def accumulate(ref, value):
    first = pl.program_id(0) == 0

    @pl.when(first)
    def _():
        ref[...] = value

    @pl.when(jnp.logical_not(first))
    def _():
        ref[...] += value


def stay(value):
    return pltpu.with_memory_space_constraint(value, pltpu.HBM)


def fence(*arrays):
    def nothing(*refs):
        pass

    anywhere = pl.BlockSpec(memory_space=pl.ANY)
    return pl.pallas_call(
        nothing,
        out_shape=[jax.ShapeDtypeStruct(a.shape, a.dtype) for a in arrays],
        in_specs=[anywhere] * len(arrays),
        out_specs=[anywhere] * len(arrays),
        input_output_aliases={i: i for i in range(len(arrays))},
        compiler_params=pltpu.CompilerParams(vmem_limit_bytes=MIB),
    )(*[stay(a) if a.size > 32 * 1024 else a for a in arrays])


def gather_kernel(slots, count_a, count_b, owner, drow, dcol, flag, *refs):
    first = refs[:count_a]
    second = refs[count_a : count_a + count_b]
    *panels, vectors, held, sem, vec_sem = refs[count_a + count_b :]

    def copy_all(sources):
        at = 0
        for src in sources:
            for n in range(src.shape[0]):
                who = owner[at]
                at += 1

                def body(i, carried, src=src, n=n, who=who):
                    slot = who * slots + i
                    row = drow[slot]

                    @pl.when(row >= 0)
                    def _():
                        start = pl.multiple_of(i * BS, BS)
                        pltpu.make_async_copy(
                            src.at[n, pl.ds(start, BS), :],
                            held.at[
                                pl.ds(pl.multiple_of(row, BS), BS),
                                pl.ds(pl.multiple_of(dcol[slot], BS), BS),
                            ],
                            sem,
                        ).start()

                    return carried

                lax.fori_loop(0, slots, body, 0)
                pltpu.make_async_copy(
                    src.at[n, pl.ds(slots * BS, VEC_ROWS), :], vectors.at[who], vec_sem
                ).start()

    if count_b:

        @pl.when(flag[0] == 1)
        def _():
            copy_all(first)

        @pl.when(flag[0] == 0)
        def _():
            copy_all(second)
    else:
        copy_all(first)
    pltpu.make_async_copy(held, held, sem).wait()
    at = 0
    for panel in panels:
        size = panel.shape[0]
        pltpu.make_async_copy(held.at[pl.ds(at, size), :], panel, sem).start()
        at += size
    pltpu.make_async_copy(vectors, vectors, vec_sem).wait()
    pltpu.make_async_copy(held, held, sem).wait()


def gather_tiles(first, second, owner, drow, dcol, flag, slots, owners):
    anywhere = pl.BlockSpec(memory_space=pl.ANY)
    *panels, vectors = pl.pallas_call(
        functools.partial(gather_kernel, slots, len(first), len(second)),
        out_shape=[pltpu.HBM((size, HALF), bf16) for unused, unused2, size in WEIGHTS]
        + [jax.ShapeDtypeStruct((owners, VEC_ROWS, BS), bf16)],
        grid_spec=pltpu.PrefetchScalarGridSpec(
            num_scalar_prefetch=4,
            grid=(1,),
            in_specs=[anywhere] * (len(first) + len(second)),
            out_specs=[anywhere] * len(WEIGHTS) + [fixed((owners, VEC_ROWS, BS))],
            scratch_shapes=[
                pltpu.VMEM((PANEL_ROWS, HALF), bf16),
                pltpu.SemaphoreType.DMA,
                pltpu.SemaphoreType.DMA,
            ],
        ),
        compiler_params=params(),
        cost_estimate=cost(0, 4 * PANEL_ROWS * HALF),
    )(owner, drow, dcol, flag, *[stay(v) for v in first], *[stay(v) for v in second])
    return {(name, layer): p for (name, layer, unused), p in zip(WEIGHTS, panels)}, vectors


def scatter_kernel(rows_n, cols_n, steps, paired, parts, pos, part, own, *refs):
    @pl.when(part[1] > 0)
    def _():
        scatter_body(rows_n, cols_n, steps, paired, parts, pos, part, own, *refs)


def scatter_body(rows_n, cols_n, steps, paired, parts, pos, part, own, *refs):
    if paired:
        recv, *refs = refs
        span = pl.num_programs(0) // parts
        here = jnp.logical_or(parts == 1, pl.program_id(0) // span == part[0])
    target, buf, sems = refs[-3:]
    step = pl.program_id(0)
    slot = lax.rem(step, 2)
    per = rows_n // BS * (cols_n // BS)

    def wait(at):
        pltpu.make_async_copy(buf.at[at], buf.at[at], sems.at[at]).wait()

    @pl.when(step >= 2)
    def _():
        wait(slot)

    for i in range(rows_n // BS):
        for j in range(cols_n // BS):
            area = (slice(i * BS, (i + 1) * BS), slice(j * BS, (j + 1) * BS))
            value = own[area]
            if paired:
                more = jnp.where(here, recv[area].astype(f32), 0.0)
                value = (value.astype(f32) + more).astype(bf16)
            buf[slot, i * (cols_n // BS) + j] = value
    for n in range(per):
        pltpu.make_async_copy(
            buf.at[slot, n],
            target.at[pl.ds(pl.multiple_of(pos[step * per + n], 16), BS), :],
            sems.at[slot],
        ).start()

    @pl.when(step == pl.num_programs(0) - 1)
    def _():
        if steps > 1:
            wait(1 - slot)
        wait(slot)


def scatter_matrix(pos, own, recv, part, target, total_rows, rows_n):
    cols_n = own.shape[1]
    steps = own.shape[0] // rows_n
    anywhere = pl.BlockSpec(memory_space=pl.ANY)
    block = pl.BlockSpec((rows_n, cols_n), lambda i, *_: (i, 0))
    paired = recv is not None
    parts = own.shape[0] // recv.shape[0] if paired else 1
    span = steps // parts
    arrived = pl.BlockSpec(
        (rows_n, cols_n), lambda i, pos, part: (jnp.clip(i - part[0] * span, 0, span - 1), 0)
    )
    operands = [stay(own)] + ([stay(recv)] if paired else []) + ([] if target is None else [stay(target)])
    specs = [block] + ([block if parts == 1 else arrived] if paired else [])
    specs += [] if target is None else [anywhere]
    return pl.pallas_call(
        functools.partial(scatter_kernel, rows_n, cols_n, steps, paired, parts),
        out_shape=pltpu.HBM((total_rows, BS), bf16),
        grid_spec=pltpu.PrefetchScalarGridSpec(
            num_scalar_prefetch=2,
            grid=(steps,),
            in_specs=specs,
            out_specs=anywhere,
            scratch_shapes=[
                pltpu.VMEM((2, rows_n // BS * (cols_n // BS), BS, BS), bf16),
                pltpu.SemaphoreType.DMA((2,)),
            ],
        ),
        input_output_aliases={} if target is None else {len(operands) + 1: 0},
        compiler_params=params(12),
        cost_estimate=cost(own.size, own.size * 6),
    )(pos, part, *operands)


def half_sum_kernel(part, own, arrived, out):
    out[...] = (own[...].astype(f32) + arrived[...].astype(f32)).astype(bf16)


def half_sum(part, own, arrived):
    block = arrived.shape
    return pl.pallas_call(
        half_sum_kernel,
        out_shape=pltpu.HBM(block, bf16),
        grid_spec=pltpu.PrefetchScalarGridSpec(
            num_scalar_prefetch=1,
            grid=(1,),
            in_specs=[pl.BlockSpec(block, lambda i, part: (part[0], 0)), fixed(block)],
            out_specs=fixed(block),
        ),
        compiler_params=params(8),
        cost_estimate=cost(arrived.size, arrived.size * 6),
    )(part, stay(own), stay(arrived))


def half_copy_kernel(part, own, out):
    out[...] = own[...]


def other_half(part, own):
    block = (own.shape[0] // 2, own.shape[1])
    return pl.pallas_call(
        half_copy_kernel,
        out_shape=pltpu.HBM(block, bf16),
        grid_spec=pltpu.PrefetchScalarGridSpec(
            num_scalar_prefetch=1,
            grid=(1,),
            in_specs=[pl.BlockSpec(block, lambda i, part: (1 - part[0], 0))],
            out_specs=fixed(block),
        ),
        compiler_params=params(8),
        cost_estimate=cost(0, own.size * 2),
    )(part, stay(own))


def scatter_vec_kernel(paired, pos, own, *refs):
    if paired:
        recv, *refs = refs
    target, buf, sem = refs[-3:]
    value = own[...]
    if paired:
        value = (value.astype(f32) + recv[...].astype(f32)).astype(bf16)
    buf[...] = value

    def body(n, carried):
        pltpu.make_async_copy(
            buf.at[n], target.at[pl.ds(pl.multiple_of(pos[n], 16), VEC_ROWS), :], sem
        ).start()
        return carried

    lax.fori_loop(0, own.shape[0], body, 0)
    pltpu.make_async_copy(buf, buf, sem).wait()


def scatter_vec(pos, own, recv, target):
    anywhere = pl.BlockSpec(memory_space=pl.ANY)
    block = fixed(own.shape)
    paired = recv is not None
    operands = [own] + ([recv] if paired else []) + [stay(target)]
    return pl.pallas_call(
        functools.partial(scatter_vec_kernel, paired),
        out_shape=pltpu.HBM(target.shape, bf16),
        grid_spec=pltpu.PrefetchScalarGridSpec(
            num_scalar_prefetch=1,
            grid=(1,),
            in_specs=[block] * (len(operands) - 1) + [anywhere],
            out_specs=anywhere,
            scratch_shapes=[pltpu.VMEM(own.shape, bf16), pltpu.SemaphoreType.DMA],
        ),
        input_output_aliases={len(operands): 0},
        compiler_params=params(4),
    )(pos, *operands)


def expand_kernel(present, half, patch_ref, class_ref, pinv_ref, out, total):
    for block in range(patch_ref.shape[0] // ROWS):
        rows = slice(block * ROWS, (block + 1) * ROWS)
        total[...] = jnp.zeros_like(total)
        for which in range(3):

            @pl.when(present[block, which] > 0)
            def _(which=which, rows=rows):
                chosen = jnp.where(class_ref[rows, :] == which, patch_ref[rows, :].astype(f32), 0.0)
                total[...] += dot_nt(chosen.astype(bf16), pinv_ref[which])

        out[rows, :] = total[...].astype(bf16)


def expand_call(which, present, half, patches, class_col, pinv):
    tokens = patches.shape[0]
    size = BASE_PIX // CHUNKS
    step = size
    return pl.pallas_call(
        expand_kernel,
        out_shape=jax.ShapeDtypeStruct((tokens, size), bf16),
        grid_spec=pltpu.PrefetchScalarGridSpec(
            num_scalar_prefetch=2,
            grid=(1,),
            in_specs=[
                fixed(patches.shape),
                fixed(class_col.shape),
                pl.BlockSpec(
                    (3, step, pinv.shape[2]),
                    lambda i, present, half: (0, (which + half[0] * (CHUNKS // 2)) % CHUNKS, 0),
                ),
            ],
            out_specs=pl.BlockSpec((tokens, step), lambda i, *_: (0, i)),
            scratch_shapes=[pltpu.VMEM((ROWS, step), f32)],
        ),
        compiler_params=params(),
        cost_estimate=cost(3 * tokens * size * D, tokens * size * 4 + size * D * 6),
    )(present, half, stay(patches), class_col, stay(pinv))


def resize_kernel(base, pinv_ref, out, turned):
    @pl.when(pl.program_id(0) == 0)
    def _():
        turned[...] = base[...].T

    out[0] = dot(turned[...], pinv_ref[0]).astype(bf16)


def resize_call(weights, pinv):
    return pl.pallas_call(
        resize_kernel,
        out_shape=jax.ShapeDtypeStruct((3, HALF, pinv.shape[2]), bf16),
        grid=(3,),
        in_specs=[
            fixed((BASE_PIX, HALF)),
            pl.BlockSpec((1, BASE_PIX, pinv.shape[2]), lambda i: (i, 0, 0)),
        ],
        out_specs=pl.BlockSpec((1, HALF, pinv.shape[2]), lambda i: (i, 0, 0)),
        scratch_shapes=[pltpu.VMEM((HALF, BASE_PIX), bf16)],
        compiler_params=params(),
        cost_estimate=cost(6 * D * BASE_PIX * HALF, 6 * D * BASE_PIX),
    )(stay(weights["base", 0]), stay(pinv))


def embed_back_kernel(core, token, base, own, recv, out, bias):
    low = (base[...] + (own[...].astype(f32) + recv[...].astype(f32))).astype(bf16)
    out[...] = low
    accumulate(bias, jnp.sum(low.astype(f32), axis=0, keepdims=True))


def embed_back_call(core, token, base, own, recv):
    tokens = base.shape[0]
    half = pl.BlockSpec((ROWS, HALF), lambda i, core: (i, core[0]))
    return pl.pallas_call(
        embed_back_kernel,
        out_shape=[
            jax.ShapeDtypeStruct((tokens, HALF), bf16),
            jax.ShapeDtypeStruct((1, HALF), f32),
        ],
        grid_spec=pltpu.PrefetchScalarGridSpec(
            num_scalar_prefetch=1,
            grid=(tokens // ROWS,),
            in_specs=[fixed(token.shape)] + [half] * 3,
            out_specs=[rows_spec(HALF), fixed((1, HALF))],
        ),
        compiler_params=params(8),
        cost_estimate=cost(tokens * D, tokens * D * 5),
    )(core, token, base, own, recv)


def pack_kernel(vec_per, *refs):
    *pieces, out = refs
    out[...] = jnp.zeros_like(out)
    at = 0
    for piece in pieces:
        for k in range(piece.shape[1] // BS):
            owner, row = divmod(at, vec_per // BS)
            out[owner, row : row + 1, :] = piece[:, k * BS : (k + 1) * BS]
            at += 1


def pack_call(pieces, owners, vec_per):
    if vec_per % BS:
        joined = jnp.concatenate(pieces, axis=1)[0]
        joined = jnp.pad(joined, (0, owners * vec_per - joined.shape[0])).reshape(owners, vec_per)
        joined = jnp.pad(joined, ((0, 0), (0, VEC_ROWS * BS - vec_per)))
        return joined.astype(bf16).reshape(owners, VEC_ROWS, BS)
    return pl.pallas_call(
        functools.partial(pack_kernel, vec_per),
        out_shape=jax.ShapeDtypeStruct((owners, VEC_ROWS, BS), f32),
        grid=(1,),
        in_specs=[fixed(p.shape) for p in pieces],
        out_specs=fixed((owners, VEC_ROWS, BS)),
        compiler_params=params(4),
        cost_estimate=cost(0, owners * vec_per * 8),
    )(*pieces).astype(bf16)


def embed_kernel(half, *refs):
    *parts, vec, weight, out = refs
    size = BASE_PIX // CHUNKS
    total = vec[:, :HALF]
    for c in range(CHUNKS):
        at = lax.rem(c + half[0] * (CHUNKS // 2), CHUNKS)
        rows = pl.ds(pl.multiple_of(at * size, size), size)
        total = total + dot(parts[c][...], weight[rows, :])
    out[...] = total.astype(bf16)


def embed_call(half, chunks, vec, weights):
    tokens = chunks[0].shape[0]
    return pl.pallas_call(
        embed_kernel,
        out_shape=jax.ShapeDtypeStruct((tokens, HALF), bf16),
        grid_spec=pltpu.PrefetchScalarGridSpec(
            num_scalar_prefetch=1,
            grid=(tokens // ROWS,),
            in_specs=[rows_spec(BASE_PIX // CHUNKS)] * CHUNKS
            + [fixed(vec.shape), fixed((BASE_PIX, HALF))],
            out_specs=rows_spec(HALF),
        ),
        compiler_params=params(),
        cost_estimate=cost(2 * tokens * BASE_PIX * HALF, tokens * BASE_PIX * 3),
    )(half, *[stay(c) for c in chunks], vec, stay(weights["base", 0]))


def qkv_kernel(layer, first, core, *refs):
    if first:
        own, recv, vec, weight, hid, normed, q_ref, k_ref, v_ref = refs
        mine, theirs = own[...].astype(f32), recv[...].astype(f32)
        low = core[0] == 0
        values = jnp.concatenate(
            [jnp.where(low, mine, theirs), jnp.where(low, theirs, mine)], axis=1
        )
    else:
        base, own, recv, vec, weight, hid, normed, q_ref, k_ref, v_ref = refs
        values = base[...] + (own[...].astype(f32) + recv[...].astype(f32))
    hid[...] = values
    unit, unused = norm_stats(values)
    low = (unit * vec_piece(vec, layer, "g1") + vec_piece(vec, layer, "s1")).astype(bf16)
    normed[...] = low
    made = dot(low, joined(weight, 0, D, 3))
    q_ref[...] = (made[:, :HALF] + vec_piece(vec, layer, "bq")).astype(bf16)
    k_ref[...] = made[:, HALF : 2 * HALF].astype(bf16)
    v_ref[...] = (made[:, 2 * HALF :] + vec_piece(vec, layer, "bv")).astype(bf16)


def qkv_call(layer, base, own, recv, core, vec, weights):
    tokens = own.shape[0]
    shape = lambda width, kind: jax.ShapeDtypeStruct((tokens, width), kind)
    outs = [shape(D, f32), pltpu.HBM((tokens, D), bf16)] + [shape(HALF, bf16)] * 3
    operands = ([] if base is None else [base]) + [own, recv]
    return pl.pallas_call(
        functools.partial(qkv_kernel, layer, base is None),
        out_shape=outs,
        grid_spec=pltpu.PrefetchScalarGridSpec(
            num_scalar_prefetch=1,
            grid=(tokens // ROWS,),
            in_specs=[rows_spec(o.shape[1]) for o in operands]
            + [fixed(vec.shape), fixed((3 * D, HALF))],
            out_specs=[rows_spec(o.shape[1]) for o in outs],
        ),
        compiler_params=params(),
        cost_estimate=cost(2 * tokens * D * 3 * HALF, tokens * D * 14),
    )(core, *operands, vec, weights["qkv", layer])


def head_masks():
    lane = lax.broadcasted_iota(jnp.int32, (1, 2 * HEAD_DIM), 1)
    low = (lane < HEAD_DIM).astype(f32).astype(bf16)
    high = (lane >= HEAD_DIM).astype(f32).astype(bf16)
    return low, high


def attend_kernel(
    layer, low_ref, high_ref, q_ref, k_ref, v_ref, seg_q, seg_k, vec, w_out, o_ref, lse_ref, part,
    scores_ref, top_ref, acc_ref,
):
    step = pl.program_id(0)
    first, last = low_ref[step], high_ref[step]
    masks = head_masks()
    scale = jnp.asarray(HEAD_DIM ** (-0.5), bf16)
    lane = lax.broadcasted_iota(jnp.int32, (1, BS), 1)
    sums = [(lane == HEAD_DIM).astype(f32).astype(bf16), (lane == 0).astype(f32).astype(bf16)]
    top_ref[...] = jnp.full(top_ref.shape, masked_score, f32)
    acc_ref[...] = jnp.zeros_like(acc_ref)
    seg_col = seg_q[...]

    def score_block(block, carried):
        rows = pl.ds(pl.multiple_of(block * ROWS, ROWS), ROWS)
        same = seg_col == seg_k[:, rows]
        for pair in range(HEADS // 2):
            cols = slice(pair * BS, (pair + 1) * BS)
            q_two = q_ref[:, cols] * scale
            k_two = k_ref[rows, cols]
            for side in range(2):
                head = 2 * pair + side
                scores = jnp.where(same, dot_nt(q_two * masks[side], k_two), masked_score)
                scores_ref[head, block] = scores
                top = top_ref[head]
                for piece in range(ROWS // BS):
                    top = jnp.maximum(top, scores[:, piece * BS : (piece + 1) * BS])
                top_ref[head] = top
        return carried

    lax.fori_loop(first, last, score_block, 0)
    tops = [jnp.max(top_ref[head], axis=1, keepdims=True) for head in range(HEADS)]

    def mix_block(block, carried):
        rows = pl.ds(pl.multiple_of(block * ROWS, ROWS), ROWS)
        for pair in range(HEADS // 2):
            v_two = v_ref[rows, pair * BS : (pair + 1) * BS]
            for side in range(2):
                head = 2 * pair + side
                expo = jnp.exp(scores_ref[head, block] - tops[head]).astype(bf16)
                acc_ref[head] += dot(expo, v_two * masks[side] + sums[side])
        return carried

    lax.fori_loop(first, last, mix_block, 0)
    totals = jnp.zeros((ROWS, BS), f32)
    for pair in range(HEADS // 2):
        sides = []
        for side in range(2):
            head = 2 * pair + side
            mixed = acc_ref[head]
            at = HEAD_DIM * (1 - side)
            total = mixed[:, at : at + 1]
            totals = jnp.where(lane == head, tops[head] + jnp.log(total), totals)
            sides.append(mixed * (1.0 / total))
        o_ref[:, pair * BS : (pair + 1) * BS] = jnp.where(lane < HEAD_DIM, *sides).astype(bf16)
    lse_ref[...] = totals.T[0:8, :]
    low = o_ref[...]
    bias = vec_piece(vec, layer, "bo")
    part[...] = (dot(low, joined(w_out, 0, HALF, TENSOR)) + bias).astype(bf16)


def attend_call(layer, first, last, queries, keys, values, seg_col, seg_row, vec, weights):
    tokens = queries.shape[0]
    return pl.pallas_call(
        functools.partial(attend_kernel, layer),
        out_shape=[
            jax.ShapeDtypeStruct((tokens, HALF), bf16),
            jax.ShapeDtypeStruct((8, tokens), f32),
            jax.ShapeDtypeStruct((tokens, D), bf16),
        ],
        grid_spec=pltpu.PrefetchScalarGridSpec(
            num_scalar_prefetch=2,
            grid=(tokens // ROWS,),
            in_specs=[
                rows_spec(HALF),
                fixed(keys.shape),
                fixed(values.shape),
                rows_spec(1),
                fixed(seg_row.shape),
                fixed(vec.shape),
                fixed((D, HALF)),
            ],
            out_specs=[
                rows_spec(HALF),
                pl.BlockSpec((8, ROWS), lambda i, *_: (0, i)),
                rows_spec(D),
            ],
            scratch_shapes=[
                pltpu.VMEM((HEADS, tokens // ROWS, ROWS, ROWS), f32),
                pltpu.VMEM((HEADS, ROWS, BS), f32),
                pltpu.VMEM((HEADS, ROWS, BS), f32),
            ],
        ),
        compiler_params=params(),
        cost_estimate=cost(8 * HEADS * tokens * tokens * BS, tokens * D * 8, HEADS * tokens * tokens),
    )(first, last, queries, keys, values, seg_col, seg_row, vec, weights["out", layer])


def gelu_parts(values):
    cdf = 0.5 * (1.0 + lax.erf(values * 0.7071067811865476))
    pdf = 0.3989422804014327 * jnp.exp(-0.5 * values * values)
    return values * cdf, cdf + values * pdf


def mlp_kernel(layer, base, own, recv, vec, w_up, w_down, hid, normed, act, slope, part):
    values = base[...] + (own[...].astype(f32) + recv[...].astype(f32))
    hid[...] = values
    unit, unused = norm_stats(values)
    low = (unit * vec_piece(vec, layer, "g2") + vec_piece(vec, layer, "s2")).astype(bf16)
    normed[...] = low
    bias_up = vec_piece(vec, layer, "b1")
    for pair in range(HALF_FF // D):
        area = slice(pair * D, (pair + 1) * D)
        up = dot(low, joined(w_up, pair * 2 * D, D, 2)) + bias_up[:, area]
        gelu, grad = gelu_parts(up)
        act[:, area] = gelu.astype(bf16)
        slope[:, area] = grad.astype(bf16)
    bias_down = vec_piece(vec, layer, "b2")
    part[...] = (dot(act[...], joined(w_down, 0, HALF_FF, TENSOR)) + bias_down).astype(bf16)


def mlp_call(layer, base, own, recv, vec, weights):
    tokens = base.shape[0]
    shape = lambda width, kind: jax.ShapeDtypeStruct((tokens, width), kind)
    kept = lambda width: pltpu.HBM((tokens, width), bf16)
    outs = [shape(D, f32), kept(D), kept(HALF_FF), kept(HALF_FF), shape(D, bf16)]
    return pl.pallas_call(
        functools.partial(mlp_kernel, layer),
        out_shape=outs,
        grid=(tokens // ROWS,),
        in_specs=[rows_spec(D)] * 3
        + [
            fixed(vec.shape),
            fixed((2 * HALF_FF, HALF)),
            fixed((2 * HALF_FF, HALF)),
        ],
        out_specs=[rows_spec(o.shape[1]) for o in outs],
        compiler_params=params(),
        cost_estimate=cost(4 * tokens * D * HALF_FF, tokens * D * 24, 2 * tokens * HALF_FF),
    )(base, own, recv, vec, weights["up", layer], weights["down", layer])


def mlp_back_kernel(layer, summed, *refs):
    if summed:
        base, own, recv, *refs = refs
        (hid, slope, vec, w_up, w_down, grad_full, grad_low, du_ref, back, dgain, dshift, db1, db2) = refs
        values = base[...].astype(f32) + (own[...].astype(f32) + recv[...].astype(f32))
        grad_full[...] = values
        low = values.astype(bf16)
    else:
        base, valid, *refs = refs
        (hid, slope, vec, w_up, w_down, grad_low, du_ref, back, dgain, dshift, db1, db2) = refs
        low = (base[...].astype(f32) * valid[...]).astype(bf16)
    grad_low[...] = low
    accumulate(db2, jnp.sum(low.astype(f32), axis=0, keepdims=True))
    for part in range(HALF_FF // D):
        area = slice(part * D, (part + 1) * D)
        rows = jnp.concatenate(
            [w_down[p * HALF_FF + part * D : p * HALF_FF + (part + 1) * D, :] for p in range(TENSOR)],
            axis=1,
        )
        du_ref[:, area] = (dot_nt(low, rows) * slope[:, area].astype(f32)).astype(bf16)
    grad_normed = dot_nt(du_ref[...], joined(w_up, 0, D, HALF_FF // HALF))
    accumulate(db1, jnp.sum(du_ref[...].astype(f32), axis=0, keepdims=True))
    part_back, gain_grad, shift_grad = norm_back(hid[...], vec_piece(vec, layer, "g2"), grad_normed)
    back[...] = part_back.astype(bf16)
    accumulate(dgain, gain_grad)
    accumulate(dshift, shift_grad)


def mlp_back_call(layer, base, own, recv, valid, hid, slope, vec, weights):
    tokens = base.shape[0]
    summed = own is not None
    shape = lambda width, kind: jax.ShapeDtypeStruct((tokens, width), kind)
    line = lambda width: jax.ShapeDtypeStruct((1, width), f32)
    outs = ([shape(D, f32)] if summed else []) + [shape(D, bf16), shape(HALF_FF, bf16), shape(D, bf16)]
    lines = [line(D), line(D), line(HALF_FF), line(D)]
    extra = [own, recv] if summed else [valid]
    return pl.pallas_call(
        functools.partial(mlp_back_kernel, layer, summed),
        out_shape=outs + lines,
        grid=(tokens // ROWS,),
        in_specs=[rows_spec(D)]
        + [rows_spec(e.shape[1]) for e in extra]
        + [
            rows_spec(D),
            rows_spec(HALF_FF),
            fixed(vec.shape),
            fixed((2 * HALF_FF, HALF)),
            fixed((2 * HALF_FF, HALF)),
        ],
        out_specs=[rows_spec(o.shape[1]) for o in outs] + [fixed(o.shape) for o in lines],
        compiler_params=params(),
        cost_estimate=cost(4 * tokens * D * HALF_FF, tokens * D * 24),
    )(base, *extra, stay(hid), stay(slope), vec, weights["up", layer], weights["down", layer])


def attend_back_kernel(
    low_ref, high_ref, base, own, recv, q_ref, k_ref, v_ref, o_ref, lse_ref, seg_k, seg_q, w_out,
    full_ref, grad_low, dq_ref, dk_ref, dv_ref, dbo, dk_acc, dv_acc, dq_acc, do_ref,
):
    step = pl.program_id(0)

    @pl.when(step == 0)
    def _():
        dk_acc[...] = jnp.zeros_like(dk_acc)
        dv_acc[...] = jnp.zeros_like(dv_acc)

    values = base[...].astype(f32) + (own[...].astype(f32) + recv[...].astype(f32))
    full_ref[...] = values
    low = values.astype(bf16)
    grad_low[...] = low
    accumulate(dbo, jnp.sum(low.astype(f32), axis=0, keepdims=True))
    do_ref[...] = dot_nt(low, joined(w_out, 0, HALF, TENSOR)).astype(bf16)
    product = do_ref[...].astype(f32) * o_ref[...].astype(f32)
    head = lax.broadcasted_iota(jnp.int32, (8, HALF), 0)
    lane = lax.broadcasted_iota(jnp.int32, (8, HALF), 1)
    pick = ((lane >= head * HEAD_DIM) & (lane < (head + 1) * HEAD_DIM)).astype(f32)
    high, rest = split(product)
    pick = pick.astype(bf16)
    inner = dot_nt(pick, high) + dot_nt(pick, rest)
    dq_acc[...] = jnp.zeros_like(dq_acc)
    masks = head_masks()
    scale = jnp.asarray(HEAD_DIM ** (-0.5), bf16)
    seg_row = seg_q[...]

    def one_block(block, carried):
        rows = pl.ds(pl.multiple_of(block * KEYS, KEYS), KEYS)
        same = seg_k[rows, :] == seg_row
        for pair in range(HEADS // 2):
            cols = slice(pair * BS, (pair + 1) * BS)
            q_two = q_ref[:, cols] * scale
            do_two = do_ref[:, cols]
            k_two = k_ref[rows, cols]
            v_two = v_ref[rows, cols]
            dv_two = dk_two = dq_two = None
            for side in range(2):
                at = 2 * pair + side
                q_one = q_two * masks[side]
                do_one = do_two * masks[side]
                scores = dot_nt(k_two, q_one)
                prob = jnp.where(same, jnp.exp(scores - lse_ref[at : at + 1, :]), 0.0)
                grad_prob = dot_nt(v_two, do_one)
                grad_scores = (prob * (grad_prob - inner[at : at + 1, :])).astype(bf16)
                dv_one = dot(prob.astype(bf16), do_one)
                dk_one = dot(grad_scores, q_one)
                dq_one = dot_tn(grad_scores, k_two * masks[side])
                dq_two = dq_one if dq_two is None else dq_two + dq_one
                dv_two = dv_one if dv_two is None else dv_two + dv_one
                dk_two = dk_one if dk_two is None else dk_two + dk_one
            dv_acc[rows, cols] += dv_two
            dk_acc[rows, cols] += dk_two
            dq_acc[:, cols] += dq_two
        return carried

    lax.fori_loop(low_ref[step], high_ref[step], one_block, 0)
    dq_ref[...] = (dq_acc[...] * HEAD_DIM ** (-0.5)).astype(bf16)

    @pl.when(step == pl.num_programs(0) - 1)
    def _():
        dk_ref[...] = dk_acc[...].astype(bf16)
        dv_ref[...] = dv_acc[...].astype(bf16)


def attend_back_call(
    layer, first, last, base, own, recv, queries, keys, values, mixed, lse, seg_col, seg_row, weights
):
    tokens = base.shape[0]
    shape = lambda width, kind: jax.ShapeDtypeStruct((tokens, width), kind)
    whole = (tokens, HALF)
    return pl.pallas_call(
        attend_back_kernel,
        out_shape=[
            shape(D, f32),
            shape(D, bf16),
            shape(HALF, bf16),
            shape(HALF, bf16),
            shape(HALF, bf16),
            jax.ShapeDtypeStruct((1, D), f32),
        ],
        grid_spec=pltpu.PrefetchScalarGridSpec(
            num_scalar_prefetch=2,
            grid=(tokens // ROWS,),
            in_specs=[
                rows_spec(D),
                rows_spec(D),
                rows_spec(D),
                rows_spec(HALF),
                fixed(whole),
                fixed(whole),
                rows_spec(HALF),
                pl.BlockSpec((8, ROWS), lambda i, *_: (0, i)),
                fixed(seg_col.shape),
                pl.BlockSpec((1, ROWS), lambda i, *_: (0, i)),
                fixed((D, HALF)),
            ],
            out_specs=[
                rows_spec(D),
                rows_spec(D),
                rows_spec(HALF),
                fixed(whole),
                fixed(whole),
                fixed((1, D)),
            ],
            scratch_shapes=[
                pltpu.VMEM(whole, f32),
                pltpu.VMEM(whole, f32),
                pltpu.VMEM((ROWS, HALF), f32),
                pltpu.VMEM((ROWS, HALF), bf16),
            ],
        ),
        compiler_params=params(),
        cost_estimate=cost(14 * HEADS * tokens * tokens * BS, tokens * D * 20, HEADS * tokens * tokens),
    )(
        first, last, base, own, recv, stay(queries), stay(keys), stay(values), stay(mixed), lse,
        seg_col, seg_row, weights["out", layer],
    )


def qkv_back_kernel(layer, dq, dk, dv, hid, vec, weight, back, dgain, dshift, dbq, dbv):
    grad_three = jnp.concatenate([dq[...], dk[...], dv[...]], axis=1)
    grad_normed = dot_nt(grad_three, joined(weight, 0, D, 3))
    part_back, gain_grad, shift_grad = norm_back(hid[...], vec_piece(vec, layer, "g1"), grad_normed)
    back[...] = part_back.astype(bf16)
    accumulate(dgain, gain_grad)
    accumulate(dshift, shift_grad)
    accumulate(dbq, jnp.sum(dq[...].astype(f32), axis=0, keepdims=True))
    accumulate(dbv, jnp.sum(dv[...].astype(f32), axis=0, keepdims=True))


def qkv_back_call(layer, dq, dk, dv, hid, vec, weights):
    tokens = dq.shape[0]
    line = lambda width: jax.ShapeDtypeStruct((1, width), f32)
    lines = [line(D), line(D), line(HALF), line(HALF)]
    return pl.pallas_call(
        functools.partial(qkv_back_kernel, layer),
        out_shape=[jax.ShapeDtypeStruct((tokens, D), bf16)] + lines,
        grid=(tokens // ROWS,),
        in_specs=[rows_spec(HALF)] * 3
        + [
            rows_spec(D),
            fixed(vec.shape),
            fixed((3 * D, HALF)),
        ],
        out_specs=[rows_spec(D)] + [fixed(o.shape) for o in lines],
        compiler_params=params(),
        cost_estimate=cost(2 * tokens * D * 3 * HALF, tokens * D * 10),
    )(dq, dk, dv, stay(hid), vec, weights["qkv", layer])


def split(values):
    high = values.astype(bf16)
    return high, (values - high.astype(f32)).astype(bf16)


def product(left, right, left_dim, right_dim):
    def one(a, b):
        return lax.dot_general(
            a, b, (((left_dim,), (right_dim,)), ((), ())), preferred_element_type=f32
        )

    return one(left[0], right[0]) + (one(left[0], right[1]) + one(left[1], right[0]))


def owner_kernel(per, used, home, near, far, master, left, right, moment, variance, grad, out, out_mom, out_var):
    here = range(per)
    first = pl.program_id(0) * per
    lefts = [split(left[i]) for i in here]
    rights = [split(right[i]) for i in here]
    rotated = []
    for i in here:
        rows = slice(i * BS, (i + 1) * BS)
        tile = jnp.where(home[0] > 0, near[rows, :].astype(f32), far[rows, :].astype(f32))
        tile = jnp.where(used[first + i] > 0, tile, 0.0)
        grad[i] = tile
        tile = tile.astype(bf16)
        rotated.append(split(dot_tn(lefts[i][0], tile) + dot_tn(lefts[i][1], tile)))
    rotated = [product(rotated[i], rights[i], 1, 0) for i in here]
    steps = []
    for i in here:
        new_moment = decay * moment[i] + (1.0 - decay) * rotated[i]
        new_variance = decay * variance[i] + (1.0 - decay) * rotated[i] * rotated[i]
        out_mom[i] = new_moment
        out_var[i] = new_variance
        steps.append(split(new_moment / (jnp.sqrt(new_variance) + adam_eps)))
    returned = [split(product(lefts[i], steps[i], 1, 0)) for i in here]
    returned = [product(returned[i], rights[i], 1, 1) for i in here]
    for i in here:
        out[i] = master[i] - matrix_rate * returned[i]


def owner_call(used, home, near, far, *arrays):
    count = arrays[0].shape[0]
    per = min(8, count)
    block = pl.BlockSpec((per, BS, BS), lambda i, *_: (i, 0, 0))
    return pl.pallas_call(
        functools.partial(owner_kernel, per),
        out_shape=[jax.ShapeDtypeStruct(arrays[0].shape, f32)] * 4,
        grid_spec=pltpu.PrefetchScalarGridSpec(
            num_scalar_prefetch=2,
            grid=(count // per,),
            in_specs=[pl.BlockSpec((per * BS, BS), lambda i, *_: (i, 0))] * 2 + [block] * 5,
            out_specs=[block] * 4,
        ),
        compiler_params=params(),
        cost_estimate=cost(count * 88 * BS**3, count * BS * BS * 38),
    )(used, home, stay(near), stay(far), *arrays)


def reduce_kernel(carrying, last, *refs):
    block, arrived, *refs = refs
    total = block[...].astype(f32) + arrived[...].astype(f32)
    if carrying:
        carried, *refs = refs
        total = total + carried[...].astype(f32)
    if last:
        [out] = refs
    else:
        following, out, later = refs
        later[...] = following[...]
    out[...] = total.astype(bf16)


def reduce_call(j, n, buffer, arrived, carried, payload, x_rel=0):
    last = j >= 2 or x_rel == 1
    steps = 3
    rows_n = payload // steps
    at = lambda j, x_rel: pl.BlockSpec(
        (rows_n, BS), lambda i: (((j * 2 + x_rel) * 2 + n) * steps + i, 0)
    )
    whole = pl.BlockSpec((rows_n, BS), lambda i: (i, 0))
    operands = [stay(buffer), stay(arrived)] + ([] if carried is None else [stay(carried)])
    specs = [at(j, x_rel)] + [whole] * (len(operands) - 1)
    if not last:
        operands.append(stay(buffer))
        specs.append(at(j + 2, 1))
    outs = [pltpu.HBM((payload, BS), bf16)] * (1 if last else 2)
    made = pl.pallas_call(
        functools.partial(reduce_kernel, carried is not None, last),
        out_shape=outs,
        grid=(steps,),
        in_specs=specs,
        out_specs=[whole] * len(outs),
        compiler_params=params(8),
        cost_estimate=cost(payload * BS * 3, payload * BS * 12),
    )(*operands)
    return (made[0], None) if last else made


class Routes:
    def __init__(self, dp_n):
        pairs = [(d, t) for d in range(dp_n) for t in range(TENSOR)]
        at = lambda d, t: d * TENSOR + t
        home = [(d, t) for d, t in pairs if d % 2 == t]
        away = [(d, t) for d, t in pairs if d % 2 != t]
        self.core_all = [(at(d, t), at(d ^ 1, t)) for d, t in pairs]
        self.core_out = [(at(d, t), at(d ^ 1, t)) for d, t in home]
        self.core_in = [(at(d, t), at(d ^ 1, t)) for d, t in away]
        self.y_all = [(at(d, t), at(d, 1 - t)) for d, t in pairs]
        self.y_out = [(at(d, t), at(d, 1 - t)) for d, t in home]
        self.y_in = [(at(d, t), at(d, 1 - t)) for d, t in away]
        self.x_home = [(at(d, t), at(d ^ 2, t)) for d, t in home]
        self.x_away = [(at(d, t), at(d ^ 2, t)) for d, t in away]
        self.x_all = [(at(d, t), at(d ^ 2, t)) for d, t in pairs]
        self.z_all = [(at(d, t), at((d + 4) % dp_n, t)) for d, t in pairs]
        self.z_home = [(at(d, t), at((d + 4) % dp_n, t)) for d, t in home]


def send(value, route):
    return lax.ppermute(value, AXES, route)


def shards(
    patches,
    cotangent,
    image_size,
    block_slot,
    pinv,
    master_slots,
    left_basis,
    right_basis,
    mom_slots,
    var_slots,
    vec_master,
    vec_mom,
    vec_var,
):
    dp_n = lax.axis_size("dp")
    dp_pos = lax.axis_index("dp")
    y_pos = lax.axis_index("tensor")
    core = dp_pos % 2
    home = core == y_pos
    routes = Routes(dp_n)
    grid3 = dp_n == 16
    x_pos = (dp_pos // 2) % 2
    half_at = (x_pos if grid3 else x_pos * 0).astype(jnp.int32).reshape(1)
    tokens_n = patches.shape[0]
    slots_per = master_slots.shape[1]
    vec_per = vec_master.shape[1]
    slots_n = slots_per * dp_n
    payload = slots_per * BS + VEC_ROWS

    patches = jnp.where(home, patches, send(patches, routes.core_out))
    cotangent = jnp.where(home, cotangent, send(cotangent, routes.core_out))
    size_row = jnp.where(home, image_size, send(image_size, routes.core_out))[0]
    own_slots = block_slot[0]
    slot_other = send(block_slot, routes.y_all)

    lengths = jnp.where(
        size_row == 0, LEN_A, jnp.where(size_row == 1, LEN_B, jnp.where(size_row == 2, LEN_C, 0))
    )
    order = jnp.arange(IMG_DEV)
    ends_at = jnp.sum(jnp.where(order[None, :] <= order[:, None], lengths[None, :], 0), axis=1)
    places = jnp.arange(tokens_n)
    segment = jnp.sum((places[:, None] >= ends_at[None, :]).astype(jnp.int32), axis=1)
    in_image = segment[:, None] == order[None, :]
    select = jnp.stack(
        [jnp.any(in_image & (size_row == s)[None, :], axis=1) for s in range(3)], axis=1
    )
    valid_col = (segment < IMG_DEV).astype(f32)[:, None]
    seg_col = segment[:, None]
    seg_row = segment[None, :]
    blocks_n = tokens_n // ROWS
    starts = jnp.arange(blocks_n) * ROWS
    begun = ends_at[None, :] <= starts[:, None]
    first_tok = jnp.max(jnp.where(begun, ends_at[None, :], 0), axis=1)
    after = ends_at[None, :] > (starts + ROWS - 1)[:, None]
    last_tok = jnp.min(jnp.where(after, ends_at[None, :], tokens_n), axis=1)
    first_blk = (first_tok // ROWS).astype(jnp.int32)
    last_blk = ((last_tok + ROWS - 1) // ROWS).astype(jnp.int32)
    first_key = (first_tok // KEYS).astype(jnp.int32)
    last_key = ((last_tok + KEYS - 1) // KEYS).astype(jnp.int32)

    select_low = select.astype(bf16)
    class_col = jnp.sum(jnp.where(select, jnp.arange(1, 4)[None, :], 0), axis=1, keepdims=True) - 1
    present = jnp.any(select.reshape(blocks_n, ROWS, 3), axis=1).astype(jnp.int32)

    def expand(which, rows):
        return expand_call(which, present, half_at, rows, class_col, pinv)

    vec_low = jnp.pad(vec_master[0].astype(bf16), (0, VEC_ROWS * BS - vec_per))
    own_pack = jnp.concatenate(
        [
            master_slots[0].astype(bf16).reshape(slots_per * BS, BS),
            vec_low.reshape(VEC_ROWS, BS),
        ],
        axis=0,
    )
    flag = home.astype(jnp.int32).reshape(1)
    if grid3:
        z_pos = dp_pos // 4
        pack = own_pack
        chunks, first, second, owner = [], [], [], []
        middle_row = slots_per * BS // 2
        for j in range(4):
            beside_x, beside_y = send(pack, routes.x_all), send(pack, routes.y_all)
            further = [send(pack, routes.z_all)] if j < 3 else []
            work = [slot_other] if j == 0 else []
            beside_x, beside_y, patches, chunk, *more = fence(
                beside_x, beside_y, patches, expand(j, patches), *further, *work
            )
            chunks.append(chunk)
            if j < 3:
                further = more.pop(0)
            if j == 0:
                [slot_other] = more
            corner = jnp.concatenate(
                [send(beside_x[:middle_row], routes.y_all), send(beside_y[middle_row:], routes.x_all)],
                axis=0,
            )
            near_two = send(jnp.where(home, beside_y, pack), routes.core_all)
            far_two = send(jnp.where(home, corner, beside_x), routes.core_all)
            first += [pack, near_two, beside_x, far_two]
            second += [beside_y, near_two, corner, far_two]
            for x_rel in range(2):
                for n in range(2):
                    owner.append(((z_pos - j) % 4) * 4 + (x_pos ^ x_rel) * 2 + (core ^ n))
            if j < 3:
                pack = further
        first = [v[None] for v in first]
        second = [v[None] for v in second]
        owner = jnp.stack(owner).astype(jnp.int32)
    else:
        everything = lax.all_gather(own_pack, AXES, axis=0)
        everything = everything.reshape(dp_n, TENSOR, payload, BS)
        first = [jnp.where(core == 0, everything[:, 0], everything[:, 1])]
        second = []
        owner = jnp.arange(dp_n, dtype=jnp.int32)
        chunks = [expand(c, patches) for c in range(CHUNKS)]
    slot_list = jnp.where(home, block_slot, slot_other)[0]
    named = slot_list[None, :] == jnp.arange(slots_n)[:, None]
    used = jnp.any(named, axis=1)
    drow = jnp.where(used, jnp.sum(jnp.where(named, TARGET_ROW[None, :], 0), axis=1), -1)
    dcol = jnp.sum(jnp.where(named, TARGET_COL[None, :], 0), axis=1)
    weights, vec_rows = gather_tiles(first, second, owner, drow, dcol, flag, slots_per, dp_n)
    vec = vec_rows.reshape(dp_n, VEC_ROWS * BS)[:, :vec_per].astype(f32).reshape(1, dp_n * vec_per)

    embedded = embed_call(half_at, chunks, vec, weights)
    embedded_other = send(embedded, routes.core_all)
    core_flag = core.astype(jnp.int32).reshape(1)

    caches = []
    hidden, own, recv = None, embedded, embedded_other
    for layer in range(LAYERS):
        hidden, normed, queries, keys, values = qkv_call(
            layer, hidden, own, recv, core_flag, vec, weights
        )
        mixed, lse, part = attend_call(
            layer, first_blk, last_blk, queries, keys, values, seg_col, seg_row, vec, weights
        )
        other = send(part, routes.core_all)
        middle, normed2, act, slope, own = mlp_call(layer, hidden, part, other, vec, weights)
        recv = send(own, routes.core_all)
        caches.append((hidden, normed, queries, keys, values, mixed, lse, middle, normed2, act, slope))
        hidden = middle
    out_low = ((hidden + (own.astype(f32) + recv.astype(f32))) * valid_col).astype(bf16)

    owners = jnp.arange(dp_n)
    if grid3:
        place = (
            ((z_pos - 1 - owners // 4) % 4) * 4
            + (x_pos ^ ((owners // 2) % 2)) * 2
            + (core ^ (owners % 2))
        ).astype(jnp.int32)
    else:
        place = owners.astype(jnp.int32)
    slot_owner = slot_list // slots_per
    owner_place = jnp.sum(
        jnp.where(slot_owner[:, None] == owners[None, :], place[None, :], 0), axis=1
    )
    tile_pos = (owner_place * payload + (slot_list % slots_per) * BS).astype(jnp.int32)
    vec_pos = (place * payload + slots_per * BS).astype(jnp.int32)
    total_rows = dp_n * payload
    where_to = jnp.concatenate([half_at, flag if grid3 else flag * 0 + 1])
    offsets = {"base": 0}
    count = BASE_PIX // BS * (HALF // BS)
    for layer in range(LAYERS):
        for name, size in (("qkv", 3 * D * HALF), ("out", D * HALF), ("up", D * HALF_FF), ("down", D * HALF_FF)):
            offsets[name, layer] = count
            count += size // (BS * BS)

    def place_tiles(key, matrix, arrived, buffer):
        tiles = matrix.size // (BS * BS)
        pos = tile_pos[offsets[key] : offsets[key] + tiles]
        rows_n = matrix.shape[0] // 2 if matrix.shape[0] > HALF else HALF
        return scatter_matrix(pos, matrix, arrived, where_to, buffer, total_rows, rows_n)

    def place_base(rel, matrix, arrived, buffer):
        size = BASE_PIX * HALF // (BS * BS) // 2
        low_pos, high_pos = tile_pos[:size], tile_pos[size : 2 * size]
        pos = jnp.where(half_at[0] == rel, low_pos, high_pos)
        return scatter_matrix(pos, matrix, arrived, where_to, buffer, total_rows, D)

    def over(matrix):
        return send(matrix, routes.y_in) if grid3 else None

    def beside(matrix):
        return send(other_half(half_at, matrix), routes.x_away) if grid3 else None

    def summed(matrix, arrived):
        return half_sum(half_at, matrix, arrived) if grid3 else None

    def hold(*arrays):
        kept = [a for a in arrays if a is not None]
        done = iter(fence(*kept))
        return [None if a is None else next(done) for a in arrays]

    top, low = 1, 0
    vec_grads = [None] * LAYERS

    def mlp_step(layer, grad, own, recv):
        middle, normed2, act, slope = caches[layer][7:11]
        made = mlp_back_call(layer, grad, own, recv, valid_col, middle, slope, vec, weights)
        if own is not None:
            return made
        return [made[0]] + list(made)

    def attend_step(layer, grad, part, other, lse):
        hid_in, normed, queries, keys, values, mixed = caches[layer][:6]
        return attend_back_call(
            layer, first_key, last_key, grad, part, other, queries, keys, values, mixed, lse,
            seg_col, seg_row, weights,
        )

    grad, grad_low, du, part, dg2, ds2, db1, db2 = mlp_step(top, cotangent, None, None)
    other = send(part, routes.core_all)
    gd1 = dot_tn(caches[top][9], grad_low).astype(bf16)
    gu1 = dot_tn(caches[top][8], du).astype(bf16)
    ad1 = over(gd1)
    lse, gu1 = fence(caches[top][6], gu1)
    xu1 = beside(gu1)
    grad, grad_low, dq, dk, dv, dbo = attend_step(top, grad, part, other, lse)
    vec, dbo, ad1, xu1, out_low = hold(vec, dbo, ad1, xu1, out_low)
    au1 = over(summed(gu1, xu1))
    own, dg1, ds1, dbq, dbv = qkv_back_call(top, dq, dk, dv, caches[top][0], vec, weights)
    recv = send(own, routes.core_all)
    go1 = dot_tn(caches[top][5], grad_low).astype(bf16)
    gq1 = dot_tn(caches[top][1], jnp.concatenate([dq, dk, dv], axis=1)).astype(bf16)
    vec_grads[top] = [dg1, ds1, dbq, dbv, dbo, dg2, ds2, db1, db2]
    xq1, ao1 = beside(gq1), over(go1)
    grad, grad_low, du, part, dg2, ds2, db1, db2 = mlp_step(low, grad, own, recv)
    other = send(part, routes.core_all)
    db2, xq1, au1 = hold(db2, xq1, au1)
    aq1 = over(summed(gq1, xq1))
    gd0 = dot_tn(caches[low][9], grad_low).astype(bf16)
    gu0 = dot_tn(caches[low][8], du).astype(bf16)
    lse, gd0, gu0, ao1, aq1 = hold(caches[low][6], gd0, gu0, ao1, aq1)
    ad0 = over(gd0)
    xu0 = beside(gu0)
    buffer = place_tiles(("down", top), gd1, ad1, None)
    buffer = place_tiles(("up", top), gu1, au1, buffer)
    grad, grad_low, dq, dk, dv, dbo = attend_step(low, grad, part, other, lse)
    vec, dbo, ad0, xu0, buffer = hold(vec, dbo, ad0, xu0, buffer)
    au0 = over(summed(gu0, xu0))
    own, dg1, ds1, dbq, dbv = qkv_back_call(low, dq, dk, dv, caches[low][0], vec, weights)
    recv = send(own, routes.core_all)
    gq0 = dot_tn(caches[low][1], jnp.concatenate([dq, dk, dv], axis=1)).astype(bf16)
    vec_grads[low] = [dg1, ds1, dbq, dbv, dbo, dg2, ds2, db1, db2]
    xq0 = beside(gq0)
    turn = jnp.zeros((8, BS), f32)
    grad_emb, grad_emb_bias = embed_back_call(core_flag, turn, grad, own, recv)
    middle = CHUNKS // 2

    def base_grad(parts):
        return jnp.concatenate([dot_tn(c, grad_emb).astype(bf16) for c in parts], axis=0)

    gbt = base_grad(chunks[middle:])
    gbt, au0, xq0 = hold(gbt, au0, xq0)
    xb = send(gbt, routes.x_away) if grid3 else None
    aq0 = over(summed(gq0, xq0))
    gbm = base_grad(chunks[:middle])
    vec_grad = pack_call([grad_emb_bias] + vec_grads[0] + vec_grads[1], dp_n, vec_per)
    go0 = dot_tn(caches[low][5], grad_low).astype(bf16)
    ao0, av = over(go0), over(vec_grad)
    buffer = place_tiles(("out", top), go1, ao1, buffer)
    buffer = place_tiles(("qkv", top), gq1, aq1, buffer)
    buffer = place_tiles(("down", low), gd0, ad0, buffer)
    gbm, xb, aq0, ao0, av, buffer = hold(gbm, xb, aq0, ao0, av, buffer)
    ab = over(half_sum(half_at * 0, gbm, xb)) if grid3 else None
    buffer = place_tiles(("up", low), gu0, au0, buffer)
    buffer = place_base(1, gbt, None, buffer)
    buffer = scatter_vec(vec_pos, vec_grad, av, buffer)
    buffer = place_tiles(("qkv", low), gq0, aq0, buffer)
    buffer = place_tiles(("out", low), go0, ao0, buffer)
    base_weight = weights["base", 0]
    ab, buffer, base_weight, out_low = hold(ab, buffer, base_weight, out_low)
    weights["base", 0] = base_weight
    buffer = place_base(0, gbm, ab, buffer)

    if grid3:
        token = jnp.zeros((8, BS), f32)
        order = (1, 0)
        resized = resize_call(weights, pinv)
        carried = {n: None for n in order}
        blocks = buffer.reshape(4, 2, 2, payload, BS)
        across = {order[1]: send(blocks[0, 1, order[1]], routes.x_home), order[0]: None}
        following = {order[1]: blocks[1, 1, order[1]], order[0]: blocks[2, 1, order[0]]}
        far_side = send(blocks[0, 1, order[0]], routes.z_home)
        carried[order[0]] = send(blocks[0, 0, order[0]], routes.z_home)
        rounded = {}
        for j in range(4):
            for n in order:
                extra = None
                if j == 0 and n == order[0]:
                    token, far_side, resized = hold(token, far_side, resized)
                    later, unused = reduce_call(1, n, buffer, far_side, None, payload, 1)
                    across[n] = send(later, routes.x_home)
                    continue
                token, across[n], carried[n], extra = hold(token, across[n], carried[n], extra)
                if extra is not None:
                    resized = extra
                arrived = across[n]
                if j < 3:
                    across[n] = send(following[n], routes.x_home)
                total, following[n] = reduce_call(j, n, buffer, arrived, carried[n], payload)
                if j < 3:
                    carried[n] = send(total, routes.z_home)
                else:
                    rounded[n] = total
        near_grad, far_grad = rounded[0], send(rounded[1], routes.core_out)
    else:
        held = buffer.reshape(dp_n, 1, payload, BS).astype(f32)
        nothing = jnp.zeros_like(held)
        both = jnp.concatenate(
            [jnp.where(core == 0, held, nothing), jnp.where(core == 0, nothing, held)], axis=1
        )
        used_rows = jnp.repeat(used, BS).reshape(dp_n, 1, slots_per * BS, 1)
        used_rows = jnp.concatenate(
            [used_rows, jnp.ones((dp_n, 1, VEC_ROWS, 1), bool)], axis=2
        )
        both = jnp.where(used_rows, both, 0.0).reshape(dp_n * TENSOR * payload, BS)
        near_grad = lax.psum_scatter(both, AXES, scatter_dimension=0, tiled=True).astype(bf16)
        far_grad = near_grad
        resized = resize_call(weights, pinv)

    output = jnp.where(home, out_low, send(out_low, routes.y_out)).astype(f32)
    grad_pixels = sum(
        dot(grad_emb * select_low[:, s : s + 1], resized[s]) for s in range(3)
    ).astype(bf16)
    pixels_other = send(grad_pixels, routes.core_all)
    pixel_sides = [
        grad_pixels[:, s * HALF : (s + 1) * HALF].astype(f32)
        + pixels_other[:, s * HALF : (s + 1) * HALF].astype(f32)
        for s in range(TENSOR)
    ]
    near = jnp.where(core == 0, pixel_sides[0], pixel_sides[1])
    far = jnp.where(core == 0, pixel_sides[1], pixel_sides[0]).astype(bf16)
    patch_grad = jnp.where(home, near, send(far, routes.y_out).astype(f32))

    my_slots = dp_pos * slots_per + jnp.arange(slots_per)
    mine_used = jnp.any(own_slots[None, :] == my_slots[:, None], axis=1).astype(jnp.int32)
    owned_grad, new_master, new_mom, new_var = owner_call(
        mine_used, flag, near_grad, far_grad, master_slots[0], left_basis[0], right_basis[0], mom_slots[0], var_slots[0]
    )
    vec_rows = jnp.where(home, near_grad[slots_per * BS :], far_grad[slots_per * BS :])
    owned_vec_grad = vec_rows.astype(f32).reshape(VEC_ROWS * BS)[:vec_per]
    new_vec_mom = decay * vec_mom[0] + (1.0 - decay) * owned_vec_grad
    new_vec_var = decay * vec_var[0] + (1.0 - decay) * owned_vec_grad * owned_vec_grad
    new_vec = vec_master[0] - vector_rate * new_vec_mom / (jnp.sqrt(new_vec_var) + adam_eps)
    return (
        output,
        patch_grad,
        owned_grad[None],
        new_master[None],
        new_mom[None],
        new_var[None],
        owned_vec_grad[None],
        new_vec[None],
        new_vec_mom[None],
        new_vec_var[None],
    )


def solution(mesh):
    slots = P("tensor", "dp", None, None)
    vectors = P("tensor", "dp")
    tokens = P("dp", None)
    in_specs = (tokens, tokens, tokens, P("tensor", None), P()) + (slots,) * 5 + (vectors,) * 3
    out_specs = (tokens, P("dp", "tensor")) + (slots,) * 4 + (vectors,) * 4
    return jax.shard_map(shards, mesh=mesh, in_specs=in_specs, out_specs=out_specs, check_vma=False)
```

```python
import functools

import jax
import jax.numpy as jnp
import numpy as np
from jax import lax
from jax.experimental import pallas as pl
from jax.experimental.pallas import tpu as pltpu
from jax.sharding import PartitionSpec as P

D = 768
HEAD_DIM = 64
FF = 3072
BASE_PIX = 3072
LAYERS = 2
LEN_A = 196
LEN_B = 225
LEN_C = 576
IMG_DEV = 5
BS = 128
TENSOR = 2
HALF = D // TENSOR
HALF_FF = FF // TENSOR
HEADS = HALF // HEAD_DIM
ROWS = 256
KEYS = 512
VEC_ROWS = 16
CHUNKS = 4

AXES = ("dp", "tensor")
precise = lax.Precision.HIGHEST
masked_score = -1e30
norm_eps = 1e-06
adam_eps = 1e-08
decay = 0.5
matrix_rate = 0.05
vector_rate = 0.3
f32 = jnp.float32
bf16 = jnp.bfloat16
MIB = 1024 * 1024

WEIGHTS = [("base", 0, BASE_PIX)]
for layer in range(LAYERS):
    WEIGHTS += [("qkv", layer, 3 * D), ("out", layer, D), ("up", layer, FF), ("down", layer, FF)]
STARTS = {}
PANEL_ROWS = 0
for name, layer, size in WEIGHTS:
    STARTS[name, layer] = PANEL_ROWS
    PANEL_ROWS += size


def tile_targets():
    rows, cols = [], []

    def add(start, rows_n, cols_n):
        for i in range(rows_n // BS):
            for j in range(cols_n // BS):
                panel, inner = divmod(j * BS, HALF)
                rows.append(start + panel * rows_n + i * BS)
                cols.append(inner)

    add(STARTS["base", 0], BASE_PIX, HALF)
    for layer in range(LAYERS):
        add(STARTS["qkv", layer], D, 3 * HALF)
        add(STARTS["out", layer], HALF, D)
        add(STARTS["up", layer], D, HALF_FF)
        add(STARTS["down", layer], HALF_FF, D)
    return np.array(rows, np.int32), np.array(cols, np.int32)


TARGET_ROW, TARGET_COL = tile_targets()
LAYER_VECS = (D, D, HALF, HALF, D, D, D, HALF_FF, D)
VEC_NAMES = ("g1", "s1", "bq", "bv", "bo", "g2", "s2", "b1", "b2")


def vec_offsets():
    offset = HALF
    found = []
    for layer in range(LAYERS):
        here = {}
        for name, length in zip(VEC_NAMES, LAYER_VECS):
            here[name] = (offset, length)
            offset += length
        found.append(here)
    return found


VEC_AT = vec_offsets()


def params(limit=24):
    return pltpu.CompilerParams(
        dimension_semantics=("arbitrary",), vmem_limit_bytes=limit * MIB
    )


def cost(flops, nbytes, trans=0):
    return pl.CostEstimate(flops=flops, bytes_accessed=nbytes, transcendentals=trans)


def rows_spec(width):
    return pl.BlockSpec((ROWS, width), lambda i, *_: (i, 0))


def fixed(shape, at=0):
    return pl.BlockSpec(shape, lambda i, *_: (at,) + (0,) * (len(shape) - 1))


def vec_piece(vec_ref, layer, name):
    start, length = VEC_AT[layer][name]
    return vec_ref[:, start : start + length]


def dot(left, right):
    return jnp.dot(left, right, preferred_element_type=f32)


def dot_nt(left, right, precision=None):
    return lax.dot_general(
        left, right, (((1,), (1,)), ((), ())), precision=precision, preferred_element_type=f32
    )


def dot_tn(left, right):
    return lax.dot_general(left, right, (((0,), (0,)), ((), ())), preferred_element_type=f32)


def joined(ref, start, rows_n, panels):
    return jnp.concatenate(
        [ref[start + p * rows_n : start + (p + 1) * rows_n, :] for p in range(panels)], axis=1
    )


def norm_stats(values):
    mean_val = jnp.mean(values, axis=-1, keepdims=True)
    centered = values - mean_val
    inv_std = lax.rsqrt(jnp.mean(centered * centered, axis=-1, keepdims=True) + norm_eps)
    return centered * inv_std, inv_std


def norm_back(values, gain, grad):
    unit, inv_std = norm_stats(values)
    scaled = grad * gain
    mean_s = jnp.mean(scaled, axis=-1, keepdims=True)
    mean_u = jnp.mean(scaled * unit, axis=-1, keepdims=True)
    back = inv_std * (scaled - mean_s - unit * mean_u)
    return (
        back,
        jnp.sum(grad * unit, axis=0, keepdims=True),
        jnp.sum(grad, axis=0, keepdims=True),
    )


def accumulate(ref, value):
    first = pl.program_id(0) == 0

    @pl.when(first)
    def _():
        ref[...] = value

    @pl.when(jnp.logical_not(first))
    def _():
        ref[...] += value


def stay(value):
    return pltpu.with_memory_space_constraint(value, pltpu.HBM)


def fence(*arrays):
    def nothing(*refs):
        pass

    anywhere = pl.BlockSpec(memory_space=pl.ANY)
    return pl.pallas_call(
        nothing,
        out_shape=[jax.ShapeDtypeStruct(a.shape, a.dtype) for a in arrays],
        in_specs=[anywhere] * len(arrays),
        out_specs=[anywhere] * len(arrays),
        input_output_aliases={i: i for i in range(len(arrays))},
        compiler_params=pltpu.CompilerParams(vmem_limit_bytes=MIB),
    )(*[stay(a) if a.size > 32 * 1024 else a for a in arrays])


def gather_kernel(slots, count_a, count_b, owner, drow, dcol, flag, *refs):
    first = refs[:count_a]
    second = refs[count_a : count_a + count_b]
    *panels, vectors, held, sem, vec_sem = refs[count_a + count_b :]

    def copy_all(sources):
        at = 0
        for src in sources:
            for n in range(src.shape[0]):
                who = owner[at]
                at += 1

                def body(i, carried, src=src, n=n, who=who):
                    slot = who * slots + i
                    row = drow[slot]

                    @pl.when(row >= 0)
                    def _():
                        start = pl.multiple_of(i * BS, BS)
                        pltpu.make_async_copy(
                            src.at[n, pl.ds(start, BS), :],
                            held.at[
                                pl.ds(pl.multiple_of(row, BS), BS),
                                pl.ds(pl.multiple_of(dcol[slot], BS), BS),
                            ],
                            sem,
                        ).start()

                    return carried

                lax.fori_loop(0, slots, body, 0)
                pltpu.make_async_copy(
                    src.at[n, pl.ds(slots * BS, VEC_ROWS), :], vectors.at[who], vec_sem
                ).start()

    if count_b:

        @pl.when(flag[0] == 1)
        def _():
            copy_all(first)

        @pl.when(flag[0] == 0)
        def _():
            copy_all(second)
    else:
        copy_all(first)
    pltpu.make_async_copy(held, held, sem).wait()
    at = 0
    for panel in panels:
        size = panel.shape[0]
        pltpu.make_async_copy(held.at[pl.ds(at, size), :], panel, sem).start()
        at += size
    pltpu.make_async_copy(vectors, vectors, vec_sem).wait()
    pltpu.make_async_copy(held, held, sem).wait()


def gather_tiles(first, second, owner, drow, dcol, flag, slots, owners):
    anywhere = pl.BlockSpec(memory_space=pl.ANY)
    *panels, vectors = pl.pallas_call(
        functools.partial(gather_kernel, slots, len(first), len(second)),
        out_shape=[pltpu.HBM((size, HALF), bf16) for unused, unused2, size in WEIGHTS]
        + [jax.ShapeDtypeStruct((owners, VEC_ROWS, BS), bf16)],
        grid_spec=pltpu.PrefetchScalarGridSpec(
            num_scalar_prefetch=4,
            grid=(1,),
            in_specs=[anywhere] * (len(first) + len(second)),
            out_specs=[anywhere] * len(WEIGHTS) + [fixed((owners, VEC_ROWS, BS))],
            scratch_shapes=[
                pltpu.VMEM((PANEL_ROWS, HALF), bf16),
                pltpu.SemaphoreType.DMA,
                pltpu.SemaphoreType.DMA,
            ],
        ),
        compiler_params=params(),
        cost_estimate=cost(0, 4 * PANEL_ROWS * HALF),
    )(owner, drow, dcol, flag, *[stay(v) for v in first], *[stay(v) for v in second])
    return {(name, layer): p for (name, layer, unused), p in zip(WEIGHTS, panels)}, vectors


def scatter_kernel(rows_n, cols_n, steps, paired, parts, pos, part, own, *refs):
    @pl.when(part[1] > 0)
    def _():
        scatter_body(rows_n, cols_n, steps, paired, parts, pos, part, own, *refs)


def scatter_body(rows_n, cols_n, steps, paired, parts, pos, part, own, *refs):
    if paired:
        recv, *refs = refs
        span = pl.num_programs(0) // parts
        here = jnp.logical_or(parts == 1, pl.program_id(0) // span == part[0])
    target, buf, sems = refs[-3:]
    step = pl.program_id(0)
    slot = lax.rem(step, 2)
    per = rows_n // BS * (cols_n // BS)

    def wait(at):
        pltpu.make_async_copy(buf.at[at], buf.at[at], sems.at[at]).wait()

    @pl.when(step >= 2)
    def _():
        wait(slot)

    for i in range(rows_n // BS):
        for j in range(cols_n // BS):
            area = (slice(i * BS, (i + 1) * BS), slice(j * BS, (j + 1) * BS))
            value = own[area]
            if paired:
                more = jnp.where(here, recv[area].astype(f32), 0.0)
                value = (value.astype(f32) + more).astype(bf16)
            buf[slot, i * (cols_n // BS) + j] = value
    for n in range(per):
        pltpu.make_async_copy(
            buf.at[slot, n],
            target.at[pl.ds(pl.multiple_of(pos[step * per + n], 16), BS), :],
            sems.at[slot],
        ).start()

    @pl.when(step == pl.num_programs(0) - 1)
    def _():
        if steps > 1:
            wait(1 - slot)
        wait(slot)


def scatter_matrix(pos, own, recv, part, target, total_rows, rows_n):
    cols_n = own.shape[1]
    steps = own.shape[0] // rows_n
    anywhere = pl.BlockSpec(memory_space=pl.ANY)
    block = pl.BlockSpec((rows_n, cols_n), lambda i, *_: (i, 0))
    paired = recv is not None
    parts = own.shape[0] // recv.shape[0] if paired else 1
    span = steps // parts
    arrived = pl.BlockSpec(
        (rows_n, cols_n), lambda i, pos, part: (jnp.clip(i - part[0] * span, 0, span - 1), 0)
    )
    operands = [stay(own)] + ([stay(recv)] if paired else []) + ([] if target is None else [stay(target)])
    specs = [block] + ([block if parts == 1 else arrived] if paired else [])
    specs += [] if target is None else [anywhere]
    return pl.pallas_call(
        functools.partial(scatter_kernel, rows_n, cols_n, steps, paired, parts),
        out_shape=pltpu.HBM((total_rows, BS), bf16),
        grid_spec=pltpu.PrefetchScalarGridSpec(
            num_scalar_prefetch=2,
            grid=(steps,),
            in_specs=specs,
            out_specs=anywhere,
            scratch_shapes=[
                pltpu.VMEM((2, rows_n // BS * (cols_n // BS), BS, BS), bf16),
                pltpu.SemaphoreType.DMA((2,)),
            ],
        ),
        input_output_aliases={} if target is None else {len(operands) + 1: 0},
        compiler_params=params(12),
        cost_estimate=cost(own.size, own.size * 6),
    )(pos, part, *operands)


def half_sum_kernel(part, own, arrived, out):
    out[...] = (own[...].astype(f32) + arrived[...].astype(f32)).astype(bf16)


def half_sum(part, own, arrived):
    block = arrived.shape
    return pl.pallas_call(
        half_sum_kernel,
        out_shape=pltpu.HBM(block, bf16),
        grid_spec=pltpu.PrefetchScalarGridSpec(
            num_scalar_prefetch=1,
            grid=(1,),
            in_specs=[pl.BlockSpec(block, lambda i, part: (part[0], 0)), fixed(block)],
            out_specs=fixed(block),
        ),
        compiler_params=params(8),
        cost_estimate=cost(arrived.size, arrived.size * 6),
    )(part, stay(own), stay(arrived))


def half_copy_kernel(part, own, out):
    out[...] = own[...]


def other_half(part, own):
    block = (own.shape[0] // 2, own.shape[1])
    return pl.pallas_call(
        half_copy_kernel,
        out_shape=pltpu.HBM(block, bf16),
        grid_spec=pltpu.PrefetchScalarGridSpec(
            num_scalar_prefetch=1,
            grid=(1,),
            in_specs=[pl.BlockSpec(block, lambda i, part: (1 - part[0], 0))],
            out_specs=fixed(block),
        ),
        compiler_params=params(8),
        cost_estimate=cost(0, own.size * 2),
    )(part, stay(own))


def scatter_vec_kernel(paired, pos, own, *refs):
    if paired:
        recv, *refs = refs
    target, buf, sem = refs[-3:]
    value = own[...]
    if paired:
        value = (value.astype(f32) + recv[...].astype(f32)).astype(bf16)
    buf[...] = value

    def body(n, carried):
        pltpu.make_async_copy(
            buf.at[n], target.at[pl.ds(pl.multiple_of(pos[n], 16), VEC_ROWS), :], sem
        ).start()
        return carried

    lax.fori_loop(0, own.shape[0], body, 0)
    pltpu.make_async_copy(buf, buf, sem).wait()


def scatter_vec(pos, own, recv, target):
    anywhere = pl.BlockSpec(memory_space=pl.ANY)
    block = fixed(own.shape)
    paired = recv is not None
    operands = [own] + ([recv] if paired else []) + [stay(target)]
    return pl.pallas_call(
        functools.partial(scatter_vec_kernel, paired),
        out_shape=pltpu.HBM(target.shape, bf16),
        grid_spec=pltpu.PrefetchScalarGridSpec(
            num_scalar_prefetch=1,
            grid=(1,),
            in_specs=[block] * (len(operands) - 1) + [anywhere],
            out_specs=anywhere,
            scratch_shapes=[pltpu.VMEM(own.shape, bf16), pltpu.SemaphoreType.DMA],
        ),
        input_output_aliases={len(operands): 0},
        compiler_params=params(4),
    )(pos, *operands)


def expand_kernel(present, half, patch_ref, class_ref, pinv_ref, out, total):
    for block in range(patch_ref.shape[0] // ROWS):
        rows = slice(block * ROWS, (block + 1) * ROWS)
        total[...] = jnp.zeros_like(total)
        for which in range(3):

            @pl.when(present[block, which] > 0)
            def _(which=which, rows=rows):
                chosen = jnp.where(class_ref[rows, :] == which, patch_ref[rows, :].astype(f32), 0.0)
                total[...] += dot_nt(chosen.astype(bf16), pinv_ref[which])

        out[rows, :] = total[...].astype(bf16)


def expand_call(which, present, half, patches, class_col, pinv):
    tokens = patches.shape[0]
    size = BASE_PIX // CHUNKS
    step = size
    return pl.pallas_call(
        expand_kernel,
        out_shape=jax.ShapeDtypeStruct((tokens, size), bf16),
        grid_spec=pltpu.PrefetchScalarGridSpec(
            num_scalar_prefetch=2,
            grid=(1,),
            in_specs=[
                fixed(patches.shape),
                fixed(class_col.shape),
                pl.BlockSpec(
                    (3, step, pinv.shape[2]),
                    lambda i, present, half: (0, (which + half[0] * (CHUNKS // 2)) % CHUNKS, 0),
                ),
            ],
            out_specs=pl.BlockSpec((tokens, step), lambda i, *_: (0, i)),
            scratch_shapes=[pltpu.VMEM((ROWS, step), f32)],
        ),
        compiler_params=params(),
        cost_estimate=cost(3 * tokens * size * D, tokens * size * 4 + size * D * 6),
    )(present, half, stay(patches), class_col, stay(pinv))


def resize_kernel(base, pinv_ref, out, turned):
    @pl.when(pl.program_id(0) == 0)
    def _():
        turned[...] = base[...].T

    out[0] = dot(turned[...], pinv_ref[0]).astype(bf16)


def resize_call(weights, pinv):
    return pl.pallas_call(
        resize_kernel,
        out_shape=jax.ShapeDtypeStruct((3, HALF, pinv.shape[2]), bf16),
        grid=(3,),
        in_specs=[
            fixed((BASE_PIX, HALF)),
            pl.BlockSpec((1, BASE_PIX, pinv.shape[2]), lambda i: (i, 0, 0)),
        ],
        out_specs=pl.BlockSpec((1, HALF, pinv.shape[2]), lambda i: (i, 0, 0)),
        scratch_shapes=[pltpu.VMEM((HALF, BASE_PIX), bf16)],
        compiler_params=params(),
        cost_estimate=cost(6 * D * BASE_PIX * HALF, 6 * D * BASE_PIX),
    )(stay(weights["base", 0]), stay(pinv))


def embed_back_kernel(core, token, base, own, recv, out, bias):
    low = (base[...] + (own[...].astype(f32) + recv[...].astype(f32))).astype(bf16)
    out[...] = low
    accumulate(bias, jnp.sum(low.astype(f32), axis=0, keepdims=True))


def embed_back_call(core, token, base, own, recv):
    tokens = base.shape[0]
    half = pl.BlockSpec((ROWS, HALF), lambda i, core: (i, core[0]))
    return pl.pallas_call(
        embed_back_kernel,
        out_shape=[
            jax.ShapeDtypeStruct((tokens, HALF), bf16),
            jax.ShapeDtypeStruct((1, HALF), f32),
        ],
        grid_spec=pltpu.PrefetchScalarGridSpec(
            num_scalar_prefetch=1,
            grid=(tokens // ROWS,),
            in_specs=[fixed(token.shape)] + [half] * 3,
            out_specs=[rows_spec(HALF), fixed((1, HALF))],
        ),
        compiler_params=params(8),
        cost_estimate=cost(tokens * D, tokens * D * 5),
    )(core, token, base, own, recv)


def pack_kernel(vec_per, *refs):
    *pieces, out = refs
    out[...] = jnp.zeros_like(out)
    at = 0
    for piece in pieces:
        for k in range(piece.shape[1] // BS):
            owner, row = divmod(at, vec_per // BS)
            out[owner, row : row + 1, :] = piece[:, k * BS : (k + 1) * BS]
            at += 1


def pack_call(pieces, owners, vec_per):
    if vec_per % BS:
        joined = jnp.concatenate(pieces, axis=1)[0]
        joined = jnp.pad(joined, (0, owners * vec_per - joined.shape[0])).reshape(owners, vec_per)
        joined = jnp.pad(joined, ((0, 0), (0, VEC_ROWS * BS - vec_per)))
        return joined.astype(bf16).reshape(owners, VEC_ROWS, BS)
    return pl.pallas_call(
        functools.partial(pack_kernel, vec_per),
        out_shape=jax.ShapeDtypeStruct((owners, VEC_ROWS, BS), f32),
        grid=(1,),
        in_specs=[fixed(p.shape) for p in pieces],
        out_specs=fixed((owners, VEC_ROWS, BS)),
        compiler_params=params(4),
        cost_estimate=cost(0, owners * vec_per * 8),
    )(*pieces).astype(bf16)


def embed_kernel(half, *refs):
    *parts, vec, weight, out = refs
    size = BASE_PIX // CHUNKS
    total = vec[:, :HALF]
    for c in range(CHUNKS):
        at = lax.rem(c + half[0] * (CHUNKS // 2), CHUNKS)
        rows = pl.ds(pl.multiple_of(at * size, size), size)
        total = total + dot(parts[c][...], weight[rows, :])
    out[...] = total.astype(bf16)


def embed_call(half, chunks, vec, weights):
    tokens = chunks[0].shape[0]
    return pl.pallas_call(
        embed_kernel,
        out_shape=jax.ShapeDtypeStruct((tokens, HALF), bf16),
        grid_spec=pltpu.PrefetchScalarGridSpec(
            num_scalar_prefetch=1,
            grid=(tokens // ROWS,),
            in_specs=[rows_spec(BASE_PIX // CHUNKS)] * CHUNKS
            + [fixed(vec.shape), fixed((BASE_PIX, HALF))],
            out_specs=rows_spec(HALF),
        ),
        compiler_params=params(),
        cost_estimate=cost(2 * tokens * BASE_PIX * HALF, tokens * BASE_PIX * 3),
    )(half, *[stay(c) for c in chunks], vec, stay(weights["base", 0]))


def qkv_kernel(layer, first, core, *refs):
    if first:
        own, recv, vec, weight, hid, normed, q_ref, k_ref, v_ref = refs
        mine, theirs = own[...].astype(f32), recv[...].astype(f32)
        low = core[0] == 0
        values = jnp.concatenate(
            [jnp.where(low, mine, theirs), jnp.where(low, theirs, mine)], axis=1
        )
    else:
        base, own, recv, vec, weight, hid, normed, q_ref, k_ref, v_ref = refs
        values = base[...] + (own[...].astype(f32) + recv[...].astype(f32))
    hid[...] = values
    unit, unused = norm_stats(values)
    low = (unit * vec_piece(vec, layer, "g1") + vec_piece(vec, layer, "s1")).astype(bf16)
    normed[...] = low
    made = dot(low, joined(weight, 0, D, 3))
    q_ref[...] = (made[:, :HALF] + vec_piece(vec, layer, "bq")).astype(bf16)
    k_ref[...] = made[:, HALF : 2 * HALF].astype(bf16)
    v_ref[...] = (made[:, 2 * HALF :] + vec_piece(vec, layer, "bv")).astype(bf16)


def qkv_call(layer, base, own, recv, core, vec, weights):
    tokens = own.shape[0]
    shape = lambda width, kind: jax.ShapeDtypeStruct((tokens, width), kind)
    outs = [shape(D, f32), pltpu.HBM((tokens, D), bf16)] + [shape(HALF, bf16)] * 3
    operands = ([] if base is None else [base]) + [own, recv]
    return pl.pallas_call(
        functools.partial(qkv_kernel, layer, base is None),
        out_shape=outs,
        grid_spec=pltpu.PrefetchScalarGridSpec(
            num_scalar_prefetch=1,
            grid=(tokens // ROWS,),
            in_specs=[rows_spec(o.shape[1]) for o in operands]
            + [fixed(vec.shape), fixed((3 * D, HALF))],
            out_specs=[rows_spec(o.shape[1]) for o in outs],
        ),
        compiler_params=params(),
        cost_estimate=cost(2 * tokens * D * 3 * HALF, tokens * D * 14),
    )(core, *operands, vec, weights["qkv", layer])


def head_masks():
    lane = lax.broadcasted_iota(jnp.int32, (1, 2 * HEAD_DIM), 1)
    low = (lane < HEAD_DIM).astype(f32).astype(bf16)
    high = (lane >= HEAD_DIM).astype(f32).astype(bf16)
    return low, high


def attend_kernel(
    layer, low_ref, high_ref, q_ref, k_ref, v_ref, seg_q, seg_k, vec, w_out, o_ref, lse_ref, part,
    scores_ref, top_ref, acc_ref,
):
    step = pl.program_id(0)
    first, last = low_ref[step], high_ref[step]
    masks = head_masks()
    scale = jnp.asarray(HEAD_DIM ** (-0.5), bf16)
    lane = lax.broadcasted_iota(jnp.int32, (1, BS), 1)
    sums = [(lane == HEAD_DIM).astype(f32).astype(bf16), (lane == 0).astype(f32).astype(bf16)]
    top_ref[...] = jnp.full(top_ref.shape, masked_score, f32)
    acc_ref[...] = jnp.zeros_like(acc_ref)
    seg_col = seg_q[...]

    def score_block(block, carried):
        rows = pl.ds(pl.multiple_of(block * ROWS, ROWS), ROWS)
        same = seg_col == seg_k[:, rows]
        for pair in range(HEADS // 2):
            cols = slice(pair * BS, (pair + 1) * BS)
            q_two = q_ref[:, cols] * scale
            k_two = k_ref[rows, cols]
            for side in range(2):
                head = 2 * pair + side
                scores = jnp.where(same, dot_nt(q_two * masks[side], k_two), masked_score)
                scores_ref[head, block] = scores
                top = top_ref[head]
                for piece in range(ROWS // BS):
                    top = jnp.maximum(top, scores[:, piece * BS : (piece + 1) * BS])
                top_ref[head] = top
        return carried

    lax.fori_loop(first, last, score_block, 0)
    tops = [jnp.max(top_ref[head], axis=1, keepdims=True) for head in range(HEADS)]

    def mix_block(block, carried):
        rows = pl.ds(pl.multiple_of(block * ROWS, ROWS), ROWS)
        for pair in range(HEADS // 2):
            v_two = v_ref[rows, pair * BS : (pair + 1) * BS]
            for side in range(2):
                head = 2 * pair + side
                expo = jnp.exp(scores_ref[head, block] - tops[head]).astype(bf16)
                acc_ref[head] += dot(expo, v_two * masks[side] + sums[side])
        return carried

    lax.fori_loop(first, last, mix_block, 0)
    totals = jnp.zeros((ROWS, BS), f32)
    for pair in range(HEADS // 2):
        sides = []
        for side in range(2):
            head = 2 * pair + side
            mixed = acc_ref[head]
            at = HEAD_DIM * (1 - side)
            total = mixed[:, at : at + 1]
            totals = jnp.where(lane == head, tops[head] + jnp.log(total), totals)
            sides.append(mixed * (1.0 / total))
        o_ref[:, pair * BS : (pair + 1) * BS] = jnp.where(lane < HEAD_DIM, *sides).astype(bf16)
    lse_ref[...] = totals.T[0:8, :]
    low = o_ref[...]
    bias = vec_piece(vec, layer, "bo")
    part[...] = (dot(low, joined(w_out, 0, HALF, TENSOR)) + bias).astype(bf16)


def attend_call(layer, first, last, queries, keys, values, seg_col, seg_row, vec, weights):
    tokens = queries.shape[0]
    return pl.pallas_call(
        functools.partial(attend_kernel, layer),
        out_shape=[
            jax.ShapeDtypeStruct((tokens, HALF), bf16),
            jax.ShapeDtypeStruct((8, tokens), f32),
            jax.ShapeDtypeStruct((tokens, D), bf16),
        ],
        grid_spec=pltpu.PrefetchScalarGridSpec(
            num_scalar_prefetch=2,
            grid=(tokens // ROWS,),
            in_specs=[
                rows_spec(HALF),
                fixed(keys.shape),
                fixed(values.shape),
                rows_spec(1),
                fixed(seg_row.shape),
                fixed(vec.shape),
                fixed((D, HALF)),
            ],
            out_specs=[
                rows_spec(HALF),
                pl.BlockSpec((8, ROWS), lambda i, *_: (0, i)),
                rows_spec(D),
            ],
            scratch_shapes=[
                pltpu.VMEM((HEADS, tokens // ROWS, ROWS, ROWS), f32),
                pltpu.VMEM((HEADS, ROWS, BS), f32),
                pltpu.VMEM((HEADS, ROWS, BS), f32),
            ],
        ),
        compiler_params=params(),
        cost_estimate=cost(8 * HEADS * tokens * tokens * BS, tokens * D * 8, HEADS * tokens * tokens),
    )(first, last, queries, keys, values, seg_col, seg_row, vec, weights["out", layer])


def gelu_parts(values):
    cdf = 0.5 * (1.0 + lax.erf(values * 0.7071067811865476))
    pdf = 0.3989422804014327 * jnp.exp(-0.5 * values * values)
    return values * cdf, cdf + values * pdf


def mlp_kernel(layer, base, own, recv, vec, w_up, w_down, hid, normed, act, slope, part):
    values = base[...] + (own[...].astype(f32) + recv[...].astype(f32))
    hid[...] = values
    unit, unused = norm_stats(values)
    low = (unit * vec_piece(vec, layer, "g2") + vec_piece(vec, layer, "s2")).astype(bf16)
    normed[...] = low
    bias_up = vec_piece(vec, layer, "b1")
    for pair in range(HALF_FF // D):
        area = slice(pair * D, (pair + 1) * D)
        up = dot(low, joined(w_up, pair * 2 * D, D, 2)) + bias_up[:, area]
        gelu, grad = gelu_parts(up)
        act[:, area] = gelu.astype(bf16)
        slope[:, area] = grad.astype(bf16)
    bias_down = vec_piece(vec, layer, "b2")
    part[...] = (dot(act[...], joined(w_down, 0, HALF_FF, TENSOR)) + bias_down).astype(bf16)


def mlp_call(layer, base, own, recv, vec, weights):
    tokens = base.shape[0]
    shape = lambda width, kind: jax.ShapeDtypeStruct((tokens, width), kind)
    kept = lambda width: pltpu.HBM((tokens, width), bf16)
    outs = [shape(D, f32), kept(D), kept(HALF_FF), kept(HALF_FF), shape(D, bf16)]
    return pl.pallas_call(
        functools.partial(mlp_kernel, layer),
        out_shape=outs,
        grid=(tokens // ROWS,),
        in_specs=[rows_spec(D)] * 3
        + [
            fixed(vec.shape),
            fixed((2 * HALF_FF, HALF)),
            fixed((2 * HALF_FF, HALF)),
        ],
        out_specs=[rows_spec(o.shape[1]) for o in outs],
        compiler_params=params(),
        cost_estimate=cost(4 * tokens * D * HALF_FF, tokens * D * 24, 2 * tokens * HALF_FF),
    )(base, own, recv, vec, weights["up", layer], weights["down", layer])


def mlp_back_kernel(layer, summed, *refs):
    if summed:
        base, own, recv, *refs = refs
        (hid, slope, vec, w_up, w_down, grad_full, grad_low, du_ref, back, dgain, dshift, db1, db2) = refs
        values = base[...].astype(f32) + (own[...].astype(f32) + recv[...].astype(f32))
        grad_full[...] = values
        low = values.astype(bf16)
    else:
        base, valid, *refs = refs
        (hid, slope, vec, w_up, w_down, grad_low, du_ref, back, dgain, dshift, db1, db2) = refs
        low = (base[...].astype(f32) * valid[...]).astype(bf16)
    grad_low[...] = low
    accumulate(db2, jnp.sum(low.astype(f32), axis=0, keepdims=True))
    for part in range(HALF_FF // D):
        area = slice(part * D, (part + 1) * D)
        rows = jnp.concatenate(
            [w_down[p * HALF_FF + part * D : p * HALF_FF + (part + 1) * D, :] for p in range(TENSOR)],
            axis=1,
        )
        du_ref[:, area] = (dot_nt(low, rows) * slope[:, area].astype(f32)).astype(bf16)
    grad_normed = dot_nt(du_ref[...], joined(w_up, 0, D, HALF_FF // HALF))
    accumulate(db1, jnp.sum(du_ref[...].astype(f32), axis=0, keepdims=True))
    part_back, gain_grad, shift_grad = norm_back(hid[...], vec_piece(vec, layer, "g2"), grad_normed)
    back[...] = part_back.astype(bf16)
    accumulate(dgain, gain_grad)
    accumulate(dshift, shift_grad)


def mlp_back_call(layer, base, own, recv, valid, hid, slope, vec, weights):
    tokens = base.shape[0]
    summed = own is not None
    shape = lambda width, kind: jax.ShapeDtypeStruct((tokens, width), kind)
    line = lambda width: jax.ShapeDtypeStruct((1, width), f32)
    outs = ([shape(D, f32)] if summed else []) + [shape(D, bf16), shape(HALF_FF, bf16), shape(D, bf16)]
    lines = [line(D), line(D), line(HALF_FF), line(D)]
    extra = [own, recv] if summed else [valid]
    return pl.pallas_call(
        functools.partial(mlp_back_kernel, layer, summed),
        out_shape=outs + lines,
        grid=(tokens // ROWS,),
        in_specs=[rows_spec(D)]
        + [rows_spec(e.shape[1]) for e in extra]
        + [
            rows_spec(D),
            rows_spec(HALF_FF),
            fixed(vec.shape),
            fixed((2 * HALF_FF, HALF)),
            fixed((2 * HALF_FF, HALF)),
        ],
        out_specs=[rows_spec(o.shape[1]) for o in outs] + [fixed(o.shape) for o in lines],
        compiler_params=params(),
        cost_estimate=cost(4 * tokens * D * HALF_FF, tokens * D * 24),
    )(base, *extra, stay(hid), stay(slope), vec, weights["up", layer], weights["down", layer])


def attend_back_kernel(
    low_ref, high_ref, base, own, recv, q_ref, k_ref, v_ref, o_ref, lse_ref, seg_k, seg_q, w_out,
    full_ref, grad_low, dq_ref, dk_ref, dv_ref, dbo, dk_acc, dv_acc, dq_acc, do_ref,
):
    step = pl.program_id(0)

    @pl.when(step == 0)
    def _():
        dk_acc[...] = jnp.zeros_like(dk_acc)
        dv_acc[...] = jnp.zeros_like(dv_acc)

    values = base[...].astype(f32) + (own[...].astype(f32) + recv[...].astype(f32))
    full_ref[...] = values
    low = values.astype(bf16)
    grad_low[...] = low
    accumulate(dbo, jnp.sum(low.astype(f32), axis=0, keepdims=True))
    do_ref[...] = dot_nt(low, joined(w_out, 0, HALF, TENSOR)).astype(bf16)
    product = do_ref[...].astype(f32) * o_ref[...].astype(f32)
    head = lax.broadcasted_iota(jnp.int32, (8, HALF), 0)
    lane = lax.broadcasted_iota(jnp.int32, (8, HALF), 1)
    pick = ((lane >= head * HEAD_DIM) & (lane < (head + 1) * HEAD_DIM)).astype(f32)
    high, rest = split(product)
    pick = pick.astype(bf16)
    inner = dot_nt(pick, high) + dot_nt(pick, rest)
    dq_acc[...] = jnp.zeros_like(dq_acc)
    masks = head_masks()
    scale = jnp.asarray(HEAD_DIM ** (-0.5), bf16)
    seg_row = seg_q[...]

    def one_block(block, carried):
        rows = pl.ds(pl.multiple_of(block * KEYS, KEYS), KEYS)
        same = seg_k[rows, :] == seg_row
        for pair in range(HEADS // 2):
            cols = slice(pair * BS, (pair + 1) * BS)
            q_two = q_ref[:, cols] * scale
            do_two = do_ref[:, cols]
            k_two = k_ref[rows, cols]
            v_two = v_ref[rows, cols]
            dv_two = dk_two = dq_two = None
            for side in range(2):
                at = 2 * pair + side
                q_one = q_two * masks[side]
                do_one = do_two * masks[side]
                scores = dot_nt(k_two, q_one)
                prob = jnp.where(same, jnp.exp(scores - lse_ref[at : at + 1, :]), 0.0)
                grad_prob = dot_nt(v_two, do_one)
                grad_scores = (prob * (grad_prob - inner[at : at + 1, :])).astype(bf16)
                dv_one = dot(prob.astype(bf16), do_one)
                dk_one = dot(grad_scores, q_one)
                dq_one = dot_tn(grad_scores, k_two * masks[side])
                dq_two = dq_one if dq_two is None else dq_two + dq_one
                dv_two = dv_one if dv_two is None else dv_two + dv_one
                dk_two = dk_one if dk_two is None else dk_two + dk_one
            dv_acc[rows, cols] += dv_two
            dk_acc[rows, cols] += dk_two
            dq_acc[:, cols] += dq_two
        return carried

    lax.fori_loop(low_ref[step], high_ref[step], one_block, 0)
    dq_ref[...] = (dq_acc[...] * HEAD_DIM ** (-0.5)).astype(bf16)

    @pl.when(step == pl.num_programs(0) - 1)
    def _():
        dk_ref[...] = dk_acc[...].astype(bf16)
        dv_ref[...] = dv_acc[...].astype(bf16)


def attend_back_call(
    layer, first, last, base, own, recv, queries, keys, values, mixed, lse, seg_col, seg_row, weights
):
    tokens = base.shape[0]
    shape = lambda width, kind: jax.ShapeDtypeStruct((tokens, width), kind)
    whole = (tokens, HALF)
    return pl.pallas_call(
        attend_back_kernel,
        out_shape=[
            shape(D, f32),
            shape(D, bf16),
            shape(HALF, bf16),
            shape(HALF, bf16),
            shape(HALF, bf16),
            jax.ShapeDtypeStruct((1, D), f32),
        ],
        grid_spec=pltpu.PrefetchScalarGridSpec(
            num_scalar_prefetch=2,
            grid=(tokens // ROWS,),
            in_specs=[
                rows_spec(D),
                rows_spec(D),
                rows_spec(D),
                rows_spec(HALF),
                fixed(whole),
                fixed(whole),
                rows_spec(HALF),
                pl.BlockSpec((8, ROWS), lambda i, *_: (0, i)),
                fixed(seg_col.shape),
                pl.BlockSpec((1, ROWS), lambda i, *_: (0, i)),
                fixed((D, HALF)),
            ],
            out_specs=[
                rows_spec(D),
                rows_spec(D),
                rows_spec(HALF),
                fixed(whole),
                fixed(whole),
                fixed((1, D)),
            ],
            scratch_shapes=[
                pltpu.VMEM(whole, f32),
                pltpu.VMEM(whole, f32),
                pltpu.VMEM((ROWS, HALF), f32),
                pltpu.VMEM((ROWS, HALF), bf16),
            ],
        ),
        compiler_params=params(),
        cost_estimate=cost(14 * HEADS * tokens * tokens * BS, tokens * D * 20, HEADS * tokens * tokens),
    )(
        first, last, base, own, recv, stay(queries), stay(keys), stay(values), stay(mixed), lse,
        seg_col, seg_row, weights["out", layer],
    )


def qkv_back_kernel(layer, dq, dk, dv, hid, vec, weight, back, dgain, dshift, dbq, dbv):
    grad_three = jnp.concatenate([dq[...], dk[...], dv[...]], axis=1)
    grad_normed = dot_nt(grad_three, joined(weight, 0, D, 3))
    part_back, gain_grad, shift_grad = norm_back(hid[...], vec_piece(vec, layer, "g1"), grad_normed)
    back[...] = part_back.astype(bf16)
    accumulate(dgain, gain_grad)
    accumulate(dshift, shift_grad)
    accumulate(dbq, jnp.sum(dq[...].astype(f32), axis=0, keepdims=True))
    accumulate(dbv, jnp.sum(dv[...].astype(f32), axis=0, keepdims=True))


def qkv_back_call(layer, dq, dk, dv, hid, vec, weights):
    tokens = dq.shape[0]
    line = lambda width: jax.ShapeDtypeStruct((1, width), f32)
    lines = [line(D), line(D), line(HALF), line(HALF)]
    return pl.pallas_call(
        functools.partial(qkv_back_kernel, layer),
        out_shape=[jax.ShapeDtypeStruct((tokens, D), bf16)] + lines,
        grid=(tokens // ROWS,),
        in_specs=[rows_spec(HALF)] * 3
        + [
            rows_spec(D),
            fixed(vec.shape),
            fixed((3 * D, HALF)),
        ],
        out_specs=[rows_spec(D)] + [fixed(o.shape) for o in lines],
        compiler_params=params(),
        cost_estimate=cost(2 * tokens * D * 3 * HALF, tokens * D * 10),
    )(dq, dk, dv, stay(hid), vec, weights["qkv", layer])


def split(values):
    high = values.astype(bf16)
    return high, (values - high.astype(f32)).astype(bf16)


def product(left, right, left_dim, right_dim):
    def one(a, b):
        return lax.dot_general(
            a, b, (((left_dim,), (right_dim,)), ((), ())), preferred_element_type=f32
        )

    return one(left[0], right[0]) + (one(left[0], right[1]) + one(left[1], right[0]))


def owner_kernel(per, used, home, near, far, master, left, right, moment, variance, grad, out, out_mom, out_var):
    here = range(per)
    first = pl.program_id(0) * per
    lefts = [split(left[i]) for i in here]
    rights = [split(right[i]) for i in here]
    rotated = []
    for i in here:
        rows = slice(i * BS, (i + 1) * BS)
        tile = jnp.where(home[0] > 0, near[rows, :].astype(f32), far[rows, :].astype(f32))
        tile = jnp.where(used[first + i] > 0, tile, 0.0)
        grad[i] = tile
        tile = tile.astype(bf16)
        rotated.append(split(dot_tn(lefts[i][0], tile) + dot_tn(lefts[i][1], tile)))
    rotated = [product(rotated[i], rights[i], 1, 0) for i in here]
    steps = []
    for i in here:
        new_moment = decay * moment[i] + (1.0 - decay) * rotated[i]
        new_variance = decay * variance[i] + (1.0 - decay) * rotated[i] * rotated[i]
        out_mom[i] = new_moment
        out_var[i] = new_variance
        steps.append(split(new_moment / (jnp.sqrt(new_variance) + adam_eps)))
    returned = [split(product(lefts[i], steps[i], 1, 0)) for i in here]
    returned = [product(returned[i], rights[i], 1, 1) for i in here]
    for i in here:
        out[i] = master[i] - matrix_rate * returned[i]


def owner_call(used, home, near, far, *arrays):
    count = arrays[0].shape[0]
    per = min(8, count)
    block = pl.BlockSpec((per, BS, BS), lambda i, *_: (i, 0, 0))
    return pl.pallas_call(
        functools.partial(owner_kernel, per),
        out_shape=[jax.ShapeDtypeStruct(arrays[0].shape, f32)] * 4,
        grid_spec=pltpu.PrefetchScalarGridSpec(
            num_scalar_prefetch=2,
            grid=(count // per,),
            in_specs=[pl.BlockSpec((per * BS, BS), lambda i, *_: (i, 0))] * 2 + [block] * 5,
            out_specs=[block] * 4,
        ),
        compiler_params=params(),
        cost_estimate=cost(count * 88 * BS**3, count * BS * BS * 38),
    )(used, home, stay(near), stay(far), *arrays)


def reduce_kernel(carrying, last, *refs):
    token, block, arrived, *refs = refs
    total = block[...].astype(f32) + arrived[...].astype(f32)
    if carrying:
        carried, *refs = refs
        total = total + carried[...].astype(f32)
    if last:
        token_out, out = refs
    else:
        following, token_out, out, later = refs
        later[...] = following[...]
    out[...] = total.astype(bf16)
    token_out[...] = token[...]


def reduce_call(j, n, token, buffer, arrived, carried, payload, x_rel=0):
    last = j >= 2 or x_rel == 1
    at = lambda j, x_rel: pl.BlockSpec((payload, BS), lambda i: ((j * 2 + x_rel) * 2 + n, 0))
    whole = fixed((payload, BS))
    small = fixed(token.shape)
    operands = [token, stay(buffer), arrived] + ([] if carried is None else [carried])
    specs = [small, at(j, x_rel)] + [whole] * (len(operands) - 2)
    if not last:
        operands.append(stay(buffer))
        specs.append(at(j + 2, 1))
    block = jax.ShapeDtypeStruct((payload, BS), bf16)
    outs = [jax.ShapeDtypeStruct(token.shape, f32)] + [block] * (1 if last else 2)
    made = pl.pallas_call(
        functools.partial(reduce_kernel, carried is not None, last),
        out_shape=outs,
        grid=(1,),
        in_specs=specs,
        out_specs=[small] + [whole] * (len(outs) - 1),
        compiler_params=params(12),
        cost_estimate=cost(payload * BS * 3, payload * BS * 12),
    )(*operands)
    return (*made, None) if last else made


class Routes:
    def __init__(self, dp_n):
        pairs = [(d, t) for d in range(dp_n) for t in range(TENSOR)]
        at = lambda d, t: d * TENSOR + t
        home = [(d, t) for d, t in pairs if d % 2 == t]
        away = [(d, t) for d, t in pairs if d % 2 != t]
        self.core_all = [(at(d, t), at(d ^ 1, t)) for d, t in pairs]
        self.core_out = [(at(d, t), at(d ^ 1, t)) for d, t in home]
        self.core_in = [(at(d, t), at(d ^ 1, t)) for d, t in away]
        self.y_all = [(at(d, t), at(d, 1 - t)) for d, t in pairs]
        self.y_out = [(at(d, t), at(d, 1 - t)) for d, t in home]
        self.y_in = [(at(d, t), at(d, 1 - t)) for d, t in away]
        self.x_home = [(at(d, t), at(d ^ 2, t)) for d, t in home]
        self.x_away = [(at(d, t), at(d ^ 2, t)) for d, t in away]
        self.x_all = [(at(d, t), at(d ^ 2, t)) for d, t in pairs]
        self.z_all = [(at(d, t), at((d + 4) % dp_n, t)) for d, t in pairs]
        self.z_home = [(at(d, t), at((d + 4) % dp_n, t)) for d, t in home]


def send(value, route):
    return lax.ppermute(value, AXES, route)


def shards(
    patches,
    cotangent,
    image_size,
    block_slot,
    pinv,
    master_slots,
    left_basis,
    right_basis,
    mom_slots,
    var_slots,
    vec_master,
    vec_mom,
    vec_var,
):
    dp_n = lax.axis_size("dp")
    dp_pos = lax.axis_index("dp")
    y_pos = lax.axis_index("tensor")
    core = dp_pos % 2
    home = core == y_pos
    routes = Routes(dp_n)
    grid3 = dp_n == 16
    x_pos = (dp_pos // 2) % 2
    half_at = (x_pos if grid3 else x_pos * 0).astype(jnp.int32).reshape(1)
    tokens_n = patches.shape[0]
    slots_per = master_slots.shape[1]
    vec_per = vec_master.shape[1]
    slots_n = slots_per * dp_n
    payload = slots_per * BS + VEC_ROWS

    patches = jnp.where(home, patches, send(patches, routes.core_out))
    cotangent = jnp.where(home, cotangent, send(cotangent, routes.core_out))
    size_row = jnp.where(home, image_size, send(image_size, routes.core_out))[0]
    own_slots = block_slot[0]
    slot_other = send(block_slot, routes.y_all)

    lengths = jnp.where(
        size_row == 0, LEN_A, jnp.where(size_row == 1, LEN_B, jnp.where(size_row == 2, LEN_C, 0))
    )
    order = jnp.arange(IMG_DEV)
    ends_at = jnp.sum(jnp.where(order[None, :] <= order[:, None], lengths[None, :], 0), axis=1)
    places = jnp.arange(tokens_n)
    segment = jnp.sum((places[:, None] >= ends_at[None, :]).astype(jnp.int32), axis=1)
    in_image = segment[:, None] == order[None, :]
    select = jnp.stack(
        [jnp.any(in_image & (size_row == s)[None, :], axis=1) for s in range(3)], axis=1
    )
    valid_col = (segment < IMG_DEV).astype(f32)[:, None]
    seg_col = segment[:, None]
    seg_row = segment[None, :]
    blocks_n = tokens_n // ROWS
    starts = jnp.arange(blocks_n) * ROWS
    begun = ends_at[None, :] <= starts[:, None]
    first_tok = jnp.max(jnp.where(begun, ends_at[None, :], 0), axis=1)
    after = ends_at[None, :] > (starts + ROWS - 1)[:, None]
    last_tok = jnp.min(jnp.where(after, ends_at[None, :], tokens_n), axis=1)
    first_blk = (first_tok // ROWS).astype(jnp.int32)
    last_blk = ((last_tok + ROWS - 1) // ROWS).astype(jnp.int32)
    first_key = (first_tok // KEYS).astype(jnp.int32)
    last_key = ((last_tok + KEYS - 1) // KEYS).astype(jnp.int32)

    select_low = select.astype(bf16)
    class_col = jnp.sum(jnp.where(select, jnp.arange(1, 4)[None, :], 0), axis=1, keepdims=True) - 1
    present = jnp.any(select.reshape(blocks_n, ROWS, 3), axis=1).astype(jnp.int32)

    def expand(which, rows):
        return expand_call(which, present, half_at, rows, class_col, pinv)

    vec_low = jnp.pad(vec_master[0].astype(bf16), (0, VEC_ROWS * BS - vec_per))
    own_pack = jnp.concatenate(
        [
            master_slots[0].astype(bf16).reshape(slots_per * BS, BS),
            vec_low.reshape(VEC_ROWS, BS),
        ],
        axis=0,
    )
    flag = home.astype(jnp.int32).reshape(1)
    if grid3:
        z_pos = dp_pos // 4
        pack = own_pack
        chunks, first, second, owner = [], [], [], []
        middle_row = slots_per * BS // 2
        for j in range(4):
            beside_x, beside_y = send(pack, routes.x_all), send(pack, routes.y_all)
            further = [send(pack, routes.z_all)] if j < 3 else []
            work = [slot_other] if j == 0 else []
            beside_x, beside_y, patches, chunk, *more = fence(
                beside_x, beside_y, patches, expand(j, patches), *further, *work
            )
            chunks.append(chunk)
            if j < 3:
                further = more.pop(0)
            if j == 0:
                [slot_other] = more
            corner = jnp.concatenate(
                [send(beside_x[:middle_row], routes.y_all), send(beside_y[middle_row:], routes.x_all)],
                axis=0,
            )
            near_two = send(jnp.where(home, beside_y, pack), routes.core_all)
            far_two = send(jnp.where(home, corner, beside_x), routes.core_all)
            first += [pack, near_two, beside_x, far_two]
            second += [beside_y, near_two, corner, far_two]
            for x_rel in range(2):
                for n in range(2):
                    owner.append(((z_pos - j) % 4) * 4 + (x_pos ^ x_rel) * 2 + (core ^ n))
            if j < 3:
                pack = further
        first = [v[None] for v in first]
        second = [v[None] for v in second]
        owner = jnp.stack(owner).astype(jnp.int32)
    else:
        everything = lax.all_gather(own_pack, AXES, axis=0)
        everything = everything.reshape(dp_n, TENSOR, payload, BS)
        first = [jnp.where(core == 0, everything[:, 0], everything[:, 1])]
        second = []
        owner = jnp.arange(dp_n, dtype=jnp.int32)
        chunks = [expand(c, patches) for c in range(CHUNKS)]
    slot_list = jnp.where(home, block_slot, slot_other)[0]
    named = slot_list[None, :] == jnp.arange(slots_n)[:, None]
    used = jnp.any(named, axis=1)
    drow = jnp.where(used, jnp.sum(jnp.where(named, TARGET_ROW[None, :], 0), axis=1), -1)
    dcol = jnp.sum(jnp.where(named, TARGET_COL[None, :], 0), axis=1)
    weights, vec_rows = gather_tiles(first, second, owner, drow, dcol, flag, slots_per, dp_n)
    vec = vec_rows.reshape(dp_n, VEC_ROWS * BS)[:, :vec_per].astype(f32).reshape(1, dp_n * vec_per)

    embedded = embed_call(half_at, chunks, vec, weights)
    embedded_other = send(embedded, routes.core_all)
    core_flag = core.astype(jnp.int32).reshape(1)

    caches = []
    hidden, own, recv = None, embedded, embedded_other
    for layer in range(LAYERS):
        hidden, normed, queries, keys, values = qkv_call(
            layer, hidden, own, recv, core_flag, vec, weights
        )
        mixed, lse, part = attend_call(
            layer, first_blk, last_blk, queries, keys, values, seg_col, seg_row, vec, weights
        )
        other = send(part, routes.core_all)
        middle, normed2, act, slope, own = mlp_call(layer, hidden, part, other, vec, weights)
        recv = send(own, routes.core_all)
        caches.append((hidden, normed, queries, keys, values, mixed, lse, middle, normed2, act, slope))
        hidden = middle
    out_low = ((hidden + (own.astype(f32) + recv.astype(f32))) * valid_col).astype(bf16)

    owners = jnp.arange(dp_n)
    if grid3:
        place = (
            ((z_pos - 1 - owners // 4) % 4) * 4
            + (x_pos ^ ((owners // 2) % 2)) * 2
            + (core ^ (owners % 2))
        ).astype(jnp.int32)
    else:
        place = owners.astype(jnp.int32)
    slot_owner = slot_list // slots_per
    owner_place = jnp.sum(
        jnp.where(slot_owner[:, None] == owners[None, :], place[None, :], 0), axis=1
    )
    tile_pos = (owner_place * payload + (slot_list % slots_per) * BS).astype(jnp.int32)
    vec_pos = (place * payload + slots_per * BS).astype(jnp.int32)
    total_rows = dp_n * payload
    where_to = jnp.concatenate([half_at, flag if grid3 else flag * 0 + 1])
    offsets = {"base": 0}
    count = BASE_PIX // BS * (HALF // BS)
    for layer in range(LAYERS):
        for name, size in (("qkv", 3 * D * HALF), ("out", D * HALF), ("up", D * HALF_FF), ("down", D * HALF_FF)):
            offsets[name, layer] = count
            count += size // (BS * BS)

    def place_tiles(key, matrix, arrived, buffer):
        tiles = matrix.size // (BS * BS)
        pos = tile_pos[offsets[key] : offsets[key] + tiles]
        rows_n = matrix.shape[0] // 2 if matrix.shape[0] > HALF else HALF
        return scatter_matrix(pos, matrix, arrived, where_to, buffer, total_rows, rows_n)

    def place_base(rel, matrix, arrived, buffer):
        size = BASE_PIX * HALF // (BS * BS) // 2
        low_pos, high_pos = tile_pos[:size], tile_pos[size : 2 * size]
        pos = jnp.where(half_at[0] == rel, low_pos, high_pos)
        return scatter_matrix(pos, matrix, arrived, where_to, buffer, total_rows, D)

    def over(matrix):
        return send(matrix, routes.y_in) if grid3 else None

    def beside(matrix):
        return send(other_half(half_at, matrix), routes.x_away) if grid3 else None

    def summed(matrix, arrived):
        return half_sum(half_at, matrix, arrived) if grid3 else None

    def hold(*arrays):
        kept = [a for a in arrays if a is not None]
        done = iter(fence(*kept))
        return [None if a is None else next(done) for a in arrays]

    top, low = 1, 0
    vec_grads = [None] * LAYERS

    def mlp_step(layer, grad, own, recv):
        middle, normed2, act, slope = caches[layer][7:11]
        made = mlp_back_call(layer, grad, own, recv, valid_col, middle, slope, vec, weights)
        if own is not None:
            return made
        return [made[0]] + list(made)

    def attend_step(layer, grad, part, other, lse):
        hid_in, normed, queries, keys, values, mixed = caches[layer][:6]
        return attend_back_call(
            layer, first_key, last_key, grad, part, other, queries, keys, values, mixed, lse,
            seg_col, seg_row, weights,
        )

    grad, grad_low, du, part, dg2, ds2, db1, db2 = mlp_step(top, cotangent, None, None)
    other = send(part, routes.core_all)
    gd1 = dot_tn(caches[top][9], grad_low).astype(bf16)
    gu1 = dot_tn(caches[top][8], du).astype(bf16)
    ad1 = over(gd1)
    lse, gu1 = fence(caches[top][6], gu1)
    xu1 = beside(gu1)
    grad, grad_low, dq, dk, dv, dbo = attend_step(top, grad, part, other, lse)
    vec, dbo, ad1, xu1, out_low = hold(vec, dbo, ad1, xu1, out_low)
    au1 = over(summed(gu1, xu1))
    own, dg1, ds1, dbq, dbv = qkv_back_call(top, dq, dk, dv, caches[top][0], vec, weights)
    recv = send(own, routes.core_all)
    go1 = dot_tn(caches[top][5], grad_low).astype(bf16)
    gq1 = dot_tn(caches[top][1], jnp.concatenate([dq, dk, dv], axis=1)).astype(bf16)
    vec_grads[top] = [dg1, ds1, dbq, dbv, dbo, dg2, ds2, db1, db2]
    xq1, ao1 = beside(gq1), over(go1)
    grad, grad_low, du, part, dg2, ds2, db1, db2 = mlp_step(low, grad, own, recv)
    other = send(part, routes.core_all)
    db2, xq1, au1 = hold(db2, xq1, au1)
    aq1 = over(summed(gq1, xq1))
    gd0 = dot_tn(caches[low][9], grad_low).astype(bf16)
    gu0 = dot_tn(caches[low][8], du).astype(bf16)
    lse, gd0, gu0, ao1, aq1 = hold(caches[low][6], gd0, gu0, ao1, aq1)
    ad0 = over(gd0)
    xu0 = beside(gu0)
    buffer = place_tiles(("down", top), gd1, ad1, None)
    buffer = place_tiles(("up", top), gu1, au1, buffer)
    grad, grad_low, dq, dk, dv, dbo = attend_step(low, grad, part, other, lse)
    vec, dbo, ad0, xu0, buffer = hold(vec, dbo, ad0, xu0, buffer)
    au0 = over(summed(gu0, xu0))
    own, dg1, ds1, dbq, dbv = qkv_back_call(low, dq, dk, dv, caches[low][0], vec, weights)
    recv = send(own, routes.core_all)
    gq0 = dot_tn(caches[low][1], jnp.concatenate([dq, dk, dv], axis=1)).astype(bf16)
    vec_grads[low] = [dg1, ds1, dbq, dbv, dbo, dg2, ds2, db1, db2]
    xq0 = beside(gq0)
    turn = jnp.zeros((8, BS), f32)
    grad_emb, grad_emb_bias = embed_back_call(core_flag, turn, grad, own, recv)
    middle = CHUNKS // 2

    def base_grad(parts):
        return jnp.concatenate([dot_tn(c, grad_emb).astype(bf16) for c in parts], axis=0)

    gbt = base_grad(chunks[middle:])
    gbt, au0, xq0 = hold(gbt, au0, xq0)
    xb = send(gbt, routes.x_away) if grid3 else None
    aq0 = over(summed(gq0, xq0))
    gbm = base_grad(chunks[:middle])
    vec_grad = pack_call([grad_emb_bias] + vec_grads[0] + vec_grads[1], dp_n, vec_per)
    go0 = dot_tn(caches[low][5], grad_low).astype(bf16)
    ao0, av = over(go0), over(vec_grad)
    buffer = place_tiles(("out", top), go1, ao1, buffer)
    buffer = place_tiles(("qkv", top), gq1, aq1, buffer)
    buffer = place_tiles(("down", low), gd0, ad0, buffer)
    gbm, xb, aq0, ao0, av, buffer = hold(gbm, xb, aq0, ao0, av, buffer)
    ab = over(half_sum(half_at * 0, gbm, xb)) if grid3 else None
    buffer = place_tiles(("up", low), gu0, au0, buffer)
    buffer = place_base(1, gbt, None, buffer)
    buffer = scatter_vec(vec_pos, vec_grad, av, buffer)
    buffer = place_tiles(("qkv", low), gq0, aq0, buffer)
    buffer = place_tiles(("out", low), go0, ao0, buffer)
    base_weight = weights["base", 0]
    ab, buffer, base_weight, out_low = hold(ab, buffer, base_weight, out_low)
    weights["base", 0] = base_weight
    buffer = place_base(0, gbm, ab, buffer)

    if grid3:
        token = jnp.zeros((8, BS), f32)
        order = (1, 0)
        resized = resize_call(weights, pinv)
        carried = {n: None for n in order}
        blocks = buffer.reshape(4, 2, 2, payload, BS)
        across = {order[1]: send(blocks[0, 1, order[1]], routes.x_home), order[0]: None}
        following = {order[1]: blocks[1, 1, order[1]], order[0]: blocks[2, 1, order[0]]}
        far_side = send(blocks[0, 1, order[0]], routes.z_home)
        carried[order[0]] = send(blocks[0, 0, order[0]], routes.z_home)
        rounded = {}
        token, resized = hold(token, resized)
        for j in range(4):
            for n in order:
                if j == 0 and n == order[0]:
                    token, later, unused = reduce_call(1, n, token, buffer, far_side, None, payload, 1)
                    across[n] = send(later, routes.x_home)
                    continue
                arrived = across[n]
                if j < 3:
                    across[n] = send(following[n], routes.x_home)
                token, total, following[n] = reduce_call(
                    j, n, token, buffer, arrived, carried[n], payload
                )
                if j < 3:
                    carried[n] = send(total, routes.z_home)
                else:
                    rounded[n] = total
        near_grad, far_grad = rounded[0], send(rounded[1], routes.core_out)
    else:
        held = buffer.reshape(dp_n, 1, payload, BS).astype(f32)
        nothing = jnp.zeros_like(held)
        both = jnp.concatenate(
            [jnp.where(core == 0, held, nothing), jnp.where(core == 0, nothing, held)], axis=1
        )
        used_rows = jnp.repeat(used, BS).reshape(dp_n, 1, slots_per * BS, 1)
        used_rows = jnp.concatenate(
            [used_rows, jnp.ones((dp_n, 1, VEC_ROWS, 1), bool)], axis=2
        )
        both = jnp.where(used_rows, both, 0.0).reshape(dp_n * TENSOR * payload, BS)
        near_grad = lax.psum_scatter(both, AXES, scatter_dimension=0, tiled=True).astype(bf16)
        far_grad = near_grad
        resized = resize_call(weights, pinv)

    output = jnp.where(home, out_low, send(out_low, routes.y_out)).astype(f32)
    grad_pixels = sum(
        dot(grad_emb * select_low[:, s : s + 1], resized[s]) for s in range(3)
    ).astype(bf16)
    pixels_other = send(grad_pixels, routes.core_all)
    pixel_sides = [
        grad_pixels[:, s * HALF : (s + 1) * HALF].astype(f32)
        + pixels_other[:, s * HALF : (s + 1) * HALF].astype(f32)
        for s in range(TENSOR)
    ]
    near = jnp.where(core == 0, pixel_sides[0], pixel_sides[1])
    far = jnp.where(core == 0, pixel_sides[1], pixel_sides[0]).astype(bf16)
    patch_grad = jnp.where(home, near, send(far, routes.y_out).astype(f32))

    my_slots = dp_pos * slots_per + jnp.arange(slots_per)
    mine_used = jnp.any(own_slots[None, :] == my_slots[:, None], axis=1).astype(jnp.int32)
    owned_grad, new_master, new_mom, new_var = owner_call(
        mine_used, flag, near_grad, far_grad, master_slots[0], left_basis[0], right_basis[0], mom_slots[0], var_slots[0]
    )
    vec_rows = jnp.where(home, near_grad[slots_per * BS :], far_grad[slots_per * BS :])
    owned_vec_grad = vec_rows.astype(f32).reshape(VEC_ROWS * BS)[:vec_per]
    new_vec_mom = decay * vec_mom[0] + (1.0 - decay) * owned_vec_grad
    new_vec_var = decay * vec_var[0] + (1.0 - decay) * owned_vec_grad * owned_vec_grad
    new_vec = vec_master[0] - vector_rate * new_vec_mom / (jnp.sqrt(new_vec_var) + adam_eps)
    return (
        output,
        patch_grad,
        owned_grad[None],
        new_master[None],
        new_mom[None],
        new_var[None],
        owned_vec_grad[None],
        new_vec[None],
        new_vec_mom[None],
        new_vec_var[None],
    )


def solution(mesh):
    slots = P("tensor", "dp", None, None)
    vectors = P("tensor", "dp")
    tokens = P("dp", None)
    in_specs = (tokens, tokens, tokens, P("tensor", None), P()) + (slots,) * 5 + (vectors,) * 3
    out_specs = (tokens, P("dp", "tensor")) + (slots,) * 4 + (vectors,) * 4
    return jax.shard_map(shards, mesh=mesh, in_specs=in_specs, out_specs=out_specs, check_vma=False)
```

```python
import functools

import jax
import jax.numpy as jnp
import numpy as np
from jax import lax
from jax.experimental import pallas as pl
from jax.experimental.pallas import tpu as pltpu
from jax.sharding import PartitionSpec as P

D = 768
HEAD_DIM = 64
FF = 3072
BASE_PIX = 3072
LAYERS = 2
LEN_A = 196
LEN_B = 225
LEN_C = 576
IMG_DEV = 5
BS = 128
TENSOR = 2
HALF = D // TENSOR
HALF_FF = FF // TENSOR
HEADS = HALF // HEAD_DIM
ROWS = 256
KEYS = 512
VEC_ROWS = 16
CHUNKS = 4

AXES = ("dp", "tensor")
precise = lax.Precision.HIGHEST
masked_score = -1e30
norm_eps = 1e-06
adam_eps = 1e-08
decay = 0.5
matrix_rate = 0.05
vector_rate = 0.3
f32 = jnp.float32
bf16 = jnp.bfloat16
MIB = 1024 * 1024

WEIGHTS = [("base", 0, BASE_PIX)]
for layer in range(LAYERS):
    WEIGHTS += [("qkv", layer, 3 * D), ("out", layer, D), ("up", layer, FF), ("down", layer, FF)]
STARTS = {}
PANEL_ROWS = 0
for name, layer, size in WEIGHTS:
    STARTS[name, layer] = PANEL_ROWS
    PANEL_ROWS += size


def tile_targets():
    rows, cols = [], []

    def add(start, rows_n, cols_n):
        for i in range(rows_n // BS):
            for j in range(cols_n // BS):
                panel, inner = divmod(j * BS, HALF)
                rows.append(start + panel * rows_n + i * BS)
                cols.append(inner)

    add(STARTS["base", 0], BASE_PIX, HALF)
    for layer in range(LAYERS):
        add(STARTS["qkv", layer], D, 3 * HALF)
        add(STARTS["out", layer], HALF, D)
        add(STARTS["up", layer], D, HALF_FF)
        add(STARTS["down", layer], HALF_FF, D)
    return np.array(rows, np.int32), np.array(cols, np.int32)


TARGET_ROW, TARGET_COL = tile_targets()
LAYER_VECS = (D, D, HALF, HALF, D, D, D, HALF_FF, D)
VEC_NAMES = ("g1", "s1", "bq", "bv", "bo", "g2", "s2", "b1", "b2")


def vec_offsets():
    offset = HALF
    found = []
    for layer in range(LAYERS):
        here = {}
        for name, length in zip(VEC_NAMES, LAYER_VECS):
            here[name] = (offset, length)
            offset += length
        found.append(here)
    return found


VEC_AT = vec_offsets()


def params(limit=24):
    return pltpu.CompilerParams(
        dimension_semantics=("arbitrary",), vmem_limit_bytes=limit * MIB
    )


def cost(flops, nbytes, trans=0):
    return pl.CostEstimate(flops=flops, bytes_accessed=nbytes, transcendentals=trans)


def rows_spec(width):
    return pl.BlockSpec((ROWS, width), lambda i, *_: (i, 0))


def fixed(shape, at=0):
    return pl.BlockSpec(shape, lambda i, *_: (at,) + (0,) * (len(shape) - 1))


def vec_piece(vec_ref, layer, name):
    start, length = VEC_AT[layer][name]
    return vec_ref[:, start : start + length]


def dot(left, right):
    return jnp.dot(left, right, preferred_element_type=f32)


def dot_nt(left, right, precision=None):
    return lax.dot_general(
        left, right, (((1,), (1,)), ((), ())), precision=precision, preferred_element_type=f32
    )


def dot_tn(left, right):
    return lax.dot_general(left, right, (((0,), (0,)), ((), ())), preferred_element_type=f32)


def joined(ref, start, rows_n, panels):
    return jnp.concatenate(
        [ref[start + p * rows_n : start + (p + 1) * rows_n, :] for p in range(panels)], axis=1
    )


def norm_stats(values):
    mean_val = jnp.mean(values, axis=-1, keepdims=True)
    centered = values - mean_val
    inv_std = lax.rsqrt(jnp.mean(centered * centered, axis=-1, keepdims=True) + norm_eps)
    return centered * inv_std, inv_std


def norm_back(values, gain, grad):
    unit, inv_std = norm_stats(values)
    scaled = grad * gain
    mean_s = jnp.mean(scaled, axis=-1, keepdims=True)
    mean_u = jnp.mean(scaled * unit, axis=-1, keepdims=True)
    back = inv_std * (scaled - mean_s - unit * mean_u)
    return (
        back,
        jnp.sum(grad * unit, axis=0, keepdims=True),
        jnp.sum(grad, axis=0, keepdims=True),
    )


def accumulate(ref, value):
    first = pl.program_id(0) == 0

    @pl.when(first)
    def _():
        ref[...] = value

    @pl.when(jnp.logical_not(first))
    def _():
        ref[...] += value


def stay(value):
    return pltpu.with_memory_space_constraint(value, pltpu.HBM)


def fence(*arrays):
    def nothing(*refs):
        pass

    anywhere = pl.BlockSpec(memory_space=pl.ANY)
    return pl.pallas_call(
        nothing,
        out_shape=[jax.ShapeDtypeStruct(a.shape, a.dtype) for a in arrays],
        in_specs=[anywhere] * len(arrays),
        out_specs=[anywhere] * len(arrays),
        input_output_aliases={i: i for i in range(len(arrays))},
        compiler_params=pltpu.CompilerParams(vmem_limit_bytes=MIB),
    )(*[stay(a) if a.size > 32 * 1024 else a for a in arrays])


def gather_kernel(slots, count_a, count_b, owner, drow, dcol, flag, *refs):
    first = refs[:count_a]
    second = refs[count_a : count_a + count_b]
    *panels, vectors, held, sem, vec_sem = refs[count_a + count_b :]

    def copy_all(sources):
        at = 0
        for src in sources:
            for n in range(src.shape[0]):
                who = owner[at]
                at += 1

                def body(i, carried, src=src, n=n, who=who):
                    slot = who * slots + i
                    row = drow[slot]

                    @pl.when(row >= 0)
                    def _():
                        start = pl.multiple_of(i * BS, BS)
                        pltpu.make_async_copy(
                            src.at[n, pl.ds(start, BS), :],
                            held.at[
                                pl.ds(pl.multiple_of(row, BS), BS),
                                pl.ds(pl.multiple_of(dcol[slot], BS), BS),
                            ],
                            sem,
                        ).start()

                    return carried

                lax.fori_loop(0, slots, body, 0)
                pltpu.make_async_copy(
                    src.at[n, pl.ds(slots * BS, VEC_ROWS), :], vectors.at[who], vec_sem
                ).start()

    if count_b:

        @pl.when(flag[0] == 1)
        def _():
            copy_all(first)

        @pl.when(flag[0] == 0)
        def _():
            copy_all(second)
    else:
        copy_all(first)
    pltpu.make_async_copy(held, held, sem).wait()
    at = 0
    for panel in panels:
        size = panel.shape[0]
        pltpu.make_async_copy(held.at[pl.ds(at, size), :], panel, sem).start()
        at += size
    pltpu.make_async_copy(vectors, vectors, vec_sem).wait()
    pltpu.make_async_copy(held, held, sem).wait()


def gather_tiles(first, second, owner, drow, dcol, flag, slots, owners):
    anywhere = pl.BlockSpec(memory_space=pl.ANY)
    *panels, vectors = pl.pallas_call(
        functools.partial(gather_kernel, slots, len(first), len(second)),
        out_shape=[pltpu.HBM((size, HALF), bf16) for unused, unused2, size in WEIGHTS]
        + [jax.ShapeDtypeStruct((owners, VEC_ROWS, BS), bf16)],
        grid_spec=pltpu.PrefetchScalarGridSpec(
            num_scalar_prefetch=4,
            grid=(1,),
            in_specs=[anywhere] * (len(first) + len(second)),
            out_specs=[anywhere] * len(WEIGHTS) + [fixed((owners, VEC_ROWS, BS))],
            scratch_shapes=[
                pltpu.VMEM((PANEL_ROWS, HALF), bf16),
                pltpu.SemaphoreType.DMA,
                pltpu.SemaphoreType.DMA,
            ],
        ),
        compiler_params=params(),
        cost_estimate=cost(0, 4 * PANEL_ROWS * HALF),
    )(owner, drow, dcol, flag, *[stay(v) for v in first], *[stay(v) for v in second])
    return {(name, layer): p for (name, layer, unused), p in zip(WEIGHTS, panels)}, vectors


def scatter_kernel(rows_n, cols_n, steps, paired, parts, pos, part, own, *refs):
    @pl.when(part[1] > 0)
    def _():
        scatter_body(rows_n, cols_n, steps, paired, parts, pos, part, own, *refs)


def scatter_body(rows_n, cols_n, steps, paired, parts, pos, part, own, *refs):
    if paired:
        recv, *refs = refs
        span = pl.num_programs(0) // parts
        here = jnp.logical_or(parts == 1, pl.program_id(0) // span == part[0])
    target, buf, sems = refs[-3:]
    step = pl.program_id(0)
    slot = lax.rem(step, 2)
    per = rows_n // BS * (cols_n // BS)

    def wait(at):
        pltpu.make_async_copy(buf.at[at], buf.at[at], sems.at[at]).wait()

    @pl.when(step >= 2)
    def _():
        wait(slot)

    for i in range(rows_n // BS):
        for j in range(cols_n // BS):
            area = (slice(i * BS, (i + 1) * BS), slice(j * BS, (j + 1) * BS))
            value = own[area]
            if paired:
                more = jnp.where(here, recv[area].astype(f32), 0.0)
                value = (value.astype(f32) + more).astype(bf16)
            buf[slot, i * (cols_n // BS) + j] = value
    for n in range(per):
        pltpu.make_async_copy(
            buf.at[slot, n],
            target.at[pl.ds(pl.multiple_of(pos[step * per + n], 16), BS), :],
            sems.at[slot],
        ).start()

    @pl.when(step == pl.num_programs(0) - 1)
    def _():
        if steps > 1:
            wait(1 - slot)
        wait(slot)


def scatter_matrix(pos, own, recv, part, target, total_rows, rows_n):
    cols_n = own.shape[1]
    steps = own.shape[0] // rows_n
    anywhere = pl.BlockSpec(memory_space=pl.ANY)
    block = pl.BlockSpec((rows_n, cols_n), lambda i, *_: (i, 0))
    paired = recv is not None
    parts = own.shape[0] // recv.shape[0] if paired else 1
    span = steps // parts
    arrived = pl.BlockSpec(
        (rows_n, cols_n), lambda i, pos, part: (jnp.clip(i - part[0] * span, 0, span - 1), 0)
    )
    operands = [stay(own)] + ([stay(recv)] if paired else []) + ([] if target is None else [stay(target)])
    specs = [block] + ([block if parts == 1 else arrived] if paired else [])
    specs += [] if target is None else [anywhere]
    return pl.pallas_call(
        functools.partial(scatter_kernel, rows_n, cols_n, steps, paired, parts),
        out_shape=pltpu.HBM((total_rows, BS), bf16),
        grid_spec=pltpu.PrefetchScalarGridSpec(
            num_scalar_prefetch=2,
            grid=(steps,),
            in_specs=specs,
            out_specs=anywhere,
            scratch_shapes=[
                pltpu.VMEM((2, rows_n // BS * (cols_n // BS), BS, BS), bf16),
                pltpu.SemaphoreType.DMA((2,)),
            ],
        ),
        input_output_aliases={} if target is None else {len(operands) + 1: 0},
        compiler_params=params(12),
        cost_estimate=cost(own.size, own.size * 6),
    )(pos, part, *operands)


def half_sum_kernel(part, own, arrived, out):
    out[...] = (own[...].astype(f32) + arrived[...].astype(f32)).astype(bf16)


def half_sum(part, own, arrived):
    block = arrived.shape
    return pl.pallas_call(
        half_sum_kernel,
        out_shape=pltpu.HBM(block, bf16),
        grid_spec=pltpu.PrefetchScalarGridSpec(
            num_scalar_prefetch=1,
            grid=(1,),
            in_specs=[pl.BlockSpec(block, lambda i, part: (part[0], 0)), fixed(block)],
            out_specs=fixed(block),
        ),
        compiler_params=params(8),
        cost_estimate=cost(arrived.size, arrived.size * 6),
    )(part, stay(own), stay(arrived))


def half_copy_kernel(part, own, out):
    out[...] = own[...]


def other_half(part, own):
    block = (own.shape[0] // 2, own.shape[1])
    return pl.pallas_call(
        half_copy_kernel,
        out_shape=pltpu.HBM(block, bf16),
        grid_spec=pltpu.PrefetchScalarGridSpec(
            num_scalar_prefetch=1,
            grid=(1,),
            in_specs=[pl.BlockSpec(block, lambda i, part: (1 - part[0], 0))],
            out_specs=fixed(block),
        ),
        compiler_params=params(8),
        cost_estimate=cost(0, own.size * 2),
    )(part, stay(own))


def scatter_vec_kernel(paired, pos, own, *refs):
    if paired:
        recv, *refs = refs
    target, buf, sem = refs[-3:]
    value = own[...]
    if paired:
        value = (value.astype(f32) + recv[...].astype(f32)).astype(bf16)
    buf[...] = value

    def body(n, carried):
        pltpu.make_async_copy(
            buf.at[n], target.at[pl.ds(pl.multiple_of(pos[n], 16), VEC_ROWS), :], sem
        ).start()
        return carried

    lax.fori_loop(0, own.shape[0], body, 0)
    pltpu.make_async_copy(buf, buf, sem).wait()


def scatter_vec(pos, own, recv, target):
    anywhere = pl.BlockSpec(memory_space=pl.ANY)
    block = fixed(own.shape)
    paired = recv is not None
    operands = [own] + ([recv] if paired else []) + [stay(target)]
    return pl.pallas_call(
        functools.partial(scatter_vec_kernel, paired),
        out_shape=pltpu.HBM(target.shape, bf16),
        grid_spec=pltpu.PrefetchScalarGridSpec(
            num_scalar_prefetch=1,
            grid=(1,),
            in_specs=[block] * (len(operands) - 1) + [anywhere],
            out_specs=anywhere,
            scratch_shapes=[pltpu.VMEM(own.shape, bf16), pltpu.SemaphoreType.DMA],
        ),
        input_output_aliases={len(operands): 0},
        compiler_params=params(4),
    )(pos, *operands)


def expand_kernel(present, half, patch_ref, class_ref, pinv_ref, out, total):
    for block in range(patch_ref.shape[0] // ROWS):
        rows = slice(block * ROWS, (block + 1) * ROWS)
        total[...] = jnp.zeros_like(total)
        for which in range(3):

            @pl.when(present[block, which] > 0)
            def _(which=which, rows=rows):
                chosen = jnp.where(class_ref[rows, :] == which, patch_ref[rows, :].astype(f32), 0.0)
                total[...] += dot_nt(chosen.astype(bf16), pinv_ref[which])

        out[rows, :] = total[...].astype(bf16)


def expand_call(which, present, half, patches, class_col, pinv):
    tokens = patches.shape[0]
    size = BASE_PIX // CHUNKS
    step = size
    return pl.pallas_call(
        expand_kernel,
        out_shape=jax.ShapeDtypeStruct((tokens, size), bf16),
        grid_spec=pltpu.PrefetchScalarGridSpec(
            num_scalar_prefetch=2,
            grid=(1,),
            in_specs=[
                fixed(patches.shape),
                fixed(class_col.shape),
                pl.BlockSpec(
                    (3, step, pinv.shape[2]),
                    lambda i, present, half: (0, (which + half[0] * (CHUNKS // 2)) % CHUNKS, 0),
                ),
            ],
            out_specs=pl.BlockSpec((tokens, step), lambda i, *_: (0, i)),
            scratch_shapes=[pltpu.VMEM((ROWS, step), f32)],
        ),
        compiler_params=params(),
        cost_estimate=cost(3 * tokens * size * D, tokens * size * 4 + size * D * 6),
    )(present, half, stay(patches), class_col, stay(pinv))


def resize_kernel(base, pinv_ref, out, turned):
    @pl.when(pl.program_id(0) == 0)
    def _():
        turned[...] = base[...].T

    out[0] = dot(turned[...], pinv_ref[0]).astype(bf16)


def resize_call(weights, pinv):
    return pl.pallas_call(
        resize_kernel,
        out_shape=jax.ShapeDtypeStruct((3, HALF, pinv.shape[2]), bf16),
        grid=(3,),
        in_specs=[
            fixed((BASE_PIX, HALF)),
            pl.BlockSpec((1, BASE_PIX, pinv.shape[2]), lambda i: (i, 0, 0)),
        ],
        out_specs=pl.BlockSpec((1, HALF, pinv.shape[2]), lambda i: (i, 0, 0)),
        scratch_shapes=[pltpu.VMEM((HALF, BASE_PIX), bf16)],
        compiler_params=params(),
        cost_estimate=cost(6 * D * BASE_PIX * HALF, 6 * D * BASE_PIX),
    )(stay(weights["base", 0]), stay(pinv))


def embed_back_kernel(core, token, base, own, recv, out, bias):
    low = (base[...] + (own[...].astype(f32) + recv[...].astype(f32))).astype(bf16)
    out[...] = low
    accumulate(bias, jnp.sum(low.astype(f32), axis=0, keepdims=True))


def embed_back_call(core, token, base, own, recv):
    tokens = base.shape[0]
    half = pl.BlockSpec((ROWS, HALF), lambda i, core: (i, core[0]))
    return pl.pallas_call(
        embed_back_kernel,
        out_shape=[
            jax.ShapeDtypeStruct((tokens, HALF), bf16),
            jax.ShapeDtypeStruct((1, HALF), f32),
        ],
        grid_spec=pltpu.PrefetchScalarGridSpec(
            num_scalar_prefetch=1,
            grid=(tokens // ROWS,),
            in_specs=[fixed(token.shape)] + [half] * 3,
            out_specs=[rows_spec(HALF), fixed((1, HALF))],
        ),
        compiler_params=params(8),
        cost_estimate=cost(tokens * D, tokens * D * 5),
    )(core, token, base, own, recv)


def pack_kernel(vec_per, *refs):
    *pieces, out = refs
    out[...] = jnp.zeros_like(out)
    at = 0
    for piece in pieces:
        for k in range(piece.shape[1] // BS):
            owner, row = divmod(at, vec_per // BS)
            out[owner, row : row + 1, :] = piece[:, k * BS : (k + 1) * BS]
            at += 1


def pack_call(pieces, owners, vec_per):
    if vec_per % BS:
        joined = jnp.concatenate(pieces, axis=1)[0]
        joined = jnp.pad(joined, (0, owners * vec_per - joined.shape[0])).reshape(owners, vec_per)
        joined = jnp.pad(joined, ((0, 0), (0, VEC_ROWS * BS - vec_per)))
        return joined.astype(bf16).reshape(owners, VEC_ROWS, BS)
    return pl.pallas_call(
        functools.partial(pack_kernel, vec_per),
        out_shape=jax.ShapeDtypeStruct((owners, VEC_ROWS, BS), f32),
        grid=(1,),
        in_specs=[fixed(p.shape) for p in pieces],
        out_specs=fixed((owners, VEC_ROWS, BS)),
        compiler_params=params(4),
        cost_estimate=cost(0, owners * vec_per * 8),
    )(*pieces).astype(bf16)


def embed_kernel(half, *refs):
    *parts, vec, weight, out = refs
    size = BASE_PIX // CHUNKS
    total = vec[:, :HALF]
    for c in range(CHUNKS):
        at = lax.rem(c + half[0] * (CHUNKS // 2), CHUNKS)
        rows = pl.ds(pl.multiple_of(at * size, size), size)
        total = total + dot(parts[c][...], weight[rows, :])
    out[...] = total.astype(bf16)


def embed_call(half, chunks, vec, weights):
    tokens = chunks[0].shape[0]
    return pl.pallas_call(
        embed_kernel,
        out_shape=jax.ShapeDtypeStruct((tokens, HALF), bf16),
        grid_spec=pltpu.PrefetchScalarGridSpec(
            num_scalar_prefetch=1,
            grid=(tokens // ROWS,),
            in_specs=[rows_spec(BASE_PIX // CHUNKS)] * CHUNKS
            + [fixed(vec.shape), fixed((BASE_PIX, HALF))],
            out_specs=rows_spec(HALF),
        ),
        compiler_params=params(),
        cost_estimate=cost(2 * tokens * BASE_PIX * HALF, tokens * BASE_PIX * 3),
    )(half, *[stay(c) for c in chunks], vec, stay(weights["base", 0]))


def qkv_kernel(layer, first, core, *refs):
    if first:
        own, recv, vec, weight, hid, normed, q_ref, k_ref, v_ref = refs
        mine, theirs = own[...].astype(f32), recv[...].astype(f32)
        low = core[0] == 0
        values = jnp.concatenate(
            [jnp.where(low, mine, theirs), jnp.where(low, theirs, mine)], axis=1
        )
    else:
        base, own, recv, vec, weight, hid, normed, q_ref, k_ref, v_ref = refs
        values = base[...] + (own[...].astype(f32) + recv[...].astype(f32))
    hid[...] = values
    unit, unused = norm_stats(values)
    low = (unit * vec_piece(vec, layer, "g1") + vec_piece(vec, layer, "s1")).astype(bf16)
    normed[...] = low
    made = dot(low, joined(weight, 0, D, 3))
    q_ref[...] = (made[:, :HALF] + vec_piece(vec, layer, "bq")).astype(bf16)
    k_ref[...] = made[:, HALF : 2 * HALF].astype(bf16)
    v_ref[...] = (made[:, 2 * HALF :] + vec_piece(vec, layer, "bv")).astype(bf16)


def qkv_call(layer, base, own, recv, core, vec, weights):
    tokens = own.shape[0]
    shape = lambda width, kind: jax.ShapeDtypeStruct((tokens, width), kind)
    outs = [shape(D, f32), pltpu.HBM((tokens, D), bf16)] + [shape(HALF, bf16)] * 3
    operands = ([] if base is None else [base]) + [own, recv]
    return pl.pallas_call(
        functools.partial(qkv_kernel, layer, base is None),
        out_shape=outs,
        grid_spec=pltpu.PrefetchScalarGridSpec(
            num_scalar_prefetch=1,
            grid=(tokens // ROWS,),
            in_specs=[rows_spec(o.shape[1]) for o in operands]
            + [fixed(vec.shape), fixed((3 * D, HALF))],
            out_specs=[rows_spec(o.shape[1]) for o in outs],
        ),
        compiler_params=params(),
        cost_estimate=cost(2 * tokens * D * 3 * HALF, tokens * D * 14),
    )(core, *operands, vec, weights["qkv", layer])


def head_masks():
    lane = lax.broadcasted_iota(jnp.int32, (1, 2 * HEAD_DIM), 1)
    low = (lane < HEAD_DIM).astype(f32).astype(bf16)
    high = (lane >= HEAD_DIM).astype(f32).astype(bf16)
    return low, high


def attend_kernel(
    layer, low_ref, high_ref, q_ref, k_ref, v_ref, seg_q, seg_k, vec, w_out, o_ref, lse_ref, part,
    scores_ref, top_ref, acc_ref,
):
    step = pl.program_id(0)
    first, last = low_ref[step], high_ref[step]
    masks = head_masks()
    scale = jnp.asarray(HEAD_DIM ** (-0.5), bf16)
    lane = lax.broadcasted_iota(jnp.int32, (1, BS), 1)
    sums = [(lane == HEAD_DIM).astype(f32).astype(bf16), (lane == 0).astype(f32).astype(bf16)]
    top_ref[...] = jnp.full(top_ref.shape, masked_score, f32)
    acc_ref[...] = jnp.zeros_like(acc_ref)
    seg_col = seg_q[...]

    def score_block(block, carried):
        rows = pl.ds(pl.multiple_of(block * ROWS, ROWS), ROWS)
        same = seg_col == seg_k[:, rows]
        for pair in range(HEADS // 2):
            cols = slice(pair * BS, (pair + 1) * BS)
            q_two = q_ref[:, cols] * scale
            k_two = k_ref[rows, cols]
            for side in range(2):
                head = 2 * pair + side
                scores = jnp.where(same, dot_nt(q_two * masks[side], k_two), masked_score)
                scores_ref[head, block] = scores
                top = top_ref[head]
                for piece in range(ROWS // BS):
                    top = jnp.maximum(top, scores[:, piece * BS : (piece + 1) * BS])
                top_ref[head] = top
        return carried

    lax.fori_loop(first, last, score_block, 0)
    tops = [jnp.max(top_ref[head], axis=1, keepdims=True) for head in range(HEADS)]

    def mix_block(block, carried):
        rows = pl.ds(pl.multiple_of(block * ROWS, ROWS), ROWS)
        for pair in range(HEADS // 2):
            v_two = v_ref[rows, pair * BS : (pair + 1) * BS]
            for side in range(2):
                head = 2 * pair + side
                expo = jnp.exp(scores_ref[head, block] - tops[head]).astype(bf16)
                acc_ref[head] += dot(expo, v_two * masks[side] + sums[side])
        return carried

    lax.fori_loop(first, last, mix_block, 0)
    totals = jnp.zeros((ROWS, BS), f32)
    for pair in range(HEADS // 2):
        sides = []
        for side in range(2):
            head = 2 * pair + side
            mixed = acc_ref[head]
            at = HEAD_DIM * (1 - side)
            total = mixed[:, at : at + 1]
            totals = jnp.where(lane == head, tops[head] + jnp.log(total), totals)
            sides.append(mixed * (1.0 / total))
        o_ref[:, pair * BS : (pair + 1) * BS] = jnp.where(lane < HEAD_DIM, *sides).astype(bf16)
    lse_ref[...] = totals.T[0:8, :]
    low = o_ref[...]
    bias = vec_piece(vec, layer, "bo")
    part[...] = (dot(low, joined(w_out, 0, HALF, TENSOR)) + bias).astype(bf16)


def attend_call(layer, first, last, queries, keys, values, seg_col, seg_row, vec, weights):
    tokens = queries.shape[0]
    return pl.pallas_call(
        functools.partial(attend_kernel, layer),
        out_shape=[
            jax.ShapeDtypeStruct((tokens, HALF), bf16),
            jax.ShapeDtypeStruct((8, tokens), f32),
            jax.ShapeDtypeStruct((tokens, D), bf16),
        ],
        grid_spec=pltpu.PrefetchScalarGridSpec(
            num_scalar_prefetch=2,
            grid=(tokens // ROWS,),
            in_specs=[
                rows_spec(HALF),
                fixed(keys.shape),
                fixed(values.shape),
                rows_spec(1),
                fixed(seg_row.shape),
                fixed(vec.shape),
                fixed((D, HALF)),
            ],
            out_specs=[
                rows_spec(HALF),
                pl.BlockSpec((8, ROWS), lambda i, *_: (0, i)),
                rows_spec(D),
            ],
            scratch_shapes=[
                pltpu.VMEM((HEADS, tokens // ROWS, ROWS, ROWS), f32),
                pltpu.VMEM((HEADS, ROWS, BS), f32),
                pltpu.VMEM((HEADS, ROWS, BS), f32),
            ],
        ),
        compiler_params=params(),
        cost_estimate=cost(8 * HEADS * tokens * tokens * BS, tokens * D * 8, HEADS * tokens * tokens),
    )(first, last, queries, keys, values, seg_col, seg_row, vec, weights["out", layer])


def gelu_parts(values):
    cdf = 0.5 * (1.0 + lax.erf(values * 0.7071067811865476))
    pdf = 0.3989422804014327 * jnp.exp(-0.5 * values * values)
    return values * cdf, cdf + values * pdf


def mlp_kernel(layer, base, own, recv, vec, w_up, w_down, hid, normed, act, slope, part):
    values = base[...] + (own[...].astype(f32) + recv[...].astype(f32))
    hid[...] = values
    unit, unused = norm_stats(values)
    low = (unit * vec_piece(vec, layer, "g2") + vec_piece(vec, layer, "s2")).astype(bf16)
    normed[...] = low
    bias_up = vec_piece(vec, layer, "b1")
    for pair in range(HALF_FF // D):
        area = slice(pair * D, (pair + 1) * D)
        up = dot(low, joined(w_up, pair * 2 * D, D, 2)) + bias_up[:, area]
        gelu, grad = gelu_parts(up)
        act[:, area] = gelu.astype(bf16)
        slope[:, area] = grad.astype(bf16)
    bias_down = vec_piece(vec, layer, "b2")
    part[...] = (dot(act[...], joined(w_down, 0, HALF_FF, TENSOR)) + bias_down).astype(bf16)


def mlp_call(layer, base, own, recv, vec, weights):
    tokens = base.shape[0]
    shape = lambda width, kind: jax.ShapeDtypeStruct((tokens, width), kind)
    kept = lambda width: pltpu.HBM((tokens, width), bf16)
    outs = [shape(D, f32), kept(D), kept(HALF_FF), kept(HALF_FF), shape(D, bf16)]
    return pl.pallas_call(
        functools.partial(mlp_kernel, layer),
        out_shape=outs,
        grid=(tokens // ROWS,),
        in_specs=[rows_spec(D)] * 3
        + [
            fixed(vec.shape),
            fixed((2 * HALF_FF, HALF)),
            fixed((2 * HALF_FF, HALF)),
        ],
        out_specs=[rows_spec(o.shape[1]) for o in outs],
        compiler_params=params(),
        cost_estimate=cost(4 * tokens * D * HALF_FF, tokens * D * 24, 2 * tokens * HALF_FF),
    )(base, own, recv, vec, weights["up", layer], weights["down", layer])


def mlp_back_kernel(layer, summed, *refs):
    if summed:
        base, own, recv, *refs = refs
        (hid, slope, vec, w_up, w_down, grad_full, grad_low, du_ref, back, dgain, dshift, db1, db2) = refs
        values = base[...].astype(f32) + (own[...].astype(f32) + recv[...].astype(f32))
        grad_full[...] = values
        low = values.astype(bf16)
    else:
        base, valid, *refs = refs
        (hid, slope, vec, w_up, w_down, grad_low, du_ref, back, dgain, dshift, db1, db2) = refs
        low = (base[...].astype(f32) * valid[...]).astype(bf16)
    grad_low[...] = low
    accumulate(db2, jnp.sum(low.astype(f32), axis=0, keepdims=True))
    for part in range(HALF_FF // D):
        area = slice(part * D, (part + 1) * D)
        rows = jnp.concatenate(
            [w_down[p * HALF_FF + part * D : p * HALF_FF + (part + 1) * D, :] for p in range(TENSOR)],
            axis=1,
        )
        du_ref[:, area] = (dot_nt(low, rows) * slope[:, area].astype(f32)).astype(bf16)
    grad_normed = dot_nt(du_ref[...], joined(w_up, 0, D, HALF_FF // HALF))
    accumulate(db1, jnp.sum(du_ref[...].astype(f32), axis=0, keepdims=True))
    part_back, gain_grad, shift_grad = norm_back(hid[...], vec_piece(vec, layer, "g2"), grad_normed)
    back[...] = part_back.astype(bf16)
    accumulate(dgain, gain_grad)
    accumulate(dshift, shift_grad)


def mlp_back_call(layer, base, own, recv, valid, hid, slope, vec, weights):
    tokens = base.shape[0]
    summed = own is not None
    shape = lambda width, kind: jax.ShapeDtypeStruct((tokens, width), kind)
    line = lambda width: jax.ShapeDtypeStruct((1, width), f32)
    outs = ([shape(D, f32)] if summed else []) + [shape(D, bf16), shape(HALF_FF, bf16), shape(D, bf16)]
    lines = [line(D), line(D), line(HALF_FF), line(D)]
    extra = [own, recv] if summed else [valid]
    return pl.pallas_call(
        functools.partial(mlp_back_kernel, layer, summed),
        out_shape=outs + lines,
        grid=(tokens // ROWS,),
        in_specs=[rows_spec(D)]
        + [rows_spec(e.shape[1]) for e in extra]
        + [
            rows_spec(D),
            rows_spec(HALF_FF),
            fixed(vec.shape),
            fixed((2 * HALF_FF, HALF)),
            fixed((2 * HALF_FF, HALF)),
        ],
        out_specs=[rows_spec(o.shape[1]) for o in outs] + [fixed(o.shape) for o in lines],
        compiler_params=params(),
        cost_estimate=cost(4 * tokens * D * HALF_FF, tokens * D * 24),
    )(base, *extra, stay(hid), stay(slope), vec, weights["up", layer], weights["down", layer])


def attend_back_kernel(
    low_ref, high_ref, base, own, recv, q_ref, k_ref, v_ref, o_ref, lse_ref, seg_k, seg_q, w_out,
    full_ref, grad_low, dq_ref, dk_ref, dv_ref, dbo, dk_acc, dv_acc, dq_acc, do_ref,
):
    step = pl.program_id(0)

    @pl.when(step == 0)
    def _():
        dk_acc[...] = jnp.zeros_like(dk_acc)
        dv_acc[...] = jnp.zeros_like(dv_acc)

    values = base[...].astype(f32) + (own[...].astype(f32) + recv[...].astype(f32))
    full_ref[...] = values
    low = values.astype(bf16)
    grad_low[...] = low
    accumulate(dbo, jnp.sum(low.astype(f32), axis=0, keepdims=True))
    do_ref[...] = dot_nt(low, joined(w_out, 0, HALF, TENSOR)).astype(bf16)
    product = do_ref[...].astype(f32) * o_ref[...].astype(f32)
    head = lax.broadcasted_iota(jnp.int32, (8, HALF), 0)
    lane = lax.broadcasted_iota(jnp.int32, (8, HALF), 1)
    pick = ((lane >= head * HEAD_DIM) & (lane < (head + 1) * HEAD_DIM)).astype(f32)
    high, rest = split(product)
    pick = pick.astype(bf16)
    inner = dot_nt(pick, high) + dot_nt(pick, rest)
    dq_acc[...] = jnp.zeros_like(dq_acc)
    masks = head_masks()
    scale = jnp.asarray(HEAD_DIM ** (-0.5), bf16)
    seg_row = seg_q[...]

    def one_block(block, carried):
        rows = pl.ds(pl.multiple_of(block * KEYS, KEYS), KEYS)
        same = seg_k[rows, :] == seg_row
        for pair in range(HEADS // 2):
            cols = slice(pair * BS, (pair + 1) * BS)
            q_two = q_ref[:, cols] * scale
            do_two = do_ref[:, cols]
            k_two = k_ref[rows, cols]
            v_two = v_ref[rows, cols]
            dv_two = dk_two = dq_two = None
            for side in range(2):
                at = 2 * pair + side
                q_one = q_two * masks[side]
                do_one = do_two * masks[side]
                scores = dot_nt(k_two, q_one)
                prob = jnp.where(same, jnp.exp(scores - lse_ref[at : at + 1, :]), 0.0)
                grad_prob = dot_nt(v_two, do_one)
                grad_scores = (prob * (grad_prob - inner[at : at + 1, :])).astype(bf16)
                dv_one = dot(prob.astype(bf16), do_one)
                dk_one = dot(grad_scores, q_one)
                dq_one = dot_tn(grad_scores, k_two * masks[side])
                dq_two = dq_one if dq_two is None else dq_two + dq_one
                dv_two = dv_one if dv_two is None else dv_two + dv_one
                dk_two = dk_one if dk_two is None else dk_two + dk_one
            dv_acc[rows, cols] += dv_two
            dk_acc[rows, cols] += dk_two
            dq_acc[:, cols] += dq_two
        return carried

    lax.fori_loop(low_ref[step], high_ref[step], one_block, 0)
    dq_ref[...] = (dq_acc[...] * HEAD_DIM ** (-0.5)).astype(bf16)

    @pl.when(step == pl.num_programs(0) - 1)
    def _():
        dk_ref[...] = dk_acc[...].astype(bf16)
        dv_ref[...] = dv_acc[...].astype(bf16)


def attend_back_call(
    layer, first, last, base, own, recv, queries, keys, values, mixed, lse, seg_col, seg_row, weights
):
    tokens = base.shape[0]
    shape = lambda width, kind: jax.ShapeDtypeStruct((tokens, width), kind)
    whole = (tokens, HALF)
    return pl.pallas_call(
        attend_back_kernel,
        out_shape=[
            shape(D, f32),
            shape(D, bf16),
            shape(HALF, bf16),
            shape(HALF, bf16),
            shape(HALF, bf16),
            jax.ShapeDtypeStruct((1, D), f32),
        ],
        grid_spec=pltpu.PrefetchScalarGridSpec(
            num_scalar_prefetch=2,
            grid=(tokens // ROWS,),
            in_specs=[
                rows_spec(D),
                rows_spec(D),
                rows_spec(D),
                rows_spec(HALF),
                fixed(whole),
                fixed(whole),
                rows_spec(HALF),
                pl.BlockSpec((8, ROWS), lambda i, *_: (0, i)),
                fixed(seg_col.shape),
                pl.BlockSpec((1, ROWS), lambda i, *_: (0, i)),
                fixed((D, HALF)),
            ],
            out_specs=[
                rows_spec(D),
                rows_spec(D),
                rows_spec(HALF),
                fixed(whole),
                fixed(whole),
                fixed((1, D)),
            ],
            scratch_shapes=[
                pltpu.VMEM(whole, f32),
                pltpu.VMEM(whole, f32),
                pltpu.VMEM((ROWS, HALF), f32),
                pltpu.VMEM((ROWS, HALF), bf16),
            ],
        ),
        compiler_params=params(),
        cost_estimate=cost(14 * HEADS * tokens * tokens * BS, tokens * D * 20, HEADS * tokens * tokens),
    )(
        first, last, base, own, recv, stay(queries), stay(keys), stay(values), stay(mixed), lse,
        seg_col, seg_row, weights["out", layer],
    )


def qkv_back_kernel(layer, dq, dk, dv, hid, vec, weight, back, dgain, dshift, dbq, dbv):
    grad_three = jnp.concatenate([dq[...], dk[...], dv[...]], axis=1)
    grad_normed = dot_nt(grad_three, joined(weight, 0, D, 3))
    part_back, gain_grad, shift_grad = norm_back(hid[...], vec_piece(vec, layer, "g1"), grad_normed)
    back[...] = part_back.astype(bf16)
    accumulate(dgain, gain_grad)
    accumulate(dshift, shift_grad)
    accumulate(dbq, jnp.sum(dq[...].astype(f32), axis=0, keepdims=True))
    accumulate(dbv, jnp.sum(dv[...].astype(f32), axis=0, keepdims=True))


def qkv_back_call(layer, dq, dk, dv, hid, vec, weights):
    tokens = dq.shape[0]
    line = lambda width: jax.ShapeDtypeStruct((1, width), f32)
    lines = [line(D), line(D), line(HALF), line(HALF)]
    return pl.pallas_call(
        functools.partial(qkv_back_kernel, layer),
        out_shape=[jax.ShapeDtypeStruct((tokens, D), bf16)] + lines,
        grid=(tokens // ROWS,),
        in_specs=[rows_spec(HALF)] * 3
        + [
            rows_spec(D),
            fixed(vec.shape),
            fixed((3 * D, HALF)),
        ],
        out_specs=[rows_spec(D)] + [fixed(o.shape) for o in lines],
        compiler_params=params(),
        cost_estimate=cost(2 * tokens * D * 3 * HALF, tokens * D * 10),
    )(dq, dk, dv, stay(hid), vec, weights["qkv", layer])


def split(values):
    high = values.astype(bf16)
    return high, (values - high.astype(f32)).astype(bf16)


def product(left, right, left_dim, right_dim):
    def one(a, b):
        return lax.dot_general(
            a, b, (((left_dim,), (right_dim,)), ((), ())), preferred_element_type=f32
        )

    return one(left[0], right[0]) + (one(left[0], right[1]) + one(left[1], right[0]))


def owner_kernel(per, used, home, near, far, master, left, right, moment, variance, grad, out, out_mom, out_var):
    here = range(per)
    first = pl.program_id(0) * per
    lefts = [split(left[i]) for i in here]
    rights = [split(right[i]) for i in here]
    rotated = []
    for i in here:
        rows = slice(i * BS, (i + 1) * BS)
        tile = jnp.where(home[0] > 0, near[rows, :].astype(f32), far[rows, :].astype(f32))
        tile = jnp.where(used[first + i] > 0, tile, 0.0)
        grad[i] = tile
        tile = tile.astype(bf16)
        rotated.append(split(dot_tn(lefts[i][0], tile) + dot_tn(lefts[i][1], tile)))
    rotated = [product(rotated[i], rights[i], 1, 0) for i in here]
    steps = []
    for i in here:
        new_moment = decay * moment[i] + (1.0 - decay) * rotated[i]
        new_variance = decay * variance[i] + (1.0 - decay) * rotated[i] * rotated[i]
        out_mom[i] = new_moment
        out_var[i] = new_variance
        steps.append(split(new_moment / (jnp.sqrt(new_variance) + adam_eps)))
    returned = [split(product(lefts[i], steps[i], 1, 0)) for i in here]
    returned = [product(returned[i], rights[i], 1, 1) for i in here]
    for i in here:
        out[i] = master[i] - matrix_rate * returned[i]


def owner_call(used, home, near, far, *arrays):
    count = arrays[0].shape[0]
    per = min(8, count)
    block = pl.BlockSpec((per, BS, BS), lambda i, *_: (i, 0, 0))
    return pl.pallas_call(
        functools.partial(owner_kernel, per),
        out_shape=[jax.ShapeDtypeStruct(arrays[0].shape, f32)] * 4,
        grid_spec=pltpu.PrefetchScalarGridSpec(
            num_scalar_prefetch=2,
            grid=(count // per,),
            in_specs=[pl.BlockSpec((per * BS, BS), lambda i, *_: (i, 0))] * 2 + [block] * 5,
            out_specs=[block] * 4,
        ),
        compiler_params=params(),
        cost_estimate=cost(count * 88 * BS**3, count * BS * BS * 38),
    )(used, home, stay(near), stay(far), *arrays)


def reduce_kernel(carrying, last, *refs):
    token, block, arrived, *refs = refs
    total = block[...].astype(f32) + arrived[...].astype(f32)
    if carrying:
        carried, *refs = refs
        total = total + carried[...].astype(f32)
    if last:
        token_out, out = refs
    else:
        following, token_out, out, later = refs
        later[...] = following[...]
    out[...] = total.astype(bf16)
    token_out[...] = token[...]


def reduce_call(j, n, token, buffer, arrived, carried, payload, x_rel=0):
    last = j >= 2 or x_rel == 1
    at = lambda j, x_rel: pl.BlockSpec((payload, BS), lambda i: ((j * 2 + x_rel) * 2 + n, 0))
    whole = fixed((payload, BS))
    small = fixed(token.shape)
    operands = [token, stay(buffer), arrived] + ([] if carried is None else [carried])
    specs = [small, at(j, x_rel)] + [whole] * (len(operands) - 2)
    if not last:
        operands.append(stay(buffer))
        specs.append(at(j + 2, 1))
    block = jax.ShapeDtypeStruct((payload, BS), bf16)
    outs = [jax.ShapeDtypeStruct(token.shape, f32)] + [block] * (1 if last else 2)
    made = pl.pallas_call(
        functools.partial(reduce_kernel, carried is not None, last),
        out_shape=outs,
        grid=(1,),
        in_specs=specs,
        out_specs=[small] + [whole] * (len(outs) - 1),
        compiler_params=params(12),
        cost_estimate=cost(payload * BS * 3, payload * BS * 12),
    )(*operands)
    return (*made, None) if last else made


class Routes:
    def __init__(self, dp_n):
        pairs = [(d, t) for d in range(dp_n) for t in range(TENSOR)]
        at = lambda d, t: d * TENSOR + t
        home = [(d, t) for d, t in pairs if d % 2 == t]
        away = [(d, t) for d, t in pairs if d % 2 != t]
        self.core_all = [(at(d, t), at(d ^ 1, t)) for d, t in pairs]
        self.core_out = [(at(d, t), at(d ^ 1, t)) for d, t in home]
        self.core_in = [(at(d, t), at(d ^ 1, t)) for d, t in away]
        self.y_all = [(at(d, t), at(d, 1 - t)) for d, t in pairs]
        self.y_out = [(at(d, t), at(d, 1 - t)) for d, t in home]
        self.y_in = [(at(d, t), at(d, 1 - t)) for d, t in away]
        self.x_home = [(at(d, t), at(d ^ 2, t)) for d, t in home]
        self.x_away = [(at(d, t), at(d ^ 2, t)) for d, t in away]
        self.x_all = [(at(d, t), at(d ^ 2, t)) for d, t in pairs]
        self.z_all = [(at(d, t), at((d + 4) % dp_n, t)) for d, t in pairs]
        self.z_home = [(at(d, t), at((d + 4) % dp_n, t)) for d, t in home]


def send(value, route):
    return lax.ppermute(value, AXES, route)


def shards(
    patches,
    cotangent,
    image_size,
    block_slot,
    pinv,
    master_slots,
    left_basis,
    right_basis,
    mom_slots,
    var_slots,
    vec_master,
    vec_mom,
    vec_var,
):
    dp_n = lax.axis_size("dp")
    dp_pos = lax.axis_index("dp")
    y_pos = lax.axis_index("tensor")
    core = dp_pos % 2
    home = core == y_pos
    routes = Routes(dp_n)
    grid3 = dp_n == 16
    x_pos = (dp_pos // 2) % 2
    half_at = (x_pos if grid3 else x_pos * 0).astype(jnp.int32).reshape(1)
    tokens_n = patches.shape[0]
    slots_per = master_slots.shape[1]
    vec_per = vec_master.shape[1]
    slots_n = slots_per * dp_n
    payload = slots_per * BS + VEC_ROWS

    patches = jnp.where(home, patches, send(patches, routes.core_out))
    cotangent = jnp.where(home, cotangent, send(cotangent, routes.core_out))
    size_row = jnp.where(home, image_size, send(image_size, routes.core_out))[0]
    own_slots = block_slot[0]
    slot_other = send(block_slot, routes.y_all)

    lengths = jnp.where(
        size_row == 0, LEN_A, jnp.where(size_row == 1, LEN_B, jnp.where(size_row == 2, LEN_C, 0))
    )
    order = jnp.arange(IMG_DEV)
    ends_at = jnp.sum(jnp.where(order[None, :] <= order[:, None], lengths[None, :], 0), axis=1)
    places = jnp.arange(tokens_n)
    segment = jnp.sum((places[:, None] >= ends_at[None, :]).astype(jnp.int32), axis=1)
    in_image = segment[:, None] == order[None, :]
    select = jnp.stack(
        [jnp.any(in_image & (size_row == s)[None, :], axis=1) for s in range(3)], axis=1
    )
    valid_col = (segment < IMG_DEV).astype(f32)[:, None]
    seg_col = segment[:, None]
    seg_row = segment[None, :]
    blocks_n = tokens_n // ROWS
    starts = jnp.arange(blocks_n) * ROWS
    begun = ends_at[None, :] <= starts[:, None]
    first_tok = jnp.max(jnp.where(begun, ends_at[None, :], 0), axis=1)
    after = ends_at[None, :] > (starts + ROWS - 1)[:, None]
    last_tok = jnp.min(jnp.where(after, ends_at[None, :], tokens_n), axis=1)
    first_blk = (first_tok // ROWS).astype(jnp.int32)
    last_blk = ((last_tok + ROWS - 1) // ROWS).astype(jnp.int32)
    first_key = (first_tok // KEYS).astype(jnp.int32)
    last_key = ((last_tok + KEYS - 1) // KEYS).astype(jnp.int32)

    select_low = select.astype(bf16)
    class_col = jnp.sum(jnp.where(select, jnp.arange(1, 4)[None, :], 0), axis=1, keepdims=True) - 1
    present = jnp.any(select.reshape(blocks_n, ROWS, 3), axis=1).astype(jnp.int32)

    def expand(which, rows):
        return expand_call(which, present, half_at, rows, class_col, pinv)

    vec_low = jnp.pad(vec_master[0].astype(bf16), (0, VEC_ROWS * BS - vec_per))
    own_pack = jnp.concatenate(
        [
            master_slots[0].astype(bf16).reshape(slots_per * BS, BS),
            vec_low.reshape(VEC_ROWS, BS),
        ],
        axis=0,
    )
    flag = home.astype(jnp.int32).reshape(1)
    if grid3:
        z_pos = dp_pos // 4
        pack = own_pack
        chunks, first, second, owner = [], [], [], []
        middle_row = slots_per * BS // 2
        for j in range(4):
            beside_x, beside_y = send(pack, routes.x_all), send(pack, routes.y_all)
            further = [send(pack, routes.z_all)] if j < 3 else []
            work = [slot_other] if j == 0 else []
            beside_x, beside_y, patches, chunk, *more = fence(
                beside_x, beside_y, patches, expand(j, patches), *further, *work
            )
            chunks.append(chunk)
            if j < 3:
                further = more.pop(0)
            if j == 0:
                [slot_other] = more
            corner = jnp.concatenate(
                [send(beside_x[:middle_row], routes.y_all), send(beside_y[middle_row:], routes.x_all)],
                axis=0,
            )
            near_two = send(jnp.where(home, beside_y, pack), routes.core_all)
            far_two = send(jnp.where(home, corner, beside_x), routes.core_all)
            first += [pack, near_two, beside_x, far_two]
            second += [beside_y, near_two, corner, far_two]
            for x_rel in range(2):
                for n in range(2):
                    owner.append(((z_pos - j) % 4) * 4 + (x_pos ^ x_rel) * 2 + (core ^ n))
            if j < 3:
                pack = further
        first = [v[None] for v in first]
        second = [v[None] for v in second]
        owner = jnp.stack(owner).astype(jnp.int32)
    else:
        everything = lax.all_gather(own_pack, AXES, axis=0)
        everything = everything.reshape(dp_n, TENSOR, payload, BS)
        first = [jnp.where(core == 0, everything[:, 0], everything[:, 1])]
        second = []
        owner = jnp.arange(dp_n, dtype=jnp.int32)
        chunks = [expand(c, patches) for c in range(CHUNKS)]
    slot_list = jnp.where(home, block_slot, slot_other)[0]
    named = slot_list[None, :] == jnp.arange(slots_n)[:, None]
    used = jnp.any(named, axis=1)
    drow = jnp.where(used, jnp.sum(jnp.where(named, TARGET_ROW[None, :], 0), axis=1), -1)
    dcol = jnp.sum(jnp.where(named, TARGET_COL[None, :], 0), axis=1)
    weights, vec_rows = gather_tiles(first, second, owner, drow, dcol, flag, slots_per, dp_n)
    vec = vec_rows.reshape(dp_n, VEC_ROWS * BS)[:, :vec_per].astype(f32).reshape(1, dp_n * vec_per)

    embedded = embed_call(half_at, chunks, vec, weights)
    embedded_other = send(embedded, routes.core_all)
    core_flag = core.astype(jnp.int32).reshape(1)

    caches = []
    hidden, own, recv = None, embedded, embedded_other
    for layer in range(LAYERS):
        hidden, normed, queries, keys, values = qkv_call(
            layer, hidden, own, recv, core_flag, vec, weights
        )
        mixed, lse, part = attend_call(
            layer, first_blk, last_blk, queries, keys, values, seg_col, seg_row, vec, weights
        )
        other = send(part, routes.core_all)
        middle, normed2, act, slope, own = mlp_call(layer, hidden, part, other, vec, weights)
        recv = send(own, routes.core_all)
        caches.append((hidden, normed, queries, keys, values, mixed, lse, middle, normed2, act, slope))
        hidden = middle
    out_low = ((hidden + (own.astype(f32) + recv.astype(f32))) * valid_col).astype(bf16)

    owners = jnp.arange(dp_n)
    if grid3:
        place = (
            ((z_pos - 1 - owners // 4) % 4) * 4
            + (x_pos ^ ((owners // 2) % 2)) * 2
            + (core ^ (owners % 2))
        ).astype(jnp.int32)
    else:
        place = owners.astype(jnp.int32)
    slot_owner = slot_list // slots_per
    owner_place = jnp.sum(
        jnp.where(slot_owner[:, None] == owners[None, :], place[None, :], 0), axis=1
    )
    tile_pos = (owner_place * payload + (slot_list % slots_per) * BS).astype(jnp.int32)
    vec_pos = (place * payload + slots_per * BS).astype(jnp.int32)
    total_rows = dp_n * payload
    where_to = jnp.concatenate([half_at, flag if grid3 else flag * 0 + 1])
    offsets = {"base": 0}
    count = BASE_PIX // BS * (HALF // BS)
    for layer in range(LAYERS):
        for name, size in (("qkv", 3 * D * HALF), ("out", D * HALF), ("up", D * HALF_FF), ("down", D * HALF_FF)):
            offsets[name, layer] = count
            count += size // (BS * BS)

    def place_tiles(key, matrix, arrived, buffer):
        tiles = matrix.size // (BS * BS)
        pos = tile_pos[offsets[key] : offsets[key] + tiles]
        rows_n = matrix.shape[0] // 2 if matrix.shape[0] > HALF else HALF
        return scatter_matrix(pos, matrix, arrived, where_to, buffer, total_rows, rows_n)

    def place_base(rel, matrix, arrived, buffer):
        size = BASE_PIX * HALF // (BS * BS) // 2
        low_pos, high_pos = tile_pos[:size], tile_pos[size : 2 * size]
        pos = jnp.where(half_at[0] == rel, low_pos, high_pos)
        return scatter_matrix(pos, matrix, arrived, where_to, buffer, total_rows, D)

    def over(matrix):
        return send(matrix, routes.y_in) if grid3 else None

    def beside(matrix):
        return send(other_half(half_at, matrix), routes.x_away) if grid3 else None

    def summed(matrix, arrived):
        return half_sum(half_at, matrix, arrived) if grid3 else None

    def hold(*arrays):
        kept = [a for a in arrays if a is not None]
        done = iter(fence(*kept))
        return [None if a is None else next(done) for a in arrays]

    top, low = 1, 0
    vec_grads = [None] * LAYERS

    def mlp_step(layer, grad, own, recv):
        middle, normed2, act, slope = caches[layer][7:11]
        made = mlp_back_call(layer, grad, own, recv, valid_col, middle, slope, vec, weights)
        if own is not None:
            return made
        return [made[0]] + list(made)

    def attend_step(layer, grad, part, other, lse):
        hid_in, normed, queries, keys, values, mixed = caches[layer][:6]
        return attend_back_call(
            layer, first_key, last_key, grad, part, other, queries, keys, values, mixed, lse,
            seg_col, seg_row, weights,
        )

    grad, grad_low, du, part, dg2, ds2, db1, db2 = mlp_step(top, cotangent, None, None)
    other = send(part, routes.core_all)
    gd1 = dot_tn(caches[top][9], grad_low).astype(bf16)
    gu1 = dot_tn(caches[top][8], du).astype(bf16)
    ad1 = over(gd1)
    lse, gu1 = fence(caches[top][6], gu1)
    xu1 = beside(gu1)
    grad, grad_low, dq, dk, dv, dbo = attend_step(top, grad, part, other, lse)
    vec, dbo, ad1, xu1, out_low = hold(vec, dbo, ad1, xu1, out_low)
    au1 = over(summed(gu1, xu1))
    own, dg1, ds1, dbq, dbv = qkv_back_call(top, dq, dk, dv, caches[top][0], vec, weights)
    recv = send(own, routes.core_all)
    go1 = dot_tn(caches[top][5], grad_low).astype(bf16)
    gq1 = dot_tn(caches[top][1], jnp.concatenate([dq, dk, dv], axis=1)).astype(bf16)
    vec_grads[top] = [dg1, ds1, dbq, dbv, dbo, dg2, ds2, db1, db2]
    xq1, ao1 = beside(gq1), over(go1)
    grad, grad_low, du, part, dg2, ds2, db1, db2 = mlp_step(low, grad, own, recv)
    other = send(part, routes.core_all)
    db2, xq1, au1 = hold(db2, xq1, au1)
    aq1 = over(summed(gq1, xq1))
    gd0 = dot_tn(caches[low][9], grad_low).astype(bf16)
    gu0 = dot_tn(caches[low][8], du).astype(bf16)
    lse, gd0, gu0, ao1, aq1 = hold(caches[low][6], gd0, gu0, ao1, aq1)
    ad0 = over(gd0)
    xu0 = beside(gu0)
    buffer = place_tiles(("down", top), gd1, ad1, None)
    buffer = place_tiles(("up", top), gu1, au1, buffer)
    grad, grad_low, dq, dk, dv, dbo = attend_step(low, grad, part, other, lse)
    vec, dbo, ad0, xu0, buffer = hold(vec, dbo, ad0, xu0, buffer)
    au0 = over(summed(gu0, xu0))
    own, dg1, ds1, dbq, dbv = qkv_back_call(low, dq, dk, dv, caches[low][0], vec, weights)
    recv = send(own, routes.core_all)
    gq0 = dot_tn(caches[low][1], jnp.concatenate([dq, dk, dv], axis=1)).astype(bf16)
    vec_grads[low] = [dg1, ds1, dbq, dbv, dbo, dg2, ds2, db1, db2]
    xq0 = beside(gq0)
    turn = jnp.zeros((8, BS), f32)
    grad_emb, grad_emb_bias = embed_back_call(core_flag, turn, grad, own, recv)
    middle = CHUNKS // 2

    def base_grad(parts):
        return jnp.concatenate([dot_tn(c, grad_emb).astype(bf16) for c in parts], axis=0)

    gbt = base_grad(chunks[middle:])
    gbt, au0, xq0 = hold(gbt, au0, xq0)
    xb = send(gbt, routes.x_away) if grid3 else None
    aq0 = over(summed(gq0, xq0))
    gbm = base_grad(chunks[:middle])
    vec_grad = pack_call([grad_emb_bias] + vec_grads[0] + vec_grads[1], dp_n, vec_per)
    go0 = dot_tn(caches[low][5], grad_low).astype(bf16)
    ao0, av = over(go0), over(vec_grad)
    buffer = place_tiles(("out", top), go1, ao1, buffer)
    buffer = place_tiles(("qkv", top), gq1, aq1, buffer)
    buffer = place_tiles(("down", low), gd0, ad0, buffer)
    gbm, xb, aq0, ao0, av, buffer = hold(gbm, xb, aq0, ao0, av, buffer)
    ab = over(half_sum(half_at * 0, gbm, xb)) if grid3 else None
    buffer = place_tiles(("up", low), gu0, au0, buffer)
    buffer = place_base(1, gbt, None, buffer)
    buffer = scatter_vec(vec_pos, vec_grad, av, buffer)
    buffer = place_tiles(("qkv", low), gq0, aq0, buffer)
    buffer = place_tiles(("out", low), go0, ao0, buffer)
    base_weight = weights["base", 0]
    ab, buffer, base_weight, out_low = hold(ab, buffer, base_weight, out_low)
    weights["base", 0] = base_weight
    buffer = place_base(0, gbm, ab, buffer)

    if grid3:
        token = jnp.zeros((8, BS), f32)
        order = (1, 0)
        resized = resize_call(weights, pinv)
        carried = {n: None for n in order}
        blocks = buffer.reshape(4, 2, 2, payload, BS)
        across = {order[1]: send(blocks[0, 1, order[1]], routes.x_home), order[0]: None}
        following = {order[1]: blocks[1, 1, order[1]], order[0]: blocks[2, 1, order[0]]}
        far_side = send(blocks[0, 1, order[0]], routes.z_home)
        carried[order[0]] = send(blocks[0, 0, order[0]], routes.z_home)
        rounded = {}
        token, far_side, across[order[1]], resized = hold(token, far_side, across[order[1]], resized)
        for j in range(4):
            for n in order:
                if j == 0 and n == order[0]:
                    token, later, unused = reduce_call(1, n, token, buffer, far_side, None, payload, 1)
                    across[n] = send(later, routes.x_home)
                    continue
                arrived = across[n]
                if j < 3:
                    across[n] = send(following[n], routes.x_home)
                token, total, following[n] = reduce_call(
                    j, n, token, buffer, arrived, carried[n], payload
                )
                if j < 3:
                    carried[n] = send(total, routes.z_home)
                else:
                    rounded[n] = total
        near_grad, far_grad = rounded[0], send(rounded[1], routes.core_out)
    else:
        held = buffer.reshape(dp_n, 1, payload, BS).astype(f32)
        nothing = jnp.zeros_like(held)
        both = jnp.concatenate(
            [jnp.where(core == 0, held, nothing), jnp.where(core == 0, nothing, held)], axis=1
        )
        used_rows = jnp.repeat(used, BS).reshape(dp_n, 1, slots_per * BS, 1)
        used_rows = jnp.concatenate(
            [used_rows, jnp.ones((dp_n, 1, VEC_ROWS, 1), bool)], axis=2
        )
        both = jnp.where(used_rows, both, 0.0).reshape(dp_n * TENSOR * payload, BS)
        near_grad = lax.psum_scatter(both, AXES, scatter_dimension=0, tiled=True).astype(bf16)
        far_grad = near_grad
        resized = resize_call(weights, pinv)

    output = jnp.where(home, out_low, send(out_low, routes.y_out)).astype(f32)
    grad_pixels = sum(
        dot(grad_emb * select_low[:, s : s + 1], resized[s]) for s in range(3)
    ).astype(bf16)
    pixels_other = send(grad_pixels, routes.core_all)
    pixel_sides = [
        grad_pixels[:, s * HALF : (s + 1) * HALF].astype(f32)
        + pixels_other[:, s * HALF : (s + 1) * HALF].astype(f32)
        for s in range(TENSOR)
    ]
    near = jnp.where(core == 0, pixel_sides[0], pixel_sides[1])
    far = jnp.where(core == 0, pixel_sides[1], pixel_sides[0]).astype(bf16)
    patch_grad = jnp.where(home, near, send(far, routes.y_out).astype(f32))

    my_slots = dp_pos * slots_per + jnp.arange(slots_per)
    mine_used = jnp.any(own_slots[None, :] == my_slots[:, None], axis=1).astype(jnp.int32)
    owned_grad, new_master, new_mom, new_var = owner_call(
        mine_used, flag, near_grad, far_grad, master_slots[0], left_basis[0], right_basis[0], mom_slots[0], var_slots[0]
    )
    vec_rows = jnp.where(home, near_grad[slots_per * BS :], far_grad[slots_per * BS :])
    owned_vec_grad = vec_rows.astype(f32).reshape(VEC_ROWS * BS)[:vec_per]
    new_vec_mom = decay * vec_mom[0] + (1.0 - decay) * owned_vec_grad
    new_vec_var = decay * vec_var[0] + (1.0 - decay) * owned_vec_grad * owned_vec_grad
    new_vec = vec_master[0] - vector_rate * new_vec_mom / (jnp.sqrt(new_vec_var) + adam_eps)
    return (
        output,
        patch_grad,
        owned_grad[None],
        new_master[None],
        new_mom[None],
        new_var[None],
        owned_vec_grad[None],
        new_vec[None],
        new_vec_mom[None],
        new_vec_var[None],
    )


def solution(mesh):
    slots = P("tensor", "dp", None, None)
    vectors = P("tensor", "dp")
    tokens = P("dp", None)
    in_specs = (tokens, tokens, tokens, P("tensor", None), P()) + (slots,) * 5 + (vectors,) * 3
    out_specs = (tokens, P("dp", "tensor")) + (slots,) * 4 + (vectors,) * 4
    return jax.shard_map(shards, mesh=mesh, in_specs=in_specs, out_specs=out_specs, check_vma=False)
```
